32 devices in a mesh: ctx: 16 (over z, x, core), wa: 2 (over y).
Axes of the slice: x: 2, y: 2, z: 4, core: 2. Of those that a mesh axis runs over, the one named last changes fastest.
Arguments:
- tokens: bfloat16 [8192, 1472], P(('ctx', 'wa')), may hold values from -6 to 6
- doc_lengths: int32 [8], replicated, may hold values from 1 to 4096, 8192 in all
- key_mask: bfloat16 [8192], P('ctx'), may hold values from -3 to 0
- gain_attn: float32 [1472], replicated, may hold values from 0.1 to 1.9
- w_query: bfloat16 [1472, 384], P(None, 'wa'), may hold values from -0.0625 to 0.0625
- w_key: bfloat16 [1472, 384], P(None, 'wa'), may hold values from -0.0625 to 0.0625
- w_value: bfloat16 [1472, 384], P(None, 'wa'), may hold values from -0.15625 to 0.15625
- w_out: bfloat16 [384, 1472], P('wa'), may hold values from -1.5 to 1.5
- bias_table: float32 [32, 6], P(None, 'wa'), may hold values from -4 to 4
- gain_ffn: float32 [1472], replicated, may hold values from 0.1 to 1.9
- w_gate: bfloat16 [1472, 3584], P(None, 'wa'), may hold values from -0.15625 to 0.15625
- w_up: bfloat16 [1472, 3584], P(None, 'wa'), may hold values from -0.15625 to 0.15625
- w_down: bfloat16 [3584, 1472], P('wa'), may hold values from -0.09375 to 0.09375
- cotangent: bfloat16 [8192, 1472], P(('ctx', 'wa')), may hold values from -6 to 6
Outputs:
- layer_out: bfloat16 [8192, 1472], P(('ctx', 'wa'))
- grad_tokens: float32 [8192, 1472], P(('ctx', 'wa'))
- grad_mask: float32 [8192], P(('ctx', 'wa'))
- grad_gain_attn: float32 [1472], replicated
- grad_w_query: float32 [1472, 384], P(None, 'wa')
- grad_w_key: float32 [1472, 384], P(None, 'wa')
- grad_w_value: float32 [1472, 384], P(None, 'wa')
- grad_w_out: float32 [384, 1472], P('wa')
- grad_table: float32 [32, 6], P(None, 'wa')
- grad_gain_ffn: float32 [1472], replicated
- grad_w_gate: float32 [1472, 3584], P(None, ('wa', 'ctx'))
- grad_w_up: float32 [1472, 3584], P(None, ('wa', 'ctx'))
- grad_w_down: float32 [3584, 1472], P(('wa', 'ctx'))
The draws below stay inside these ranges and needn't reach their ends.
Inputs may be any that keep to these rules, and one draw needn't show every extreme that they name: `doc_lengths`: document lengths in stream order; they add up to 8192, and the longest is exactly 4096.
All inputs are finite; a program needn't handle non-finite values.
Results may differ from the reference program's by a relative error of at most 0.018.
Values may be sent and summed in bfloat16 or wider, within the bound.
A program may use at most 192 MiB of HBM per device.

```python
import math
import jax
import jax.numpy as jnp
import numpy as np
from jax import lax

D = 1472
HEADS = 6
HEAD_DIM = 64
FF = 3584
BUCKETS = 32
TOKENS = 8192
MAXDOC = 4096
DOCS = 8


def shard_levels(rng, shape, split, low, high):
    def one(dim, shards_of):
        steps = jax.random.uniform(jax.random.fold_in(jax.random.fold_in(rng, 6), dim), (shards_of,), jnp.float32, low / len(split), high / len(split))
        return jnp.repeat(jnp.exp(steps), shape[dim] // shards_of).reshape((-1,) + (1,) * (len(shape) - dim - 1))

    level = one(*split[0])
    for cut in split[1:]:
        level = level * one(*cut)
    return level


def split_up(count, total, most, skew):
    portions = [(1 << 20) // math.isqrt(rank ** skew) + 1 for rank in range(2, count + 1)]
    spare, given = total - most - (count - 1), [1] * (count - 1)
    while spare > 0:
        movable = [i for i in range(count - 1) if given[i] < most]
        pool, budget = sum([portions[i] for i in movable]), spare
        for i in movable:
            addition = min(most - given[i], max(1, budget * portions[i] // pool), spare)
            given[i] = given[i] + addition
            spare = spare - addition
    return np.array([most] + given)


def uneven(rng, amount, total, limit, slope):
    if amount == 2:
        one = jax.random.randint(rng, (), max(1, total - limit), min(limit, total - 1) + 1)
        return jnp.stack([one, total - one])
    tallies = jnp.asarray(split_up(amount, total, limit, slope), jnp.int32)
    pairs = (amount - 1) // 2
    giver, taker = tallies[1:1 + 2 * pairs:2], tallies[2:2 + 2 * pairs:2]
    room = jnp.minimum(giver - 1, limit - taker)
    moved = jax.random.randint(jax.random.fold_in(rng, 1), (pairs,), 0, 1 << 20) % (room + 1)
    tallies = tallies.at[1:1 + 2 * pairs:2].set(giver - moved).at[2:2 + 2 * pairs:2].set(taker + moved)
    return tallies[jax.random.permutation(jax.random.fold_in(rng, 2), amount)]


def noise(own_key, extent, width, limit, shards=(), kind=jnp.bfloat16):
    values = jax.random.normal(own_key, extent, jnp.float32) * width
    if len(shards) > 0:
        values = shard_levels(own_key, extent, shards, -0.22, 0.18) * values
    return jnp.clip(values, min=-limit, max=limit).astype(kind)


def setup_inputs(seed: int = 0) -> dict:
    splits = jax.random.split(jax.random.key(seed), 15)
    tokens = noise(splits[0], (TOKENS, D), 1.0, 6.0, ((0, 32),))
    doc_lengths = uneven(splits[1], DOCS, TOKENS, MAXDOC, 2).astype(jnp.int32)
    key_mask = jnp.clip(-3.0 + 3.0 * jax.random.uniform(splits[2], (TOKENS,), jnp.float32) ** shard_levels(splits[2], (TOKENS,), ((0, 16),), -0.2, 0.2), -3.0, 0.0).astype(jnp.bfloat16)
    gain_attn = jnp.clip(1.0 + 0.18 * jax.random.normal(splits[3], (D,), jnp.float32), 0.1, 1.9)
    w_query = noise(splits[4], (D, HEADS * HEAD_DIM), (5 * D) ** -0.5, 0.0625, ((1, 2),))
    w_key = noise(splits[5], (D, HEADS * HEAD_DIM), (5 * D) ** -0.5, 0.0625, ((1, 2),))
    w_value = noise(splits[6], (D, HEADS * HEAD_DIM), D ** -0.5, 0.15625, ((1, 2),))
    w_out = noise(splits[7], (HEADS * HEAD_DIM, D), 16 ** -0.5, 1.5, ((0, 2),))
    bias_table = noise(splits[8], (BUCKETS, HEADS), 1.0, 4.0, ((1, 2),), jnp.float32)
    gain_ffn = jnp.clip(1.0 + 0.18 * jax.random.normal(splits[9], (D,), jnp.float32), 0.1, 1.9)
    w_gate = noise(splits[10], (D, FF), D ** -0.5, 0.15625, ((1, 2),))
    w_up = noise(splits[11], (D, FF), D ** -0.5, 0.15625, ((1, 2),))
    w_down = noise(splits[12], (FF, D), FF ** -0.5, 0.09375, ((0, 2),))
    cotangent = noise(splits[13], (TOKENS, D), 1.0, 6.0, ((0, 32),))
    return {"tokens": tokens, "doc_lengths": doc_lengths, "key_mask": key_mask, "gain_attn": gain_attn, "w_query": w_query, "w_key": w_key, "w_value": w_value, "w_out": w_out, "bias_table": bias_table, "gain_ffn": gain_ffn, "w_gate": w_gate, "w_up": w_up, "w_down": w_down, "cotangent": cotangent}


@jax.custom_vjp
def low(v):
    return lax.optimization_barrier(v.astype(jnp.bfloat16)).astype(jnp.float32)

@jax.custom_vjp
def low_back(v):
    return v

def low_keep(v):
    return (low(v), None)

def low_pass(kept, grad):
    return (grad,)

def back_keep(v):
    return (v, None)

def back_low(kept, grad):
    return (low(grad),)
low.defvjp(low_keep, low_pass)
low_back.defvjp(back_keep, back_low)
bucket_edges = (12, 16, 23, 32, 46, 64, 91)
neg_big = -1e+30
eps = 1e-06
highest = lax.Precision.HIGHEST

def bucket_of(relative):
    distance = jnp.abs(relative)
    bucket = jnp.minimum(distance, 8) + 16 * (relative > 0).astype(jnp.int32)
    for edge in bucket_edges:
        bucket = bucket + (distance >= edge).astype(jnp.int32)
    return bucket

def rms_norm(inputs, gain):
    inv_root = lax.rsqrt(lax.optimization_barrier(jnp.mean(inputs * inputs, axis=-1, keepdims=True)) + eps)
    return inputs * inv_root * gain

def layer_forward(doc_lengths, tokens, key_mask, gain_attn, w_query, w_key, w_value, w_out, bias_table, gain_ffn, w_gate, w_up, w_down):
    total_rows = tokens.shape[0]
    head_count = bias_table.shape[1]
    normed = low(rms_norm(tokens, gain_attn))
    queries = low_back(low(jnp.dot(normed, w_query, precision=highest))).reshape(total_rows, head_count, -1)
    keys_all = low_back(low(jnp.dot(normed, w_key, precision=highest))).reshape(total_rows, head_count, -1)
    values_all = low_back(low(jnp.dot(normed, w_value, precision=highest))).reshape(total_rows, head_count, -1)
    starts = jnp.cumsum(doc_lengths).astype(jnp.int32) - doc_lengths
    positions = jnp.arange(total_rows, dtype=jnp.int32)
    doc_of = lax.optimization_barrier(jnp.sum((positions[:, None] >= starts[None, :]).astype(jnp.int32), axis=1)) - 1
    margin = MAXDOC
    rows = min(512, total_rows)
    window = rows + 2 * margin
    key_pad = jnp.pad(keys_all, ((margin, margin), (0, 0), (0, 0)))
    value_pad = jnp.pad(values_all, ((margin, margin), (0, 0), (0, 0)))
    mask_pad = jnp.pad(key_mask, (margin, margin))
    doc_pad = jnp.pad(doc_of, (margin, margin), constant_values=-1)
    relative = jnp.arange(window, dtype=jnp.int32)[None, :] - jnp.arange(rows, dtype=jnp.int32)[:, None] - margin
    bucket_index = bucket_of(relative)

    def one_block(index):
        begin = (index * rows).astype(jnp.int32)
        block_q = lax.dynamic_slice_in_dim(queries, begin, rows, 0)
        block_k = lax.dynamic_slice_in_dim(key_pad, begin, window, 0)
        block_v = lax.dynamic_slice_in_dim(value_pad, begin, window, 0)
        block_m = lax.dynamic_slice_in_dim(mask_pad, begin, window, 0)
        docs_q = lax.dynamic_slice_in_dim(doc_of, begin, rows, 0)
        docs_k = lax.dynamic_slice_in_dim(doc_pad, begin, window, 0)
        product = low_back(jnp.einsum('qhd,khd->hqk', block_q, block_k, precision=highest))
        bias = jnp.transpose(jnp.take(bias_table, bucket_index, axis=0), (2, 0, 1))
        scores = product + bias + block_m[None, None, :]
        scores = jnp.where((docs_q[:, None] == docs_k[None, :])[None], scores, neg_big)
        row_max = lax.optimization_barrier(jnp.max(scores, axis=-1, keepdims=True))
        log_total = row_max + jnp.log(lax.optimization_barrier(jnp.sum(jnp.exp(scores - row_max), axis=-1, keepdims=True)))
        weights = low(jnp.exp(scores - log_total))
        mixed = jnp.einsum('hqk,khd->qhd', weights, block_v, precision=highest)
        return mixed.reshape(rows, -1)
    attended = lax.map(jax.checkpoint(one_block), jnp.arange(total_rows // rows, dtype=jnp.int32))
    attended = low_back(low(attended.reshape(total_rows, -1)))
    hidden = tokens + low_back(jnp.dot(attended, w_out, precision=highest))
    normed_ffn = low(rms_norm(hidden, gain_ffn))
    gate = low_back(jnp.dot(normed_ffn, w_gate, precision=highest))
    upward = low_back(jnp.dot(normed_ffn, w_up, precision=highest))
    inner = low(jax.nn.gelu(gate, approximate=True) * upward)
    return hidden + jnp.dot(inner, w_down, precision=highest)

def reference(tokens, doc_lengths, key_mask, gain_attn, w_query, w_key, w_value, w_out, bias_table, gain_ffn, w_gate, w_up, w_down, cotangent):
    floats = (tokens, key_mask, gain_attn, w_query, w_key, w_value, w_out, bias_table, gain_ffn, w_gate, w_up, w_down)
    floats = tuple((argument.astype(jnp.float32) for argument in floats))

    def forward(*params):
        return layer_forward(doc_lengths, *params)
    result, pullback = jax.vjp(forward, *floats)
    grads = pullback(cotangent.astype(jnp.float32))
    return (result.astype(jnp.bfloat16), grads[0], grads[1], grads[2], grads[3], grads[4], grads[5], grads[6], grads[7], grads[8], grads[9], grads[10], grads[11])
```

```python
import functools

import jax
import jax.numpy as jnp
from jax import lax
from jax.experimental import pallas as pl
from jax.experimental.pallas import tpu as pltpu
from jax.sharding import PartitionSpec as P

MAXLEN = 8192

bucket_edges = (12, 16, 23, 32, 46, 64, 91)
neg_big = -1e30
eps = 1e-06
far_left_bucket = 15
far_right_bucket = 31
WIDE = 256
TQ = 256
TK = 512
EDGE = 128
PAD = TK + EDGE
f32 = jnp.float32
bf16 = jnp.bfloat16


def bucket_of(relative):
    distance = jnp.abs(relative)
    bucket = jnp.minimum(distance, 8) + 16 * (relative > 0).astype(jnp.int32)
    for edge in bucket_edges:
        bucket = bucket + (distance >= edge).astype(jnp.int32)
    return bucket


def norm_forward(inputs, gain):
    inv_root = lax.rsqrt(jnp.mean(inputs * inputs, axis=-1, keepdims=True) + eps)
    return (inputs * inv_root * gain, inv_root)


def norm_backward(inputs, inv_root, gain, grad_normed):
    scaled = gain * grad_normed
    cubed = inv_root * inv_root * inv_root
    grad_inputs = inv_root * scaled - inputs * cubed * jnp.mean(
        inputs * scaled, axis=-1, keepdims=True
    )
    grad_gain = jnp.sum(grad_normed * inputs * inv_root, axis=0)
    return (grad_inputs, grad_gain)


def gated(gate, upward):
    return jax.nn.gelu(gate, approximate=True) * upward


def nt(a, b):
    return lax.dot_general(a, b, (((1,), (1,)), ((), ())), preferred_element_type=f32)


def nn(a, b):
    return lax.dot_general(a, b, (((1,), (0,)), ((), ())), preferred_element_type=f32)


def split3(x):
    hi = x.astype(bf16)
    rest = x - hi.astype(f32)
    mid = rest.astype(bf16)
    return (hi, mid, (rest - mid.astype(f32)).astype(bf16))


class Plan:
    def __init__(self, heads, width, docs):
        self.heads = heads
        self.width = width
        self.bits = max(1, (docs - 1).bit_length())
        self.cols = heads * width
        self.mask_lane = self.cols
        self.doc_lane = self.cols + 1
        self.stat_lane = self.doc_lane + 2 * self.bits
        assert self.stat_lane + 3 * heads <= WIDE and self.cols + 64 == WIDE and width == 64

    def key_lanes(self, lane, h):
        own = (lane >= h * self.width) & (lane < (h + 1) * self.width)
        aug = (lane >= self.mask_lane) & (lane < self.stat_lane)
        stat = (lane >= self.stat_lane + 3 * h) & (lane < self.stat_lane + 3 * h + 3)
        return own | aug | stat

    def value_lanes(self, lane, h):
        own = (lane >= 64 + h * self.width) & (lane < 64 + (h + 1) * self.width)
        return own | ((lane >= 3 * h) & (lane < 3 * h + 3))


def lanes_of(rows, width=WIDE):
    return lax.broadcasted_iota(jnp.int32, (rows, width), 1)


def near_kernel(heads, table_ref, near_ref):
    row = lax.broadcasted_iota(jnp.int32, (EDGE, 3 * EDGE), 0)
    col = lax.broadcasted_iota(jnp.int32, (EDGE, 3 * EDGE), 1)
    relative = col - EDGE - row
    for flip in range(2):
        bucket = bucket_of(-relative if flip else relative)
        left, right = (far_left_bucket, far_right_bucket)
        if flip:
            left, right = (right, left)
        for h in range(heads):
            base = jnp.full((EDGE, 3 * EDGE), table_ref[0, h], f32)
            for b in range(1, 32):
                base = jnp.where(bucket == b, table_ref[b, h], base)
            far_l = jnp.full((EDGE, EDGE), table_ref[left, h], f32)
            far_r = jnp.full((EDGE, EDGE), table_ref[right, h], f32)
            near_ref[flip, h, :EDGE, : 3 * EDGE] = base
            near_ref[flip, h, :EDGE, 3 * EDGE :] = far_r
            near_ref[flip, h, EDGE:, EDGE:] = base
            near_ref[flip, h, EDGE:, :EDGE] = far_l


def build_keys(plan, g_ref, kaug_ref, km, vm, rows):
    km[:PAD, :] = jnp.broadcast_to(
        jnp.where(pad_lanes(plan), neg_big, 0.0).astype(bf16), (PAD, WIDE)
    )
    km[pl.ds(PAD + rows, PAD), :] = km[:PAD, :]
    vm[:PAD, :] = jnp.zeros((PAD, WIDE), bf16)
    vm[pl.ds(PAD + rows, PAD), :] = jnp.zeros((PAD, WIDE), bf16)
    step = 512
    low = lanes_of(step, 128) < 64
    ones = (lanes_of(step, 128) < 3 * plan.heads).astype(bf16)

    def body(n, unused):
        at = pl.multiple_of(n * step, step)
        to = pl.multiple_of(PAD + n * step, 128)
        middle = g_ref[pl.ds(at, step), 128:256]
        km[pl.ds(to, step), 0:128] = g_ref[pl.ds(at, step), 0:128]
        km[pl.ds(to, step), 128:256] = jnp.where(low, middle, kaug_ref[pl.ds(at, step), :])
        vm[pl.ds(to, step), 0:128] = jnp.where(low, ones, middle)
        vm[pl.ds(to, step), 128:256] = g_ref[pl.ds(at, step), 256:384]
        return unused

    lax.fori_loop(0, rows // step, body, 0)


def pad_lanes(plan):
    lane = lanes_of(1)
    return (lane >= plan.doc_lane) & (lane < plan.stat_lane)


def fwd_kernel(
    plan, rows, pair, bounds, table_ref, g_ref, kaug_ref, q_ref, near_ref,
    low_ref, wide_ref, qb_ref, km, vm, acc, row_max, qh_ref,
):
    build_keys(plan, g_ref, kaug_ref, km, vm, rows)
    lane = lanes_of(TQ)

    def tile(t, unused):
        start = pl.multiple_of(bounds[0] + t * TQ, 128)
        n_left, n_right = (bounds[1 + 2 * t], bounds[2 + 2 * t])
        out = pl.ds(pl.multiple_of(t * TQ, TQ), TQ)
        q = q_ref[out, :]
        near = pl.ds(pl.multiple_of(start + PAD - EDGE, 128), TK)
        for h in range(plan.heads):
            qh = jnp.where(plan.key_lanes(lane, h), q, jnp.zeros_like(q))
            qh_ref[h] = qh
            s = nt(qh, km[near, :]) + near_ref[0, h]
            top = jnp.max(s, axis=1, keepdims=True)
            p = jnp.exp(s - top).astype(bf16)
            acc[h] = nn(p, vm[near, :])
            row_max[h] = jnp.broadcast_to(top, (TQ, 128))

        def far(bucket):
            def step(first, n):
                span = pl.ds(pl.multiple_of(first + n, 128), TK)
                for h in range(plan.heads):
                    s = nt(qh_ref[h], km[span, :])
                    offset = table_ref[bucket, h]
                    old = row_max[h][:, :1]
                    top = jnp.maximum(old, jnp.max(s, axis=1, keepdims=True) + offset)
                    p = jnp.exp(s - (top - offset)).astype(bf16)
                    acc[h] = acc[h] * jnp.exp(old - top) + nn(p, vm[span, :])
                    row_max[h] = jnp.broadcast_to(top, (TQ, 128))
            return step

        left, right = (far(far_left_bucket), far(far_right_bucket))

        @pl.loop(0, n_left)
        def _(n):
            left(start + PAD - EDGE - TK, -n * TK)

        @pl.loop(0, n_right)
        def _(n):
            right(start + PAD - EDGE + TK, n * TK)

        wide = jnp.zeros((TQ, WIDE), f32)
        qb = jnp.where(lane < plan.stat_lane, q, jnp.zeros_like(q))
        for h in range(plan.heads):
            total = acc[h][:, 3 * h : 3 * h + 1]
            log_total = row_max[h][:, :1] + jnp.log(total)
            wide = jnp.where(lane // 64 == h + 1, acc[h] / total, wide)
            for i, part in enumerate(split3(-log_total)):
                qb = jnp.where(lane == plan.stat_lane + 3 * h + i, part, qb)
        wide_ref[out, :] = wide
        low_ref[out, :] = wide.astype(bf16)
        qb_ref[out, :] = qb
        return unused

    lax.fori_loop(0, pair // TQ, tile, 0)


def dq_kernel(
    plan, rows, pair, bounds, table_ref, g_ref, kaug_ref, qb_ref, do_ref, near_ref,
    dq_ref, tab_ref, km, vm, acc, qh_ref, doh_ref, near_acc, far_acc,
):
    build_keys(plan, g_ref, kaug_ref, km, vm, rows)
    lane = lanes_of(TQ)
    near_acc[...] = jnp.zeros_like(near_acc)
    far_acc[...] = jnp.zeros_like(far_acc)

    def tile(t, unused):
        start = pl.multiple_of(bounds[0] + t * TQ, 128)
        n_left, n_right = (bounds[1 + 2 * t], bounds[2 + 2 * t])
        out = pl.ds(pl.multiple_of(t * TQ, TQ), TQ)
        q = qb_ref[out, :]
        do = do_ref[out, :]
        near = pl.ds(pl.multiple_of(start + PAD - EDGE, 128), TK)

        def grads(h, s, span):
            p = jnp.exp(s)
            return p * nt(doh_ref[h], vm[span, :])

        for h in range(plan.heads):
            qh_ref[h] = jnp.where(plan.key_lanes(lane, h), q, jnp.zeros_like(q))
            doh_ref[h] = jnp.where(plan.value_lanes(lane, h), do, jnp.zeros_like(do))
            ds = grads(h, nt(qh_ref[h], km[near, :]) + near_ref[0, h], near)
            near_acc[h] += ds
            acc[h] = nn(ds.astype(bf16), km[near, :])

        def far(bucket, slot):
            def step(first, n):
                span = pl.ds(pl.multiple_of(first + n, 128), TK)
                for h in range(plan.heads):
                    ds = grads(h, nt(qh_ref[h], km[span, :]) + table_ref[bucket, h], span)
                    acc[h] += nn(ds.astype(bf16), km[span, :])
                    far_acc[slot, h] += (
                        ds[:, 0:128] + ds[:, 128:256] + ds[:, 256:384] + ds[:, 384:512]
                    )
            return step

        left, right = (far(far_left_bucket, 0), far(far_right_bucket, 1))

        @pl.loop(0, n_left)
        def _(n):
            left(start + PAD - EDGE - TK, -n * TK)

        @pl.loop(0, n_right)
        def _(n):
            right(start + PAD - EDGE + TK, n * TK)

        total = jnp.zeros((TQ, WIDE), f32)
        for h in range(plan.heads):
            total = jnp.where(lane // 64 == h, acc[h], total)
        dq_ref[out, :] = total.astype(bf16)
        return unused

    lax.fori_loop(0, pair // TQ, tile, 0)
    row = lax.broadcasted_iota(jnp.int32, (EDGE, 3 * EDGE), 0)
    col = lax.broadcasted_iota(jnp.int32, (EDGE, 3 * EDGE), 1)
    bucket = bucket_of(col - EDGE - row)
    for h in range(plan.heads):
        band = near_acc[h, :EDGE, : 3 * EDGE] + near_acc[h, EDGE:, EDGE:]
        extra_right = near_acc[h, :EDGE, 3 * EDGE :]
        extra_left = near_acc[h, EDGE:, :EDGE]
        for b in range(32):
            part = jnp.sum(jnp.where(bucket == b, band, 0.0), axis=0, keepdims=True)
            part = part[:, :128] + part[:, 128:256] + part[:, 256:]
            if b == far_left_bucket:
                part = part + jnp.sum(far_acc[0, h], axis=0, keepdims=True)
                part = part + jnp.sum(extra_left, axis=0, keepdims=True)
            if b == far_right_bucket:
                part = part + jnp.sum(far_acc[1, h], axis=0, keepdims=True)
                part = part + jnp.sum(extra_right, axis=0, keepdims=True)
            tab_ref[h, b : b + 1, :] = part


def dkv_kernel(
    plan, rows, pair, bounds, table_ref, qall_ref, doall_ref, g_ref, kaug_ref, near_ref,
    dk_ref, dv_ref, qp, dop, kh_ref, vh_ref, acc_k, acc_v,
):
    lane = lanes_of(TQ)
    first = lanes_of(1)
    stat = (first >= plan.stat_lane) & (first < plan.stat_lane + 3 * plan.heads)
    qp[:PAD, :] = jnp.broadcast_to(jnp.where(stat, neg_big, 0.0).astype(bf16), (PAD, WIDE))
    qp[pl.ds(PAD + rows, PAD), :] = qp[:PAD, :]
    dop[:PAD, :] = jnp.zeros((PAD, WIDE), bf16)
    dop[pl.ds(PAD + rows, PAD), :] = jnp.zeros((PAD, WIDE), bf16)
    step = 512

    def fill(n, unused):
        at = pl.multiple_of(n * step, step)
        to = pl.multiple_of(PAD + n * step, 128)
        qp[pl.ds(to, step), :] = qall_ref[pl.ds(at, step), :]
        dop[pl.ds(to, step), :] = doall_ref[pl.ds(at, step), :]
        return unused

    lax.fori_loop(0, rows // step, fill, 0)
    low = lanes_of(TQ, 128) < 64
    ones = (lanes_of(TQ, 128) < 3 * plan.heads).astype(bf16)

    def tile(t, unused):
        start = pl.multiple_of(bounds[0] + t * TQ, 128)
        n_left, n_right = (bounds[1 + 2 * t], bounds[2 + 2 * t])
        out = pl.ds(pl.multiple_of(t * TQ, TQ), TQ)
        middle = g_ref[out, 128:256]
        k = jnp.concatenate([g_ref[out, 0:128], jnp.where(low, middle, kaug_ref[out, :])], axis=1)
        v = jnp.concatenate([jnp.where(low, ones, middle), g_ref[out, 256:384]], axis=1)
        near = pl.ds(pl.multiple_of(start + PAD - EDGE, 128), TK)

        def grads(h, s, span):
            p = jnp.exp(s)
            ds = p * nt(vh_ref[h], dop[span, :])
            return nn(p.astype(bf16), dop[span, :]), nn(ds.astype(bf16), qp[span, :])

        for h in range(plan.heads):
            kh_ref[h] = jnp.where(plan.key_lanes(lane, h), k, jnp.zeros_like(k))
            vh_ref[h] = jnp.where(plan.value_lanes(lane, h), v, jnp.zeros_like(v))
            acc_v[h], acc_k[h] = grads(h, nt(kh_ref[h], qp[near, :]) + near_ref[1, h], near)

        def far(bucket):
            def step(first, n):
                span = pl.ds(pl.multiple_of(first + n, 128), TK)
                for h in range(plan.heads):
                    add_v, add_k = grads(
                        h, nt(kh_ref[h], qp[span, :]) + table_ref[bucket, h], span
                    )
                    acc_v[h] += add_v
                    acc_k[h] += add_k
            return step

        left, right = (far(far_right_bucket), far(far_left_bucket))

        @pl.loop(0, n_left)
        def _(n):
            left(start + PAD - EDGE - TK, -n * TK)

        @pl.loop(0, n_right)
        def _(n):
            right(start + PAD - EDGE + TK, n * TK)

        dk = jnp.zeros((TQ, WIDE), f32)
        dv = jnp.zeros((TQ, WIDE), f32)
        mask_grad = jnp.zeros((TQ, 1), f32)
        for h in range(plan.heads):
            dk = jnp.where(lane // 64 == h, acc_k[h], dk)
            dv = jnp.where(lane // 64 == h + 1, acc_v[h], dv)
            mask_grad = mask_grad + acc_k[h][:, plan.mask_lane : plan.mask_lane + 1]
        dk_ref[out, :] = jnp.where(lane == plan.mask_lane, mask_grad, dk)
        dv_ref[out, :] = dv.astype(bf16)
        return unused

    lax.fori_loop(0, pair // TQ, tile, 0)


def grad_attended_kernel(plan, branch_ref, w_ref, wide_ref, do_ref):
    rows = branch_ref.shape[0]
    lane = lanes_of(rows)
    grad = nt(branch_ref[...], w_ref[...]).astype(bf16)
    terms = grad.astype(f32) * wide_ref[...]
    out = grad
    for h in range(plan.heads):
        row_term = jnp.sum(
            jnp.where(lane // 64 == h + 1, terms, 0.0), axis=1, keepdims=True
        )
        for i, part in enumerate(split3(-row_term)):
            out = jnp.where(lane == 3 * h + i, part, out)
    do_ref[...] = out


vmem = pl.BlockSpec(memory_space=pltpu.VMEM)
smem = pl.BlockSpec(memory_space=pltpu.SMEM)


def params():
    return pltpu.CompilerParams(vmem_limit_bytes=56 * 2**20)


def shards(
    tokens,
    doc_lengths,
    key_mask,
    gain_attn,
    w_query,
    w_key,
    w_value,
    w_out,
    bias_table,
    gain_ffn,
    w_gate,
    w_up,
    w_down,
    cotangent,
):
    own_rows, model = tokens.shape
    group = lax.axis_size("wa")
    cycle_size = lax.axis_size("ctx")
    pair = own_rows * group
    heads = bias_table.shape[1]
    docs = doc_lengths.shape[0]
    plan = Plan(heads, w_query.shape[1] // heads, docs)
    total_rows = pair * cycle_size
    doc_most = min(MAXLEN, total_rows // 2)
    reach = min(cycle_size - 1, (doc_most - 1) // pair + 1)
    base = lax.axis_index("ctx") * pair
    rows = min(total_rows, (2 * reach + 1) * pair)
    origin = jnp.clip(base - reach * pair, 0, total_rows - rows).astype(jnp.int32)
    ends = jnp.cumsum(doc_lengths).astype(jnp.int32)
    starts = ends - doc_lengths

    def doc_at(positions):
        return jnp.sum((positions[:, None] >= starts[None, :]).astype(jnp.int32), axis=1) - 1

    tiles = pair // TQ
    tile_start = base + TQ * jnp.arange(tiles, dtype=jnp.int32)
    first_doc = jnp.arange(docs, dtype=jnp.int32)[None, :] == doc_at(tile_start)[:, None]
    last_doc = jnp.arange(docs, dtype=jnp.int32)[None, :] == doc_at(tile_start + TQ - 1)[:, None]
    low_end = jnp.sum(jnp.where(first_doc, starts[None, :], 0), axis=1)
    high_end = jnp.sum(jnp.where(last_doc, ends[None, :], 0), axis=1)
    n_left = jnp.maximum(0, (tile_start - EDGE - low_end + TK - 1) // TK)
    n_right = jnp.maximum(0, (high_end - (tile_start - EDGE + TK) + TK - 1) // TK)
    bounds = jnp.concatenate(
        [(base - origin)[None], jnp.stack([n_left, n_right], axis=1).reshape(-1)]
    ).astype(jnp.int32)

    mask_all = lax.all_gather(key_mask, "ctx", axis=0, tiled=True)
    tokens_wide = tokens.astype(f32)
    normed_attn, inv_attn = norm_forward(tokens_wide, gain_attn)
    normed_low = normed_attn.astype(bf16)
    pair_normed, pair_cot = (
        lax.all_gather(normed_low, "wa", axis=0, tiled=True),
        lax.all_gather(cotangent, "wa", axis=0, tiled=True),
    )
    w_kv = jnp.concatenate([w_key, w_value], axis=1)
    own_kv = jnp.dot(pair_normed, w_kv, preferred_element_type=f32).astype(bf16)
    queries = jnp.dot(pair_normed, w_query, preferred_element_type=f32).astype(bf16)

    def window(gathered):
        if rows == total_rows:
            return gathered
        return lax.dynamic_slice_in_dim(gathered, origin, rows, 0)

    gather = functools.partial(lax.all_gather, axis_name="ctx", axis=0, tiled=True)
    kv_all = window(gather(own_kv))
    positions = origin + jnp.arange(rows, dtype=jnp.int32)
    doc_of = doc_at(positions)
    lane = jnp.arange(128, dtype=jnp.int32)[None, :] + 128
    code = lane - plan.doc_lane
    bit_differs = ((doc_of[:, None] >> (code >> 1)) & 1) != (code & 1)
    k_aug = jnp.where(
        lane == plan.mask_lane,
        window(mask_all).astype(f32)[:, None],
        jnp.where(
            lane < plan.stat_lane,
            jnp.where(bit_differs & (code >= 0), neg_big, 0.0),
            (lane < plan.stat_lane + 3 * heads).astype(f32),
        ),
    ).astype(bf16)
    own_docs = doc_at(base + jnp.arange(pair, dtype=jnp.int32))
    own_differs = ((own_docs[:, None] >> (code >> 1)) & 1) != (code & 1)
    q_aug = jnp.where(
        lane == plan.mask_lane, 1.0, ((lane < plan.stat_lane) & ~own_differs).astype(f32)
    ).astype(bf16)
    q_wide = jnp.concatenate(
        [queries, q_aug[:, plan.cols - 128 :]], axis=1
    )
    near_bias = pl.pallas_call(
        functools.partial(near_kernel, heads),
        out_shape=jax.ShapeDtypeStruct((2, heads, TQ, TK), f32),
        in_specs=[smem],
        out_specs=vmem,
        compiler_params=params(),
        name="near_bias",
    )(bias_table)

    padded = rows + 2 * PAD
    attended, mixed, q_back = pl.pallas_call(
        functools.partial(fwd_kernel, plan, rows, pair),
        out_shape=(
            jax.ShapeDtypeStruct((pair, WIDE), bf16),
            jax.ShapeDtypeStruct((pair, WIDE), f32),
            jax.ShapeDtypeStruct((pair, WIDE), bf16),
        ),
        in_specs=[smem, smem, vmem, vmem, vmem, vmem],
        out_specs=(vmem, vmem, vmem),
        scratch_shapes=[
            pltpu.VMEM((padded, WIDE), bf16),
            pltpu.VMEM((padded, WIDE), bf16),
            pltpu.VMEM((heads, TQ, WIDE), f32),
            pltpu.VMEM((heads, TQ, 128), f32),
            pltpu.VMEM((heads, TQ, WIDE), bf16),
        ],
        compiler_params=params(),
        name="attention_forward",
    )(bounds, bias_table, kv_all, k_aug, q_wide, near_bias)
    q_all = window(gather(q_back))
    w_out_pad = jnp.concatenate([jnp.zeros((64, model), bf16), w_out], axis=0)
    branch = lax.psum_scatter(
        jnp.dot(attended, w_out_pad, preferred_element_type=f32).astype(bf16),
        "wa",
        scatter_dimension=0,
        tiled=True,
    ).astype(f32)
    hidden = tokens_wide + branch
    normed_ffn, inv_ffn = norm_forward(hidden, gain_ffn)
    ffn_low = normed_ffn.astype(bf16)
    pair_ffn = lax.all_gather(ffn_low, "wa", axis=0, tiled=True)
    gate = jnp.dot(pair_ffn, w_gate, preferred_element_type=f32)
    upward = jnp.dot(pair_ffn, w_up, preferred_element_type=f32)
    inner = gated(gate, upward).astype(bf16)
    ffn_part = jnp.dot(inner, w_down, preferred_element_type=f32)
    layer_out = (
        hidden
        + lax.psum_scatter(
            ffn_part.astype(bf16), "wa", scatter_dimension=0, tiled=True
        ).astype(f32)
    ).astype(bf16)
    grad_inner = jnp.dot(pair_cot, w_down.T, preferred_element_type=f32)
    down_half = jnp.dot(inner.T, pair_cot, preferred_element_type=f32).astype(bf16)
    unused_value, pullback = jax.vjp(gated, gate, upward)
    grad_gate, grad_upward = pullback(grad_inner)
    grad_gate = grad_gate.astype(bf16)
    grad_upward = grad_upward.astype(bf16)
    grad_pair_ffn = jnp.dot(grad_gate, w_gate.T, preferred_element_type=f32) + jnp.dot(
        grad_upward, w_up.T, preferred_element_type=f32
    )
    grad_normed_ffn = lax.psum_scatter(
        grad_pair_ffn.astype(bf16), "wa", scatter_dimension=0, tiled=True
    ).astype(f32)
    gate_half = jnp.dot(pair_ffn.T, grad_gate, preferred_element_type=f32).astype(bf16)
    up_half = jnp.dot(pair_ffn.T, grad_upward, preferred_element_type=f32).astype(bf16)
    grad_w_gate, grad_w_up, grad_w_down = (
        lax.psum_scatter(gate_half, "ctx", scatter_dimension=1, tiled=True).astype(f32),
        lax.psum_scatter(up_half, "ctx", scatter_dimension=1, tiled=True).astype(f32),
        lax.psum_scatter(down_half, "ctx", scatter_dimension=0, tiled=True).astype(f32),
    )
    hidden_step, gain_ffn_part = norm_backward(hidden, inv_ffn, gain_ffn, grad_normed_ffn)
    grad_hidden = cotangent.astype(f32) + hidden_step
    pair_branch = lax.all_gather(grad_hidden.astype(bf16), "wa", axis=0, tiled=True)
    out_part = jnp.dot(attended.T, pair_branch, preferred_element_type=f32)[64:]
    do_wide = pl.pallas_call(
        functools.partial(grad_attended_kernel, plan),
        out_shape=jax.ShapeDtypeStruct((pair, WIDE), bf16),
        in_specs=[vmem, vmem, vmem],
        out_specs=vmem,
        compiler_params=params(),
        name="grad_attended",
    )(pair_branch, w_out_pad, mixed)
    do_all = window(gather(do_wide))

    grad_queries, table_part = pl.pallas_call(
        functools.partial(dq_kernel, plan, rows, pair),
        out_shape=(
            jax.ShapeDtypeStruct((pair, WIDE), bf16),
            jax.ShapeDtypeStruct((heads, 32, 128), f32),
        ),
        in_specs=[smem, smem, vmem, vmem, vmem, vmem, vmem],
        out_specs=(vmem, vmem),
        scratch_shapes=[
            pltpu.VMEM((padded, WIDE), bf16),
            pltpu.VMEM((padded, WIDE), bf16),
            pltpu.VMEM((heads, TQ, WIDE), f32),
            pltpu.VMEM((heads, TQ, WIDE), bf16),
            pltpu.VMEM((heads, TQ, WIDE), bf16),
            pltpu.VMEM((heads, TQ, TK), f32),
            pltpu.VMEM((2, heads, TQ, 128), f32),
        ],
        compiler_params=params(),
        name="attention_grad_queries",
    )(bounds, bias_table, kv_all, k_aug, q_back, do_wide, near_bias)
    own_aug = lax.dynamic_slice_in_dim(k_aug, base - origin, pair, 0)
    grad_keys, grad_values = pl.pallas_call(
        functools.partial(dkv_kernel, plan, rows, pair),
        out_shape=(
            jax.ShapeDtypeStruct((pair, WIDE), f32),
            jax.ShapeDtypeStruct((pair, WIDE), bf16),
        ),
        in_specs=[smem, smem, vmem, vmem, vmem, vmem, vmem],
        out_specs=(vmem, vmem),
        scratch_shapes=[
            pltpu.VMEM((padded, WIDE), bf16),
            pltpu.VMEM((padded, WIDE), bf16),
            pltpu.VMEM((heads, TQ, WIDE), bf16),
            pltpu.VMEM((heads, TQ, WIDE), bf16),
            pltpu.VMEM((heads, TQ, WIDE), f32),
            pltpu.VMEM((heads, TQ, WIDE), f32),
        ],
        compiler_params=params(),
        name="attention_grad_keys",
    )(bounds, bias_table, q_all, do_all, own_kv, own_aug, near_bias)
    grad_tab = jnp.sum(table_part, axis=2).T
    mask_total = grad_keys[:, plan.mask_lane]
    cols = plan.cols
    grad_qkv = jnp.concatenate(
        [grad_queries[:, :cols], grad_keys[:, :cols].astype(bf16), grad_values[:, 64:]], axis=1
    )
    w_qkv = jnp.concatenate([w_query, w_key, w_value], axis=1)
    qkv_part = jnp.dot(pair_normed.T, grad_qkv, preferred_element_type=f32)
    grad_pair = jnp.dot(grad_qkv, w_qkv.T, preferred_element_type=f32)
    grad_normed_attn, grad_mask = (
        lax.psum_scatter(
            grad_pair.astype(bf16), "wa", scatter_dimension=0, tiled=True
        ).astype(f32),
        lax.psum_scatter(
            mask_total.astype(bf16), "wa", scatter_dimension=0, tiled=True
        ).astype(f32),
    )
    token_step, gain_attn_part = norm_backward(tokens_wide, inv_attn, gain_attn, grad_normed_attn)
    grad_tokens = grad_hidden + token_step
    grad_gain_attn, grad_gain_ffn = lax.psum((gain_attn_part, gain_ffn_part), ("ctx", "wa"))
    grad_w_qkv, grad_w_out, grad_table = lax.psum((qkv_part, out_part, grad_tab), "ctx")
    return (
        layer_out,
        grad_tokens,
        grad_mask,
        grad_gain_attn,
        grad_w_qkv[:, :cols],
        grad_w_qkv[:, cols : 2 * cols],
        grad_w_qkv[:, 2 * cols :],
        grad_w_out,
        grad_table,
        grad_gain_ffn,
        grad_w_gate,
        grad_w_up,
        grad_w_down,
    )


def solution(mesh):
    placed = (
        P(("ctx", "wa"), None),
        P(),
        P("ctx"),
        P(),
        P(None, "wa"),
        P(None, "wa"),
        P(None, "wa"),
        P("wa", None),
        P(None, "wa"),
        P(),
        P(None, "wa"),
        P(None, "wa"),
        P("wa", None),
        P(("ctx", "wa"), None),
    )
    return jax.shard_map(
        shards,
        mesh=mesh,
        in_specs=placed,
        out_specs=(
            P(("ctx", "wa"), None),
            P(("ctx", "wa"), None),
            P(("ctx", "wa")),
            P(),
            P(None, "wa"),
            P(None, "wa"),
            P(None, "wa"),
            P("wa", None),
            P(None, "wa"),
            P(),
            P(None, ("wa", "ctx")),
            P(None, ("wa", "ctx")),
            P(("wa", "ctx"), None),
        ),
        check_vma=False,
    )
```

```python
import functools

import jax
import jax.numpy as jnp
from jax import lax
from jax.experimental import pallas as pl
from jax.experimental.pallas import tpu as pltpu
from jax.sharding import PartitionSpec as P

MAXLEN = 8192

bucket_edges = (12, 16, 23, 32, 46, 64, 91)
neg_big = -1e30
eps = 1e-06
far_left_bucket = 15
far_right_bucket = 31
WIDE = 256
TQ = 256
TK = 512
EDGE = 128
PAD = TK + EDGE
f32 = jnp.float32
bf16 = jnp.bfloat16


def bucket_of(relative):
    distance = jnp.abs(relative)
    bucket = jnp.minimum(distance, 8) + 16 * (relative > 0).astype(jnp.int32)
    for edge in bucket_edges:
        bucket = bucket + (distance >= edge).astype(jnp.int32)
    return bucket


def norm_forward(inputs, gain):
    inv_root = lax.rsqrt(jnp.mean(inputs * inputs, axis=-1, keepdims=True) + eps)
    return (inputs * inv_root * gain, inv_root)


def norm_backward(inputs, inv_root, gain, grad_normed):
    scaled = gain * grad_normed
    cubed = inv_root * inv_root * inv_root
    grad_inputs = inv_root * scaled - inputs * cubed * jnp.mean(
        inputs * scaled, axis=-1, keepdims=True
    )
    grad_gain = jnp.sum(grad_normed * inputs * inv_root, axis=0)
    return (grad_inputs, grad_gain)


def gated(gate, upward):
    return jax.nn.gelu(gate, approximate=True) * upward


def nt(a, b):
    return lax.dot_general(a, b, (((1,), (1,)), ((), ())), preferred_element_type=f32)


def nn(a, b):
    return lax.dot_general(a, b, (((1,), (0,)), ((), ())), preferred_element_type=f32)


def split3(x):
    hi = x.astype(bf16)
    rest = x - hi.astype(f32)
    mid = rest.astype(bf16)
    return (hi, mid, (rest - mid.astype(f32)).astype(bf16))


class Plan:
    def __init__(self, heads, width, docs):
        self.heads = heads
        self.width = width
        self.bits = max(1, (docs - 1).bit_length())
        self.cols = heads * width
        self.mask_lane = self.cols
        self.doc_lane = self.cols + 1
        self.stat_lane = self.doc_lane + 2 * self.bits
        assert self.stat_lane + 3 * heads <= WIDE and self.cols + 64 == WIDE and width == 64

    def key_lanes(self, lane, h):
        own = (lane >= h * self.width) & (lane < (h + 1) * self.width)
        aug = (lane >= self.mask_lane) & (lane < self.stat_lane)
        stat = (lane >= self.stat_lane + 3 * h) & (lane < self.stat_lane + 3 * h + 3)
        return own | aug | stat

    def value_lanes(self, lane, h):
        own = (lane >= 64 + h * self.width) & (lane < 64 + (h + 1) * self.width)
        return own | ((lane >= 3 * h) & (lane < 3 * h + 3))


def lanes_of(rows, width=WIDE):
    return lax.broadcasted_iota(jnp.int32, (rows, width), 1)


def near_kernel(heads, table_ref, near_ref):
    row = lax.broadcasted_iota(jnp.int32, (EDGE, 3 * EDGE), 0)
    col = lax.broadcasted_iota(jnp.int32, (EDGE, 3 * EDGE), 1)
    relative = col - EDGE - row
    for flip in range(2):
        bucket = bucket_of(-relative if flip else relative)
        left, right = (far_left_bucket, far_right_bucket)
        if flip:
            left, right = (right, left)
        for h in range(heads):
            base = jnp.full((EDGE, 3 * EDGE), table_ref[0, h], f32)
            for b in range(1, 32):
                base = jnp.where(bucket == b, table_ref[b, h], base)
            far_l = jnp.full((EDGE, EDGE), table_ref[left, h], f32)
            far_r = jnp.full((EDGE, EDGE), table_ref[right, h], f32)
            near_ref[flip, h, :EDGE, : 3 * EDGE] = base
            near_ref[flip, h, :EDGE, 3 * EDGE :] = far_r
            near_ref[flip, h, EDGE:, EDGE:] = base
            near_ref[flip, h, EDGE:, :EDGE] = far_l


def build_keys(plan, g_ref, kaug_ref, km, vm, rows):
    km[:PAD, :] = jnp.broadcast_to(
        jnp.where(pad_lanes(plan), neg_big, 0.0).astype(bf16), (PAD, WIDE)
    )
    km[pl.ds(PAD + rows, PAD), :] = km[:PAD, :]
    vm[:PAD, :] = jnp.zeros((PAD, WIDE), bf16)
    vm[pl.ds(PAD + rows, PAD), :] = jnp.zeros((PAD, WIDE), bf16)
    step = 512
    low = lanes_of(step, 128) < 64
    ones = (lanes_of(step, 128) < 3 * plan.heads).astype(bf16)

    def body(n, unused):
        at = pl.multiple_of(n * step, step)
        to = pl.multiple_of(PAD + n * step, 128)
        middle = g_ref[pl.ds(at, step), 128:256]
        km[pl.ds(to, step), 0:128] = g_ref[pl.ds(at, step), 0:128]
        km[pl.ds(to, step), 128:256] = jnp.where(low, middle, kaug_ref[pl.ds(at, step), :])
        vm[pl.ds(to, step), 0:128] = jnp.where(low, ones, middle)
        vm[pl.ds(to, step), 128:256] = g_ref[pl.ds(at, step), 256:384]
        return unused

    lax.fori_loop(0, rows // step, body, 0)


def pad_lanes(plan):
    lane = lanes_of(1)
    return (lane >= plan.doc_lane) & (lane < plan.stat_lane)


def fwd_kernel(
    plan, rows, pair, bounds, table_ref, g_ref, kaug_ref, q_ref, near_ref,
    low_ref, wide_ref, qb_ref, km, vm, acc, row_max, qh_ref,
):
    build_keys(plan, g_ref, kaug_ref, km, vm, rows)
    lane = lanes_of(TQ)

    def tile(t, unused):
        start = pl.multiple_of(bounds[0] + t * TQ, 128)
        n_left, n_right = (bounds[1 + 2 * t], bounds[2 + 2 * t])
        out = pl.ds(pl.multiple_of(t * TQ, TQ), TQ)
        q = q_ref[out, :]
        near = pl.ds(pl.multiple_of(start + PAD - EDGE, 128), TK)
        for h in range(plan.heads):
            qh = jnp.where(plan.key_lanes(lane, h), q, jnp.zeros_like(q))
            qh_ref[h] = qh
            s = nt(qh, km[near, :]) + near_ref[0, h]
            top = jnp.max(s, axis=1, keepdims=True)
            p = jnp.exp(s - top).astype(bf16)
            acc[h] = nn(p, vm[near, :])
            row_max[h] = jnp.broadcast_to(top, (TQ, 128))

        def far(bucket):
            def step(first, n):
                span = pl.ds(pl.multiple_of(first + n, 128), TK)
                for h in range(plan.heads):
                    s = nt(qh_ref[h], km[span, :])
                    offset = table_ref[bucket, h]
                    old = row_max[h][:, :1]
                    top = jnp.maximum(old, jnp.max(s, axis=1, keepdims=True) + offset)
                    p = jnp.exp(s - (top - offset)).astype(bf16)
                    acc[h] = acc[h] * jnp.exp(old - top) + nn(p, vm[span, :])
                    row_max[h] = jnp.broadcast_to(top, (TQ, 128))
            return step

        left, right = (far(far_left_bucket), far(far_right_bucket))

        @pl.loop(0, n_left)
        def _(n):
            left(start + PAD - EDGE - TK, -n * TK)

        @pl.loop(0, n_right)
        def _(n):
            right(start + PAD - EDGE + TK, n * TK)

        wide = jnp.zeros((TQ, WIDE), f32)
        qb = jnp.where(lane < plan.stat_lane, q, jnp.zeros_like(q))
        for h in range(plan.heads):
            total = acc[h][:, 3 * h : 3 * h + 1]
            log_total = row_max[h][:, :1] + jnp.log(total)
            wide = jnp.where(lane // 64 == h + 1, acc[h] / total, wide)
            for i, part in enumerate(split3(-log_total)):
                qb = jnp.where(lane == plan.stat_lane + 3 * h + i, part, qb)
        wide_ref[out, :] = wide
        low_ref[out, :] = wide.astype(bf16)
        qb_ref[out, :] = qb
        return unused

    lax.fori_loop(0, pair // TQ, tile, 0)


def dq_kernel(
    plan, rows, pair, bounds, table_ref, g_ref, kaug_ref, qb_ref, do_ref, near_ref,
    dq_ref, tab_ref, km, vm, acc, qh_ref, doh_ref, near_acc, far_acc,
):
    build_keys(plan, g_ref, kaug_ref, km, vm, rows)
    lane = lanes_of(TQ)
    near_acc[...] = jnp.zeros_like(near_acc)
    far_acc[...] = jnp.zeros_like(far_acc)

    def tile(t, unused):
        start = pl.multiple_of(bounds[0] + t * TQ, 128)
        n_left, n_right = (bounds[1 + 2 * t], bounds[2 + 2 * t])
        out = pl.ds(pl.multiple_of(t * TQ, TQ), TQ)
        q = qb_ref[out, :]
        do = do_ref[out, :]
        near = pl.ds(pl.multiple_of(start + PAD - EDGE, 128), TK)

        def grads(h, s, span):
            p = jnp.exp(s)
            return p * nt(doh_ref[h], vm[span, :])

        for h in range(plan.heads):
            qh_ref[h] = jnp.where(plan.key_lanes(lane, h), q, jnp.zeros_like(q))
            doh_ref[h] = jnp.where(plan.value_lanes(lane, h), do, jnp.zeros_like(do))
            ds = grads(h, nt(qh_ref[h], km[near, :]) + near_ref[0, h], near)
            near_acc[h] += ds
            acc[h] = nn(ds.astype(bf16), km[near, :])

        def far(bucket, slot):
            def step(first, n):
                span = pl.ds(pl.multiple_of(first + n, 128), TK)
                for h in range(plan.heads):
                    ds = grads(h, nt(qh_ref[h], km[span, :]) + table_ref[bucket, h], span)
                    acc[h] += nn(ds.astype(bf16), km[span, :])
                    far_acc[slot, h] += (
                        ds[:, 0:128] + ds[:, 128:256] + ds[:, 256:384] + ds[:, 384:512]
                    )
            return step

        left, right = (far(far_left_bucket, 0), far(far_right_bucket, 1))

        @pl.loop(0, n_left)
        def _(n):
            left(start + PAD - EDGE - TK, -n * TK)

        @pl.loop(0, n_right)
        def _(n):
            right(start + PAD - EDGE + TK, n * TK)

        total = jnp.zeros((TQ, WIDE), f32)
        for h in range(plan.heads):
            total = jnp.where(lane // 64 == h, acc[h], total)
        dq_ref[out, :] = total.astype(bf16)
        return unused

    lax.fori_loop(0, pair // TQ, tile, 0)
    row = lax.broadcasted_iota(jnp.int32, (EDGE, 3 * EDGE), 0)
    col = lax.broadcasted_iota(jnp.int32, (EDGE, 3 * EDGE), 1)
    bucket = bucket_of(col - EDGE - row)
    for h in range(plan.heads):
        band = near_acc[h, :EDGE, : 3 * EDGE] + near_acc[h, EDGE:, EDGE:]
        extra_right = near_acc[h, :EDGE, 3 * EDGE :]
        extra_left = near_acc[h, EDGE:, :EDGE]
        for b in range(32):
            part = jnp.sum(jnp.where(bucket == b, band, 0.0), axis=0, keepdims=True)
            part = part[:, :128] + part[:, 128:256] + part[:, 256:]
            if b == far_left_bucket:
                part = part + jnp.sum(far_acc[0, h], axis=0, keepdims=True)
                part = part + jnp.sum(extra_left, axis=0, keepdims=True)
            if b == far_right_bucket:
                part = part + jnp.sum(far_acc[1, h], axis=0, keepdims=True)
                part = part + jnp.sum(extra_right, axis=0, keepdims=True)
            tab_ref[h, b : b + 1, :] = part


def dkv_kernel(
    plan, rows, pair, bounds, table_ref, qall_ref, doall_ref, g_ref, kaug_ref, near_ref,
    dk_ref, dv_ref, qp, dop, kh_ref, vh_ref, acc_k, acc_v,
):
    lane = lanes_of(TQ)
    first = lanes_of(1)
    stat = (first >= plan.stat_lane) & (first < plan.stat_lane + 3 * plan.heads)
    qp[:PAD, :] = jnp.broadcast_to(jnp.where(stat, neg_big, 0.0).astype(bf16), (PAD, WIDE))
    qp[pl.ds(PAD + rows, PAD), :] = qp[:PAD, :]
    dop[:PAD, :] = jnp.zeros((PAD, WIDE), bf16)
    dop[pl.ds(PAD + rows, PAD), :] = jnp.zeros((PAD, WIDE), bf16)
    step = 512

    def fill(n, unused):
        at = pl.multiple_of(n * step, step)
        to = pl.multiple_of(PAD + n * step, 128)
        qp[pl.ds(to, step), :] = qall_ref[pl.ds(at, step), :]
        dop[pl.ds(to, step), :] = doall_ref[pl.ds(at, step), :]
        return unused

    lax.fori_loop(0, rows // step, fill, 0)
    low = lanes_of(TQ, 128) < 64
    ones = (lanes_of(TQ, 128) < 3 * plan.heads).astype(bf16)

    def tile(t, unused):
        start = pl.multiple_of(bounds[0] + t * TQ, 128)
        n_left, n_right = (bounds[1 + 2 * t], bounds[2 + 2 * t])
        out = pl.ds(pl.multiple_of(t * TQ, TQ), TQ)
        middle = g_ref[out, 128:256]
        k = jnp.concatenate([g_ref[out, 0:128], jnp.where(low, middle, kaug_ref[out, :])], axis=1)
        v = jnp.concatenate([jnp.where(low, ones, middle), g_ref[out, 256:384]], axis=1)
        near = pl.ds(pl.multiple_of(start + PAD - EDGE, 128), TK)

        def grads(h, s, span):
            p = jnp.exp(s)
            ds = p * nt(vh_ref[h], dop[span, :])
            return nn(p.astype(bf16), dop[span, :]), nn(ds.astype(bf16), qp[span, :])

        for h in range(plan.heads):
            kh_ref[h] = jnp.where(plan.key_lanes(lane, h), k, jnp.zeros_like(k))
            vh_ref[h] = jnp.where(plan.value_lanes(lane, h), v, jnp.zeros_like(v))
            acc_v[h], acc_k[h] = grads(h, nt(kh_ref[h], qp[near, :]) + near_ref[1, h], near)

        def far(bucket):
            def step(first, n):
                span = pl.ds(pl.multiple_of(first + n, 128), TK)
                for h in range(plan.heads):
                    add_v, add_k = grads(
                        h, nt(kh_ref[h], qp[span, :]) + table_ref[bucket, h], span
                    )
                    acc_v[h] += add_v
                    acc_k[h] += add_k
            return step

        left, right = (far(far_right_bucket), far(far_left_bucket))

        @pl.loop(0, n_left)
        def _(n):
            left(start + PAD - EDGE - TK, -n * TK)

        @pl.loop(0, n_right)
        def _(n):
            right(start + PAD - EDGE + TK, n * TK)

        dk = jnp.zeros((TQ, WIDE), f32)
        dv = jnp.zeros((TQ, WIDE), f32)
        mask_grad = jnp.zeros((TQ, 1), f32)
        for h in range(plan.heads):
            dk = jnp.where(lane // 64 == h, acc_k[h], dk)
            dv = jnp.where(lane // 64 == h + 1, acc_v[h], dv)
            mask_grad = mask_grad + acc_k[h][:, plan.mask_lane : plan.mask_lane + 1]
        dk_ref[out, :] = jnp.where(lane == plan.mask_lane, mask_grad, dk)
        dv_ref[out, :] = dv.astype(bf16)
        return unused

    lax.fori_loop(0, pair // TQ, tile, 0)


def grad_attended_kernel(plan, branch_ref, w_ref, wide_ref, do_ref):
    rows = branch_ref.shape[0]
    lane = lanes_of(rows)
    grad = nt(branch_ref[...], w_ref[...]).astype(bf16)
    terms = grad.astype(f32) * wide_ref[...]
    out = grad
    for h in range(plan.heads):
        row_term = jnp.sum(
            jnp.where(lane // 64 == h + 1, terms, 0.0), axis=1, keepdims=True
        )
        for i, part in enumerate(split3(-row_term)):
            out = jnp.where(lane == 3 * h + i, part, out)
    do_ref[...] = out


vmem = pl.BlockSpec(memory_space=pltpu.VMEM)
smem = pl.BlockSpec(memory_space=pltpu.SMEM)


def params():
    return pltpu.CompilerParams(vmem_limit_bytes=56 * 2**20)


class Spot:
    def __init__(self, lines):
        index = lax.axis_index("ctx")
        self.wa = lax.axis_index("wa")
        self.index = index
        self.lines = lines
        self.z = index // 4
        self.x = (index // 2) % 2
        self.core = index % 2

    def core_mate(self):
        return (self.index + 1 - 2 * self.core, self.wa)

    def x_mate(self):
        return (self.index + 2 - 4 * self.x, self.wa)

    def z_mate(self, step):
        return (jnp.clip(self.index + 4 * step, 0, 4 * self.lines - 1), self.wa)

    def y_mate(self):
        return (self.index, 1 - self.wa)


def send(src, dst, send_sem, recv_sem, device):
    return pltpu.make_async_remote_copy(
        src_ref=src,
        dst_ref=dst,
        send_sem=send_sem,
        recv_sem=recv_sem,
        device_id=device,
        device_id_type=pl.DeviceIdType.MESH,
    )


def greet(spot, with_y):
    barrier = pltpu.get_barrier_semaphore()
    mates = [spot.core_mate(), spot.x_mate()] + ([spot.y_mate()] if with_y else [])
    for mate in mates:
        pl.semaphore_signal(barrier, inc=1, device_id=mate, device_id_type=pl.DeviceIdType.MESH)

    @pl.when(spot.z + 1 < spot.lines)
    def _():
        pl.semaphore_signal(
            barrier, inc=1, device_id=spot.z_mate(1), device_id_type=pl.DeviceIdType.MESH
        )

    @pl.when(spot.z > 0)
    def _():
        pl.semaphore_signal(
            barrier, inc=1, device_id=spot.z_mate(-1), device_id_type=pl.DeviceIdType.MESH
        )

    above = (spot.z + 1 < spot.lines).astype(jnp.int32)
    below = (spot.z > 0).astype(jnp.int32)
    pl.semaphore_wait(barrier, len(mates) + above + below)


def added(a, b):
    return (a.astype(f32) + b.astype(f32)).astype(bf16)


def scatter_kernel(lines, units, z_first, *refs):
    count = 3
    parts, outs = (refs[:count], refs[count : 2 * count])
    mine, core_in, x_in, up_in, down_in, load_sem, core_sem, x_sem, up_sem, down_sem = refs[
        2 * count :
    ]
    spot = Spot(lines)
    z, x, core = (spot.z, spot.x, spot.core)
    greet(spot, False)
    loads = []
    cores = []
    order = z_first + [u for u in range(len(units)) if u not in z_first]

    def rows_of(u):
        return pl.ds(units[u][1], units[u][2])

    for u in order:
        m = units[u][0]
        load = pltpu.make_async_copy(
            parts[m].at[:, :, core, rows_of(u)], mine.at[m, :, :, rows_of(u)], load_sem.at[u]
        )
        load.start()
        loads.append(load)
        copy = send(
            parts[m].at[:, :, 1 - core, rows_of(u)],
            core_in.at[m, :, :, rows_of(u)],
            core_sem.at[0, u],
            core_sem.at[1, u],
            spot.core_mate(),
        )
        copy.start()
        cores.append(copy)

    def add_slices(into, source, u, x_slot):
        m = units[u][0]

        def body(line, unused):
            at = (m, line, x_slot, rows_of(u))
            into[at] = added(into[at], source[at])
            return unused

        lax.fori_loop(0, lines, body, 0)

    def x_copy(u, both):
        m = units[u][0]
        if both:
            src = mine.at[m, :, 1 - x, rows_of(u)]
            dst = x_in.at[m, :, rows_of(u)]
        else:
            src = mine.at[m, z, 1 - x, rows_of(u)]
            dst = x_in.at[m, z, rows_of(u)]
        return send(src, dst, x_sem.at[0, u], x_sem.at[1, u], spot.x_mate())

    def line_flow(u, slots):
        m = units[u][0]
        n = len(slots)

        def slot_copies(step, d):
            ring, sem = (up_in, up_sem) if step > 0 else (down_in, down_sem)
            return [
                send(
                    mine.at[m, d, s, rows_of(u)],
                    ring.at[m, d, s, rows_of(u)],
                    sem.at[0, u, d, i],
                    sem.at[1, u, d, i],
                    spot.z_mate(step),
                )
                for i, s in enumerate(slots)
            ]

        def receive(step, d):
            ring = up_in if step > 0 else down_in
            for copy, s in zip(slot_copies(step, d), slots):
                copy.wait_recv()
                at = (m, d, s, rows_of(u))
                mine[at] = added(mine[at], ring[at])

        def ends_first():
            @pl.when(z == 0)
            def _():
                for d in range(lines - 1, 0, -1):
                    for copy in slot_copies(1, d):
                        copy.start()

            @pl.when(z == lines - 1)
            def _():
                for d in range(lines - 1):
                    for copy in slot_copies(-1, d):
                        copy.start()

        def relay():
            def body(k, unused):
                high = lines - 1 - k

                @pl.when((z < high) & (z > 0))
                def _():
                    receive(1, high)
                    for copy in slot_copies(1, high):
                        copy.start()

                @pl.when((z > k) & (z + 1 < lines))
                def _():
                    receive(-1, k)
                    for copy in slot_copies(-1, k):
                        copy.start()

                return unused

            lax.fori_loop(0, lines - 1, body, 0)

        def arrive():
            @pl.when(z > 0)
            def _():
                receive(1, z)

            @pl.when(z + 1 < lines)
            def _():
                receive(-1, z)

        def finish(k, unused):
            @pl.when(z < lines - 1 - k)
            def _():
                for copy in slot_copies(1, lines - 1 - k):
                    copy.wait_send()

            @pl.when(z > k)
            def _():
                for copy in slot_copies(-1, k):
                    copy.wait_send()

            return unused

        return (
            ends_first,
            relay,
            arrive,
            lambda: lax.fori_loop(0, lines - 1, finish, 0),
        )

    def store(u):
        m = units[u][0]
        outs[m][rows_of(u), :] = mine[m, z, x, rows_of(u)].astype(f32)

    pending = {}
    for i, u in enumerate(order):
        loads[i].wait()
        cores[i].wait()
        if u in z_first:
            add_slices(mine, core_in, u, 0)
            add_slices(mine, core_in, u, 1)
        else:
            add_slices(mine, core_in, u, 1 - x)
            copy = x_copy(u, True)
            copy.start()
            pending[u] = copy
            add_slices(mine, core_in, u, x)
    x_first = [u for u in order if u not in z_first]
    flows = {u: line_flow(u, [0, 1] if u in z_first else [x]) for u in order}
    last = {}

    def x_stage(u):
        m = units[u][0]
        pending[u].wait()

        def body(line, unused):
            at = (m, line, x, rows_of(u))
            mine[at] = added(mine[at], x_in[m, line, rows_of(u)])
            return unused

        lax.fori_loop(0, lines, body, 0)

    def settle(u):
        flows[u][2]()
        if u in z_first:
            last[u] = x_copy(u, False)
            last[u].start()
        else:
            store(u)

    for t in range(len(order) + 2):
        if t < len(order):
            u = order[t]
            if u not in z_first:
                x_stage(u)
            flows[u][0]()
        if 0 <= t - 1 < len(order):
            flows[order[t - 1]][1]()
        if 0 <= t - 2 < len(order):
            settle(order[t - 2])
    for u, copy in last.items():
        m = units[u][0]
        copy.wait()
        at = (m, z, x, rows_of(u))
        mine[at] = added(mine[at], x_in[m, z, rows_of(u)])
        store(u)
    for u in order:
        flows[u][3]()


def reduce_scatter(parts, cycle_size):
    lines = cycle_size // 4
    units_here, model = parts[0].shape
    rows = units_here // cycle_size
    cut = (rows // 2 + 15) // 16 * 16
    pieces = [(0, cut), (cut, rows - cut)] if cut < rows else [(0, rows)]
    units = [(m, at, size) for m in range(3) for at, size in pieces]
    z_first = [len(units) - 1]
    shaped = [part.reshape(lines, 2, 2, rows, model) for part in parts]
    hbm = pl.BlockSpec(memory_space=pl.ANY)
    n = len(units)
    return pl.pallas_call(
        functools.partial(scatter_kernel, lines, units, z_first),
        out_shape=[jax.ShapeDtypeStruct((rows, model), f32)] * 3,
        in_specs=[hbm] * 3,
        out_specs=[vmem] * 3,
        scratch_shapes=[
            pltpu.VMEM((3, lines, 2, rows, model), bf16),
            pltpu.VMEM((3, lines, 2, rows, model), bf16),
            pltpu.VMEM((3, lines, rows, model), bf16),
            pltpu.VMEM((3, lines, 2, rows, model), bf16),
            pltpu.VMEM((3, lines, 2, rows, model), bf16),
            pltpu.SemaphoreType.DMA((n,)),
            pltpu.SemaphoreType.DMA((2, n)),
            pltpu.SemaphoreType.DMA((2, n)),
            pltpu.SemaphoreType.DMA((2, n, lines, 2)),
            pltpu.SemaphoreType.DMA((2, n, lines, 2)),
        ],
        compiler_params=pltpu.CompilerParams(
            vmem_limit_bytes=58 * 2**20, collective_id=1, has_side_effects=True
        ),
        name="weight_scatter",
    )(*shaped)


def shards(
    tokens,
    doc_lengths,
    key_mask,
    gain_attn,
    w_query,
    w_key,
    w_value,
    w_out,
    bias_table,
    gain_ffn,
    w_gate,
    w_up,
    w_down,
    cotangent,
):
    own_rows, model = tokens.shape
    group = lax.axis_size("wa")
    cycle_size = lax.axis_size("ctx")
    pair = own_rows * group
    heads = bias_table.shape[1]
    docs = doc_lengths.shape[0]
    plan = Plan(heads, w_query.shape[1] // heads, docs)
    total_rows = pair * cycle_size
    doc_most = min(MAXLEN, total_rows // 2)
    reach = min(cycle_size - 1, (doc_most - 1) // pair + 1)
    base = lax.axis_index("ctx") * pair
    rows = min(total_rows, (2 * reach + 1) * pair)
    origin = jnp.clip(base - reach * pair, 0, total_rows - rows).astype(jnp.int32)
    ends = jnp.cumsum(doc_lengths).astype(jnp.int32)
    starts = ends - doc_lengths

    def doc_at(positions):
        return jnp.sum((positions[:, None] >= starts[None, :]).astype(jnp.int32), axis=1) - 1

    tiles = pair // TQ
    tile_start = base + TQ * jnp.arange(tiles, dtype=jnp.int32)
    first_doc = jnp.arange(docs, dtype=jnp.int32)[None, :] == doc_at(tile_start)[:, None]
    last_doc = jnp.arange(docs, dtype=jnp.int32)[None, :] == doc_at(tile_start + TQ - 1)[:, None]
    low_end = jnp.sum(jnp.where(first_doc, starts[None, :], 0), axis=1)
    high_end = jnp.sum(jnp.where(last_doc, ends[None, :], 0), axis=1)
    n_left = jnp.maximum(0, (tile_start - EDGE - low_end + TK - 1) // TK)
    n_right = jnp.maximum(0, (high_end - (tile_start - EDGE + TK) + TK - 1) // TK)
    bounds = jnp.concatenate(
        [(base - origin)[None], jnp.stack([n_left, n_right], axis=1).reshape(-1)]
    ).astype(jnp.int32)

    mask_all = lax.all_gather(key_mask, "ctx", axis=0, tiled=True)
    tokens_wide = tokens.astype(f32)
    normed_attn, inv_attn = norm_forward(tokens_wide, gain_attn)
    normed_low = normed_attn.astype(bf16)
    pair_normed, pair_cot = (
        lax.all_gather(normed_low, "wa", axis=0, tiled=True),
        lax.all_gather(cotangent, "wa", axis=0, tiled=True),
    )
    w_kv = jnp.concatenate([w_key, w_value], axis=1)
    own_kv = jnp.dot(pair_normed, w_kv, preferred_element_type=f32).astype(bf16)
    queries = jnp.dot(pair_normed, w_query, preferred_element_type=f32).astype(bf16)

    def window(gathered):
        if rows == total_rows:
            return gathered
        return lax.dynamic_slice_in_dim(gathered, origin, rows, 0)

    gather = functools.partial(lax.all_gather, axis_name="ctx", axis=0, tiled=True)
    kv_all = window(gather(own_kv))
    positions = origin + jnp.arange(rows, dtype=jnp.int32)
    doc_of = doc_at(positions)
    lane = jnp.arange(128, dtype=jnp.int32)[None, :] + 128
    code = lane - plan.doc_lane
    bit_differs = ((doc_of[:, None] >> (code >> 1)) & 1) != (code & 1)
    k_aug = jnp.where(
        lane == plan.mask_lane,
        window(mask_all).astype(f32)[:, None],
        jnp.where(
            lane < plan.stat_lane,
            jnp.where(bit_differs & (code >= 0), neg_big, 0.0),
            (lane < plan.stat_lane + 3 * heads).astype(f32),
        ),
    ).astype(bf16)
    own_docs = doc_at(base + jnp.arange(pair, dtype=jnp.int32))
    own_differs = ((own_docs[:, None] >> (code >> 1)) & 1) != (code & 1)
    q_aug = jnp.where(
        lane == plan.mask_lane, 1.0, ((lane < plan.stat_lane) & ~own_differs).astype(f32)
    ).astype(bf16)
    q_wide = jnp.concatenate(
        [queries, q_aug[:, plan.cols - 128 :]], axis=1
    )
    near_bias = pl.pallas_call(
        functools.partial(near_kernel, heads),
        out_shape=jax.ShapeDtypeStruct((2, heads, TQ, TK), f32),
        in_specs=[smem],
        out_specs=vmem,
        compiler_params=params(),
        name="near_bias",
    )(bias_table)

    padded = rows + 2 * PAD
    attended, mixed, q_back = pl.pallas_call(
        functools.partial(fwd_kernel, plan, rows, pair),
        out_shape=(
            jax.ShapeDtypeStruct((pair, WIDE), bf16),
            jax.ShapeDtypeStruct((pair, WIDE), f32),
            jax.ShapeDtypeStruct((pair, WIDE), bf16),
        ),
        in_specs=[smem, smem, vmem, vmem, vmem, vmem],
        out_specs=(vmem, vmem, vmem),
        scratch_shapes=[
            pltpu.VMEM((padded, WIDE), bf16),
            pltpu.VMEM((padded, WIDE), bf16),
            pltpu.VMEM((heads, TQ, WIDE), f32),
            pltpu.VMEM((heads, TQ, 128), f32),
            pltpu.VMEM((heads, TQ, WIDE), bf16),
        ],
        compiler_params=params(),
        name="attention_forward",
    )(bounds, bias_table, kv_all, k_aug, q_wide, near_bias)
    q_all = window(gather(q_back))
    w_out_pad = jnp.concatenate([jnp.zeros((64, model), bf16), w_out], axis=0)
    branch = lax.psum_scatter(
        jnp.dot(attended, w_out_pad, preferred_element_type=f32).astype(bf16),
        "wa",
        scatter_dimension=0,
        tiled=True,
    ).astype(f32)
    hidden = tokens_wide + branch
    normed_ffn, inv_ffn = norm_forward(hidden, gain_ffn)
    ffn_low = normed_ffn.astype(bf16)
    pair_ffn = lax.all_gather(ffn_low, "wa", axis=0, tiled=True)
    gate = jnp.dot(pair_ffn, w_gate, preferred_element_type=f32)
    upward = jnp.dot(pair_ffn, w_up, preferred_element_type=f32)
    inner = gated(gate, upward).astype(bf16)
    ffn_part = jnp.dot(inner, w_down, preferred_element_type=f32)
    layer_out = (
        hidden
        + lax.psum_scatter(
            ffn_part.astype(bf16), "wa", scatter_dimension=0, tiled=True
        ).astype(f32)
    ).astype(bf16)
    grad_inner = jnp.dot(pair_cot, w_down.T, preferred_element_type=f32)
    down_half = jnp.dot(inner.T, pair_cot, preferred_element_type=f32).astype(bf16)
    unused_value, pullback = jax.vjp(gated, gate, upward)
    grad_gate, grad_upward = pullback(grad_inner)
    grad_gate = grad_gate.astype(bf16)
    grad_upward = grad_upward.astype(bf16)
    grad_pair_ffn = jnp.dot(grad_gate, w_gate.T, preferred_element_type=f32) + jnp.dot(
        grad_upward, w_up.T, preferred_element_type=f32
    )
    grad_normed_ffn = lax.psum_scatter(
        grad_pair_ffn.astype(bf16), "wa", scatter_dimension=0, tiled=True
    ).astype(f32)
    gate_half = jnp.dot(grad_gate.T, pair_ffn, preferred_element_type=f32).astype(bf16)
    up_half = jnp.dot(grad_upward.T, pair_ffn, preferred_element_type=f32).astype(bf16)
    grad_w_down, grad_w_gate, grad_w_up = reduce_scatter(
        [down_half, gate_half, up_half], cycle_size
    )
    grad_w_gate, grad_w_up = (grad_w_gate.T, grad_w_up.T)
    hidden_step, gain_ffn_part = norm_backward(hidden, inv_ffn, gain_ffn, grad_normed_ffn)
    grad_hidden = cotangent.astype(f32) + hidden_step
    pair_branch = lax.all_gather(grad_hidden.astype(bf16), "wa", axis=0, tiled=True)
    out_part = jnp.dot(attended.T, pair_branch, preferred_element_type=f32)[64:]
    do_wide = pl.pallas_call(
        functools.partial(grad_attended_kernel, plan),
        out_shape=jax.ShapeDtypeStruct((pair, WIDE), bf16),
        in_specs=[vmem, vmem, vmem],
        out_specs=vmem,
        compiler_params=params(),
        name="grad_attended",
    )(pair_branch, w_out_pad, mixed)
    do_all = window(gather(do_wide))

    grad_queries, table_part = pl.pallas_call(
        functools.partial(dq_kernel, plan, rows, pair),
        out_shape=(
            jax.ShapeDtypeStruct((pair, WIDE), bf16),
            jax.ShapeDtypeStruct((heads, 32, 128), f32),
        ),
        in_specs=[smem, smem, vmem, vmem, vmem, vmem, vmem],
        out_specs=(vmem, vmem),
        scratch_shapes=[
            pltpu.VMEM((padded, WIDE), bf16),
            pltpu.VMEM((padded, WIDE), bf16),
            pltpu.VMEM((heads, TQ, WIDE), f32),
            pltpu.VMEM((heads, TQ, WIDE), bf16),
            pltpu.VMEM((heads, TQ, WIDE), bf16),
            pltpu.VMEM((heads, TQ, TK), f32),
            pltpu.VMEM((2, heads, TQ, 128), f32),
        ],
        compiler_params=params(),
        name="attention_grad_queries",
    )(bounds, bias_table, kv_all, k_aug, q_back, do_wide, near_bias)
    own_aug = lax.dynamic_slice_in_dim(k_aug, base - origin, pair, 0)
    grad_keys, grad_values = pl.pallas_call(
        functools.partial(dkv_kernel, plan, rows, pair),
        out_shape=(
            jax.ShapeDtypeStruct((pair, WIDE), f32),
            jax.ShapeDtypeStruct((pair, WIDE), bf16),
        ),
        in_specs=[smem, smem, vmem, vmem, vmem, vmem, vmem],
        out_specs=(vmem, vmem),
        scratch_shapes=[
            pltpu.VMEM((padded, WIDE), bf16),
            pltpu.VMEM((padded, WIDE), bf16),
            pltpu.VMEM((heads, TQ, WIDE), bf16),
            pltpu.VMEM((heads, TQ, WIDE), bf16),
            pltpu.VMEM((heads, TQ, WIDE), f32),
            pltpu.VMEM((heads, TQ, WIDE), f32),
        ],
        compiler_params=params(),
        name="attention_grad_keys",
    )(bounds, bias_table, q_all, do_all, own_kv, own_aug, near_bias)
    grad_tab = jnp.sum(table_part, axis=2).T
    mask_total = grad_keys[:, plan.mask_lane]
    cols = plan.cols
    grad_qkv = jnp.concatenate(
        [grad_queries[:, :cols], grad_keys[:, :cols].astype(bf16), grad_values[:, 64:]], axis=1
    )
    w_qkv = jnp.concatenate([w_query, w_key, w_value], axis=1)
    qkv_part = jnp.dot(pair_normed.T, grad_qkv, preferred_element_type=f32)
    grad_pair = jnp.dot(grad_qkv, w_qkv.T, preferred_element_type=f32)
    grad_normed_attn, grad_mask = (
        lax.psum_scatter(
            grad_pair.astype(bf16), "wa", scatter_dimension=0, tiled=True
        ).astype(f32),
        lax.psum_scatter(
            mask_total.astype(bf16), "wa", scatter_dimension=0, tiled=True
        ).astype(f32),
    )
    token_step, gain_attn_part = norm_backward(tokens_wide, inv_attn, gain_attn, grad_normed_attn)
    grad_tokens = grad_hidden + token_step
    grad_gain_attn, grad_gain_ffn = lax.psum((gain_attn_part, gain_ffn_part), ("ctx", "wa"))
    grad_w_qkv, grad_w_out, grad_table = lax.psum((qkv_part, out_part, grad_tab), "ctx")
    return (
        layer_out,
        grad_tokens,
        grad_mask,
        grad_gain_attn,
        grad_w_qkv[:, :cols],
        grad_w_qkv[:, cols : 2 * cols],
        grad_w_qkv[:, 2 * cols :],
        grad_w_out,
        grad_table,
        grad_gain_ffn,
        grad_w_gate,
        grad_w_up,
        grad_w_down,
    )


def solution(mesh):
    placed = (
        P(("ctx", "wa"), None),
        P(),
        P("ctx"),
        P(),
        P(None, "wa"),
        P(None, "wa"),
        P(None, "wa"),
        P("wa", None),
        P(None, "wa"),
        P(),
        P(None, "wa"),
        P(None, "wa"),
        P("wa", None),
        P(("ctx", "wa"), None),
    )
    return jax.shard_map(
        shards,
        mesh=mesh,
        in_specs=placed,
        out_specs=(
            P(("ctx", "wa"), None),
            P(("ctx", "wa"), None),
            P(("ctx", "wa")),
            P(),
            P(None, "wa"),
            P(None, "wa"),
            P(None, "wa"),
            P("wa", None),
            P(None, "wa"),
            P(),
            P(None, ("wa", "ctx")),
            P(None, ("wa", "ctx")),
            P(("wa", "ctx"), None),
        ),
        check_vma=False,
    )
```

```python
import functools

import jax
import jax.numpy as jnp
from jax import lax
from jax.experimental import pallas as pl
from jax.experimental.pallas import tpu as pltpu
from jax.sharding import PartitionSpec as P

MAXLEN = 8192

bucket_edges = (12, 16, 23, 32, 46, 64, 91)
neg_big = -1e30
eps = 1e-06
far_left_bucket = 15
far_right_bucket = 31
WIDE = 256
TQ = 256
TK = 512
EDGE = 128
PAD = TK + EDGE
f32 = jnp.float32
bf16 = jnp.bfloat16


def bucket_of(relative):
    distance = jnp.abs(relative)
    bucket = jnp.minimum(distance, 8) + 16 * (relative > 0).astype(jnp.int32)
    for edge in bucket_edges:
        bucket = bucket + (distance >= edge).astype(jnp.int32)
    return bucket


def norm_forward(inputs, gain):
    inv_root = lax.rsqrt(jnp.mean(inputs * inputs, axis=-1, keepdims=True) + eps)
    return (inputs * inv_root * gain, inv_root)


def norm_backward(inputs, inv_root, gain, grad_normed):
    scaled = gain * grad_normed
    cubed = inv_root * inv_root * inv_root
    grad_inputs = inv_root * scaled - inputs * cubed * jnp.mean(
        inputs * scaled, axis=-1, keepdims=True
    )
    grad_gain = jnp.sum(grad_normed * inputs * inv_root, axis=0)
    return (grad_inputs, grad_gain)


def gated(gate, upward):
    return jax.nn.gelu(gate, approximate=True) * upward


def nt(a, b):
    return lax.dot_general(a, b, (((1,), (1,)), ((), ())), preferred_element_type=f32)


def nn(a, b):
    return lax.dot_general(a, b, (((1,), (0,)), ((), ())), preferred_element_type=f32)


def split3(x):
    hi = x.astype(bf16)
    rest = x - hi.astype(f32)
    mid = rest.astype(bf16)
    return (hi, mid, (rest - mid.astype(f32)).astype(bf16))


class Plan:
    def __init__(self, heads, width, docs):
        self.heads = heads
        self.width = width
        self.bits = max(1, (docs - 1).bit_length())
        self.cols = heads * width
        self.mask_lane = self.cols
        self.doc_lane = self.cols + 1
        self.stat_lane = self.doc_lane + 2 * self.bits
        assert self.stat_lane + 3 * heads <= WIDE and self.cols + 64 == WIDE and width == 64

    def key_lanes(self, lane, h):
        own = (lane >= h * self.width) & (lane < (h + 1) * self.width)
        aug = (lane >= self.mask_lane) & (lane < self.stat_lane)
        stat = (lane >= self.stat_lane + 3 * h) & (lane < self.stat_lane + 3 * h + 3)
        return own | aug | stat

    def value_lanes(self, lane, h):
        own = (lane >= 64 + h * self.width) & (lane < 64 + (h + 1) * self.width)
        return own | ((lane >= 3 * h) & (lane < 3 * h + 3))


def lanes_of(rows, width=WIDE):
    return lax.broadcasted_iota(jnp.int32, (rows, width), 1)


def near_kernel(heads, table_ref, near_ref):
    row = lax.broadcasted_iota(jnp.int32, (EDGE, 3 * EDGE), 0)
    col = lax.broadcasted_iota(jnp.int32, (EDGE, 3 * EDGE), 1)
    relative = col - EDGE - row
    for flip in range(2):
        bucket = bucket_of(-relative if flip else relative)
        left, right = (far_left_bucket, far_right_bucket)
        if flip:
            left, right = (right, left)
        for h in range(heads):
            base = jnp.full((EDGE, 3 * EDGE), table_ref[0, h], f32)
            for b in range(1, 32):
                base = jnp.where(bucket == b, table_ref[b, h], base)
            far_l = jnp.full((EDGE, EDGE), table_ref[left, h], f32)
            far_r = jnp.full((EDGE, EDGE), table_ref[right, h], f32)
            near_ref[flip, h, :EDGE, : 3 * EDGE] = base
            near_ref[flip, h, :EDGE, 3 * EDGE :] = far_r
            near_ref[flip, h, EDGE:, EDGE:] = base
            near_ref[flip, h, EDGE:, :EDGE] = far_l


def build_keys(plan, g_ref, kaug_ref, km, vm, rows):
    km[:PAD, :] = jnp.broadcast_to(
        jnp.where(pad_lanes(plan), neg_big, 0.0).astype(bf16), (PAD, WIDE)
    )
    km[pl.ds(PAD + rows, PAD), :] = km[:PAD, :]
    vm[:PAD, :] = jnp.zeros((PAD, WIDE), bf16)
    vm[pl.ds(PAD + rows, PAD), :] = jnp.zeros((PAD, WIDE), bf16)
    step = 512
    low = lanes_of(step, 128) < 64
    ones = (lanes_of(step, 128) < 3 * plan.heads).astype(bf16)

    def body(n, unused):
        at = pl.multiple_of(n * step, step)
        to = pl.multiple_of(PAD + n * step, 128)
        middle = g_ref[pl.ds(at, step), 128:256]
        km[pl.ds(to, step), 0:128] = g_ref[pl.ds(at, step), 0:128]
        km[pl.ds(to, step), 128:256] = jnp.where(low, middle, kaug_ref[pl.ds(at, step), :])
        vm[pl.ds(to, step), 0:128] = jnp.where(low, ones, middle)
        vm[pl.ds(to, step), 128:256] = g_ref[pl.ds(at, step), 256:384]
        return unused

    lax.fori_loop(0, rows // step, body, 0)


def pad_lanes(plan):
    lane = lanes_of(1)
    return (lane >= plan.doc_lane) & (lane < plan.stat_lane)


def fwd_kernel(
    plan, rows, pair, bounds, table_ref, g_ref, kaug_ref, q_ref, near_ref,
    low_ref, wide_ref, qb_ref, km, vm, acc, row_max, qh_ref,
):
    build_keys(plan, g_ref, kaug_ref, km, vm, rows)
    lane = lanes_of(TQ)

    def tile(t, unused):
        start = pl.multiple_of(bounds[0] + t * TQ, 128)
        n_left, n_right = (bounds[1 + 2 * t], bounds[2 + 2 * t])
        out = pl.ds(pl.multiple_of(t * TQ, TQ), TQ)
        q = q_ref[out, :]
        near = pl.ds(pl.multiple_of(start + PAD - EDGE, 128), TK)
        for h in range(plan.heads):
            qh = jnp.where(plan.key_lanes(lane, h), q, jnp.zeros_like(q))
            qh_ref[h] = qh
            s = nt(qh, km[near, :]) + near_ref[0, h]
            top = jnp.max(s, axis=1, keepdims=True)
            p = jnp.exp(s - top).astype(bf16)
            acc[h] = nn(p, vm[near, :])
            row_max[h] = jnp.broadcast_to(top, (TQ, 128))

        def far(bucket):
            def step(first, n):
                span = pl.ds(pl.multiple_of(first + n, 128), TK)
                for h in range(plan.heads):
                    s = nt(qh_ref[h], km[span, :])
                    offset = table_ref[bucket, h]
                    old = row_max[h][:, :1]
                    top = jnp.maximum(old, jnp.max(s, axis=1, keepdims=True) + offset)
                    p = jnp.exp(s - (top - offset)).astype(bf16)
                    acc[h] = acc[h] * jnp.exp(old - top) + nn(p, vm[span, :])
                    row_max[h] = jnp.broadcast_to(top, (TQ, 128))
            return step

        left, right = (far(far_left_bucket), far(far_right_bucket))

        @pl.loop(0, n_left)
        def _(n):
            left(start + PAD - EDGE - TK, -n * TK)

        @pl.loop(0, n_right)
        def _(n):
            right(start + PAD - EDGE + TK, n * TK)

        wide = jnp.zeros((TQ, WIDE), f32)
        qb = jnp.where(lane < plan.stat_lane, q, jnp.zeros_like(q))
        for h in range(plan.heads):
            total = acc[h][:, 3 * h : 3 * h + 1]
            log_total = row_max[h][:, :1] + jnp.log(total)
            wide = jnp.where(lane // 64 == h + 1, acc[h] / total, wide)
            for i, part in enumerate(split3(-log_total)):
                qb = jnp.where(lane == plan.stat_lane + 3 * h + i, part, qb)
        wide_ref[out, :] = wide
        low_ref[out, :] = wide.astype(bf16)
        qb_ref[out, :] = qb
        return unused

    lax.fori_loop(0, pair // TQ, tile, 0)


def dq_kernel(
    plan, rows, pair, bounds, table_ref, g_ref, kaug_ref, qb_ref, do_ref, near_ref,
    dq_ref, tab_ref, km, vm, acc, qh_ref, doh_ref, near_acc, far_acc,
):
    build_keys(plan, g_ref, kaug_ref, km, vm, rows)
    lane = lanes_of(TQ)
    near_acc[...] = jnp.zeros_like(near_acc)
    far_acc[...] = jnp.zeros_like(far_acc)

    def tile(t, unused):
        start = pl.multiple_of(bounds[0] + t * TQ, 128)
        n_left, n_right = (bounds[1 + 2 * t], bounds[2 + 2 * t])
        out = pl.ds(pl.multiple_of(t * TQ, TQ), TQ)
        q = qb_ref[out, :]
        do = do_ref[out, :]
        near = pl.ds(pl.multiple_of(start + PAD - EDGE, 128), TK)

        def grads(h, s, span):
            p = jnp.exp(s)
            return p * nt(doh_ref[h], vm[span, :])

        for h in range(plan.heads):
            qh_ref[h] = jnp.where(plan.key_lanes(lane, h), q, jnp.zeros_like(q))
            doh_ref[h] = jnp.where(plan.value_lanes(lane, h), do, jnp.zeros_like(do))
            ds = grads(h, nt(qh_ref[h], km[near, :]) + near_ref[0, h], near)
            near_acc[h] += ds
            acc[h] = nn(ds.astype(bf16), km[near, :])

        def far(bucket, slot):
            def step(first, n):
                span = pl.ds(pl.multiple_of(first + n, 128), TK)
                for h in range(plan.heads):
                    ds = grads(h, nt(qh_ref[h], km[span, :]) + table_ref[bucket, h], span)
                    acc[h] += nn(ds.astype(bf16), km[span, :])
                    far_acc[slot, h] += (
                        ds[:, 0:128] + ds[:, 128:256] + ds[:, 256:384] + ds[:, 384:512]
                    )
            return step

        left, right = (far(far_left_bucket, 0), far(far_right_bucket, 1))

        @pl.loop(0, n_left)
        def _(n):
            left(start + PAD - EDGE - TK, -n * TK)

        @pl.loop(0, n_right)
        def _(n):
            right(start + PAD - EDGE + TK, n * TK)

        total = jnp.zeros((TQ, WIDE), f32)
        for h in range(plan.heads):
            total = jnp.where(lane // 64 == h, acc[h], total)
        dq_ref[out, :] = total.astype(bf16)
        return unused

    lax.fori_loop(0, pair // TQ, tile, 0)
    row = lax.broadcasted_iota(jnp.int32, (EDGE, 3 * EDGE), 0)
    col = lax.broadcasted_iota(jnp.int32, (EDGE, 3 * EDGE), 1)
    bucket = bucket_of(col - EDGE - row)
    for h in range(plan.heads):
        band = near_acc[h, :EDGE, : 3 * EDGE] + near_acc[h, EDGE:, EDGE:]
        extra_right = near_acc[h, :EDGE, 3 * EDGE :]
        extra_left = near_acc[h, EDGE:, :EDGE]
        for b in range(32):
            part = jnp.sum(jnp.where(bucket == b, band, 0.0), axis=0, keepdims=True)
            part = part[:, :128] + part[:, 128:256] + part[:, 256:]
            if b == far_left_bucket:
                part = part + jnp.sum(far_acc[0, h], axis=0, keepdims=True)
                part = part + jnp.sum(extra_left, axis=0, keepdims=True)
            if b == far_right_bucket:
                part = part + jnp.sum(far_acc[1, h], axis=0, keepdims=True)
                part = part + jnp.sum(extra_right, axis=0, keepdims=True)
            tab_ref[h, b : b + 1, :] = part


def dkv_kernel(
    plan, rows, pair, bounds, table_ref, qall_ref, doall_ref, g_ref, kaug_ref, near_ref,
    dk_ref, dv_ref, mask_ref, qp, dop, kh_ref, vh_ref, acc_k, acc_v,
):
    lane = lanes_of(TQ)
    first = lanes_of(1)
    stat = (first >= plan.stat_lane) & (first < plan.stat_lane + 3 * plan.heads)
    qp[:PAD, :] = jnp.broadcast_to(jnp.where(stat, neg_big, 0.0).astype(bf16), (PAD, WIDE))
    qp[pl.ds(PAD + rows, PAD), :] = qp[:PAD, :]
    dop[:PAD, :] = jnp.zeros((PAD, WIDE), bf16)
    dop[pl.ds(PAD + rows, PAD), :] = jnp.zeros((PAD, WIDE), bf16)
    step = 512

    def fill(n, unused):
        at = pl.multiple_of(n * step, step)
        to = pl.multiple_of(PAD + n * step, 128)
        qp[pl.ds(to, step), :] = qall_ref[pl.ds(at, step), :]
        dop[pl.ds(to, step), :] = doall_ref[pl.ds(at, step), :]
        return unused

    lax.fori_loop(0, rows // step, fill, 0)
    low = lanes_of(TQ, 128) < 64
    ones = (lanes_of(TQ, 128) < 3 * plan.heads).astype(bf16)

    def tile(t, unused):
        start = pl.multiple_of(bounds[0] + t * TQ, 128)
        n_left, n_right = (bounds[1 + 2 * t], bounds[2 + 2 * t])
        out = pl.ds(pl.multiple_of(t * TQ, TQ), TQ)
        middle = g_ref[out, 128:256]
        k = jnp.concatenate([g_ref[out, 0:128], jnp.where(low, middle, kaug_ref[out, :])], axis=1)
        v = jnp.concatenate([jnp.where(low, ones, middle), g_ref[out, 256:384]], axis=1)
        near = pl.ds(pl.multiple_of(start + PAD - EDGE, 128), TK)

        def grads(h, s, span):
            p = jnp.exp(s)
            ds = p * nt(vh_ref[h], dop[span, :])
            return nn(p.astype(bf16), dop[span, :]), nn(ds.astype(bf16), qp[span, :])

        for h in range(plan.heads):
            kh_ref[h] = jnp.where(plan.key_lanes(lane, h), k, jnp.zeros_like(k))
            vh_ref[h] = jnp.where(plan.value_lanes(lane, h), v, jnp.zeros_like(v))
            acc_v[h], acc_k[h] = grads(h, nt(kh_ref[h], qp[near, :]) + near_ref[1, h], near)

        def far(bucket):
            def step(first, n):
                span = pl.ds(pl.multiple_of(first + n, 128), TK)
                for h in range(plan.heads):
                    add_v, add_k = grads(
                        h, nt(kh_ref[h], qp[span, :]) + table_ref[bucket, h], span
                    )
                    acc_v[h] += add_v
                    acc_k[h] += add_k
            return step

        left, right = (far(far_right_bucket), far(far_left_bucket))

        @pl.loop(0, n_left)
        def _(n):
            left(start + PAD - EDGE - TK, -n * TK)

        @pl.loop(0, n_right)
        def _(n):
            right(start + PAD - EDGE + TK, n * TK)

        dk = jnp.zeros((TQ, WIDE), f32)
        dv = jnp.zeros((TQ, WIDE), f32)
        mask_grad = jnp.zeros((TQ, 1), f32)
        for h in range(plan.heads):
            dk = jnp.where(lane // 64 == h, acc_k[h], dk)
            dv = jnp.where(lane // 64 == h + 1, acc_v[h], dv)
            mask_grad = mask_grad + acc_k[h][:, plan.mask_lane : plan.mask_lane + 1]
        mask_ref[t] = jnp.transpose(jnp.broadcast_to(mask_grad, (TQ, 128)))[:8, :]
        dk_ref[out, :] = dk.astype(bf16)
        dv_ref[out, :] = dv.astype(bf16)
        return unused

    lax.fori_loop(0, pair // TQ, tile, 0)


def grad_attended_kernel(plan, branch_ref, w_ref, wide_ref, do_ref):
    rows = branch_ref.shape[0]
    lane = lanes_of(rows)
    grad = nt(branch_ref[...], w_ref[...]).astype(bf16)
    terms = grad.astype(f32) * wide_ref[...]
    out = grad
    for h in range(plan.heads):
        row_term = jnp.sum(
            jnp.where(lane // 64 == h + 1, terms, 0.0), axis=1, keepdims=True
        )
        for i, part in enumerate(split3(-row_term)):
            out = jnp.where(lane == 3 * h + i, part, out)
    do_ref[...] = out


vmem = pl.BlockSpec(memory_space=pltpu.VMEM)
smem = pl.BlockSpec(memory_space=pltpu.SMEM)


def params():
    return pltpu.CompilerParams(vmem_limit_bytes=56 * 2**20)


class Spot:
    def __init__(self, lines):
        index = lax.axis_index("ctx")
        self.wa = lax.axis_index("wa")
        self.index = index
        self.lines = lines
        self.z = index // 4
        self.x = (index // 2) % 2
        self.core = index % 2

    def core_mate(self):
        return (self.index + 1 - 2 * self.core, self.wa)

    def x_mate(self):
        return (self.index + 2 - 4 * self.x, self.wa)

    def z_mate(self, step):
        return (jnp.clip(self.index + 4 * step, 0, 4 * self.lines - 1), self.wa)

    def y_mate(self):
        return (self.index, 1 - self.wa)


def send(src, dst, send_sem, recv_sem, device):
    return pltpu.make_async_remote_copy(
        src_ref=src,
        dst_ref=dst,
        send_sem=send_sem,
        recv_sem=recv_sem,
        device_id=device,
        device_id_type=pl.DeviceIdType.MESH,
    )


def greet(spot, with_y):
    barrier = pltpu.get_barrier_semaphore()
    mates = [spot.core_mate(), spot.x_mate()] + ([spot.y_mate()] if with_y else [])
    for mate in mates:
        pl.semaphore_signal(barrier, inc=1, device_id=mate, device_id_type=pl.DeviceIdType.MESH)

    @pl.when(spot.z + 1 < spot.lines)
    def _():
        pl.semaphore_signal(
            barrier, inc=1, device_id=spot.z_mate(1), device_id_type=pl.DeviceIdType.MESH
        )

    @pl.when(spot.z > 0)
    def _():
        pl.semaphore_signal(
            barrier, inc=1, device_id=spot.z_mate(-1), device_id_type=pl.DeviceIdType.MESH
        )

    above = (spot.z + 1 < spot.lines).astype(jnp.int32)
    below = (spot.z > 0).astype(jnp.int32)
    pl.semaphore_wait(barrier, len(mates) + above + below)


def added(a, b):
    return (a.astype(f32) + b.astype(f32)).astype(bf16)


def scatter_kernel(lines, units, z_first, *refs):
    count = 3
    parts, outs = (refs[:count], refs[count : 2 * count])
    mine, core_in, x_in, up_in, down_in, load_sem, core_sem, x_sem, up_sem, down_sem = refs[
        2 * count :
    ]
    spot = Spot(lines)
    z, x, core = (spot.z, spot.x, spot.core)
    greet(spot, False)
    loads = []
    cores = []
    order = z_first + [u for u in range(len(units)) if u not in z_first]

    def rows_of(u):
        return pl.ds(units[u][1], units[u][2])

    for u in order:
        m = units[u][0]
        load = pltpu.make_async_copy(
            parts[m].at[:, :, core, rows_of(u)], mine.at[m, :, :, rows_of(u)], load_sem.at[u]
        )
        load.start()
        loads.append(load)
        copy = send(
            parts[m].at[:, :, 1 - core, rows_of(u)],
            core_in.at[m, :, :, rows_of(u)],
            core_sem.at[0, u],
            core_sem.at[1, u],
            spot.core_mate(),
        )
        copy.start()
        cores.append(copy)

    def add_slices(into, source, u, x_slot):
        m = units[u][0]

        def body(line, unused):
            at = (m, line, x_slot, rows_of(u))
            into[at] = added(into[at], source[at])
            return unused

        lax.fori_loop(0, lines, body, 0)

    def x_copy(u, both):
        m = units[u][0]
        if both:
            src = mine.at[m, :, 1 - x, rows_of(u)]
            dst = x_in.at[m, :, rows_of(u)]
        else:
            src = mine.at[m, z, 1 - x, rows_of(u)]
            dst = x_in.at[m, z, rows_of(u)]
        return send(src, dst, x_sem.at[0, u], x_sem.at[1, u], spot.x_mate())

    def line_flow(u, slots):
        m = units[u][0]
        n = len(slots)

        def slot_copies(step, d):
            ring, sem = (up_in, up_sem) if step > 0 else (down_in, down_sem)
            return [
                send(
                    mine.at[m, d, s, rows_of(u)],
                    ring.at[m, d, s, rows_of(u)],
                    sem.at[0, u, d, i],
                    sem.at[1, u, d, i],
                    spot.z_mate(step),
                )
                for i, s in enumerate(slots)
            ]

        def receive(step, d):
            ring = up_in if step > 0 else down_in
            for copy, s in zip(slot_copies(step, d), slots):
                copy.wait_recv()
                at = (m, d, s, rows_of(u))
                mine[at] = added(mine[at], ring[at])

        def ends_first():
            @pl.when(z == 0)
            def _():
                for d in range(lines - 1, 0, -1):
                    for copy in slot_copies(1, d):
                        copy.start()

            @pl.when(z == lines - 1)
            def _():
                for d in range(lines - 1):
                    for copy in slot_copies(-1, d):
                        copy.start()

        def relay():
            def body(k, unused):
                high = lines - 1 - k

                @pl.when((z < high) & (z > 0))
                def _():
                    receive(1, high)
                    for copy in slot_copies(1, high):
                        copy.start()

                @pl.when((z > k) & (z + 1 < lines))
                def _():
                    receive(-1, k)
                    for copy in slot_copies(-1, k):
                        copy.start()

                return unused

            lax.fori_loop(0, lines - 1, body, 0)

        def arrive():
            @pl.when(z > 0)
            def _():
                receive(1, z)

            @pl.when(z + 1 < lines)
            def _():
                receive(-1, z)

        def finish(k, unused):
            @pl.when(z < lines - 1 - k)
            def _():
                for copy in slot_copies(1, lines - 1 - k):
                    copy.wait_send()

            @pl.when(z > k)
            def _():
                for copy in slot_copies(-1, k):
                    copy.wait_send()

            return unused

        return (
            ends_first,
            relay,
            arrive,
            lambda: lax.fori_loop(0, lines - 1, finish, 0),
        )

    def store(u):
        m = units[u][0]
        outs[m][rows_of(u), :] = mine[m, z, x, rows_of(u)].astype(f32)

    pending = {}
    for i, u in enumerate(order):
        loads[i].wait()
        cores[i].wait()
        if u in z_first:
            add_slices(mine, core_in, u, 0)
            add_slices(mine, core_in, u, 1)
        else:
            add_slices(mine, core_in, u, 1 - x)
            copy = x_copy(u, True)
            copy.start()
            pending[u] = copy
            add_slices(mine, core_in, u, x)
    x_first = [u for u in order if u not in z_first]
    flows = {u: line_flow(u, [0, 1] if u in z_first else [x]) for u in order}
    last = {}

    def x_stage(u):
        m = units[u][0]
        pending[u].wait()

        def body(line, unused):
            at = (m, line, x, rows_of(u))
            mine[at] = added(mine[at], x_in[m, line, rows_of(u)])
            return unused

        lax.fori_loop(0, lines, body, 0)

    def settle(u):
        flows[u][2]()
        if u in z_first:
            last[u] = x_copy(u, False)
            last[u].start()
        else:
            store(u)

    for t in range(len(order) + 2):
        if t < len(order):
            u = order[t]
            if u not in z_first:
                x_stage(u)
            flows[u][0]()
        if 0 <= t - 1 < len(order):
            flows[order[t - 1]][1]()
        if 0 <= t - 2 < len(order):
            settle(order[t - 2])
    for u, copy in last.items():
        m = units[u][0]
        copy.wait()
        at = (m, z, x, rows_of(u))
        mine[at] = added(mine[at], x_in[m, z, rows_of(u)])
        store(u)
    for u in order:
        flows[u][3]()


def reduce_scatter(parts, cycle_size):
    lines = cycle_size // 4
    units_here, model = parts[0].shape
    rows = units_here // cycle_size
    cut = (rows // 2 + 15) // 16 * 16
    pieces = [(0, cut), (cut, rows - cut)] if cut < rows else [(0, rows)]
    units = [(m, at, size) for m in range(3) for at, size in pieces]
    z_first = [len(units) - 1]
    shaped = [part.reshape(lines, 2, 2, rows, model) for part in parts]
    hbm = pl.BlockSpec(memory_space=pl.ANY)
    n = len(units)
    return pl.pallas_call(
        functools.partial(scatter_kernel, lines, units, z_first),
        out_shape=[jax.ShapeDtypeStruct((rows, model), f32)] * 3,
        in_specs=[hbm] * 3,
        out_specs=[vmem] * 3,
        scratch_shapes=[
            pltpu.VMEM((3, lines, 2, rows, model), bf16),
            pltpu.VMEM((3, lines, 2, rows, model), bf16),
            pltpu.VMEM((3, lines, rows, model), bf16),
            pltpu.VMEM((3, lines, 2, rows, model), bf16),
            pltpu.VMEM((3, lines, 2, rows, model), bf16),
            pltpu.SemaphoreType.DMA((n,)),
            pltpu.SemaphoreType.DMA((2, n)),
            pltpu.SemaphoreType.DMA((2, n)),
            pltpu.SemaphoreType.DMA((2, n, lines, 2)),
            pltpu.SemaphoreType.DMA((2, n, lines, 2)),
        ],
        compiler_params=pltpu.CompilerParams(
            vmem_limit_bytes=58 * 2**20, collective_id=1, has_side_effects=True
        ),
        name="weight_scatter",
    )(*shaped)

def tn(a, b):
    return lax.dot_general(a, b, (((0,), (0,)), ((), ())), preferred_element_type=f32)


def line_relay(spot, start, receive):
    def level(k, unused):
        @pl.when(spot.z - k >= 0)
        def _():
            if_first(k, lambda: receive(1, spot.z - k))

            @pl.when(spot.z + 1 < spot.lines)
            def _():
                start(1, spot.z - k)

        @pl.when(spot.z + k < spot.lines)
        def _():
            if_first(k, lambda: receive(-1, spot.z + k))

            @pl.when(spot.z > 0)
            def _():
                start(-1, spot.z + k)

        return unused

    def if_first(k, run):
        @pl.when(k > 0)
        def _():
            run()

    return level


def finish_kernel(
    plan, lines, dq_ref, dk_ref, dv_ref, mask_ref, w3_ref, normed_ref, att_ref, branch_ref,
    tokens_ref, gain_ref, hidden_ref, gh_ref, ffn_ref, small_ref,
    out_ref, gt_ref, gm_ref, weights_ref, total_ref,
    mine, core_in, x_in, up_in, down_in, all_w, y_out, y_in, own_part, ffn_in, mask_in,
    small_own, small_y, small_core, small_x, small_all,
    y_sem, core_sem, x_sem, up_sem, down_sem, gz_sem, gx_sem, gc_sem, sz_sem,
):
    spot = Spot(lines)
    z, x, core, wa = (spot.z, spot.x, spot.core, spot.wa)
    greet(spot, True)
    half = tokens_ref.shape[0]
    quarter = half // 2
    model = tokens_ref.shape[1]
    rows = mine.shape[3]

    def grad_rows(at):
        at = pl.ds(pl.multiple_of(at, quarter), quarter)
        return (
            nt(dq_ref[at, :], w3_ref[:, 0:256])
            + nt(dk_ref[at, :], w3_ref[:, 256:512])
            + nt(dv_ref[at, :], w3_ref[:, 512:768])
        )

    def y_copy(i):
        return send(y_out.at[i], y_in.at[i], y_sem.at[0, i], y_sem.at[1, i], spot.y_mate())

    def theirs(i, unused):
        y_out[i] = grad_rows((1 - wa) * half + i * quarter).astype(bf16)
        y_copy(i).start()
        return unused

    lax.fori_loop(0, 2, theirs, 0)
    mask_copy = send(
        mask_ref.at[1 - wa], mask_in, y_sem.at[0, 2], y_sem.at[1, 2], spot.y_mate()
    )
    mask_copy.start()

    def fill(product, matrix):
        for j in range(plan.cols // rows):
            s = matrix * (plan.cols // rows) + j
            mine[s // 4, (s // 2) % 2, s % 2] = product[j * rows : (j + 1) * rows].astype(bf16)

    fill(tn(dq_ref[...], normed_ref[...])[: plan.cols], 0)
    fill(tn(dk_ref[...], normed_ref[...])[: plan.cols], 1)
    fill(tn(dv_ref[...], normed_ref[...])[64:], 2)
    fill(tn(att_ref[...], branch_ref[...])[64:], 3)
    core_copy = send(
        mine.at[:, :, 1 - core], core_in, core_sem.at[0, 0], core_sem.at[1, 0], spot.core_mate()
    )
    core_copy.start()
    their_rows = pl.ds(pl.multiple_of((1 - wa) * half, half), half)
    ffn_copy = send(
        ffn_ref.at[their_rows], ffn_in, y_sem.at[0, 3], y_sem.at[1, 3], spot.y_mate()
    )
    ffn_copy.start()

    def ours(i, unused):
        own_part[pl.ds(pl.multiple_of(i * quarter, quarter), quarter), :] = grad_rows(
            wa * half + i * quarter
        )
        return unused

    lax.fori_loop(0, 2, ours, 0)
    core_copy.wait()

    def x_copy(d):
        return send(
            mine.at[d, 1 - x, core], x_in.at[d], x_sem.at[0, d], x_sem.at[1, d], spot.x_mate()
        )

    def core_add(d, unused):
        mine[d, 1 - x, core] = added(mine[d, 1 - x, core], core_in[d, 1 - x])
        x_copy(d).start()
        return unused

    lax.fori_loop(0, lines, core_add, 0)

    def core_add_own(d, unused):
        mine[d, x, core] = added(mine[d, x, core], core_in[d, x])
        return unused

    lax.fori_loop(0, lines, core_add_own, 0)

    gain_sum = jnp.zeros((1, model), f32)
    step = 32
    for i in range(2):
        y_copy(i).wait()

        def normal(j, total, i=i):
            at = pl.ds(pl.multiple_of(i * quarter + j * step, step), step)
            there = pl.ds(pl.multiple_of(j * step, step), step)
            grad = own_part[at, :] + y_in[i, there, :].astype(f32)
            rows_in = tokens_ref[at, :].astype(f32)
            inv = lax.rsqrt(jnp.mean(rows_in * rows_in, axis=-1, keepdims=True) + eps)
            scaled = gain_ref[...] * grad
            mean = jnp.mean(rows_in * scaled, axis=-1, keepdims=True)
            gt_ref[at, :] = gh_ref[at, :] + inv * scaled - rows_in * (inv * inv * inv * mean)
            return total + jnp.sum(grad * rows_in * inv, axis=0, keepdims=True)

        gain_sum = lax.fori_loop(0, quarter // step, normal, gain_sum)
    small_own[...] = small_ref[...]
    small_own[0:1, :] = gain_sum
    small_copy = send(
        small_own, small_y, y_sem.at[0, 4], y_sem.at[1, 4], spot.y_mate()
    )
    small_copy.start()
    mask_copy.wait()
    gm_ref[...] = mask_ref[wa] + mask_in[...]

    def flow(step, d):
        ring, sem = (up_in, up_sem) if step > 0 else (down_in, down_sem)
        return send(
            mine.at[d, x, core], ring.at[d], sem.at[0, d], sem.at[1, d], spot.z_mate(step)
        )

    def merge(step, d):
        flow(step, d).wait_recv()
        ring = up_in if step > 0 else down_in
        mine[d, x, core] = added(mine[d, x, core], ring[d])

    def x_add(d, unused):
        x_copy(d).wait()
        mine[d, x, core] = added(mine[d, x, core], x_in[d])

        @pl.when((z == 0) & (d > 0))
        def _():
            flow(1, d).start()

        @pl.when((z == lines - 1) & (d < lines - 1))
        def _():
            flow(-1, d).start()

        return unused

    lax.fori_loop(0, lines, x_add, 0)
    small_copy.wait()
    row = lax.broadcasted_iota(jnp.int32, small_own.shape, 0)
    small_x[0] = small_own[...] + jnp.where(row < 2, small_y[...], 0.0)
    small_core_copy = send(
        small_x.at[0], small_core, core_sem.at[0, 1], core_sem.at[1, 1], spot.core_mate()
    )
    small_core_copy.start()

    def relay(k, unused):
        high = lines - 1 - k

        @pl.when((z < high) & (z > 0))
        def _():
            merge(1, high)
            flow(1, high).start()

        @pl.when((z > k) & (z + 1 < lines))
        def _():
            merge(-1, k)
            flow(-1, k).start()

        return unused

    lax.fori_loop(0, lines - 1, relay, 0)
    small_core_copy.wait()
    small_x[1] = small_x[0] + small_core[...]
    small_x_copy = send(
        small_x.at[1], small_x.at[2], x_sem.at[0, lines], x_sem.at[1, lines], spot.x_mate()
    )
    small_x_copy.start()

    @pl.when(z > 0)
    def _():
        merge(1, z)

    @pl.when(z + 1 < lines)
    def _():
        merge(-1, z)

    all_w[z, x, core] = mine[z, x, core]

    def pass_w(step, d):
        i = 0 if step > 0 else 1
        return send(
            all_w.at[d, x, core], all_w.at[d, x, core], gz_sem.at[i, d], gz_sem.at[2 + i, d],
            spot.z_mate(step),
        )

    def pass_s(step, d):
        i = 0 if step > 0 else 1
        return send(
            small_all.at[d], small_all.at[d], sz_sem.at[i, d], sz_sem.at[2 + i, d],
            spot.z_mate(step),
        )

    def across(d):
        return send(
            all_w.at[d, x, core], all_w.at[d, x, core], gx_sem.at[0, d], gx_sem.at[1, d],
            spot.x_mate(),
        )

    def beside(d):
        return send(
            all_w.at[d, :, core], all_w.at[d, :, core], gc_sem.at[0, d], gc_sem.at[1, d],
            spot.core_mate(),
        )

    small_x_copy.wait()
    small_all[z] = small_x[1] + small_x[2]

    def receive(step, d):
        pass_w(step, d).wait_recv()
        across(d).start()

    across(z).start()
    lax.fori_loop(
        0, lines, line_relay(spot, lambda s, d: pass_w(s, d).start(), receive), 0
    )
    lax.fori_loop(
        0,
        lines,
        line_relay(
            spot, lambda s, d: pass_s(s, d).start(), lambda s, d: pass_s(s, d).wait_recv()
        ),
        0,
    )

    def add_small(d, total):
        return total + small_all[d]

    total_ref[...] = lax.fori_loop(1, lines, add_small, small_all[0])
    ffn_copy.wait()

    def last(j, unused):
        at = pl.ds(pl.multiple_of(j * step, step), step)
        here = pl.ds(pl.multiple_of(wa * half + j * step, step), step)
        total = hidden_ref[at, :] + ffn_ref[here, :].astype(f32) + ffn_in[at, :].astype(f32)
        out_ref[at, :] = total.astype(bf16)
        return unused

    lax.fori_loop(0, half // step, last, 0)

    def spread(d, unused):
        across(d).wait()
        beside(d).start()
        return unused

    lax.fori_loop(0, lines, spread, 0)

    def copy_out(d, unused):
        beside(d).wait()
        weights_ref[d] = all_w[d]
        return unused

    lax.fori_loop(0, lines, copy_out, 0)

    def drain(d, unused):
        @pl.when((z < d))
        def _():
            flow(1, d).wait_send()

        @pl.when((z > d))
        def _():
            flow(-1, d).wait_send()

        @pl.when((d <= z) & (z + 1 < lines))
        def _():
            pass_w(1, d).wait_send()
            pass_s(1, d).wait_send()

        @pl.when((d >= z) & (z > 0))
        def _():
            pass_w(-1, d).wait_send()
            pass_s(-1, d).wait_send()

        return unused

    lax.fori_loop(0, lines, drain, 0)


def finish(plan, cycle_size, *operands):
    lines = cycle_size // 4
    half, model = operands[8].shape
    rows = 4 * plan.cols // cycle_size
    dma = pltpu.SemaphoreType.DMA
    return pl.pallas_call(
        functools.partial(finish_kernel, plan, lines),
        out_shape=[
            jax.ShapeDtypeStruct((half, model), bf16),
            jax.ShapeDtypeStruct((half, model), f32),
            jax.ShapeDtypeStruct((8, half), f32),
            jax.ShapeDtypeStruct((lines, 2, 2, rows, model), bf16),
            jax.ShapeDtypeStruct((8, model), f32),
        ],
        in_specs=[vmem] * len(operands),
        out_specs=[vmem] * 5,
        scratch_shapes=[
            pltpu.VMEM((lines, 2, 2, rows, model), bf16),
            pltpu.VMEM((lines, 2, rows, model), bf16),
            pltpu.VMEM((lines, rows, model), bf16),
            pltpu.VMEM((lines, rows, model), bf16),
            pltpu.VMEM((lines, rows, model), bf16),
            pltpu.VMEM((lines, 2, 2, rows, model), bf16),
            pltpu.VMEM((2, half // 2, model), bf16),
            pltpu.VMEM((2, half // 2, model), bf16),
            pltpu.VMEM((half, model), f32),
            pltpu.VMEM((half, model), bf16),
            pltpu.VMEM((8, half), f32),
            pltpu.VMEM((8, model), f32),
            pltpu.VMEM((8, model), f32),
            pltpu.VMEM((8, model), f32),
            pltpu.VMEM((3, 8, model), f32),
            pltpu.VMEM((lines, 8, model), f32),
            dma((2, 5)),
            dma((2, 2)),
            dma((2, lines + 1)),
            dma((2, lines)),
            dma((2, lines)),
            dma((4, lines)),
            dma((2, lines)),
            dma((2, lines)),
            dma((4, lines)),
        ],
        compiler_params=pltpu.CompilerParams(
            vmem_limit_bytes=58 * 2**20, collective_id=2, has_side_effects=True
        ),
        name="finish",
    )(*operands)


def shards(
    tokens,
    doc_lengths,
    key_mask,
    gain_attn,
    w_query,
    w_key,
    w_value,
    w_out,
    bias_table,
    gain_ffn,
    w_gate,
    w_up,
    w_down,
    cotangent,
):
    own_rows, model = tokens.shape
    group = lax.axis_size("wa")
    cycle_size = lax.axis_size("ctx")
    pair = own_rows * group
    heads = bias_table.shape[1]
    docs = doc_lengths.shape[0]
    plan = Plan(heads, w_query.shape[1] // heads, docs)
    total_rows = pair * cycle_size
    doc_most = min(MAXLEN, total_rows // 2)
    reach = min(cycle_size - 1, (doc_most - 1) // pair + 1)
    base = lax.axis_index("ctx") * pair
    rows = min(total_rows, (2 * reach + 1) * pair)
    origin = jnp.clip(base - reach * pair, 0, total_rows - rows).astype(jnp.int32)
    ends = jnp.cumsum(doc_lengths).astype(jnp.int32)
    starts = ends - doc_lengths

    def doc_at(positions):
        return jnp.sum((positions[:, None] >= starts[None, :]).astype(jnp.int32), axis=1) - 1

    tiles = pair // TQ
    tile_start = base + TQ * jnp.arange(tiles, dtype=jnp.int32)
    first_doc = jnp.arange(docs, dtype=jnp.int32)[None, :] == doc_at(tile_start)[:, None]
    last_doc = jnp.arange(docs, dtype=jnp.int32)[None, :] == doc_at(tile_start + TQ - 1)[:, None]
    low_end = jnp.sum(jnp.where(first_doc, starts[None, :], 0), axis=1)
    high_end = jnp.sum(jnp.where(last_doc, ends[None, :], 0), axis=1)
    n_left = jnp.maximum(0, (tile_start - EDGE - low_end + TK - 1) // TK)
    n_right = jnp.maximum(0, (high_end - (tile_start - EDGE + TK) + TK - 1) // TK)
    bounds = jnp.concatenate(
        [(base - origin)[None], jnp.stack([n_left, n_right], axis=1).reshape(-1)]
    ).astype(jnp.int32)

    mask_all = lax.all_gather(key_mask, "ctx", axis=0, tiled=True)
    tokens_wide = tokens.astype(f32)
    normed_attn, inv_attn = norm_forward(tokens_wide, gain_attn)
    normed_low = normed_attn.astype(bf16)
    pair_normed, pair_cot = (
        lax.all_gather(normed_low, "wa", axis=0, tiled=True),
        lax.all_gather(cotangent, "wa", axis=0, tiled=True),
    )
    w_kv = jnp.concatenate([w_key, w_value], axis=1)
    own_kv = jnp.dot(pair_normed, w_kv, preferred_element_type=f32).astype(bf16)
    queries = jnp.dot(pair_normed, w_query, preferred_element_type=f32).astype(bf16)

    def window(gathered):
        if rows == total_rows:
            return gathered
        return lax.dynamic_slice_in_dim(gathered, origin, rows, 0)

    gather = functools.partial(lax.all_gather, axis_name="ctx", axis=0, tiled=True)
    kv_all = window(gather(own_kv))
    positions = origin + jnp.arange(rows, dtype=jnp.int32)
    doc_of = doc_at(positions)
    lane = jnp.arange(128, dtype=jnp.int32)[None, :] + 128
    code = lane - plan.doc_lane
    bit_differs = ((doc_of[:, None] >> (code >> 1)) & 1) != (code & 1)
    k_aug = jnp.where(
        lane == plan.mask_lane,
        window(mask_all).astype(f32)[:, None],
        jnp.where(
            lane < plan.stat_lane,
            jnp.where(bit_differs & (code >= 0), neg_big, 0.0),
            (lane < plan.stat_lane + 3 * heads).astype(f32),
        ),
    ).astype(bf16)
    own_docs = doc_at(base + jnp.arange(pair, dtype=jnp.int32))
    own_differs = ((own_docs[:, None] >> (code >> 1)) & 1) != (code & 1)
    q_aug = jnp.where(
        lane == plan.mask_lane, 1.0, ((lane < plan.stat_lane) & ~own_differs).astype(f32)
    ).astype(bf16)
    q_wide = jnp.concatenate(
        [queries, q_aug[:, plan.cols - 128 :]], axis=1
    )
    near_bias = pl.pallas_call(
        functools.partial(near_kernel, heads),
        out_shape=jax.ShapeDtypeStruct((2, heads, TQ, TK), f32),
        in_specs=[smem],
        out_specs=vmem,
        compiler_params=params(),
        name="near_bias",
    )(bias_table)

    padded = rows + 2 * PAD
    attended, mixed, q_back = pl.pallas_call(
        functools.partial(fwd_kernel, plan, rows, pair),
        out_shape=(
            jax.ShapeDtypeStruct((pair, WIDE), bf16),
            jax.ShapeDtypeStruct((pair, WIDE), f32),
            jax.ShapeDtypeStruct((pair, WIDE), bf16),
        ),
        in_specs=[smem, smem, vmem, vmem, vmem, vmem],
        out_specs=(vmem, vmem, vmem),
        scratch_shapes=[
            pltpu.VMEM((padded, WIDE), bf16),
            pltpu.VMEM((padded, WIDE), bf16),
            pltpu.VMEM((heads, TQ, WIDE), f32),
            pltpu.VMEM((heads, TQ, 128), f32),
            pltpu.VMEM((heads, TQ, WIDE), bf16),
        ],
        compiler_params=params(),
        name="attention_forward",
    )(bounds, bias_table, kv_all, k_aug, q_wide, near_bias)
    q_all = window(gather(q_back))
    w_out_pad = jnp.concatenate([jnp.zeros((64, model), bf16), w_out], axis=0)
    branch = lax.psum_scatter(
        jnp.dot(attended, w_out_pad, preferred_element_type=f32).astype(bf16),
        "wa",
        scatter_dimension=0,
        tiled=True,
    ).astype(f32)
    hidden = tokens_wide + branch
    normed_ffn, inv_ffn = norm_forward(hidden, gain_ffn)
    ffn_low = normed_ffn.astype(bf16)
    pair_ffn = lax.all_gather(ffn_low, "wa", axis=0, tiled=True)
    gate = jnp.dot(pair_ffn, w_gate, preferred_element_type=f32)
    upward = jnp.dot(pair_ffn, w_up, preferred_element_type=f32)
    inner = gated(gate, upward).astype(bf16)
    ffn_part = jnp.dot(inner, w_down, preferred_element_type=f32)
    grad_inner = jnp.dot(pair_cot, w_down.T, preferred_element_type=f32)
    down_half = jnp.dot(inner.T, pair_cot, preferred_element_type=f32).astype(bf16)
    unused_value, pullback = jax.vjp(gated, gate, upward)
    grad_gate, grad_upward = pullback(grad_inner)
    grad_gate = grad_gate.astype(bf16)
    grad_upward = grad_upward.astype(bf16)
    grad_pair_ffn = jnp.dot(grad_gate, w_gate.T, preferred_element_type=f32) + jnp.dot(
        grad_upward, w_up.T, preferred_element_type=f32
    )
    grad_normed_ffn = lax.psum_scatter(
        grad_pair_ffn.astype(bf16), "wa", scatter_dimension=0, tiled=True
    ).astype(f32)
    gate_half = jnp.dot(grad_gate.T, pair_ffn, preferred_element_type=f32).astype(bf16)
    up_half = jnp.dot(grad_upward.T, pair_ffn, preferred_element_type=f32).astype(bf16)
    grad_w_down, grad_w_gate, grad_w_up = reduce_scatter(
        [down_half, gate_half, up_half], cycle_size
    )
    grad_w_gate, grad_w_up = (grad_w_gate.T, grad_w_up.T)
    hidden_step, gain_ffn_part = norm_backward(hidden, inv_ffn, gain_ffn, grad_normed_ffn)
    grad_hidden = cotangent.astype(f32) + hidden_step
    pair_branch = lax.all_gather(grad_hidden.astype(bf16), "wa", axis=0, tiled=True)
    do_wide = pl.pallas_call(
        functools.partial(grad_attended_kernel, plan),
        out_shape=jax.ShapeDtypeStruct((pair, WIDE), bf16),
        in_specs=[vmem, vmem, vmem],
        out_specs=vmem,
        compiler_params=params(),
        name="grad_attended",
    )(pair_branch, w_out_pad, mixed)
    do_all = window(gather(do_wide))

    grad_queries, table_part = pl.pallas_call(
        functools.partial(dq_kernel, plan, rows, pair),
        out_shape=(
            jax.ShapeDtypeStruct((pair, WIDE), bf16),
            jax.ShapeDtypeStruct((heads, 32, 128), f32),
        ),
        in_specs=[smem, smem, vmem, vmem, vmem, vmem, vmem],
        out_specs=(vmem, vmem),
        scratch_shapes=[
            pltpu.VMEM((padded, WIDE), bf16),
            pltpu.VMEM((padded, WIDE), bf16),
            pltpu.VMEM((heads, TQ, WIDE), f32),
            pltpu.VMEM((heads, TQ, WIDE), bf16),
            pltpu.VMEM((heads, TQ, WIDE), bf16),
            pltpu.VMEM((heads, TQ, TK), f32),
            pltpu.VMEM((2, heads, TQ, 128), f32),
        ],
        compiler_params=params(),
        name="attention_grad_queries",
    )(bounds, bias_table, kv_all, k_aug, q_back, do_wide, near_bias)
    own_aug = lax.dynamic_slice_in_dim(k_aug, base - origin, pair, 0)
    grad_keys, grad_values, mask_part = pl.pallas_call(
        functools.partial(dkv_kernel, plan, rows, pair),
        out_shape=(
            jax.ShapeDtypeStruct((pair, WIDE), bf16),
            jax.ShapeDtypeStruct((pair, WIDE), bf16),
            jax.ShapeDtypeStruct((tiles, 8, TQ), f32),
        ),
        in_specs=[smem, smem, vmem, vmem, vmem, vmem, vmem],
        out_specs=(vmem, vmem, vmem),
        scratch_shapes=[
            pltpu.VMEM((padded, WIDE), bf16),
            pltpu.VMEM((padded, WIDE), bf16),
            pltpu.VMEM((heads, TQ, WIDE), bf16),
            pltpu.VMEM((heads, TQ, WIDE), bf16),
            pltpu.VMEM((heads, TQ, WIDE), f32),
            pltpu.VMEM((heads, TQ, WIDE), f32),
        ],
        compiler_params=params(),
        name="attention_grad_keys",
    )(bounds, bias_table, q_all, do_all, own_kv, own_aug, near_bias)
    cols = plan.cols
    gap = jnp.zeros((model, WIDE - cols), bf16)
    w_wide = jnp.concatenate([w_query, gap, w_key, gap, gap, w_value], axis=1)
    table_row = jnp.sum(table_part, axis=2).reshape(1, -1)
    table_row = jnp.pad(table_row, ((0, 0), (0, model - table_row.shape[1])))
    small = jnp.concatenate(
        [jnp.zeros((1, model), f32), gain_ffn_part[None], table_row, jnp.zeros((5, model), f32)],
        axis=0,
    )
    layer_out, grad_tokens, grad_mask, weights, totals = finish(
        plan,
        cycle_size,
        grad_queries,
        grad_keys,
        grad_values,
        mask_part.reshape(group, 8, own_rows),
        w_wide,
        pair_normed,
        attended,
        pair_branch,
        tokens,
        gain_attn[None],
        hidden,
        grad_hidden,
        ffn_part.astype(bf16),
        small,
    )
    weights = weights.reshape(4, cols, model).astype(f32)
    return (
        layer_out,
        grad_tokens,
        grad_mask[0],
        totals[0],
        weights[0].T,
        weights[1].T,
        weights[2].T,
        weights[3],
        totals[2, : heads * 32].reshape(heads, 32).T,
        totals[1],
        grad_w_gate,
        grad_w_up,
        grad_w_down,
    )


def solution(mesh):
    placed = (
        P(("ctx", "wa"), None),
        P(),
        P("ctx"),
        P(),
        P(None, "wa"),
        P(None, "wa"),
        P(None, "wa"),
        P("wa", None),
        P(None, "wa"),
        P(),
        P(None, "wa"),
        P(None, "wa"),
        P("wa", None),
        P(("ctx", "wa"), None),
    )
    return jax.shard_map(
        shards,
        mesh=mesh,
        in_specs=placed,
        out_specs=(
            P(("ctx", "wa"), None),
            P(("ctx", "wa"), None),
            P(("ctx", "wa")),
            P(),
            P(None, "wa"),
            P(None, "wa"),
            P(None, "wa"),
            P("wa", None),
            P(None, "wa"),
            P(),
            P(None, ("wa", "ctx")),
            P(None, ("wa", "ctx")),
            P(("wa", "ctx"), None),
        ),
        check_vma=False,
    )
```

```python
import functools

import jax
import jax.numpy as jnp
from jax import lax
from jax.experimental import pallas as pl
from jax.experimental.pallas import tpu as pltpu
from jax.sharding import PartitionSpec as P

MAXLEN = 8192

bucket_edges = (12, 16, 23, 32, 46, 64, 91)
neg_big = -1e30
eps = 1e-06
far_left_bucket = 15
far_right_bucket = 31
WIDE = 256
TQ = 256
TK = 512
EDGE = 128
PAD = TK + EDGE
f32 = jnp.float32
bf16 = jnp.bfloat16


def bucket_of(relative):
    distance = jnp.abs(relative)
    bucket = jnp.minimum(distance, 8) + 16 * (relative > 0).astype(jnp.int32)
    for edge in bucket_edges:
        bucket = bucket + (distance >= edge).astype(jnp.int32)
    return bucket


def norm_forward(inputs, gain):
    inv_root = lax.rsqrt(jnp.mean(inputs * inputs, axis=-1, keepdims=True) + eps)
    return (inputs * inv_root * gain, inv_root)


def norm_backward(inputs, inv_root, gain, grad_normed):
    scaled = gain * grad_normed
    cubed = inv_root * inv_root * inv_root
    grad_inputs = inv_root * scaled - inputs * cubed * jnp.mean(
        inputs * scaled, axis=-1, keepdims=True
    )
    grad_gain = jnp.sum(grad_normed * inputs * inv_root, axis=0)
    return (grad_inputs, grad_gain)


def gated(gate, upward):
    return jax.nn.gelu(gate, approximate=True) * upward


def nt(a, b):
    return lax.dot_general(a, b, (((1,), (1,)), ((), ())), preferred_element_type=f32)


def nn(a, b):
    return lax.dot_general(a, b, (((1,), (0,)), ((), ())), preferred_element_type=f32)


def split3(x):
    hi = x.astype(bf16)
    rest = x - hi.astype(f32)
    mid = rest.astype(bf16)
    return (hi, mid, (rest - mid.astype(f32)).astype(bf16))


class Plan:
    def __init__(self, heads, width, docs):
        self.heads = heads
        self.width = width
        self.bits = max(1, (docs - 1).bit_length())
        self.cols = heads * width
        self.mask_lane = self.cols
        self.doc_lane = self.cols + 1
        self.stat_lane = self.doc_lane + 2 * self.bits
        assert self.stat_lane + 3 * heads <= WIDE and self.cols + 64 == WIDE and width == 64

    def key_lanes(self, lane, h):
        own = (lane >= h * self.width) & (lane < (h + 1) * self.width)
        aug = (lane >= self.mask_lane) & (lane < self.stat_lane)
        stat = (lane >= self.stat_lane + 3 * h) & (lane < self.stat_lane + 3 * h + 3)
        return own | aug | stat

    def value_lanes(self, lane, h):
        own = (lane >= 64 + h * self.width) & (lane < 64 + (h + 1) * self.width)
        return own | ((lane >= 3 * h) & (lane < 3 * h + 3))


def lanes_of(rows, width=WIDE):
    return lax.broadcasted_iota(jnp.int32, (rows, width), 1)


def near_kernel(heads, table_ref, near_ref):
    row = lax.broadcasted_iota(jnp.int32, (EDGE, 3 * EDGE), 0)
    col = lax.broadcasted_iota(jnp.int32, (EDGE, 3 * EDGE), 1)
    relative = col - EDGE - row
    for flip in range(2):
        bucket = bucket_of(-relative if flip else relative)
        left, right = (far_left_bucket, far_right_bucket)
        if flip:
            left, right = (right, left)
        for h in range(heads):
            base = jnp.full((EDGE, 3 * EDGE), table_ref[0, h], f32)
            for b in range(1, 32):
                base = jnp.where(bucket == b, table_ref[b, h], base)
            far_l = jnp.full((EDGE, EDGE), table_ref[left, h], f32)
            far_r = jnp.full((EDGE, EDGE), table_ref[right, h], f32)
            near_ref[flip, h, :EDGE, : 3 * EDGE] = base
            near_ref[flip, h, :EDGE, 3 * EDGE :] = far_r
            near_ref[flip, h, EDGE:, EDGE:] = base
            near_ref[flip, h, EDGE:, :EDGE] = far_l


def build_keys(plan, g_ref, kaug_ref, km, vm, rows):
    km[:PAD, :] = jnp.broadcast_to(
        jnp.where(pad_lanes(plan), neg_big, 0.0).astype(bf16), (PAD, WIDE)
    )
    km[pl.ds(PAD + rows, PAD), :] = km[:PAD, :]
    vm[:PAD, :] = jnp.zeros((PAD, WIDE), bf16)
    vm[pl.ds(PAD + rows, PAD), :] = jnp.zeros((PAD, WIDE), bf16)
    step = 512
    low = lanes_of(step, 128) < 64
    ones = (lanes_of(step, 128) < 3 * plan.heads).astype(bf16)

    def body(n, unused):
        at = pl.multiple_of(n * step, step)
        to = pl.multiple_of(PAD + n * step, 128)
        middle = g_ref[pl.ds(at, step), 128:256]
        km[pl.ds(to, step), 0:128] = g_ref[pl.ds(at, step), 0:128]
        km[pl.ds(to, step), 128:256] = jnp.where(low, middle, kaug_ref[pl.ds(at, step), :])
        vm[pl.ds(to, step), 0:128] = jnp.where(low, ones, middle)
        vm[pl.ds(to, step), 128:256] = g_ref[pl.ds(at, step), 256:384]
        return unused

    lax.fori_loop(0, rows // step, body, 0)


def pad_lanes(plan):
    lane = lanes_of(1)
    return (lane >= plan.doc_lane) & (lane < plan.stat_lane)


def fwd_kernel(
    plan, rows, pair, bounds, table_ref, g_ref, kaug_ref, q_ref, near_ref,
    low_ref, wide_ref, qb_ref, km, vm, acc, row_max, qh_ref,
):
    build_keys(plan, g_ref, kaug_ref, km, vm, rows)
    lane = lanes_of(TQ)

    def tile(t, unused):
        start = pl.multiple_of(bounds[0] + t * TQ, 128)
        n_left, n_right = (bounds[1 + 2 * t], bounds[2 + 2 * t])
        out = pl.ds(pl.multiple_of(t * TQ, TQ), TQ)
        q = q_ref[out, :]
        near = pl.ds(pl.multiple_of(start + PAD - EDGE, 128), TK)
        for h in range(plan.heads):
            qh = jnp.where(plan.key_lanes(lane, h), q, jnp.zeros_like(q))
            qh_ref[h] = qh
            s = nt(qh, km[near, :]) + near_ref[0, h]
            top = jnp.max(s, axis=1, keepdims=True)
            p = jnp.exp(s - top).astype(bf16)
            acc[h] = nn(p, vm[near, :])
            row_max[h] = jnp.broadcast_to(top, (TQ, 128))

        def far(bucket):
            def step(first, n):
                span = pl.ds(pl.multiple_of(first + n, 128), TK)
                for h in range(plan.heads):
                    s = nt(qh_ref[h], km[span, :])
                    offset = table_ref[bucket, h]
                    old = row_max[h][:, :1]
                    top = jnp.maximum(old, jnp.max(s, axis=1, keepdims=True) + offset)
                    p = jnp.exp(s - (top - offset)).astype(bf16)
                    acc[h] = acc[h] * jnp.exp(old - top) + nn(p, vm[span, :])
                    row_max[h] = jnp.broadcast_to(top, (TQ, 128))
            return step

        left, right = (far(far_left_bucket), far(far_right_bucket))

        @pl.loop(0, n_left)
        def _(n):
            left(start + PAD - EDGE - TK, -n * TK)

        @pl.loop(0, n_right)
        def _(n):
            right(start + PAD - EDGE + TK, n * TK)

        wide = jnp.zeros((TQ, WIDE), f32)
        qb = jnp.where(lane < plan.stat_lane, q, jnp.zeros_like(q))
        for h in range(plan.heads):
            total = acc[h][:, 3 * h : 3 * h + 1]
            log_total = row_max[h][:, :1] + jnp.log(total)
            wide = jnp.where(lane // 64 == h + 1, acc[h] / total, wide)
            for i, part in enumerate(split3(-log_total)):
                qb = jnp.where(lane == plan.stat_lane + 3 * h + i, part, qb)
        wide_ref[out, :] = wide
        low_ref[out, :] = wide.astype(bf16)
        qb_ref[out, :] = qb
        return unused

    lax.fori_loop(0, pair // TQ, tile, 0)


def dq_kernel(
    plan, rows, pair, bounds, table_ref, g_ref, kaug_ref, qb_ref, do_ref, near_ref,
    dq_ref, tab_ref, km, vm, acc, qh_ref, doh_ref, near_acc, far_acc,
):
    build_keys(plan, g_ref, kaug_ref, km, vm, rows)
    lane = lanes_of(TQ)
    near_acc[...] = jnp.zeros_like(near_acc)
    far_acc[...] = jnp.zeros_like(far_acc)

    def tile(t, unused):
        start = pl.multiple_of(bounds[0] + t * TQ, 128)
        n_left, n_right = (bounds[1 + 2 * t], bounds[2 + 2 * t])
        out = pl.ds(pl.multiple_of(t * TQ, TQ), TQ)
        q = qb_ref[out, :]
        do = do_ref[out, :]
        near = pl.ds(pl.multiple_of(start + PAD - EDGE, 128), TK)

        def grads(h, s, span):
            p = jnp.exp(s)
            return p * nt(doh_ref[h], vm[span, :])

        for h in range(plan.heads):
            qh_ref[h] = jnp.where(plan.key_lanes(lane, h), q, jnp.zeros_like(q))
            doh_ref[h] = jnp.where(plan.value_lanes(lane, h), do, jnp.zeros_like(do))
            ds = grads(h, nt(qh_ref[h], km[near, :]) + near_ref[0, h], near)
            near_acc[h] += ds
            acc[h] = nn(ds.astype(bf16), km[near, :])

        def far(bucket, slot):
            def step(first, n):
                span = pl.ds(pl.multiple_of(first + n, 128), TK)
                for h in range(plan.heads):
                    ds = grads(h, nt(qh_ref[h], km[span, :]) + table_ref[bucket, h], span)
                    acc[h] += nn(ds.astype(bf16), km[span, :])
                    far_acc[slot, h] += (
                        ds[:, 0:128] + ds[:, 128:256] + ds[:, 256:384] + ds[:, 384:512]
                    )
            return step

        left, right = (far(far_left_bucket, 0), far(far_right_bucket, 1))

        @pl.loop(0, n_left)
        def _(n):
            left(start + PAD - EDGE - TK, -n * TK)

        @pl.loop(0, n_right)
        def _(n):
            right(start + PAD - EDGE + TK, n * TK)

        total = jnp.zeros((TQ, WIDE), f32)
        for h in range(plan.heads):
            total = jnp.where(lane // 64 == h, acc[h], total)
        dq_ref[out, :] = total.astype(bf16)
        return unused

    lax.fori_loop(0, pair // TQ, tile, 0)
    row = lax.broadcasted_iota(jnp.int32, (EDGE, 3 * EDGE), 0)
    col = lax.broadcasted_iota(jnp.int32, (EDGE, 3 * EDGE), 1)
    bucket = bucket_of(col - EDGE - row)
    for h in range(plan.heads):
        band = near_acc[h, :EDGE, : 3 * EDGE] + near_acc[h, EDGE:, EDGE:]
        extra_right = near_acc[h, :EDGE, 3 * EDGE :]
        extra_left = near_acc[h, EDGE:, :EDGE]
        for b in range(32):
            part = jnp.sum(jnp.where(bucket == b, band, 0.0), axis=0, keepdims=True)
            part = part[:, :128] + part[:, 128:256] + part[:, 256:]
            if b == far_left_bucket:
                part = part + jnp.sum(far_acc[0, h], axis=0, keepdims=True)
                part = part + jnp.sum(extra_left, axis=0, keepdims=True)
            if b == far_right_bucket:
                part = part + jnp.sum(far_acc[1, h], axis=0, keepdims=True)
                part = part + jnp.sum(extra_right, axis=0, keepdims=True)
            tab_ref[h, b : b + 1, :] = part


def dkv_kernel(
    plan, rows, pair, bounds, table_ref, qall_ref, doall_ref, g_ref, kaug_ref, near_ref,
    dk_ref, dv_ref, mask_ref, qp, dop, kh_ref, vh_ref, acc_k, acc_v,
):
    lane = lanes_of(TQ)
    first = lanes_of(1)
    stat = (first >= plan.stat_lane) & (first < plan.stat_lane + 3 * plan.heads)
    qp[:PAD, :] = jnp.broadcast_to(jnp.where(stat, neg_big, 0.0).astype(bf16), (PAD, WIDE))
    qp[pl.ds(PAD + rows, PAD), :] = qp[:PAD, :]
    dop[:PAD, :] = jnp.zeros((PAD, WIDE), bf16)
    dop[pl.ds(PAD + rows, PAD), :] = jnp.zeros((PAD, WIDE), bf16)
    step = 512

    def fill(n, unused):
        at = pl.multiple_of(n * step, step)
        to = pl.multiple_of(PAD + n * step, 128)
        qp[pl.ds(to, step), :] = qall_ref[pl.ds(at, step), :]
        dop[pl.ds(to, step), :] = doall_ref[pl.ds(at, step), :]
        return unused

    lax.fori_loop(0, rows // step, fill, 0)
    low = lanes_of(TQ, 128) < 64
    ones = (lanes_of(TQ, 128) < 3 * plan.heads).astype(bf16)

    def tile(t, unused):
        start = pl.multiple_of(bounds[0] + t * TQ, 128)
        n_left, n_right = (bounds[1 + 2 * t], bounds[2 + 2 * t])
        out = pl.ds(pl.multiple_of(t * TQ, TQ), TQ)
        middle = g_ref[out, 128:256]
        k = jnp.concatenate([g_ref[out, 0:128], jnp.where(low, middle, kaug_ref[out, :])], axis=1)
        v = jnp.concatenate([jnp.where(low, ones, middle), g_ref[out, 256:384]], axis=1)
        near = pl.ds(pl.multiple_of(start + PAD - EDGE, 128), TK)

        def grads(h, s, span):
            p = jnp.exp(s)
            ds = p * nt(vh_ref[h], dop[span, :])
            return nn(p.astype(bf16), dop[span, :]), nn(ds.astype(bf16), qp[span, :])

        for h in range(plan.heads):
            kh_ref[h] = jnp.where(plan.key_lanes(lane, h), k, jnp.zeros_like(k))
            vh_ref[h] = jnp.where(plan.value_lanes(lane, h), v, jnp.zeros_like(v))
            acc_v[h], acc_k[h] = grads(h, nt(kh_ref[h], qp[near, :]) + near_ref[1, h], near)

        def far(bucket):
            def step(first, n):
                span = pl.ds(pl.multiple_of(first + n, 128), TK)
                for h in range(plan.heads):
                    add_v, add_k = grads(
                        h, nt(kh_ref[h], qp[span, :]) + table_ref[bucket, h], span
                    )
                    acc_v[h] += add_v
                    acc_k[h] += add_k
            return step

        left, right = (far(far_right_bucket), far(far_left_bucket))

        @pl.loop(0, n_left)
        def _(n):
            left(start + PAD - EDGE - TK, -n * TK)

        @pl.loop(0, n_right)
        def _(n):
            right(start + PAD - EDGE + TK, n * TK)

        dk = jnp.zeros((TQ, WIDE), f32)
        dv = jnp.zeros((TQ, WIDE), f32)
        mask_grad = jnp.zeros((TQ, 1), f32)
        for h in range(plan.heads):
            dk = jnp.where(lane // 64 == h, acc_k[h], dk)
            dv = jnp.where(lane // 64 == h + 1, acc_v[h], dv)
            mask_grad = mask_grad + acc_k[h][:, plan.mask_lane : plan.mask_lane + 1]
        mask_ref[t] = jnp.transpose(jnp.broadcast_to(mask_grad, (TQ, 128)))[:8, :]
        dk_ref[out, :] = dk.astype(bf16)
        dv_ref[out, :] = dv.astype(bf16)
        return unused

    lax.fori_loop(0, pair // TQ, tile, 0)


def grad_attended_kernel(plan, branch_ref, w_ref, wide_ref, do_ref):
    rows = branch_ref.shape[0]
    lane = lanes_of(rows)
    grad = nt(branch_ref[...], w_ref[...]).astype(bf16)
    terms = grad.astype(f32) * wide_ref[...]
    out = grad
    for h in range(plan.heads):
        row_term = jnp.sum(
            jnp.where(lane // 64 == h + 1, terms, 0.0), axis=1, keepdims=True
        )
        for i, part in enumerate(split3(-row_term)):
            out = jnp.where(lane == 3 * h + i, part, out)
    do_ref[...] = out


vmem = pl.BlockSpec(memory_space=pltpu.VMEM)
smem = pl.BlockSpec(memory_space=pltpu.SMEM)


def params():
    return pltpu.CompilerParams(vmem_limit_bytes=56 * 2**20)


class Spot:
    def __init__(self, lines):
        index = lax.axis_index("ctx")
        self.wa = lax.axis_index("wa")
        self.index = index
        self.lines = lines
        self.z = index // 4
        self.x = (index // 2) % 2
        self.core = index % 2

    def core_mate(self):
        return (self.index + 1 - 2 * self.core, self.wa)

    def x_mate(self):
        return (self.index + 2 - 4 * self.x, self.wa)

    def z_mate(self, step):
        return (jnp.clip(self.index + 4 * step, 0, 4 * self.lines - 1), self.wa)

    def y_mate(self):
        return (self.index, 1 - self.wa)


def send(src, dst, send_sem, recv_sem, device):
    return pltpu.make_async_remote_copy(
        src_ref=src,
        dst_ref=dst,
        send_sem=send_sem,
        recv_sem=recv_sem,
        device_id=device,
        device_id_type=pl.DeviceIdType.MESH,
    )


def greet(spot, with_y):
    barrier = pltpu.get_barrier_semaphore()
    mates = [spot.core_mate(), spot.x_mate()] + ([spot.y_mate()] if with_y else [])
    for mate in mates:
        pl.semaphore_signal(barrier, inc=1, device_id=mate, device_id_type=pl.DeviceIdType.MESH)

    @pl.when(spot.z + 1 < spot.lines)
    def _():
        pl.semaphore_signal(
            barrier, inc=1, device_id=spot.z_mate(1), device_id_type=pl.DeviceIdType.MESH
        )

    @pl.when(spot.z > 0)
    def _():
        pl.semaphore_signal(
            barrier, inc=1, device_id=spot.z_mate(-1), device_id_type=pl.DeviceIdType.MESH
        )

    above = (spot.z + 1 < spot.lines).astype(jnp.int32)
    below = (spot.z > 0).astype(jnp.int32)
    pl.semaphore_wait(barrier, len(mates) + above + below)


def added(a, b):
    return (a.astype(f32) + b.astype(f32)).astype(bf16)


def scatter_kernel(lines, units, z_first, *refs):
    count = 3
    parts, outs = (refs[:count], refs[count : 2 * count])
    mine, core_in, x_in, up_in, down_in, load_sem, core_sem, x_sem, up_sem, down_sem = refs[
        2 * count :
    ]
    spot = Spot(lines)
    z, x, core = (spot.z, spot.x, spot.core)
    greet(spot, False)
    loads = []
    cores = []
    order = z_first + [u for u in range(len(units)) if u not in z_first]

    def rows_of(u):
        return pl.ds(units[u][1], units[u][2])

    for u in order:
        m = units[u][0]
        load = pltpu.make_async_copy(
            parts[m].at[:, :, core, rows_of(u)], mine.at[m, :, :, rows_of(u)], load_sem.at[u]
        )
        load.start()
        loads.append(load)
        copy = send(
            parts[m].at[:, :, 1 - core, rows_of(u)],
            core_in.at[m, :, :, rows_of(u)],
            core_sem.at[0, u],
            core_sem.at[1, u],
            spot.core_mate(),
        )
        copy.start()
        cores.append(copy)

    def add_slices(into, source, u, x_slot):
        m = units[u][0]

        def body(line, unused):
            at = (m, line, x_slot, rows_of(u))
            into[at] = added(into[at], source[at])
            return unused

        lax.fori_loop(0, lines, body, 0)

    def x_copy(u, both):
        m = units[u][0]
        if both:
            src = mine.at[m, :, 1 - x, rows_of(u)]
            dst = x_in.at[m, :, rows_of(u)]
        else:
            src = mine.at[m, z, 1 - x, rows_of(u)]
            dst = x_in.at[m, z, rows_of(u)]
        return send(src, dst, x_sem.at[0, u], x_sem.at[1, u], spot.x_mate())

    def line_flow(u, slots):
        m = units[u][0]
        n = len(slots)

        def slot_copies(step, d):
            ring, sem = (up_in, up_sem) if step > 0 else (down_in, down_sem)
            return [
                send(
                    mine.at[m, d, s, rows_of(u)],
                    ring.at[m, d, s, rows_of(u)],
                    sem.at[0, u, d, i],
                    sem.at[1, u, d, i],
                    spot.z_mate(step),
                )
                for i, s in enumerate(slots)
            ]

        def receive(step, d):
            ring = up_in if step > 0 else down_in
            for copy, s in zip(slot_copies(step, d), slots):
                copy.wait_recv()
                at = (m, d, s, rows_of(u))
                mine[at] = added(mine[at], ring[at])

        def ends_first():
            @pl.when(z == 0)
            def _():
                for d in range(lines - 1, 0, -1):
                    for copy in slot_copies(1, d):
                        copy.start()

            @pl.when(z == lines - 1)
            def _():
                for d in range(lines - 1):
                    for copy in slot_copies(-1, d):
                        copy.start()

        def relay():
            def body(k, unused):
                high = lines - 1 - k

                @pl.when((z < high) & (z > 0))
                def _():
                    receive(1, high)
                    for copy in slot_copies(1, high):
                        copy.start()

                @pl.when((z > k) & (z + 1 < lines))
                def _():
                    receive(-1, k)
                    for copy in slot_copies(-1, k):
                        copy.start()

                return unused

            lax.fori_loop(0, lines - 1, body, 0)

        def arrive():
            @pl.when(z > 0)
            def _():
                receive(1, z)

            @pl.when(z + 1 < lines)
            def _():
                receive(-1, z)

        def finish(k, unused):
            @pl.when(z < lines - 1 - k)
            def _():
                for copy in slot_copies(1, lines - 1 - k):
                    copy.wait_send()

            @pl.when(z > k)
            def _():
                for copy in slot_copies(-1, k):
                    copy.wait_send()

            return unused

        return (
            ends_first,
            relay,
            arrive,
            lambda: lax.fori_loop(0, lines - 1, finish, 0),
        )

    def store(u):
        m = units[u][0]
        outs[m][rows_of(u), :] = mine[m, z, x, rows_of(u)].astype(f32)

    pending = {}
    for i, u in enumerate(order):
        loads[i].wait()
        cores[i].wait()
        if u in z_first:
            add_slices(mine, core_in, u, 0)
            add_slices(mine, core_in, u, 1)
        else:
            add_slices(mine, core_in, u, 1 - x)
            copy = x_copy(u, True)
            copy.start()
            pending[u] = copy
            add_slices(mine, core_in, u, x)
    x_first = [u for u in order if u not in z_first]
    flows = {u: line_flow(u, [0, 1] if u in z_first else [x]) for u in order}
    last = {}

    def x_stage(u):
        m = units[u][0]
        pending[u].wait()

        def body(line, unused):
            at = (m, line, x, rows_of(u))
            mine[at] = added(mine[at], x_in[m, line, rows_of(u)])
            return unused

        lax.fori_loop(0, lines, body, 0)

    def settle(u):
        flows[u][2]()
        if u in z_first:
            last[u] = x_copy(u, False)
            last[u].start()
        else:
            store(u)

    for t in range(len(order) + 2):
        if t < len(order):
            u = order[t]
            if u not in z_first:
                x_stage(u)
            flows[u][0]()
        if 0 <= t - 1 < len(order):
            flows[order[t - 1]][1]()
        if 0 <= t - 2 < len(order):
            settle(order[t - 2])
    for u, copy in last.items():
        m = units[u][0]
        copy.wait()
        at = (m, z, x, rows_of(u))
        mine[at] = added(mine[at], x_in[m, z, rows_of(u)])
        store(u)
    for u in order:
        flows[u][3]()


def reduce_scatter(parts, cycle_size):
    lines = cycle_size // 4
    units_here, model = parts[0].shape
    rows = units_here // cycle_size
    cut = (rows // 2 + 15) // 16 * 16
    pieces = [(0, cut), (cut, rows - cut)] if cut < rows else [(0, rows)]
    units = [(m, at, size) for m in range(3) for at, size in pieces]
    z_first = [len(units) - 1]
    shaped = [part.reshape(lines, 2, 2, rows, model) for part in parts]
    hbm = pl.BlockSpec(memory_space=pl.ANY)
    n = len(units)
    return pl.pallas_call(
        functools.partial(scatter_kernel, lines, units, z_first),
        out_shape=[jax.ShapeDtypeStruct((rows, model), f32)] * 3,
        in_specs=[hbm] * 3,
        out_specs=[vmem] * 3,
        scratch_shapes=[
            pltpu.VMEM((3, lines, 2, rows, model), bf16),
            pltpu.VMEM((3, lines, 2, rows, model), bf16),
            pltpu.VMEM((3, lines, rows, model), bf16),
            pltpu.VMEM((3, lines, 2, rows, model), bf16),
            pltpu.VMEM((3, lines, 2, rows, model), bf16),
            pltpu.SemaphoreType.DMA((n,)),
            pltpu.SemaphoreType.DMA((2, n)),
            pltpu.SemaphoreType.DMA((2, n)),
            pltpu.SemaphoreType.DMA((2, n, lines, 2)),
            pltpu.SemaphoreType.DMA((2, n, lines, 2)),
        ],
        compiler_params=pltpu.CompilerParams(
            vmem_limit_bytes=58 * 2**20, collective_id=1, has_side_effects=True
        ),
        name="weight_scatter",
    )(*shaped)

def tn(a, b):
    return lax.dot_general(a, b, (((0,), (0,)), ((), ())), preferred_element_type=f32)


def line_relay(spot, start, receive):
    def level(k, unused):
        @pl.when(spot.z - k >= 0)
        def _():
            if_first(k, lambda: receive(1, spot.z - k))

            @pl.when(spot.z + 1 < spot.lines)
            def _():
                start(1, spot.z - k)

        @pl.when(spot.z + k < spot.lines)
        def _():
            if_first(k, lambda: receive(-1, spot.z + k))

            @pl.when(spot.z > 0)
            def _():
                start(-1, spot.z + k)

        return unused

    def if_first(k, run):
        @pl.when(k > 0)
        def _():
            run()

    return level


def finish_kernel(
    plan, lines, dq_ref, dk_ref, dv_ref, mask_ref, w3_ref, normed_ref, att_ref, branch_ref,
    tokens_ref, gain_ref, hidden_ref, gh_ref, ffn_ref, small_ref,
    out_ref, gt_ref, gm_ref, weights_ref, total_ref,
    mine, core_in, x_in, up_in, down_in, all_w, y_out, y_in, own_part, ffn_in, mask_in,
    small_own, small_y, small_core, small_x, small_all,
    y_sem, core_sem, x_sem, up_sem, down_sem, gz_sem, gx_sem, gc_sem, sz_sem,
):
    spot = Spot(lines)
    z, x, core, wa = (spot.z, spot.x, spot.core, spot.wa)
    greet(spot, True)
    half = tokens_ref.shape[0]
    quarter = half // 2
    model = tokens_ref.shape[1]
    rows = mine.shape[3]

    def grad_rows(at):
        at = pl.ds(pl.multiple_of(at, quarter), quarter)
        return (
            nt(dq_ref[at, :], w3_ref[:, 0:256])
            + nt(dk_ref[at, :], w3_ref[:, 256:512])
            + nt(dv_ref[at, :], w3_ref[:, 512:768])
        )

    def y_copy(i):
        return send(y_out.at[i], y_in.at[i], y_sem.at[0, i], y_sem.at[1, i], spot.y_mate())

    def theirs(i, unused):
        y_out[i] = grad_rows((1 - wa) * half + i * quarter).astype(bf16)
        y_copy(i).start()
        return unused

    lax.fori_loop(0, 2, theirs, 0)
    mask_copy = send(
        mask_ref.at[1 - wa], mask_in, y_sem.at[0, 2], y_sem.at[1, 2], spot.y_mate()
    )
    mask_copy.start()

    def fill(product, matrix):
        for j in range(plan.cols // rows):
            s = matrix * (plan.cols // rows) + j
            mine[s // 4, (s // 2) % 2, s % 2] = product[j * rows : (j + 1) * rows].astype(bf16)

    fill(tn(dq_ref[...], normed_ref[...])[: plan.cols], 0)
    fill(tn(dk_ref[...], normed_ref[...])[: plan.cols], 1)
    fill(tn(dv_ref[...], normed_ref[...])[64:], 2)
    fill(tn(att_ref[...], branch_ref[...])[64:], 3)
    core_copy = send(
        mine.at[:, :, 1 - core], core_in, core_sem.at[0, 0], core_sem.at[1, 0], spot.core_mate()
    )
    core_copy.start()
    their_rows = pl.ds(pl.multiple_of((1 - wa) * half, half), half)
    ffn_copy = send(
        ffn_ref.at[their_rows], ffn_in, y_sem.at[0, 3], y_sem.at[1, 3], spot.y_mate()
    )
    ffn_copy.start()

    def ours(i, unused):
        own_part[pl.ds(pl.multiple_of(i * quarter, quarter), quarter), :] = grad_rows(
            wa * half + i * quarter
        )
        return unused

    lax.fori_loop(0, 2, ours, 0)
    core_copy.wait()

    def x_copy(d):
        return send(
            mine.at[d, 1 - x, core], x_in.at[d], x_sem.at[0, d], x_sem.at[1, d], spot.x_mate()
        )

    def core_add(d, unused):
        mine[d, 1 - x, core] = added(mine[d, 1 - x, core], core_in[d, 1 - x])
        x_copy(d).start()
        return unused

    lax.fori_loop(0, lines, core_add, 0)

    def core_add_own(d, unused):
        mine[d, x, core] = added(mine[d, x, core], core_in[d, x])
        return unused

    lax.fori_loop(0, lines, core_add_own, 0)

    gain_sum = jnp.zeros((1, model), f32)
    step = 32
    for i in range(2):
        y_copy(i).wait()

        def normal(j, total, i=i):
            at = pl.ds(pl.multiple_of(i * quarter + j * step, step), step)
            there = pl.ds(pl.multiple_of(j * step, step), step)
            grad = own_part[at, :] + y_in[i, there, :].astype(f32)
            rows_in = tokens_ref[at, :].astype(f32)
            inv = lax.rsqrt(jnp.mean(rows_in * rows_in, axis=-1, keepdims=True) + eps)
            scaled = gain_ref[...] * grad
            mean = jnp.mean(rows_in * scaled, axis=-1, keepdims=True)
            gt_ref[at, :] = gh_ref[at, :] + inv * scaled - rows_in * (inv * inv * inv * mean)
            return total + jnp.sum(grad * rows_in * inv, axis=0, keepdims=True)

        gain_sum = lax.fori_loop(0, quarter // step, normal, gain_sum)
    small_own[...] = small_ref[...]
    small_own[0:1, :] = gain_sum
    small_copy = send(
        small_own, small_y, y_sem.at[0, 4], y_sem.at[1, 4], spot.y_mate()
    )
    small_copy.start()
    mask_copy.wait()
    gm_ref[...] = mask_ref[wa] + mask_in[...]

    def flow(step, d):
        ring, sem = (up_in, up_sem) if step > 0 else (down_in, down_sem)
        return send(
            mine.at[d, x, core], ring.at[d], sem.at[0, d], sem.at[1, d], spot.z_mate(step)
        )

    def merge(step, d):
        flow(step, d).wait_recv()
        ring = up_in if step > 0 else down_in
        mine[d, x, core] = added(mine[d, x, core], ring[d])

    def x_add(d, unused):
        x_copy(d).wait()
        mine[d, x, core] = added(mine[d, x, core], x_in[d])

        @pl.when((z == 0) & (d > 0))
        def _():
            flow(1, d).start()

        @pl.when((z == lines - 1) & (d < lines - 1))
        def _():
            flow(-1, d).start()

        return unused

    lax.fori_loop(0, lines, x_add, 0)
    small_copy.wait()
    row = lax.broadcasted_iota(jnp.int32, small_own.shape, 0)
    small_x[0] = small_own[...] + jnp.where(row < 2, small_y[...], 0.0)
    small_core_copy = send(
        small_x.at[0], small_core, core_sem.at[0, 1], core_sem.at[1, 1], spot.core_mate()
    )
    small_core_copy.start()

    def relay(k, unused):
        high = lines - 1 - k

        @pl.when((z < high) & (z > 0))
        def _():
            merge(1, high)
            flow(1, high).start()

        @pl.when((z > k) & (z + 1 < lines))
        def _():
            merge(-1, k)
            flow(-1, k).start()

        return unused

    lax.fori_loop(0, lines - 1, relay, 0)
    small_core_copy.wait()
    small_x[1] = small_x[0] + small_core[...]
    small_x_copy = send(
        small_x.at[1], small_x.at[2], x_sem.at[0, lines], x_sem.at[1, lines], spot.x_mate()
    )
    small_x_copy.start()

    @pl.when(z > 0)
    def _():
        merge(1, z)

    @pl.when(z + 1 < lines)
    def _():
        merge(-1, z)

    all_w[z, x, core] = mine[z, x, core]

    def pass_w(step, d):
        i = 0 if step > 0 else 1
        return send(
            all_w.at[d, x, core], all_w.at[d, x, core], gz_sem.at[i, d], gz_sem.at[2 + i, d],
            spot.z_mate(step),
        )

    def pass_s(step, d):
        i = 0 if step > 0 else 1
        return send(
            small_all.at[d], small_all.at[d], sz_sem.at[i, d], sz_sem.at[2 + i, d],
            spot.z_mate(step),
        )

    def across(d):
        return send(
            all_w.at[d, x, core], all_w.at[d, x, core], gx_sem.at[0, d], gx_sem.at[1, d],
            spot.x_mate(),
        )

    def beside(d):
        return send(
            all_w.at[d, :, core], all_w.at[d, :, core], gc_sem.at[0, d], gc_sem.at[1, d],
            spot.core_mate(),
        )

    small_x_copy.wait()
    small_all[z] = small_x[1] + small_x[2]

    def receive(step, d):
        pass_w(step, d).wait_recv()
        across(d).start()

    across(z).start()
    lax.fori_loop(
        0, lines, line_relay(spot, lambda s, d: pass_w(s, d).start(), receive), 0
    )
    lax.fori_loop(
        0,
        lines,
        line_relay(
            spot, lambda s, d: pass_s(s, d).start(), lambda s, d: pass_s(s, d).wait_recv()
        ),
        0,
    )

    def add_small(d, total):
        return total + small_all[d]

    total_ref[...] = lax.fori_loop(1, lines, add_small, small_all[0])
    ffn_copy.wait()

    def last(j, unused):
        at = pl.ds(pl.multiple_of(j * step, step), step)
        here = pl.ds(pl.multiple_of(wa * half + j * step, step), step)
        total = hidden_ref[at, :] + ffn_ref[here, :].astype(f32) + ffn_in[at, :].astype(f32)
        out_ref[at, :] = total.astype(bf16)
        return unused

    lax.fori_loop(0, half // step, last, 0)

    def spread(d, unused):
        across(d).wait()
        beside(d).start()
        return unused

    lax.fori_loop(0, lines, spread, 0)

    def copy_out(d, unused):
        beside(d).wait()
        weights_ref[d] = all_w[d]
        return unused

    lax.fori_loop(0, lines, copy_out, 0)

    def drain(d, unused):
        @pl.when((z < d))
        def _():
            flow(1, d).wait_send()

        @pl.when((z > d))
        def _():
            flow(-1, d).wait_send()

        @pl.when((d <= z) & (z + 1 < lines))
        def _():
            pass_w(1, d).wait_send()
            pass_s(1, d).wait_send()

        @pl.when((d >= z) & (z > 0))
        def _():
            pass_w(-1, d).wait_send()
            pass_s(-1, d).wait_send()

        return unused

    lax.fori_loop(0, lines, drain, 0)


def finish(plan, cycle_size, *operands):
    lines = cycle_size // 4
    half, model = operands[8].shape
    rows = 4 * plan.cols // cycle_size
    dma = pltpu.SemaphoreType.DMA
    return pl.pallas_call(
        functools.partial(finish_kernel, plan, lines),
        out_shape=[
            jax.ShapeDtypeStruct((half, model), bf16),
            jax.ShapeDtypeStruct((half, model), f32),
            jax.ShapeDtypeStruct((8, half), f32),
            jax.ShapeDtypeStruct((lines, 2, 2, rows, model), bf16),
            jax.ShapeDtypeStruct((8, model), f32),
        ],
        in_specs=[vmem] * len(operands),
        out_specs=[vmem] * 5,
        scratch_shapes=[
            pltpu.VMEM((lines, 2, 2, rows, model), bf16),
            pltpu.VMEM((lines, 2, rows, model), bf16),
            pltpu.VMEM((lines, rows, model), bf16),
            pltpu.VMEM((lines, rows, model), bf16),
            pltpu.VMEM((lines, rows, model), bf16),
            pltpu.VMEM((lines, 2, 2, rows, model), bf16),
            pltpu.VMEM((2, half // 2, model), bf16),
            pltpu.VMEM((2, half // 2, model), bf16),
            pltpu.VMEM((half, model), f32),
            pltpu.VMEM((half, model), bf16),
            pltpu.VMEM((8, half), f32),
            pltpu.VMEM((8, model), f32),
            pltpu.VMEM((8, model), f32),
            pltpu.VMEM((8, model), f32),
            pltpu.VMEM((3, 8, model), f32),
            pltpu.VMEM((lines, 8, model), f32),
            dma((2, 5)),
            dma((2, 2)),
            dma((2, lines + 1)),
            dma((2, lines)),
            dma((2, lines)),
            dma((4, lines)),
            dma((2, lines)),
            dma((2, lines)),
            dma((4, lines)),
        ],
        compiler_params=pltpu.CompilerParams(
            vmem_limit_bytes=58 * 2**20, collective_id=2, has_side_effects=True
        ),
        name="finish",
    )(*operands)


root = 0.7978845608028654
cubic = 0.044715


def middle_kernel(
    plan, cycle_size, att_ref, mixed_ref, wout_ref, tokens_ref, cot_ref, gain_ref,
    wg_hbm, wu_hbm, wd_hbm,
    hidden_ref, gh_ref, branch_ref, ffn_ref, do_ref, gain_part_ref, stack_hbm,
    wg, wu, wd, inner, gg, gu, x_ref, a_out, a_in, d_out, d_in, acc_f, acc_g, own_g, rows_buf,
    load_sem, y_sem, out_sem,
):
    spot = Spot(cycle_size // 4)
    wa = spot.wa
    half, model = tokens_ref.shape
    units = wd.shape[0]
    chunk = half // 4
    loads = [
        pltpu.make_async_copy(src, dst, load_sem.at[i])
        for i, (src, dst) in enumerate(((wg_hbm, wg), (wu_hbm, wu), (wd_hbm, wd)))
    ]
    for load in loads:
        load.start()
    barrier = pltpu.get_barrier_semaphore()
    pl.semaphore_signal(
        barrier, inc=1, device_id=spot.y_mate(), device_id_type=pl.DeviceIdType.MESH
    )
    pl.semaphore_wait(barrier, 1)
    ours = wa * half
    theirs = (1 - wa) * half

    def rows_at(start, size):
        return pl.ds(pl.multiple_of(start, size), size)

    def a_copy(i):
        return send(a_out.at[i], a_in.at[i], y_sem.at[0, i], y_sem.at[1, i], spot.y_mate())

    def d_copy(i):
        return send(
            d_out.at[i], d_in.at[i], y_sem.at[0, 4 + i], y_sem.at[1, 4 + i], spot.y_mate()
        )

    def b_copy(i, base):
        at = rows_at(base + i * chunk, chunk)
        return send(
            x_ref.at[at], x_ref.at[at], y_sem.at[0, 8 + i], y_sem.at[1, 8 + i], spot.y_mate()
        )

    def e_copy(i, base):
        at = rows_at(base + i * chunk, chunk)
        return send(
            branch_ref.at[at], branch_ref.at[at], y_sem.at[0, 12 + i], y_sem.at[1, 12 + i],
            spot.y_mate(),
        )

    def send_branch(i, unused):
        a_out[i] = nn(att_ref[rows_at(theirs + i * chunk, chunk), :], wout_ref[...]).astype(bf16)
        a_copy(i).start()
        return unused

    lax.fori_loop(0, 4, send_branch, 0)

    def own_branch(i, unused):
        at = rows_at(i * chunk, chunk)
        hidden_ref[at, :] = tokens_ref[at, :].astype(f32) + nn(
            att_ref[rows_at(ours + i * chunk, chunk), :], wout_ref[...]
        )
        return unused

    lax.fori_loop(0, 4, own_branch, 0)

    def normal(i, unused):
        a_copy(i).wait()
        at = rows_at(i * chunk, chunk)
        hidden = hidden_ref[at, :] + a_in[i].astype(f32)
        hidden_ref[at, :] = hidden
        inv = lax.rsqrt(jnp.mean(hidden * hidden, axis=-1, keepdims=True) + eps)
        x_ref[rows_at(ours + i * chunk, chunk), :] = (hidden * inv * gain_ref[...]).astype(bf16)
        b_copy(i, ours).start()
        return unused

    lax.fori_loop(0, 4, normal, 0)
    for load in loads:
        load.wait()
    wide = 256

    def feed(base):
        rows = rows_at(base, half)
        acc_f[...] = jnp.zeros_like(acc_f)
        acc_g[...] = jnp.zeros_like(acc_g)

        def tile(u, unused):
            cols = rows_at(u * wide, wide)
            gate = nn(x_ref[rows, :], wg[:, cols])
            upward = nn(x_ref[rows, :], wu[:, cols])
            grad_inner = nt(cot_ref[rows, :], wd[cols, :])
            square = gate * gate
            bend = jnp.tanh(root * gate * (1.0 + cubic * square))
            side = 0.5 * (1.0 + bend)
            gelu = gate * side
            slope = side + 0.5 * gate * (1.0 - bend * bend) * (
                root * (1.0 + 3.0 * cubic * square)
            )
            inner_low = (gelu * upward).astype(bf16)
            gate_low = (grad_inner * upward * slope).astype(bf16)
            up_low = (grad_inner * gelu).astype(bf16)
            inner[rows, cols] = inner_low
            gg[rows, cols] = gate_low
            gu[rows, cols] = up_low
            acc_g[...] += nt(gate_low, wg[:, cols]) + nt(up_low, wu[:, cols])
            acc_f[...] += nn(inner_low, wd[cols, :])
            return unused

        lax.fori_loop(0, units // wide, tile, 0)
        ffn_ref[rows, :] = acc_f[...].astype(bf16)

    feed(ours)
    own_g[...] = acc_g[...]

    def b_wait(i, unused):
        b_copy(i, theirs).wait_recv()
        return unused

    lax.fori_loop(0, 4, b_wait, 0)
    feed(theirs)

    def send_grad(i, unused):
        d_out[i] = acc_g[rows_at(i * chunk, chunk), :].astype(bf16)
        d_copy(i).start()
        return unused

    lax.fori_loop(0, 4, send_grad, 0)
    parts = 2
    span = units // parts
    slices = cycle_size // parts
    size = units // cycle_size

    def out_copy(n):
        m, p = (n // parts, n % parts)
        return pltpu.make_async_copy(
            rows_buf.at[n % 2],
            stack_hbm.at[pl.ds(p * slices, slices), m],
            out_sem.at[n],
        )

    for n in range(3 * parts):
        m, p = (n // parts, n % parts)
        left = (inner, gg, gu)[m]
        right = (cot_ref, x_ref, x_ref)[m]
        if n >= 2:
            out_copy(n - 2).wait()
        turned = jnp.transpose(left[:, p * span : (p + 1) * span])
        for c in range(0, model, wide):
            end = min(model, c + wide)
            product = nn(turned, right[:, c:end]).astype(bf16)
            for s in range(slices):
                rows_buf[n % 2, s, :, c:end] = product[s * size : (s + 1) * size]
        out_copy(n).start()

    def normal_back(i, total):
        d_copy(i).wait()
        at = rows_at(i * chunk, chunk)
        grad = own_g[at, :] + d_in[i].astype(f32)
        hidden = hidden_ref[at, :]
        inv = lax.rsqrt(jnp.mean(hidden * hidden, axis=-1, keepdims=True) + eps)
        scaled = gain_ref[...] * grad
        mean = jnp.mean(hidden * scaled, axis=-1, keepdims=True)
        pair_at = rows_at(ours + i * chunk, chunk)
        grad_hidden = (
            cot_ref[pair_at, :].astype(f32) + inv * scaled - hidden * (inv * inv * inv * mean)
        )
        gh_ref[at, :] = grad_hidden
        branch_ref[pair_at, :] = grad_hidden.astype(bf16)
        e_copy(i, ours).start()
        return total + jnp.sum(grad * hidden * inv, axis=0, keepdims=True)

    gain_part_ref[...] = lax.fori_loop(0, 4, normal_back, jnp.zeros((1, model), f32))

    def attended_grads(base):
        rows = rows_at(base, half)
        lane = lanes_of(half)
        grad = nt(branch_ref[rows, :], wout_ref[...]).astype(bf16)
        terms = grad.astype(f32) * mixed_ref[rows, :]
        out = grad
        for h in range(plan.heads):
            row_term = jnp.sum(
                jnp.where(lane // 64 == h + 1, terms, 0.0), axis=1, keepdims=True
            )
            for i, part in enumerate(split3(-row_term)):
                out = jnp.where(lane == 3 * h + i, part, out)
        do_ref[rows, :] = out

    attended_grads(ours)

    def e_wait(i, unused):
        e_copy(i, theirs).wait_recv()
        return unused

    lax.fori_loop(0, 4, e_wait, 0)
    attended_grads(theirs)
    for n in (3 * parts - 2, 3 * parts - 1):
        out_copy(n).wait()

    def drain(i, unused):
        b_copy(i, ours).wait_send()
        e_copy(i, ours).wait_send()
        return unused

    lax.fori_loop(0, 4, drain, 0)


def middle(plan, cycle_size, attended, mixed, w_out, tokens, cot, gain, w_gate, w_up, w_down):
    half, model = tokens.shape
    pair = attended.shape[0]
    units = w_down.shape[0]
    size = units // cycle_size
    chunk = half // 4
    hbm = pl.BlockSpec(memory_space=pl.ANY)
    dma = pltpu.SemaphoreType.DMA
    return pl.pallas_call(
        functools.partial(middle_kernel, plan, cycle_size),
        out_shape=[
            jax.ShapeDtypeStruct((half, model), f32),
            jax.ShapeDtypeStruct((half, model), f32),
            jax.ShapeDtypeStruct((pair, model), bf16),
            jax.ShapeDtypeStruct((pair, model), bf16),
            jax.ShapeDtypeStruct((pair, WIDE), bf16),
            jax.ShapeDtypeStruct((1, model), f32),
            jax.ShapeDtypeStruct((cycle_size, 3, size, model), bf16),
        ],
        in_specs=[vmem] * 6 + [hbm] * 3,
        out_specs=[vmem] * 6 + [hbm],
        scratch_shapes=[
            pltpu.VMEM((model, units), bf16),
            pltpu.VMEM((model, units), bf16),
            pltpu.VMEM((units, model), bf16),
            pltpu.VMEM((pair, units), bf16),
            pltpu.VMEM((pair, units), bf16),
            pltpu.VMEM((pair, units), bf16),
            pltpu.VMEM((pair, model), bf16),
            pltpu.VMEM((4, chunk, model), bf16),
            pltpu.VMEM((4, chunk, model), bf16),
            pltpu.VMEM((4, chunk, model), bf16),
            pltpu.VMEM((4, chunk, model), bf16),
            pltpu.VMEM((half, model), f32),
            pltpu.VMEM((half, model), f32),
            pltpu.VMEM((half, model), f32),
            pltpu.VMEM((2, cycle_size // 2, size, model), bf16),
            dma((3,)),
            dma((2, 16)),
            dma((6,)),
        ],
        compiler_params=pltpu.CompilerParams(
            vmem_limit_bytes=60 * 2**20, collective_id=3, has_side_effects=True
        ),
        name="feed_forward",
    )(attended, mixed, w_out, tokens, cot, gain, w_gate, w_up, w_down)


def shards(
    tokens,
    doc_lengths,
    key_mask,
    gain_attn,
    w_query,
    w_key,
    w_value,
    w_out,
    bias_table,
    gain_ffn,
    w_gate,
    w_up,
    w_down,
    cotangent,
):
    own_rows, model = tokens.shape
    group = lax.axis_size("wa")
    cycle_size = lax.axis_size("ctx")
    pair = own_rows * group
    heads = bias_table.shape[1]
    docs = doc_lengths.shape[0]
    plan = Plan(heads, w_query.shape[1] // heads, docs)
    total_rows = pair * cycle_size
    doc_most = min(MAXLEN, total_rows // 2)
    reach = min(cycle_size - 1, (doc_most - 1) // pair + 1)
    base = lax.axis_index("ctx") * pair
    rows = min(total_rows, (2 * reach + 1) * pair)
    origin = jnp.clip(base - reach * pair, 0, total_rows - rows).astype(jnp.int32)
    ends = jnp.cumsum(doc_lengths).astype(jnp.int32)
    starts = ends - doc_lengths

    def doc_at(positions):
        return jnp.sum((positions[:, None] >= starts[None, :]).astype(jnp.int32), axis=1) - 1

    tiles = pair // TQ
    tile_start = base + TQ * jnp.arange(tiles, dtype=jnp.int32)
    first_doc = jnp.arange(docs, dtype=jnp.int32)[None, :] == doc_at(tile_start)[:, None]
    last_doc = jnp.arange(docs, dtype=jnp.int32)[None, :] == doc_at(tile_start + TQ - 1)[:, None]
    low_end = jnp.sum(jnp.where(first_doc, starts[None, :], 0), axis=1)
    high_end = jnp.sum(jnp.where(last_doc, ends[None, :], 0), axis=1)
    n_left = jnp.maximum(0, (tile_start - EDGE - low_end + TK - 1) // TK)
    n_right = jnp.maximum(0, (high_end - (tile_start - EDGE + TK) + TK - 1) // TK)
    bounds = jnp.concatenate(
        [(base - origin)[None], jnp.stack([n_left, n_right], axis=1).reshape(-1)]
    ).astype(jnp.int32)

    mask_all = lax.all_gather(key_mask, "ctx", axis=0, tiled=True)
    tokens_wide = tokens.astype(f32)
    normed_attn, inv_attn = norm_forward(tokens_wide, gain_attn)
    normed_low = normed_attn.astype(bf16)
    pair_normed, pair_cot = (
        lax.all_gather(normed_low, "wa", axis=0, tiled=True),
        lax.all_gather(cotangent, "wa", axis=0, tiled=True),
    )
    w_kv = jnp.concatenate([w_key, w_value], axis=1)
    own_kv = jnp.dot(pair_normed, w_kv, preferred_element_type=f32).astype(bf16)
    queries = jnp.dot(pair_normed, w_query, preferred_element_type=f32).astype(bf16)

    def window(gathered):
        if rows == total_rows:
            return gathered
        return lax.dynamic_slice_in_dim(gathered, origin, rows, 0)

    gather = functools.partial(lax.all_gather, axis_name="ctx", axis=0, tiled=True)
    kv_all = window(gather(own_kv))
    positions = origin + jnp.arange(rows, dtype=jnp.int32)
    doc_of = doc_at(positions)
    lane = jnp.arange(128, dtype=jnp.int32)[None, :] + 128
    code = lane - plan.doc_lane
    bit_differs = ((doc_of[:, None] >> (code >> 1)) & 1) != (code & 1)
    k_aug = jnp.where(
        lane == plan.mask_lane,
        window(mask_all).astype(f32)[:, None],
        jnp.where(
            lane < plan.stat_lane,
            jnp.where(bit_differs & (code >= 0), neg_big, 0.0),
            (lane < plan.stat_lane + 3 * heads).astype(f32),
        ),
    ).astype(bf16)
    own_docs = doc_at(base + jnp.arange(pair, dtype=jnp.int32))
    own_differs = ((own_docs[:, None] >> (code >> 1)) & 1) != (code & 1)
    q_aug = jnp.where(
        lane == plan.mask_lane, 1.0, ((lane < plan.stat_lane) & ~own_differs).astype(f32)
    ).astype(bf16)
    q_wide = jnp.concatenate(
        [queries, q_aug[:, plan.cols - 128 :]], axis=1
    )
    near_bias = pl.pallas_call(
        functools.partial(near_kernel, heads),
        out_shape=jax.ShapeDtypeStruct((2, heads, TQ, TK), f32),
        in_specs=[smem],
        out_specs=vmem,
        compiler_params=params(),
        name="near_bias",
    )(bias_table)

    padded = rows + 2 * PAD
    attended, mixed, q_back = pl.pallas_call(
        functools.partial(fwd_kernel, plan, rows, pair),
        out_shape=(
            jax.ShapeDtypeStruct((pair, WIDE), bf16),
            jax.ShapeDtypeStruct((pair, WIDE), f32),
            jax.ShapeDtypeStruct((pair, WIDE), bf16),
        ),
        in_specs=[smem, smem, vmem, vmem, vmem, vmem],
        out_specs=(vmem, vmem, vmem),
        scratch_shapes=[
            pltpu.VMEM((padded, WIDE), bf16),
            pltpu.VMEM((padded, WIDE), bf16),
            pltpu.VMEM((heads, TQ, WIDE), f32),
            pltpu.VMEM((heads, TQ, 128), f32),
            pltpu.VMEM((heads, TQ, WIDE), bf16),
        ],
        compiler_params=params(),
        name="attention_forward",
    )(bounds, bias_table, kv_all, k_aug, q_wide, near_bias)
    q_all = window(gather(q_back))
    w_out_pad = jnp.concatenate([jnp.zeros((64, model), bf16), w_out], axis=0)
    hidden, grad_hidden, pair_branch, ffn_part, do_wide, gain_ffn_part, stacked = middle(
        plan,
        cycle_size,
        attended,
        mixed,
        w_out_pad,
        tokens,
        pair_cot,
        gain_ffn[None],
        w_gate,
        w_up,
        w_down,
    )
    units = stacked.shape[2]
    stacked = lax.psum_scatter(
        stacked.reshape(-1, model), "ctx", scatter_dimension=0, tiled=True
    ).astype(f32)
    grad_w_down = stacked[:units]
    grad_w_gate, grad_w_up = (stacked[units : 2 * units].T, stacked[2 * units :].T)
    do_all = window(gather(do_wide))

    grad_queries, table_part = pl.pallas_call(
        functools.partial(dq_kernel, plan, rows, pair),
        out_shape=(
            jax.ShapeDtypeStruct((pair, WIDE), bf16),
            jax.ShapeDtypeStruct((heads, 32, 128), f32),
        ),
        in_specs=[smem, smem, vmem, vmem, vmem, vmem, vmem],
        out_specs=(vmem, vmem),
        scratch_shapes=[
            pltpu.VMEM((padded, WIDE), bf16),
            pltpu.VMEM((padded, WIDE), bf16),
            pltpu.VMEM((heads, TQ, WIDE), f32),
            pltpu.VMEM((heads, TQ, WIDE), bf16),
            pltpu.VMEM((heads, TQ, WIDE), bf16),
            pltpu.VMEM((heads, TQ, TK), f32),
            pltpu.VMEM((2, heads, TQ, 128), f32),
        ],
        compiler_params=params(),
        name="attention_grad_queries",
    )(bounds, bias_table, kv_all, k_aug, q_back, do_wide, near_bias)
    own_aug = lax.dynamic_slice_in_dim(k_aug, base - origin, pair, 0)
    grad_keys, grad_values, mask_part = pl.pallas_call(
        functools.partial(dkv_kernel, plan, rows, pair),
        out_shape=(
            jax.ShapeDtypeStruct((pair, WIDE), bf16),
            jax.ShapeDtypeStruct((pair, WIDE), bf16),
            jax.ShapeDtypeStruct((tiles, 8, TQ), f32),
        ),
        in_specs=[smem, smem, vmem, vmem, vmem, vmem, vmem],
        out_specs=(vmem, vmem, vmem),
        scratch_shapes=[
            pltpu.VMEM((padded, WIDE), bf16),
            pltpu.VMEM((padded, WIDE), bf16),
            pltpu.VMEM((heads, TQ, WIDE), bf16),
            pltpu.VMEM((heads, TQ, WIDE), bf16),
            pltpu.VMEM((heads, TQ, WIDE), f32),
            pltpu.VMEM((heads, TQ, WIDE), f32),
        ],
        compiler_params=params(),
        name="attention_grad_keys",
    )(bounds, bias_table, q_all, do_all, own_kv, own_aug, near_bias)
    cols = plan.cols
    gap = jnp.zeros((model, WIDE - cols), bf16)
    w_wide = jnp.concatenate([w_query, gap, w_key, gap, gap, w_value], axis=1)
    table_row = jnp.sum(table_part, axis=2).reshape(1, -1)
    table_row = jnp.pad(table_row, ((0, 0), (0, model - table_row.shape[1])))
    small = jnp.concatenate(
        [jnp.zeros((1, model), f32), gain_ffn_part, table_row, jnp.zeros((5, model), f32)],
        axis=0,
    )
    layer_out, grad_tokens, grad_mask, weights, totals = finish(
        plan,
        cycle_size,
        grad_queries,
        grad_keys,
        grad_values,
        mask_part.reshape(group, 8, own_rows),
        w_wide,
        pair_normed,
        attended,
        pair_branch,
        tokens,
        gain_attn[None],
        hidden,
        grad_hidden,
        ffn_part,
        small,
    )
    weights = weights.reshape(4, cols, model).astype(f32)
    return (
        layer_out,
        grad_tokens,
        grad_mask[0],
        totals[0],
        weights[0].T,
        weights[1].T,
        weights[2].T,
        weights[3],
        totals[2, : heads * 32].reshape(heads, 32).T,
        totals[1],
        grad_w_gate,
        grad_w_up,
        grad_w_down,
    )


def solution(mesh):
    placed = (
        P(("ctx", "wa"), None),
        P(),
        P("ctx"),
        P(),
        P(None, "wa"),
        P(None, "wa"),
        P(None, "wa"),
        P("wa", None),
        P(None, "wa"),
        P(),
        P(None, "wa"),
        P(None, "wa"),
        P("wa", None),
        P(("ctx", "wa"), None),
    )
    return jax.shard_map(
        shards,
        mesh=mesh,
        in_specs=placed,
        out_specs=(
            P(("ctx", "wa"), None),
            P(("ctx", "wa"), None),
            P(("ctx", "wa")),
            P(),
            P(None, "wa"),
            P(None, "wa"),
            P(None, "wa"),
            P("wa", None),
            P(None, "wa"),
            P(),
            P(None, ("wa", "ctx")),
            P(None, ("wa", "ctx")),
            P(("wa", "ctx"), None),
        ),
        check_vma=False,
    )
```

```python
import functools

import jax
import jax.numpy as jnp
from jax import lax
from jax.experimental import pallas as pl
from jax.experimental.pallas import tpu as pltpu
from jax.sharding import PartitionSpec as P

MAXLEN = 8192

bucket_edges = (12, 16, 23, 32, 46, 64, 91)
neg_big = -1e30
eps = 1e-06
far_left_bucket = 15
far_right_bucket = 31
WIDE = 256
TQ = 256
TK = 512
EDGE = 128
PAD = TK + EDGE
f32 = jnp.float32
bf16 = jnp.bfloat16


def bucket_of(relative):
    distance = jnp.abs(relative)
    bucket = jnp.minimum(distance, 8) + 16 * (relative > 0).astype(jnp.int32)
    for edge in bucket_edges:
        bucket = bucket + (distance >= edge).astype(jnp.int32)
    return bucket


def norm_forward(inputs, gain):
    inv_root = lax.rsqrt(jnp.mean(inputs * inputs, axis=-1, keepdims=True) + eps)
    return (inputs * inv_root * gain, inv_root)


def norm_backward(inputs, inv_root, gain, grad_normed):
    scaled = gain * grad_normed
    cubed = inv_root * inv_root * inv_root
    grad_inputs = inv_root * scaled - inputs * cubed * jnp.mean(
        inputs * scaled, axis=-1, keepdims=True
    )
    grad_gain = jnp.sum(grad_normed * inputs * inv_root, axis=0)
    return (grad_inputs, grad_gain)


def gated(gate, upward):
    return jax.nn.gelu(gate, approximate=True) * upward


def nt(a, b):
    return lax.dot_general(a, b, (((1,), (1,)), ((), ())), preferred_element_type=f32)


def nn(a, b):
    return lax.dot_general(a, b, (((1,), (0,)), ((), ())), preferred_element_type=f32)


def split3(x):
    hi = x.astype(bf16)
    rest = x - hi.astype(f32)
    mid = rest.astype(bf16)
    return (hi, mid, (rest - mid.astype(f32)).astype(bf16))


class Plan:
    def __init__(self, heads, width, docs):
        self.heads = heads
        self.width = width
        self.bits = max(1, (docs - 1).bit_length())
        self.cols = heads * width
        self.mask_lane = self.cols
        self.doc_lane = self.cols + 1
        self.stat_lane = self.doc_lane + 2 * self.bits
        assert self.stat_lane + 3 * heads <= WIDE and self.cols + 64 == WIDE and width == 64

    def key_lanes(self, lane, h):
        own = (lane >= h * self.width) & (lane < (h + 1) * self.width)
        aug = (lane >= self.mask_lane) & (lane < self.stat_lane)
        stat = (lane >= self.stat_lane + 3 * h) & (lane < self.stat_lane + 3 * h + 3)
        return own | aug | stat

    def value_lanes(self, lane, h):
        own = (lane >= 64 + h * self.width) & (lane < 64 + (h + 1) * self.width)
        return own | ((lane >= 3 * h) & (lane < 3 * h + 3))


def lanes_of(rows, width=WIDE):
    return lax.broadcasted_iota(jnp.int32, (rows, width), 1)


def near_kernel(heads, table_ref, near_ref):
    row = lax.broadcasted_iota(jnp.int32, (EDGE, 3 * EDGE), 0)
    col = lax.broadcasted_iota(jnp.int32, (EDGE, 3 * EDGE), 1)
    relative = col - EDGE - row
    for flip in range(2):
        bucket = bucket_of(-relative if flip else relative)
        left, right = (far_left_bucket, far_right_bucket)
        if flip:
            left, right = (right, left)
        for h in range(heads):
            base = jnp.full((EDGE, 3 * EDGE), table_ref[0, h], f32)
            for b in range(1, 32):
                base = jnp.where(bucket == b, table_ref[b, h], base)
            far_l = jnp.full((EDGE, EDGE), table_ref[left, h], f32)
            far_r = jnp.full((EDGE, EDGE), table_ref[right, h], f32)
            near_ref[flip, h, :EDGE, : 3 * EDGE] = base
            near_ref[flip, h, :EDGE, 3 * EDGE :] = far_r
            near_ref[flip, h, EDGE:, EDGE:] = base
            near_ref[flip, h, EDGE:, :EDGE] = far_l


def build_keys(plan, g_ref, kaug_ref, km, vm, rows):
    km[:PAD, :] = jnp.broadcast_to(
        jnp.where(pad_lanes(plan), neg_big, 0.0).astype(bf16), (PAD, WIDE)
    )
    km[pl.ds(PAD + rows, PAD), :] = km[:PAD, :]
    vm[:PAD, :] = jnp.zeros((PAD, WIDE), bf16)
    vm[pl.ds(PAD + rows, PAD), :] = jnp.zeros((PAD, WIDE), bf16)
    step = 512
    low = lanes_of(step, 128) < 64
    ones = (lanes_of(step, 128) < 3 * plan.heads).astype(bf16)

    def body(n, unused):
        at = pl.multiple_of(n * step, step)
        to = pl.multiple_of(PAD + n * step, 128)
        middle = g_ref[pl.ds(at, step), 128:256]
        km[pl.ds(to, step), 0:128] = g_ref[pl.ds(at, step), 0:128]
        km[pl.ds(to, step), 128:256] = jnp.where(low, middle, kaug_ref[pl.ds(at, step), :])
        vm[pl.ds(to, step), 0:128] = jnp.where(low, ones, middle)
        vm[pl.ds(to, step), 128:256] = g_ref[pl.ds(at, step), 256:384]
        return unused

    lax.fori_loop(0, rows // step, body, 0)


def pad_lanes(plan):
    lane = lanes_of(1)
    return (lane >= plan.doc_lane) & (lane < plan.stat_lane)


def fwd_kernel(
    plan, rows, pair, bounds, table_ref, g_ref, kaug_ref, q_ref, near_ref,
    low_ref, wide_ref, qb_ref, km, vm, acc, row_max, qh_ref,
):
    build_keys(plan, g_ref, kaug_ref, km, vm, rows)
    lane = lanes_of(TQ)

    def tile(t, unused):
        start = pl.multiple_of(bounds[0] + t * TQ, 128)
        n_left, n_right = (bounds[1 + 2 * t], bounds[2 + 2 * t])
        out = pl.ds(pl.multiple_of(t * TQ, TQ), TQ)
        q = q_ref[out, :]
        near = pl.ds(pl.multiple_of(start + PAD - EDGE, 128), TK)
        for h in range(plan.heads):
            qh = jnp.where(plan.key_lanes(lane, h), q, jnp.zeros_like(q))
            qh_ref[h] = qh
            s = nt(qh, km[near, :]) + near_ref[0, h]
            top = jnp.max(s, axis=1, keepdims=True)
            p = jnp.exp(s - top).astype(bf16)
            acc[h] = nn(p, vm[near, :])
            row_max[h] = jnp.broadcast_to(top, (TQ, 128))

        def far(bucket):
            def step(first, n):
                span = pl.ds(pl.multiple_of(first + n, 128), TK)
                for h in range(plan.heads):
                    s = nt(qh_ref[h], km[span, :])
                    offset = table_ref[bucket, h]
                    old = row_max[h][:, :1]
                    top = jnp.maximum(old, jnp.max(s, axis=1, keepdims=True) + offset)
                    p = jnp.exp(s - (top - offset)).astype(bf16)
                    acc[h] = acc[h] * jnp.exp(old - top) + nn(p, vm[span, :])
                    row_max[h] = jnp.broadcast_to(top, (TQ, 128))
            return step

        left, right = (far(far_left_bucket), far(far_right_bucket))

        @pl.loop(0, n_left)
        def _(n):
            left(start + PAD - EDGE - TK, -n * TK)

        @pl.loop(0, n_right)
        def _(n):
            right(start + PAD - EDGE + TK, n * TK)

        wide = jnp.zeros((TQ, WIDE), f32)
        qb = jnp.where(lane < plan.stat_lane, q, jnp.zeros_like(q))
        for h in range(plan.heads):
            total = acc[h][:, 3 * h : 3 * h + 1]
            log_total = row_max[h][:, :1] + jnp.log(total)
            wide = jnp.where(lane // 64 == h + 1, acc[h] / total, wide)
            for i, part in enumerate(split3(-log_total)):
                qb = jnp.where(lane == plan.stat_lane + 3 * h + i, part, qb)
        wide_ref[out, :] = wide
        low_ref[out, :] = wide.astype(bf16)
        qb_ref[out, :] = qb
        return unused

    lax.fori_loop(0, pair // TQ, tile, 0)


def dq_kernel(
    plan, rows, pair, bounds, table_ref, g_ref, kaug_ref, qb_ref, do_ref, near_ref,
    dq_ref, tab_ref, km, vm, acc, qh_ref, doh_ref, near_acc, far_acc,
):
    build_keys(plan, g_ref, kaug_ref, km, vm, rows)
    lane = lanes_of(TQ)
    near_acc[...] = jnp.zeros_like(near_acc)
    far_acc[...] = jnp.zeros_like(far_acc)

    def tile(t, unused):
        start = pl.multiple_of(bounds[0] + t * TQ, 128)
        n_left, n_right = (bounds[1 + 2 * t], bounds[2 + 2 * t])
        out = pl.ds(pl.multiple_of(t * TQ, TQ), TQ)
        q = qb_ref[out, :]
        do = do_ref[out, :]
        near = pl.ds(pl.multiple_of(start + PAD - EDGE, 128), TK)

        def grads(h, s, span):
            p = jnp.exp(s)
            return p * nt(doh_ref[h], vm[span, :])

        for h in range(plan.heads):
            qh_ref[h] = jnp.where(plan.key_lanes(lane, h), q, jnp.zeros_like(q))
            doh_ref[h] = jnp.where(plan.value_lanes(lane, h), do, jnp.zeros_like(do))
            ds = grads(h, nt(qh_ref[h], km[near, :]) + near_ref[0, h], near)
            near_acc[h] += ds
            acc[h] = nn(ds.astype(bf16), km[near, :])

        def far(bucket, slot):
            def step(first, n):
                span = pl.ds(pl.multiple_of(first + n, 128), TK)
                for h in range(plan.heads):
                    ds = grads(h, nt(qh_ref[h], km[span, :]) + table_ref[bucket, h], span)
                    acc[h] += nn(ds.astype(bf16), km[span, :])
                    far_acc[slot, h] += (
                        ds[:, 0:128] + ds[:, 128:256] + ds[:, 256:384] + ds[:, 384:512]
                    )
            return step

        left, right = (far(far_left_bucket, 0), far(far_right_bucket, 1))

        @pl.loop(0, n_left)
        def _(n):
            left(start + PAD - EDGE - TK, -n * TK)

        @pl.loop(0, n_right)
        def _(n):
            right(start + PAD - EDGE + TK, n * TK)

        total = jnp.zeros((TQ, WIDE), f32)
        for h in range(plan.heads):
            total = jnp.where(lane // 64 == h, acc[h], total)
        dq_ref[out, :] = total.astype(bf16)
        return unused

    lax.fori_loop(0, pair // TQ, tile, 0)
    row = lax.broadcasted_iota(jnp.int32, (EDGE, 3 * EDGE), 0)
    col = lax.broadcasted_iota(jnp.int32, (EDGE, 3 * EDGE), 1)
    bucket = bucket_of(col - EDGE - row)
    for h in range(plan.heads):
        band = near_acc[h, :EDGE, : 3 * EDGE] + near_acc[h, EDGE:, EDGE:]
        extra_right = near_acc[h, :EDGE, 3 * EDGE :]
        extra_left = near_acc[h, EDGE:, :EDGE]
        for b in range(32):
            part = jnp.sum(jnp.where(bucket == b, band, 0.0), axis=0, keepdims=True)
            part = part[:, :128] + part[:, 128:256] + part[:, 256:]
            if b == far_left_bucket:
                part = part + jnp.sum(far_acc[0, h], axis=0, keepdims=True)
                part = part + jnp.sum(extra_left, axis=0, keepdims=True)
            if b == far_right_bucket:
                part = part + jnp.sum(far_acc[1, h], axis=0, keepdims=True)
                part = part + jnp.sum(extra_right, axis=0, keepdims=True)
            tab_ref[h, b : b + 1, :] = part


def dkv_kernel(
    plan, rows, pair, bounds, table_ref, qall_ref, doall_ref, g_ref, kaug_ref, near_ref,
    dk_ref, dv_ref, mask_ref, qp, dop, kh_ref, vh_ref, acc_k, acc_v,
):
    lane = lanes_of(TQ)
    first = lanes_of(1)
    stat = (first >= plan.stat_lane) & (first < plan.stat_lane + 3 * plan.heads)
    qp[:PAD, :] = jnp.broadcast_to(jnp.where(stat, neg_big, 0.0).astype(bf16), (PAD, WIDE))
    qp[pl.ds(PAD + rows, PAD), :] = qp[:PAD, :]
    dop[:PAD, :] = jnp.zeros((PAD, WIDE), bf16)
    dop[pl.ds(PAD + rows, PAD), :] = jnp.zeros((PAD, WIDE), bf16)
    step = 512

    def fill(n, unused):
        at = pl.multiple_of(n * step, step)
        to = pl.multiple_of(PAD + n * step, 128)
        qp[pl.ds(to, step), :] = qall_ref[pl.ds(at, step), :]
        dop[pl.ds(to, step), :] = doall_ref[pl.ds(at, step), :]
        return unused

    lax.fori_loop(0, rows // step, fill, 0)
    low = lanes_of(TQ, 128) < 64
    ones = (lanes_of(TQ, 128) < 3 * plan.heads).astype(bf16)

    def tile(t, unused):
        start = pl.multiple_of(bounds[0] + t * TQ, 128)
        n_left, n_right = (bounds[1 + 2 * t], bounds[2 + 2 * t])
        out = pl.ds(pl.multiple_of(t * TQ, TQ), TQ)
        middle = g_ref[out, 128:256]
        k = jnp.concatenate([g_ref[out, 0:128], jnp.where(low, middle, kaug_ref[out, :])], axis=1)
        v = jnp.concatenate([jnp.where(low, ones, middle), g_ref[out, 256:384]], axis=1)
        near = pl.ds(pl.multiple_of(start + PAD - EDGE, 128), TK)

        def grads(h, s, span):
            p = jnp.exp(s)
            ds = p * nt(vh_ref[h], dop[span, :])
            return nn(p.astype(bf16), dop[span, :]), nn(ds.astype(bf16), qp[span, :])

        for h in range(plan.heads):
            kh_ref[h] = jnp.where(plan.key_lanes(lane, h), k, jnp.zeros_like(k))
            vh_ref[h] = jnp.where(plan.value_lanes(lane, h), v, jnp.zeros_like(v))
            acc_v[h], acc_k[h] = grads(h, nt(kh_ref[h], qp[near, :]) + near_ref[1, h], near)

        def far(bucket):
            def step(first, n):
                span = pl.ds(pl.multiple_of(first + n, 128), TK)
                for h in range(plan.heads):
                    add_v, add_k = grads(
                        h, nt(kh_ref[h], qp[span, :]) + table_ref[bucket, h], span
                    )
                    acc_v[h] += add_v
                    acc_k[h] += add_k
            return step

        left, right = (far(far_right_bucket), far(far_left_bucket))

        @pl.loop(0, n_left)
        def _(n):
            left(start + PAD - EDGE - TK, -n * TK)

        @pl.loop(0, n_right)
        def _(n):
            right(start + PAD - EDGE + TK, n * TK)

        dk = jnp.zeros((TQ, WIDE), f32)
        dv = jnp.zeros((TQ, WIDE), f32)
        mask_grad = jnp.zeros((TQ, 1), f32)
        for h in range(plan.heads):
            dk = jnp.where(lane // 64 == h, acc_k[h], dk)
            dv = jnp.where(lane // 64 == h + 1, acc_v[h], dv)
            mask_grad = mask_grad + acc_k[h][:, plan.mask_lane : plan.mask_lane + 1]
        mask_ref[t] = jnp.transpose(jnp.broadcast_to(mask_grad, (TQ, 128)))[:8, :]
        dk_ref[out, :] = dk.astype(bf16)
        dv_ref[out, :] = dv.astype(bf16)
        return unused

    lax.fori_loop(0, pair // TQ, tile, 0)


def grad_attended_kernel(plan, branch_ref, w_ref, wide_ref, do_ref):
    rows = branch_ref.shape[0]
    lane = lanes_of(rows)
    grad = nt(branch_ref[...], w_ref[...]).astype(bf16)
    terms = grad.astype(f32) * wide_ref[...]
    out = grad
    for h in range(plan.heads):
        row_term = jnp.sum(
            jnp.where(lane // 64 == h + 1, terms, 0.0), axis=1, keepdims=True
        )
        for i, part in enumerate(split3(-row_term)):
            out = jnp.where(lane == 3 * h + i, part, out)
    do_ref[...] = out


vmem = pl.BlockSpec(memory_space=pltpu.VMEM)
smem = pl.BlockSpec(memory_space=pltpu.SMEM)


def params():
    return pltpu.CompilerParams(vmem_limit_bytes=56 * 2**20)


class Spot:
    def __init__(self, lines):
        index = lax.axis_index("ctx")
        self.wa = lax.axis_index("wa")
        self.index = index
        self.lines = lines
        self.z = index // 4
        self.x = (index // 2) % 2
        self.core = index % 2

    def core_mate(self):
        return (self.index + 1 - 2 * self.core, self.wa)

    def x_mate(self):
        return (self.index + 2 - 4 * self.x, self.wa)

    def z_mate(self, step):
        return (jnp.clip(self.index + 4 * step, 0, 4 * self.lines - 1), self.wa)

    def y_mate(self):
        return (self.index, 1 - self.wa)


def send(src, dst, send_sem, recv_sem, device):
    return pltpu.make_async_remote_copy(
        src_ref=src,
        dst_ref=dst,
        send_sem=send_sem,
        recv_sem=recv_sem,
        device_id=device,
        device_id_type=pl.DeviceIdType.MESH,
    )


def greet(spot, with_y):
    barrier = pltpu.get_barrier_semaphore()
    mates = [spot.core_mate(), spot.x_mate()] + ([spot.y_mate()] if with_y else [])
    for mate in mates:
        pl.semaphore_signal(barrier, inc=1, device_id=mate, device_id_type=pl.DeviceIdType.MESH)

    @pl.when(spot.z + 1 < spot.lines)
    def _():
        pl.semaphore_signal(
            barrier, inc=1, device_id=spot.z_mate(1), device_id_type=pl.DeviceIdType.MESH
        )

    @pl.when(spot.z > 0)
    def _():
        pl.semaphore_signal(
            barrier, inc=1, device_id=spot.z_mate(-1), device_id_type=pl.DeviceIdType.MESH
        )

    above = (spot.z + 1 < spot.lines).astype(jnp.int32)
    below = (spot.z > 0).astype(jnp.int32)
    pl.semaphore_wait(barrier, len(mates) + above + below)


def added(a, b):
    return (a.astype(f32) + b.astype(f32)).astype(bf16)


def scatter_kernel(lines, units, z_first, *refs):
    count = 3
    parts, outs = (refs[:count], refs[count : 2 * count])
    mine, core_in, x_in, up_in, down_in, load_sem, core_sem, x_sem, up_sem, down_sem = refs[
        2 * count :
    ]
    spot = Spot(lines)
    z, x, core = (spot.z, spot.x, spot.core)
    greet(spot, False)
    loads = []
    cores = []
    order = z_first + [u for u in range(len(units)) if u not in z_first]

    def rows_of(u):
        return pl.ds(units[u][1], units[u][2])

    for u in order:
        m = units[u][0]
        load = pltpu.make_async_copy(
            parts[m].at[:, :, core, rows_of(u)], mine.at[m, :, :, rows_of(u)], load_sem.at[u]
        )
        load.start()
        loads.append(load)
        copy = send(
            parts[m].at[:, :, 1 - core, rows_of(u)],
            core_in.at[m, :, :, rows_of(u)],
            core_sem.at[0, u],
            core_sem.at[1, u],
            spot.core_mate(),
        )
        copy.start()
        cores.append(copy)

    def add_slices(into, source, u, x_slot):
        m = units[u][0]

        def body(line, unused):
            at = (m, line, x_slot, rows_of(u))
            into[at] = added(into[at], source[at])
            return unused

        lax.fori_loop(0, lines, body, 0)

    def x_copy(u, both):
        m = units[u][0]
        if both:
            src = mine.at[m, :, 1 - x, rows_of(u)]
            dst = x_in.at[m, :, rows_of(u)]
        else:
            src = mine.at[m, z, 1 - x, rows_of(u)]
            dst = x_in.at[m, z, rows_of(u)]
        return send(src, dst, x_sem.at[0, u], x_sem.at[1, u], spot.x_mate())

    def line_flow(u, slots):
        m = units[u][0]
        n = len(slots)

        def slot_copies(step, d):
            ring, sem = (up_in, up_sem) if step > 0 else (down_in, down_sem)
            return [
                send(
                    mine.at[m, d, s, rows_of(u)],
                    ring.at[m, d, s, rows_of(u)],
                    sem.at[0, u, d, i],
                    sem.at[1, u, d, i],
                    spot.z_mate(step),
                )
                for i, s in enumerate(slots)
            ]

        def receive(step, d):
            ring = up_in if step > 0 else down_in
            for copy, s in zip(slot_copies(step, d), slots):
                copy.wait_recv()
                at = (m, d, s, rows_of(u))
                mine[at] = added(mine[at], ring[at])

        def ends_first():
            @pl.when(z == 0)
            def _():
                for d in range(lines - 1, 0, -1):
                    for copy in slot_copies(1, d):
                        copy.start()

            @pl.when(z == lines - 1)
            def _():
                for d in range(lines - 1):
                    for copy in slot_copies(-1, d):
                        copy.start()

        def relay():
            def body(k, unused):
                high = lines - 1 - k

                @pl.when((z < high) & (z > 0))
                def _():
                    receive(1, high)
                    for copy in slot_copies(1, high):
                        copy.start()

                @pl.when((z > k) & (z + 1 < lines))
                def _():
                    receive(-1, k)
                    for copy in slot_copies(-1, k):
                        copy.start()

                return unused

            lax.fori_loop(0, lines - 1, body, 0)

        def arrive():
            @pl.when(z > 0)
            def _():
                receive(1, z)

            @pl.when(z + 1 < lines)
            def _():
                receive(-1, z)

        def finish(k, unused):
            @pl.when(z < lines - 1 - k)
            def _():
                for copy in slot_copies(1, lines - 1 - k):
                    copy.wait_send()

            @pl.when(z > k)
            def _():
                for copy in slot_copies(-1, k):
                    copy.wait_send()

            return unused

        return (
            ends_first,
            relay,
            arrive,
            lambda: lax.fori_loop(0, lines - 1, finish, 0),
        )

    def store(u):
        m = units[u][0]
        outs[m][rows_of(u), :] = mine[m, z, x, rows_of(u)].astype(f32)

    pending = {}
    for i, u in enumerate(order):
        loads[i].wait()
        cores[i].wait()
        if u in z_first:
            add_slices(mine, core_in, u, 0)
            add_slices(mine, core_in, u, 1)
        else:
            add_slices(mine, core_in, u, 1 - x)
            copy = x_copy(u, True)
            copy.start()
            pending[u] = copy
            add_slices(mine, core_in, u, x)
    x_first = [u for u in order if u not in z_first]
    flows = {u: line_flow(u, [0, 1] if u in z_first else [x]) for u in order}
    last = {}

    def x_stage(u):
        m = units[u][0]
        pending[u].wait()

        def body(line, unused):
            at = (m, line, x, rows_of(u))
            mine[at] = added(mine[at], x_in[m, line, rows_of(u)])
            return unused

        lax.fori_loop(0, lines, body, 0)

    def settle(u):
        flows[u][2]()
        if u in z_first:
            last[u] = x_copy(u, False)
            last[u].start()
        else:
            store(u)

    for t in range(len(order) + 2):
        if t < len(order):
            u = order[t]
            if u not in z_first:
                x_stage(u)
            flows[u][0]()
        if 0 <= t - 1 < len(order):
            flows[order[t - 1]][1]()
        if 0 <= t - 2 < len(order):
            settle(order[t - 2])
    for u, copy in last.items():
        m = units[u][0]
        copy.wait()
        at = (m, z, x, rows_of(u))
        mine[at] = added(mine[at], x_in[m, z, rows_of(u)])
        store(u)
    for u in order:
        flows[u][3]()


def reduce_scatter(parts, cycle_size):
    lines = cycle_size // 4
    units_here, model = parts[0].shape
    rows = units_here // cycle_size
    cut = (rows // 2 + 15) // 16 * 16
    pieces = [(0, cut), (cut, rows - cut)] if cut < rows else [(0, rows)]
    units = [(m, at, size) for m in range(3) for at, size in pieces]
    z_first = [len(units) - 1]
    shaped = [part.reshape(lines, 2, 2, rows, model) for part in parts]
    hbm = pl.BlockSpec(memory_space=pl.ANY)
    n = len(units)
    return pl.pallas_call(
        functools.partial(scatter_kernel, lines, units, z_first),
        out_shape=[jax.ShapeDtypeStruct((rows, model), f32)] * 3,
        in_specs=[hbm] * 3,
        out_specs=[vmem] * 3,
        scratch_shapes=[
            pltpu.VMEM((3, lines, 2, rows, model), bf16),
            pltpu.VMEM((3, lines, 2, rows, model), bf16),
            pltpu.VMEM((3, lines, rows, model), bf16),
            pltpu.VMEM((3, lines, 2, rows, model), bf16),
            pltpu.VMEM((3, lines, 2, rows, model), bf16),
            pltpu.SemaphoreType.DMA((n,)),
            pltpu.SemaphoreType.DMA((2, n)),
            pltpu.SemaphoreType.DMA((2, n)),
            pltpu.SemaphoreType.DMA((2, n, lines, 2)),
            pltpu.SemaphoreType.DMA((2, n, lines, 2)),
        ],
        compiler_params=pltpu.CompilerParams(
            vmem_limit_bytes=58 * 2**20, collective_id=1, has_side_effects=True
        ),
        name="weight_scatter",
    )(*shaped)

def first_kernel(
    plan, lines, span, tokens_ref, gain_ref, aug_ref, wq_hbm, wk_hbm, wv_hbm,
    x_ref, q_ref, own_ref, all_hbm,
    weights, zeros, load_sem, y_sem, own_sem, zero_sem, z_sem, x_sem, c_sem,
):
    spot = Spot(lines)
    z, x, core, wa = (spot.z, spot.x, spot.core, spot.wa)
    half, model = tokens_ref.shape
    cols = plan.cols
    chunk = half // 4
    loads = [
        pltpu.make_async_copy(src, weights.at[pl.ds(i * cols, cols)], load_sem.at[i])
        for i, src in enumerate((wk_hbm, wv_hbm, wq_hbm))
    ]
    for load in loads:
        load.start()
    greet(spot, True)
    zeros[...] = jnp.zeros_like(zeros)

    def outside(d):
        return (d < z - span) | (d > z + span)

    def zero_copies(d):
        return [
            pltpu.make_async_copy(zeros, all_hbm.at[d, a, b], zero_sem.at[d, a, b])
            for a in range(2)
            for b in range(2)
        ]

    def zero_start(d, unused):
        @pl.when(outside(d))
        def _():
            for copy in zero_copies(d):
                copy.start()

        return unused

    def rows_at(start, size):
        return pl.ds(pl.multiple_of(start, size), size)

    ours = wa * half
    theirs = (1 - wa) * half

    def y_copy(i, base):
        at = rows_at(base + i * chunk, chunk)
        return send(x_ref.at[at], x_ref.at[at], y_sem.at[0, i], y_sem.at[1, i], spot.y_mate())

    def normal(i, unused):
        rows_in = tokens_ref[rows_at(i * chunk, chunk), :].astype(f32)
        inv = lax.rsqrt(jnp.mean(rows_in * rows_in, axis=-1, keepdims=True) + eps)
        x_ref[rows_at(ours + i * chunk, chunk), :] = (rows_in * inv * gain_ref[...]).astype(bf16)
        y_copy(i, ours).start()
        return unused

    lax.fori_loop(0, 4, normal, 0)
    for load in loads:
        load.wait()

    def project(base):
        rows = rows_at(base, half)
        qkv = nt(x_ref[rows, :], weights[...]).astype(bf16)
        own_ref[rows, :] = qkv[:, : 2 * cols]
        q_ref[rows, :] = aug_ref[rows, :]
        q_ref[rows, :cols] = qkv[:, 2 * cols :]

    pieces = [
        (ours, half, True),
        (theirs, half // 2, True),
        (theirs + half // 2, half // 2, False),
    ]

    def piece_rows(p):
        return rows_at(pieces[p][0], pieces[p][1])

    def source(p, d, a):
        return all_hbm.at[d, a, core, piece_rows(p)]

    def pass_copy(p, step, d, own):
        i = 0 if step > 0 else 1
        if pieces[p][2]:
            dst = source(p, d, x)
            src = own_ref.at[piece_rows(p)] if own else dst
        else:
            dst = all_hbm.at[d, :, core, piece_rows(p)]
            src = dst
        return send(src, dst, z_sem.at[p, i, d], z_sem.at[p, 2 + i, d], spot.z_mate(step))

    def across(p, d, own):
        dst = source(p, d, x)
        src = own_ref.at[piece_rows(p)] if own else dst
        return send(src, dst, x_sem.at[p, 0, d], x_sem.at[p, 1, d], spot.x_mate())

    def beside(p, d):
        part = all_hbm.at[d, :, core, piece_rows(p)]
        return send(part, part, c_sem.at[p, 0, d], c_sem.at[p, 1, d], spot.core_mate())

    def own_copy(p):
        return pltpu.make_async_copy(
            own_ref.at[piece_rows(p)], source(p, z, x), own_sem.at[p]
        )

    def both_ways(p, own):
        @pl.when(z + 1 < lines)
        def _():
            pass_copy(p, 1, z, own).start()

        @pl.when(z > 0)
        def _():
            pass_copy(p, -1, z, own).start()

    def begin(p):
        own_copy(p).start()
        across(p, z, True).start()
        if pieces[p][2]:
            both_ways(p, True)

    def level(p, k):
        @pl.when(z - k >= 0)
        def _():
            d = jnp.maximum(z - k, 0)
            pass_copy(p, 1, d, False).wait_recv()
            if k < span:

                @pl.when(z + 1 < lines)
                def _():
                    pass_copy(p, 1, d, False).start()

            if pieces[p][2]:
                across(p, d, False).start()
            else:
                beside(p, d).start()

        @pl.when(z + k < lines)
        def _():
            d = jnp.minimum(z + k, lines - 1)
            pass_copy(p, -1, d, False).wait_recv()
            if k < span:

                @pl.when(z > 0)
                def _():
                    pass_copy(p, -1, d, False).start()

            if pieces[p][2]:
                across(p, d, False).start()
            else:
                beside(p, d).start()

    def turn(p):
        across(p, z, True).wait()
        own_copy(p).wait()
        both_ways(p, False)
        beside(p, z).start()

    def settle(p, k):
        for sign in (1, -1) if k else (1,):
            d = z - sign * k

            @pl.when((d >= 0) & (d < lines))
            def _(d=d):
                d = jnp.clip(d, 0, lines - 1)
                across(p, d, k == 0).wait()
                if k == 0:
                    own_copy(p).wait()
                beside(p, d).start()

    project(ours)
    begin(0)
    lax.fori_loop(0, lines, zero_start, 0)

    def y_wait(i, unused):
        y_copy(i, theirs).wait_recv()
        return unused

    lax.fori_loop(0, 2, y_wait, 0)
    level(0, 1)
    lax.fori_loop(2, 4, y_wait, 0)
    project(theirs)
    begin(2)
    begin(1)
    if span > 1:
        level(0, 2)
    settle(0, 0)
    turn(2)
    level(1, 1)
    settle(0, 1)
    level(2, 1)
    if span > 1:
        level(1, 2)
        settle(0, 2)
    settle(1, 0)
    settle(1, 1)
    if span > 1:
        level(2, 2)
        settle(1, 2)
    for k in range(3, span + 1):
        for p in range(3):
            level(p, k)
        for p in range(2):
            settle(p, k)

    def finish_line(d, unused):
        @pl.when(~outside(d))
        def _():
            for p in range(3):
                beside(p, d).wait()

        @pl.when(outside(d))
        def _():
            for copy in zero_copies(d):
                copy.wait()

        for p in range(3):

            @pl.when((z + 1 < lines) & (d <= z) & (d > z - span))
            def _(p=p):
                pass_copy(p, 1, d, False).wait_send()

            @pl.when((z > 0) & (d >= z) & (d < z + span))
            def _(p=p):
                pass_copy(p, -1, d, False).wait_send()

        return unused

    lax.fori_loop(0, lines, finish_line, 0)

    def y_drain(i, unused):
        y_copy(i, ours).wait_send()
        return unused

    lax.fori_loop(0, 4, y_drain, 0)


def first(plan, cycle_size, reach, tokens, gain, aug, w_query, w_key, w_value):
    lines = cycle_size // 4
    span = min(lines - 1, (reach + 3) // 4)
    half, model = tokens.shape
    pair = 2 * half
    hbm = pl.BlockSpec(memory_space=pl.ANY)
    dma = pltpu.SemaphoreType.DMA
    return pl.pallas_call(
        functools.partial(first_kernel, plan, lines, span),
        out_shape=[
            jax.ShapeDtypeStruct((pair, model), bf16),
            jax.ShapeDtypeStruct((pair, WIDE), bf16),
            jax.ShapeDtypeStruct((pair, 2 * plan.cols), bf16),
            jax.ShapeDtypeStruct((lines, 2, 2, pair, 2 * plan.cols), bf16),
        ],
        in_specs=[vmem] * 3 + [hbm] * 3,
        out_specs=[vmem] * 3 + [hbm],
        scratch_shapes=[
            pltpu.VMEM((3 * plan.cols, model), bf16),
            pltpu.VMEM((pair, 2 * plan.cols), bf16),
            dma((3,)),
            dma((2, 4)),
            dma((3,)),
            dma((lines, 2, 2)),
            dma((3, 4, lines)),
            dma((3, 2, lines)),
            dma((3, 2, lines)),
        ],
        compiler_params=pltpu.CompilerParams(
            vmem_limit_bytes=56 * 2**20, collective_id=4, has_side_effects=True
        ),
        name="project_gather",
    )(tokens, gain, aug, w_query.T, w_key.T, w_value.T)


def tn(a, b):
    return lax.dot_general(a, b, (((0,), (0,)), ((), ())), preferred_element_type=f32)


def line_relay(spot, start, receive):
    def level(k, unused):
        @pl.when(spot.z - k >= 0)
        def _():
            if_first(k, lambda: receive(1, spot.z - k))

            @pl.when(spot.z + 1 < spot.lines)
            def _():
                start(1, spot.z - k)

        @pl.when(spot.z + k < spot.lines)
        def _():
            if_first(k, lambda: receive(-1, spot.z + k))

            @pl.when(spot.z > 0)
            def _():
                start(-1, spot.z + k)

        return unused

    def if_first(k, run):
        @pl.when(k > 0)
        def _():
            run()

    return level


def finish_kernel(
    plan, lines, dq_ref, dk_ref, dv_ref, mask_ref, w3_ref, normed_ref, att_ref, branch_ref,
    tokens_ref, gain_ref, hidden_ref, gh_ref, ffn_ref, small_ref,
    out_ref, gt_ref, gm_ref, weights_ref, total_ref,
    mine, core_in, x_in, up_in, down_in, all_w, y_out, y_in, own_part, ffn_in, mask_in,
    small_own, small_y, small_core, small_x, small_all,
    y_sem, core_sem, x_sem, up_sem, down_sem, gz_sem, gx_sem, gc_sem, sz_sem,
):
    spot = Spot(lines)
    z, x, core, wa = (spot.z, spot.x, spot.core, spot.wa)
    greet(spot, True)
    half = tokens_ref.shape[0]
    quarter = half // 2
    model = tokens_ref.shape[1]
    rows = mine.shape[3]

    def grad_rows(at):
        at = pl.ds(pl.multiple_of(at, quarter), quarter)
        return (
            nt(dq_ref[at, :], w3_ref[:, 0:256])
            + nt(dk_ref[at, :], w3_ref[:, 256:512])
            + nt(dv_ref[at, :], w3_ref[:, 512:768])
        )

    def y_copy(i):
        return send(y_out.at[i], y_in.at[i], y_sem.at[0, i], y_sem.at[1, i], spot.y_mate())

    def theirs(i, unused):
        y_out[i] = grad_rows((1 - wa) * half + i * quarter).astype(bf16)
        y_copy(i).start()
        return unused

    lax.fori_loop(0, 2, theirs, 0)
    mask_copy = send(
        mask_ref.at[1 - wa], mask_in, y_sem.at[0, 2], y_sem.at[1, 2], spot.y_mate()
    )
    mask_copy.start()

    def fill(product, matrix):
        for j in range(plan.cols // rows):
            s = matrix * (plan.cols // rows) + j
            mine[s // 4, (s // 2) % 2, s % 2] = product[j * rows : (j + 1) * rows].astype(bf16)

    fill(tn(dq_ref[...], normed_ref[...])[: plan.cols], 0)
    fill(tn(dk_ref[...], normed_ref[...])[: plan.cols], 1)
    fill(tn(dv_ref[...], normed_ref[...])[64:], 2)
    fill(tn(att_ref[...], branch_ref[...])[64:], 3)
    core_copy = send(
        mine.at[:, :, 1 - core], core_in, core_sem.at[0, 0], core_sem.at[1, 0], spot.core_mate()
    )
    core_copy.start()
    their_rows = pl.ds(pl.multiple_of((1 - wa) * half, half), half)
    ffn_copy = send(
        ffn_ref.at[their_rows], ffn_in, y_sem.at[0, 3], y_sem.at[1, 3], spot.y_mate()
    )
    ffn_copy.start()

    def ours(i, unused):
        own_part[pl.ds(pl.multiple_of(i * quarter, quarter), quarter), :] = grad_rows(
            wa * half + i * quarter
        )
        return unused

    lax.fori_loop(0, 2, ours, 0)
    core_copy.wait()

    def x_copy(d):
        return send(
            mine.at[d, 1 - x, core], x_in.at[d], x_sem.at[0, d], x_sem.at[1, d], spot.x_mate()
        )

    def core_add(d, unused):
        mine[d, 1 - x, core] = added(mine[d, 1 - x, core], core_in[d, 1 - x])
        x_copy(d).start()
        return unused

    lax.fori_loop(0, lines, core_add, 0)

    def core_add_own(d, unused):
        mine[d, x, core] = added(mine[d, x, core], core_in[d, x])
        return unused

    lax.fori_loop(0, lines, core_add_own, 0)

    gain_sum = jnp.zeros((1, model), f32)
    step = 32
    for i in range(2):
        y_copy(i).wait()

        def normal(j, total, i=i):
            at = pl.ds(pl.multiple_of(i * quarter + j * step, step), step)
            there = pl.ds(pl.multiple_of(j * step, step), step)
            grad = own_part[at, :] + y_in[i, there, :].astype(f32)
            rows_in = tokens_ref[at, :].astype(f32)
            inv = lax.rsqrt(jnp.mean(rows_in * rows_in, axis=-1, keepdims=True) + eps)
            scaled = gain_ref[...] * grad
            mean = jnp.mean(rows_in * scaled, axis=-1, keepdims=True)
            gt_ref[at, :] = gh_ref[at, :] + inv * scaled - rows_in * (inv * inv * inv * mean)
            return total + jnp.sum(grad * rows_in * inv, axis=0, keepdims=True)

        gain_sum = lax.fori_loop(0, quarter // step, normal, gain_sum)
    small_own[...] = small_ref[...]
    small_own[0:1, :] = gain_sum
    small_copy = send(
        small_own, small_y, y_sem.at[0, 4], y_sem.at[1, 4], spot.y_mate()
    )
    small_copy.start()
    mask_copy.wait()
    gm_ref[...] = mask_ref[wa] + mask_in[...]

    def flow(step, d):
        ring, sem = (up_in, up_sem) if step > 0 else (down_in, down_sem)
        return send(
            mine.at[d, x, core], ring.at[d], sem.at[0, d], sem.at[1, d], spot.z_mate(step)
        )

    def merge(step, d):
        flow(step, d).wait_recv()
        ring = up_in if step > 0 else down_in
        mine[d, x, core] = added(mine[d, x, core], ring[d])

    def x_add(d, unused):
        x_copy(d).wait()
        mine[d, x, core] = added(mine[d, x, core], x_in[d])

        @pl.when((z == 0) & (d > 0))
        def _():
            flow(1, d).start()

        @pl.when((z == lines - 1) & (d < lines - 1))
        def _():
            flow(-1, d).start()

        return unused

    lax.fori_loop(0, lines, x_add, 0)
    small_copy.wait()
    row = lax.broadcasted_iota(jnp.int32, small_own.shape, 0)
    small_x[0] = small_own[...] + jnp.where(row < 2, small_y[...], 0.0)
    small_core_copy = send(
        small_x.at[0], small_core, core_sem.at[0, 1], core_sem.at[1, 1], spot.core_mate()
    )
    small_core_copy.start()

    def relay(k, unused):
        high = lines - 1 - k

        @pl.when((z < high) & (z > 0))
        def _():
            merge(1, high)
            flow(1, high).start()

        @pl.when((z > k) & (z + 1 < lines))
        def _():
            merge(-1, k)
            flow(-1, k).start()

        return unused

    lax.fori_loop(0, lines - 1, relay, 0)
    small_core_copy.wait()
    small_x[1] = small_x[0] + small_core[...]
    small_x_copy = send(
        small_x.at[1], small_x.at[2], x_sem.at[0, lines], x_sem.at[1, lines], spot.x_mate()
    )
    small_x_copy.start()

    @pl.when(z > 0)
    def _():
        merge(1, z)

    @pl.when(z + 1 < lines)
    def _():
        merge(-1, z)

    all_w[z, x, core] = mine[z, x, core]

    def pass_w(step, d):
        i = 0 if step > 0 else 1
        return send(
            all_w.at[d, x, core], all_w.at[d, x, core], gz_sem.at[i, d], gz_sem.at[2 + i, d],
            spot.z_mate(step),
        )

    def pass_s(step, d):
        i = 0 if step > 0 else 1
        return send(
            small_all.at[d], small_all.at[d], sz_sem.at[i, d], sz_sem.at[2 + i, d],
            spot.z_mate(step),
        )

    def across(d):
        return send(
            all_w.at[d, x, core], all_w.at[d, x, core], gx_sem.at[0, d], gx_sem.at[1, d],
            spot.x_mate(),
        )

    def beside(d):
        return send(
            all_w.at[d, :, core], all_w.at[d, :, core], gc_sem.at[0, d], gc_sem.at[1, d],
            spot.core_mate(),
        )

    small_x_copy.wait()
    small_all[z] = small_x[1] + small_x[2]

    def receive(step, d):
        pass_w(step, d).wait_recv()
        across(d).start()

    across(z).start()
    lax.fori_loop(
        0, lines, line_relay(spot, lambda s, d: pass_w(s, d).start(), receive), 0
    )
    lax.fori_loop(
        0,
        lines,
        line_relay(
            spot, lambda s, d: pass_s(s, d).start(), lambda s, d: pass_s(s, d).wait_recv()
        ),
        0,
    )

    def add_small(d, total):
        return total + small_all[d]

    total_ref[...] = lax.fori_loop(1, lines, add_small, small_all[0])
    ffn_copy.wait()

    def last(j, unused):
        at = pl.ds(pl.multiple_of(j * step, step), step)
        here = pl.ds(pl.multiple_of(wa * half + j * step, step), step)
        total = hidden_ref[at, :] + ffn_ref[here, :].astype(f32) + ffn_in[at, :].astype(f32)
        out_ref[at, :] = total.astype(bf16)
        return unused

    lax.fori_loop(0, half // step, last, 0)

    def spread(d, unused):
        across(d).wait()
        beside(d).start()
        return unused

    lax.fori_loop(0, lines, spread, 0)

    def copy_out(d, unused):
        beside(d).wait()
        weights_ref[d] = all_w[d]
        return unused

    lax.fori_loop(0, lines, copy_out, 0)

    def drain(d, unused):
        @pl.when((z < d))
        def _():
            flow(1, d).wait_send()

        @pl.when((z > d))
        def _():
            flow(-1, d).wait_send()

        @pl.when((d <= z) & (z + 1 < lines))
        def _():
            pass_w(1, d).wait_send()
            pass_s(1, d).wait_send()

        @pl.when((d >= z) & (z > 0))
        def _():
            pass_w(-1, d).wait_send()
            pass_s(-1, d).wait_send()

        return unused

    lax.fori_loop(0, lines, drain, 0)


def finish(plan, cycle_size, *operands):
    lines = cycle_size // 4
    half, model = operands[8].shape
    rows = 4 * plan.cols // cycle_size
    dma = pltpu.SemaphoreType.DMA
    return pl.pallas_call(
        functools.partial(finish_kernel, plan, lines),
        out_shape=[
            jax.ShapeDtypeStruct((half, model), bf16),
            jax.ShapeDtypeStruct((half, model), f32),
            jax.ShapeDtypeStruct((8, half), f32),
            jax.ShapeDtypeStruct((lines, 2, 2, rows, model), bf16),
            jax.ShapeDtypeStruct((8, model), f32),
        ],
        in_specs=[vmem] * len(operands),
        out_specs=[vmem] * 5,
        scratch_shapes=[
            pltpu.VMEM((lines, 2, 2, rows, model), bf16),
            pltpu.VMEM((lines, 2, rows, model), bf16),
            pltpu.VMEM((lines, rows, model), bf16),
            pltpu.VMEM((lines, rows, model), bf16),
            pltpu.VMEM((lines, rows, model), bf16),
            pltpu.VMEM((lines, 2, 2, rows, model), bf16),
            pltpu.VMEM((2, half // 2, model), bf16),
            pltpu.VMEM((2, half // 2, model), bf16),
            pltpu.VMEM((half, model), f32),
            pltpu.VMEM((half, model), bf16),
            pltpu.VMEM((8, half), f32),
            pltpu.VMEM((8, model), f32),
            pltpu.VMEM((8, model), f32),
            pltpu.VMEM((8, model), f32),
            pltpu.VMEM((3, 8, model), f32),
            pltpu.VMEM((lines, 8, model), f32),
            dma((2, 5)),
            dma((2, 2)),
            dma((2, lines + 1)),
            dma((2, lines)),
            dma((2, lines)),
            dma((4, lines)),
            dma((2, lines)),
            dma((2, lines)),
            dma((4, lines)),
        ],
        compiler_params=pltpu.CompilerParams(
            vmem_limit_bytes=58 * 2**20, collective_id=2, has_side_effects=True
        ),
        name="finish",
    )(*operands)


root = 0.7978845608028654
cubic = 0.044715


def middle_kernel(
    plan, cycle_size, att_ref, mixed_ref, wout_ref, tokens_ref, cot_ref, gain_ref,
    wg_hbm, wu_hbm, wd_hbm,
    hidden_ref, gh_ref, branch_ref, ffn_ref, do_ref, gain_part_ref, stack_hbm,
    wg, wu, wd, inner, gg, gu, x_ref, a_out, a_in, d_out, d_in, acc_f, acc_g, own_g, rows_buf,
    load_sem, y_sem, out_sem,
):
    spot = Spot(cycle_size // 4)
    wa = spot.wa
    half, model = tokens_ref.shape
    units = wd.shape[1]
    chunk = half // 4
    loads = [
        pltpu.make_async_copy(src, dst, load_sem.at[i])
        for i, (src, dst) in enumerate(((wg_hbm, wg), (wu_hbm, wu), (wd_hbm, wd)))
    ]
    for load in loads:
        load.start()
    barrier = pltpu.get_barrier_semaphore()
    pl.semaphore_signal(
        barrier, inc=1, device_id=spot.y_mate(), device_id_type=pl.DeviceIdType.MESH
    )
    pl.semaphore_wait(barrier, 1)
    ours = wa * half
    theirs = (1 - wa) * half

    def rows_at(start, size):
        return pl.ds(pl.multiple_of(start, size), size)

    def a_copy(i):
        return send(a_out.at[i], a_in.at[i], y_sem.at[0, i], y_sem.at[1, i], spot.y_mate())

    def d_copy(i):
        return send(
            d_out.at[i], d_in.at[i], y_sem.at[0, 4 + i], y_sem.at[1, 4 + i], spot.y_mate()
        )

    def b_copy(i, base):
        at = rows_at(base + i * chunk, chunk)
        return send(
            x_ref.at[at], x_ref.at[at], y_sem.at[0, 8 + i], y_sem.at[1, 8 + i], spot.y_mate()
        )

    def e_copy(i, base):
        at = rows_at(base + i * chunk, chunk)
        return send(
            branch_ref.at[at], branch_ref.at[at], y_sem.at[0, 12 + i], y_sem.at[1, 12 + i],
            spot.y_mate(),
        )

    def send_branch(i, unused):
        a_out[i] = nn(att_ref[rows_at(theirs + i * chunk, chunk), :], wout_ref[...]).astype(bf16)
        a_copy(i).start()
        return unused

    lax.fori_loop(0, 4, send_branch, 0)

    def own_branch(i, unused):
        at = rows_at(i * chunk, chunk)
        hidden_ref[at, :] = tokens_ref[at, :].astype(f32) + nn(
            att_ref[rows_at(ours + i * chunk, chunk), :], wout_ref[...]
        )
        return unused

    lax.fori_loop(0, 4, own_branch, 0)

    def normal(i, unused):
        a_copy(i).wait()
        at = rows_at(i * chunk, chunk)
        hidden = hidden_ref[at, :] + a_in[i].astype(f32)
        hidden_ref[at, :] = hidden
        inv = lax.rsqrt(jnp.mean(hidden * hidden, axis=-1, keepdims=True) + eps)
        x_ref[rows_at(ours + i * chunk, chunk), :] = (hidden * inv * gain_ref[...]).astype(bf16)
        b_copy(i, ours).start()
        return unused

    lax.fori_loop(0, 4, normal, 0)
    for load in loads:
        load.wait()
    wide = 256

    def feed(base):
        rows = rows_at(base, half)
        acc_f[...] = jnp.zeros_like(acc_f)
        acc_g[...] = jnp.zeros_like(acc_g)

        def tile(u, unused):
            cols = rows_at(u * wide, wide)
            gate = nn(x_ref[rows, :], wg[:, cols])
            upward = nn(x_ref[rows, :], wu[:, cols])
            grad_inner = nn(cot_ref[rows, :], wd[:, cols])
            square = gate * gate
            bend = jnp.tanh(root * gate * (1.0 + cubic * square))
            side = 0.5 * (1.0 + bend)
            gelu = gate * side
            slope = side + 0.5 * gate * (1.0 - bend * bend) * (
                root * (1.0 + 3.0 * cubic * square)
            )
            inner_low = (gelu * upward).astype(bf16)
            gate_low = (grad_inner * upward * slope).astype(bf16)
            up_low = (grad_inner * gelu).astype(bf16)
            inner[rows, cols] = inner_low
            gg[rows, cols] = gate_low
            gu[rows, cols] = up_low
            acc_g[...] += nt(gate_low, wg[:, cols]) + nt(up_low, wu[:, cols])
            acc_f[...] += nt(inner_low, wd[:, cols])
            return unused

        lax.fori_loop(0, units // wide, tile, 0)
        ffn_ref[rows, :] = acc_f[...].astype(bf16)

    feed(ours)
    own_g[...] = acc_g[...]

    def b_wait(i, unused):
        b_copy(i, theirs).wait_recv()
        return unused

    lax.fori_loop(0, 4, b_wait, 0)
    feed(theirs)

    def send_grad(i, unused):
        d_out[i] = acc_g[rows_at(i * chunk, chunk), :].astype(bf16)
        d_copy(i).start()
        return unused

    lax.fori_loop(0, 4, send_grad, 0)
    parts = 2
    span = units // parts
    slices = cycle_size // parts
    size = units // cycle_size

    def out_copy(n):
        m, p = (n // parts, n % parts)
        return pltpu.make_async_copy(
            rows_buf.at[n % 2],
            stack_hbm.at[pl.ds(p * slices, slices), m],
            out_sem.at[n],
        )

    for n in range(3 * parts):
        m, p = (n // parts, n % parts)
        left = (inner, gg, gu)[m]
        right = (cot_ref, x_ref, x_ref)[m]
        if n >= 2:
            out_copy(n - 2).wait()
        turned = jnp.transpose(left[:, p * span : (p + 1) * span])
        for c in range(0, model, wide):
            end = min(model, c + wide)
            product = nn(turned, right[:, c:end]).astype(bf16)
            for s in range(slices):
                rows_buf[n % 2, s, :, c:end] = product[s * size : (s + 1) * size]
        out_copy(n).start()

    def normal_back(i, total):
        d_copy(i).wait()
        at = rows_at(i * chunk, chunk)
        grad = own_g[at, :] + d_in[i].astype(f32)
        hidden = hidden_ref[at, :]
        inv = lax.rsqrt(jnp.mean(hidden * hidden, axis=-1, keepdims=True) + eps)
        scaled = gain_ref[...] * grad
        mean = jnp.mean(hidden * scaled, axis=-1, keepdims=True)
        pair_at = rows_at(ours + i * chunk, chunk)
        grad_hidden = (
            cot_ref[pair_at, :].astype(f32) + inv * scaled - hidden * (inv * inv * inv * mean)
        )
        gh_ref[at, :] = grad_hidden
        branch_ref[pair_at, :] = grad_hidden.astype(bf16)
        e_copy(i, ours).start()
        return total + jnp.sum(grad * hidden * inv, axis=0, keepdims=True)

    gain_part_ref[...] = lax.fori_loop(0, 4, normal_back, jnp.zeros((1, model), f32))

    def attended_grads(base):
        rows = rows_at(base, half)
        lane = lanes_of(half)
        grad = nt(branch_ref[rows, :], wout_ref[...]).astype(bf16)
        terms = grad.astype(f32) * mixed_ref[rows, :]
        out = grad
        for h in range(plan.heads):
            row_term = jnp.sum(
                jnp.where(lane // 64 == h + 1, terms, 0.0), axis=1, keepdims=True
            )
            for i, part in enumerate(split3(-row_term)):
                out = jnp.where(lane == 3 * h + i, part, out)
        do_ref[rows, :] = out

    attended_grads(ours)

    def e_wait(i, unused):
        e_copy(i, theirs).wait_recv()
        return unused

    lax.fori_loop(0, 4, e_wait, 0)
    attended_grads(theirs)
    for n in (3 * parts - 2, 3 * parts - 1):
        out_copy(n).wait()

    def drain(i, unused):
        b_copy(i, ours).wait_send()
        e_copy(i, ours).wait_send()
        return unused

    lax.fori_loop(0, 4, drain, 0)


def middle(plan, cycle_size, attended, mixed, w_out, tokens, cot, gain, w_gate, w_up, w_down):
    half, model = tokens.shape
    pair = attended.shape[0]
    units = w_down.shape[0]
    size = units // cycle_size
    chunk = half // 4
    hbm = pl.BlockSpec(memory_space=pl.ANY)
    dma = pltpu.SemaphoreType.DMA
    return pl.pallas_call(
        functools.partial(middle_kernel, plan, cycle_size),
        out_shape=[
            jax.ShapeDtypeStruct((half, model), f32),
            jax.ShapeDtypeStruct((half, model), f32),
            jax.ShapeDtypeStruct((pair, model), bf16),
            jax.ShapeDtypeStruct((pair, model), bf16),
            jax.ShapeDtypeStruct((pair, WIDE), bf16),
            jax.ShapeDtypeStruct((1, model), f32),
            jax.ShapeDtypeStruct((cycle_size, 3, size, model), bf16),
        ],
        in_specs=[vmem] * 6 + [hbm] * 3,
        out_specs=[vmem] * 6 + [hbm],
        scratch_shapes=[
            pltpu.VMEM((model, units), bf16),
            pltpu.VMEM((model, units), bf16),
            pltpu.VMEM((model, units), bf16),
            pltpu.VMEM((pair, units), bf16),
            pltpu.VMEM((pair, units), bf16),
            pltpu.VMEM((pair, units), bf16),
            pltpu.VMEM((pair, model), bf16),
            pltpu.VMEM((4, chunk, model), bf16),
            pltpu.VMEM((4, chunk, model), bf16),
            pltpu.VMEM((4, chunk, model), bf16),
            pltpu.VMEM((4, chunk, model), bf16),
            pltpu.VMEM((half, model), f32),
            pltpu.VMEM((half, model), f32),
            pltpu.VMEM((half, model), f32),
            pltpu.VMEM((2, cycle_size // 2, size, model), bf16),
            dma((3,)),
            dma((2, 16)),
            dma((6,)),
        ],
        compiler_params=pltpu.CompilerParams(
            vmem_limit_bytes=60 * 2**20, collective_id=3, has_side_effects=True
        ),
        name="feed_forward",
    )(attended, mixed, w_out, tokens, cot, gain, w_gate, w_up, w_down.T)


def shards(
    tokens,
    doc_lengths,
    key_mask,
    gain_attn,
    w_query,
    w_key,
    w_value,
    w_out,
    bias_table,
    gain_ffn,
    w_gate,
    w_up,
    w_down,
    cotangent,
):
    own_rows, model = tokens.shape
    group = lax.axis_size("wa")
    cycle_size = lax.axis_size("ctx")
    pair = own_rows * group
    heads = bias_table.shape[1]
    docs = doc_lengths.shape[0]
    plan = Plan(heads, w_query.shape[1] // heads, docs)
    total_rows = pair * cycle_size
    doc_most = min(MAXLEN, total_rows // 2)
    reach = min(cycle_size - 1, (doc_most - 1) // pair + 1)
    base = lax.axis_index("ctx") * pair
    rows = min(total_rows, (2 * reach + 1) * pair)
    origin = jnp.clip(base - reach * pair, 0, total_rows - rows).astype(jnp.int32)
    ends = jnp.cumsum(doc_lengths).astype(jnp.int32)
    starts = ends - doc_lengths

    def doc_at(positions):
        return jnp.sum((positions[:, None] >= starts[None, :]).astype(jnp.int32), axis=1) - 1

    tiles = pair // TQ
    tile_start = base + TQ * jnp.arange(tiles, dtype=jnp.int32)
    first_doc = jnp.arange(docs, dtype=jnp.int32)[None, :] == doc_at(tile_start)[:, None]
    last_doc = jnp.arange(docs, dtype=jnp.int32)[None, :] == doc_at(tile_start + TQ - 1)[:, None]
    low_end = jnp.sum(jnp.where(first_doc, starts[None, :], 0), axis=1)
    high_end = jnp.sum(jnp.where(last_doc, ends[None, :], 0), axis=1)
    n_left = jnp.maximum(0, (tile_start - EDGE - low_end + TK - 1) // TK)
    n_right = jnp.maximum(0, (high_end - (tile_start - EDGE + TK) + TK - 1) // TK)
    bounds = jnp.concatenate(
        [(base - origin)[None], jnp.stack([n_left, n_right], axis=1).reshape(-1)]
    ).astype(jnp.int32)

    mask_all = lax.all_gather(key_mask, "ctx", axis=0, tiled=True)
    pair_cot = lax.all_gather(cotangent, "wa", axis=0, tiled=True)

    def window(gathered):
        if rows == total_rows:
            return gathered
        return lax.dynamic_slice_in_dim(gathered, origin, rows, 0)

    gather = functools.partial(lax.all_gather, axis_name="ctx", axis=0, tiled=True)
    positions = origin + jnp.arange(rows, dtype=jnp.int32)
    doc_of = doc_at(positions)
    lane = jnp.arange(128, dtype=jnp.int32)[None, :] + 128
    code = lane - plan.doc_lane
    bit_differs = ((doc_of[:, None] >> (code >> 1)) & 1) != (code & 1)
    k_aug = jnp.where(
        lane == plan.mask_lane,
        window(mask_all).astype(f32)[:, None],
        jnp.where(
            lane < plan.stat_lane,
            jnp.where(bit_differs & (code >= 0), neg_big, 0.0),
            (lane < plan.stat_lane + 3 * heads).astype(f32),
        ),
    ).astype(bf16)
    own_docs = doc_at(base + jnp.arange(pair, dtype=jnp.int32))
    own_differs = ((own_docs[:, None] >> (code >> 1)) & 1) != (code & 1)
    q_aug = jnp.where(
        lane == plan.mask_lane, 1.0, ((lane < plan.stat_lane) & ~own_differs).astype(f32)
    ).astype(bf16)
    q_aug = jnp.concatenate([jnp.zeros((pair, 128), bf16), q_aug], axis=1)
    pair_normed, q_wide, own_kv, kv_all = first(
        plan, cycle_size, reach, tokens, gain_attn[None], q_aug, w_query, w_key, w_value
    )
    kv_all = window(kv_all.reshape(total_rows, 2 * plan.cols))
    near_bias = pl.pallas_call(
        functools.partial(near_kernel, heads),
        out_shape=jax.ShapeDtypeStruct((2, heads, TQ, TK), f32),
        in_specs=[smem],
        out_specs=vmem,
        compiler_params=params(),
        name="near_bias",
    )(bias_table)

    padded = rows + 2 * PAD
    attended, mixed, q_back = pl.pallas_call(
        functools.partial(fwd_kernel, plan, rows, pair),
        out_shape=(
            jax.ShapeDtypeStruct((pair, WIDE), bf16),
            jax.ShapeDtypeStruct((pair, WIDE), f32),
            jax.ShapeDtypeStruct((pair, WIDE), bf16),
        ),
        in_specs=[smem, smem, vmem, vmem, vmem, vmem],
        out_specs=(vmem, vmem, vmem),
        scratch_shapes=[
            pltpu.VMEM((padded, WIDE), bf16),
            pltpu.VMEM((padded, WIDE), bf16),
            pltpu.VMEM((heads, TQ, WIDE), f32),
            pltpu.VMEM((heads, TQ, 128), f32),
            pltpu.VMEM((heads, TQ, WIDE), bf16),
        ],
        compiler_params=params(),
        name="attention_forward",
    )(bounds, bias_table, kv_all, k_aug, q_wide, near_bias)
    q_all = window(gather(q_back))
    w_out_pad = jnp.concatenate([jnp.zeros((64, model), bf16), w_out], axis=0)
    hidden, grad_hidden, pair_branch, ffn_part, do_wide, gain_ffn_part, stacked = middle(
        plan,
        cycle_size,
        attended,
        mixed,
        w_out_pad,
        tokens,
        pair_cot,
        gain_ffn[None],
        w_gate,
        w_up,
        w_down,
    )
    units = stacked.shape[2]
    stacked = lax.psum_scatter(
        stacked.reshape(-1, model), "ctx", scatter_dimension=0, tiled=True
    ).astype(f32)
    grad_w_down = stacked[:units]
    grad_w_gate, grad_w_up = (stacked[units : 2 * units].T, stacked[2 * units :].T)
    do_all = window(gather(do_wide))

    grad_queries, table_part = pl.pallas_call(
        functools.partial(dq_kernel, plan, rows, pair),
        out_shape=(
            jax.ShapeDtypeStruct((pair, WIDE), bf16),
            jax.ShapeDtypeStruct((heads, 32, 128), f32),
        ),
        in_specs=[smem, smem, vmem, vmem, vmem, vmem, vmem],
        out_specs=(vmem, vmem),
        scratch_shapes=[
            pltpu.VMEM((padded, WIDE), bf16),
            pltpu.VMEM((padded, WIDE), bf16),
            pltpu.VMEM((heads, TQ, WIDE), f32),
            pltpu.VMEM((heads, TQ, WIDE), bf16),
            pltpu.VMEM((heads, TQ, WIDE), bf16),
            pltpu.VMEM((heads, TQ, TK), f32),
            pltpu.VMEM((2, heads, TQ, 128), f32),
        ],
        compiler_params=params(),
        name="attention_grad_queries",
    )(bounds, bias_table, kv_all, k_aug, q_back, do_wide, near_bias)
    own_aug = lax.dynamic_slice_in_dim(k_aug, base - origin, pair, 0)
    grad_keys, grad_values, mask_part = pl.pallas_call(
        functools.partial(dkv_kernel, plan, rows, pair),
        out_shape=(
            jax.ShapeDtypeStruct((pair, WIDE), bf16),
            jax.ShapeDtypeStruct((pair, WIDE), bf16),
            jax.ShapeDtypeStruct((tiles, 8, TQ), f32),
        ),
        in_specs=[smem, smem, vmem, vmem, vmem, vmem, vmem],
        out_specs=(vmem, vmem, vmem),
        scratch_shapes=[
            pltpu.VMEM((padded, WIDE), bf16),
            pltpu.VMEM((padded, WIDE), bf16),
            pltpu.VMEM((heads, TQ, WIDE), bf16),
            pltpu.VMEM((heads, TQ, WIDE), bf16),
            pltpu.VMEM((heads, TQ, WIDE), f32),
            pltpu.VMEM((heads, TQ, WIDE), f32),
        ],
        compiler_params=params(),
        name="attention_grad_keys",
    )(bounds, bias_table, q_all, do_all, own_kv, own_aug, near_bias)
    cols = plan.cols
    gap = jnp.zeros((model, WIDE - cols), bf16)
    w_wide = jnp.concatenate([w_query, gap, w_key, gap, gap, w_value], axis=1)
    table_row = jnp.sum(table_part, axis=2).reshape(1, -1)
    table_row = jnp.pad(table_row, ((0, 0), (0, model - table_row.shape[1])))
    small = jnp.concatenate(
        [jnp.zeros((1, model), f32), gain_ffn_part, table_row, jnp.zeros((5, model), f32)],
        axis=0,
    )
    layer_out, grad_tokens, grad_mask, weights, totals = finish(
        plan,
        cycle_size,
        grad_queries,
        grad_keys,
        grad_values,
        mask_part.reshape(group, 8, own_rows),
        w_wide,
        pair_normed,
        attended,
        pair_branch,
        tokens,
        gain_attn[None],
        hidden,
        grad_hidden,
        ffn_part,
        small,
    )
    weights = weights.reshape(4, cols, model).astype(f32)
    return (
        layer_out,
        grad_tokens,
        grad_mask[0],
        totals[0],
        weights[0].T,
        weights[1].T,
        weights[2].T,
        weights[3],
        totals[2, : heads * 32].reshape(heads, 32).T,
        totals[1],
        grad_w_gate,
        grad_w_up,
        grad_w_down,
    )


def solution(mesh):
    placed = (
        P(("ctx", "wa"), None),
        P(),
        P("ctx"),
        P(),
        P(None, "wa"),
        P(None, "wa"),
        P(None, "wa"),
        P("wa", None),
        P(None, "wa"),
        P(),
        P(None, "wa"),
        P(None, "wa"),
        P("wa", None),
        P(("ctx", "wa"), None),
    )
    return jax.shard_map(
        shards,
        mesh=mesh,
        in_specs=placed,
        out_specs=(
            P(("ctx", "wa"), None),
            P(("ctx", "wa"), None),
            P(("ctx", "wa")),
            P(),
            P(None, "wa"),
            P(None, "wa"),
            P(None, "wa"),
            P("wa", None),
            P(None, "wa"),
            P(),
            P(None, ("wa", "ctx")),
            P(None, ("wa", "ctx")),
            P(("wa", "ctx"), None),
        ),
        check_vma=False,
    )
```

```python
import functools

import jax
import jax.numpy as jnp
from jax import lax
from jax.experimental import pallas as pl
from jax.experimental.pallas import tpu as pltpu
from jax.sharding import PartitionSpec as P

MAXLEN = 8192

bucket_edges = (12, 16, 23, 32, 46, 64, 91)
neg_big = -1e30
eps = 1e-06
far_left_bucket = 15
far_right_bucket = 31
WIDE = 256
TQ = 256
TK = 512
EDGE = 128
PAD = TK + EDGE
f32 = jnp.float32
bf16 = jnp.bfloat16


def bucket_of(relative):
    distance = jnp.abs(relative)
    bucket = jnp.minimum(distance, 8) + 16 * (relative > 0).astype(jnp.int32)
    for edge in bucket_edges:
        bucket = bucket + (distance >= edge).astype(jnp.int32)
    return bucket


def norm_forward(inputs, gain):
    inv_root = lax.rsqrt(jnp.mean(inputs * inputs, axis=-1, keepdims=True) + eps)
    return (inputs * inv_root * gain, inv_root)


def norm_backward(inputs, inv_root, gain, grad_normed):
    scaled = gain * grad_normed
    cubed = inv_root * inv_root * inv_root
    grad_inputs = inv_root * scaled - inputs * cubed * jnp.mean(
        inputs * scaled, axis=-1, keepdims=True
    )
    grad_gain = jnp.sum(grad_normed * inputs * inv_root, axis=0)
    return (grad_inputs, grad_gain)


def gated(gate, upward):
    return jax.nn.gelu(gate, approximate=True) * upward


def nt(a, b):
    return lax.dot_general(a, b, (((1,), (1,)), ((), ())), preferred_element_type=f32)


def nn(a, b):
    return lax.dot_general(a, b, (((1,), (0,)), ((), ())), preferred_element_type=f32)


def split3(x):
    hi = x.astype(bf16)
    rest = x - hi.astype(f32)
    mid = rest.astype(bf16)
    return (hi, mid, (rest - mid.astype(f32)).astype(bf16))


class Plan:
    def __init__(self, heads, width, docs):
        self.heads = heads
        self.width = width
        self.bits = max(1, (docs - 1).bit_length())
        self.cols = heads * width
        self.mask_lane = self.cols
        self.doc_lane = self.cols + 1
        self.stat_lane = self.doc_lane + 2 * self.bits
        assert self.stat_lane + 3 * heads <= WIDE and self.cols + 64 == WIDE and width == 64

    def key_lanes(self, lane, h):
        own = (lane >= h * self.width) & (lane < (h + 1) * self.width)
        aug = (lane >= self.mask_lane) & (lane < self.stat_lane)
        stat = (lane >= self.stat_lane + 3 * h) & (lane < self.stat_lane + 3 * h + 3)
        return own | aug | stat

    def value_lanes(self, lane, h):
        own = (lane >= 64 + h * self.width) & (lane < 64 + (h + 1) * self.width)
        return own | ((lane >= 3 * h) & (lane < 3 * h + 3))


def lanes_of(rows, width=WIDE):
    return lax.broadcasted_iota(jnp.int32, (rows, width), 1)


def near_kernel(heads, table_ref, near_ref):
    row = lax.broadcasted_iota(jnp.int32, (EDGE, 3 * EDGE), 0)
    col = lax.broadcasted_iota(jnp.int32, (EDGE, 3 * EDGE), 1)
    relative = col - EDGE - row
    for flip in range(2):
        bucket = bucket_of(-relative if flip else relative)
        left, right = (far_left_bucket, far_right_bucket)
        if flip:
            left, right = (right, left)
        for h in range(heads):
            base = jnp.full((EDGE, 3 * EDGE), table_ref[0, h], f32)
            for b in range(1, 32):
                base = jnp.where(bucket == b, table_ref[b, h], base)
            far_l = jnp.full((EDGE, EDGE), table_ref[left, h], f32)
            far_r = jnp.full((EDGE, EDGE), table_ref[right, h], f32)
            near_ref[flip, h, :EDGE, : 3 * EDGE] = base
            near_ref[flip, h, :EDGE, 3 * EDGE :] = far_r
            near_ref[flip, h, EDGE:, EDGE:] = base
            near_ref[flip, h, EDGE:, :EDGE] = far_l


def build_keys(plan, g_ref, kaug_ref, km, vm, rows):
    km[:PAD, :] = jnp.broadcast_to(
        jnp.where(pad_lanes(plan), neg_big, 0.0).astype(bf16), (PAD, WIDE)
    )
    km[pl.ds(PAD + rows, PAD), :] = km[:PAD, :]
    vm[:PAD, :] = jnp.zeros((PAD, WIDE), bf16)
    vm[pl.ds(PAD + rows, PAD), :] = jnp.zeros((PAD, WIDE), bf16)
    step = 512
    low = lanes_of(step, 128) < 64
    ones = (lanes_of(step, 128) < 3 * plan.heads).astype(bf16)

    def body(n, unused):
        at = pl.multiple_of(n * step, step)
        to = pl.multiple_of(PAD + n * step, 128)
        middle = g_ref[pl.ds(at, step), 128:256]
        km[pl.ds(to, step), 0:128] = g_ref[pl.ds(at, step), 0:128]
        km[pl.ds(to, step), 128:256] = jnp.where(low, middle, kaug_ref[pl.ds(at, step), :])
        vm[pl.ds(to, step), 0:128] = jnp.where(low, ones, middle)
        vm[pl.ds(to, step), 128:256] = g_ref[pl.ds(at, step), 256:384]
        return unused

    lax.fori_loop(0, rows // step, body, 0)


def pad_lanes(plan):
    lane = lanes_of(1)
    return (lane >= plan.doc_lane) & (lane < plan.stat_lane)


def fwd_kernel(
    plan, rows, pair, bounds, table_ref, g_ref, kaug_ref, q_ref, near_ref,
    low_ref, wide_ref, qb_ref, km, vm, acc, row_max, qh_ref,
):
    build_keys(plan, g_ref, kaug_ref, km, vm, rows)
    lane = lanes_of(TQ)

    def tile(t, unused):
        start = pl.multiple_of(bounds[0] + t * TQ, 128)
        n_left, n_right = (bounds[1 + 2 * t], bounds[2 + 2 * t])
        out = pl.ds(pl.multiple_of(t * TQ, TQ), TQ)
        q = q_ref[out, :]
        near = pl.ds(pl.multiple_of(start + PAD - EDGE, 128), TK)
        for h in range(plan.heads):
            qh = jnp.where(plan.key_lanes(lane, h), q, jnp.zeros_like(q))
            qh_ref[h] = qh
            s = nt(qh, km[near, :]) + near_ref[0, h]
            top = jnp.max(s, axis=1, keepdims=True)
            p = jnp.exp(s - top).astype(bf16)
            acc[h] = nn(p, vm[near, :])
            row_max[h] = jnp.broadcast_to(top, (TQ, 128))

        def far(bucket):
            def step(first, n):
                span = pl.ds(pl.multiple_of(first + n, 128), TK)
                for h in range(plan.heads):
                    s = nt(qh_ref[h], km[span, :])
                    offset = table_ref[bucket, h]
                    old = row_max[h][:, :1]
                    top = jnp.maximum(old, jnp.max(s, axis=1, keepdims=True) + offset)
                    p = jnp.exp(s - (top - offset)).astype(bf16)
                    acc[h] = acc[h] * jnp.exp(old - top) + nn(p, vm[span, :])
                    row_max[h] = jnp.broadcast_to(top, (TQ, 128))
            return step

        left, right = (far(far_left_bucket), far(far_right_bucket))

        @pl.loop(0, n_left)
        def _(n):
            left(start + PAD - EDGE - TK, -n * TK)

        @pl.loop(0, n_right)
        def _(n):
            right(start + PAD - EDGE + TK, n * TK)

        wide = jnp.zeros((TQ, WIDE), f32)
        qb = jnp.where(lane < plan.stat_lane, q, jnp.zeros_like(q))
        for h in range(plan.heads):
            total = acc[h][:, 3 * h : 3 * h + 1]
            log_total = row_max[h][:, :1] + jnp.log(total)
            wide = jnp.where(lane // 64 == h + 1, acc[h] / total, wide)
            for i, part in enumerate(split3(-log_total)):
                qb = jnp.where(lane == plan.stat_lane + 3 * h + i, part, qb)
        wide_ref[out, :] = wide
        low_ref[out, :] = wide.astype(bf16)
        qb_ref[out, :] = qb
        return unused

    lax.fori_loop(0, pair // TQ, tile, 0)


def dq_kernel(
    plan, rows, pair, bounds, table_ref, g_ref, kaug_ref, qb_ref, do_ref, near_ref,
    dq_ref, tab_ref, km, vm, acc, qh_ref, doh_ref, near_acc, far_acc,
):
    build_keys(plan, g_ref, kaug_ref, km, vm, rows)
    lane = lanes_of(TQ)
    near_acc[...] = jnp.zeros_like(near_acc)
    far_acc[...] = jnp.zeros_like(far_acc)

    def tile(t, unused):
        start = pl.multiple_of(bounds[0] + t * TQ, 128)
        n_left, n_right = (bounds[1 + 2 * t], bounds[2 + 2 * t])
        out = pl.ds(pl.multiple_of(t * TQ, TQ), TQ)
        q = qb_ref[out, :]
        do = do_ref[out, :]
        near = pl.ds(pl.multiple_of(start + PAD - EDGE, 128), TK)

        def grads(h, s, span):
            p = jnp.exp(s)
            return p * nt(doh_ref[h], vm[span, :])

        for h in range(plan.heads):
            qh_ref[h] = jnp.where(plan.key_lanes(lane, h), q, jnp.zeros_like(q))
            doh_ref[h] = jnp.where(plan.value_lanes(lane, h), do, jnp.zeros_like(do))
            ds = grads(h, nt(qh_ref[h], km[near, :]) + near_ref[0, h], near)
            near_acc[h] += ds
            acc[h] = nn(ds.astype(bf16), km[near, :])

        def far(bucket, slot):
            def step(first, n):
                span = pl.ds(pl.multiple_of(first + n, 128), TK)
                for h in range(plan.heads):
                    ds = grads(h, nt(qh_ref[h], km[span, :]) + table_ref[bucket, h], span)
                    acc[h] += nn(ds.astype(bf16), km[span, :])
                    far_acc[slot, h] += (
                        ds[:, 0:128] + ds[:, 128:256] + ds[:, 256:384] + ds[:, 384:512]
                    )
            return step

        left, right = (far(far_left_bucket, 0), far(far_right_bucket, 1))

        @pl.loop(0, n_left)
        def _(n):
            left(start + PAD - EDGE - TK, -n * TK)

        @pl.loop(0, n_right)
        def _(n):
            right(start + PAD - EDGE + TK, n * TK)

        total = jnp.zeros((TQ, WIDE), f32)
        for h in range(plan.heads):
            total = jnp.where(lane // 64 == h, acc[h], total)
        dq_ref[out, :] = total.astype(bf16)
        return unused

    lax.fori_loop(0, pair // TQ, tile, 0)
    row = lax.broadcasted_iota(jnp.int32, (EDGE, 3 * EDGE), 0)
    col = lax.broadcasted_iota(jnp.int32, (EDGE, 3 * EDGE), 1)
    bucket = bucket_of(col - EDGE - row)
    for h in range(plan.heads):
        band = near_acc[h, :EDGE, : 3 * EDGE] + near_acc[h, EDGE:, EDGE:]
        extra_right = near_acc[h, :EDGE, 3 * EDGE :]
        extra_left = near_acc[h, EDGE:, :EDGE]
        for b in range(32):
            part = jnp.sum(jnp.where(bucket == b, band, 0.0), axis=0, keepdims=True)
            part = part[:, :128] + part[:, 128:256] + part[:, 256:]
            if b == far_left_bucket:
                part = part + jnp.sum(far_acc[0, h], axis=0, keepdims=True)
                part = part + jnp.sum(extra_left, axis=0, keepdims=True)
            if b == far_right_bucket:
                part = part + jnp.sum(far_acc[1, h], axis=0, keepdims=True)
                part = part + jnp.sum(extra_right, axis=0, keepdims=True)
            tab_ref[h, b : b + 1, :] = part


def dkv_kernel(
    plan, rows, pair, bounds, table_ref, qall_ref, doall_ref, g_ref, kaug_ref, near_ref,
    dk_ref, dv_ref, mask_ref, qp, dop, kh_ref, vh_ref, acc_k, acc_v,
):
    lane = lanes_of(TQ)
    first = lanes_of(1)
    stat = (first >= plan.stat_lane) & (first < plan.stat_lane + 3 * plan.heads)
    qp[:PAD, :] = jnp.broadcast_to(jnp.where(stat, neg_big, 0.0).astype(bf16), (PAD, WIDE))
    qp[pl.ds(PAD + rows, PAD), :] = qp[:PAD, :]
    dop[:PAD, :] = jnp.zeros((PAD, WIDE), bf16)
    dop[pl.ds(PAD + rows, PAD), :] = jnp.zeros((PAD, WIDE), bf16)
    step = 512

    def fill(n, unused):
        at = pl.multiple_of(n * step, step)
        to = pl.multiple_of(PAD + n * step, 128)
        qp[pl.ds(to, step), :] = qall_ref[pl.ds(at, step), :]
        dop[pl.ds(to, step), :] = doall_ref[pl.ds(at, step), :]
        return unused

    lax.fori_loop(0, rows // step, fill, 0)
    low = lanes_of(TQ, 128) < 64
    ones = (lanes_of(TQ, 128) < 3 * plan.heads).astype(bf16)

    def tile(t, unused):
        start = pl.multiple_of(bounds[0] + t * TQ, 128)
        n_left, n_right = (bounds[1 + 2 * t], bounds[2 + 2 * t])
        out = pl.ds(pl.multiple_of(t * TQ, TQ), TQ)
        middle = g_ref[out, 128:256]
        k = jnp.concatenate([g_ref[out, 0:128], jnp.where(low, middle, kaug_ref[out, :])], axis=1)
        v = jnp.concatenate([jnp.where(low, ones, middle), g_ref[out, 256:384]], axis=1)
        near = pl.ds(pl.multiple_of(start + PAD - EDGE, 128), TK)

        def grads(h, s, span):
            p = jnp.exp(s)
            ds = p * nt(vh_ref[h], dop[span, :])
            return nn(p.astype(bf16), dop[span, :]), nn(ds.astype(bf16), qp[span, :])

        for h in range(plan.heads):
            kh_ref[h] = jnp.where(plan.key_lanes(lane, h), k, jnp.zeros_like(k))
            vh_ref[h] = jnp.where(plan.value_lanes(lane, h), v, jnp.zeros_like(v))
            acc_v[h], acc_k[h] = grads(h, nt(kh_ref[h], qp[near, :]) + near_ref[1, h], near)

        def far(bucket):
            def step(first, n):
                span = pl.ds(pl.multiple_of(first + n, 128), TK)
                for h in range(plan.heads):
                    add_v, add_k = grads(
                        h, nt(kh_ref[h], qp[span, :]) + table_ref[bucket, h], span
                    )
                    acc_v[h] += add_v
                    acc_k[h] += add_k
            return step

        left, right = (far(far_right_bucket), far(far_left_bucket))

        @pl.loop(0, n_left)
        def _(n):
            left(start + PAD - EDGE - TK, -n * TK)

        @pl.loop(0, n_right)
        def _(n):
            right(start + PAD - EDGE + TK, n * TK)

        dk = jnp.zeros((TQ, WIDE), f32)
        dv = jnp.zeros((TQ, WIDE), f32)
        mask_grad = jnp.zeros((TQ, 1), f32)
        for h in range(plan.heads):
            dk = jnp.where(lane // 64 == h, acc_k[h], dk)
            dv = jnp.where(lane // 64 == h + 1, acc_v[h], dv)
            mask_grad = mask_grad + acc_k[h][:, plan.mask_lane : plan.mask_lane + 1]
        mask_ref[t] = jnp.transpose(jnp.broadcast_to(mask_grad, (TQ, 128)))[:8, :]
        dk_ref[out, :] = dk.astype(bf16)
        dv_ref[out, :] = dv.astype(bf16)
        return unused

    lax.fori_loop(0, pair // TQ, tile, 0)


def grad_attended_kernel(plan, branch_ref, w_ref, wide_ref, do_ref):
    rows = branch_ref.shape[0]
    lane = lanes_of(rows)
    grad = nt(branch_ref[...], w_ref[...]).astype(bf16)
    terms = grad.astype(f32) * wide_ref[...]
    out = grad
    for h in range(plan.heads):
        row_term = jnp.sum(
            jnp.where(lane // 64 == h + 1, terms, 0.0), axis=1, keepdims=True
        )
        for i, part in enumerate(split3(-row_term)):
            out = jnp.where(lane == 3 * h + i, part, out)
    do_ref[...] = out


vmem = pl.BlockSpec(memory_space=pltpu.VMEM)
smem = pl.BlockSpec(memory_space=pltpu.SMEM)


def params():
    return pltpu.CompilerParams(vmem_limit_bytes=56 * 2**20)


class Spot:
    def __init__(self, lines):
        index = lax.axis_index("ctx")
        self.wa = lax.axis_index("wa")
        self.index = index
        self.lines = lines
        self.z = index // 4
        self.x = (index // 2) % 2
        self.core = index % 2

    def core_mate(self):
        return (self.index + 1 - 2 * self.core, self.wa)

    def x_mate(self):
        return (self.index + 2 - 4 * self.x, self.wa)

    def z_mate(self, step):
        return (jnp.clip(self.index + 4 * step, 0, 4 * self.lines - 1), self.wa)

    def y_mate(self):
        return (self.index, 1 - self.wa)


def send(src, dst, send_sem, recv_sem, device):
    return pltpu.make_async_remote_copy(
        src_ref=src,
        dst_ref=dst,
        send_sem=send_sem,
        recv_sem=recv_sem,
        device_id=device,
        device_id_type=pl.DeviceIdType.MESH,
    )


def greet(spot, with_y):
    barrier = pltpu.get_barrier_semaphore()
    mates = [spot.core_mate(), spot.x_mate()] + ([spot.y_mate()] if with_y else [])
    for mate in mates:
        pl.semaphore_signal(barrier, inc=1, device_id=mate, device_id_type=pl.DeviceIdType.MESH)

    @pl.when(spot.z + 1 < spot.lines)
    def _():
        pl.semaphore_signal(
            barrier, inc=1, device_id=spot.z_mate(1), device_id_type=pl.DeviceIdType.MESH
        )

    @pl.when(spot.z > 0)
    def _():
        pl.semaphore_signal(
            barrier, inc=1, device_id=spot.z_mate(-1), device_id_type=pl.DeviceIdType.MESH
        )

    above = (spot.z + 1 < spot.lines).astype(jnp.int32)
    below = (spot.z > 0).astype(jnp.int32)
    pl.semaphore_wait(barrier, len(mates) + above + below)


def added(a, b):
    return (a.astype(f32) + b.astype(f32)).astype(bf16)


def scatter_kernel(lines, units, z_first, count, *refs):
    parts, outs = (refs[:count], refs[count : 2 * count])
    mine, core_in, x_in, up_in, down_in, load_sem, core_sem, x_sem, up_sem, down_sem = refs[
        2 * count :
    ]
    spot = Spot(lines)
    z, x, core = (spot.z, spot.x, spot.core)
    greet(spot, False)
    loads = []
    cores = []
    order = z_first + [u for u in range(len(units)) if u not in z_first]

    def rows_of(u):
        return pl.ds(units[u][1], units[u][2])

    for u in order:
        m = units[u][0]
        load = pltpu.make_async_copy(
            parts[m].at[:, :, core, rows_of(u)], mine.at[m, :, :, rows_of(u)], load_sem.at[u]
        )
        load.start()
        loads.append(load)
        copy = send(
            parts[m].at[:, :, 1 - core, rows_of(u)],
            core_in.at[m, :, :, rows_of(u)],
            core_sem.at[0, u],
            core_sem.at[1, u],
            spot.core_mate(),
        )
        copy.start()
        cores.append(copy)

    def add_slices(into, source, u, x_slot):
        m = units[u][0]

        def body(line, unused):
            at = (m, line, x_slot, rows_of(u))
            into[at] = added(into[at], source[at])
            return unused

        lax.fori_loop(0, lines, body, 0)

    def x_copy(u, both):
        m = units[u][0]
        if both:
            src = mine.at[m, :, 1 - x, rows_of(u)]
            dst = x_in.at[m, :, rows_of(u)]
        else:
            src = mine.at[m, z, 1 - x, rows_of(u)]
            dst = x_in.at[m, z, rows_of(u)]
        return send(src, dst, x_sem.at[0, u], x_sem.at[1, u], spot.x_mate())

    def line_flow(u, slots):
        m = units[u][0]
        n = len(slots)

        def slot_copies(step, d):
            ring, sem = (up_in, up_sem) if step > 0 else (down_in, down_sem)
            return [
                send(
                    mine.at[m, d, s, rows_of(u)],
                    ring.at[m, d, s, rows_of(u)],
                    sem.at[0, u, d, i],
                    sem.at[1, u, d, i],
                    spot.z_mate(step),
                )
                for i, s in enumerate(slots)
            ]

        def receive(step, d):
            ring = up_in if step > 0 else down_in
            for copy, s in zip(slot_copies(step, d), slots):
                copy.wait_recv()
                at = (m, d, s, rows_of(u))
                mine[at] = added(mine[at], ring[at])

        def ends_first():
            @pl.when(z == 0)
            def _():
                for d in range(lines - 1, 0, -1):
                    for copy in slot_copies(1, d):
                        copy.start()

            @pl.when(z == lines - 1)
            def _():
                for d in range(lines - 1):
                    for copy in slot_copies(-1, d):
                        copy.start()

        def relay():
            def body(k, unused):
                high = lines - 1 - k

                @pl.when((z < high) & (z > 0))
                def _():
                    receive(1, high)
                    for copy in slot_copies(1, high):
                        copy.start()

                @pl.when((z > k) & (z + 1 < lines))
                def _():
                    receive(-1, k)
                    for copy in slot_copies(-1, k):
                        copy.start()

                return unused

            lax.fori_loop(0, lines - 1, body, 0)

        def arrive():
            @pl.when(z > 0)
            def _():
                receive(1, z)

            @pl.when(z + 1 < lines)
            def _():
                receive(-1, z)

        def finish(k, unused):
            @pl.when(z < lines - 1 - k)
            def _():
                for copy in slot_copies(1, lines - 1 - k):
                    copy.wait_send()

            @pl.when(z > k)
            def _():
                for copy in slot_copies(-1, k):
                    copy.wait_send()

            return unused

        return (
            ends_first,
            relay,
            arrive,
            lambda: lax.fori_loop(0, lines - 1, finish, 0),
        )

    def store(u):
        m = units[u][0]
        outs[m][rows_of(u), :] = mine[m, z, x, rows_of(u)].astype(f32)

    pending = {}
    for i, u in enumerate(order):
        loads[i].wait()
        cores[i].wait()
        if u in z_first:
            add_slices(mine, core_in, u, 0)
            add_slices(mine, core_in, u, 1)
        else:
            add_slices(mine, core_in, u, 1 - x)
            copy = x_copy(u, True)
            copy.start()
            pending[u] = copy
            add_slices(mine, core_in, u, x)
    x_first = [u for u in order if u not in z_first]
    flows = {u: line_flow(u, [0, 1] if u in z_first else [x]) for u in order}
    last = {}

    def x_stage(u):
        m = units[u][0]
        pending[u].wait()

        def body(line, unused):
            at = (m, line, x, rows_of(u))
            mine[at] = added(mine[at], x_in[m, line, rows_of(u)])
            return unused

        lax.fori_loop(0, lines, body, 0)

    def settle(u):
        flows[u][2]()
        if u in z_first:
            last[u] = x_copy(u, False)
            last[u].start()
        else:
            store(u)

    for t in range(len(order) + 2):
        if t < len(order):
            u = order[t]
            if u not in z_first:
                x_stage(u)
            flows[u][0]()
        if 0 <= t - 1 < len(order):
            flows[order[t - 1]][1]()
        if 0 <= t - 2 < len(order):
            settle(order[t - 2])
    for u, copy in last.items():
        m = units[u][0]
        copy.wait()
        at = (m, z, x, rows_of(u))
        mine[at] = added(mine[at], x_in[m, z, rows_of(u)])
        store(u)
    for u in order:
        flows[u][3]()


def reduce_scatter(parts, cycle_size):
    lines = cycle_size // 4
    count = len(parts)
    rows, model = parts[0].shape[1:]
    cut = (rows // 2 + 15) // 16 * 16
    pieces = [(0, cut), (cut, rows - cut)] if cut < rows else [(0, rows)]
    units = [(m, at, size) for m in range(count) for at, size in pieces]
    z_first = [len(units) - 1]
    shaped = [part.reshape(lines, 2, 2, rows, model) for part in parts]
    hbm = pl.BlockSpec(memory_space=pl.ANY)
    n = len(units)
    return pl.pallas_call(
        functools.partial(scatter_kernel, lines, units, z_first, count),
        out_shape=[jax.ShapeDtypeStruct((rows, model), f32)] * count,
        in_specs=[hbm] * count,
        out_specs=[vmem] * count,
        scratch_shapes=[
            pltpu.VMEM((count, lines, 2, rows, model), bf16),
            pltpu.VMEM((count, lines, 2, rows, model), bf16),
            pltpu.VMEM((count, lines, rows, model), bf16),
            pltpu.VMEM((count, lines, 2, rows, model), bf16),
            pltpu.VMEM((count, lines, 2, rows, model), bf16),
            pltpu.SemaphoreType.DMA((n,)),
            pltpu.SemaphoreType.DMA((2, n)),
            pltpu.SemaphoreType.DMA((2, n)),
            pltpu.SemaphoreType.DMA((2, n, lines, 2)),
            pltpu.SemaphoreType.DMA((2, n, lines, 2)),
        ],
        compiler_params=pltpu.CompilerParams(
            vmem_limit_bytes=58 * 2**20, collective_id=1, has_side_effects=True
        ),
        name="weight_scatter",
    )(*shaped)

def first_kernel(
    plan, lines, span, tokens_ref, gain_ref, aug_ref, wq_hbm, wk_hbm, wv_hbm,
    x_ref, tok_ref, q_ref, own_ref, all_hbm,
    weights, zeros, load_sem, y_sem, own_sem, zero_sem, z_sem, x_sem, c_sem,
):
    spot = Spot(lines)
    z, x, core, wa = (spot.z, spot.x, spot.core, spot.wa)
    half, model = tokens_ref.shape
    cols = plan.cols
    chunk = half // 4
    loads = [
        pltpu.make_async_copy(src, weights.at[pl.ds(i * cols, cols)], load_sem.at[i])
        for i, src in enumerate((wk_hbm, wv_hbm, wq_hbm))
    ]
    for load in loads:
        load.start()
    greet(spot, True)
    zeros[...] = jnp.zeros_like(zeros)

    def outside(d):
        return (d < z - span) | (d > z + span)

    def zero_copies(d):
        return [
            pltpu.make_async_copy(zeros, all_hbm.at[d, a, b], zero_sem.at[d, a, b])
            for a in range(2)
            for b in range(2)
        ]

    def zero_start(d, unused):
        @pl.when(outside(d))
        def _():
            for copy in zero_copies(d):
                copy.start()

        return unused

    def rows_at(start, size):
        return pl.ds(pl.multiple_of(start, size), size)

    ours = wa * half
    theirs = (1 - wa) * half

    def y_copy(i, base):
        return send(
            tokens_ref.at[rows_at(i * chunk, chunk)],
            tok_ref.at[rows_at(base + i * chunk, chunk)],
            y_sem.at[0, i],
            y_sem.at[1, i],
            spot.y_mate(),
        )

    def y_start(i, unused):
        y_copy(i, ours).start()
        return unused

    lax.fori_loop(0, 4, y_start, 0)

    def scaled(rows_in):
        rows_in = rows_in.astype(f32)
        inv = lax.rsqrt(jnp.mean(rows_in * rows_in, axis=-1, keepdims=True) + eps)
        return (rows_in * inv * gain_ref[...]).astype(bf16)

    def normal(i, unused):
        at = rows_at(ours + i * chunk, chunk)
        rows_in = tokens_ref[rows_at(i * chunk, chunk), :]
        tok_ref[at, :] = rows_in
        x_ref[at, :] = scaled(rows_in)
        return unused

    lax.fori_loop(0, 4, normal, 0)
    for load in loads:
        load.wait()

    def project(base):
        rows = rows_at(base, half)
        qkv = nt(x_ref[rows, :], weights[...]).astype(bf16)
        own_ref[rows, :] = qkv[:, : 2 * cols]
        q_ref[rows, :] = aug_ref[rows, :]
        q_ref[rows, :cols] = qkv[:, 2 * cols :]

    pieces = [
        (ours, half, True),
        (theirs, half // 2, True),
        (theirs + half // 2, half // 2, False),
    ]

    def piece_rows(p):
        return rows_at(pieces[p][0], pieces[p][1])

    def source(p, d, a):
        return all_hbm.at[d, a, core, piece_rows(p)]

    def pass_copy(p, step, d, own):
        i = 0 if step > 0 else 1
        if pieces[p][2]:
            dst = source(p, d, x)
            src = own_ref.at[piece_rows(p)] if own else dst
        else:
            dst = all_hbm.at[d, :, core, piece_rows(p)]
            src = dst
        return send(src, dst, z_sem.at[p, i, d], z_sem.at[p, 2 + i, d], spot.z_mate(step))

    def across(p, d, own):
        dst = source(p, d, x)
        src = own_ref.at[piece_rows(p)] if own else dst
        return send(src, dst, x_sem.at[p, 0, d], x_sem.at[p, 1, d], spot.x_mate())

    def beside(p, d):
        part = all_hbm.at[d, :, core, piece_rows(p)]
        return send(part, part, c_sem.at[p, 0, d], c_sem.at[p, 1, d], spot.core_mate())

    def own_copy(p):
        return pltpu.make_async_copy(
            own_ref.at[piece_rows(p)], source(p, z, x), own_sem.at[p]
        )

    def both_ways(p, own):
        @pl.when(z + 1 < lines)
        def _():
            pass_copy(p, 1, z, own).start()

        @pl.when(z > 0)
        def _():
            pass_copy(p, -1, z, own).start()

    def begin(p):
        own_copy(p).start()
        across(p, z, True).start()
        if pieces[p][2]:
            both_ways(p, True)

    def level(p, k):
        @pl.when(z - k >= 0)
        def _():
            d = jnp.maximum(z - k, 0)
            pass_copy(p, 1, d, False).wait_recv()
            if k < span:

                @pl.when(z + 1 < lines)
                def _():
                    pass_copy(p, 1, d, False).start()

            if pieces[p][2]:
                across(p, d, False).start()
            else:
                beside(p, d).start()

        @pl.when(z + k < lines)
        def _():
            d = jnp.minimum(z + k, lines - 1)
            pass_copy(p, -1, d, False).wait_recv()
            if k < span:

                @pl.when(z > 0)
                def _():
                    pass_copy(p, -1, d, False).start()

            if pieces[p][2]:
                across(p, d, False).start()
            else:
                beside(p, d).start()

    def turn(p):
        across(p, z, True).wait()
        own_copy(p).wait()
        both_ways(p, False)
        beside(p, z).start()

    def settle(p, k):
        for sign in (1, -1) if k else (1,):
            d = z - sign * k

            @pl.when((d >= 0) & (d < lines))
            def _(d=d):
                d = jnp.clip(d, 0, lines - 1)
                across(p, d, k == 0).wait()
                if k == 0:
                    own_copy(p).wait()
                beside(p, d).start()

    project(ours)
    begin(0)
    lax.fori_loop(0, lines, zero_start, 0)

    def y_wait(i, unused):
        y_copy(i, theirs).wait_recv()
        at = rows_at(theirs + i * chunk, chunk)
        x_ref[at, :] = scaled(tok_ref[at, :])
        return unused

    lax.fori_loop(0, 2, y_wait, 0)
    level(0, 1)
    lax.fori_loop(2, 4, y_wait, 0)
    project(theirs)
    begin(2)
    begin(1)
    if span > 1:
        level(0, 2)
    settle(0, 0)
    turn(2)
    level(1, 1)
    settle(0, 1)
    level(2, 1)
    if span > 1:
        level(1, 2)
        settle(0, 2)
    settle(1, 0)
    settle(1, 1)
    if span > 1:
        level(2, 2)
        settle(1, 2)
    for k in range(3, span + 1):
        for p in range(3):
            level(p, k)
        for p in range(2):
            settle(p, k)

    def finish_line(d, unused):
        @pl.when(~outside(d))
        def _():
            for p in range(3):
                beside(p, d).wait()

        @pl.when(outside(d))
        def _():
            for copy in zero_copies(d):
                copy.wait()

        for p in range(3):

            @pl.when((z + 1 < lines) & (d <= z) & (d > z - span))
            def _(p=p):
                pass_copy(p, 1, d, False).wait_send()

            @pl.when((z > 0) & (d >= z) & (d < z + span))
            def _(p=p):
                pass_copy(p, -1, d, False).wait_send()

        return unused

    lax.fori_loop(0, lines, finish_line, 0)

    def y_drain(i, unused):
        y_copy(i, ours).wait_send()
        return unused

    lax.fori_loop(0, 4, y_drain, 0)


def first(plan, cycle_size, reach, tokens, gain, aug, w_query, w_key, w_value):
    lines = cycle_size // 4
    span = min(lines - 1, (reach + 3) // 4)
    half, model = tokens.shape
    pair = 2 * half
    hbm = pl.BlockSpec(memory_space=pl.ANY)
    dma = pltpu.SemaphoreType.DMA
    return pl.pallas_call(
        functools.partial(first_kernel, plan, lines, span),
        out_shape=[
            jax.ShapeDtypeStruct((pair, model), bf16),
            jax.ShapeDtypeStruct((pair, model), bf16),
            jax.ShapeDtypeStruct((pair, WIDE), bf16),
            jax.ShapeDtypeStruct((pair, 2 * plan.cols), bf16),
            jax.ShapeDtypeStruct((lines, 2, 2, pair, 2 * plan.cols), bf16),
        ],
        in_specs=[vmem] * 3 + [hbm] * 3,
        out_specs=[vmem] * 4 + [hbm],
        scratch_shapes=[
            pltpu.VMEM((3 * plan.cols, model), bf16),
            pltpu.VMEM((pair, 2 * plan.cols), bf16),
            dma((3,)),
            dma((2, 4)),
            dma((3,)),
            dma((lines, 2, 2)),
            dma((3, 4, lines)),
            dma((3, 2, lines)),
            dma((3, 2, lines)),
        ],
        compiler_params=pltpu.CompilerParams(
            vmem_limit_bytes=56 * 2**20, collective_id=4, has_side_effects=True
        ),
        name="project_gather",
    )(tokens, gain, aug, w_query.T, w_key.T, w_value.T)


def tn(a, b):
    return lax.dot_general(a, b, (((0,), (0,)), ((), ())), preferred_element_type=f32)


def line_relay(spot, start, receive):
    def level(k, unused):
        @pl.when(spot.z - k >= 0)
        def _():
            if_first(k, lambda: receive(1, spot.z - k))

            @pl.when(spot.z + 1 < spot.lines)
            def _():
                start(1, spot.z - k)

        @pl.when(spot.z + k < spot.lines)
        def _():
            if_first(k, lambda: receive(-1, spot.z + k))

            @pl.when(spot.z > 0)
            def _():
                start(-1, spot.z + k)

        return unused

    def if_first(k, run):
        @pl.when(k > 0)
        def _():
            run()

    return level


def finish_kernel(
    plan, lines, dq_ref, dk_ref, dv_ref, mask_ref, w3_ref, normed_ref, att_ref, branch_ref, far_ref,
    tokens_ref, gain_ref, hidden_ref, gh_ref, ffn_ref, small_ref,
    out_ref, gt_ref, gm_ref, weights_ref, total_ref,
    mine, core_in, x_in, up_in, down_in, all_w, y_out, y_in, own_part, ffn_in, mask_in,
    small_own, small_y, small_core, small_x, small_all,
    y_sem, core_sem, x_sem, up_sem, down_sem, gz_sem, gx_sem, gc_sem, sz_sem,
):
    spot = Spot(lines)
    z, x, core, wa = (spot.z, spot.x, spot.core, spot.wa)
    greet(spot, True)
    half = tokens_ref.shape[0]
    quarter = half // 2
    model = tokens_ref.shape[1]
    rows = mine.shape[3]

    def grad_rows(at):
        at = pl.ds(pl.multiple_of(at, quarter), quarter)
        return (
            nt(dq_ref[at, :], w3_ref[:, 0:256])
            + nt(dk_ref[at, :], w3_ref[:, 256:512])
            + nt(dv_ref[at, :], w3_ref[:, 512:768])
        )

    def y_copy(i):
        return send(y_out.at[i], y_in.at[i], y_sem.at[0, i], y_sem.at[1, i], spot.y_mate())

    def theirs(i, unused):
        y_out[i] = grad_rows((1 - wa) * half + i * quarter).astype(bf16)
        y_copy(i).start()
        return unused

    lax.fori_loop(0, 2, theirs, 0)
    mask_copy = send(
        mask_ref.at[1 - wa], mask_in, y_sem.at[0, 2], y_sem.at[1, 2], spot.y_mate()
    )
    mask_copy.start()

    def fill(product, matrix):
        for j in range(plan.cols // rows):
            s = matrix * (plan.cols // rows) + j
            mine[s // 4, (s // 2) % 2, s % 2] = product[j * rows : (j + 1) * rows].astype(bf16)

    fill(tn(dq_ref[...], normed_ref[...])[: plan.cols], 0)
    fill(tn(dk_ref[...], normed_ref[...])[: plan.cols], 1)
    fill(tn(dv_ref[...], normed_ref[...])[64:], 2)
    our_rows = pl.ds(pl.multiple_of(wa * half, half), half)
    their_rows = pl.ds(pl.multiple_of((1 - wa) * half, half), half)
    fill(
        (tn(att_ref[our_rows, :], branch_ref[...]) + tn(att_ref[their_rows, :], far_ref[...]))[64:],
        3,
    )
    core_copy = send(
        mine.at[:, :, 1 - core], core_in, core_sem.at[0, 0], core_sem.at[1, 0], spot.core_mate()
    )
    core_copy.start()
    ffn_copy = send(
        ffn_ref.at[their_rows], ffn_in, y_sem.at[0, 3], y_sem.at[1, 3], spot.y_mate()
    )
    ffn_copy.start()

    def ours(i, unused):
        own_part[pl.ds(pl.multiple_of(i * quarter, quarter), quarter), :] = grad_rows(
            wa * half + i * quarter
        )
        return unused

    lax.fori_loop(0, 2, ours, 0)
    core_copy.wait()

    def x_copy(d):
        return send(
            mine.at[d, 1 - x, core], x_in.at[d], x_sem.at[0, d], x_sem.at[1, d], spot.x_mate()
        )

    def core_add(d, unused):
        mine[d, 1 - x, core] = added(mine[d, 1 - x, core], core_in[d, 1 - x])
        x_copy(d).start()
        return unused

    lax.fori_loop(0, lines, core_add, 0)

    def core_add_own(d, unused):
        mine[d, x, core] = added(mine[d, x, core], core_in[d, x])
        return unused

    lax.fori_loop(0, lines, core_add_own, 0)

    gain_sum = jnp.zeros((1, model), f32)
    step = 32
    for i in range(2):
        y_copy(i).wait()

        def normal(j, total, i=i):
            at = pl.ds(pl.multiple_of(i * quarter + j * step, step), step)
            there = pl.ds(pl.multiple_of(j * step, step), step)
            grad = own_part[at, :] + y_in[i, there, :].astype(f32)
            rows_in = tokens_ref[at, :].astype(f32)
            inv = lax.rsqrt(jnp.mean(rows_in * rows_in, axis=-1, keepdims=True) + eps)
            scaled = gain_ref[...] * grad
            mean = jnp.mean(rows_in * scaled, axis=-1, keepdims=True)
            gt_ref[at, :] = gh_ref[at, :] + inv * scaled - rows_in * (inv * inv * inv * mean)
            return total + jnp.sum(grad * rows_in * inv, axis=0, keepdims=True)

        gain_sum = lax.fori_loop(0, quarter // step, normal, gain_sum)
    small_own[...] = small_ref[...]
    small_own[0:1, :] = gain_sum
    small_copy = send(
        small_own, small_y, y_sem.at[0, 4], y_sem.at[1, 4], spot.y_mate()
    )
    small_copy.start()
    mask_copy.wait()
    gm_ref[...] = mask_ref[wa] + mask_in[...]

    def flow(step, d):
        ring, sem = (up_in, up_sem) if step > 0 else (down_in, down_sem)
        return send(
            mine.at[d, x, core], ring.at[d], sem.at[0, d], sem.at[1, d], spot.z_mate(step)
        )

    def merge(step, d):
        flow(step, d).wait_recv()
        ring = up_in if step > 0 else down_in
        mine[d, x, core] = added(mine[d, x, core], ring[d])

    def x_add(d, unused):
        x_copy(d).wait()
        mine[d, x, core] = added(mine[d, x, core], x_in[d])

        @pl.when((z == 0) & (d > 0))
        def _():
            flow(1, d).start()

        @pl.when((z == lines - 1) & (d < lines - 1))
        def _():
            flow(-1, d).start()

        return unused

    lax.fori_loop(0, lines, x_add, 0)
    small_copy.wait()
    row = lax.broadcasted_iota(jnp.int32, small_own.shape, 0)
    small_x[0] = small_own[...] + jnp.where(row < 2, small_y[...], 0.0)
    small_core_copy = send(
        small_x.at[0], small_core, core_sem.at[0, 1], core_sem.at[1, 1], spot.core_mate()
    )
    small_core_copy.start()

    def relay(k, unused):
        high = lines - 1 - k

        @pl.when((z < high) & (z > 0))
        def _():
            merge(1, high)
            flow(1, high).start()

        @pl.when((z > k) & (z + 1 < lines))
        def _():
            merge(-1, k)
            flow(-1, k).start()

        return unused

    lax.fori_loop(0, lines - 1, relay, 0)
    small_core_copy.wait()
    small_x[1] = small_x[0] + small_core[...]
    small_x_copy = send(
        small_x.at[1], small_x.at[2], x_sem.at[0, lines], x_sem.at[1, lines], spot.x_mate()
    )
    small_x_copy.start()

    @pl.when(z > 0)
    def _():
        merge(1, z)

    @pl.when(z + 1 < lines)
    def _():
        merge(-1, z)

    all_w[z, x, core] = mine[z, x, core]

    def pass_w(step, d):
        i = 0 if step > 0 else 1
        return send(
            all_w.at[d, x, core], all_w.at[d, x, core], gz_sem.at[i, d], gz_sem.at[2 + i, d],
            spot.z_mate(step),
        )

    def pass_s(step, d):
        i = 0 if step > 0 else 1
        return send(
            small_all.at[d], small_all.at[d], sz_sem.at[i, d], sz_sem.at[2 + i, d],
            spot.z_mate(step),
        )

    def across(d):
        return send(
            all_w.at[d, x, core], all_w.at[d, x, core], gx_sem.at[0, d], gx_sem.at[1, d],
            spot.x_mate(),
        )

    def beside(d):
        return send(
            all_w.at[d, :, core], all_w.at[d, :, core], gc_sem.at[0, d], gc_sem.at[1, d],
            spot.core_mate(),
        )

    small_x_copy.wait()
    small_all[z] = small_x[1] + small_x[2]

    def receive(step, d):
        pass_w(step, d).wait_recv()
        across(d).start()

    across(z).start()
    lax.fori_loop(
        0, lines, line_relay(spot, lambda s, d: pass_w(s, d).start(), receive), 0
    )
    lax.fori_loop(
        0,
        lines,
        line_relay(
            spot, lambda s, d: pass_s(s, d).start(), lambda s, d: pass_s(s, d).wait_recv()
        ),
        0,
    )

    def add_small(d, total):
        return total + small_all[d]

    total_ref[...] = lax.fori_loop(1, lines, add_small, small_all[0])
    ffn_copy.wait()

    def last(j, unused):
        at = pl.ds(pl.multiple_of(j * step, step), step)
        here = pl.ds(pl.multiple_of(wa * half + j * step, step), step)
        total = hidden_ref[at, :] + ffn_ref[here, :].astype(f32) + ffn_in[at, :].astype(f32)
        out_ref[at, :] = total.astype(bf16)
        return unused

    lax.fori_loop(0, half // step, last, 0)

    def spread(d, unused):
        across(d).wait()
        beside(d).start()
        return unused

    lax.fori_loop(0, lines, spread, 0)

    def copy_out(d, unused):
        beside(d).wait()
        weights_ref[d] = all_w[d]
        return unused

    lax.fori_loop(0, lines, copy_out, 0)

    def drain(d, unused):
        @pl.when((z < d))
        def _():
            flow(1, d).wait_send()

        @pl.when((z > d))
        def _():
            flow(-1, d).wait_send()

        @pl.when((d <= z) & (z + 1 < lines))
        def _():
            pass_w(1, d).wait_send()
            pass_s(1, d).wait_send()

        @pl.when((d >= z) & (z > 0))
        def _():
            pass_w(-1, d).wait_send()
            pass_s(-1, d).wait_send()

        return unused

    lax.fori_loop(0, lines, drain, 0)


def finish(plan, cycle_size, *operands):
    lines = cycle_size // 4
    half, model = operands[9].shape
    rows = 4 * plan.cols // cycle_size
    dma = pltpu.SemaphoreType.DMA
    return pl.pallas_call(
        functools.partial(finish_kernel, plan, lines),
        out_shape=[
            jax.ShapeDtypeStruct((half, model), bf16),
            jax.ShapeDtypeStruct((half, model), f32),
            jax.ShapeDtypeStruct((8, half), f32),
            jax.ShapeDtypeStruct((lines, 2, 2, rows, model), bf16),
            jax.ShapeDtypeStruct((8, model), f32),
        ],
        in_specs=[vmem] * len(operands),
        out_specs=[vmem] * 5,
        scratch_shapes=[
            pltpu.VMEM((lines, 2, 2, rows, model), bf16),
            pltpu.VMEM((lines, 2, rows, model), bf16),
            pltpu.VMEM((lines, rows, model), bf16),
            pltpu.VMEM((lines, rows, model), bf16),
            pltpu.VMEM((lines, rows, model), bf16),
            pltpu.VMEM((lines, 2, 2, rows, model), bf16),
            pltpu.VMEM((2, half // 2, model), bf16),
            pltpu.VMEM((2, half // 2, model), bf16),
            pltpu.VMEM((half, model), f32),
            pltpu.VMEM((half, model), bf16),
            pltpu.VMEM((8, half), f32),
            pltpu.VMEM((8, model), f32),
            pltpu.VMEM((8, model), f32),
            pltpu.VMEM((8, model), f32),
            pltpu.VMEM((3, 8, model), f32),
            pltpu.VMEM((lines, 8, model), f32),
            dma((2, 5)),
            dma((2, 2)),
            dma((2, lines + 1)),
            dma((2, lines)),
            dma((2, lines)),
            dma((4, lines)),
            dma((2, lines)),
            dma((2, lines)),
            dma((4, lines)),
        ],
        compiler_params=pltpu.CompilerParams(
            vmem_limit_bytes=58 * 2**20, collective_id=2, has_side_effects=True
        ),
        name="finish",
    )(*operands)


root = 0.7978845608028654
cubic = 0.044715


def middle_kernel(
    plan, cycle_size, att_ref, mixed_ref, tokens_ref, cot_ref, gain_ref,
    wo_hbm, wo_far_hbm, wg_hbm, wu_hbm, wd_hbm,
    hidden_ref, gh_ref, branch_ref, ffn_ref, do_ref, gain_part_ref, *refs,
):
    stacks, refs = (refs[:3], refs[3:])
    (
        wg, wu, wd, wo, inner, gg, gu, x_ref, att_in, d_out, d_in, e_out, e_in,
        acc_f, acc_g, rows_buf, load_sem, y_sem, out_sem,
    ) = refs
    spot = Spot(cycle_size // 4)
    wa = spot.wa
    pair, model = tokens_ref.shape
    half = pair // 2
    units = wd.shape[1]
    chunk = half // 4
    block = pair // 4
    loads = [
        pltpu.make_async_copy(src, dst, load_sem.at[i])
        for i, (src, dst) in enumerate(
            (
                (wo_hbm, wo.at[0, 64:]),
                (wo_far_hbm, wo.at[1, 64:]),
                (wg_hbm, wg),
                (wu_hbm, wu),
                (wd_hbm, wd),
            )
        )
    ]
    for load in loads:
        load.start()
    barrier = pltpu.get_barrier_semaphore()
    pl.semaphore_signal(
        barrier, inc=1, device_id=spot.y_mate(), device_id_type=pl.DeviceIdType.MESH
    )
    wo[:, :64, :] = jnp.zeros((2, 64, model), bf16)
    pl.semaphore_wait(barrier, 1)
    ours = wa * half
    theirs = (1 - wa) * half

    def rows_at(start, size):
        return pl.ds(pl.multiple_of(start, size), size)

    def a_start(i):
        return (theirs + i * block) if i < 2 else (ours + (i - 2) * block)

    def a_copy(i, base):
        at = rows_at(base + (i % 2) * block, block)
        return send(att_ref.at[at], att_in.at[at], y_sem.at[0, i], y_sem.at[1, i], spot.y_mate())

    order = (0, 1, 2, 3)
    for i in order:
        a_copy(i, ours if i < 2 else theirs).start()
    loads[0].wait()
    loads[1].wait()

    def normal(i, base, keep):
        a_copy(i, base).wait_recv()
        at = rows_at(base + (i % 2) * block, block)
        branch = nn(att_ref[at, :], wo[0]) + nn(att_in[at, :], wo[1])
        hidden = tokens_ref[at, :].astype(f32) + branch
        if keep:
            hidden_ref[(i % 2) * block : (i % 2 + 1) * block, :] = hidden
        inv = lax.rsqrt(jnp.mean(hidden * hidden, axis=-1, keepdims=True) + eps)
        x_ref[at, :] = (hidden * inv * gain_ref[...]).astype(bf16)

    normal(0, theirs, False)
    normal(1, theirs, False)
    for load in loads[2:]:
        load.wait()
    wide = 256

    def feed(base):
        rows = rows_at(base, half)
        acc_f[...] = jnp.zeros_like(acc_f)
        acc_g[...] = jnp.zeros_like(acc_g)

        def tile(u, unused):
            cols = rows_at(u * wide, wide)
            gate = nn(x_ref[rows, :], wg[:, cols])
            upward = nn(x_ref[rows, :], wu[:, cols])
            grad_inner = nn(cot_ref[rows, :], wd[:, cols])
            square = gate * gate
            bend = jnp.tanh(root * gate * (1.0 + cubic * square))
            side = 0.5 * (1.0 + bend)
            gelu = gate * side
            slope = side + 0.5 * gate * (1.0 - bend * bend) * (
                root * (1.0 + 3.0 * cubic * square)
            )
            inner_low = (gelu * upward).astype(bf16)
            gate_low = (grad_inner * upward * slope).astype(bf16)
            up_low = (grad_inner * gelu).astype(bf16)
            inner[rows, cols] = inner_low
            gg[rows, cols] = gate_low
            gu[rows, cols] = up_low
            acc_g[...] += nt(gate_low, wg[:, cols]) + nt(up_low, wu[:, cols])
            acc_f[...] += nt(inner_low, wd[:, cols])
            return unused

        lax.fori_loop(0, units // wide, tile, 0)
        ffn_ref[rows, :] = acc_f[...].astype(bf16)

    def d_copy(i):
        return send(
            d_out.at[i], d_in.at[i], y_sem.at[0, 4 + i], y_sem.at[1, 4 + i], spot.y_mate()
        )

    def send_grad(i, unused):
        d_out[i] = acc_g[rows_at(i * chunk, chunk), :].astype(bf16)
        d_copy(i).start()
        return unused

    def half_pass(k, unused):
        base = theirs + k * (ours - theirs)
        feed(base)

        @pl.when(k == 0)
        def _():
            lax.fori_loop(0, 4, send_grad, 0)
            normal(2, ours, True)
            normal(3, ours, True)

        return unused

    lax.fori_loop(0, 2, half_pass, 0)
    parts = 2
    span = units // parts
    slices = cycle_size // parts
    size = units // cycle_size

    def out_copy(n):
        m, p = (n // parts, n % parts)
        return pltpu.make_async_copy(
            rows_buf.at[n % 2], stacks[m].at[pl.ds(p * slices, slices)], out_sem.at[n]
        )

    for n in range(3 * parts):
        m, p = (n // parts, n % parts)
        left = (inner, gg, gu)[m]
        right = (cot_ref, x_ref, x_ref)[m]
        if n >= 2:
            out_copy(n - 2).wait()
        turned = jnp.transpose(left[:, p * span : (p + 1) * span])
        for c in range(0, model, wide):
            end = min(model, c + wide)
            product = nn(turned, right[:, c:end]).astype(bf16)
            for s in range(slices):
                rows_buf[n % 2, s, :, c:end] = product[s * size : (s + 1) * size]
        out_copy(n).start()

    def e_copy(i):
        return send(
            e_out.at[i], e_in.at[i], y_sem.at[0, 8 + i], y_sem.at[1, 8 + i], spot.y_mate()
        )

    def normal_back(i, total):
        d_copy(i).wait()
        at = rows_at(i * chunk, chunk)
        grad = acc_g[at, :] + d_in[i].astype(f32)
        hidden = hidden_ref[at, :]
        inv = lax.rsqrt(jnp.mean(hidden * hidden, axis=-1, keepdims=True) + eps)
        scaled = gain_ref[...] * grad
        mean = jnp.mean(hidden * scaled, axis=-1, keepdims=True)
        grad_hidden = (
            cot_ref[rows_at(ours + i * chunk, chunk), :].astype(f32)
            + inv * scaled
            - hidden * (inv * inv * inv * mean)
        )
        gh_ref[at, :] = grad_hidden
        low = grad_hidden.astype(bf16)
        branch_ref[at, :] = low
        e_out[i] = nt(low, wo[1]).astype(bf16)
        e_copy(i).start()
        do_ref[rows_at(ours + i * chunk, chunk), :] = nt(low, wo[0]).astype(bf16)
        return total + jnp.sum(grad * hidden * inv, axis=0, keepdims=True)

    gain_part_ref[...] = lax.fori_loop(0, 4, normal_back, jnp.zeros((1, model), f32))

    def row_terms(at, grad):
        lane = lanes_of(chunk)
        terms = grad.astype(f32) * mixed_ref[at, :]
        out = grad
        for h in range(plan.heads):
            row_term = jnp.sum(
                jnp.where(lane // 64 == h + 1, terms, 0.0), axis=1, keepdims=True
            )
            for i, part in enumerate(split3(-row_term)):
                out = jnp.where(lane == 3 * h + i, part, out)
        do_ref[at, :] = out

    def own_terms(i, unused):
        at = rows_at(ours + i * chunk, chunk)
        row_terms(at, do_ref[at, :])
        return unused

    lax.fori_loop(0, 4, own_terms, 0)

    def far_terms(i, unused):
        e_copy(i).wait()
        row_terms(rows_at(theirs + i * chunk, chunk), e_in[i])
        return unused

    lax.fori_loop(0, 4, far_terms, 0)
    for n in (3 * parts - 2, 3 * parts - 1):
        out_copy(n).wait()
    for i in order:
        a_copy(i, ours if i < 2 else theirs).wait_send()


def middle(
    plan, cycle_size, attended, mixed, tokens, cot, gain, w_out, w_out_far, w_gate, w_up, w_down
):
    pair, model = tokens.shape
    half = pair // 2
    units = w_down.shape[0]
    size = units // cycle_size
    chunk = half // 4
    hbm = pl.BlockSpec(memory_space=pl.ANY)
    dma = pltpu.SemaphoreType.DMA
    return pl.pallas_call(
        functools.partial(middle_kernel, plan, cycle_size),
        out_shape=[
            jax.ShapeDtypeStruct((half, model), f32),
            jax.ShapeDtypeStruct((half, model), f32),
            jax.ShapeDtypeStruct((half, model), bf16),
            jax.ShapeDtypeStruct((pair, model), bf16),
            jax.ShapeDtypeStruct((pair, WIDE), bf16),
            jax.ShapeDtypeStruct((1, model), f32),
        ]
        + [jax.ShapeDtypeStruct((cycle_size, size, model), bf16)] * 3,
        in_specs=[vmem] * 5 + [hbm] * 5,
        out_specs=[vmem] * 6 + [hbm] * 3,
        scratch_shapes=[
            pltpu.VMEM((model, units), bf16),
            pltpu.VMEM((model, units), bf16),
            pltpu.VMEM((model, units), bf16),
            pltpu.VMEM((2, WIDE, model), bf16),
            pltpu.VMEM((pair, units), bf16),
            pltpu.VMEM((pair, units), bf16),
            pltpu.VMEM((pair, units), bf16),
            pltpu.VMEM((pair, model), bf16),
            pltpu.VMEM((pair, WIDE), bf16),
            pltpu.VMEM((4, chunk, model), bf16),
            pltpu.VMEM((4, chunk, model), bf16),
            pltpu.VMEM((4, chunk, WIDE), bf16),
            pltpu.VMEM((4, chunk, WIDE), bf16),
            pltpu.VMEM((half, model), f32),
            pltpu.VMEM((half, model), f32),
            pltpu.VMEM((2, cycle_size // 2, size, model), bf16),
            dma((5,)),
            dma((2, 12)),
            dma((6,)),
        ],
        compiler_params=pltpu.CompilerParams(
            vmem_limit_bytes=60 * 2**20, collective_id=3, has_side_effects=True
        ),
        name="feed_forward",
    )(attended, mixed, tokens, cot, gain, w_out, w_out_far, w_gate, w_up, w_down.T)


def shards(
    tokens,
    doc_lengths,
    key_mask,
    gain_attn,
    w_query,
    w_key,
    w_value,
    w_out,
    bias_table,
    gain_ffn,
    w_gate,
    w_up,
    w_down,
    cotangent,
):
    own_rows, model = tokens.shape
    group = lax.axis_size("wa")
    cycle_size = lax.axis_size("ctx")
    pair = own_rows * group
    heads = bias_table.shape[1]
    docs = doc_lengths.shape[0]
    plan = Plan(heads, w_query.shape[1] // heads, docs)
    total_rows = pair * cycle_size
    doc_most = min(MAXLEN, total_rows // 2)
    reach = min(cycle_size - 1, (doc_most - 1) // pair + 1)
    base = lax.axis_index("ctx") * pair
    rows = min(total_rows, (2 * reach + 1) * pair)
    origin = jnp.clip(base - reach * pair, 0, total_rows - rows).astype(jnp.int32)
    ends = jnp.cumsum(doc_lengths).astype(jnp.int32)
    starts = ends - doc_lengths

    def doc_at(positions):
        return jnp.sum((positions[:, None] >= starts[None, :]).astype(jnp.int32), axis=1) - 1

    tiles = pair // TQ
    tile_start = base + TQ * jnp.arange(tiles, dtype=jnp.int32)
    first_doc = jnp.arange(docs, dtype=jnp.int32)[None, :] == doc_at(tile_start)[:, None]
    last_doc = jnp.arange(docs, dtype=jnp.int32)[None, :] == doc_at(tile_start + TQ - 1)[:, None]
    low_end = jnp.sum(jnp.where(first_doc, starts[None, :], 0), axis=1)
    high_end = jnp.sum(jnp.where(last_doc, ends[None, :], 0), axis=1)
    n_left = jnp.maximum(0, (tile_start - EDGE - low_end + TK - 1) // TK)
    n_right = jnp.maximum(0, (high_end - (tile_start - EDGE + TK) + TK - 1) // TK)
    bounds = jnp.concatenate(
        [(base - origin)[None], jnp.stack([n_left, n_right], axis=1).reshape(-1)]
    ).astype(jnp.int32)

    mask_all = lax.all_gather(key_mask, "ctx", axis=0, tiled=True)
    pair_cot = lax.all_gather(cotangent, "wa", axis=0, tiled=True)

    def window(gathered):
        if rows == total_rows:
            return gathered
        return lax.dynamic_slice_in_dim(gathered, origin, rows, 0)

    gather = functools.partial(lax.all_gather, axis_name="ctx", axis=0, tiled=True)
    positions = origin + jnp.arange(rows, dtype=jnp.int32)
    doc_of = doc_at(positions)
    lane = jnp.arange(128, dtype=jnp.int32)[None, :] + 128
    code = lane - plan.doc_lane
    bit_differs = ((doc_of[:, None] >> (code >> 1)) & 1) != (code & 1)
    k_aug = jnp.where(
        lane == plan.mask_lane,
        window(mask_all).astype(f32)[:, None],
        jnp.where(
            lane < plan.stat_lane,
            jnp.where(bit_differs & (code >= 0), neg_big, 0.0),
            (lane < plan.stat_lane + 3 * heads).astype(f32),
        ),
    ).astype(bf16)
    own_docs = doc_at(base + jnp.arange(pair, dtype=jnp.int32))
    own_differs = ((own_docs[:, None] >> (code >> 1)) & 1) != (code & 1)
    q_aug = jnp.where(
        lane == plan.mask_lane, 1.0, ((lane < plan.stat_lane) & ~own_differs).astype(f32)
    ).astype(bf16)
    q_aug = jnp.concatenate([jnp.zeros((pair, 128), bf16), q_aug], axis=1)
    pair_normed, pair_tokens, q_wide, own_kv, kv_all = first(
        plan, cycle_size, reach, tokens, gain_attn[None], q_aug, w_query, w_key, w_value
    )
    kv_all = window(kv_all.reshape(total_rows, 2 * plan.cols))
    near_bias = pl.pallas_call(
        functools.partial(near_kernel, heads),
        out_shape=jax.ShapeDtypeStruct((2, heads, TQ, TK), f32),
        in_specs=[smem],
        out_specs=vmem,
        compiler_params=params(),
        name="near_bias",
    )(bias_table)

    padded = rows + 2 * PAD
    attended, mixed, q_back = pl.pallas_call(
        functools.partial(fwd_kernel, plan, rows, pair),
        out_shape=(
            jax.ShapeDtypeStruct((pair, WIDE), bf16),
            jax.ShapeDtypeStruct((pair, WIDE), f32),
            jax.ShapeDtypeStruct((pair, WIDE), bf16),
        ),
        in_specs=[smem, smem, vmem, vmem, vmem, vmem],
        out_specs=(vmem, vmem, vmem),
        scratch_shapes=[
            pltpu.VMEM((padded, WIDE), bf16),
            pltpu.VMEM((padded, WIDE), bf16),
            pltpu.VMEM((heads, TQ, WIDE), f32),
            pltpu.VMEM((heads, TQ, 128), f32),
            pltpu.VMEM((heads, TQ, WIDE), bf16),
        ],
        compiler_params=params(),
        name="attention_forward",
    )(bounds, bias_table, kv_all, k_aug, q_wide, near_bias)
    q_all = window(gather(q_back))
    swap = functools.partial(lax.ppermute, axis_name="wa", perm=((0, 1), (1, 0)))
    hidden, grad_hidden, branch, ffn_part, do_wide, gain_ffn_part, *stacks = middle(
        plan,
        cycle_size,
        attended,
        mixed,
        pair_tokens,
        pair_cot,
        gain_ffn[None],
        w_out,
        swap(w_out),
        w_gate,
        w_up,
        w_down,
    )
    far_branch = swap(branch)
    do_all = window(gather(do_wide))
    grad_w_down, grad_w_gate = reduce_scatter(stacks[:2], cycle_size)
    grad_w_up = lax.psum_scatter(
        stacks[2].reshape(-1, model), "ctx", scatter_dimension=0, tiled=True
    ).astype(f32)
    grad_w_gate, grad_w_up = (grad_w_gate.T, grad_w_up.T)

    grad_queries, table_part = pl.pallas_call(
        functools.partial(dq_kernel, plan, rows, pair),
        out_shape=(
            jax.ShapeDtypeStruct((pair, WIDE), bf16),
            jax.ShapeDtypeStruct((heads, 32, 128), f32),
        ),
        in_specs=[smem, smem, vmem, vmem, vmem, vmem, vmem],
        out_specs=(vmem, vmem),
        scratch_shapes=[
            pltpu.VMEM((padded, WIDE), bf16),
            pltpu.VMEM((padded, WIDE), bf16),
            pltpu.VMEM((heads, TQ, WIDE), f32),
            pltpu.VMEM((heads, TQ, WIDE), bf16),
            pltpu.VMEM((heads, TQ, WIDE), bf16),
            pltpu.VMEM((heads, TQ, TK), f32),
            pltpu.VMEM((2, heads, TQ, 128), f32),
        ],
        compiler_params=params(),
        name="attention_grad_queries",
    )(bounds, bias_table, kv_all, k_aug, q_back, do_wide, near_bias)
    own_aug = lax.dynamic_slice_in_dim(k_aug, base - origin, pair, 0)
    grad_keys, grad_values, mask_part = pl.pallas_call(
        functools.partial(dkv_kernel, plan, rows, pair),
        out_shape=(
            jax.ShapeDtypeStruct((pair, WIDE), bf16),
            jax.ShapeDtypeStruct((pair, WIDE), bf16),
            jax.ShapeDtypeStruct((tiles, 8, TQ), f32),
        ),
        in_specs=[smem, smem, vmem, vmem, vmem, vmem, vmem],
        out_specs=(vmem, vmem, vmem),
        scratch_shapes=[
            pltpu.VMEM((padded, WIDE), bf16),
            pltpu.VMEM((padded, WIDE), bf16),
            pltpu.VMEM((heads, TQ, WIDE), bf16),
            pltpu.VMEM((heads, TQ, WIDE), bf16),
            pltpu.VMEM((heads, TQ, WIDE), f32),
            pltpu.VMEM((heads, TQ, WIDE), f32),
        ],
        compiler_params=params(),
        name="attention_grad_keys",
    )(bounds, bias_table, q_all, do_all, own_kv, own_aug, near_bias)
    cols = plan.cols
    gap = jnp.zeros((model, WIDE - cols), bf16)
    w_wide = jnp.concatenate([w_query, gap, w_key, gap, gap, w_value], axis=1)
    table_row = jnp.sum(table_part, axis=2).reshape(1, -1)
    table_row = jnp.pad(table_row, ((0, 0), (0, model - table_row.shape[1])))
    small = jnp.concatenate(
        [jnp.zeros((1, model), f32), gain_ffn_part, table_row, jnp.zeros((5, model), f32)],
        axis=0,
    )
    layer_out, grad_tokens, grad_mask, weights, totals = finish(
        plan,
        cycle_size,
        grad_queries,
        grad_keys,
        grad_values,
        mask_part.reshape(group, 8, own_rows),
        w_wide,
        pair_normed,
        attended,
        branch,
        far_branch,
        tokens,
        gain_attn[None],
        hidden,
        grad_hidden,
        ffn_part,
        small,
    )
    weights = weights.reshape(4, cols, model).astype(f32)
    return (
        layer_out,
        grad_tokens,
        grad_mask[0],
        totals[0],
        weights[0].T,
        weights[1].T,
        weights[2].T,
        weights[3],
        totals[2, : heads * 32].reshape(heads, 32).T,
        totals[1],
        grad_w_gate,
        grad_w_up,
        grad_w_down,
    )


def solution(mesh):
    placed = (
        P(("ctx", "wa"), None),
        P(),
        P("ctx"),
        P(),
        P(None, "wa"),
        P(None, "wa"),
        P(None, "wa"),
        P("wa", None),
        P(None, "wa"),
        P(),
        P(None, "wa"),
        P(None, "wa"),
        P("wa", None),
        P(("ctx", "wa"), None),
    )
    return jax.shard_map(
        shards,
        mesh=mesh,
        in_specs=placed,
        out_specs=(
            P(("ctx", "wa"), None),
            P(("ctx", "wa"), None),
            P(("ctx", "wa")),
            P(),
            P(None, "wa"),
            P(None, "wa"),
            P(None, "wa"),
            P("wa", None),
            P(None, "wa"),
            P(),
            P(None, ("wa", "ctx")),
            P(None, ("wa", "ctx")),
            P(("wa", "ctx"), None),
        ),
        check_vma=False,
    )
```

```python
import functools

import jax
import jax.numpy as jnp
from jax import lax
from jax.experimental import pallas as pl
from jax.experimental.pallas import tpu as pltpu
from jax.sharding import PartitionSpec as P

MAXLEN = 8192

bucket_edges = (12, 16, 23, 32, 46, 64, 91)
neg_big = -1e30
eps = 1e-06
far_left_bucket = 15
far_right_bucket = 31
WIDE = 256
TQ = 256
TK = 512
EDGE = 128
PAD = TK + EDGE
f32 = jnp.float32
bf16 = jnp.bfloat16


def bucket_of(relative):
    distance = jnp.abs(relative)
    bucket = jnp.minimum(distance, 8) + 16 * (relative > 0).astype(jnp.int32)
    for edge in bucket_edges:
        bucket = bucket + (distance >= edge).astype(jnp.int32)
    return bucket


def norm_forward(inputs, gain):
    inv_root = lax.rsqrt(jnp.mean(inputs * inputs, axis=-1, keepdims=True) + eps)
    return (inputs * inv_root * gain, inv_root)


def norm_backward(inputs, inv_root, gain, grad_normed):
    scaled = gain * grad_normed
    cubed = inv_root * inv_root * inv_root
    grad_inputs = inv_root * scaled - inputs * cubed * jnp.mean(
        inputs * scaled, axis=-1, keepdims=True
    )
    grad_gain = jnp.sum(grad_normed * inputs * inv_root, axis=0)
    return (grad_inputs, grad_gain)


def gated(gate, upward):
    return jax.nn.gelu(gate, approximate=True) * upward


def nt(a, b):
    return lax.dot_general(a, b, (((1,), (1,)), ((), ())), preferred_element_type=f32)


def nn(a, b):
    return lax.dot_general(a, b, (((1,), (0,)), ((), ())), preferred_element_type=f32)


def split3(x):
    hi = x.astype(bf16)
    rest = x - hi.astype(f32)
    mid = rest.astype(bf16)
    return (hi, mid, (rest - mid.astype(f32)).astype(bf16))


class Plan:
    def __init__(self, heads, width, docs):
        self.heads = heads
        self.width = width
        self.bits = max(1, (docs - 1).bit_length())
        self.cols = heads * width
        self.mask_lane = self.cols
        self.doc_lane = self.cols + 1
        self.stat_lane = self.doc_lane + 2 * self.bits
        assert self.stat_lane + 3 * heads <= WIDE and self.cols + 64 == WIDE and width == 64

    def key_lanes(self, lane, h):
        own = (lane >= h * self.width) & (lane < (h + 1) * self.width)
        aug = (lane >= self.mask_lane) & (lane < self.stat_lane)
        stat = (lane >= self.stat_lane + 3 * h) & (lane < self.stat_lane + 3 * h + 3)
        return own | aug | stat

    def value_lanes(self, lane, h):
        own = (lane >= 64 + h * self.width) & (lane < 64 + (h + 1) * self.width)
        return own | ((lane >= 3 * h) & (lane < 3 * h + 3))


def lanes_of(rows, width=WIDE):
    return lax.broadcasted_iota(jnp.int32, (rows, width), 1)


def near_lanes(heads, table_ref, near_ref):
    row = lax.broadcasted_iota(jnp.int32, (EDGE, 3 * EDGE), 0)
    col = lax.broadcasted_iota(jnp.int32, (EDGE, 3 * EDGE), 1)
    relative = col - EDGE - row
    for flip in range(2):
        bucket = bucket_of(-relative if flip else relative)
        left, right = (far_left_bucket, far_right_bucket)
        if flip:
            left, right = (right, left)
        for h in range(heads):
            base = jnp.full((EDGE, 3 * EDGE), table_ref[0, h], f32)
            for b in range(1, 32):
                base = jnp.where(bucket == b, table_ref[b, h], base)
            far_l = jnp.full((EDGE, EDGE), table_ref[left, h], f32)
            far_r = jnp.full((EDGE, EDGE), table_ref[right, h], f32)
            near_ref[flip, h, :EDGE, : 3 * EDGE] = base
            near_ref[flip, h, :EDGE, 3 * EDGE :] = far_r
            near_ref[flip, h, EDGE:, EDGE:] = base
            near_ref[flip, h, EDGE:, :EDGE] = far_l


def build_keys(plan, g_ref, kaug_ref, masks_ref, km, vm, mask_row, rows):
    mask_row[...] = jnp.zeros_like(mask_row)
    size = masks_ref.shape[2]
    for n in range(masks_ref.shape[0]):
        mask_row[:, PAD + n * size : PAD + (n + 1) * size] = masks_ref[n]
    km[:PAD, :] = jnp.broadcast_to(
        jnp.where(pad_lanes(plan), neg_big, 0.0).astype(bf16), (PAD, WIDE)
    )
    km[pl.ds(PAD + rows, PAD), :] = km[:PAD, :]
    vm[:PAD, :] = jnp.zeros((PAD, WIDE), bf16)
    vm[pl.ds(PAD + rows, PAD), :] = jnp.zeros((PAD, WIDE), bf16)
    step = 512
    low = lanes_of(step, 128) < 64
    ones = (lanes_of(step, 128) < 3 * plan.heads).astype(bf16)

    def body(n, unused):
        at = pl.multiple_of(n * step, step)
        to = pl.multiple_of(PAD + n * step, 128)
        middle = g_ref[pl.ds(at, step), 128:256]
        km[pl.ds(to, step), 0:128] = g_ref[pl.ds(at, step), 0:128]
        km[pl.ds(to, step), 128:256] = jnp.where(low, middle, kaug_ref[pl.ds(at, step), :])
        vm[pl.ds(to, step), 0:128] = jnp.where(low, ones, middle)
        vm[pl.ds(to, step), 128:256] = g_ref[pl.ds(at, step), 256:384]
        return unused

    lax.fori_loop(0, rows // step, body, 0)


def pad_lanes(plan):
    lane = lanes_of(1)
    return (lane >= plan.doc_lane) & (lane < plan.stat_lane)


def fwd_kernel(
    plan, rows, pair, bounds, table_ref, g_ref, kaug_ref, masks_ref, q_ref, near_ref,
    low_ref, wide_ref, qb_ref, km, vm, mask_row, acc, row_max, qh_ref,
):
    build_keys(plan, g_ref, kaug_ref, masks_ref, km, vm, mask_row, rows)
    lane = lanes_of(TQ)

    def tile(t, unused):
        start = pl.multiple_of(bounds[0] + t * TQ, 128)
        n_left, n_right = (bounds[1 + 2 * t], bounds[2 + 2 * t])
        out = pl.ds(pl.multiple_of(t * TQ, TQ), TQ)
        q = q_ref[out, :]
        near = pl.ds(pl.multiple_of(start + PAD - EDGE, 128), TK)
        for h in range(plan.heads):
            qh = jnp.where(plan.key_lanes(lane, h), q, jnp.zeros_like(q))
            qh_ref[h] = qh
            s = nt(qh, km[near, :]) + near_ref[0, h] + mask_row[0:1, near]
            top = jnp.max(s, axis=1, keepdims=True)
            p = jnp.exp(s - top).astype(bf16)
            acc[h] = nn(p, vm[near, :])
            row_max[h] = jnp.broadcast_to(top, (TQ, 128))

        def far(bucket):
            def step(first, n):
                span = pl.ds(pl.multiple_of(first + n, 128), TK)
                for h in range(plan.heads):
                    s = nt(qh_ref[h], km[span, :]) + mask_row[0:1, span]
                    offset = table_ref[bucket, h]
                    old = row_max[h][:, :1]
                    top = jnp.maximum(old, jnp.max(s, axis=1, keepdims=True) + offset)
                    p = jnp.exp(s - (top - offset)).astype(bf16)
                    acc[h] = acc[h] * jnp.exp(old - top) + nn(p, vm[span, :])
                    row_max[h] = jnp.broadcast_to(top, (TQ, 128))
            return step

        left, right = (far(far_left_bucket), far(far_right_bucket))

        @pl.loop(0, n_left)
        def _(n):
            left(start + PAD - EDGE - TK, -n * TK)

        @pl.loop(0, n_right)
        def _(n):
            right(start + PAD - EDGE + TK, n * TK)

        wide = jnp.zeros((TQ, WIDE), f32)
        qb = jnp.where(lane < plan.stat_lane, q, jnp.zeros_like(q))
        for h in range(plan.heads):
            total = acc[h][:, 3 * h : 3 * h + 1]
            log_total = row_max[h][:, :1] + jnp.log(total)
            wide = jnp.where(lane // 64 == h + 1, acc[h] / total, wide)
            for i, part in enumerate(split3(-log_total)):
                qb = jnp.where(lane == plan.stat_lane + 3 * h + i, part, qb)
        wide_ref[out, :] = wide
        low_ref[out, :] = wide.astype(bf16)
        qb_ref[out, :] = qb
        return unused

    lax.fori_loop(0, pair // TQ, tile, 0)


def dq_kernel(
    plan, rows, pair, bounds, table_ref, g_ref, kaug_ref, masks_ref, qb_ref, do_ref, near_ref,
    dq_ref, tab_ref, km, vm, mask_row, acc, qh_ref, doh_ref, near_acc, far_acc,
):
    build_keys(plan, g_ref, kaug_ref, masks_ref, km, vm, mask_row, rows)
    lane = lanes_of(TQ)
    near_acc[...] = jnp.zeros_like(near_acc)
    far_acc[...] = jnp.zeros_like(far_acc)

    def tile(t, unused):
        start = pl.multiple_of(bounds[0] + t * TQ, 128)
        n_left, n_right = (bounds[1 + 2 * t], bounds[2 + 2 * t])
        out = pl.ds(pl.multiple_of(t * TQ, TQ), TQ)
        q = qb_ref[out, :]
        do = do_ref[out, :]
        near = pl.ds(pl.multiple_of(start + PAD - EDGE, 128), TK)

        def grads(h, s, span):
            p = jnp.exp(s)
            return p * nt(doh_ref[h], vm[span, :])

        for h in range(plan.heads):
            qh_ref[h] = jnp.where(plan.key_lanes(lane, h), q, jnp.zeros_like(q))
            doh_ref[h] = jnp.where(plan.value_lanes(lane, h), do, jnp.zeros_like(do))
            ds = grads(
                h, nt(qh_ref[h], km[near, :]) + near_ref[0, h] + mask_row[0:1, near], near
            )
            near_acc[h] += ds
            acc[h] = nn(ds.astype(bf16), km[near, :])

        def far(bucket, slot):
            def step(first, n):
                span = pl.ds(pl.multiple_of(first + n, 128), TK)
                for h in range(plan.heads):
                    offset = mask_row[0:1, span] + table_ref[bucket, h]
                    ds = grads(h, nt(qh_ref[h], km[span, :]) + offset, span)
                    acc[h] += nn(ds.astype(bf16), km[span, :])
                    far_acc[slot, h] += (
                        ds[:, 0:128] + ds[:, 128:256] + ds[:, 256:384] + ds[:, 384:512]
                    )
            return step

        left, right = (far(far_left_bucket, 0), far(far_right_bucket, 1))

        @pl.loop(0, n_left)
        def _(n):
            left(start + PAD - EDGE - TK, -n * TK)

        @pl.loop(0, n_right)
        def _(n):
            right(start + PAD - EDGE + TK, n * TK)

        total = jnp.zeros((TQ, WIDE), f32)
        for h in range(plan.heads):
            total = jnp.where(lane // 64 == h, acc[h], total)
        dq_ref[out, :] = total.astype(bf16)
        return unused

    lax.fori_loop(0, pair // TQ, tile, 0)
    row = lax.broadcasted_iota(jnp.int32, (EDGE, 3 * EDGE), 0)
    col = lax.broadcasted_iota(jnp.int32, (EDGE, 3 * EDGE), 1)
    bucket = bucket_of(col - EDGE - row)
    for h in range(plan.heads):
        band = near_acc[h, :EDGE, : 3 * EDGE] + near_acc[h, EDGE:, EDGE:]
        extra_right = near_acc[h, :EDGE, 3 * EDGE :]
        extra_left = near_acc[h, EDGE:, :EDGE]
        for b in range(32):
            part = jnp.sum(jnp.where(bucket == b, band, 0.0), axis=0, keepdims=True)
            part = part[:, :128] + part[:, 128:256] + part[:, 256:]
            if b == far_left_bucket:
                part = part + jnp.sum(far_acc[0, h], axis=0, keepdims=True)
                part = part + jnp.sum(extra_left, axis=0, keepdims=True)
            if b == far_right_bucket:
                part = part + jnp.sum(far_acc[1, h], axis=0, keepdims=True)
                part = part + jnp.sum(extra_right, axis=0, keepdims=True)
            tab_ref[h, b : b + 1, :] = part


def dkv_kernel(
    plan, rows, pair, bounds, table_ref, qall_ref, doall_ref, g_ref, kaug_ref, near_ref,
    dk_ref, dv_ref, mask_ref, qp, dop, kh_ref, vh_ref, acc_k, acc_v,
):
    lane = lanes_of(TQ)
    first = lanes_of(1)
    stat = (first >= plan.stat_lane) & (first < plan.stat_lane + 3 * plan.heads)
    qp[:PAD, :] = jnp.broadcast_to(jnp.where(stat, neg_big, 0.0).astype(bf16), (PAD, WIDE))
    qp[pl.ds(PAD + rows, PAD), :] = qp[:PAD, :]
    dop[:PAD, :] = jnp.zeros((PAD, WIDE), bf16)
    dop[pl.ds(PAD + rows, PAD), :] = jnp.zeros((PAD, WIDE), bf16)
    step = 512

    def fill(n, unused):
        at = pl.multiple_of(n * step, step)
        to = pl.multiple_of(PAD + n * step, 128)
        qp[pl.ds(to, step), :] = qall_ref[pl.ds(at, step), :]
        dop[pl.ds(to, step), :] = doall_ref[pl.ds(at, step), :]
        return unused

    lax.fori_loop(0, rows // step, fill, 0)
    low = lanes_of(TQ, 128) < 64
    ones = (lanes_of(TQ, 128) < 3 * plan.heads).astype(bf16)

    def tile(t, unused):
        start = pl.multiple_of(bounds[0] + t * TQ, 128)
        n_left, n_right = (bounds[1 + 2 * t], bounds[2 + 2 * t])
        out = pl.ds(pl.multiple_of(t * TQ, TQ), TQ)
        middle = g_ref[out, 128:256]
        k = jnp.concatenate([g_ref[out, 0:128], jnp.where(low, middle, kaug_ref[out, :])], axis=1)
        v = jnp.concatenate([jnp.where(low, ones, middle), g_ref[out, 256:384]], axis=1)
        near = pl.ds(pl.multiple_of(start + PAD - EDGE, 128), TK)

        def grads(h, s, span):
            p = jnp.exp(s)
            ds = p * nt(vh_ref[h], dop[span, :])
            return nn(p.astype(bf16), dop[span, :]), nn(ds.astype(bf16), qp[span, :])

        for h in range(plan.heads):
            kh_ref[h] = jnp.where(plan.key_lanes(lane, h), k, jnp.zeros_like(k))
            vh_ref[h] = jnp.where(plan.value_lanes(lane, h), v, jnp.zeros_like(v))
            acc_v[h], acc_k[h] = grads(h, nt(kh_ref[h], qp[near, :]) + near_ref[1, h], near)

        def far(bucket):
            def step(first, n):
                span = pl.ds(pl.multiple_of(first + n, 128), TK)
                for h in range(plan.heads):
                    add_v, add_k = grads(
                        h, nt(kh_ref[h], qp[span, :]) + table_ref[bucket, h], span
                    )
                    acc_v[h] += add_v
                    acc_k[h] += add_k
            return step

        left, right = (far(far_right_bucket), far(far_left_bucket))

        @pl.loop(0, n_left)
        def _(n):
            left(start + PAD - EDGE - TK, -n * TK)

        @pl.loop(0, n_right)
        def _(n):
            right(start + PAD - EDGE + TK, n * TK)

        dk = jnp.zeros((TQ, WIDE), f32)
        dv = jnp.zeros((TQ, WIDE), f32)
        mask_grad = jnp.zeros((TQ, 1), f32)
        for h in range(plan.heads):
            dk = jnp.where(lane // 64 == h, acc_k[h], dk)
            dv = jnp.where(lane // 64 == h + 1, acc_v[h], dv)
            mask_grad = mask_grad + acc_k[h][:, plan.mask_lane : plan.mask_lane + 1]
        mask_ref[t] = jnp.transpose(jnp.broadcast_to(mask_grad, (TQ, 128)))[:8, :]
        dk_ref[out, :] = dk.astype(bf16)
        dv_ref[out, :] = dv.astype(bf16)
        return unused

    lax.fori_loop(0, pair // TQ, tile, 0)


def grad_attended_kernel(plan, branch_ref, w_ref, wide_ref, do_ref):
    rows = branch_ref.shape[0]
    lane = lanes_of(rows)
    grad = nt(branch_ref[...], w_ref[...]).astype(bf16)
    terms = grad.astype(f32) * wide_ref[...]
    out = grad
    for h in range(plan.heads):
        row_term = jnp.sum(
            jnp.where(lane // 64 == h + 1, terms, 0.0), axis=1, keepdims=True
        )
        for i, part in enumerate(split3(-row_term)):
            out = jnp.where(lane == 3 * h + i, part, out)
    do_ref[...] = out


vmem = pl.BlockSpec(memory_space=pltpu.VMEM)
smem = pl.BlockSpec(memory_space=pltpu.SMEM)


def params():
    return pltpu.CompilerParams(vmem_limit_bytes=56 * 2**20)


class Spot:
    def __init__(self, lines):
        index = lax.axis_index("ctx")
        self.wa = lax.axis_index("wa")
        self.index = index
        self.lines = lines
        self.z = index // 4
        self.x = (index // 2) % 2
        self.core = index % 2

    def core_mate(self):
        return (self.index + 1 - 2 * self.core, self.wa)

    def x_mate(self):
        return (self.index + 2 - 4 * self.x, self.wa)

    def z_mate(self, step):
        return (jnp.clip(self.index + 4 * step, 0, 4 * self.lines - 1), self.wa)

    def y_mate(self):
        return (self.index, 1 - self.wa)


def send(src, dst, send_sem, recv_sem, device):
    return pltpu.make_async_remote_copy(
        src_ref=src,
        dst_ref=dst,
        send_sem=send_sem,
        recv_sem=recv_sem,
        device_id=device,
        device_id_type=pl.DeviceIdType.MESH,
    )


def greet(spot, with_y):
    barrier = pltpu.get_barrier_semaphore()
    mates = [spot.core_mate(), spot.x_mate()] + ([spot.y_mate()] if with_y else [])
    for mate in mates:
        pl.semaphore_signal(barrier, inc=1, device_id=mate, device_id_type=pl.DeviceIdType.MESH)

    @pl.when(spot.z + 1 < spot.lines)
    def _():
        pl.semaphore_signal(
            barrier, inc=1, device_id=spot.z_mate(1), device_id_type=pl.DeviceIdType.MESH
        )

    @pl.when(spot.z > 0)
    def _():
        pl.semaphore_signal(
            barrier, inc=1, device_id=spot.z_mate(-1), device_id_type=pl.DeviceIdType.MESH
        )

    above = (spot.z + 1 < spot.lines).astype(jnp.int32)
    below = (spot.z > 0).astype(jnp.int32)
    pl.semaphore_wait(barrier, len(mates) + above + below)


def added(a, b):
    return a + b


def scatter_kernel(lines, units, z_first, count, *refs):
    parts, outs = (refs[:count], refs[count : 2 * count])
    mine, core_in, x_in, up_in, down_in, load_sem, core_sem, x_sem, up_sem, down_sem = refs[
        2 * count :
    ]
    spot = Spot(lines)
    z, x, core = (spot.z, spot.x, spot.core)
    greet(spot, False)
    loads = []
    cores = []
    order = z_first + [u for u in range(len(units)) if u not in z_first]

    def rows_of(u):
        return pl.ds(units[u][1], units[u][2])

    for u in order:
        m = units[u][0]
        load = pltpu.make_async_copy(
            parts[m].at[:, :, core, rows_of(u)], mine.at[m, :, :, rows_of(u)], load_sem.at[u]
        )
        load.start()
        loads.append(load)
        copy = send(
            parts[m].at[:, :, 1 - core, rows_of(u)],
            core_in.at[m, :, :, rows_of(u)],
            core_sem.at[0, u],
            core_sem.at[1, u],
            spot.core_mate(),
        )
        copy.start()
        cores.append(copy)

    def add_slices(into, source, u, x_slot):
        m = units[u][0]

        def body(line, unused):
            at = (m, line, x_slot, rows_of(u))
            into[at] = added(into[at], source[at])
            return unused

        lax.fori_loop(0, lines, body, 0)

    def x_copy(u, both):
        m = units[u][0]
        if both:
            src = mine.at[m, :, 1 - x, rows_of(u)]
            dst = x_in.at[m, :, rows_of(u)]
        else:
            src = mine.at[m, z, 1 - x, rows_of(u)]
            dst = x_in.at[m, z, rows_of(u)]
        return send(src, dst, x_sem.at[0, u], x_sem.at[1, u], spot.x_mate())

    def line_flow(u, slots):
        m = units[u][0]
        n = len(slots)

        def slot_copies(step, d):
            ring, sem = (up_in, up_sem) if step > 0 else (down_in, down_sem)
            return [
                send(
                    mine.at[m, d, s, rows_of(u)],
                    ring.at[m, d, s, rows_of(u)],
                    sem.at[0, u, d, i],
                    sem.at[1, u, d, i],
                    spot.z_mate(step),
                )
                for i, s in enumerate(slots)
            ]

        def receive(step, d):
            ring = up_in if step > 0 else down_in
            for copy, s in zip(slot_copies(step, d), slots):
                copy.wait_recv()
                at = (m, d, s, rows_of(u))
                mine[at] = added(mine[at], ring[at])

        def ends_first():
            @pl.when(z == 0)
            def _():
                for d in range(lines - 1, 0, -1):
                    for copy in slot_copies(1, d):
                        copy.start()

            @pl.when(z == lines - 1)
            def _():
                for d in range(lines - 1):
                    for copy in slot_copies(-1, d):
                        copy.start()

        def relay(lag):
            top = lines - 2 if lag == 2 else lag

            @pl.when((z >= lag) & (z <= top))
            def _():
                def up(k, unused):
                    receive(1, lines - 1 - k)
                    for copy in slot_copies(1, lines - 1 - k):
                        copy.start()
                    return unused

                lax.fori_loop(0, lines - 1 - z, up, 0)

            @pl.when((lines - 1 - z >= lag) & (lines - 1 - z <= top))
            def _():
                def down(k, unused):
                    receive(-1, k)
                    for copy in slot_copies(-1, k):
                        copy.start()
                    return unused

                lax.fori_loop(0, z, down, 0)

        def arrive():
            @pl.when(z > 0)
            def _():
                receive(1, z)

            @pl.when(z + 1 < lines)
            def _():
                receive(-1, z)

        def finish(k, unused):
            @pl.when(z < lines - 1 - k)
            def _():
                for copy in slot_copies(1, lines - 1 - k):
                    copy.wait_send()

            @pl.when(z > k)
            def _():
                for copy in slot_copies(-1, k):
                    copy.wait_send()

            return unused

        return (
            ends_first,
            relay,
            arrive,
            lambda: lax.fori_loop(0, lines - 1, finish, 0),
        )

    def store(u):
        m = units[u][0]
        outs[m][rows_of(u), :] = mine[m, z, x, rows_of(u)].astype(f32)

    pending = {}
    for i, u in enumerate(order):
        loads[i].wait()
        cores[i].wait()
        if u in z_first:
            add_slices(mine, core_in, u, 0)
            add_slices(mine, core_in, u, 1)
        else:
            add_slices(mine, core_in, u, 1 - x)
            copy = x_copy(u, True)
            copy.start()
            pending[u] = copy
            add_slices(mine, core_in, u, x)
    x_first = [u for u in order if u not in z_first]
    flows = {u: line_flow(u, [0, 1] if u in z_first else [x]) for u in order}
    last = {}

    def x_stage(u):
        m = units[u][0]
        pending[u].wait()

        def body(line, unused):
            at = (m, line, x, rows_of(u))
            mine[at] = added(mine[at], x_in[m, line, rows_of(u)])
            return unused

        lax.fori_loop(0, lines, body, 0)

    def settle(u):
        flows[u][2]()
        if u in z_first:
            last[u] = x_copy(u, False)
            last[u].start()
        else:
            store(u)

    for t in range(len(order) + 3):
        if t < len(order):
            u = order[t]
            if u not in z_first:
                x_stage(u)
            flows[u][0]()
        for lag in (1, 2):
            if 0 <= t - lag < len(order):
                flows[order[t - lag]][1](lag)
        if 0 <= t - 3 < len(order):
            settle(order[t - 3])
    for u, copy in last.items():
        m = units[u][0]
        copy.wait()
        at = (m, z, x, rows_of(u))
        mine[at] = added(mine[at], x_in[m, z, rows_of(u)])
        store(u)
    for u in order:
        flows[u][3]()


def reduce_scatter(parts, cycle_size):
    lines = cycle_size // 4
    count = len(parts)
    rows, model = parts[0].shape[1:]
    cut = (rows // 2 + 15) // 16 * 16
    pieces = [(0, cut), (cut, rows - cut)] if cut < rows else [(0, rows)]
    units = [(m, at, size) for m in range(count) for at, size in pieces]
    z_first = [len(units) - 1]
    shaped = [part.reshape(lines, 2, 2, rows, model) for part in parts]
    hbm = pl.BlockSpec(memory_space=pl.ANY)
    n = len(units)
    return pl.pallas_call(
        functools.partial(scatter_kernel, lines, units, z_first, count),
        out_shape=[jax.ShapeDtypeStruct((rows, model), f32)] * count,
        in_specs=[hbm] * count,
        out_specs=[vmem] * count,
        scratch_shapes=[
            pltpu.VMEM((count, lines, 2, rows, model), bf16),
            pltpu.VMEM((count, lines, 2, rows, model), bf16),
            pltpu.VMEM((count, lines, rows, model), bf16),
            pltpu.VMEM((count, lines, 2, rows, model), bf16),
            pltpu.VMEM((count, lines, 2, rows, model), bf16),
            pltpu.SemaphoreType.DMA((n,)),
            pltpu.SemaphoreType.DMA((2, n)),
            pltpu.SemaphoreType.DMA((2, n)),
            pltpu.SemaphoreType.DMA((2, n, lines, 2)),
            pltpu.SemaphoreType.DMA((2, n, lines, 2)),
        ],
        compiler_params=pltpu.CompilerParams(
            vmem_limit_bytes=58 * 2**20, collective_id=1, has_side_effects=True
        ),
        name="weight_scatter",
    )(*shaped)

def first_kernel(
    plan, lines, span, reach, rows, starts, table_ref, tokens_ref, gain_ref, mask_ref,
    wq_hbm, wk_hbm, wv_hbm, wo_hbm,
    x_ref, tok_ref, q_ref, own_ref, aug_ref, own_aug_ref, near_ref, masks_ref, wo_far_hbm, all_hbm,
    weights, zeros, load_sem, y_sem, own_sem, zero_sem, z_sem, x_sem, c_sem,
):
    spot = Spot(lines)
    z, x, core, wa = (spot.z, spot.x, spot.core, spot.wa)
    half, model = tokens_ref.shape
    cols = plan.cols
    chunk = half // 4
    loads = [
        pltpu.make_async_copy(src, weights.at[pl.ds(i * cols, cols)], load_sem.at[i])
        for i, src in enumerate((wk_hbm, wv_hbm, wq_hbm))
    ]
    for load in loads:
        load.start()
    greet(spot, True)
    zeros[...] = jnp.zeros_like(zeros)

    def outside(d):
        return (d < z - span) | (d > z + span)

    def zero_copies(d):
        return [
            pltpu.make_async_copy(zeros, all_hbm.at[d, a, b], zero_sem.at[d, a, b])
            for a in range(2)
            for b in range(2)
        ]

    def zero_start(d, unused):
        @pl.when(outside(d))
        def _():
            masks_ref[d] = jnp.zeros((2, 2) + mask_ref.shape, f32)
            for copy in zero_copies(d):
                copy.start()

        return unused

    def rows_at(start, size):
        return pl.ds(pl.multiple_of(start, size), size)

    ours = wa * half
    theirs = (1 - wa) * half

    def y_copy(i, base):
        return send(
            tokens_ref.at[rows_at(i * chunk, chunk)],
            tok_ref.at[rows_at(base + i * chunk, chunk)],
            y_sem.at[0, i],
            y_sem.at[1, i],
            spot.y_mate(),
        )

    def y_start(i, unused):
        y_copy(i, ours).start()
        return unused

    lax.fori_loop(0, 4, y_start, 0)
    far_copy = send(wo_hbm, wo_far_hbm, y_sem.at[0, 4], y_sem.at[1, 4], spot.y_mate())
    far_copy.start()

    def scaled(rows_in):
        rows_in = rows_in.astype(f32)
        inv = lax.rsqrt(jnp.mean(rows_in * rows_in, axis=-1, keepdims=True) + eps)
        return (rows_in * inv * gain_ref[...]).astype(bf16)

    def normal(i, unused):
        at = rows_at(ours + i * chunk, chunk)
        rows_in = tokens_ref[rows_at(i * chunk, chunk), :]
        tok_ref[at, :] = rows_in
        x_ref[at, :] = scaled(rows_in)
        return unused

    lax.fori_loop(0, 4, normal, 0)
    for load in loads:
        load.wait()

    def project(base):
        rows = rows_at(base, half)
        qkv = nt(x_ref[rows, :], weights[...]).astype(bf16)
        own_ref[rows, :] = qkv[:, : 2 * cols]
        q_ref[rows, :cols] = qkv[:, 2 * cols :]

    pieces = [
        (ours, half, True),
        (theirs, half // 2, True),
        (theirs + half // 2, half // 2, False),
        None,
    ]
    mask_piece = 3

    def line_first(p):
        return p == mask_piece or pieces[p][2]

    def piece_rows(p):
        return rows_at(pieces[p][0], pieces[p][1])

    def source(p, d, a):
        if p == mask_piece:
            return masks_ref.at[d, a, core]
        return all_hbm.at[d, a, core, piece_rows(p)]

    def own_source(p):
        return mask_ref if p == mask_piece else own_ref.at[piece_rows(p)]

    def pass_copy(p, step, d, own):
        i = 0 if step > 0 else 1
        if line_first(p):
            dst = source(p, d, x)
            src = own_source(p) if own else dst
        else:
            dst = all_hbm.at[d, :, core, piece_rows(p)]
            src = dst
        return send(src, dst, z_sem.at[p, i, d], z_sem.at[p, 2 + i, d], spot.z_mate(step))

    def across(p, d, own):
        dst = source(p, d, x)
        src = own_source(p) if own else dst
        return send(src, dst, x_sem.at[p, 0, d], x_sem.at[p, 1, d], spot.x_mate())

    def beside(p, d):
        if p == mask_piece:
            part = masks_ref.at[d, :, core]
        else:
            part = all_hbm.at[d, :, core, piece_rows(p)]
        return send(part, part, c_sem.at[p, 0, d], c_sem.at[p, 1, d], spot.core_mate())

    def own_copy(p):
        return pltpu.make_async_copy(
            own_source(p), source(p, z, x), own_sem.at[p]
        )

    def both_ways(p, own):
        @pl.when(z + 1 < lines)
        def _():
            pass_copy(p, 1, z, own).start()

        @pl.when(z > 0)
        def _():
            pass_copy(p, -1, z, own).start()

    def begin(p):
        own_copy(p).start()
        across(p, z, True).start()
        if line_first(p):
            both_ways(p, True)

    def level(p, k):
        @pl.when(z - k >= 0)
        def _():
            d = jnp.maximum(z - k, 0)
            pass_copy(p, 1, d, False).wait_recv()
            if k < span:

                @pl.when(z + 1 < lines)
                def _():
                    pass_copy(p, 1, d, False).start()

            if line_first(p):
                across(p, d, False).start()
            else:
                beside(p, d).start()

        @pl.when(z + k < lines)
        def _():
            d = jnp.minimum(z + k, lines - 1)
            pass_copy(p, -1, d, False).wait_recv()
            if k < span:

                @pl.when(z > 0)
                def _():
                    pass_copy(p, -1, d, False).start()

            if line_first(p):
                across(p, d, False).start()
            else:
                beside(p, d).start()

    def turn(p):
        across(p, z, True).wait()
        own_copy(p).wait()
        both_ways(p, False)
        beside(p, z).start()

    def settle(p, k):
        for sign in (1, -1) if k else (1,):
            d = z - sign * k

            @pl.when((d >= 0) & (d < lines))
            def _(d=d):
                d = jnp.clip(d, 0, lines - 1)
                across(p, d, k == 0).wait()
                if k == 0:
                    own_copy(p).wait()
                beside(p, d).start()

    def doc_of(start, size):
        position = start + lax.broadcasted_iota(jnp.int32, (size, 128), 0)

        def count(e, total):
            return total + (position >= starts[e]).astype(jnp.int32)

        return lax.fori_loop(1, starts.shape[0], count, jnp.zeros((size, 128), jnp.int32))

    def code_lanes(start, size):
        lane = lanes_of(size, 128) + 128
        code = jnp.maximum(lane - plan.doc_lane, 0)
        bit = jnp.bitwise_and(jnp.right_shift(doc_of(start, size), code // 2), 1)
        coded = (lane >= plan.doc_lane) & (lane < plan.stat_lane)
        ones = (lane >= plan.stat_lane) & (lane < plan.stat_lane + 3 * plan.heads)
        return lane, coded, bit != code % 2, ones

    pair = 2 * half
    base = spot.index * pair
    origin = jnp.clip(base - reach * pair, 0, 4 * lines * pair - rows)

    def key_lanes(n, unused):
        at = rows_at(n * half, half)
        lane, coded, differs, ones = code_lanes(origin + n * half, half)
        aug_ref[at, :] = jnp.where(
            coded & differs, neg_big, jnp.where(ones, 1.0, 0.0)
        ).astype(bf16)
        return unused

    def own_lanes(n, unused):
        at = rows_at(n * half, half)
        lane, coded, differs, ones = code_lanes(base + n * half, half)
        column = jnp.transpose(
            jnp.broadcast_to(mask_ref[0:1, at], (128, half))
        )
        own_aug_ref[at, :] = jnp.where(
            lane == plan.mask_lane,
            column,
            jnp.where(coded & differs, neg_big, jnp.where(ones, 1.0, 0.0)),
        ).astype(bf16)
        tail = jnp.where(
            (lane == plan.mask_lane) | (coded & ~differs), 1.0, 0.0
        ).astype(bf16)
        q_ref[at, 128:] = tail
        return unused

    begin(mask_piece)
    lax.fori_loop(0, 2, own_lanes, 0)
    project(ours)
    begin(0)
    lax.fori_loop(0, lines, zero_start, 0)
    near_lanes(plan.heads, table_ref, near_ref)
    lax.fori_loop(0, rows // half, key_lanes, 0)

    def y_wait(i, unused):
        y_copy(i, theirs).wait_recv()
        at = rows_at(theirs + i * chunk, chunk)
        x_ref[at, :] = scaled(tok_ref[at, :])
        return unused

    lax.fori_loop(0, 2, y_wait, 0)
    level(0, 1)
    level(mask_piece, 1)
    lax.fori_loop(2, 4, y_wait, 0)
    project(theirs)
    begin(2)
    begin(1)
    if span > 1:
        level(0, 2)
        level(mask_piece, 2)
    settle(0, 0)
    settle(mask_piece, 0)
    turn(2)
    level(1, 1)
    settle(0, 1)
    settle(mask_piece, 1)
    level(2, 1)
    if span > 1:
        level(1, 2)
        settle(0, 2)
        settle(mask_piece, 2)
    settle(1, 0)
    settle(1, 1)
    if span > 1:
        level(2, 2)
        settle(1, 2)
    for k in range(3, span + 1):
        for p in range(4):
            level(p, k)
        for p in (0, 1, mask_piece):
            settle(p, k)

    def finish_line(d, unused):
        @pl.when(~outside(d))
        def _():
            for p in range(4):
                beside(p, d).wait()

        @pl.when(outside(d))
        def _():
            for copy in zero_copies(d):
                copy.wait()

        for p in range(4):

            @pl.when((z + 1 < lines) & (d <= z) & (d > z - span))
            def _(p=p):
                pass_copy(p, 1, d, False).wait_send()

            @pl.when((z > 0) & (d >= z) & (d < z + span))
            def _(p=p):
                pass_copy(p, -1, d, False).wait_send()

        return unused

    lax.fori_loop(0, lines, finish_line, 0)

    def y_drain(i, unused):
        y_copy(i, ours).wait_send()
        return unused

    lax.fori_loop(0, 4, y_drain, 0)
    far_copy.wait()


def first(
    plan, cycle_size, reach, rows, starts, table, tokens, gain, mask, w_query, w_key, w_value, w_out
):
    lines = cycle_size // 4
    span = min(lines - 1, (reach + 3) // 4)
    half, model = tokens.shape
    pair = 2 * half
    hbm = pl.BlockSpec(memory_space=pl.ANY)
    dma = pltpu.SemaphoreType.DMA
    return pl.pallas_call(
        functools.partial(first_kernel, plan, lines, span, reach, rows),
        out_shape=[
            jax.ShapeDtypeStruct((pair, model), bf16),
            jax.ShapeDtypeStruct((pair, model), bf16),
            jax.ShapeDtypeStruct((pair, WIDE), bf16),
            jax.ShapeDtypeStruct((pair, 2 * plan.cols), bf16),
            jax.ShapeDtypeStruct((rows, 128), bf16),
            jax.ShapeDtypeStruct((pair, 128), bf16),
            jax.ShapeDtypeStruct((2, plan.heads, TQ, TK), f32),
            jax.ShapeDtypeStruct((lines, 2, 2, 8, pair), f32),
            jax.ShapeDtypeStruct(w_out.shape, bf16),
            jax.ShapeDtypeStruct((lines, 2, 2, pair, 2 * plan.cols), bf16),
        ],
        in_specs=[smem] * 2 + [vmem] * 3 + [hbm] * 4,
        out_specs=[vmem] * 8 + [hbm] * 2,
        scratch_shapes=[
            pltpu.VMEM((3 * plan.cols, model), bf16),
            pltpu.VMEM((pair, 2 * plan.cols), bf16),
            dma((3,)),
            dma((2, 5)),
            dma((4,)),
            dma((lines, 2, 2)),
            dma((4, 4, lines)),
            dma((4, 2, lines)),
            dma((4, 2, lines)),
        ],
        compiler_params=pltpu.CompilerParams(
            vmem_limit_bytes=56 * 2**20, collective_id=4, has_side_effects=True
        ),
        name="project_gather",
    )(starts, table, tokens, gain, mask, w_query.T, w_key.T, w_value.T, w_out)


def tn(a, b):
    return lax.dot_general(a, b, (((0,), (0,)), ((), ())), preferred_element_type=f32)


def line_relay(spot, start, receive):
    def level(k, unused):
        @pl.when(spot.z - k >= 0)
        def _():
            if_first(k, lambda: receive(1, spot.z - k))

            @pl.when(spot.z + 1 < spot.lines)
            def _():
                start(1, spot.z - k)

        @pl.when(spot.z + k < spot.lines)
        def _():
            if_first(k, lambda: receive(-1, spot.z + k))

            @pl.when(spot.z > 0)
            def _():
                start(-1, spot.z + k)

        return unused

    def if_first(k, run):
        @pl.when(k > 0)
        def _():
            run()

    return level


def finish_kernel(
    plan, lines, dq_ref, dk_ref, dv_ref, mask_ref, w3_ref, normed_ref, att_ref, branch_ref, far_ref,
    tokens_ref, gain_ref, hidden_ref, gh_ref, ffn_ref, small_ref,
    out_ref, gt_ref, gm_ref, weights_ref, total_ref,
    mine, core_in, x_in, up_in, down_in, all_w, y_out, y_in, own_part, ffn_in, mask_in,
    small_own, small_y, small_core, small_x, small_all,
    y_sem, core_sem, x_sem, up_sem, down_sem, gz_sem, gx_sem, gc_sem, sz_sem,
):
    spot = Spot(lines)
    z, x, core, wa = (spot.z, spot.x, spot.core, spot.wa)
    greet(spot, True)
    half = tokens_ref.shape[0]
    quarter = half // 2
    model = tokens_ref.shape[1]
    rows = mine.shape[3]

    def grad_rows(at):
        at = pl.ds(pl.multiple_of(at, quarter), quarter)
        return (
            nt(dq_ref[at, :], w3_ref[:, 0:256])
            + nt(dk_ref[at, :], w3_ref[:, 256:512])
            + nt(dv_ref[at, :], w3_ref[:, 512:768])
        )

    def y_copy(i):
        return send(y_out.at[i], y_in.at[i], y_sem.at[0, i], y_sem.at[1, i], spot.y_mate())

    def theirs(i, unused):
        y_out[i] = grad_rows((1 - wa) * half + i * quarter).astype(bf16)
        y_copy(i).start()
        return unused

    lax.fori_loop(0, 2, theirs, 0)
    mask_copy = send(
        mask_ref.at[1 - wa], mask_in, y_sem.at[0, 2], y_sem.at[1, 2], spot.y_mate()
    )
    mask_copy.start()

    def fill(product, matrix):
        for j in range(plan.cols // rows):
            s = matrix * (plan.cols // rows) + j
            mine[s // 4, (s // 2) % 2, s % 2] = product[j * rows : (j + 1) * rows].astype(bf16)

    fill(tn(dq_ref[...], normed_ref[...])[: plan.cols], 0)
    fill(tn(dk_ref[...], normed_ref[...])[: plan.cols], 1)
    fill(tn(dv_ref[...], normed_ref[...])[64:], 2)
    our_rows = pl.ds(pl.multiple_of(wa * half, half), half)
    their_rows = pl.ds(pl.multiple_of((1 - wa) * half, half), half)
    fill(
        (tn(att_ref[our_rows, :], branch_ref[...]) + tn(att_ref[their_rows, :], far_ref[...]))[64:],
        3,
    )
    core_copy = send(
        mine.at[:, :, 1 - core], core_in, core_sem.at[0, 0], core_sem.at[1, 0], spot.core_mate()
    )
    core_copy.start()
    ffn_copy = send(
        ffn_ref.at[their_rows], ffn_in, y_sem.at[0, 3], y_sem.at[1, 3], spot.y_mate()
    )
    ffn_copy.start()

    def ours(i, unused):
        own_part[pl.ds(pl.multiple_of(i * quarter, quarter), quarter), :] = grad_rows(
            wa * half + i * quarter
        )
        return unused

    lax.fori_loop(0, 2, ours, 0)
    core_copy.wait()

    def x_copy(d):
        return send(
            mine.at[d, 1 - x, core], x_in.at[d], x_sem.at[0, d], x_sem.at[1, d], spot.x_mate()
        )

    def core_add(d, unused):
        mine[d, 1 - x, core] = added(mine[d, 1 - x, core], core_in[d, 1 - x])
        x_copy(d).start()
        return unused

    lax.fori_loop(0, lines, core_add, 0)

    def core_add_own(d, unused):
        mine[d, x, core] = added(mine[d, x, core], core_in[d, x])
        return unused

    lax.fori_loop(0, lines, core_add_own, 0)

    gain_sum = jnp.zeros((1, model), f32)
    step = 32
    for i in range(2):
        y_copy(i).wait()

        def normal(j, total, i=i):
            at = pl.ds(pl.multiple_of(i * quarter + j * step, step), step)
            there = pl.ds(pl.multiple_of(j * step, step), step)
            grad = own_part[at, :] + y_in[i, there, :].astype(f32)
            rows_in = tokens_ref[at, :].astype(f32)
            inv = lax.rsqrt(jnp.mean(rows_in * rows_in, axis=-1, keepdims=True) + eps)
            scaled = gain_ref[...] * grad
            mean = jnp.mean(rows_in * scaled, axis=-1, keepdims=True)
            gt_ref[at, :] = gh_ref[at, :] + inv * scaled - rows_in * (inv * inv * inv * mean)
            return total + jnp.sum(grad * rows_in * inv, axis=0, keepdims=True)

        gain_sum = lax.fori_loop(0, quarter // step, normal, gain_sum)
    small_own[...] = small_ref[...]
    small_own[0:1, :] = gain_sum
    small_copy = send(
        small_own, small_y, y_sem.at[0, 4], y_sem.at[1, 4], spot.y_mate()
    )
    small_copy.start()
    mask_copy.wait()
    gm_ref[...] = mask_ref[wa] + mask_in[...]

    def flow(step, d):
        ring, sem = (up_in, up_sem) if step > 0 else (down_in, down_sem)
        return send(
            mine.at[d, x, core], ring.at[d], sem.at[0, d], sem.at[1, d], spot.z_mate(step)
        )

    def merge(step, d):
        flow(step, d).wait_recv()
        ring = up_in if step > 0 else down_in
        mine[d, x, core] = added(mine[d, x, core], ring[d])

    def x_add(d, unused):
        x_copy(d).wait()
        mine[d, x, core] = added(mine[d, x, core], x_in[d])

        @pl.when((z == 0) & (d > 0))
        def _():
            flow(1, d).start()

        @pl.when((z == lines - 1) & (d < lines - 1))
        def _():
            flow(-1, d).start()

        return unused

    lax.fori_loop(0, lines, x_add, 0)
    small_copy.wait()
    row = lax.broadcasted_iota(jnp.int32, small_own.shape, 0)
    small_x[0] = small_own[...] + jnp.where(row < 2, small_y[...], 0.0)
    small_core_copy = send(
        small_x.at[0], small_core, core_sem.at[0, 1], core_sem.at[1, 1], spot.core_mate()
    )
    small_core_copy.start()

    def relay(k, unused):
        high = lines - 1 - k

        @pl.when((z < high) & (z > 0))
        def _():
            merge(1, high)
            flow(1, high).start()

        @pl.when((z > k) & (z + 1 < lines))
        def _():
            merge(-1, k)
            flow(-1, k).start()

        return unused

    lax.fori_loop(0, lines - 1, relay, 0)
    small_core_copy.wait()
    small_x[1] = small_x[0] + small_core[...]
    small_x_copy = send(
        small_x.at[1], small_x.at[2], x_sem.at[0, lines], x_sem.at[1, lines], spot.x_mate()
    )
    small_x_copy.start()

    @pl.when(z > 0)
    def _():
        merge(1, z)

    @pl.when(z + 1 < lines)
    def _():
        merge(-1, z)

    all_w[z, x, core] = mine[z, x, core]

    def pass_w(step, d):
        i = 0 if step > 0 else 1
        return send(
            all_w.at[d, x, core], all_w.at[d, x, core], gz_sem.at[i, d], gz_sem.at[2 + i, d],
            spot.z_mate(step),
        )

    def pass_s(step, d):
        i = 0 if step > 0 else 1
        return send(
            small_all.at[d], small_all.at[d], sz_sem.at[i, d], sz_sem.at[2 + i, d],
            spot.z_mate(step),
        )

    def across(d):
        return send(
            all_w.at[d, x, core], all_w.at[d, x, core], gx_sem.at[0, d], gx_sem.at[1, d],
            spot.x_mate(),
        )

    def beside(d):
        return send(
            all_w.at[d, :, core], all_w.at[d, :, core], gc_sem.at[0, d], gc_sem.at[1, d],
            spot.core_mate(),
        )

    small_x_copy.wait()
    small_all[z] = small_x[1] + small_x[2]

    def receive(step, d):
        pass_w(step, d).wait_recv()
        across(d).start()

    across(z).start()
    lax.fori_loop(
        0, lines, line_relay(spot, lambda s, d: pass_w(s, d).start(), receive), 0
    )
    lax.fori_loop(
        0,
        lines,
        line_relay(
            spot, lambda s, d: pass_s(s, d).start(), lambda s, d: pass_s(s, d).wait_recv()
        ),
        0,
    )

    def add_small(d, total):
        return total + small_all[d]

    total_ref[...] = lax.fori_loop(1, lines, add_small, small_all[0])
    ffn_copy.wait()

    def last(j, unused):
        at = pl.ds(pl.multiple_of(j * step, step), step)
        here = pl.ds(pl.multiple_of(wa * half + j * step, step), step)
        total = hidden_ref[at, :] + ffn_ref[here, :].astype(f32) + ffn_in[at, :].astype(f32)
        out_ref[at, :] = total.astype(bf16)
        return unused

    lax.fori_loop(0, half // step, last, 0)

    def spread(d, unused):
        across(d).wait()
        beside(d).start()
        return unused

    lax.fori_loop(0, lines, spread, 0)

    def copy_out(d, unused):
        beside(d).wait()
        weights_ref[d] = all_w[d]
        return unused

    lax.fori_loop(0, lines, copy_out, 0)

    def drain(d, unused):
        @pl.when((z < d))
        def _():
            flow(1, d).wait_send()

        @pl.when((z > d))
        def _():
            flow(-1, d).wait_send()

        @pl.when((d <= z) & (z + 1 < lines))
        def _():
            pass_w(1, d).wait_send()
            pass_s(1, d).wait_send()

        @pl.when((d >= z) & (z > 0))
        def _():
            pass_w(-1, d).wait_send()
            pass_s(-1, d).wait_send()

        return unused

    lax.fori_loop(0, lines, drain, 0)


def finish(plan, cycle_size, *operands):
    lines = cycle_size // 4
    half, model = operands[9].shape
    rows = 4 * plan.cols // cycle_size
    dma = pltpu.SemaphoreType.DMA
    return pl.pallas_call(
        functools.partial(finish_kernel, plan, lines),
        out_shape=[
            jax.ShapeDtypeStruct((half, model), bf16),
            jax.ShapeDtypeStruct((half, model), f32),
            jax.ShapeDtypeStruct((8, half), f32),
            jax.ShapeDtypeStruct((lines, 2, 2, rows, model), bf16),
            jax.ShapeDtypeStruct((8, model), f32),
        ],
        in_specs=[vmem] * len(operands),
        out_specs=[vmem] * 5,
        scratch_shapes=[
            pltpu.VMEM((lines, 2, 2, rows, model), bf16),
            pltpu.VMEM((lines, 2, rows, model), bf16),
            pltpu.VMEM((lines, rows, model), bf16),
            pltpu.VMEM((lines, rows, model), bf16),
            pltpu.VMEM((lines, rows, model), bf16),
            pltpu.VMEM((lines, 2, 2, rows, model), bf16),
            pltpu.VMEM((2, half // 2, model), bf16),
            pltpu.VMEM((2, half // 2, model), bf16),
            pltpu.VMEM((half, model), f32),
            pltpu.VMEM((half, model), bf16),
            pltpu.VMEM((8, half), f32),
            pltpu.VMEM((8, model), f32),
            pltpu.VMEM((8, model), f32),
            pltpu.VMEM((8, model), f32),
            pltpu.VMEM((3, 8, model), f32),
            pltpu.VMEM((lines, 8, model), f32),
            dma((2, 5)),
            dma((2, 2)),
            dma((2, lines + 1)),
            dma((2, lines)),
            dma((2, lines)),
            dma((4, lines)),
            dma((2, lines)),
            dma((2, lines)),
            dma((4, lines)),
        ],
        compiler_params=pltpu.CompilerParams(
            vmem_limit_bytes=58 * 2**20, collective_id=2, has_side_effects=True
        ),
        name="finish",
    )(*operands)


root = 0.7978845608028654
cubic = 0.044715


def middle_kernel(
    plan, cycle_size, att_ref, mixed_ref, tokens_ref, cot_ref, gain_ref,
    wo_hbm, wo_far_hbm, wg_hbm, wu_hbm, wd_hbm,
    hidden_ref, gh_ref, branch_ref, ffn_ref, do_ref, gain_part_ref, *refs,
):
    stacks, refs = (refs[:3], refs[3:])
    (
        wg, wu, wd, wo, inner, gg, gu, x_ref, att_in, d_out, d_in, e_out, e_in,
        acc_f, acc_g, rows_buf, load_sem, y_sem, out_sem,
    ) = refs
    spot = Spot(cycle_size // 4)
    wa = spot.wa
    pair, model = tokens_ref.shape
    half = pair // 2
    units = wd.shape[1]
    chunk = half // 4
    block = pair // 4
    loads = [
        pltpu.make_async_copy(src, dst, load_sem.at[i])
        for i, (src, dst) in enumerate(
            (
                (wo_hbm, wo.at[0, 64:]),
                (wo_far_hbm, wo.at[1, 64:]),
                (wg_hbm, wg),
                (wu_hbm, wu),
                (wd_hbm, wd),
            )
        )
    ]
    for load in loads:
        load.start()
    barrier = pltpu.get_barrier_semaphore()
    pl.semaphore_signal(
        barrier, inc=1, device_id=spot.y_mate(), device_id_type=pl.DeviceIdType.MESH
    )
    wo[:, :64, :] = jnp.zeros((2, 64, model), bf16)
    pl.semaphore_wait(barrier, 1)
    ours = wa * half
    theirs = (1 - wa) * half

    def rows_at(start, size):
        return pl.ds(pl.multiple_of(start, size), size)

    def a_start(i):
        return (theirs + i * block) if i < 2 else (ours + (i - 2) * block)

    def a_copy(i, base):
        at = rows_at(base + (i % 2) * block, block)
        return send(att_ref.at[at], att_in.at[at], y_sem.at[0, i], y_sem.at[1, i], spot.y_mate())

    order = (0, 1, 2, 3)
    for i in order:
        a_copy(i, ours if i < 2 else theirs).start()
    loads[0].wait()
    loads[1].wait()

    def normal(i, base, keep):
        a_copy(i, base).wait_recv()
        at = rows_at(base + (i % 2) * block, block)
        branch = nn(att_ref[at, :], wo[0]) + nn(att_in[at, :], wo[1])
        hidden = tokens_ref[at, :].astype(f32) + branch
        if keep:
            hidden_ref[(i % 2) * block : (i % 2 + 1) * block, :] = hidden
        inv = lax.rsqrt(jnp.mean(hidden * hidden, axis=-1, keepdims=True) + eps)
        x_ref[at, :] = (hidden * inv * gain_ref[...]).astype(bf16)

    normal(0, theirs, False)
    normal(1, theirs, False)
    for load in loads[2:]:
        load.wait()
    wide = 256

    def feed(base):
        rows = rows_at(base, half)
        acc_f[...] = jnp.zeros_like(acc_f)
        acc_g[...] = jnp.zeros_like(acc_g)

        def tile(u, unused):
            cols = rows_at(u * wide, wide)
            gate = nn(x_ref[rows, :], wg[:, cols])
            upward = nn(x_ref[rows, :], wu[:, cols])
            grad_inner = nn(cot_ref[rows, :], wd[:, cols])
            square = gate * gate
            bend = jnp.tanh(root * gate * (1.0 + cubic * square))
            side = 0.5 * (1.0 + bend)
            gelu = gate * side
            slope = side + 0.5 * gate * (1.0 - bend * bend) * (
                root * (1.0 + 3.0 * cubic * square)
            )
            inner_low = (gelu * upward).astype(bf16)
            gate_low = (grad_inner * upward * slope).astype(bf16)
            up_low = (grad_inner * gelu).astype(bf16)
            inner[rows, cols] = inner_low
            gg[rows, cols] = gate_low
            gu[rows, cols] = up_low
            acc_g[...] += nt(gate_low, wg[:, cols]) + nt(up_low, wu[:, cols])
            acc_f[...] += nt(inner_low, wd[:, cols])
            return unused

        lax.fori_loop(0, units // wide, tile, 0)
        ffn_ref[rows, :] = acc_f[...].astype(bf16)

    def d_copy(i):
        return send(
            d_out.at[i], d_in.at[i], y_sem.at[0, 4 + i], y_sem.at[1, 4 + i], spot.y_mate()
        )

    def send_grad(i, unused):
        d_out[i] = acc_g[rows_at(i * chunk, chunk), :].astype(bf16)
        d_copy(i).start()
        return unused

    def half_pass(k, unused):
        base = theirs + k * (ours - theirs)
        feed(base)

        @pl.when(k == 0)
        def _():
            lax.fori_loop(0, 4, send_grad, 0)
            normal(2, ours, True)
            normal(3, ours, True)

        return unused

    lax.fori_loop(0, 2, half_pass, 0)
    parts = 2
    span = units // parts
    slices = cycle_size // parts
    size = units // cycle_size

    def out_copy(n):
        m, p = (n // parts, n % parts)
        return pltpu.make_async_copy(
            rows_buf.at[n % 2], stacks[m].at[pl.ds(p * slices, slices)], out_sem.at[n]
        )

    for n in range(3 * parts):
        m, p = (n // parts, n % parts)
        left = (inner, gg, gu)[m]
        right = (cot_ref, x_ref, x_ref)[m]
        if n >= 2:
            out_copy(n - 2).wait()
        turned = jnp.transpose(left[:, p * span : (p + 1) * span])
        for c in range(0, model, wide):
            end = min(model, c + wide)
            product = nn(turned, right[:, c:end]).astype(bf16)
            for s in range(slices):
                rows_buf[n % 2, s, :, c:end] = product[s * size : (s + 1) * size]
        out_copy(n).start()

    def e_copy(i):
        return send(
            e_out.at[i], e_in.at[i], y_sem.at[0, 8 + i], y_sem.at[1, 8 + i], spot.y_mate()
        )

    def normal_back(i, total):
        d_copy(i).wait()
        at = rows_at(i * chunk, chunk)
        grad = acc_g[at, :] + d_in[i].astype(f32)
        hidden = hidden_ref[at, :]
        inv = lax.rsqrt(jnp.mean(hidden * hidden, axis=-1, keepdims=True) + eps)
        scaled = gain_ref[...] * grad
        mean = jnp.mean(hidden * scaled, axis=-1, keepdims=True)
        grad_hidden = (
            cot_ref[rows_at(ours + i * chunk, chunk), :].astype(f32)
            + inv * scaled
            - hidden * (inv * inv * inv * mean)
        )
        gh_ref[at, :] = grad_hidden
        low = grad_hidden.astype(bf16)
        branch_ref[at, :] = low
        e_out[i] = nt(low, wo[1]).astype(bf16)
        e_copy(i).start()
        do_ref[rows_at(ours + i * chunk, chunk), :] = nt(low, wo[0]).astype(bf16)
        return total + jnp.sum(grad * hidden * inv, axis=0, keepdims=True)

    gain_part_ref[...] = lax.fori_loop(0, 4, normal_back, jnp.zeros((1, model), f32))

    def row_terms(at, grad):
        lane = lanes_of(chunk)
        terms = grad.astype(f32) * mixed_ref[at, :]
        out = grad
        for h in range(plan.heads):
            row_term = jnp.sum(
                jnp.where(lane // 64 == h + 1, terms, 0.0), axis=1, keepdims=True
            )
            for i, part in enumerate(split3(-row_term)):
                out = jnp.where(lane == 3 * h + i, part, out)
        do_ref[at, :] = out

    def own_terms(i, unused):
        at = rows_at(ours + i * chunk, chunk)
        row_terms(at, do_ref[at, :])
        return unused

    lax.fori_loop(0, 4, own_terms, 0)

    def far_terms(i, unused):
        e_copy(i).wait()
        row_terms(rows_at(theirs + i * chunk, chunk), e_in[i])
        return unused

    lax.fori_loop(0, 4, far_terms, 0)
    for n in (3 * parts - 2, 3 * parts - 1):
        out_copy(n).wait()
    for i in order:
        a_copy(i, ours if i < 2 else theirs).wait_send()


def middle(
    plan, cycle_size, attended, mixed, tokens, cot, gain, w_out, w_out_far, w_gate, w_up, w_down
):
    pair, model = tokens.shape
    half = pair // 2
    units = w_down.shape[0]
    size = units // cycle_size
    chunk = half // 4
    hbm = pl.BlockSpec(memory_space=pl.ANY)
    dma = pltpu.SemaphoreType.DMA
    return pl.pallas_call(
        functools.partial(middle_kernel, plan, cycle_size),
        out_shape=[
            jax.ShapeDtypeStruct((half, model), f32),
            jax.ShapeDtypeStruct((half, model), f32),
            jax.ShapeDtypeStruct((half, model), bf16),
            jax.ShapeDtypeStruct((pair, model), bf16),
            jax.ShapeDtypeStruct((pair, WIDE), bf16),
            jax.ShapeDtypeStruct((1, model), f32),
        ]
        + [jax.ShapeDtypeStruct((cycle_size, size, model), bf16)] * 3,
        in_specs=[vmem] * 5 + [hbm] * 5,
        out_specs=[vmem] * 6 + [hbm] * 3,
        scratch_shapes=[
            pltpu.VMEM((model, units), bf16),
            pltpu.VMEM((model, units), bf16),
            pltpu.VMEM((model, units), bf16),
            pltpu.VMEM((2, WIDE, model), bf16),
            pltpu.VMEM((pair, units), bf16),
            pltpu.VMEM((pair, units), bf16),
            pltpu.VMEM((pair, units), bf16),
            pltpu.VMEM((pair, model), bf16),
            pltpu.VMEM((pair, WIDE), bf16),
            pltpu.VMEM((4, chunk, model), bf16),
            pltpu.VMEM((4, chunk, model), bf16),
            pltpu.VMEM((4, chunk, WIDE), bf16),
            pltpu.VMEM((4, chunk, WIDE), bf16),
            pltpu.VMEM((half, model), f32),
            pltpu.VMEM((half, model), f32),
            pltpu.VMEM((2, cycle_size // 2, size, model), bf16),
            dma((5,)),
            dma((2, 12)),
            dma((6,)),
        ],
        compiler_params=pltpu.CompilerParams(
            vmem_limit_bytes=60 * 2**20, collective_id=3, has_side_effects=True
        ),
        name="feed_forward",
    )(attended, mixed, tokens, cot, gain, w_out, w_out_far, w_gate, w_up, w_down.T)


def shards(
    tokens,
    doc_lengths,
    key_mask,
    gain_attn,
    w_query,
    w_key,
    w_value,
    w_out,
    bias_table,
    gain_ffn,
    w_gate,
    w_up,
    w_down,
    cotangent,
):
    own_rows, model = tokens.shape
    group = lax.axis_size("wa")
    cycle_size = lax.axis_size("ctx")
    pair = own_rows * group
    heads = bias_table.shape[1]
    docs = doc_lengths.shape[0]
    plan = Plan(heads, w_query.shape[1] // heads, docs)
    total_rows = pair * cycle_size
    doc_most = min(MAXLEN, total_rows // 2)
    reach = min(cycle_size - 1, (doc_most - 1) // pair + 1)
    base = lax.axis_index("ctx") * pair
    rows = min(total_rows, (2 * reach + 1) * pair)
    origin = jnp.clip(base - reach * pair, 0, total_rows - rows).astype(jnp.int32)
    ends = jnp.cumsum(doc_lengths).astype(jnp.int32)
    starts = ends - doc_lengths

    def doc_at(positions):
        return jnp.sum((positions[:, None] >= starts[None, :]).astype(jnp.int32), axis=1) - 1

    tiles = pair // TQ
    tile_start = base + TQ * jnp.arange(tiles, dtype=jnp.int32)
    first_doc = jnp.arange(docs, dtype=jnp.int32)[None, :] == doc_at(tile_start)[:, None]
    last_doc = jnp.arange(docs, dtype=jnp.int32)[None, :] == doc_at(tile_start + TQ - 1)[:, None]
    low_end = jnp.sum(jnp.where(first_doc, starts[None, :], 0), axis=1)
    high_end = jnp.sum(jnp.where(last_doc, ends[None, :], 0), axis=1)
    n_left = jnp.maximum(0, (tile_start - EDGE - low_end + TK - 1) // TK)
    n_right = jnp.maximum(0, (high_end - (tile_start - EDGE + TK) + TK - 1) // TK)
    bounds = jnp.concatenate(
        [(base - origin)[None], jnp.stack([n_left, n_right], axis=1).reshape(-1)]
    ).astype(jnp.int32)

    pair_cot = lax.all_gather(cotangent, "wa", axis=0, tiled=True)

    def window(gathered):
        if rows == total_rows:
            return gathered
        return lax.dynamic_slice_in_dim(gathered, origin, rows, 0)

    gather = functools.partial(lax.all_gather, axis_name="ctx", axis=0, tiled=True)
    (
        pair_normed, pair_tokens, q_wide, own_kv, k_aug, own_aug, near_bias, masks, far_out, kv_all,
    ) = first(
        plan,
        cycle_size,
        reach,
        rows,
        starts,
        bias_table,
        tokens,
        gain_attn[None],
        jnp.broadcast_to(key_mask.astype(f32)[None], (8, pair)),
        w_query,
        w_key,
        w_value,
        w_out,
    )
    masks = masks.reshape(cycle_size, 8, pair)
    if rows < total_rows:
        masks = lax.dynamic_slice_in_dim(masks, origin // pair, rows // pair, 0)
    kv_all = window(kv_all.reshape(total_rows, 2 * plan.cols))
    padded = rows + 2 * PAD
    attended, mixed, q_back = pl.pallas_call(
        functools.partial(fwd_kernel, plan, rows, pair),
        out_shape=(
            jax.ShapeDtypeStruct((pair, WIDE), bf16),
            jax.ShapeDtypeStruct((pair, WIDE), f32),
            jax.ShapeDtypeStruct((pair, WIDE), bf16),
        ),
        in_specs=[smem, smem] + [vmem] * 5,
        out_specs=(vmem, vmem, vmem),
        scratch_shapes=[
            pltpu.VMEM((padded, WIDE), bf16),
            pltpu.VMEM((padded, WIDE), bf16),
            pltpu.VMEM((8, padded), f32),
            pltpu.VMEM((heads, TQ, WIDE), f32),
            pltpu.VMEM((heads, TQ, 128), f32),
            pltpu.VMEM((heads, TQ, WIDE), bf16),
        ],
        compiler_params=params(),
        name="attention_forward",
    )(bounds, bias_table, kv_all, k_aug, masks, q_wide, near_bias)
    q_all = window(gather(q_back))
    swap = functools.partial(lax.ppermute, axis_name="wa", perm=((0, 1), (1, 0)))
    hidden, grad_hidden, branch, ffn_part, do_wide, gain_ffn_part, *stacks = middle(
        plan,
        cycle_size,
        attended,
        mixed,
        pair_tokens,
        pair_cot,
        gain_ffn[None],
        w_out,
        far_out,
        w_gate,
        w_up,
        w_down,
    )
    far_branch = swap(branch)
    do_all = window(gather(do_wide))
    grad_w_down, grad_w_gate, grad_w_up = reduce_scatter(stacks, cycle_size)
    grad_w_gate, grad_w_up = (grad_w_gate.T, grad_w_up.T)

    grad_queries, table_part = pl.pallas_call(
        functools.partial(dq_kernel, plan, rows, pair),
        out_shape=(
            jax.ShapeDtypeStruct((pair, WIDE), bf16),
            jax.ShapeDtypeStruct((heads, 32, 128), f32),
        ),
        in_specs=[smem, smem] + [vmem] * 6,
        out_specs=(vmem, vmem),
        scratch_shapes=[
            pltpu.VMEM((padded, WIDE), bf16),
            pltpu.VMEM((padded, WIDE), bf16),
            pltpu.VMEM((8, padded), f32),
            pltpu.VMEM((heads, TQ, WIDE), f32),
            pltpu.VMEM((heads, TQ, WIDE), bf16),
            pltpu.VMEM((heads, TQ, WIDE), bf16),
            pltpu.VMEM((heads, TQ, TK), f32),
            pltpu.VMEM((2, heads, TQ, 128), f32),
        ],
        compiler_params=params(),
        name="attention_grad_queries",
    )(bounds, bias_table, kv_all, k_aug, masks, q_back, do_wide, near_bias)
    grad_keys, grad_values, mask_part = pl.pallas_call(
        functools.partial(dkv_kernel, plan, rows, pair),
        out_shape=(
            jax.ShapeDtypeStruct((pair, WIDE), bf16),
            jax.ShapeDtypeStruct((pair, WIDE), bf16),
            jax.ShapeDtypeStruct((tiles, 8, TQ), f32),
        ),
        in_specs=[smem, smem, vmem, vmem, vmem, vmem, vmem],
        out_specs=(vmem, vmem, vmem),
        scratch_shapes=[
            pltpu.VMEM((padded, WIDE), bf16),
            pltpu.VMEM((padded, WIDE), bf16),
            pltpu.VMEM((heads, TQ, WIDE), bf16),
            pltpu.VMEM((heads, TQ, WIDE), bf16),
            pltpu.VMEM((heads, TQ, WIDE), f32),
            pltpu.VMEM((heads, TQ, WIDE), f32),
        ],
        compiler_params=params(),
        name="attention_grad_keys",
    )(bounds, bias_table, q_all, do_all, own_kv, own_aug, near_bias)
    cols = plan.cols
    gap = jnp.zeros((model, WIDE - cols), bf16)
    w_wide = jnp.concatenate([w_query, gap, w_key, gap, gap, w_value], axis=1)
    table_row = jnp.sum(table_part, axis=2).reshape(1, -1)
    table_row = jnp.pad(table_row, ((0, 0), (0, model - table_row.shape[1])))
    small = jnp.concatenate(
        [jnp.zeros((1, model), f32), gain_ffn_part, table_row, jnp.zeros((5, model), f32)],
        axis=0,
    )
    layer_out, grad_tokens, grad_mask, weights, totals = finish(
        plan,
        cycle_size,
        grad_queries,
        grad_keys,
        grad_values,
        mask_part.reshape(group, 8, own_rows),
        w_wide,
        pair_normed,
        attended,
        branch,
        far_branch,
        tokens,
        gain_attn[None],
        hidden,
        grad_hidden,
        ffn_part,
        small,
    )
    weights = weights.reshape(4, cols, model).astype(f32)
    return (
        layer_out,
        grad_tokens,
        grad_mask[0],
        totals[0],
        weights[0].T,
        weights[1].T,
        weights[2].T,
        weights[3],
        totals[2, : heads * 32].reshape(heads, 32).T,
        totals[1],
        grad_w_gate,
        grad_w_up,
        grad_w_down,
    )


def solution(mesh):
    placed = (
        P(("ctx", "wa"), None),
        P(),
        P("ctx"),
        P(),
        P(None, "wa"),
        P(None, "wa"),
        P(None, "wa"),
        P("wa", None),
        P(None, "wa"),
        P(),
        P(None, "wa"),
        P(None, "wa"),
        P("wa", None),
        P(("ctx", "wa"), None),
    )
    return jax.shard_map(
        shards,
        mesh=mesh,
        in_specs=placed,
        out_specs=(
            P(("ctx", "wa"), None),
            P(("ctx", "wa"), None),
            P(("ctx", "wa")),
            P(),
            P(None, "wa"),
            P(None, "wa"),
            P(None, "wa"),
            P("wa", None),
            P(None, "wa"),
            P(),
            P(None, ("wa", "ctx")),
            P(None, ("wa", "ctx")),
            P(("wa", "ctx"), None),
        ),
        check_vma=False,
    )
```

```python
import functools

import jax
import jax.numpy as jnp
from jax import lax
from jax.experimental import pallas as pl
from jax.experimental.pallas import tpu as pltpu
from jax.sharding import PartitionSpec as P

MAXLEN = 8192

bucket_edges = (12, 16, 23, 32, 46, 64, 91)
neg_big = -1e30
eps = 1e-06
far_left_bucket = 15
far_right_bucket = 31
WIDE = 256
TQ = 256
TK = 512
EDGE = 128
PAD = TK + EDGE
f32 = jnp.float32
bf16 = jnp.bfloat16


def bucket_of(relative):
    distance = jnp.abs(relative)
    bucket = jnp.minimum(distance, 8) + 16 * (relative > 0).astype(jnp.int32)
    for edge in bucket_edges:
        bucket = bucket + (distance >= edge).astype(jnp.int32)
    return bucket


def norm_forward(inputs, gain):
    inv_root = lax.rsqrt(jnp.mean(inputs * inputs, axis=-1, keepdims=True) + eps)
    return (inputs * inv_root * gain, inv_root)


def norm_backward(inputs, inv_root, gain, grad_normed):
    scaled = gain * grad_normed
    cubed = inv_root * inv_root * inv_root
    grad_inputs = inv_root * scaled - inputs * cubed * jnp.mean(
        inputs * scaled, axis=-1, keepdims=True
    )
    grad_gain = jnp.sum(grad_normed * inputs * inv_root, axis=0)
    return (grad_inputs, grad_gain)


def gated(gate, upward):
    return jax.nn.gelu(gate, approximate=True) * upward


def nt(a, b):
    return lax.dot_general(a, b, (((1,), (1,)), ((), ())), preferred_element_type=f32)


def nn(a, b):
    return lax.dot_general(a, b, (((1,), (0,)), ((), ())), preferred_element_type=f32)


def split3(x):
    hi = x.astype(bf16)
    rest = x - hi.astype(f32)
    mid = rest.astype(bf16)
    return (hi, mid, (rest - mid.astype(f32)).astype(bf16))


class Plan:
    def __init__(self, heads, width, docs):
        self.heads = heads
        self.width = width
        self.bits = max(1, (docs - 1).bit_length())
        self.cols = heads * width
        self.mask_lane = self.cols
        self.doc_lane = self.cols + 1
        self.stat_lane = self.doc_lane + 2 * self.bits
        assert self.stat_lane + 3 * heads <= WIDE and self.cols + 64 == WIDE and width == 64

    def key_lanes(self, lane, h):
        own = (lane >= h * self.width) & (lane < (h + 1) * self.width)
        aug = (lane >= self.mask_lane) & (lane < self.stat_lane)
        stat = (lane >= self.stat_lane + 3 * h) & (lane < self.stat_lane + 3 * h + 3)
        return own | aug | stat

    def value_lanes(self, lane, h):
        own = (lane >= 64 + h * self.width) & (lane < 64 + (h + 1) * self.width)
        return own | ((lane >= 3 * h) & (lane < 3 * h + 3))


def lanes_of(rows, width=WIDE):
    return lax.broadcasted_iota(jnp.int32, (rows, width), 1)


def near_lanes(heads, table_ref, near_ref):
    row = lax.broadcasted_iota(jnp.int32, (EDGE, 3 * EDGE), 0)
    col = lax.broadcasted_iota(jnp.int32, (EDGE, 3 * EDGE), 1)
    relative = col - EDGE - row
    for flip in range(2):
        bucket = bucket_of(-relative if flip else relative)
        left, right = (far_left_bucket, far_right_bucket)
        if flip:
            left, right = (right, left)
        for h in range(heads):
            base = jnp.full((EDGE, 3 * EDGE), table_ref[0, h], f32)
            for b in range(1, 32):
                base = jnp.where(bucket == b, table_ref[b, h], base)
            far_l = jnp.full((EDGE, EDGE), table_ref[left, h], f32)
            far_r = jnp.full((EDGE, EDGE), table_ref[right, h], f32)
            near_ref[flip, h, :EDGE, : 3 * EDGE] = base
            near_ref[flip, h, :EDGE, 3 * EDGE :] = far_r
            near_ref[flip, h, EDGE:, EDGE:] = base
            near_ref[flip, h, EDGE:, :EDGE] = far_l


def build_keys(plan, g_ref, kaug_ref, masks_ref, km, vm, mask_row, rows):
    mask_row[...] = jnp.zeros_like(mask_row)
    size = masks_ref.shape[2]
    for n in range(masks_ref.shape[0]):
        mask_row[:, PAD + n * size : PAD + (n + 1) * size] = masks_ref[n]
    km[:PAD, :] = jnp.broadcast_to(
        jnp.where(pad_lanes(plan), neg_big, 0.0).astype(bf16), (PAD, WIDE)
    )
    km[pl.ds(PAD + rows, PAD), :] = km[:PAD, :]
    vm[:PAD, :] = jnp.zeros((PAD, WIDE), bf16)
    vm[pl.ds(PAD + rows, PAD), :] = jnp.zeros((PAD, WIDE), bf16)
    step = 512
    low = lanes_of(step, 128) < 64
    ones = (lanes_of(step, 128) < 3 * plan.heads).astype(bf16)

    def body(n, unused):
        at = pl.multiple_of(n * step, step)
        to = pl.multiple_of(PAD + n * step, 128)
        middle = g_ref[pl.ds(at, step), 128:256]
        km[pl.ds(to, step), 0:128] = g_ref[pl.ds(at, step), 0:128]
        km[pl.ds(to, step), 128:256] = jnp.where(low, middle, kaug_ref[pl.ds(at, step), :])
        vm[pl.ds(to, step), 0:128] = jnp.where(low, ones, middle)
        vm[pl.ds(to, step), 128:256] = g_ref[pl.ds(at, step), 256:384]
        return unused

    lax.fori_loop(0, rows // step, body, 0)


def far_span(start, n, n_left, left_bucket, right_bucket):
    on_left = n < n_left
    at = start + PAD - EDGE + TK * jnp.where(on_left, -1 - n, 1 + n - n_left)
    bucket = jnp.where(on_left, left_bucket, right_bucket)
    return pl.ds(pl.multiple_of(at, 128), TK), bucket


def pad_lanes(plan):
    lane = lanes_of(1)
    return (lane >= plan.doc_lane) & (lane < plan.stat_lane)


def fwd_kernel(
    plan, rows, pair, bounds, table_ref, g_ref, kaug_ref, masks_ref, q_ref, near_ref,
    low_ref, wide_ref, qb_ref, km, vm, mask_row, acc, row_max, qh_ref,
):
    build_keys(plan, g_ref, kaug_ref, masks_ref, km, vm, mask_row, rows)
    lane = lanes_of(TQ)

    def tile(t, unused):
        start = pl.multiple_of(bounds[0] + t * TQ, 128)
        n_left, n_right = (bounds[1 + 2 * t], bounds[2 + 2 * t])
        out = pl.ds(pl.multiple_of(t * TQ, TQ), TQ)
        q = q_ref[out, :]
        near = pl.ds(pl.multiple_of(start + PAD - EDGE, 128), TK)
        for h in range(plan.heads):
            qh = jnp.where(plan.key_lanes(lane, h), q, jnp.zeros_like(q))
            qh_ref[h] = qh
            s = nt(qh, km[near, :]) + near_ref[0, h] + mask_row[0:1, near]
            top = jnp.max(s, axis=1, keepdims=True)
            p = jnp.exp(s - top).astype(bf16)
            acc[h] = nn(p, vm[near, :])
            row_max[h] = jnp.broadcast_to(top, (TQ, 128))

        def far(n, unused):
            span, bucket = far_span(start, n, n_left, far_left_bucket, far_right_bucket)
            if True:
                for h in range(plan.heads):
                    s = nt(qh_ref[h], km[span, :]) + mask_row[0:1, span]
                    offset = table_ref[bucket, h]
                    old = row_max[h][:, :1]
                    top = jnp.maximum(old, jnp.max(s, axis=1, keepdims=True) + offset)
                    p = jnp.exp(s - (top - offset)).astype(bf16)
                    acc[h] = acc[h] * jnp.exp(old - top) + nn(p, vm[span, :])
                    row_max[h] = jnp.broadcast_to(top, (TQ, 128))
            return unused

        lax.fori_loop(0, n_left + n_right, far, 0)

        wide = jnp.zeros((TQ, WIDE), f32)
        qb = jnp.where(lane < plan.stat_lane, q, jnp.zeros_like(q))
        for h in range(plan.heads):
            total = acc[h][:, 3 * h : 3 * h + 1]
            log_total = row_max[h][:, :1] + jnp.log(total)
            wide = jnp.where(lane // 64 == h + 1, acc[h] / total, wide)
            for i, part in enumerate(split3(-log_total)):
                qb = jnp.where(lane == plan.stat_lane + 3 * h + i, part, qb)
        wide_ref[out, :] = wide
        low_ref[out, :] = wide.astype(bf16)
        qb_ref[out, :] = qb
        return unused

    lax.fori_loop(0, pair // TQ, tile, 0)


def dq_kernel(
    plan, rows, pair, bounds, table_ref, g_ref, kaug_ref, masks_ref, qb_ref, do_ref, near_ref,
    dq_ref, tab_ref, km, vm, mask_row, acc, qh_ref, doh_ref, near_acc, far_acc,
):
    build_keys(plan, g_ref, kaug_ref, masks_ref, km, vm, mask_row, rows)
    lane = lanes_of(TQ)
    near_acc[...] = jnp.zeros_like(near_acc)
    far_acc[...] = jnp.zeros_like(far_acc)

    def tile(t, unused):
        start = pl.multiple_of(bounds[0] + t * TQ, 128)
        n_left, n_right = (bounds[1 + 2 * t], bounds[2 + 2 * t])
        out = pl.ds(pl.multiple_of(t * TQ, TQ), TQ)
        q = qb_ref[out, :]
        do = do_ref[out, :]
        near = pl.ds(pl.multiple_of(start + PAD - EDGE, 128), TK)

        def grads(h, s, span):
            p = jnp.exp(s)
            return p * nt(doh_ref[h], vm[span, :])

        for h in range(plan.heads):
            qh_ref[h] = jnp.where(plan.key_lanes(lane, h), q, jnp.zeros_like(q))
            doh_ref[h] = jnp.where(plan.value_lanes(lane, h), do, jnp.zeros_like(do))
            ds = grads(
                h, nt(qh_ref[h], km[near, :]) + near_ref[0, h] + mask_row[0:1, near], near
            )
            near_acc[h] += ds
            acc[h] = nn(ds.astype(bf16), km[near, :])

        def far(n, unused):
            span, bucket = far_span(start, n, n_left, far_left_bucket, far_right_bucket)
            slot = (n >= n_left).astype(jnp.int32)
            if True:
                for h in range(plan.heads):
                    offset = mask_row[0:1, span] + table_ref[bucket, h]
                    ds = grads(h, nt(qh_ref[h], km[span, :]) + offset, span)
                    acc[h] += nn(ds.astype(bf16), km[span, :])
                    far_acc[slot, h] += (
                        ds[:, 0:128] + ds[:, 128:256] + ds[:, 256:384] + ds[:, 384:512]
                    )
            return unused

        lax.fori_loop(0, n_left + n_right, far, 0)

        total = jnp.zeros((TQ, WIDE), f32)
        for h in range(plan.heads):
            total = jnp.where(lane // 64 == h, acc[h], total)
        dq_ref[out, :] = total.astype(bf16)
        return unused

    lax.fori_loop(0, pair // TQ, tile, 0)
    row = lax.broadcasted_iota(jnp.int32, (EDGE, 3 * EDGE), 0)
    col = lax.broadcasted_iota(jnp.int32, (EDGE, 3 * EDGE), 1)
    bucket = bucket_of(col - EDGE - row)
    for h in range(plan.heads):
        band = near_acc[h, :EDGE, : 3 * EDGE] + near_acc[h, EDGE:, EDGE:]
        extra_right = near_acc[h, :EDGE, 3 * EDGE :]
        extra_left = near_acc[h, EDGE:, :EDGE]
        for b in range(32):
            part = jnp.sum(jnp.where(bucket == b, band, 0.0), axis=0, keepdims=True)
            part = part[:, :128] + part[:, 128:256] + part[:, 256:]
            if b == far_left_bucket:
                part = part + jnp.sum(far_acc[0, h], axis=0, keepdims=True)
                part = part + jnp.sum(extra_left, axis=0, keepdims=True)
            if b == far_right_bucket:
                part = part + jnp.sum(far_acc[1, h], axis=0, keepdims=True)
                part = part + jnp.sum(extra_right, axis=0, keepdims=True)
            tab_ref[h, b : b + 1, :] = part


def dkv_kernel(
    plan, rows, pair, bounds, table_ref, qall_ref, doall_ref, g_ref, kaug_ref, near_ref,
    dk_ref, dv_ref, mask_ref, qp, dop, kh_ref, vh_ref, acc_k, acc_v,
):
    lane = lanes_of(TQ)
    first = lanes_of(1)
    stat = (first >= plan.stat_lane) & (first < plan.stat_lane + 3 * plan.heads)
    qp[:PAD, :] = jnp.broadcast_to(jnp.where(stat, neg_big, 0.0).astype(bf16), (PAD, WIDE))
    qp[pl.ds(PAD + rows, PAD), :] = qp[:PAD, :]
    dop[:PAD, :] = jnp.zeros((PAD, WIDE), bf16)
    dop[pl.ds(PAD + rows, PAD), :] = jnp.zeros((PAD, WIDE), bf16)
    step = 512

    def fill(n, unused):
        at = pl.multiple_of(n * step, step)
        to = pl.multiple_of(PAD + n * step, 128)
        qp[pl.ds(to, step), :] = qall_ref[pl.ds(at, step), :]
        dop[pl.ds(to, step), :] = doall_ref[pl.ds(at, step), :]
        return unused

    lax.fori_loop(0, rows // step, fill, 0)
    low = lanes_of(TQ, 128) < 64
    ones = (lanes_of(TQ, 128) < 3 * plan.heads).astype(bf16)

    def tile(t, unused):
        start = pl.multiple_of(bounds[0] + t * TQ, 128)
        n_left, n_right = (bounds[1 + 2 * t], bounds[2 + 2 * t])
        out = pl.ds(pl.multiple_of(t * TQ, TQ), TQ)
        middle = g_ref[out, 128:256]
        k = jnp.concatenate([g_ref[out, 0:128], jnp.where(low, middle, kaug_ref[out, :])], axis=1)
        v = jnp.concatenate([jnp.where(low, ones, middle), g_ref[out, 256:384]], axis=1)
        near = pl.ds(pl.multiple_of(start + PAD - EDGE, 128), TK)

        def grads(h, s, span):
            p = jnp.exp(s)
            ds = p * nt(vh_ref[h], dop[span, :])
            return nn(p.astype(bf16), dop[span, :]), nn(ds.astype(bf16), qp[span, :])

        for h in range(plan.heads):
            kh_ref[h] = jnp.where(plan.key_lanes(lane, h), k, jnp.zeros_like(k))
            vh_ref[h] = jnp.where(plan.value_lanes(lane, h), v, jnp.zeros_like(v))
            acc_v[h], acc_k[h] = grads(h, nt(kh_ref[h], qp[near, :]) + near_ref[1, h], near)

        def far(n, unused):
            span, bucket = far_span(start, n, n_left, far_right_bucket, far_left_bucket)
            if True:
                for h in range(plan.heads):
                    add_v, add_k = grads(
                        h, nt(kh_ref[h], qp[span, :]) + table_ref[bucket, h], span
                    )
                    acc_v[h] += add_v
                    acc_k[h] += add_k
            return unused

        lax.fori_loop(0, n_left + n_right, far, 0)

        dk = jnp.zeros((TQ, WIDE), f32)
        dv = jnp.zeros((TQ, WIDE), f32)
        mask_grad = jnp.zeros((TQ, 1), f32)
        for h in range(plan.heads):
            dk = jnp.where(lane // 64 == h, acc_k[h], dk)
            dv = jnp.where(lane // 64 == h + 1, acc_v[h], dv)
            mask_grad = mask_grad + acc_k[h][:, plan.mask_lane : plan.mask_lane + 1]
        mask_ref[t] = jnp.transpose(jnp.broadcast_to(mask_grad, (TQ, 128)))[:8, :]
        dk_ref[out, :] = dk.astype(bf16)
        dv_ref[out, :] = dv.astype(bf16)
        return unused

    lax.fori_loop(0, pair // TQ, tile, 0)


def grad_attended_kernel(plan, branch_ref, w_ref, wide_ref, do_ref):
    rows = branch_ref.shape[0]
    lane = lanes_of(rows)
    grad = nt(branch_ref[...], w_ref[...]).astype(bf16)
    terms = grad.astype(f32) * wide_ref[...]
    out = grad
    for h in range(plan.heads):
        row_term = jnp.sum(
            jnp.where(lane // 64 == h + 1, terms, 0.0), axis=1, keepdims=True
        )
        for i, part in enumerate(split3(-row_term)):
            out = jnp.where(lane == 3 * h + i, part, out)
    do_ref[...] = out


vmem = pl.BlockSpec(memory_space=pltpu.VMEM)
smem = pl.BlockSpec(memory_space=pltpu.SMEM)


def params():
    return pltpu.CompilerParams(vmem_limit_bytes=56 * 2**20)


class Spot:
    def __init__(self, lines):
        index = lax.axis_index("ctx")
        self.wa = lax.axis_index("wa")
        self.index = index
        self.lines = lines
        self.z = index // 4
        self.x = (index // 2) % 2
        self.core = index % 2

    def core_mate(self):
        return (self.index + 1 - 2 * self.core, self.wa)

    def x_mate(self):
        return (self.index + 2 - 4 * self.x, self.wa)

    def z_mate(self, step):
        return (jnp.clip(self.index + 4 * step, 0, 4 * self.lines - 1), self.wa)

    def y_mate(self):
        return (self.index, 1 - self.wa)


def send(src, dst, send_sem, recv_sem, device):
    return pltpu.make_async_remote_copy(
        src_ref=src,
        dst_ref=dst,
        send_sem=send_sem,
        recv_sem=recv_sem,
        device_id=device,
        device_id_type=pl.DeviceIdType.MESH,
    )


def greet(spot, with_y):
    barrier = pltpu.get_barrier_semaphore()
    mates = [spot.core_mate(), spot.x_mate()] + ([spot.y_mate()] if with_y else [])
    for mate in mates:
        pl.semaphore_signal(barrier, inc=1, device_id=mate, device_id_type=pl.DeviceIdType.MESH)

    @pl.when(spot.z + 1 < spot.lines)
    def _():
        pl.semaphore_signal(
            barrier, inc=1, device_id=spot.z_mate(1), device_id_type=pl.DeviceIdType.MESH
        )

    @pl.when(spot.z > 0)
    def _():
        pl.semaphore_signal(
            barrier, inc=1, device_id=spot.z_mate(-1), device_id_type=pl.DeviceIdType.MESH
        )

    above = (spot.z + 1 < spot.lines).astype(jnp.int32)
    below = (spot.z > 0).astype(jnp.int32)
    pl.semaphore_wait(barrier, len(mates) + above + below)


def added(a, b):
    return a + b


def scatter_kernel(lines, units, z_first, count, *refs):
    parts, outs = (refs[:count], refs[count : 2 * count])
    mine, core_in, x_in, up_in, down_in, load_sem, core_sem, x_sem, up_sem, down_sem = refs[
        2 * count :
    ]
    spot = Spot(lines)
    z, x, core = (spot.z, spot.x, spot.core)
    greet(spot, False)
    loads = []
    cores = []
    order = z_first + [u for u in range(len(units)) if u not in z_first]

    def rows_of(u):
        return pl.ds(units[u][1], units[u][2])

    for u in order:
        m = units[u][0]
        load = pltpu.make_async_copy(
            parts[m].at[:, :, core, rows_of(u)], mine.at[m, :, :, rows_of(u)], load_sem.at[u]
        )
        load.start()
        loads.append(load)
        copy = send(
            parts[m].at[:, :, 1 - core, rows_of(u)],
            core_in.at[m, :, :, rows_of(u)],
            core_sem.at[0, u],
            core_sem.at[1, u],
            spot.core_mate(),
        )
        copy.start()
        cores.append(copy)

    def add_slices(into, source, u, x_slot):
        m = units[u][0]

        def body(line, unused):
            at = (m, line, x_slot, rows_of(u))
            into[at] = added(into[at], source[at])
            return unused

        lax.fori_loop(0, lines, body, 0)

    def x_copy(u, both):
        m = units[u][0]
        if both:
            src = mine.at[m, :, 1 - x, rows_of(u)]
            dst = x_in.at[m, :, rows_of(u)]
        else:
            src = mine.at[m, z, 1 - x, rows_of(u)]
            dst = x_in.at[m, z, rows_of(u)]
        return send(src, dst, x_sem.at[0, u], x_sem.at[1, u], spot.x_mate())

    def line_flow(u, slots):
        m = units[u][0]
        n = len(slots)

        def slot_copies(step, d):
            ring, sem = (up_in, up_sem) if step > 0 else (down_in, down_sem)
            return [
                send(
                    mine.at[m, d, s, rows_of(u)],
                    ring.at[m, d, s, rows_of(u)],
                    sem.at[0, u, d, i],
                    sem.at[1, u, d, i],
                    spot.z_mate(step),
                )
                for i, s in enumerate(slots)
            ]

        def receive(step, d):
            ring = up_in if step > 0 else down_in
            for copy, s in zip(slot_copies(step, d), slots):
                copy.wait_recv()
                at = (m, d, s, rows_of(u))
                mine[at] = added(mine[at], ring[at])

        def ends_first():
            @pl.when(z == 0)
            def _():
                for d in range(lines - 1, 0, -1):
                    for copy in slot_copies(1, d):
                        copy.start()

            @pl.when(z == lines - 1)
            def _():
                for d in range(lines - 1):
                    for copy in slot_copies(-1, d):
                        copy.start()

        def relay(lag):
            top = lines - 2 if lag == 2 else lag

            @pl.when((z >= lag) & (z <= top))
            def _():
                def up(k, unused):
                    receive(1, lines - 1 - k)
                    for copy in slot_copies(1, lines - 1 - k):
                        copy.start()
                    return unused

                lax.fori_loop(0, lines - 1 - z, up, 0)

            @pl.when((lines - 1 - z >= lag) & (lines - 1 - z <= top))
            def _():
                def down(k, unused):
                    receive(-1, k)
                    for copy in slot_copies(-1, k):
                        copy.start()
                    return unused

                lax.fori_loop(0, z, down, 0)

        def arrive():
            @pl.when(z > 0)
            def _():
                receive(1, z)

            @pl.when(z + 1 < lines)
            def _():
                receive(-1, z)

        def finish(k, unused):
            @pl.when(z < lines - 1 - k)
            def _():
                for copy in slot_copies(1, lines - 1 - k):
                    copy.wait_send()

            @pl.when(z > k)
            def _():
                for copy in slot_copies(-1, k):
                    copy.wait_send()

            return unused

        return (
            ends_first,
            relay,
            arrive,
            lambda: lax.fori_loop(0, lines - 1, finish, 0),
        )

    def store(u):
        m = units[u][0]
        outs[m][rows_of(u), :] = mine[m, z, x, rows_of(u)].astype(f32)

    pending = {}
    for i, u in enumerate(order):
        loads[i].wait()
        cores[i].wait()
        if u in z_first:
            add_slices(mine, core_in, u, 0)
            add_slices(mine, core_in, u, 1)
        else:
            add_slices(mine, core_in, u, 1 - x)
            copy = x_copy(u, True)
            copy.start()
            pending[u] = copy
            add_slices(mine, core_in, u, x)
    x_first = [u for u in order if u not in z_first]
    flows = {u: line_flow(u, [0, 1] if u in z_first else [x]) for u in order}
    last = {}

    def x_stage(u):
        m = units[u][0]
        pending[u].wait()

        def body(line, unused):
            at = (m, line, x, rows_of(u))
            mine[at] = added(mine[at], x_in[m, line, rows_of(u)])
            return unused

        lax.fori_loop(0, lines, body, 0)

    def settle(u):
        flows[u][2]()
        if u in z_first:
            last[u] = x_copy(u, False)
            last[u].start()
        else:
            store(u)

    for t in range(len(order) + 3):
        if t < len(order):
            u = order[t]
            if u not in z_first:
                x_stage(u)
            flows[u][0]()
        for lag in (1, 2):
            if 0 <= t - lag < len(order):
                flows[order[t - lag]][1](lag)
        if 0 <= t - 3 < len(order):
            settle(order[t - 3])
    for u, copy in last.items():
        m = units[u][0]
        copy.wait()
        at = (m, z, x, rows_of(u))
        mine[at] = added(mine[at], x_in[m, z, rows_of(u)])
        store(u)
    for u in order:
        flows[u][3]()


def reduce_scatter(parts, cycle_size):
    lines = cycle_size // 4
    count = len(parts)
    units_here, model = parts[0].shape
    rows = units_here // cycle_size
    cut = (rows // 2 + 15) // 16 * 16
    pieces = [(0, cut), (cut, rows - cut)] if cut < rows else [(0, rows)]
    units = [(m, at, size) for m in range(count) for at, size in pieces]
    z_first = [len(units) - 1]
    shaped = [part.reshape(lines, 2, 2, rows, model) for part in parts]
    hbm = pl.BlockSpec(memory_space=pl.ANY)
    n = len(units)
    return pl.pallas_call(
        functools.partial(scatter_kernel, lines, units, z_first, count),
        out_shape=[jax.ShapeDtypeStruct((rows, model), f32)] * count,
        in_specs=[hbm] * count,
        out_specs=[vmem] * count,
        scratch_shapes=[
            pltpu.VMEM((count, lines, 2, rows, model), bf16),
            pltpu.VMEM((count, lines, 2, rows, model), bf16),
            pltpu.VMEM((count, lines, rows, model), bf16),
            pltpu.VMEM((count, lines, 2, rows, model), bf16),
            pltpu.VMEM((count, lines, 2, rows, model), bf16),
            pltpu.SemaphoreType.DMA((n,)),
            pltpu.SemaphoreType.DMA((2, n)),
            pltpu.SemaphoreType.DMA((2, n)),
            pltpu.SemaphoreType.DMA((2, n, lines, 2)),
            pltpu.SemaphoreType.DMA((2, n, lines, 2)),
        ],
        compiler_params=pltpu.CompilerParams(
            vmem_limit_bytes=58 * 2**20, collective_id=1, has_side_effects=True
        ),
        name="weight_scatter",
    )(*shaped)

def first_kernel(
    plan, lines, span, reach, rows, starts, table_ref, tokens_ref, gain_ref, mask_ref,
    wq_hbm, wk_hbm, wv_hbm, wo_hbm,
    x_ref, tok_ref, q_ref, own_ref, aug_ref, own_aug_ref, near_ref, masks_ref, wo_far_hbm, all_hbm,
    weights, zeros, load_sem, y_sem, own_sem, zero_sem, z_sem, x_sem, c_sem,
):
    spot = Spot(lines)
    z, x, core, wa = (spot.z, spot.x, spot.core, spot.wa)
    half, model = tokens_ref.shape
    cols = plan.cols
    chunk = half // 4
    loads = [
        pltpu.make_async_copy(src, weights.at[pl.ds(i * cols, cols)], load_sem.at[i])
        for i, src in enumerate((wk_hbm, wv_hbm, wq_hbm))
    ]
    for load in loads:
        load.start()
    greet(spot, True)
    zeros[...] = jnp.zeros_like(zeros)

    def outside(d):
        return (d < z - span) | (d > z + span)

    def zero_copies(d):
        return [
            pltpu.make_async_copy(zeros, all_hbm.at[d, a, b], zero_sem.at[d, a, b])
            for a in range(2)
            for b in range(2)
        ]

    def zero_start(d, unused):
        @pl.when(outside(d))
        def _():
            masks_ref[d] = jnp.zeros((2, 2) + mask_ref.shape, f32)
            for copy in zero_copies(d):
                copy.start()

        return unused

    def rows_at(start, size):
        return pl.ds(pl.multiple_of(start, size), size)

    ours = wa * half
    theirs = (1 - wa) * half

    def y_copy(i, base):
        return send(
            tokens_ref.at[rows_at(i * chunk, chunk)],
            tok_ref.at[rows_at(base + i * chunk, chunk)],
            y_sem.at[0, i],
            y_sem.at[1, i],
            spot.y_mate(),
        )

    def y_start(i, unused):
        y_copy(i, ours).start()
        return unused

    lax.fori_loop(0, 4, y_start, 0)
    far_copy = send(wo_hbm, wo_far_hbm, y_sem.at[0, 4], y_sem.at[1, 4], spot.y_mate())

    def scaled(rows_in):
        rows_in = rows_in.astype(f32)
        inv = lax.rsqrt(jnp.mean(rows_in * rows_in, axis=-1, keepdims=True) + eps)
        return (rows_in * inv * gain_ref[...]).astype(bf16)

    def normal(i, unused):
        at = rows_at(ours + i * chunk, chunk)
        rows_in = tokens_ref[rows_at(i * chunk, chunk), :]
        tok_ref[at, :] = rows_in
        x_ref[at, :] = scaled(rows_in)
        return unused

    lax.fori_loop(0, 4, normal, 0)
    for load in loads:
        load.wait()

    def project(base):
        rows = rows_at(base, half)
        qkv = nt(x_ref[rows, :], weights[...]).astype(bf16)
        own_ref[rows, :] = qkv[:, : 2 * cols]
        q_ref[rows, :cols] = qkv[:, 2 * cols :]

    pieces = [
        (ours, half, True),
        (theirs, half // 2, True),
        (theirs + half // 2, half // 2, False),
        None,
    ]
    mask_piece = 3

    def line_first(p):
        return p == mask_piece or pieces[p][2]

    def piece_rows(p):
        return rows_at(pieces[p][0], pieces[p][1])

    def source(p, d, a):
        if p == mask_piece:
            return masks_ref.at[d, a, core]
        return all_hbm.at[d, a, core, piece_rows(p)]

    def own_source(p):
        return mask_ref if p == mask_piece else own_ref.at[piece_rows(p)]

    def pass_copy(p, step, d, own):
        i = 0 if step > 0 else 1
        if line_first(p):
            dst = source(p, d, x)
            src = own_source(p) if own else dst
        else:
            dst = all_hbm.at[d, :, core, piece_rows(p)]
            src = dst
        return send(src, dst, z_sem.at[p, i, d], z_sem.at[p, 2 + i, d], spot.z_mate(step))

    def across(p, d, own):
        dst = source(p, d, x)
        src = own_source(p) if own else dst
        return send(src, dst, x_sem.at[p, 0, d], x_sem.at[p, 1, d], spot.x_mate())

    def beside(p, d):
        if p == mask_piece:
            part = masks_ref.at[d, :, core]
        else:
            part = all_hbm.at[d, :, core, piece_rows(p)]
        return send(part, part, c_sem.at[p, 0, d], c_sem.at[p, 1, d], spot.core_mate())

    def own_copy(p):
        return pltpu.make_async_copy(
            own_source(p), source(p, z, x), own_sem.at[p]
        )

    def both_ways(p, own):
        @pl.when(z + 1 < lines)
        def _():
            pass_copy(p, 1, z, own).start()

        @pl.when(z > 0)
        def _():
            pass_copy(p, -1, z, own).start()

    def begin(p):
        own_copy(p).start()
        across(p, z, True).start()
        if line_first(p):
            both_ways(p, True)

    def level(p, k):
        @pl.when(z - k >= 0)
        def _():
            d = jnp.maximum(z - k, 0)
            pass_copy(p, 1, d, False).wait_recv()
            if k < span:

                @pl.when(z + 1 < lines)
                def _():
                    pass_copy(p, 1, d, False).start()

            if line_first(p):
                across(p, d, False).start()
            else:
                beside(p, d).start()

        @pl.when(z + k < lines)
        def _():
            d = jnp.minimum(z + k, lines - 1)
            pass_copy(p, -1, d, False).wait_recv()
            if k < span:

                @pl.when(z > 0)
                def _():
                    pass_copy(p, -1, d, False).start()

            if line_first(p):
                across(p, d, False).start()
            else:
                beside(p, d).start()

    def turn(p):
        across(p, z, True).wait()
        own_copy(p).wait()
        both_ways(p, False)
        beside(p, z).start()

    def settle(p, k):
        for sign in (1, -1) if k else (1,):
            d = z - sign * k

            @pl.when((d >= 0) & (d < lines))
            def _(d=d):
                d = jnp.clip(d, 0, lines - 1)
                across(p, d, k == 0).wait()
                if k == 0:
                    own_copy(p).wait()
                beside(p, d).start()

    def doc_of(start, size):
        position = start + lax.broadcasted_iota(jnp.int32, (size, 128), 0)

        def count(e, total):
            return total + (position >= starts[e]).astype(jnp.int32)

        return lax.fori_loop(1, starts.shape[0], count, jnp.zeros((size, 128), jnp.int32))

    def code_lanes(start, size):
        lane = lanes_of(size, 128) + 128
        code = jnp.maximum(lane - plan.doc_lane, 0)
        bit = jnp.bitwise_and(jnp.right_shift(doc_of(start, size), code // 2), 1)
        coded = (lane >= plan.doc_lane) & (lane < plan.stat_lane)
        ones = (lane >= plan.stat_lane) & (lane < plan.stat_lane + 3 * plan.heads)
        return lane, coded, bit != code % 2, ones

    pair = 2 * half
    base = spot.index * pair
    origin = jnp.clip(base - reach * pair, 0, 4 * lines * pair - rows)

    def key_lanes(n, unused):
        at = rows_at(n * half, half)
        lane, coded, differs, ones = code_lanes(origin + n * half, half)
        aug_ref[at, :] = jnp.where(
            coded & differs, neg_big, jnp.where(ones, 1.0, 0.0)
        ).astype(bf16)
        return unused

    def own_lanes(n, unused):
        at = rows_at(n * half, half)
        lane, coded, differs, ones = code_lanes(base + n * half, half)
        column = jnp.transpose(
            jnp.broadcast_to(mask_ref[0:1, at], (128, half))
        )
        own_aug_ref[at, :] = jnp.where(
            lane == plan.mask_lane,
            column,
            jnp.where(coded & differs, neg_big, jnp.where(ones, 1.0, 0.0)),
        ).astype(bf16)
        tail = jnp.where(
            (lane == plan.mask_lane) | (coded & ~differs), 1.0, 0.0
        ).astype(bf16)
        q_ref[at, 128:] = tail
        return unused

    begin(mask_piece)
    lax.fori_loop(0, 2, own_lanes, 0)
    project(ours)
    begin(0)
    lax.fori_loop(0, lines, zero_start, 0)
    near_lanes(plan.heads, table_ref, near_ref)
    lax.fori_loop(0, rows // half, key_lanes, 0)

    def y_wait(i, unused):
        y_copy(i, theirs).wait_recv()
        at = rows_at(theirs + i * chunk, chunk)
        x_ref[at, :] = scaled(tok_ref[at, :])
        return unused

    lax.fori_loop(0, 2, y_wait, 0)
    level(0, 1)
    level(mask_piece, 1)
    lax.fori_loop(2, 4, y_wait, 0)
    far_copy.start()
    project(theirs)
    begin(2)
    begin(1)
    if span > 1:
        level(0, 2)
        level(mask_piece, 2)
    settle(0, 0)
    settle(mask_piece, 0)
    turn(2)
    level(1, 1)
    settle(0, 1)
    settle(mask_piece, 1)
    level(2, 1)
    if span > 1:
        level(1, 2)
        settle(0, 2)
        settle(mask_piece, 2)
    settle(1, 0)
    settle(1, 1)
    if span > 1:
        level(2, 2)
        settle(1, 2)
    for k in range(3, span + 1):
        for p in range(4):
            level(p, k)
        for p in (0, 1, mask_piece):
            settle(p, k)

    def finish_line(d, unused):
        @pl.when(~outside(d))
        def _():
            for p in range(4):
                beside(p, d).wait()

        @pl.when(outside(d))
        def _():
            for copy in zero_copies(d):
                copy.wait()

        for p in range(4):

            @pl.when((z + 1 < lines) & (d <= z) & (d > z - span))
            def _(p=p):
                pass_copy(p, 1, d, False).wait_send()

            @pl.when((z > 0) & (d >= z) & (d < z + span))
            def _(p=p):
                pass_copy(p, -1, d, False).wait_send()

        return unused

    lax.fori_loop(0, lines, finish_line, 0)

    def y_drain(i, unused):
        y_copy(i, ours).wait_send()
        return unused

    lax.fori_loop(0, 4, y_drain, 0)
    far_copy.wait()


def first(
    plan, cycle_size, reach, rows, starts, table, tokens, gain, mask, w_query, w_key, w_value, w_out
):
    lines = cycle_size // 4
    span = min(lines - 1, (reach + 3) // 4)
    half, model = tokens.shape
    pair = 2 * half
    hbm = pl.BlockSpec(memory_space=pl.ANY)
    dma = pltpu.SemaphoreType.DMA
    return pl.pallas_call(
        functools.partial(first_kernel, plan, lines, span, reach, rows),
        out_shape=[
            jax.ShapeDtypeStruct((pair, model), bf16),
            jax.ShapeDtypeStruct((pair, model), bf16),
            jax.ShapeDtypeStruct((pair, WIDE), bf16),
            jax.ShapeDtypeStruct((pair, 2 * plan.cols), bf16),
            jax.ShapeDtypeStruct((rows, 128), bf16),
            jax.ShapeDtypeStruct((pair, 128), bf16),
            jax.ShapeDtypeStruct((2, plan.heads, TQ, TK), f32),
            jax.ShapeDtypeStruct((lines, 2, 2, 8, pair), f32),
            jax.ShapeDtypeStruct(w_out.shape, bf16),
            jax.ShapeDtypeStruct((lines, 2, 2, pair, 2 * plan.cols), bf16),
        ],
        in_specs=[smem] * 2 + [vmem] * 3 + [hbm] * 4,
        out_specs=[vmem] * 8 + [hbm] * 2,
        scratch_shapes=[
            pltpu.VMEM((3 * plan.cols, model), bf16),
            pltpu.VMEM((pair, 2 * plan.cols), bf16),
            dma((3,)),
            dma((2, 5)),
            dma((4,)),
            dma((lines, 2, 2)),
            dma((4, 4, lines)),
            dma((4, 2, lines)),
            dma((4, 2, lines)),
        ],
        compiler_params=pltpu.CompilerParams(
            vmem_limit_bytes=56 * 2**20, collective_id=4, has_side_effects=True
        ),
        name="project_gather",
    )(starts, table, tokens, gain, mask, w_query.T, w_key.T, w_value.T, w_out)


def tn(a, b):
    return lax.dot_general(a, b, (((0,), (0,)), ((), ())), preferred_element_type=f32)


def line_relay(spot, start, receive):
    def level(k, unused):
        @pl.when(spot.z - k >= 0)
        def _():
            if_first(k, lambda: receive(1, spot.z - k))

            @pl.when(spot.z + 1 < spot.lines)
            def _():
                start(1, spot.z - k)

        @pl.when(spot.z + k < spot.lines)
        def _():
            if_first(k, lambda: receive(-1, spot.z + k))

            @pl.when(spot.z > 0)
            def _():
                start(-1, spot.z + k)

        return unused

    def if_first(k, run):
        @pl.when(k > 0)
        def _():
            run()

    return level


def finish_kernel(
    plan, lines, dq_ref, dk_ref, dv_ref, mask_ref, wq_hbm, wk_hbm, wv_hbm, normed_ref, att_ref, branch_ref, far_ref,
    tokens_ref, gain_ref, hidden_ref, gh_ref, ffn_ref, small_ref,
    out_ref, gt_ref, gm_ref, weights_ref, total_ref,
    w3_ref, load_sem, lefts, rights, product, mine, core_in, x_in, up_in, down_in, all_w, y_out, y_in, own_part, ffn_in, mask_in,
    small_own, small_y, small_core, small_x, small_all,
    y_sem, core_sem, x_sem, up_sem, down_sem, gz_sem, gx_sem, gc_sem, sz_sem,
):
    spot = Spot(lines)
    z, x, core, wa = (spot.z, spot.x, spot.core, spot.wa)
    cols = plan.cols
    loads = [
        pltpu.make_async_copy(src, w3_ref.at[pl.ds(at, cols)], load_sem.at[i])
        for i, (src, at) in enumerate(((wq_hbm, 0), (wk_hbm, WIDE), (wv_hbm, 3 * WIDE - cols)))
    ]
    for load in loads:
        load.start()
    gap = jnp.zeros((WIDE - cols, tokens_ref.shape[1]), bf16)
    w3_ref[cols:WIDE] = gap
    w3_ref[WIDE + cols : 2 * WIDE] = gap
    w3_ref[2 * WIDE : 3 * WIDE - cols] = gap
    greet(spot, True)
    for load in loads:
        load.wait()
    half = tokens_ref.shape[0]
    quarter = half // 2
    model = tokens_ref.shape[1]
    rows = mine.shape[3]

    def grad_rows(at):
        at = pl.ds(pl.multiple_of(at, quarter), quarter)
        return (
            nn(dq_ref[at, :], w3_ref[0:256])
            + nn(dk_ref[at, :], w3_ref[256:512])
            + nn(dv_ref[at, :], w3_ref[512:768])
        )

    def y_copy(i):
        return send(y_out.at[i], y_in.at[i], y_sem.at[0, i], y_sem.at[1, i], spot.y_mate())

    def theirs(i, unused):
        y_out[i] = grad_rows((1 - wa) * half + i * quarter).astype(bf16)
        y_copy(i).start()
        return unused

    lax.fori_loop(0, 2, theirs, 0)
    mask_copy = send(
        mask_ref.at[1 - wa], mask_in, y_sem.at[0, 2], y_sem.at[1, 2], spot.y_mate()
    )
    mask_copy.start()

    our_rows = pl.ds(pl.multiple_of(wa * half, half), half)
    their_rows = pl.ds(pl.multiple_of((1 - wa) * half, half), half)
    lefts[0] = dq_ref[...]
    lefts[1] = dk_ref[...]
    lefts[2] = dv_ref[...]
    lefts[3] = att_ref[...]
    rights[0] = normed_ref[...]
    rights[1, our_rows, :] = branch_ref[...]
    rights[1, their_rows, :] = far_ref[...]
    per = plan.cols // rows

    def core_copy(m):
        part = pl.ds(m * per // 4, per // 4)
        return send(
            mine.at[part, :, 1 - core],
            core_in.at[part],
            core_sem.at[0, m],
            core_sem.at[1, m],
            spot.core_mate(),
        )

    def fill(m, unused):
        product[...] = tn(lefts[m], rights[m // 3]).astype(bf16)

        def place(offset):
            for j in range(per):
                mine[m * per // 4 + j // 4, (j // 2) % 2, j % 2] = product[
                    offset + j * rows : offset + (j + 1) * rows, :
                ]

        @pl.when(m < 2)
        def _():
            place(0)

        @pl.when(m >= 2)
        def _():
            place(WIDE - plan.cols)

        core_copy(m).start()
        return unused

    lax.fori_loop(0, 4, fill, 0)
    ffn_copy = send(
        ffn_ref.at[their_rows], ffn_in, y_sem.at[0, 3], y_sem.at[1, 3], spot.y_mate()
    )
    ffn_copy.start()

    def x_copy(d):
        return send(
            mine.at[d, 1 - x, core], x_in.at[d], x_sem.at[0, d], x_sem.at[1, d], spot.x_mate()
        )

    def core_add(d, unused):
        mine[d, 1 - x, core] = added(mine[d, 1 - x, core], core_in[d, 1 - x])
        x_copy(d).start()
        return unused

    def ours(i, unused):
        own_part[pl.ds(pl.multiple_of(i * quarter, quarter), quarter), :] = grad_rows(
            wa * half + i * quarter
        )
        return unused

    def core_stage(m, unused):
        core_copy(m).wait()
        lax.fori_loop(m * per // 4, (m + 1) * per // 4, core_add, 0)
        return unused

    lax.fori_loop(0, 4, core_stage, 0)

    def core_add_own(d, unused):
        mine[d, x, core] = added(mine[d, x, core], core_in[d, x])
        return unused

    lax.fori_loop(0, lines, core_add_own, 0)
    lax.fori_loop(0, 2, ours, 0)

    gain_sum = jnp.zeros((1, model), f32)
    step = 32
    for i in range(2):
        y_copy(i).wait()

        def normal(j, total, i=i):
            at = pl.ds(pl.multiple_of(i * quarter + j * step, step), step)
            there = pl.ds(pl.multiple_of(j * step, step), step)
            grad = own_part[at, :] + y_in[i, there, :].astype(f32)
            rows_in = tokens_ref[at, :].astype(f32)
            inv = lax.rsqrt(jnp.mean(rows_in * rows_in, axis=-1, keepdims=True) + eps)
            scaled = gain_ref[...] * grad
            mean = jnp.mean(rows_in * scaled, axis=-1, keepdims=True)
            gt_ref[at, :] = gh_ref[at, :] + inv * scaled - rows_in * (inv * inv * inv * mean)
            return total + jnp.sum(grad * rows_in * inv, axis=0, keepdims=True)

        gain_sum = lax.fori_loop(0, quarter // step, normal, gain_sum)
    small_own[...] = small_ref[...]
    small_own[0:1, :] = gain_sum
    small_copy = send(
        small_own, small_y, y_sem.at[0, 4], y_sem.at[1, 4], spot.y_mate()
    )
    small_copy.start()
    mask_copy.wait()
    gm_ref[...] = mask_ref[wa] + mask_in[...]

    def flow(step, d):
        ring, sem = (up_in, up_sem) if step > 0 else (down_in, down_sem)
        return send(
            mine.at[d, x, core], ring.at[d], sem.at[0, d], sem.at[1, d], spot.z_mate(step)
        )

    def merge(step, d):
        flow(step, d).wait_recv()
        ring = up_in if step > 0 else down_in
        mine[d, x, core] = added(mine[d, x, core], ring[d])

    def x_add(d, unused):
        x_copy(d).wait()
        mine[d, x, core] = added(mine[d, x, core], x_in[d])

        @pl.when((z == 0) & (d > 0))
        def _():
            flow(1, d).start()

        @pl.when((z == lines - 1) & (d < lines - 1))
        def _():
            flow(-1, d).start()

        return unused

    lax.fori_loop(0, lines, x_add, 0)
    small_copy.wait()
    row = lax.broadcasted_iota(jnp.int32, small_own.shape, 0)
    small_x[0] = small_own[...] + jnp.where(row < 2, small_y[...], 0.0)
    small_core_copy = send(
        small_x.at[0], small_core, core_sem.at[0, 4], core_sem.at[1, 4], spot.core_mate()
    )
    small_core_copy.start()

    def relay(k, unused):
        high = lines - 1 - k

        @pl.when((z < high) & (z > 0))
        def _():
            merge(1, high)
            flow(1, high).start()

        @pl.when((z > k) & (z + 1 < lines))
        def _():
            merge(-1, k)
            flow(-1, k).start()

        return unused

    lax.fori_loop(0, lines - 1, relay, 0)
    small_core_copy.wait()
    small_x[1] = small_x[0] + small_core[...]
    small_x_copy = send(
        small_x.at[1], small_x.at[2], x_sem.at[0, lines], x_sem.at[1, lines], spot.x_mate()
    )
    small_x_copy.start()

    @pl.when(z > 0)
    def _():
        merge(1, z)

    @pl.when(z + 1 < lines)
    def _():
        merge(-1, z)

    all_w[z, x, core] = mine[z, x, core]

    def pass_w(step, d):
        i = 0 if step > 0 else 1
        return send(
            all_w.at[d, x, core], all_w.at[d, x, core], gz_sem.at[i, d], gz_sem.at[2 + i, d],
            spot.z_mate(step),
        )

    def pass_s(step, d):
        i = 0 if step > 0 else 1
        return send(
            small_all.at[d], small_all.at[d], sz_sem.at[i, d], sz_sem.at[2 + i, d],
            spot.z_mate(step),
        )

    def across(d):
        return send(
            all_w.at[d, x, core], all_w.at[d, x, core], gx_sem.at[0, d], gx_sem.at[1, d],
            spot.x_mate(),
        )

    def beside(d):
        return send(
            all_w.at[d, :, core], all_w.at[d, :, core], gc_sem.at[0, d], gc_sem.at[1, d],
            spot.core_mate(),
        )

    small_x_copy.wait()
    small_all[z] = small_x[1] + small_x[2]

    def receive(step, d):
        pass_w(step, d).wait_recv()
        across(d).start()

    across(z).start()
    lax.fori_loop(
        0, lines, line_relay(spot, lambda s, d: pass_w(s, d).start(), receive), 0
    )
    lax.fori_loop(
        0,
        lines,
        line_relay(
            spot, lambda s, d: pass_s(s, d).start(), lambda s, d: pass_s(s, d).wait_recv()
        ),
        0,
    )

    def add_small(d, total):
        return total + small_all[d]

    total_ref[...] = lax.fori_loop(1, lines, add_small, small_all[0])
    ffn_copy.wait()

    def last(j, unused):
        at = pl.ds(pl.multiple_of(j * step, step), step)
        here = pl.ds(pl.multiple_of(wa * half + j * step, step), step)
        total = hidden_ref[at, :] + ffn_ref[here, :].astype(f32) + ffn_in[at, :].astype(f32)
        out_ref[at, :] = total.astype(bf16)
        return unused

    lax.fori_loop(0, half // step, last, 0)

    def spread(d, unused):
        across(d).wait()
        beside(d).start()
        return unused

    lax.fori_loop(0, lines, spread, 0)

    def copy_out(d, unused):
        beside(d).wait()
        weights_ref[d] = all_w[d]
        return unused

    lax.fori_loop(0, lines, copy_out, 0)

    def drain(d, unused):
        @pl.when((z < d))
        def _():
            flow(1, d).wait_send()

        @pl.when((z > d))
        def _():
            flow(-1, d).wait_send()

        @pl.when((d <= z) & (z + 1 < lines))
        def _():
            pass_w(1, d).wait_send()
            pass_s(1, d).wait_send()

        @pl.when((d >= z) & (z > 0))
        def _():
            pass_w(-1, d).wait_send()
            pass_s(-1, d).wait_send()

        return unused

    lax.fori_loop(0, lines, drain, 0)


def finish(plan, cycle_size, *operands):
    lines = cycle_size // 4
    half, model = operands[11].shape
    rows = 4 * plan.cols // cycle_size
    dma = pltpu.SemaphoreType.DMA
    return pl.pallas_call(
        functools.partial(finish_kernel, plan, lines),
        out_shape=[
            jax.ShapeDtypeStruct((half, model), bf16),
            jax.ShapeDtypeStruct((half, model), f32),
            jax.ShapeDtypeStruct((8, half), f32),
            jax.ShapeDtypeStruct((lines, 2, 2, rows, model), bf16),
            jax.ShapeDtypeStruct((8, model), f32),
        ],
        in_specs=[vmem] * 4
        + [pl.BlockSpec(memory_space=pl.ANY)] * 3
        + [vmem] * (len(operands) - 7),
        out_specs=[vmem] * 5,
        scratch_shapes=[
            pltpu.VMEM((3 * WIDE, model), bf16),
            dma((3,)),
            pltpu.VMEM((4, 2 * half, WIDE), bf16),
            pltpu.VMEM((2, 2 * half, model), bf16),
            pltpu.VMEM((WIDE, model), bf16),
            pltpu.VMEM((lines, 2, 2, rows, model), bf16),
            pltpu.VMEM((lines, 2, rows, model), bf16),
            pltpu.VMEM((lines, rows, model), bf16),
            pltpu.VMEM((lines, rows, model), bf16),
            pltpu.VMEM((lines, rows, model), bf16),
            pltpu.VMEM((lines, 2, 2, rows, model), bf16),
            pltpu.VMEM((2, half // 2, model), bf16),
            pltpu.VMEM((2, half // 2, model), bf16),
            pltpu.VMEM((half, model), f32),
            pltpu.VMEM((half, model), bf16),
            pltpu.VMEM((8, half), f32),
            pltpu.VMEM((8, model), f32),
            pltpu.VMEM((8, model), f32),
            pltpu.VMEM((8, model), f32),
            pltpu.VMEM((3, 8, model), f32),
            pltpu.VMEM((lines, 8, model), f32),
            dma((2, 5)),
            dma((2, 5)),
            dma((2, lines + 1)),
            dma((2, lines)),
            dma((2, lines)),
            dma((4, lines)),
            dma((2, lines)),
            dma((2, lines)),
            dma((4, lines)),
        ],
        compiler_params=pltpu.CompilerParams(
            vmem_limit_bytes=58 * 2**20, collective_id=2, has_side_effects=True
        ),
        name="finish",
    )(*operands)


root = 0.7978845608028654
cubic = 0.044715


def middle_kernel(
    plan, cycle_size, att_ref, mixed_ref, tokens_ref, cot_ref, gain_ref,
    wo_hbm, wo_far_hbm, wg_hbm, wu_hbm, wd_hbm,
    hidden_ref, gh_ref, branch_ref, ffn_ref, do_ref, gain_part_ref, *refs,
):
    stacks, refs = (refs[:3], refs[3:])
    (
        wg, wu, wd, wo, inner, gg, gu, x_ref, att_in, d_out, d_in, e_out, e_in,
        acc_f, acc_g, rows_buf, load_sem, y_sem, out_sem,
    ) = refs
    spot = Spot(cycle_size // 4)
    wa = spot.wa
    pair, model = tokens_ref.shape
    half = pair // 2
    units = wd.shape[1]
    chunk = half // 4
    block = pair // 4
    loads = [
        pltpu.make_async_copy(src, dst, load_sem.at[i])
        for i, (src, dst) in enumerate(
            (
                (wo_hbm, wo.at[0, 64:]),
                (wo_far_hbm, wo.at[1, 64:]),
                (wg_hbm, wg),
                (wu_hbm, wu),
                (wd_hbm, wd),
            )
        )
    ]
    for load in loads:
        load.start()
    barrier = pltpu.get_barrier_semaphore()
    pl.semaphore_signal(
        barrier, inc=1, device_id=spot.y_mate(), device_id_type=pl.DeviceIdType.MESH
    )
    wo[:, :64, :] = jnp.zeros((2, 64, model), bf16)
    pl.semaphore_wait(barrier, 1)
    ours = wa * half
    theirs = (1 - wa) * half

    def rows_at(start, size):
        return pl.ds(pl.multiple_of(start, size), size)

    def a_start(i):
        return (theirs + i * block) if i < 2 else (ours + (i - 2) * block)

    def a_copy(i, base):
        at = rows_at(base + (i % 2) * block, block)
        return send(att_ref.at[at], att_in.at[at], y_sem.at[0, i], y_sem.at[1, i], spot.y_mate())

    order = (0, 1, 2, 3)
    for i in order:
        a_copy(i, ours if i < 2 else theirs).start()
    loads[0].wait()
    loads[1].wait()

    def normal(i, base, keep):
        a_copy(i, base).wait_recv()
        at = rows_at(base + (i % 2) * block, block)
        branch = nn(att_ref[at, :], wo[0]) + nn(att_in[at, :], wo[1])
        hidden = tokens_ref[at, :].astype(f32) + branch
        if keep:
            hidden_ref[(i % 2) * block : (i % 2 + 1) * block, :] = hidden
        inv = lax.rsqrt(jnp.mean(hidden * hidden, axis=-1, keepdims=True) + eps)
        x_ref[at, :] = (hidden * inv * gain_ref[...]).astype(bf16)

    normal(0, theirs, False)
    normal(1, theirs, False)
    for load in loads[2:]:
        load.wait()
    wide = 256

    def feed(base):
        rows = rows_at(base, half)
        acc_f[...] = jnp.zeros_like(acc_f)
        acc_g[...] = jnp.zeros_like(acc_g)

        def tile(u, unused):
            cols = rows_at(u * wide, wide)
            gate = nn(x_ref[rows, :], wg[:, cols])
            upward = nn(x_ref[rows, :], wu[:, cols])
            grad_inner = nn(cot_ref[rows, :], wd[:, cols])
            square = gate * gate
            bend = jnp.tanh(root * gate * (1.0 + cubic * square))
            side = 0.5 * (1.0 + bend)
            gelu = gate * side
            slope = side + 0.5 * gate * (1.0 - bend * bend) * (
                root * (1.0 + 3.0 * cubic * square)
            )
            inner_low = (gelu * upward).astype(bf16)
            gate_low = (grad_inner * upward * slope).astype(bf16)
            up_low = (grad_inner * gelu).astype(bf16)
            inner[rows, cols] = inner_low
            gg[rows, cols] = gate_low
            gu[rows, cols] = up_low
            acc_g[...] += nt(gate_low, wg[:, cols]) + nt(up_low, wu[:, cols])
            acc_f[...] += nt(inner_low, wd[:, cols])
            return unused

        lax.fori_loop(0, units // wide, tile, 0)
        ffn_ref[rows, :] = acc_f[...].astype(bf16)

    def d_copy(i):
        return send(
            d_out.at[i], d_in.at[i], y_sem.at[0, 4 + i], y_sem.at[1, 4 + i], spot.y_mate()
        )

    def send_grad(i, unused):
        d_out[i] = acc_g[rows_at(i * chunk, chunk), :].astype(bf16)
        d_copy(i).start()
        return unused

    def half_pass(k, unused):
        base = theirs + k * (ours - theirs)
        feed(base)

        @pl.when(k == 0)
        def _():
            lax.fori_loop(0, 4, send_grad, 0)
            normal(2, ours, True)
            normal(3, ours, True)

        return unused

    lax.fori_loop(0, 2, half_pass, 0)
    count = units // wide

    def out_copy(m, u):
        return pltpu.make_async_copy(
            rows_buf.at[m, u % 2],
            stacks[m].at[rows_at(u * wide, wide)],
            out_sem.at[m, u % 2],
        )

    for m in range(3):
        left = (inner, gg, gu)[m]
        right = (cot_ref, x_ref, x_ref)[m]

        def weight_rows(u, unused, m=m, left=left, right=right):
            @pl.when(u >= 2)
            def _():
                out_copy(m, u - 2).wait()

            turned = jnp.transpose(left[:, rows_at(u * wide, wide)])
            rows_buf[m, u % 2] = nn(turned, right[...]).astype(bf16)
            out_copy(m, u).start()
            return unused

        lax.fori_loop(0, count, weight_rows, 0)

    def e_copy(i):
        return send(
            e_out.at[i], e_in.at[i], y_sem.at[0, 8 + i], y_sem.at[1, 8 + i], spot.y_mate()
        )

    def normal_back(i, total):
        d_copy(i).wait()
        at = rows_at(i * chunk, chunk)
        grad = acc_g[at, :] + d_in[i].astype(f32)
        hidden = hidden_ref[at, :]
        inv = lax.rsqrt(jnp.mean(hidden * hidden, axis=-1, keepdims=True) + eps)
        scaled = gain_ref[...] * grad
        mean = jnp.mean(hidden * scaled, axis=-1, keepdims=True)
        grad_hidden = (
            cot_ref[rows_at(ours + i * chunk, chunk), :].astype(f32)
            + inv * scaled
            - hidden * (inv * inv * inv * mean)
        )
        gh_ref[at, :] = grad_hidden
        low = grad_hidden.astype(bf16)
        branch_ref[at, :] = low
        e_out[i] = nt(low, wo[1]).astype(bf16)
        e_copy(i).start()
        do_ref[rows_at(ours + i * chunk, chunk), :] = nt(low, wo[0]).astype(bf16)
        return total + jnp.sum(grad * hidden * inv, axis=0, keepdims=True)

    gain_part_ref[...] = lax.fori_loop(0, 4, normal_back, jnp.zeros((1, model), f32))

    def row_terms(at, grad):
        lane = lanes_of(chunk)
        terms = grad.astype(f32) * mixed_ref[at, :]
        out = grad
        for h in range(plan.heads):
            row_term = jnp.sum(
                jnp.where(lane // 64 == h + 1, terms, 0.0), axis=1, keepdims=True
            )
            for i, part in enumerate(split3(-row_term)):
                out = jnp.where(lane == 3 * h + i, part, out)
        do_ref[at, :] = out

    def own_terms(i, unused):
        at = rows_at(ours + i * chunk, chunk)
        row_terms(at, do_ref[at, :])
        return unused

    lax.fori_loop(0, 4, own_terms, 0)

    def far_terms(i, unused):
        e_copy(i).wait()
        row_terms(rows_at(theirs + i * chunk, chunk), e_in[i])
        return unused

    lax.fori_loop(0, 4, far_terms, 0)
    for m in range(3):
        for u in range(max(0, count - 2), count):
            out_copy(m, u).wait()
    for i in order:
        a_copy(i, ours if i < 2 else theirs).wait_send()


def middle(
    plan, cycle_size, attended, mixed, tokens, cot, gain, w_out, w_out_far, w_gate, w_up, w_down
):
    pair, model = tokens.shape
    half = pair // 2
    units = w_down.shape[0]
    chunk = half // 4
    hbm = pl.BlockSpec(memory_space=pl.ANY)
    dma = pltpu.SemaphoreType.DMA
    return pl.pallas_call(
        functools.partial(middle_kernel, plan, cycle_size),
        out_shape=[
            jax.ShapeDtypeStruct((half, model), f32),
            jax.ShapeDtypeStruct((half, model), f32),
            jax.ShapeDtypeStruct((half, model), bf16),
            jax.ShapeDtypeStruct((pair, model), bf16),
            jax.ShapeDtypeStruct((pair, WIDE), bf16),
            jax.ShapeDtypeStruct((1, model), f32),
        ]
        + [jax.ShapeDtypeStruct((units, model), bf16)] * 3,
        in_specs=[vmem] * 5 + [hbm] * 5,
        out_specs=[vmem] * 6 + [hbm] * 3,
        scratch_shapes=[
            pltpu.VMEM((model, units), bf16),
            pltpu.VMEM((model, units), bf16),
            pltpu.VMEM((model, units), bf16),
            pltpu.VMEM((2, WIDE, model), bf16),
            pltpu.VMEM((pair, units), bf16),
            pltpu.VMEM((pair, units), bf16),
            pltpu.VMEM((pair, units), bf16),
            pltpu.VMEM((pair, model), bf16),
            pltpu.VMEM((pair, WIDE), bf16),
            pltpu.VMEM((4, chunk, model), bf16),
            pltpu.VMEM((4, chunk, model), bf16),
            pltpu.VMEM((4, chunk, WIDE), bf16),
            pltpu.VMEM((4, chunk, WIDE), bf16),
            pltpu.VMEM((half, model), f32),
            pltpu.VMEM((half, model), f32),
            pltpu.VMEM((3, 2, WIDE, model), bf16),
            dma((5,)),
            dma((2, 12)),
            dma((3, 2)),
        ],
        compiler_params=pltpu.CompilerParams(
            vmem_limit_bytes=60 * 2**20, collective_id=3, has_side_effects=True
        ),
        name="feed_forward",
    )(attended, mixed, tokens, cot, gain, w_out, w_out_far, w_gate, w_up, w_down.T)


def shards(
    tokens,
    doc_lengths,
    key_mask,
    gain_attn,
    w_query,
    w_key,
    w_value,
    w_out,
    bias_table,
    gain_ffn,
    w_gate,
    w_up,
    w_down,
    cotangent,
):
    own_rows, model = tokens.shape
    group = lax.axis_size("wa")
    cycle_size = lax.axis_size("ctx")
    pair = own_rows * group
    heads = bias_table.shape[1]
    docs = doc_lengths.shape[0]
    plan = Plan(heads, w_query.shape[1] // heads, docs)
    total_rows = pair * cycle_size
    doc_most = min(MAXLEN, total_rows // 2)
    reach = min(cycle_size - 1, (doc_most - 1) // pair + 1)
    base = lax.axis_index("ctx") * pair
    rows = min(total_rows, (2 * reach + 1) * pair)
    origin = jnp.clip(base - reach * pair, 0, total_rows - rows).astype(jnp.int32)
    ends = jnp.cumsum(doc_lengths).astype(jnp.int32)
    starts = ends - doc_lengths

    def doc_at(positions):
        return jnp.sum((positions[:, None] >= starts[None, :]).astype(jnp.int32), axis=1) - 1

    tiles = pair // TQ
    tile_start = base + TQ * jnp.arange(tiles, dtype=jnp.int32)
    first_doc = jnp.arange(docs, dtype=jnp.int32)[None, :] == doc_at(tile_start)[:, None]
    last_doc = jnp.arange(docs, dtype=jnp.int32)[None, :] == doc_at(tile_start + TQ - 1)[:, None]
    low_end = jnp.sum(jnp.where(first_doc, starts[None, :], 0), axis=1)
    high_end = jnp.sum(jnp.where(last_doc, ends[None, :], 0), axis=1)
    n_left = jnp.maximum(0, (tile_start - EDGE - low_end + TK - 1) // TK)
    n_right = jnp.maximum(0, (high_end - (tile_start - EDGE + TK) + TK - 1) // TK)
    bounds = jnp.concatenate(
        [(base - origin)[None], jnp.stack([n_left, n_right], axis=1).reshape(-1)]
    ).astype(jnp.int32)

    def window(gathered):
        if rows == total_rows:
            return gathered
        return lax.dynamic_slice_in_dim(gathered, origin, rows, 0)

    gather = functools.partial(lax.all_gather, axis_name="ctx", axis=0, tiled=True)
    (
        pair_normed, pair_tokens, q_wide, own_kv, k_aug, own_aug, near_bias, masks, far_out, kv_all,
    ) = first(
        plan,
        cycle_size,
        reach,
        rows,
        starts,
        bias_table,
        tokens,
        gain_attn[None],
        jnp.broadcast_to(key_mask.astype(f32)[None], (8, pair)),
        w_query,
        w_key,
        w_value,
        w_out,
    )
    masks = masks.reshape(cycle_size, 8, pair)
    cot_late, near_bias = lax.optimization_barrier((cotangent, near_bias))
    pair_cot = lax.all_gather(cot_late, "wa", axis=0, tiled=True)
    if rows < total_rows:
        masks = lax.dynamic_slice_in_dim(masks, origin // pair, rows // pair, 0)
    kv_all = window(kv_all.reshape(total_rows, 2 * plan.cols))
    padded = rows + 2 * PAD
    attended, mixed, q_back = pl.pallas_call(
        functools.partial(fwd_kernel, plan, rows, pair),
        out_shape=(
            jax.ShapeDtypeStruct((pair, WIDE), bf16),
            jax.ShapeDtypeStruct((pair, WIDE), f32),
            jax.ShapeDtypeStruct((pair, WIDE), bf16),
        ),
        in_specs=[smem, smem] + [vmem] * 5,
        out_specs=(vmem, vmem, vmem),
        scratch_shapes=[
            pltpu.VMEM((padded, WIDE), bf16),
            pltpu.VMEM((padded, WIDE), bf16),
            pltpu.VMEM((8, padded), f32),
            pltpu.VMEM((heads, TQ, WIDE), f32),
            pltpu.VMEM((heads, TQ, 128), f32),
            pltpu.VMEM((heads, TQ, WIDE), bf16),
        ],
        compiler_params=params(),
        name="attention_forward",
    )(bounds, bias_table, kv_all, k_aug, masks, q_wide, near_bias)
    q_all = window(gather(q_back))
    swap = functools.partial(lax.ppermute, axis_name="wa", perm=((0, 1), (1, 0)))
    hidden, grad_hidden, branch, ffn_part, do_wide, gain_ffn_part, *stacks = middle(
        plan,
        cycle_size,
        attended,
        mixed,
        pair_tokens,
        pair_cot,
        gain_ffn[None],
        w_out,
        far_out,
        w_gate,
        w_up,
        w_down,
    )
    far_branch = swap(branch)
    do_all = window(gather(do_wide))
    grad_w_down, grad_w_gate, grad_w_up = reduce_scatter(stacks, cycle_size)
    grad_w_gate, grad_w_up = (grad_w_gate.T, grad_w_up.T)

    grad_queries, table_part = pl.pallas_call(
        functools.partial(dq_kernel, plan, rows, pair),
        out_shape=(
            jax.ShapeDtypeStruct((pair, WIDE), bf16),
            jax.ShapeDtypeStruct((heads, 32, 128), f32),
        ),
        in_specs=[smem, smem] + [vmem] * 6,
        out_specs=(vmem, vmem),
        scratch_shapes=[
            pltpu.VMEM((padded, WIDE), bf16),
            pltpu.VMEM((padded, WIDE), bf16),
            pltpu.VMEM((8, padded), f32),
            pltpu.VMEM((heads, TQ, WIDE), f32),
            pltpu.VMEM((heads, TQ, WIDE), bf16),
            pltpu.VMEM((heads, TQ, WIDE), bf16),
            pltpu.VMEM((heads, TQ, TK), f32),
            pltpu.VMEM((2, heads, TQ, 128), f32),
        ],
        compiler_params=params(),
        name="attention_grad_queries",
    )(bounds, bias_table, kv_all, k_aug, masks, q_back, do_wide, near_bias)
    grad_keys, grad_values, mask_part = pl.pallas_call(
        functools.partial(dkv_kernel, plan, rows, pair),
        out_shape=(
            jax.ShapeDtypeStruct((pair, WIDE), bf16),
            jax.ShapeDtypeStruct((pair, WIDE), bf16),
            jax.ShapeDtypeStruct((tiles, 8, TQ), f32),
        ),
        in_specs=[smem, smem, vmem, vmem, vmem, vmem, vmem],
        out_specs=(vmem, vmem, vmem),
        scratch_shapes=[
            pltpu.VMEM((padded, WIDE), bf16),
            pltpu.VMEM((padded, WIDE), bf16),
            pltpu.VMEM((heads, TQ, WIDE), bf16),
            pltpu.VMEM((heads, TQ, WIDE), bf16),
            pltpu.VMEM((heads, TQ, WIDE), f32),
            pltpu.VMEM((heads, TQ, WIDE), f32),
        ],
        compiler_params=params(),
        name="attention_grad_keys",
    )(bounds, bias_table, q_all, do_all, own_kv, own_aug, near_bias)
    cols = plan.cols
    table_row = jnp.sum(table_part, axis=2).reshape(1, -1)
    table_row = jnp.pad(table_row, ((0, 0), (0, model - table_row.shape[1])))
    small = jnp.concatenate(
        [jnp.zeros((1, model), f32), gain_ffn_part, table_row, jnp.zeros((5, model), f32)],
        axis=0,
    )
    layer_out, grad_tokens, grad_mask, weights, totals = finish(
        plan,
        cycle_size,
        grad_queries,
        grad_keys,
        grad_values,
        mask_part.reshape(group, 8, own_rows),
        w_query.T,
        w_key.T,
        w_value.T,
        pair_normed,
        attended,
        branch,
        far_branch,
        tokens,
        gain_attn[None],
        hidden,
        grad_hidden,
        ffn_part,
        small,
    )
    weights = weights.reshape(4, cols, model).astype(f32)
    return (
        layer_out,
        grad_tokens,
        grad_mask[0],
        totals[0],
        weights[0].T,
        weights[1].T,
        weights[2].T,
        weights[3],
        totals[2, : heads * 32].reshape(heads, 32).T,
        totals[1],
        grad_w_gate,
        grad_w_up,
        grad_w_down,
    )


def solution(mesh):
    placed = (
        P(("ctx", "wa"), None),
        P(),
        P("ctx"),
        P(),
        P(None, "wa"),
        P(None, "wa"),
        P(None, "wa"),
        P("wa", None),
        P(None, "wa"),
        P(),
        P(None, "wa"),
        P(None, "wa"),
        P("wa", None),
        P(("ctx", "wa"), None),
    )
    return jax.shard_map(
        shards,
        mesh=mesh,
        in_specs=placed,
        out_specs=(
            P(("ctx", "wa"), None),
            P(("ctx", "wa"), None),
            P(("ctx", "wa")),
            P(),
            P(None, "wa"),
            P(None, "wa"),
            P(None, "wa"),
            P("wa", None),
            P(None, "wa"),
            P(),
            P(None, ("wa", "ctx")),
            P(None, ("wa", "ctx")),
            P(("wa", "ctx"), None),
        ),
        check_vma=False,
    )
```

```python
import functools

import jax
import jax.numpy as jnp
from jax import lax
from jax.experimental import pallas as pl
from jax.experimental.pallas import tpu as pltpu
from jax.sharding import PartitionSpec as P

MAXLEN = 8192

bucket_edges = (12, 16, 23, 32, 46, 64, 91)
neg_big = -1e30
eps = 1e-06
far_left_bucket = 15
far_right_bucket = 31
WIDE = 256
TQ = 256
TK = 512
EDGE = 128
PAD = TK + EDGE
f32 = jnp.float32
bf16 = jnp.bfloat16


def bucket_of(relative):
    distance = jnp.abs(relative)
    bucket = jnp.minimum(distance, 8) + 16 * (relative > 0).astype(jnp.int32)
    for edge in bucket_edges:
        bucket = bucket + (distance >= edge).astype(jnp.int32)
    return bucket


def norm_forward(inputs, gain):
    inv_root = lax.rsqrt(jnp.mean(inputs * inputs, axis=-1, keepdims=True) + eps)
    return (inputs * inv_root * gain, inv_root)


def norm_backward(inputs, inv_root, gain, grad_normed):
    scaled = gain * grad_normed
    cubed = inv_root * inv_root * inv_root
    grad_inputs = inv_root * scaled - inputs * cubed * jnp.mean(
        inputs * scaled, axis=-1, keepdims=True
    )
    grad_gain = jnp.sum(grad_normed * inputs * inv_root, axis=0)
    return (grad_inputs, grad_gain)


def gated(gate, upward):
    return jax.nn.gelu(gate, approximate=True) * upward


def nt(a, b):
    return lax.dot_general(a, b, (((1,), (1,)), ((), ())), preferred_element_type=f32)


def nn(a, b):
    return lax.dot_general(a, b, (((1,), (0,)), ((), ())), preferred_element_type=f32)


def split3(x):
    hi = x.astype(bf16)
    rest = x - hi.astype(f32)
    mid = rest.astype(bf16)
    return (hi, mid, (rest - mid.astype(f32)).astype(bf16))


class Plan:
    def __init__(self, heads, width, docs):
        self.heads = heads
        self.width = width
        self.bits = max(1, (docs - 1).bit_length())
        self.cols = heads * width
        self.mask_lane = self.cols
        self.doc_lane = self.cols + 1
        self.stat_lane = self.doc_lane + 2 * self.bits
        assert self.stat_lane + 3 * heads <= WIDE and self.cols + 64 == WIDE and width == 64

    def key_lanes(self, lane, h):
        own = (lane >= h * self.width) & (lane < (h + 1) * self.width)
        aug = (lane >= self.mask_lane) & (lane < self.stat_lane)
        stat = (lane >= self.stat_lane + 3 * h) & (lane < self.stat_lane + 3 * h + 3)
        return own | aug | stat

    def value_lanes(self, lane, h):
        own = (lane >= 64 + h * self.width) & (lane < 64 + (h + 1) * self.width)
        return own | ((lane >= 3 * h) & (lane < 3 * h + 3))


def lanes_of(rows, width=WIDE):
    return lax.broadcasted_iota(jnp.int32, (rows, width), 1)


def near_lanes(heads, table_ref, near_ref):
    row = lax.broadcasted_iota(jnp.int32, (EDGE, 3 * EDGE), 0)
    col = lax.broadcasted_iota(jnp.int32, (EDGE, 3 * EDGE), 1)
    relative = col - EDGE - row
    for flip in range(2):
        bucket = bucket_of(-relative if flip else relative)
        left, right = (far_left_bucket, far_right_bucket)
        if flip:
            left, right = (right, left)
        for h in range(heads):
            base = jnp.full((EDGE, 3 * EDGE), table_ref[0, h], f32)
            for b in range(1, 32):
                base = jnp.where(bucket == b, table_ref[b, h], base)
            far_l = jnp.full((EDGE, EDGE), table_ref[left, h], f32)
            far_r = jnp.full((EDGE, EDGE), table_ref[right, h], f32)
            near_ref[flip, h, :EDGE, : 3 * EDGE] = base
            near_ref[flip, h, :EDGE, 3 * EDGE :] = far_r
            near_ref[flip, h, EDGE:, EDGE:] = base
            near_ref[flip, h, EDGE:, :EDGE] = far_l


def build_keys(plan, g_ref, kaug_ref, masks_ref, km, vm, mask_row, rows):
    mask_row[...] = jnp.zeros_like(mask_row)
    size = masks_ref.shape[2]
    for n in range(masks_ref.shape[0]):
        mask_row[:, PAD + n * size : PAD + (n + 1) * size] = masks_ref[n]
    km[:PAD, :] = jnp.broadcast_to(
        jnp.where(pad_lanes(plan), neg_big, 0.0).astype(bf16), (PAD, WIDE)
    )
    km[pl.ds(PAD + rows, PAD), :] = km[:PAD, :]
    vm[:PAD, :] = jnp.zeros((PAD, WIDE), bf16)
    vm[pl.ds(PAD + rows, PAD), :] = jnp.zeros((PAD, WIDE), bf16)
    step = 512
    low = lanes_of(step, 128) < 64
    ones = (lanes_of(step, 128) < 3 * plan.heads).astype(bf16)

    def body(n, unused):
        at = pl.multiple_of(n * step, step)
        to = pl.multiple_of(PAD + n * step, 128)
        middle = g_ref[pl.ds(at, step), 128:256]
        km[pl.ds(to, step), 0:128] = g_ref[pl.ds(at, step), 0:128]
        km[pl.ds(to, step), 128:256] = jnp.where(low, middle, kaug_ref[pl.ds(at, step), :])
        vm[pl.ds(to, step), 0:128] = jnp.where(low, ones, middle)
        vm[pl.ds(to, step), 128:256] = g_ref[pl.ds(at, step), 256:384]
        return unused

    lax.fori_loop(0, rows // step, body, 0)


def far_span(start, n, n_left, left_bucket, right_bucket):
    on_left = n < n_left
    at = start + PAD - EDGE + TK * jnp.where(on_left, -1 - n, 1 + n - n_left)
    bucket = jnp.where(on_left, left_bucket, right_bucket)
    return pl.ds(pl.multiple_of(at, 128), TK), bucket


def pad_lanes(plan):
    lane = lanes_of(1)
    return (lane >= plan.doc_lane) & (lane < plan.stat_lane)


def fwd_kernel(
    plan, rows, pair, bounds, table_ref, g_ref, kaug_ref, masks_ref, q_ref, near_ref,
    low_ref, wide_ref, qb_ref, km, vm, mask_row, acc, row_max, qh_ref,
):
    build_keys(plan, g_ref, kaug_ref, masks_ref, km, vm, mask_row, rows)
    lane = lanes_of(TQ)

    def tile(t, unused):
        start = pl.multiple_of(bounds[0] + t * TQ, 128)
        n_left, n_right = (bounds[1 + 2 * t], bounds[2 + 2 * t])
        out = pl.ds(pl.multiple_of(t * TQ, TQ), TQ)
        q = q_ref[out, :]
        near = pl.ds(pl.multiple_of(start + PAD - EDGE, 128), TK)
        for h in range(plan.heads):
            qh = jnp.where(plan.key_lanes(lane, h), q, jnp.zeros_like(q))
            qh_ref[h] = qh
            s = nt(qh, km[near, :]) + near_ref[0, h] + mask_row[0:1, near]
            top = jnp.max(s, axis=1, keepdims=True)
            p = jnp.exp(s - top).astype(bf16)
            acc[h] = nn(p, vm[near, :])
            row_max[h] = jnp.broadcast_to(top, (TQ, 128))

        def far(n, unused):
            span, bucket = far_span(start, n, n_left, far_left_bucket, far_right_bucket)
            if True:
                for h in range(plan.heads):
                    s = nt(qh_ref[h], km[span, :]) + mask_row[0:1, span]
                    offset = table_ref[bucket, h]
                    old = row_max[h][:, :1]
                    top = jnp.maximum(old, jnp.max(s, axis=1, keepdims=True) + offset)
                    p = jnp.exp(s - (top - offset)).astype(bf16)
                    acc[h] = acc[h] * jnp.exp(old - top) + nn(p, vm[span, :])
                    row_max[h] = jnp.broadcast_to(top, (TQ, 128))
            return unused

        lax.fori_loop(0, n_left + n_right, far, 0)

        wide = jnp.zeros((TQ, WIDE), f32)
        qb = jnp.where(lane < plan.stat_lane, q, jnp.zeros_like(q))
        for h in range(plan.heads):
            total = acc[h][:, 3 * h : 3 * h + 1]
            log_total = row_max[h][:, :1] + jnp.log(total)
            wide = jnp.where(lane // 64 == h + 1, acc[h] / total, wide)
            for i, part in enumerate(split3(-log_total)):
                qb = jnp.where(lane == plan.stat_lane + 3 * h + i, part, qb)
        wide_ref[out, :] = wide
        low_ref[out, :] = wide.astype(bf16)
        qb_ref[out, :] = qb
        return unused

    lax.fori_loop(0, pair // TQ, tile, 0)


vmem = pl.BlockSpec(memory_space=pltpu.VMEM)
smem = pl.BlockSpec(memory_space=pltpu.SMEM)


def params():
    return pltpu.CompilerParams(vmem_limit_bytes=56 * 2**20)


class Spot:
    def __init__(self, lines):
        index = lax.axis_index("ctx")
        self.wa = lax.axis_index("wa")
        self.index = index
        self.lines = lines
        self.z = index // 4
        self.x = (index // 2) % 2
        self.core = index % 2

    def core_mate(self):
        return (self.index + 1 - 2 * self.core, self.wa)

    def x_mate(self):
        return (self.index + 2 - 4 * self.x, self.wa)

    def z_mate(self, step):
        return (jnp.clip(self.index + 4 * step, 0, 4 * self.lines - 1), self.wa)

    def y_mate(self):
        return (self.index, 1 - self.wa)


def send(src, dst, send_sem, recv_sem, device):
    return pltpu.make_async_remote_copy(
        src_ref=src,
        dst_ref=dst,
        send_sem=send_sem,
        recv_sem=recv_sem,
        device_id=device,
        device_id_type=pl.DeviceIdType.MESH,
    )


def greet(spot, with_y):
    barrier = pltpu.get_barrier_semaphore()
    mates = [spot.core_mate(), spot.x_mate()] + ([spot.y_mate()] if with_y else [])
    for mate in mates:
        pl.semaphore_signal(barrier, inc=1, device_id=mate, device_id_type=pl.DeviceIdType.MESH)

    @pl.when(spot.z + 1 < spot.lines)
    def _():
        pl.semaphore_signal(
            barrier, inc=1, device_id=spot.z_mate(1), device_id_type=pl.DeviceIdType.MESH
        )

    @pl.when(spot.z > 0)
    def _():
        pl.semaphore_signal(
            barrier, inc=1, device_id=spot.z_mate(-1), device_id_type=pl.DeviceIdType.MESH
        )

    above = (spot.z + 1 < spot.lines).astype(jnp.int32)
    below = (spot.z > 0).astype(jnp.int32)
    pl.semaphore_wait(barrier, len(mates) + above + below)


def added(a, b):
    return a + b


def first_kernel(
    plan, lines, span, reach, rows, starts, table_ref, tokens_ref, gain_ref, mask_ref,
    wq_hbm, wk_hbm, wv_hbm, wo_hbm,
    x_ref, tok_ref, q_ref, own_ref, aug_ref, own_aug_ref, near_ref, masks_ref, wo_far_hbm, all_hbm,
    weights, zeros, load_sem, y_sem, own_sem, zero_sem, z_sem, x_sem, c_sem,
):
    spot = Spot(lines)
    z, x, core, wa = (spot.z, spot.x, spot.core, spot.wa)
    half, model = tokens_ref.shape
    cols = plan.cols
    chunk = half // 4
    loads = [
        pltpu.make_async_copy(src, weights.at[pl.ds(i * cols, cols)], load_sem.at[i])
        for i, src in enumerate((wk_hbm, wv_hbm, wq_hbm))
    ]
    for load in loads:
        load.start()
    greet(spot, True)
    zeros[...] = jnp.zeros_like(zeros)

    def outside(d):
        return (d < z - span) | (d > z + span)

    def zero_copies(d):
        return [
            pltpu.make_async_copy(zeros, all_hbm.at[d, a, b], zero_sem.at[d, a, b])
            for a in range(2)
            for b in range(2)
        ]

    def zero_start(d, unused):
        @pl.when(outside(d))
        def _():
            masks_ref[d] = jnp.zeros((2, 2) + mask_ref.shape, f32)
            for copy in zero_copies(d):
                copy.start()

        return unused

    def rows_at(start, size):
        return pl.ds(pl.multiple_of(start, size), size)

    ours = wa * half
    theirs = (1 - wa) * half

    def y_copy(i, base):
        return send(
            tokens_ref.at[rows_at(i * chunk, chunk)],
            tok_ref.at[rows_at(base + i * chunk, chunk)],
            y_sem.at[0, i],
            y_sem.at[1, i],
            spot.y_mate(),
        )

    def y_start(i, unused):
        y_copy(i, ours).start()
        return unused

    lax.fori_loop(0, 4, y_start, 0)
    far_copy = send(wo_hbm, wo_far_hbm, y_sem.at[0, 4], y_sem.at[1, 4], spot.y_mate())

    def scaled(rows_in):
        rows_in = rows_in.astype(f32)
        inv = lax.rsqrt(jnp.mean(rows_in * rows_in, axis=-1, keepdims=True) + eps)
        return (rows_in * inv * gain_ref[...]).astype(bf16)

    def normal(i, unused):
        at = rows_at(ours + i * chunk, chunk)
        rows_in = tokens_ref[rows_at(i * chunk, chunk), :]
        tok_ref[at, :] = rows_in
        x_ref[at, :] = scaled(rows_in)
        return unused

    lax.fori_loop(0, 4, normal, 0)
    for load in loads:
        load.wait()

    def project(base):
        rows = rows_at(base, half)
        qkv = nt(x_ref[rows, :], weights[...]).astype(bf16)
        own_ref[rows, :] = qkv[:, : 2 * cols]
        q_ref[rows, :cols] = qkv[:, 2 * cols :]

    pieces = [
        (ours, half, True),
        (theirs, half // 2, True),
        (theirs + half // 2, half // 2, False),
        None,
    ]
    mask_piece = 3

    def line_first(p):
        return p == mask_piece or pieces[p][2]

    def piece_rows(p):
        return rows_at(pieces[p][0], pieces[p][1])

    def source(p, d, a):
        if p == mask_piece:
            return masks_ref.at[d, a, core]
        return all_hbm.at[d, a, core, piece_rows(p)]

    def own_source(p):
        return mask_ref if p == mask_piece else own_ref.at[piece_rows(p)]

    def pass_copy(p, step, d, own):
        i = 0 if step > 0 else 1
        if line_first(p):
            dst = source(p, d, x)
            src = own_source(p) if own else dst
        else:
            dst = all_hbm.at[d, :, core, piece_rows(p)]
            src = dst
        return send(src, dst, z_sem.at[p, i, d], z_sem.at[p, 2 + i, d], spot.z_mate(step))

    def across(p, d, own):
        dst = source(p, d, x)
        src = own_source(p) if own else dst
        return send(src, dst, x_sem.at[p, 0, d], x_sem.at[p, 1, d], spot.x_mate())

    def beside(p, d):
        if p == mask_piece:
            part = masks_ref.at[d, :, core]
        else:
            part = all_hbm.at[d, :, core, piece_rows(p)]
        return send(part, part, c_sem.at[p, 0, d], c_sem.at[p, 1, d], spot.core_mate())

    def own_copy(p):
        return pltpu.make_async_copy(
            own_source(p), source(p, z, x), own_sem.at[p]
        )

    def both_ways(p, own):
        @pl.when(z + 1 < lines)
        def _():
            pass_copy(p, 1, z, own).start()

        @pl.when(z > 0)
        def _():
            pass_copy(p, -1, z, own).start()

    def begin(p):
        own_copy(p).start()
        across(p, z, True).start()
        if line_first(p):
            both_ways(p, True)

    def level(p, k):
        @pl.when(z - k >= 0)
        def _():
            d = jnp.maximum(z - k, 0)
            pass_copy(p, 1, d, False).wait_recv()
            if k < span:

                @pl.when(z + 1 < lines)
                def _():
                    pass_copy(p, 1, d, False).start()

            if line_first(p):
                across(p, d, False).start()
            else:
                beside(p, d).start()

        @pl.when(z + k < lines)
        def _():
            d = jnp.minimum(z + k, lines - 1)
            pass_copy(p, -1, d, False).wait_recv()
            if k < span:

                @pl.when(z > 0)
                def _():
                    pass_copy(p, -1, d, False).start()

            if line_first(p):
                across(p, d, False).start()
            else:
                beside(p, d).start()

    def turn(p):
        across(p, z, True).wait()
        own_copy(p).wait()
        both_ways(p, False)
        beside(p, z).start()

    def settle(p, k):
        for sign in (1, -1) if k else (1,):
            d = z - sign * k

            @pl.when((d >= 0) & (d < lines))
            def _(d=d):
                d = jnp.clip(d, 0, lines - 1)
                across(p, d, k == 0).wait()
                if k == 0:
                    own_copy(p).wait()
                beside(p, d).start()

    def doc_of(start, size):
        position = start + lax.broadcasted_iota(jnp.int32, (size, 128), 0)

        def count(e, total):
            return total + (position >= starts[e]).astype(jnp.int32)

        return lax.fori_loop(1, starts.shape[0], count, jnp.zeros((size, 128), jnp.int32))

    def code_lanes(start, size):
        lane = lanes_of(size, 128) + 128
        code = jnp.maximum(lane - plan.doc_lane, 0)
        bit = jnp.bitwise_and(jnp.right_shift(doc_of(start, size), code // 2), 1)
        coded = (lane >= plan.doc_lane) & (lane < plan.stat_lane)
        ones = (lane >= plan.stat_lane) & (lane < plan.stat_lane + 3 * plan.heads)
        return lane, coded, bit != code % 2, ones

    pair = 2 * half
    base = spot.index * pair
    origin = jnp.clip(base - reach * pair, 0, 4 * lines * pair - rows)

    def key_lanes(n, unused):
        at = rows_at(n * half, half)
        lane, coded, differs, ones = code_lanes(origin + n * half, half)
        aug_ref[at, :] = jnp.where(
            coded & differs, neg_big, jnp.where(ones, 1.0, 0.0)
        ).astype(bf16)
        return unused

    def own_lanes(n, unused):
        at = rows_at(n * half, half)
        lane, coded, differs, ones = code_lanes(base + n * half, half)
        column = jnp.transpose(
            jnp.broadcast_to(mask_ref[0:1, at], (128, half))
        )
        own_aug_ref[at, :] = jnp.where(
            lane == plan.mask_lane,
            column,
            jnp.where(coded & differs, neg_big, jnp.where(ones, 1.0, 0.0)),
        ).astype(bf16)
        tail = jnp.where(
            (lane == plan.mask_lane) | (coded & ~differs), 1.0, 0.0
        ).astype(bf16)
        q_ref[at, 128:] = tail
        return unused

    begin(mask_piece)
    lax.fori_loop(0, 2, own_lanes, 0)
    project(ours)
    begin(0)
    lax.fori_loop(0, lines, zero_start, 0)
    near_lanes(plan.heads, table_ref, near_ref)
    lax.fori_loop(0, rows // half, key_lanes, 0)

    def y_wait(i, unused):
        y_copy(i, theirs).wait_recv()
        at = rows_at(theirs + i * chunk, chunk)
        x_ref[at, :] = scaled(tok_ref[at, :])
        return unused

    lax.fori_loop(0, 2, y_wait, 0)
    level(0, 1)
    level(mask_piece, 1)
    lax.fori_loop(2, 4, y_wait, 0)
    far_copy.start()
    project(theirs)
    begin(2)
    begin(1)
    if span > 1:
        level(0, 2)
        level(mask_piece, 2)
    settle(0, 0)
    settle(mask_piece, 0)
    turn(2)
    level(1, 1)
    settle(0, 1)
    settle(mask_piece, 1)
    level(2, 1)
    if span > 1:
        level(1, 2)
        settle(0, 2)
        settle(mask_piece, 2)
    settle(1, 0)
    settle(1, 1)
    if span > 1:
        level(2, 2)
        settle(1, 2)
    for k in range(3, span + 1):
        for p in range(4):
            level(p, k)
        for p in (0, 1, mask_piece):
            settle(p, k)

    def finish_line(d, unused):
        @pl.when(~outside(d))
        def _():
            for p in range(4):
                beside(p, d).wait()

        @pl.when(outside(d))
        def _():
            for copy in zero_copies(d):
                copy.wait()

        for p in range(4):

            @pl.when((z + 1 < lines) & (d <= z) & (d > z - span))
            def _(p=p):
                pass_copy(p, 1, d, False).wait_send()

            @pl.when((z > 0) & (d >= z) & (d < z + span))
            def _(p=p):
                pass_copy(p, -1, d, False).wait_send()

        return unused

    lax.fori_loop(0, lines, finish_line, 0)

    def y_drain(i, unused):
        y_copy(i, ours).wait_send()
        return unused

    lax.fori_loop(0, 4, y_drain, 0)
    far_copy.wait()


def first(
    plan, cycle_size, reach, rows, starts, table, tokens, gain, mask, w_query, w_key, w_value, w_out
):
    lines = cycle_size // 4
    span = min(lines - 1, (reach + 3) // 4)
    half, model = tokens.shape
    pair = 2 * half
    hbm = pl.BlockSpec(memory_space=pl.ANY)
    dma = pltpu.SemaphoreType.DMA
    return pl.pallas_call(
        functools.partial(first_kernel, plan, lines, span, reach, rows),
        out_shape=[
            jax.ShapeDtypeStruct((pair, model), bf16),
            jax.ShapeDtypeStruct((pair, model), bf16),
            jax.ShapeDtypeStruct((pair, WIDE), bf16),
            jax.ShapeDtypeStruct((pair, 2 * plan.cols), bf16),
            jax.ShapeDtypeStruct((rows, 128), bf16),
            jax.ShapeDtypeStruct((pair, 128), bf16),
            jax.ShapeDtypeStruct((2, plan.heads, TQ, TK), f32),
            jax.ShapeDtypeStruct((lines, 2, 2, 8, pair), f32),
            jax.ShapeDtypeStruct(w_out.shape, bf16),
            jax.ShapeDtypeStruct((lines, 2, 2, pair, 2 * plan.cols), bf16),
        ],
        in_specs=[smem] * 2 + [vmem] * 3 + [hbm] * 4,
        out_specs=[vmem] * 8 + [hbm] * 2,
        scratch_shapes=[
            pltpu.VMEM((3 * plan.cols, model), bf16),
            pltpu.VMEM((pair, 2 * plan.cols), bf16),
            dma((3,)),
            dma((2, 5)),
            dma((4,)),
            dma((lines, 2, 2)),
            dma((4, 4, lines)),
            dma((4, 2, lines)),
            dma((4, 2, lines)),
        ],
        compiler_params=pltpu.CompilerParams(
            vmem_limit_bytes=56 * 2**20, collective_id=4, has_side_effects=True
        ),
        name="project_gather",
    )(starts, table, tokens, gain, mask, w_query.T, w_key.T, w_value.T, w_out)


def tn(a, b):
    return lax.dot_general(a, b, (((0,), (0,)), ((), ())), preferred_element_type=f32)


def line_relay(spot, start, receive):
    def level(k, unused):
        @pl.when(spot.z - k >= 0)
        def _():
            if_first(k, lambda: receive(1, spot.z - k))

            @pl.when(spot.z + 1 < spot.lines)
            def _():
                start(1, spot.z - k)

        @pl.when(spot.z + k < spot.lines)
        def _():
            if_first(k, lambda: receive(-1, spot.z + k))

            @pl.when(spot.z > 0)
            def _():
                start(-1, spot.z + k)

        return unused

    def if_first(k, run):
        @pl.when(k > 0)
        def _():
            run()

    return level


def finish_kernel(
    plan, lines, dq_ref, dk_ref, dv_ref, mask_ref, wq_hbm, wk_hbm, wv_hbm, normed_ref, att_ref, branch_ref, far_ref,
    tokens_ref, gain_ref, hidden_ref, gh_ref, ffn_ref, small_ref,
    out_ref, gt_ref, gm_ref, weights_ref, total_ref,
    w3_ref, load_sem, lefts, rights, product, mine, core_in, x_in, up_in, down_in, all_w, y_out, y_in, own_part, ffn_in, mask_in,
    small_own, small_y, small_core, small_x, small_all,
    y_sem, core_sem, x_sem, up_sem, down_sem, gz_sem, gx_sem, gc_sem, sz_sem,
):
    spot = Spot(lines)
    z, x, core, wa = (spot.z, spot.x, spot.core, spot.wa)
    cols = plan.cols
    loads = [
        pltpu.make_async_copy(src, w3_ref.at[pl.ds(at, cols)], load_sem.at[i])
        for i, (src, at) in enumerate(((wq_hbm, 0), (wk_hbm, WIDE), (wv_hbm, 3 * WIDE - cols)))
    ]
    for load in loads:
        load.start()
    gap = jnp.zeros((WIDE - cols, tokens_ref.shape[1]), bf16)
    w3_ref[cols:WIDE] = gap
    w3_ref[WIDE + cols : 2 * WIDE] = gap
    w3_ref[2 * WIDE : 3 * WIDE - cols] = gap
    greet(spot, True)
    for load in loads:
        load.wait()
    half = tokens_ref.shape[0]
    quarter = half // 2
    model = tokens_ref.shape[1]
    rows = mine.shape[3]

    def grad_rows(at):
        at = pl.ds(pl.multiple_of(at, quarter), quarter)
        return (
            nn(dq_ref[at, :], w3_ref[0:256])
            + nn(dk_ref[at, :], w3_ref[256:512])
            + nn(dv_ref[at, :], w3_ref[512:768])
        )

    def y_copy(i):
        return send(y_out.at[i], y_in.at[i], y_sem.at[0, i], y_sem.at[1, i], spot.y_mate())

    def theirs(i, unused):
        y_out[i] = grad_rows((1 - wa) * half + i * quarter).astype(bf16)
        y_copy(i).start()
        return unused

    lax.fori_loop(0, 2, theirs, 0)
    mask_copy = send(
        mask_ref.at[1 - wa], mask_in, y_sem.at[0, 2], y_sem.at[1, 2], spot.y_mate()
    )
    mask_copy.start()

    our_rows = pl.ds(pl.multiple_of(wa * half, half), half)
    their_rows = pl.ds(pl.multiple_of((1 - wa) * half, half), half)
    lefts[0] = dq_ref[...]
    lefts[1] = dk_ref[...]
    lefts[2] = dv_ref[...]
    lefts[3] = att_ref[...]
    rights[0] = normed_ref[...]
    rights[1, our_rows, :] = branch_ref[...]
    rights[1, their_rows, :] = far_ref[...]
    per = plan.cols // rows

    def core_copy(m):
        part = pl.ds(m * per // 4, per // 4)
        return send(
            mine.at[part, :, 1 - core],
            core_in.at[part],
            core_sem.at[0, m],
            core_sem.at[1, m],
            spot.core_mate(),
        )

    def fill(m, unused):
        product[...] = tn(lefts[m], rights[m // 3]).astype(bf16)

        def place(offset):
            for j in range(per):
                mine[m * per // 4 + j // 4, (j // 2) % 2, j % 2] = product[
                    offset + j * rows : offset + (j + 1) * rows, :
                ]

        @pl.when(m < 2)
        def _():
            place(0)

        @pl.when(m >= 2)
        def _():
            place(WIDE - plan.cols)

        core_copy(m).start()
        return unused

    lax.fori_loop(0, 4, fill, 0)
    ffn_copy = send(
        ffn_ref.at[their_rows], ffn_in, y_sem.at[0, 3], y_sem.at[1, 3], spot.y_mate()
    )
    ffn_copy.start()

    def x_copy(d):
        return send(
            mine.at[d, 1 - x, core], x_in.at[d], x_sem.at[0, d], x_sem.at[1, d], spot.x_mate()
        )

    def core_add(d, unused):
        mine[d, 1 - x, core] = added(mine[d, 1 - x, core], core_in[d, 1 - x])
        x_copy(d).start()
        return unused

    def ours(i, unused):
        own_part[pl.ds(pl.multiple_of(i * quarter, quarter), quarter), :] = grad_rows(
            wa * half + i * quarter
        )
        return unused

    def core_stage(m, unused):
        core_copy(m).wait()
        lax.fori_loop(m * per // 4, (m + 1) * per // 4, core_add, 0)
        return unused

    lax.fori_loop(0, 4, core_stage, 0)

    def core_add_own(d, unused):
        mine[d, x, core] = added(mine[d, x, core], core_in[d, x])
        return unused

    lax.fori_loop(0, lines, core_add_own, 0)
    lax.fori_loop(0, 2, ours, 0)

    gain_sum = jnp.zeros((1, model), f32)
    step = 32
    for i in range(2):
        y_copy(i).wait()

        def normal(j, total, i=i):
            at = pl.ds(pl.multiple_of(i * quarter + j * step, step), step)
            there = pl.ds(pl.multiple_of(j * step, step), step)
            grad = own_part[at, :] + y_in[i, there, :].astype(f32)
            rows_in = tokens_ref[at, :].astype(f32)
            inv = lax.rsqrt(jnp.mean(rows_in * rows_in, axis=-1, keepdims=True) + eps)
            scaled = gain_ref[...] * grad
            mean = jnp.mean(rows_in * scaled, axis=-1, keepdims=True)
            gt_ref[at, :] = gh_ref[at, :] + inv * scaled - rows_in * (inv * inv * inv * mean)
            return total + jnp.sum(grad * rows_in * inv, axis=0, keepdims=True)

        gain_sum = lax.fori_loop(0, quarter // step, normal, gain_sum)
    small_own[...] = small_ref[...]
    small_own[0:1, :] = gain_sum
    small_copy = send(
        small_own, small_y, y_sem.at[0, 4], y_sem.at[1, 4], spot.y_mate()
    )
    small_copy.start()
    mask_copy.wait()
    gm_ref[...] = mask_ref[wa] + mask_in[...]

    def flow(step, d):
        ring, sem = (up_in, up_sem) if step > 0 else (down_in, down_sem)
        return send(
            mine.at[d, x, core], ring.at[d], sem.at[0, d], sem.at[1, d], spot.z_mate(step)
        )

    def merge(step, d):
        flow(step, d).wait_recv()
        ring = up_in if step > 0 else down_in
        mine[d, x, core] = added(mine[d, x, core], ring[d])

    def x_add(d, unused):
        x_copy(d).wait()
        mine[d, x, core] = added(mine[d, x, core], x_in[d])

        @pl.when((z == 0) & (d > 0))
        def _():
            flow(1, d).start()

        @pl.when((z == lines - 1) & (d < lines - 1))
        def _():
            flow(-1, d).start()

        return unused

    lax.fori_loop(0, lines, x_add, 0)
    small_copy.wait()
    row = lax.broadcasted_iota(jnp.int32, small_own.shape, 0)
    small_x[0] = small_own[...] + jnp.where(row < 2, small_y[...], 0.0)
    small_core_copy = send(
        small_x.at[0], small_core, core_sem.at[0, 4], core_sem.at[1, 4], spot.core_mate()
    )
    small_core_copy.start()

    def relay(k, unused):
        high = lines - 1 - k

        @pl.when((z < high) & (z > 0))
        def _():
            merge(1, high)
            flow(1, high).start()

        @pl.when((z > k) & (z + 1 < lines))
        def _():
            merge(-1, k)
            flow(-1, k).start()

        return unused

    lax.fori_loop(0, lines - 1, relay, 0)
    small_core_copy.wait()
    small_x[1] = small_x[0] + small_core[...]
    small_x_copy = send(
        small_x.at[1], small_x.at[2], x_sem.at[0, lines], x_sem.at[1, lines], spot.x_mate()
    )
    small_x_copy.start()

    @pl.when(z > 0)
    def _():
        merge(1, z)

    @pl.when(z + 1 < lines)
    def _():
        merge(-1, z)

    all_w[z, x, core] = mine[z, x, core]

    def pass_w(step, d):
        i = 0 if step > 0 else 1
        return send(
            all_w.at[d, x, core], all_w.at[d, x, core], gz_sem.at[i, d], gz_sem.at[2 + i, d],
            spot.z_mate(step),
        )

    def pass_s(step, d):
        i = 0 if step > 0 else 1
        return send(
            small_all.at[d], small_all.at[d], sz_sem.at[i, d], sz_sem.at[2 + i, d],
            spot.z_mate(step),
        )

    def across(d):
        return send(
            all_w.at[d, x, core], all_w.at[d, x, core], gx_sem.at[0, d], gx_sem.at[1, d],
            spot.x_mate(),
        )

    def beside(d):
        return send(
            all_w.at[d, :, core], all_w.at[d, :, core], gc_sem.at[0, d], gc_sem.at[1, d],
            spot.core_mate(),
        )

    small_x_copy.wait()
    small_all[z] = small_x[1] + small_x[2]

    def receive(step, d):
        pass_w(step, d).wait_recv()
        across(d).start()

    across(z).start()
    lax.fori_loop(
        0, lines, line_relay(spot, lambda s, d: pass_w(s, d).start(), receive), 0
    )
    lax.fori_loop(
        0,
        lines,
        line_relay(
            spot, lambda s, d: pass_s(s, d).start(), lambda s, d: pass_s(s, d).wait_recv()
        ),
        0,
    )

    def add_small(d, total):
        return total + small_all[d]

    total_ref[...] = lax.fori_loop(1, lines, add_small, small_all[0])
    ffn_copy.wait()

    def last(j, unused):
        at = pl.ds(pl.multiple_of(j * step, step), step)
        here = pl.ds(pl.multiple_of(wa * half + j * step, step), step)
        total = hidden_ref[at, :] + ffn_ref[here, :].astype(f32) + ffn_in[at, :].astype(f32)
        out_ref[at, :] = total.astype(bf16)
        return unused

    lax.fori_loop(0, half // step, last, 0)

    def spread(d, unused):
        across(d).wait()
        beside(d).start()
        return unused

    lax.fori_loop(0, lines, spread, 0)

    def copy_out(d, unused):
        beside(d).wait()
        weights_ref[d] = all_w[d]
        return unused

    lax.fori_loop(0, lines, copy_out, 0)

    def drain(d, unused):
        @pl.when((z < d))
        def _():
            flow(1, d).wait_send()

        @pl.when((z > d))
        def _():
            flow(-1, d).wait_send()

        @pl.when((d <= z) & (z + 1 < lines))
        def _():
            pass_w(1, d).wait_send()
            pass_s(1, d).wait_send()

        @pl.when((d >= z) & (z > 0))
        def _():
            pass_w(-1, d).wait_send()
            pass_s(-1, d).wait_send()

        return unused

    lax.fori_loop(0, lines, drain, 0)


def finish(plan, cycle_size, *operands):
    lines = cycle_size // 4
    half, model = operands[11].shape
    rows = 4 * plan.cols // cycle_size
    dma = pltpu.SemaphoreType.DMA
    return pl.pallas_call(
        functools.partial(finish_kernel, plan, lines),
        out_shape=[
            jax.ShapeDtypeStruct((half, model), bf16),
            jax.ShapeDtypeStruct((half, model), f32),
            jax.ShapeDtypeStruct((8, half), f32),
            jax.ShapeDtypeStruct((lines, 2, 2, rows, model), bf16),
            jax.ShapeDtypeStruct((8, model), f32),
        ],
        in_specs=[vmem] * 4
        + [pl.BlockSpec(memory_space=pl.ANY)] * 3
        + [vmem] * (len(operands) - 7),
        out_specs=[vmem] * 5,
        scratch_shapes=[
            pltpu.VMEM((3 * WIDE, model), bf16),
            dma((3,)),
            pltpu.VMEM((4, 2 * half, WIDE), bf16),
            pltpu.VMEM((2, 2 * half, model), bf16),
            pltpu.VMEM((WIDE, model), bf16),
            pltpu.VMEM((lines, 2, 2, rows, model), bf16),
            pltpu.VMEM((lines, 2, rows, model), bf16),
            pltpu.VMEM((lines, rows, model), bf16),
            pltpu.VMEM((lines, rows, model), bf16),
            pltpu.VMEM((lines, rows, model), bf16),
            pltpu.VMEM((lines, 2, 2, rows, model), bf16),
            pltpu.VMEM((2, half // 2, model), bf16),
            pltpu.VMEM((2, half // 2, model), bf16),
            pltpu.VMEM((half, model), f32),
            pltpu.VMEM((half, model), bf16),
            pltpu.VMEM((8, half), f32),
            pltpu.VMEM((8, model), f32),
            pltpu.VMEM((8, model), f32),
            pltpu.VMEM((8, model), f32),
            pltpu.VMEM((3, 8, model), f32),
            pltpu.VMEM((lines, 8, model), f32),
            dma((2, 5)),
            dma((2, 5)),
            dma((2, lines + 1)),
            dma((2, lines)),
            dma((2, lines)),
            dma((4, lines)),
            dma((2, lines)),
            dma((2, lines)),
            dma((4, lines)),
        ],
        compiler_params=pltpu.CompilerParams(
            vmem_limit_bytes=58 * 2**20, collective_id=2, has_side_effects=True
        ),
        name="finish",
    )(*operands)


root = 0.7978845608028654
cubic = 0.044715


def middle_kernel(
    plan, cycle_size, att_ref, mixed_ref, tokens_ref, cot_ref, gain_ref,
    wo_hbm, wo_far_hbm, wg_hbm, wu_hbm, wd_hbm,
    hidden_ref, gh_ref, branch_ref, ffn_ref, do_ref, gain_part_ref, *refs,
):
    stacks, refs = (refs[:3], refs[3:])
    (
        wg, wu, wd, wo, inner, gg, gu, x_ref, att_in, d_out, d_in, e_out, e_in,
        acc_f, acc_g, rows_buf, load_sem, y_sem, out_sem,
    ) = refs
    spot = Spot(cycle_size // 4)
    wa = spot.wa
    pair, model = tokens_ref.shape
    half = pair // 2
    units = wd.shape[1]
    chunk = half // 4
    block = pair // 4
    loads = [
        pltpu.make_async_copy(src, dst, load_sem.at[i])
        for i, (src, dst) in enumerate(
            (
                (wo_hbm, wo.at[0, 64:]),
                (wo_far_hbm, wo.at[1, 64:]),
                (wg_hbm, wg),
                (wu_hbm, wu),
                (wd_hbm, wd),
            )
        )
    ]
    for load in loads:
        load.start()
    barrier = pltpu.get_barrier_semaphore()
    pl.semaphore_signal(
        barrier, inc=1, device_id=spot.y_mate(), device_id_type=pl.DeviceIdType.MESH
    )
    wo[:, :64, :] = jnp.zeros((2, 64, model), bf16)
    pl.semaphore_wait(barrier, 1)
    ours = wa * half
    theirs = (1 - wa) * half

    def rows_at(start, size):
        return pl.ds(pl.multiple_of(start, size), size)

    def a_start(i):
        return (theirs + i * block) if i < 2 else (ours + (i - 2) * block)

    def a_copy(i, base):
        at = rows_at(base + (i % 2) * block, block)
        return send(att_ref.at[at], att_in.at[at], y_sem.at[0, i], y_sem.at[1, i], spot.y_mate())

    order = (0, 1, 2, 3)
    for i in order:
        a_copy(i, ours if i < 2 else theirs).start()
    loads[0].wait()
    loads[1].wait()

    def normal(i, base, keep):
        a_copy(i, base).wait_recv()
        at = rows_at(base + (i % 2) * block, block)
        branch = nn(att_ref[at, :], wo[0]) + nn(att_in[at, :], wo[1])
        hidden = tokens_ref[at, :].astype(f32) + branch
        if keep:
            hidden_ref[(i % 2) * block : (i % 2 + 1) * block, :] = hidden
        inv = lax.rsqrt(jnp.mean(hidden * hidden, axis=-1, keepdims=True) + eps)
        x_ref[at, :] = (hidden * inv * gain_ref[...]).astype(bf16)

    normal(0, theirs, False)
    normal(1, theirs, False)
    for load in loads[2:]:
        load.wait()
    wide = 256

    def feed(base):
        rows = rows_at(base, half)
        acc_f[...] = jnp.zeros_like(acc_f)
        acc_g[...] = jnp.zeros_like(acc_g)

        def tile(u, unused):
            cols = rows_at(u * wide, wide)
            gate = nn(x_ref[rows, :], wg[:, cols])
            upward = nn(x_ref[rows, :], wu[:, cols])
            grad_inner = nn(cot_ref[rows, :], wd[:, cols])
            square = gate * gate
            bend = jnp.tanh(root * gate * (1.0 + cubic * square))
            side = 0.5 * (1.0 + bend)
            gelu = gate * side
            slope = side + 0.5 * gate * (1.0 - bend * bend) * (
                root * (1.0 + 3.0 * cubic * square)
            )
            inner_low = (gelu * upward).astype(bf16)
            gate_low = (grad_inner * upward * slope).astype(bf16)
            up_low = (grad_inner * gelu).astype(bf16)
            inner[rows, cols] = inner_low
            gg[rows, cols] = gate_low
            gu[rows, cols] = up_low
            acc_g[...] += nt(gate_low, wg[:, cols]) + nt(up_low, wu[:, cols])
            acc_f[...] += nt(inner_low, wd[:, cols])
            return unused

        lax.fori_loop(0, units // wide, tile, 0)
        ffn_ref[rows, :] = acc_f[...].astype(bf16)

    def d_copy(i):
        return send(
            d_out.at[i], d_in.at[i], y_sem.at[0, 4 + i], y_sem.at[1, 4 + i], spot.y_mate()
        )

    def send_grad(i, unused):
        d_out[i] = acc_g[rows_at(i * chunk, chunk), :].astype(bf16)
        d_copy(i).start()
        return unused

    def half_pass(k, unused):
        base = theirs + k * (ours - theirs)
        feed(base)

        @pl.when(k == 0)
        def _():
            lax.fori_loop(0, 4, send_grad, 0)
            normal(2, ours, True)
            normal(3, ours, True)

        return unused

    lax.fori_loop(0, 2, half_pass, 0)
    count = units // wide

    def out_copy(m, u):
        return pltpu.make_async_copy(
            rows_buf.at[m, u % 2],
            stacks[m].at[rows_at(u * wide, wide)],
            out_sem.at[m, u % 2],
        )

    for m in range(3):
        left = (inner, gg, gu)[m]
        right = (cot_ref, x_ref, x_ref)[m]

        def weight_rows(u, unused, m=m, left=left, right=right):
            @pl.when(u >= 2)
            def _():
                out_copy(m, u - 2).wait()

            turned = jnp.transpose(left[:, rows_at(u * wide, wide)])
            rows_buf[m, u % 2] = nn(turned, right[...]).astype(bf16)
            out_copy(m, u).start()
            return unused

        lax.fori_loop(0, count, weight_rows, 0)

    def e_copy(i):
        return send(
            e_out.at[i], e_in.at[i], y_sem.at[0, 8 + i], y_sem.at[1, 8 + i], spot.y_mate()
        )

    def normal_back(i, total):
        d_copy(i).wait()
        at = rows_at(i * chunk, chunk)
        grad = acc_g[at, :] + d_in[i].astype(f32)
        hidden = hidden_ref[at, :]
        inv = lax.rsqrt(jnp.mean(hidden * hidden, axis=-1, keepdims=True) + eps)
        scaled = gain_ref[...] * grad
        mean = jnp.mean(hidden * scaled, axis=-1, keepdims=True)
        grad_hidden = (
            cot_ref[rows_at(ours + i * chunk, chunk), :].astype(f32)
            + inv * scaled
            - hidden * (inv * inv * inv * mean)
        )
        gh_ref[at, :] = grad_hidden
        low = grad_hidden.astype(bf16)
        branch_ref[at, :] = low
        e_out[i] = nt(low, wo[1]).astype(bf16)
        e_copy(i).start()
        do_ref[rows_at(ours + i * chunk, chunk), :] = nt(low, wo[0]).astype(bf16)
        return total + jnp.sum(grad * hidden * inv, axis=0, keepdims=True)

    gain_part_ref[...] = lax.fori_loop(0, 4, normal_back, jnp.zeros((1, model), f32))

    def row_terms(at, grad):
        lane = lanes_of(chunk)
        terms = grad.astype(f32) * mixed_ref[at, :]
        out = grad
        for h in range(plan.heads):
            row_term = jnp.sum(
                jnp.where(lane // 64 == h + 1, terms, 0.0), axis=1, keepdims=True
            )
            for i, part in enumerate(split3(-row_term)):
                out = jnp.where(lane == 3 * h + i, part, out)
        do_ref[at, :] = out

    def own_terms(i, unused):
        at = rows_at(ours + i * chunk, chunk)
        row_terms(at, do_ref[at, :])
        return unused

    lax.fori_loop(0, 4, own_terms, 0)

    def far_terms(i, unused):
        e_copy(i).wait()
        row_terms(rows_at(theirs + i * chunk, chunk), e_in[i])
        return unused

    lax.fori_loop(0, 4, far_terms, 0)
    for m in range(3):
        for u in range(max(0, count - 2), count):
            out_copy(m, u).wait()
    for i in order:
        a_copy(i, ours if i < 2 else theirs).wait_send()


def middle(
    plan, cycle_size, attended, mixed, tokens, cot, gain, w_out, w_out_far, w_gate, w_up, w_down
):
    pair, model = tokens.shape
    half = pair // 2
    units = w_down.shape[0]
    chunk = half // 4
    hbm = pl.BlockSpec(memory_space=pl.ANY)
    dma = pltpu.SemaphoreType.DMA
    return pl.pallas_call(
        functools.partial(middle_kernel, plan, cycle_size),
        out_shape=[
            jax.ShapeDtypeStruct((half, model), f32),
            jax.ShapeDtypeStruct((half, model), f32),
            jax.ShapeDtypeStruct((half, model), bf16),
            jax.ShapeDtypeStruct((pair, model), bf16),
            jax.ShapeDtypeStruct((pair, WIDE), bf16),
            jax.ShapeDtypeStruct((1, model), f32),
        ]
        + [jax.ShapeDtypeStruct((units, model), bf16)] * 3,
        in_specs=[vmem] * 5 + [hbm] * 5,
        out_specs=[vmem] * 6 + [hbm] * 3,
        scratch_shapes=[
            pltpu.VMEM((model, units), bf16),
            pltpu.VMEM((model, units), bf16),
            pltpu.VMEM((model, units), bf16),
            pltpu.VMEM((2, WIDE, model), bf16),
            pltpu.VMEM((pair, units), bf16),
            pltpu.VMEM((pair, units), bf16),
            pltpu.VMEM((pair, units), bf16),
            pltpu.VMEM((pair, model), bf16),
            pltpu.VMEM((pair, WIDE), bf16),
            pltpu.VMEM((4, chunk, model), bf16),
            pltpu.VMEM((4, chunk, model), bf16),
            pltpu.VMEM((4, chunk, WIDE), bf16),
            pltpu.VMEM((4, chunk, WIDE), bf16),
            pltpu.VMEM((half, model), f32),
            pltpu.VMEM((half, model), f32),
            pltpu.VMEM((3, 2, WIDE, model), bf16),
            dma((5,)),
            dma((2, 12)),
            dma((3, 2)),
        ],
        compiler_params=pltpu.CompilerParams(
            vmem_limit_bytes=60 * 2**20, collective_id=3, has_side_effects=True
        ),
        name="feed_forward",
    )(attended, mixed, tokens, cot, gain, w_out, w_out_far, w_gate, w_up, w_down.T)


class Scatter:
    def __init__(self, spot, units, parts, outs, buffers, sems):
        self.spot = spot
        self.units = units
        self.parts = parts
        self.outs = outs
        self.mine, self.core_in, self.x_in, self.up_in, self.down_in = buffers
        self.load_sem, self.core_sem, self.x_sem, self.up_sem, self.down_sem = sems

    def rows_of(self, u):
        return pl.ds(self.units[u][1], self.units[u][2])

    def load(self, u):
        m = self.units[u][0]
        return pltpu.make_async_copy(
            self.parts[m].at[:, :, self.spot.core, self.rows_of(u)],
            self.mine.at[m, :, :, self.rows_of(u)],
            self.load_sem.at[u],
        )

    def core_copy(self, u):
        m = self.units[u][0]
        return send(
            self.parts[m].at[:, :, 1 - self.spot.core, self.rows_of(u)],
            self.core_in.at[m, :, :, self.rows_of(u)],
            self.core_sem.at[0, u],
            self.core_sem.at[1, u],
            self.spot.core_mate(),
        )

    def x_copy(self, u):
        m = self.units[u][0]
        x = self.spot.x
        src = self.mine.at[m, :, 1 - x, self.rows_of(u)]
        dst = self.x_in.at[m, :, self.rows_of(u)]
        return send(src, dst, self.x_sem.at[0, u], self.x_sem.at[1, u], self.spot.x_mate())

    def begin(self, u):
        self.load(u).start()
        self.core_copy(u).start()

    def core_stage(self, u):
        m = self.units[u][0]
        x = self.spot.x
        self.load(u).wait()
        self.core_copy(u).wait()

        def add(slot):
            def body(line, unused):
                at = (m, line, slot, self.rows_of(u))
                self.mine[at] = added(self.mine[at], self.core_in[at])
                return unused

            lax.fori_loop(0, self.spot.lines, body, 0)

        add(1 - x)
        self.x_copy(u).start()
        add(x)

    def x_stage(self, u):
        m = self.units[u][0]
        x = self.spot.x
        self.x_copy(u).wait()

        def body(line, unused):
            at = (m, line, x, self.rows_of(u))
            self.mine[at] = added(self.mine[at], self.x_in[m, line, self.rows_of(u)])
            return unused

        lax.fori_loop(0, self.spot.lines, body, 0)
        self.ends(u)

    def copy(self, u, step, d):
        m = self.units[u][0]
        sem = self.up_sem if step > 0 else self.down_sem
        ring = self.up_in if step > 0 else self.down_in
        return send(
            self.mine.at[m, d, self.spot.x, self.rows_of(u)],
            ring.at[m, d, self.rows_of(u)],
            sem.at[0, u, d],
            sem.at[1, u, d],
            self.spot.z_mate(step),
        )

    def receive(self, u, step, d):
        m = self.units[u][0]
        self.copy(u, step, d).wait_recv()
        ring = self.up_in if step > 0 else self.down_in
        at = (m, d, self.spot.x, self.rows_of(u))
        self.mine[at] = added(self.mine[at], ring[m, d, self.rows_of(u)])

    def start(self, u, step, d):
        self.copy(u, step, d).start()

    def ends(self, u):
        z, lines = (self.spot.z, self.spot.lines)

        @pl.when(z == 0)
        def _():
            def up(k, unused):
                self.start(u, 1, lines - 1 - k)
                return unused

            lax.fori_loop(0, lines - 1, up, 0)

        @pl.when(z == lines - 1)
        def _():
            def down(k, unused):
                self.start(u, -1, k)
                return unused

            lax.fori_loop(0, lines - 1, down, 0)

    def relay(self, u, lag):
        z, lines = (self.spot.z, self.spot.lines)
        top = lines - 2 if lag == 2 else lag

        @pl.when((z >= lag) & (z <= top))
        def _():
            def up(k, unused):
                self.receive(u, 1, lines - 1 - k)
                self.start(u, 1, lines - 1 - k)
                return unused

            lax.fori_loop(0, lines - 1 - z, up, 0)

        @pl.when((lines - 1 - z >= lag) & (lines - 1 - z <= top))
        def _():
            def down(k, unused):
                self.receive(u, -1, k)
                self.start(u, -1, k)
                return unused

            lax.fori_loop(0, z, down, 0)

    def settle(self, u):
        z, lines = (self.spot.z, self.spot.lines)

        @pl.when(z > 0)
        def _():
            self.receive(u, 1, z)

        @pl.when(z + 1 < lines)
        def _():
            self.receive(u, -1, z)

        self.store(u)

    def store(self, u):
        m = self.units[u][0]
        self.outs[m][self.rows_of(u), :] = self.mine[
            m, self.spot.z, self.spot.x, self.rows_of(u)
        ].astype(f32)

    def drain(self, u):
        z, lines = (self.spot.z, self.spot.lines)

        def body(k, unused):
            @pl.when(z < lines - 1 - k)
            def _():
                self.copy(u, 1, lines - 1 - k).wait_send()

            @pl.when(z > k)
            def _():
                self.copy(u, -1, k).wait_send()

            return unused

        lax.fori_loop(0, lines - 1, body, 0)


def scatter_units(rows):
    if rows % 16 or rows < 112:
        return [(m, 0, rows) for m in range(3)]
    tail = rows - 64
    return [
        (0, 0, 64), (1, 0, 64), (2, 0, 64), (0, 64, tail), (1, 64, tail), (2, 64, tail - 16),
        (2, rows - 16, 16),
    ]


def backward_kernel(
    plan, lines, span, reach, doc_most, rows, pair, table_ref, qb_ref, do_ref,
    own_kv, own_aug, near_hbm, aug_hbm, masks_hbm, g_hbm, qall_hbm, branch_hbm, p0, p1, p2,
    dq_ref, tab_ref, dk_ref, dv_ref, mask_ref, o0, o1, o2, far_hbm, all_do,
    mine, core_in, x_in, up_in, down_in,
    km, vm, mask_row, g_buf, aug_buf, qh_ref, doh_ref, acc, near_ref, near_acc, far_acc,
    load_sem, core_sem, rx_sem, up_sem, down_sem, own_sem, zero_sem, z_sem, x_sem, c_sem, g_sem,
    q_sem,
):
    spot = Spot(lines)
    z, x, core = (spot.z, spot.x, spot.core)
    units = scatter_units(o0.shape[0])
    scatter = Scatter(
        spot,
        units,
        (p0, p1, p2),
        (o0, o1, o2),
        (mine, core_in, x_in, up_in, down_in),
        (load_sem, core_sem, rx_sem, up_sem, down_sem),
    )
    order = range(len(units))
    greet(spot, True)
    far_copy = send(branch_hbm, far_hbm, own_sem.at[2], own_sem.at[3], spot.y_mate())
    far_copy.start()

    def outside(d):
        return (d < z - span) | (d > z + span)

    def pass_copy(step, d):
        i = 0 if step > 0 else 1
        part = all_do.at[d, :, core]
        return send(part, part, z_sem.at[i, d], z_sem.at[2 + i, d], spot.z_mate(step))

    across = send(do_ref, all_do.at[z, x, core], x_sem.at[0], x_sem.at[1], spot.x_mate())

    def beside(d):
        part = all_do.at[d, :, core]
        return send(part, part, c_sem.at[0, d], c_sem.at[1, d], spot.core_mate())

    own_copy = pltpu.make_async_copy(do_ref, all_do.at[z, x, core], own_sem.at[0])

    def zero_copies(d):
        return [
            pltpu.make_async_copy(vm.at[pl.ds(0, pair)], all_do.at[d, a, b], zero_sem.at[d, a, b])
            for a in range(2)
            for b in range(2)
        ]

    def zero_start(d, unused):
        @pl.when(outside(d))
        def _():
            for copy in zero_copies(d):
                copy.start()

        return unused

    def turn():
        across.wait()
        own_copy.wait()

        @pl.when(z + 1 < lines)
        def _():
            pass_copy(1, z).start()

        @pl.when(z > 0)
        def _():
            pass_copy(-1, z).start()

        beside(z).start()

    def level(k):
        @pl.when(z - k >= 0)
        def _():
            d = jnp.maximum(z - k, 0)
            pass_copy(1, d).wait_recv()
            if k < span:

                @pl.when(z + 1 < lines)
                def _():
                    pass_copy(1, d).start()

            beside(d).start()

        @pl.when(z + k < lines)
        def _():
            d = jnp.minimum(z + k, lines - 1)
            pass_copy(-1, d).wait_recv()
            if k < span:

                @pl.when(z > 0)
                def _():
                    pass_copy(-1, d).start()

            beside(d).start()

    def gathered(d, unused):
        @pl.when(~outside(d))
        def _():
            beside(d).wait()

        @pl.when(outside(d))
        def _():
            for copy in zero_copies(d):
                copy.wait()

        @pl.when((z + 1 < lines) & (d <= z) & (d > z - span))
        def _():
            pass_copy(1, d).wait_send()

        @pl.when((z > 0) & (d >= z) & (d < z + span))
        def _():
            pass_copy(-1, d).wait_send()

        return unused

    own_copy.start()
    across.start()
    for u in order:
        scatter.begin(u)
    vm[:PAD, :] = jnp.zeros((PAD, WIDE), bf16)
    lax.fori_loop(0, lines, zero_start, 0)

    base = spot.index * pair
    total = 4 * lines * pair
    origin = jnp.clip(base - reach * pair, 0, total - rows)
    local = base - origin
    blocks = rows // pair

    def mask_copy(n):
        to = pl.ds(pl.multiple_of(PAD + n * pair, 128), pair)
        return pltpu.make_async_copy(masks_hbm.at[n], mask_row.at[:, to], q_sem.at[1 + n])

    def mask_start(n, unused):
        mask_copy(n).start()
        return unused

    lax.fori_loop(0, blocks, mask_start, 0)
    mask_row[:, :PAD] = jnp.zeros((8, PAD), f32)
    mask_row[:, PAD + rows :] = jnp.zeros((8, PAD), f32)
    km[:PAD, :] = jnp.broadcast_to(
        jnp.where(pad_lanes(plan), neg_big, 0.0).astype(bf16), (PAD, WIDE)
    )
    km[PAD + rows :, :] = km[:PAD, :]
    vm[PAD + rows :, :] = jnp.zeros((PAD, WIDE), bf16)
    low_block = lanes_of(pair, 128) < 64
    ones_block = (lanes_of(pair, 128) < 3 * plan.heads).astype(bf16)

    def g_copy(n):
        at = pl.ds(pl.multiple_of(n * pair, pair), pair)
        return pltpu.make_async_copy(g_hbm.at[at], g_buf.at[n % 2], g_sem.at[0, n % 2])

    def aug_copy(n):
        at = pl.ds(pl.multiple_of(n * pair, pair), pair)
        return pltpu.make_async_copy(aug_hbm.at[at], aug_buf.at[n % 2], g_sem.at[1, n % 2])

    def near_copy(flip):
        return pltpu.make_async_copy(near_hbm.at[flip], near_ref, own_sem.at[1])

    g_copy(0).start()
    aug_copy(0).start()
    near_copy(0).start()

    def build(n, unused):
        g_copy(n).wait()
        aug_copy(n).wait()

        @pl.when(n + 1 < blocks)
        def _():
            g_copy(n + 1).start()
            aug_copy(n + 1).start()

        mask_copy(n).wait()
        to = pl.ds(pl.multiple_of(PAD + n * pair, 128), pair)
        middle = g_buf[n % 2, :, 128:256]
        km[to, 0:128] = g_buf[n % 2, :, 0:128]
        km[to, 128:256] = jnp.where(low_block, middle, aug_buf[n % 2])
        vm[to, 0:128] = jnp.where(low_block, ones_block, middle)
        vm[to, 128:256] = g_buf[n % 2, :, 256:384]
        return unused

    lax.fori_loop(0, blocks, build, 0)
    near_copy(0).wait()
    near_acc[...] = jnp.zeros_like(near_acc)
    far_acc[...] = jnp.zeros_like(far_acc)
    lane = lanes_of(TQ)
    low = lanes_of(TQ, 128) < 64
    ones = (lanes_of(TQ, 128) < 3 * plan.heads).astype(bf16)

    def chunks(t):
        start = local + t * TQ
        least = jnp.maximum(start - doc_most + 1, 0)
        most = jnp.minimum(start + TQ + doc_most - 1, rows)
        n_left = jnp.maximum(start - EDGE - least + TK - 1, 0) // TK
        n_right = jnp.maximum(most - (start + TK - EDGE) + TK - 1, 0) // TK
        return start, n_left, n_right

    def rows_of_tile(t):
        return pl.ds(pl.multiple_of(t * TQ, TQ), TQ)

    def near_of(start):
        return pl.ds(pl.multiple_of(start + PAD - EDGE, 128), TK)

    def query_grads(h, s, part):
        return jnp.exp(s) * nt(doh_ref[h], vm[part, :])

    def dq_near(t, start):
        out = rows_of_tile(t)
        near = near_of(start)
        q = qb_ref[out, :]
        do = do_ref[out, :]
        for h in range(plan.heads):
            qh_ref[h] = jnp.where(plan.key_lanes(lane, h), q, jnp.zeros_like(q))
            doh_ref[h] = jnp.where(plan.value_lanes(lane, h), do, jnp.zeros_like(do))
            ds = query_grads(
                h, nt(qh_ref[h], km[near, :]) + near_ref[h] + mask_row[0:1, near], near
            )
            near_acc[h] += ds
            acc[h] = nn(ds.astype(bf16), km[near, :])

    def dq_far(start, n, n_left):
        part, bucket = far_span(start, n, n_left, far_left_bucket, far_right_bucket)
        slot = (n >= n_left).astype(jnp.int32)
        for h in range(plan.heads):
            offset = mask_row[0:1, part] + table_ref[bucket, h]
            ds = query_grads(h, nt(qh_ref[h], km[part, :]) + offset, part)
            acc[h] += nn(ds.astype(bf16), km[part, :])
            far_acc[slot, h] += ds[:, 0:128] + ds[:, 128:256] + ds[:, 256:384] + ds[:, 384:512]

    def dq_end(t):
        result = jnp.zeros((TQ, WIDE), f32)
        for h in range(plan.heads):
            result = jnp.where(lane // 64 == h, acc[h], result)
        dq_ref[rows_of_tile(t), :] = result.astype(bf16)

    def table_end():
        row = lax.broadcasted_iota(jnp.int32, (EDGE, 3 * EDGE), 0)
        col = lax.broadcasted_iota(jnp.int32, (EDGE, 3 * EDGE), 1)
        bucket = bucket_of(col - EDGE - row)
        for h in range(plan.heads):
            band = near_acc[h, :EDGE, : 3 * EDGE] + near_acc[h, EDGE:, EDGE:]

            def one(b, unused, band=band, h=h):
                part = jnp.sum(jnp.where(bucket == b, band, 0.0), axis=0, keepdims=True)
                tab_ref[h, pl.ds(b, 1), :] = part[:, :128] + part[:, 128:256] + part[:, 256:]
                return unused

            lax.fori_loop(0, 32, one, 0)
            for b, slot, extra in (
                (far_left_bucket, 0, near_acc[h, EDGE:, :EDGE]),
                (far_right_bucket, 1, near_acc[h, :EDGE, 3 * EDGE :]),
            ):
                tab_ref[h, b : b + 1, :] += jnp.sum(
                    far_acc[slot, h], axis=0, keepdims=True
                ) + jnp.sum(extra, axis=0, keepdims=True)

    def swap_operands():
        near_copy(1).start()
        lax.fori_loop(0, lines, gathered, 0)
        q_copy = pltpu.make_async_copy(qall_hbm, km.at[pl.ds(PAD, rows)], q_sem.at[0])
        q_copy.start()

        def block_copy(n):
            b = origin // pair + n
            return pltpu.make_async_copy(
                all_do.at[b // 4, (b // 2) % 2, b % 2],
                vm.at[pl.ds(pl.multiple_of(PAD + n * pair, 128), pair)],
                q_sem.at[1 + n],
            )

        def block_start(n, unused):
            block_copy(n).start()
            return unused

        lax.fori_loop(0, blocks, block_start, 0)
        first = lanes_of(1)
        stat = (first >= plan.stat_lane) & (first < plan.stat_lane + 3 * plan.heads)
        km[:PAD, :] = jnp.broadcast_to(jnp.where(stat, neg_big, 0.0).astype(bf16), (PAD, WIDE))
        km[PAD + rows :, :] = km[:PAD, :]

        def block_wait(n, unused):
            block_copy(n).wait()
            return unused

        lax.fori_loop(0, blocks, block_wait, 0)
        q_copy.wait()
        near_copy(1).wait()

    def key_grads(h, s, part):
        p = jnp.exp(s)
        ds = p * nt(doh_ref[h], vm[part, :])
        return nn(p.astype(bf16), vm[part, :]), nn(ds.astype(bf16), km[part, :])

    def dkv_near(t, start):
        out = rows_of_tile(t)
        near = near_of(start)
        middle = own_kv[out, 128:256]
        k = jnp.concatenate([own_kv[out, 0:128], jnp.where(low, middle, own_aug[out, :])], axis=1)
        v = jnp.concatenate([jnp.where(low, ones, middle), own_kv[out, 256:384]], axis=1)
        for h in range(plan.heads):
            qh_ref[h] = jnp.where(plan.key_lanes(lane, h), k, jnp.zeros_like(k))
            doh_ref[h] = jnp.where(plan.value_lanes(lane, h), v, jnp.zeros_like(v))
            near_acc[h, :, :WIDE], acc[h] = key_grads(
                h, nt(qh_ref[h], km[near, :]) + near_ref[h], near
            )

    def dkv_far(start, n, n_left):
        part, bucket = far_span(start, n, n_left, far_right_bucket, far_left_bucket)
        for h in range(plan.heads):
            add_v, add_k = key_grads(h, nt(qh_ref[h], km[part, :]) + table_ref[bucket, h], part)
            near_acc[h, :, :WIDE] += add_v
            acc[h] += add_k

    def dkv_end(t):
        out = rows_of_tile(t)
        dk = jnp.zeros((TQ, WIDE), f32)
        dv = jnp.zeros((TQ, WIDE), f32)
        mask_grad = jnp.zeros((TQ, 1), f32)
        for h in range(plan.heads):
            dk = jnp.where(lane // 64 == h, acc[h], dk)
            dv = jnp.where(lane // 64 == h + 1, near_acc[h, :, :WIDE], dv)
            mask_grad = mask_grad + acc[h][:, plan.mask_lane : plan.mask_lane + 1]
        mask_ref[t] = jnp.transpose(jnp.broadcast_to(mask_grad, (TQ, 128)))[:8, :]
        dk_ref[out, :] = dk.astype(bf16)
        dv_ref[out, :] = dv.astype(bf16)

    tiles = pair // TQ
    steps = 1 + 2 * (-(-doc_most // TK)) + 1
    half_slots = tiles * steps
    last_step = steps - 1

    def attention(w):
        backward = w >= half_slots
        t = (w % half_slots) // steps
        n = w % steps
        start, n_left, n_right = chunks(t)
        live = (n > 0) & (n - 1 < n_left + n_right)

        @pl.when(~backward)
        def _():
            @pl.when(n == 0)
            def _():
                dq_near(t, start)

            @pl.when(live)
            def _():
                dq_far(start, n - 1, n_left)

            @pl.when(n == last_step)
            def _():
                dq_end(t)

        @pl.when(backward & (w < 2 * half_slots))
        def _():
            @pl.when(w == half_slots)
            def _():
                table_end()
                swap_operands()

            @pl.when(n == 0)
            def _():
                dkv_near(t, start)

            @pl.when(live)
            def _():
                dkv_far(start, n - 1, n_left)

            @pl.when(n == last_step)
            def _():
                dkv_end(t)

    work = 2 * half_slots
    events = []

    def due(time, run, *args):
        events.append((max(0, int((time - start_us) / slot_us)), functools.partial(run, *args)))

    start_us, slot_us = (6.0, 1.05)
    due(6.0, turn)
    for k in range(1, span + 1):
        due((22.0, 36.0)[min(k, 2) - 1], level, k)
    times = (
        (7.0, 26.0, 51.0, 61.0, 68.0),
        (10.5, 43.0, 64.0, 74.0, 81.0),
        (14.0, 60.0, 77.0, 87.0, 94.0),
        (17.0, 73.0, 87.0, 95.0, 101.0),
        (20.0, 86.0, 97.5, 106.0, 111.0),
        (22.0, 95.0, 104.0, 110.0, 114.0),
        (23.0, 99.0, 107.0, 111.0, 114.5),
    )
    for u in order:
        core_at, x_at, one_at, two_at, end_at = times[u]
        due(core_at, scatter.core_stage, u)
        due(x_at, scatter.x_stage, u)
        due(one_at, scatter.relay, u, 1)
        due(two_at, scatter.relay, u, 2)
        due(end_at, scatter.settle, u)
    events.sort(key=lambda event: event[0])
    end = max(work, events[-1][0] + 1)

    def slot(w, unused):
        for at, run in events:

            @pl.when(w == at)
            def _(run=run):
                run()

        attention(w)
        return unused

    lax.fori_loop(0, end, slot, 0)
    for u in order:
        scatter.drain(u)
    far_copy.wait()


def backward(
    plan, cycle_size, reach, doc_most, rows, table, aug, masks, q_back, do_wide, own_kv, own_aug,
    near_bias, kv_all, q_all, branch, parts,
):
    lines = cycle_size // 4
    span = min(lines - 1, (reach + 3) // 4)
    pair = q_back.shape[0]
    units_here, model = parts[0].shape
    size = units_here // cycle_size
    units = scatter_units(size)
    shaped = [part.reshape(lines, 2, 2, size, model) for part in parts]
    n = len(units)
    heads = plan.heads
    padded = rows + 2 * PAD
    hbm = pl.BlockSpec(memory_space=pl.ANY)
    dma = pltpu.SemaphoreType.DMA
    return pl.pallas_call(
        functools.partial(backward_kernel, plan, lines, span, reach, doc_most, rows, pair),
        out_shape=[
            jax.ShapeDtypeStruct((pair, WIDE), bf16),
            jax.ShapeDtypeStruct((heads, 32, 128), f32),
            jax.ShapeDtypeStruct((pair, WIDE), bf16),
            jax.ShapeDtypeStruct((pair, WIDE), bf16),
            jax.ShapeDtypeStruct((pair // TQ, 8, TQ), f32),
        ]
        + [jax.ShapeDtypeStruct((size, model), f32)] * 3
        + [
            jax.ShapeDtypeStruct(branch.shape, bf16),
            jax.ShapeDtypeStruct((lines, 2, 2, pair, WIDE), bf16),
        ],
        in_specs=[smem] + [vmem] * 4 + [hbm] * 9,
        out_specs=[vmem] * 8 + [hbm] * 2,
        scratch_shapes=[
            pltpu.VMEM((3, lines, 2, size, model), bf16),
            pltpu.VMEM((3, lines, 2, size, model), bf16),
            pltpu.VMEM((3, lines, size, model), bf16),
            pltpu.VMEM((3, lines, size, model), bf16),
            pltpu.VMEM((3, lines, size, model), bf16),
            pltpu.VMEM((padded, WIDE), bf16),
            pltpu.VMEM((padded, WIDE), bf16),
            pltpu.VMEM((8, padded), f32),
            pltpu.VMEM((2, pair, 2 * plan.cols), bf16),
            pltpu.VMEM((2, pair, 128), bf16),
            pltpu.VMEM((heads, TQ, WIDE), bf16),
            pltpu.VMEM((heads, TQ, WIDE), bf16),
            pltpu.VMEM((heads, TQ, WIDE), f32),
            pltpu.VMEM((heads, TQ, TK), f32),
            pltpu.VMEM((heads, TQ, TK), f32),
            pltpu.VMEM((2, heads, TQ, 128), f32),
            dma((n,)),
            dma((2, n)),
            dma((2, n)),
            dma((2, n, lines)),
            dma((2, n, lines)),
            dma((4,)),
            dma((lines, 2, 2)),
            dma((4, lines)),
            dma((2,)),
            dma((2, lines)),
            dma((2, 2)),
            dma((1 + rows // pair,)),
        ],
        compiler_params=pltpu.CompilerParams(
            vmem_limit_bytes=62 * 2**20, collective_id=1, has_side_effects=True
        ),
        name="backward",
    )(
        table, q_back, do_wide, own_kv, own_aug, near_bias, aug, masks, kv_all, q_all,
        branch, *shaped
    )


def shards(
    tokens,
    doc_lengths,
    key_mask,
    gain_attn,
    w_query,
    w_key,
    w_value,
    w_out,
    bias_table,
    gain_ffn,
    w_gate,
    w_up,
    w_down,
    cotangent,
):
    own_rows, model = tokens.shape
    group = lax.axis_size("wa")
    cycle_size = lax.axis_size("ctx")
    pair = own_rows * group
    heads = bias_table.shape[1]
    docs = doc_lengths.shape[0]
    plan = Plan(heads, w_query.shape[1] // heads, docs)
    total_rows = pair * cycle_size
    doc_most = min(MAXLEN, total_rows // 2)
    reach = min(cycle_size - 1, (doc_most - 1) // pair + 1)
    base = lax.axis_index("ctx") * pair
    rows = min(total_rows, (2 * reach + 1) * pair)
    origin = jnp.clip(base - reach * pair, 0, total_rows - rows).astype(jnp.int32)
    ends = jnp.cumsum(doc_lengths).astype(jnp.int32)
    starts = ends - doc_lengths

    def doc_at(positions):
        return jnp.sum((positions[:, None] >= starts[None, :]).astype(jnp.int32), axis=1) - 1

    tiles = pair // TQ
    tile_start = base + TQ * jnp.arange(tiles, dtype=jnp.int32)
    first_doc = jnp.arange(docs, dtype=jnp.int32)[None, :] == doc_at(tile_start)[:, None]
    last_doc = jnp.arange(docs, dtype=jnp.int32)[None, :] == doc_at(tile_start + TQ - 1)[:, None]
    low_end = jnp.sum(jnp.where(first_doc, starts[None, :], 0), axis=1)
    high_end = jnp.sum(jnp.where(last_doc, ends[None, :], 0), axis=1)
    n_left = jnp.maximum(0, (tile_start - EDGE - low_end + TK - 1) // TK)
    n_right = jnp.maximum(0, (high_end - (tile_start - EDGE + TK) + TK - 1) // TK)
    bounds = jnp.concatenate(
        [(base - origin)[None], jnp.stack([n_left, n_right], axis=1).reshape(-1)]
    ).astype(jnp.int32)

    def window(gathered):
        if rows == total_rows:
            return gathered
        return lax.dynamic_slice_in_dim(gathered, origin, rows, 0)

    gather = functools.partial(lax.all_gather, axis_name="ctx", axis=0, tiled=True)
    (
        pair_normed, pair_tokens, q_wide, own_kv, k_aug, own_aug, near_bias, masks, far_out, kv_all,
    ) = first(
        plan,
        cycle_size,
        reach,
        rows,
        starts,
        bias_table,
        tokens,
        gain_attn[None],
        jnp.broadcast_to(key_mask.astype(f32)[None], (8, pair)),
        w_query,
        w_key,
        w_value,
        w_out,
    )
    masks = masks.reshape(cycle_size, 8, pair)
    cot_late, near_bias = lax.optimization_barrier((cotangent, near_bias))
    pair_cot = lax.all_gather(cot_late, "wa", axis=0, tiled=True)
    if rows < total_rows:
        masks = lax.dynamic_slice_in_dim(masks, origin // pair, rows // pair, 0)
    kv_all = window(kv_all.reshape(total_rows, 2 * plan.cols))
    padded = rows + 2 * PAD
    attended, mixed, q_back = pl.pallas_call(
        functools.partial(fwd_kernel, plan, rows, pair),
        out_shape=(
            jax.ShapeDtypeStruct((pair, WIDE), bf16),
            jax.ShapeDtypeStruct((pair, WIDE), f32),
            jax.ShapeDtypeStruct((pair, WIDE), bf16),
        ),
        in_specs=[smem, smem] + [vmem] * 5,
        out_specs=(vmem, vmem, vmem),
        scratch_shapes=[
            pltpu.VMEM((padded, WIDE), bf16),
            pltpu.VMEM((padded, WIDE), bf16),
            pltpu.VMEM((8, padded), f32),
            pltpu.VMEM((heads, TQ, WIDE), f32),
            pltpu.VMEM((heads, TQ, 128), f32),
            pltpu.VMEM((heads, TQ, WIDE), bf16),
        ],
        compiler_params=params(),
        name="attention_forward",
    )(bounds, bias_table, kv_all, k_aug, masks, q_wide, near_bias)
    q_all = window(gather(q_back))
    hidden, grad_hidden, branch, ffn_part, do_wide, gain_ffn_part, *stacks = middle(
        plan,
        cycle_size,
        attended,
        mixed,
        pair_tokens,
        pair_cot,
        gain_ffn[None],
        w_out,
        far_out,
        w_gate,
        w_up,
        w_down,
    )
    (
        grad_queries, table_part, grad_keys, grad_values, mask_part,
        grad_w_down, grad_w_gate, grad_w_up, far_branch, unused_gathered,
    ) = backward(
        plan,
        cycle_size,
        reach,
        doc_most,
        rows,
        bias_table,
        k_aug,
        masks,
        q_back,
        do_wide,
        own_kv,
        own_aug,
        near_bias,
        kv_all,
        q_all,
        branch,
        stacks,
    )
    grad_w_gate, grad_w_up = (grad_w_gate.T, grad_w_up.T)
    cols = plan.cols
    table_row = jnp.sum(table_part, axis=2).reshape(1, -1)
    table_row = jnp.pad(table_row, ((0, 0), (0, model - table_row.shape[1])))
    small = jnp.concatenate(
        [jnp.zeros((1, model), f32), gain_ffn_part, table_row, jnp.zeros((5, model), f32)],
        axis=0,
    )
    layer_out, grad_tokens, grad_mask, weights, totals = finish(
        plan,
        cycle_size,
        grad_queries,
        grad_keys,
        grad_values,
        mask_part.reshape(group, 8, own_rows),
        w_query.T,
        w_key.T,
        w_value.T,
        pair_normed,
        attended,
        branch,
        far_branch,
        tokens,
        gain_attn[None],
        hidden,
        grad_hidden,
        ffn_part,
        small,
    )
    weights = weights.reshape(4, cols, model).astype(f32)
    return (
        layer_out,
        grad_tokens,
        grad_mask[0],
        totals[0],
        weights[0].T,
        weights[1].T,
        weights[2].T,
        weights[3],
        totals[2, : heads * 32].reshape(heads, 32).T,
        totals[1],
        grad_w_gate,
        grad_w_up,
        grad_w_down,
    )


def solution(mesh):
    placed = (
        P(("ctx", "wa"), None),
        P(),
        P("ctx"),
        P(),
        P(None, "wa"),
        P(None, "wa"),
        P(None, "wa"),
        P("wa", None),
        P(None, "wa"),
        P(),
        P(None, "wa"),
        P(None, "wa"),
        P("wa", None),
        P(("ctx", "wa"), None),
    )
    return jax.shard_map(
        shards,
        mesh=mesh,
        in_specs=placed,
        out_specs=(
            P(("ctx", "wa"), None),
            P(("ctx", "wa"), None),
            P(("ctx", "wa")),
            P(),
            P(None, "wa"),
            P(None, "wa"),
            P(None, "wa"),
            P("wa", None),
            P(None, "wa"),
            P(),
            P(None, ("wa", "ctx")),
            P(None, ("wa", "ctx")),
            P(("wa", "ctx"), None),
        ),
        check_vma=False,
    )
```

```python
import functools

import jax
import jax.numpy as jnp
from jax import lax
from jax.experimental import pallas as pl
from jax.experimental.pallas import tpu as pltpu
from jax.sharding import PartitionSpec as P

MAXLEN = 8192

bucket_edges = (12, 16, 23, 32, 46, 64, 91)
neg_big = -1e30
eps = 1e-06
far_left_bucket = 15
far_right_bucket = 31
WIDE = 256
TQ = 256
TK = 512
EDGE = 128
PAD = TK + EDGE
f32 = jnp.float32
bf16 = jnp.bfloat16


def bucket_of(relative):
    distance = jnp.abs(relative)
    bucket = jnp.minimum(distance, 8) + 16 * (relative > 0).astype(jnp.int32)
    for edge in bucket_edges:
        bucket = bucket + (distance >= edge).astype(jnp.int32)
    return bucket


def norm_forward(inputs, gain):
    inv_root = lax.rsqrt(jnp.mean(inputs * inputs, axis=-1, keepdims=True) + eps)
    return (inputs * inv_root * gain, inv_root)


def norm_backward(inputs, inv_root, gain, grad_normed):
    scaled = gain * grad_normed
    cubed = inv_root * inv_root * inv_root
    grad_inputs = inv_root * scaled - inputs * cubed * jnp.mean(
        inputs * scaled, axis=-1, keepdims=True
    )
    grad_gain = jnp.sum(grad_normed * inputs * inv_root, axis=0)
    return (grad_inputs, grad_gain)


def gated(gate, upward):
    return jax.nn.gelu(gate, approximate=True) * upward


def nt(a, b):
    return lax.dot_general(a, b, (((1,), (1,)), ((), ())), preferred_element_type=f32)


def nn(a, b):
    return lax.dot_general(a, b, (((1,), (0,)), ((), ())), preferred_element_type=f32)


def split3(x):
    hi = x.astype(bf16)
    rest = x - hi.astype(f32)
    mid = rest.astype(bf16)
    return (hi, mid, (rest - mid.astype(f32)).astype(bf16))


class Plan:
    def __init__(self, heads, width, docs):
        self.heads = heads
        self.width = width
        self.bits = max(1, (docs - 1).bit_length())
        self.cols = heads * width
        self.mask_lane = self.cols
        self.doc_lane = self.cols + 1
        self.stat_lane = self.doc_lane + 2 * self.bits
        assert self.stat_lane + 3 * heads <= WIDE and self.cols + 64 == WIDE and width == 64

    def key_lanes(self, lane, h):
        own = (lane >= h * self.width) & (lane < (h + 1) * self.width)
        aug = (lane >= self.mask_lane) & (lane < self.stat_lane)
        stat = (lane >= self.stat_lane + 3 * h) & (lane < self.stat_lane + 3 * h + 3)
        return own | aug | stat

    def value_lanes(self, lane, h):
        own = (lane >= 64 + h * self.width) & (lane < 64 + (h + 1) * self.width)
        return own | ((lane >= 3 * h) & (lane < 3 * h + 3))


def lanes_of(rows, width=WIDE):
    return lax.broadcasted_iota(jnp.int32, (rows, width), 1)


def near_lanes(heads, table_ref, near_ref):
    row = lax.broadcasted_iota(jnp.int32, (EDGE, 3 * EDGE), 0)
    col = lax.broadcasted_iota(jnp.int32, (EDGE, 3 * EDGE), 1)
    relative = col - EDGE - row
    for flip in range(2):
        bucket = bucket_of(-relative if flip else relative)
        left, right = (far_left_bucket, far_right_bucket)
        if flip:
            left, right = (right, left)
        for h in range(heads):
            base = jnp.full((EDGE, 3 * EDGE), table_ref[0, h], f32)
            for b in range(1, 32):
                base = jnp.where(bucket == b, table_ref[b, h], base)
            far_l = jnp.full((EDGE, EDGE), table_ref[left, h], f32)
            far_r = jnp.full((EDGE, EDGE), table_ref[right, h], f32)
            near_ref[flip, h, :EDGE, : 3 * EDGE] = base
            near_ref[flip, h, :EDGE, 3 * EDGE :] = far_r
            near_ref[flip, h, EDGE:, EDGE:] = base
            near_ref[flip, h, EDGE:, :EDGE] = far_l


def build_keys(plan, g_ref, kaug_ref, masks_ref, km, vm, mask_row, rows):
    mask_row[...] = jnp.zeros_like(mask_row)
    size = masks_ref.shape[2]
    for n in range(masks_ref.shape[0]):
        mask_row[:, PAD + n * size : PAD + (n + 1) * size] = masks_ref[n]
    km[:PAD, :] = jnp.broadcast_to(
        jnp.where(pad_lanes(plan), neg_big, 0.0).astype(bf16), (PAD, WIDE)
    )
    km[pl.ds(PAD + rows, PAD), :] = km[:PAD, :]
    vm[:PAD, :] = jnp.zeros((PAD, WIDE), bf16)
    vm[pl.ds(PAD + rows, PAD), :] = jnp.zeros((PAD, WIDE), bf16)
    step = 512
    low = lanes_of(step, 128) < 64
    ones = (lanes_of(step, 128) < 3 * plan.heads).astype(bf16)

    def body(n, unused):
        at = pl.multiple_of(n * step, step)
        to = pl.multiple_of(PAD + n * step, 128)
        middle = g_ref[pl.ds(at, step), 128:256]
        km[pl.ds(to, step), 0:128] = g_ref[pl.ds(at, step), 0:128]
        km[pl.ds(to, step), 128:256] = jnp.where(low, middle, kaug_ref[pl.ds(at, step), :])
        vm[pl.ds(to, step), 0:128] = jnp.where(low, ones, middle)
        vm[pl.ds(to, step), 128:256] = g_ref[pl.ds(at, step), 256:384]
        return unused

    lax.fori_loop(0, rows // step, body, 0)


def far_span(start, n, n_left, left_bucket, right_bucket):
    on_left = n < n_left
    at = start + PAD - EDGE + TK * jnp.where(on_left, -1 - n, 1 + n - n_left)
    bucket = jnp.where(on_left, left_bucket, right_bucket)
    return pl.ds(pl.multiple_of(at, 128), TK), bucket


def pad_lanes(plan):
    lane = lanes_of(1)
    return (lane >= plan.doc_lane) & (lane < plan.stat_lane)


def fwd_kernel(
    plan, rows, pair, bounds, table_ref, g_ref, kaug_ref, masks_ref, q_ref, near_ref,
    low_ref, wide_ref, qb_ref, km, vm, mask_row, acc, row_max, qh_ref,
):
    build_keys(plan, g_ref, kaug_ref, masks_ref, km, vm, mask_row, rows)
    lane = lanes_of(TQ)

    def tile(t, unused):
        start = pl.multiple_of(bounds[0] + t * TQ, 128)
        n_left, n_right = (bounds[1 + 2 * t], bounds[2 + 2 * t])
        out = pl.ds(pl.multiple_of(t * TQ, TQ), TQ)
        q = q_ref[out, :]
        near = pl.ds(pl.multiple_of(start + PAD - EDGE, 128), TK)
        for h in range(plan.heads):
            qh = jnp.where(plan.key_lanes(lane, h), q, jnp.zeros_like(q))
            qh_ref[h] = qh
            s = nt(qh, km[near, :]) + near_ref[0, h] + mask_row[0:1, near]
            top = jnp.max(s, axis=1, keepdims=True)
            p = jnp.exp(s - top).astype(bf16)
            acc[h] = nn(p, vm[near, :])
            row_max[h] = jnp.broadcast_to(top, (TQ, 128))

        def far(n, unused):
            span, bucket = far_span(start, n, n_left, far_left_bucket, far_right_bucket)
            if True:
                for h in range(plan.heads):
                    s = nt(qh_ref[h], km[span, :]) + mask_row[0:1, span]
                    offset = table_ref[bucket, h]
                    old = row_max[h][:, :1]
                    top = jnp.maximum(old, jnp.max(s, axis=1, keepdims=True) + offset)
                    p = jnp.exp(s - (top - offset)).astype(bf16)
                    acc[h] = acc[h] * jnp.exp(old - top) + nn(p, vm[span, :])
                    row_max[h] = jnp.broadcast_to(top, (TQ, 128))
            return unused

        lax.fori_loop(0, n_left + n_right, far, 0)

        wide = jnp.zeros((TQ, WIDE), f32)
        qb = jnp.where(lane < plan.stat_lane, q, jnp.zeros_like(q))
        for h in range(plan.heads):
            total = acc[h][:, 3 * h : 3 * h + 1]
            log_total = row_max[h][:, :1] + jnp.log(total)
            wide = jnp.where(lane // 64 == h + 1, acc[h] / total, wide)
            for i, part in enumerate(split3(-log_total)):
                qb = jnp.where(lane == plan.stat_lane + 3 * h + i, part, qb)
        wide_ref[out, :] = wide
        low_ref[out, :] = wide.astype(bf16)
        qb_ref[out, :] = qb
        return unused

    lax.fori_loop(0, pair // TQ, tile, 0)


vmem = pl.BlockSpec(memory_space=pltpu.VMEM)
smem = pl.BlockSpec(memory_space=pltpu.SMEM)


def params():
    return pltpu.CompilerParams(vmem_limit_bytes=56 * 2**20)


class Spot:
    def __init__(self, lines):
        index = lax.axis_index("ctx")
        self.wa = lax.axis_index("wa")
        self.index = index
        self.lines = lines
        self.z = index // 4
        self.x = (index // 2) % 2
        self.core = index % 2

    def core_mate(self):
        return (self.index + 1 - 2 * self.core, self.wa)

    def x_mate(self):
        return (self.index + 2 - 4 * self.x, self.wa)

    def z_mate(self, step):
        return (jnp.clip(self.index + 4 * step, 0, 4 * self.lines - 1), self.wa)

    def y_mate(self):
        return (self.index, 1 - self.wa)


def send(src, dst, send_sem, recv_sem, device):
    return pltpu.make_async_remote_copy(
        src_ref=src,
        dst_ref=dst,
        send_sem=send_sem,
        recv_sem=recv_sem,
        device_id=device,
        device_id_type=pl.DeviceIdType.MESH,
    )


def greet(spot, with_y):
    barrier = pltpu.get_barrier_semaphore()
    mates = [spot.core_mate(), spot.x_mate()] + ([spot.y_mate()] if with_y else [])
    for mate in mates:
        pl.semaphore_signal(barrier, inc=1, device_id=mate, device_id_type=pl.DeviceIdType.MESH)

    @pl.when(spot.z + 1 < spot.lines)
    def _():
        pl.semaphore_signal(
            barrier, inc=1, device_id=spot.z_mate(1), device_id_type=pl.DeviceIdType.MESH
        )

    @pl.when(spot.z > 0)
    def _():
        pl.semaphore_signal(
            barrier, inc=1, device_id=spot.z_mate(-1), device_id_type=pl.DeviceIdType.MESH
        )

    above = (spot.z + 1 < spot.lines).astype(jnp.int32)
    below = (spot.z > 0).astype(jnp.int32)
    pl.semaphore_wait(barrier, len(mates) + above + below)


def added(a, b):
    return a + b


def first_kernel(
    plan, lines, span, reach, rows, starts, table_ref, tokens_ref, gain_ref, mask_ref,
    wq_hbm, wk_hbm, wv_hbm, wo_hbm,
    x_ref, tok_ref, q_ref, own_ref, aug_ref, own_aug_ref, near_ref, masks_ref, wo_far_hbm, all_hbm,
    weights, zeros, load_sem, y_sem, own_sem, zero_sem, z_sem, x_sem, c_sem,
):
    spot = Spot(lines)
    z, x, core, wa = (spot.z, spot.x, spot.core, spot.wa)
    half, model = tokens_ref.shape
    cols = plan.cols
    chunk = half // 4
    loads = [
        pltpu.make_async_copy(src, weights.at[pl.ds(i * cols, cols)], load_sem.at[i])
        for i, src in enumerate((wk_hbm, wv_hbm, wq_hbm))
    ]
    for load in loads:
        load.start()
    greet(spot, True)
    zeros[...] = jnp.zeros_like(zeros)

    def outside(d):
        return (d < z - span) | (d > z + span)

    def zero_copies(d):
        return [
            pltpu.make_async_copy(zeros, all_hbm.at[d, a, b], zero_sem.at[d, a, b])
            for a in range(2)
            for b in range(2)
        ]

    def zero_start(d, unused):
        @pl.when(outside(d))
        def _():
            masks_ref[d] = jnp.zeros((2, 2) + mask_ref.shape, f32)
            for copy in zero_copies(d):
                copy.start()

        return unused

    def rows_at(start, size):
        return pl.ds(pl.multiple_of(start, size), size)

    ours = wa * half
    theirs = (1 - wa) * half

    def y_copy(i, base):
        return send(
            tokens_ref.at[rows_at(i * chunk, chunk)],
            tok_ref.at[rows_at(base + i * chunk, chunk)],
            y_sem.at[0, i],
            y_sem.at[1, i],
            spot.y_mate(),
        )

    def y_start(i, unused):
        y_copy(i, ours).start()
        return unused

    lax.fori_loop(0, 4, y_start, 0)
    far_copy = send(wo_hbm, wo_far_hbm, y_sem.at[0, 4], y_sem.at[1, 4], spot.y_mate())

    def scaled(rows_in):
        rows_in = rows_in.astype(f32)
        inv = lax.rsqrt(jnp.mean(rows_in * rows_in, axis=-1, keepdims=True) + eps)
        return (rows_in * inv * gain_ref[...]).astype(bf16)

    def normal(i, unused):
        at = rows_at(ours + i * chunk, chunk)
        rows_in = tokens_ref[rows_at(i * chunk, chunk), :]
        tok_ref[at, :] = rows_in
        x_ref[at, :] = scaled(rows_in)
        return unused

    lax.fori_loop(0, 4, normal, 0)
    for load in loads:
        load.wait()

    def project(base):
        rows = rows_at(base, half)
        qkv = nt(x_ref[rows, :], weights[...]).astype(bf16)
        own_ref[rows, :] = qkv[:, : 2 * cols]
        q_ref[rows, :cols] = qkv[:, 2 * cols :]

    pieces = [
        (ours, half, True),
        (theirs, half // 2, True),
        (theirs + half // 2, half // 2, False),
        None,
    ]
    mask_piece = 3

    def line_first(p):
        return p == mask_piece or pieces[p][2]

    def piece_rows(p):
        return rows_at(pieces[p][0], pieces[p][1])

    def source(p, d, a):
        if p == mask_piece:
            return masks_ref.at[d, a, core]
        return all_hbm.at[d, a, core, piece_rows(p)]

    def own_source(p):
        return mask_ref if p == mask_piece else own_ref.at[piece_rows(p)]

    def pass_copy(p, step, d, own):
        i = 0 if step > 0 else 1
        if line_first(p):
            dst = source(p, d, x)
            src = own_source(p) if own else dst
        else:
            dst = all_hbm.at[d, :, core, piece_rows(p)]
            src = dst
        return send(src, dst, z_sem.at[p, i, d], z_sem.at[p, 2 + i, d], spot.z_mate(step))

    def across(p, d, own):
        dst = source(p, d, x)
        src = own_source(p) if own else dst
        return send(src, dst, x_sem.at[p, 0, d], x_sem.at[p, 1, d], spot.x_mate())

    def beside(p, d):
        if p == mask_piece:
            part = masks_ref.at[d, :, core]
        else:
            part = all_hbm.at[d, :, core, piece_rows(p)]
        return send(part, part, c_sem.at[p, 0, d], c_sem.at[p, 1, d], spot.core_mate())

    def own_copy(p):
        return pltpu.make_async_copy(
            own_source(p), source(p, z, x), own_sem.at[p]
        )

    def both_ways(p, own):
        @pl.when(z + 1 < lines)
        def _():
            pass_copy(p, 1, z, own).start()

        @pl.when(z > 0)
        def _():
            pass_copy(p, -1, z, own).start()

    def begin(p):
        own_copy(p).start()
        across(p, z, True).start()
        if line_first(p):
            both_ways(p, True)

    def level(p, k):
        @pl.when(z - k >= 0)
        def _():
            d = jnp.maximum(z - k, 0)
            pass_copy(p, 1, d, False).wait_recv()
            if k < span:

                @pl.when(z + 1 < lines)
                def _():
                    pass_copy(p, 1, d, False).start()

            if line_first(p):
                across(p, d, False).start()
            else:
                beside(p, d).start()

        @pl.when(z + k < lines)
        def _():
            d = jnp.minimum(z + k, lines - 1)
            pass_copy(p, -1, d, False).wait_recv()
            if k < span:

                @pl.when(z > 0)
                def _():
                    pass_copy(p, -1, d, False).start()

            if line_first(p):
                across(p, d, False).start()
            else:
                beside(p, d).start()

    def turn(p):
        across(p, z, True).wait()
        own_copy(p).wait()
        both_ways(p, False)
        beside(p, z).start()

    def settle(p, k):
        for sign in (1, -1) if k else (1,):
            d = z - sign * k

            @pl.when((d >= 0) & (d < lines))
            def _(d=d):
                d = jnp.clip(d, 0, lines - 1)
                across(p, d, k == 0).wait()
                if k == 0:
                    own_copy(p).wait()
                beside(p, d).start()

    def doc_of(start, size):
        position = start + lax.broadcasted_iota(jnp.int32, (size, 128), 0)

        def count(e, total):
            return total + (position >= starts[e]).astype(jnp.int32)

        return lax.fori_loop(1, starts.shape[0], count, jnp.zeros((size, 128), jnp.int32))

    def code_lanes(start, size):
        lane = lanes_of(size, 128) + 128
        code = jnp.maximum(lane - plan.doc_lane, 0)
        bit = jnp.bitwise_and(jnp.right_shift(doc_of(start, size), code // 2), 1)
        coded = (lane >= plan.doc_lane) & (lane < plan.stat_lane)
        ones = (lane >= plan.stat_lane) & (lane < plan.stat_lane + 3 * plan.heads)
        return lane, coded, bit != code % 2, ones

    pair = 2 * half
    base = spot.index * pair
    origin = jnp.clip(base - reach * pair, 0, 4 * lines * pair - rows)

    def key_lanes(n, unused):
        at = rows_at(n * half, half)
        lane, coded, differs, ones = code_lanes(origin + n * half, half)
        aug_ref[at, :] = jnp.where(
            coded & differs, neg_big, jnp.where(ones, 1.0, 0.0)
        ).astype(bf16)
        return unused

    def own_lanes(n, unused):
        at = rows_at(n * half, half)
        lane, coded, differs, ones = code_lanes(base + n * half, half)
        column = jnp.transpose(
            jnp.broadcast_to(mask_ref[0:1, at], (128, half))
        )
        own_aug_ref[at, :] = jnp.where(
            lane == plan.mask_lane,
            column,
            jnp.where(coded & differs, neg_big, jnp.where(ones, 1.0, 0.0)),
        ).astype(bf16)
        tail = jnp.where(
            (lane == plan.mask_lane) | (coded & ~differs), 1.0, 0.0
        ).astype(bf16)
        q_ref[at, 128:] = tail
        return unused

    begin(mask_piece)
    lax.fori_loop(0, 2, own_lanes, 0)
    project(ours)
    begin(0)
    lax.fori_loop(0, lines, zero_start, 0)
    near_lanes(plan.heads, table_ref, near_ref)
    lax.fori_loop(0, rows // half, key_lanes, 0)

    def y_wait(i, unused):
        y_copy(i, theirs).wait_recv()
        at = rows_at(theirs + i * chunk, chunk)
        x_ref[at, :] = scaled(tok_ref[at, :])
        return unused

    lax.fori_loop(0, 2, y_wait, 0)
    level(0, 1)
    level(mask_piece, 1)
    lax.fori_loop(2, 4, y_wait, 0)
    far_copy.start()
    project(theirs)
    begin(2)
    begin(1)
    if span > 1:
        level(0, 2)
        level(mask_piece, 2)
    settle(0, 0)
    settle(mask_piece, 0)
    turn(2)
    level(1, 1)
    settle(0, 1)
    settle(mask_piece, 1)
    level(2, 1)
    if span > 1:
        level(1, 2)
        settle(0, 2)
        settle(mask_piece, 2)
    settle(1, 0)
    settle(1, 1)
    if span > 1:
        level(2, 2)
        settle(1, 2)
    for k in range(3, span + 1):
        for p in range(4):
            level(p, k)
        for p in (0, 1, mask_piece):
            settle(p, k)

    def finish_line(d, unused):
        @pl.when(~outside(d))
        def _():
            for p in range(4):
                beside(p, d).wait()

        @pl.when(outside(d))
        def _():
            for copy in zero_copies(d):
                copy.wait()

        for p in range(4):

            @pl.when((z + 1 < lines) & (d <= z) & (d > z - span))
            def _(p=p):
                pass_copy(p, 1, d, False).wait_send()

            @pl.when((z > 0) & (d >= z) & (d < z + span))
            def _(p=p):
                pass_copy(p, -1, d, False).wait_send()

        return unused

    lax.fori_loop(0, lines, finish_line, 0)

    def y_drain(i, unused):
        y_copy(i, ours).wait_send()
        return unused

    lax.fori_loop(0, 4, y_drain, 0)
    far_copy.wait()


def first(
    plan, cycle_size, reach, rows, starts, table, tokens, gain, mask, w_query, w_key, w_value, w_out
):
    lines = cycle_size // 4
    span = min(lines - 1, (reach + 3) // 4)
    half, model = tokens.shape
    pair = 2 * half
    hbm = pl.BlockSpec(memory_space=pl.ANY)
    dma = pltpu.SemaphoreType.DMA
    return pl.pallas_call(
        functools.partial(first_kernel, plan, lines, span, reach, rows),
        out_shape=[
            jax.ShapeDtypeStruct((pair, model), bf16),
            jax.ShapeDtypeStruct((pair, model), bf16),
            jax.ShapeDtypeStruct((pair, WIDE), bf16),
            jax.ShapeDtypeStruct((pair, 2 * plan.cols), bf16),
            jax.ShapeDtypeStruct((rows, 128), bf16),
            jax.ShapeDtypeStruct((pair, 128), bf16),
            jax.ShapeDtypeStruct((2, plan.heads, TQ, TK), f32),
            jax.ShapeDtypeStruct((lines, 2, 2, 8, pair), f32),
            jax.ShapeDtypeStruct(w_out.shape, bf16),
            jax.ShapeDtypeStruct((lines, 2, 2, pair, 2 * plan.cols), bf16),
        ],
        in_specs=[smem] * 2 + [vmem] * 3 + [hbm] * 4,
        out_specs=[vmem] * 8 + [hbm] * 2,
        scratch_shapes=[
            pltpu.VMEM((3 * plan.cols, model), bf16),
            pltpu.VMEM((pair, 2 * plan.cols), bf16),
            dma((3,)),
            dma((2, 5)),
            dma((4,)),
            dma((lines, 2, 2)),
            dma((4, 4, lines)),
            dma((4, 2, lines)),
            dma((4, 2, lines)),
        ],
        compiler_params=pltpu.CompilerParams(
            vmem_limit_bytes=56 * 2**20, collective_id=4, has_side_effects=True
        ),
        name="project_gather",
    )(starts, table, tokens, gain, mask, w_query.T, w_key.T, w_value.T, w_out)


def tn(a, b):
    return lax.dot_general(a, b, (((0,), (0,)), ((), ())), preferred_element_type=f32)


def line_relay(spot, start, receive):
    def level(k, unused):
        @pl.when(spot.z - k >= 0)
        def _():
            if_first(k, lambda: receive(1, spot.z - k))

            @pl.when(spot.z + 1 < spot.lines)
            def _():
                start(1, spot.z - k)

        @pl.when(spot.z + k < spot.lines)
        def _():
            if_first(k, lambda: receive(-1, spot.z + k))

            @pl.when(spot.z > 0)
            def _():
                start(-1, spot.z + k)

        return unused

    def if_first(k, run):
        @pl.when(k > 0)
        def _():
            run()

    return level


def finish_kernel(
    plan, lines, dq_ref, dk_ref, dv_ref, mask_ref, wq_hbm, wk_hbm, wv_hbm, normed_ref, att_ref, branch_ref, far_ref,
    tokens_ref, gain_ref, gh_ref, small_ref,
    gt_ref, gm_ref, weights_ref, total_ref,
    w3_ref, load_sem, lefts, rights, product, mine, core_in, x_in, up_in, down_in, all_w, y_out, y_in, own_part, mask_in,
    small_own, small_y, small_core, small_x, small_all,
    y_sem, core_sem, x_sem, up_sem, down_sem, gz_sem, gx_sem, gc_sem, sz_sem,
):
    spot = Spot(lines)
    z, x, core, wa = (spot.z, spot.x, spot.core, spot.wa)
    cols = plan.cols
    loads = [
        pltpu.make_async_copy(src, w3_ref.at[pl.ds(at, cols)], load_sem.at[i])
        for i, (src, at) in enumerate(((wq_hbm, 0), (wk_hbm, WIDE), (wv_hbm, 3 * WIDE - cols)))
    ]
    for load in loads:
        load.start()
    gap = jnp.zeros((WIDE - cols, tokens_ref.shape[1]), bf16)
    w3_ref[cols:WIDE] = gap
    w3_ref[WIDE + cols : 2 * WIDE] = gap
    w3_ref[2 * WIDE : 3 * WIDE - cols] = gap
    greet(spot, True)
    for load in loads:
        load.wait()
    half = tokens_ref.shape[0]
    quarter = half // 2
    model = tokens_ref.shape[1]
    rows = mine.shape[3]

    def grad_rows(at):
        at = pl.ds(pl.multiple_of(at, quarter), quarter)
        return (
            nn(dq_ref[at, :], w3_ref[0:256])
            + nn(dk_ref[at, :], w3_ref[256:512])
            + nn(dv_ref[at, :], w3_ref[512:768])
        )

    def y_copy(i):
        return send(y_out.at[i], y_in.at[i], y_sem.at[0, i], y_sem.at[1, i], spot.y_mate())

    def theirs(i, unused):
        y_out[i] = grad_rows((1 - wa) * half + i * quarter).astype(bf16)
        y_copy(i).start()
        return unused

    lax.fori_loop(0, 2, theirs, 0)
    mask_copy = send(
        mask_ref.at[1 - wa], mask_in, y_sem.at[0, 2], y_sem.at[1, 2], spot.y_mate()
    )
    mask_copy.start()

    our_rows = pl.ds(pl.multiple_of(wa * half, half), half)
    their_rows = pl.ds(pl.multiple_of((1 - wa) * half, half), half)
    lefts[0] = dq_ref[...]
    lefts[1] = dk_ref[...]
    lefts[2] = dv_ref[...]
    lefts[3] = att_ref[...]
    rights[0] = normed_ref[...]
    rights[1, our_rows, :] = branch_ref[...]
    rights[1, their_rows, :] = far_ref[...]
    per = plan.cols // rows

    def core_copy(m):
        part = pl.ds(m * per // 4, per // 4)
        return send(
            mine.at[part, :, 1 - core],
            core_in.at[part],
            core_sem.at[0, m],
            core_sem.at[1, m],
            spot.core_mate(),
        )

    def fill(i, unused):
        m = (3 * i) % 4
        product[...] = tn(lefts[m], rights[m // 3]).astype(bf16)

        def place(offset):
            for j in range(per):
                mine[m * per // 4 + j // 4, (j // 2) % 2, j % 2] = product[
                    offset + j * rows : offset + (j + 1) * rows, :
                ]

        @pl.when(m < 2)
        def _():
            place(0)

        @pl.when(m >= 2)
        def _():
            place(WIDE - plan.cols)

        core_copy(m).start()
        return unused

    lax.fori_loop(0, 4, fill, 0)
    def x_copy(d):
        return send(
            mine.at[d, 1 - x, core], x_in.at[d], x_sem.at[0, d], x_sem.at[1, d], spot.x_mate()
        )

    def core_add(d, unused):
        mine[d, 1 - x, core] = added(mine[d, 1 - x, core], core_in[d, 1 - x])
        x_copy(d).start()
        return unused

    def ours(i, unused):
        own_part[pl.ds(pl.multiple_of(i * quarter, quarter), quarter), :] = grad_rows(
            wa * half + i * quarter
        )
        return unused

    def core_stage(i, unused):
        m = (3 * i) % 4
        core_copy(m).wait()
        lax.fori_loop(m * per // 4, (m + 1) * per // 4, core_add, 0)
        return unused

    lax.fori_loop(0, 4, core_stage, 0)

    def core_add_own(d, unused):
        mine[d, x, core] = added(mine[d, x, core], core_in[d, x])
        return unused

    lax.fori_loop(0, lines, core_add_own, 0)
    lax.fori_loop(0, 2, ours, 0)

    gain_sum = jnp.zeros((1, model), f32)
    step = 32
    for i in range(2):
        y_copy(i).wait()

        def normal(j, total, i=i):
            at = pl.ds(pl.multiple_of(i * quarter + j * step, step), step)
            there = pl.ds(pl.multiple_of(j * step, step), step)
            grad = own_part[at, :] + y_in[i, there, :].astype(f32)
            rows_in = tokens_ref[at, :].astype(f32)
            inv = lax.rsqrt(jnp.mean(rows_in * rows_in, axis=-1, keepdims=True) + eps)
            scaled = gain_ref[...] * grad
            mean = jnp.mean(rows_in * scaled, axis=-1, keepdims=True)
            gt_ref[at, :] = gh_ref[at, :] + inv * scaled - rows_in * (inv * inv * inv * mean)
            return total + jnp.sum(grad * rows_in * inv, axis=0, keepdims=True)

        gain_sum = lax.fori_loop(0, quarter // step, normal, gain_sum)
    small_own[...] = small_ref[...]
    small_own[0:1, :] = gain_sum
    small_copy = send(
        small_own, small_y, y_sem.at[0, 4], y_sem.at[1, 4], spot.y_mate()
    )
    small_copy.start()
    mask_copy.wait()
    gm_ref[...] = mask_ref[wa] + mask_in[...]

    def flow(step, d):
        ring, sem = (up_in, up_sem) if step > 0 else (down_in, down_sem)
        return send(
            mine.at[d, x, core], ring.at[d], sem.at[0, d], sem.at[1, d], spot.z_mate(step)
        )

    def merge(step, d):
        flow(step, d).wait_recv()
        ring = up_in if step > 0 else down_in
        mine[d, x, core] = added(mine[d, x, core], ring[d])

    def x_add(i, unused):
        d = (i * (lines - 1)) % lines
        x_copy(d).wait()
        mine[d, x, core] = added(mine[d, x, core], x_in[d])

        @pl.when((z == 0) & (d > 0))
        def _():
            flow(1, d).start()

        @pl.when((z == lines - 1) & (d < lines - 1))
        def _():
            flow(-1, d).start()

        return unused

    lax.fori_loop(0, lines, x_add, 0)
    small_copy.wait()
    row = lax.broadcasted_iota(jnp.int32, small_own.shape, 0)
    small_x[0] = small_own[...] + jnp.where(row < 2, small_y[...], 0.0)
    small_core_copy = send(
        small_x.at[0], small_core, core_sem.at[0, 4], core_sem.at[1, 4], spot.core_mate()
    )
    small_core_copy.start()

    def relay(k, unused):
        high = lines - 1 - k

        @pl.when((z < high) & (z > 0))
        def _():
            merge(1, high)
            flow(1, high).start()

        @pl.when((z > k) & (z + 1 < lines))
        def _():
            merge(-1, k)
            flow(-1, k).start()

        return unused

    lax.fori_loop(0, lines - 1, relay, 0)
    small_core_copy.wait()
    small_x[1] = small_x[0] + small_core[...]
    small_x_copy = send(
        small_x.at[1], small_x.at[2], x_sem.at[0, lines], x_sem.at[1, lines], spot.x_mate()
    )
    small_x_copy.start()

    @pl.when(z > 0)
    def _():
        merge(1, z)

    @pl.when(z + 1 < lines)
    def _():
        merge(-1, z)

    all_w[z, x, core] = mine[z, x, core]

    def pass_w(step, d):
        i = 0 if step > 0 else 1
        return send(
            all_w.at[d, x, core], all_w.at[d, x, core], gz_sem.at[i, d], gz_sem.at[2 + i, d],
            spot.z_mate(step),
        )

    def pass_s(step, d):
        i = 0 if step > 0 else 1
        return send(
            small_all.at[d], small_all.at[d], sz_sem.at[i, d], sz_sem.at[2 + i, d],
            spot.z_mate(step),
        )

    def across(d):
        return send(
            all_w.at[d, x, core], all_w.at[d, x, core], gx_sem.at[0, d], gx_sem.at[1, d],
            spot.x_mate(),
        )

    def beside(d):
        return send(
            all_w.at[d, :, core], all_w.at[d, :, core], gc_sem.at[0, d], gc_sem.at[1, d],
            spot.core_mate(),
        )

    small_x_copy.wait()
    small_all[z] = small_x[1] + small_x[2]

    def receive(step, d):
        pass_w(step, d).wait_recv()
        across(d).start()

    across(z).start()
    lax.fori_loop(
        0, lines, line_relay(spot, lambda s, d: pass_w(s, d).start(), receive), 0
    )
    lax.fori_loop(
        0,
        lines,
        line_relay(
            spot, lambda s, d: pass_s(s, d).start(), lambda s, d: pass_s(s, d).wait_recv()
        ),
        0,
    )

    def add_small(d, total):
        return total + small_all[d]

    total_ref[...] = lax.fori_loop(1, lines, add_small, small_all[0])
    def spread(d, unused):
        across(d).wait()
        beside(d).start()
        return unused

    lax.fori_loop(0, lines, spread, 0)

    def copy_out(d, unused):
        beside(d).wait()
        weights_ref[d] = all_w[d]
        return unused

    lax.fori_loop(0, lines, copy_out, 0)

    def drain(d, unused):
        @pl.when((z < d))
        def _():
            flow(1, d).wait_send()

        @pl.when((z > d))
        def _():
            flow(-1, d).wait_send()

        @pl.when((d <= z) & (z + 1 < lines))
        def _():
            pass_w(1, d).wait_send()
            pass_s(1, d).wait_send()

        @pl.when((d >= z) & (z > 0))
        def _():
            pass_w(-1, d).wait_send()
            pass_s(-1, d).wait_send()

        return unused

    lax.fori_loop(0, lines, drain, 0)


def finish(plan, cycle_size, *operands):
    lines = cycle_size // 4
    half, model = operands[11].shape
    rows = 4 * plan.cols // cycle_size
    dma = pltpu.SemaphoreType.DMA
    return pl.pallas_call(
        functools.partial(finish_kernel, plan, lines),
        out_shape=[
            jax.ShapeDtypeStruct((half, model), f32),
            jax.ShapeDtypeStruct((8, half), f32),
            jax.ShapeDtypeStruct((lines, 2, 2, rows, model), bf16),
            jax.ShapeDtypeStruct((8, model), f32),
        ],
        in_specs=[vmem] * 4
        + [pl.BlockSpec(memory_space=pl.ANY)] * 3
        + [vmem] * (len(operands) - 7),
        out_specs=[vmem] * 4,
        scratch_shapes=[
            pltpu.VMEM((3 * WIDE, model), bf16),
            dma((3,)),
            pltpu.VMEM((4, 2 * half, WIDE), bf16),
            pltpu.VMEM((2, 2 * half, model), bf16),
            pltpu.VMEM((WIDE, model), bf16),
            pltpu.VMEM((lines, 2, 2, rows, model), bf16),
            pltpu.VMEM((lines, 2, rows, model), bf16),
            pltpu.VMEM((lines, rows, model), bf16),
            pltpu.VMEM((lines, rows, model), bf16),
            pltpu.VMEM((lines, rows, model), bf16),
            pltpu.VMEM((lines, 2, 2, rows, model), bf16),
            pltpu.VMEM((2, half // 2, model), bf16),
            pltpu.VMEM((2, half // 2, model), bf16),
            pltpu.VMEM((half, model), f32),
            pltpu.VMEM((8, half), f32),
            pltpu.VMEM((8, model), f32),
            pltpu.VMEM((8, model), f32),
            pltpu.VMEM((8, model), f32),
            pltpu.VMEM((3, 8, model), f32),
            pltpu.VMEM((lines, 8, model), f32),
            dma((2, 5)),
            dma((2, 5)),
            dma((2, lines + 1)),
            dma((2, lines)),
            dma((2, lines)),
            dma((4, lines)),
            dma((2, lines)),
            dma((2, lines)),
            dma((4, lines)),
        ],
        compiler_params=pltpu.CompilerParams(
            vmem_limit_bytes=58 * 2**20, collective_id=2, has_side_effects=True
        ),
        name="finish",
    )(*operands)


root = 0.7978845608028654
cubic = 0.044715


def middle_kernel(
    plan, cycle_size, att_ref, mixed_ref, tokens_ref, cot_ref, gain_ref,
    wo_hbm, wo_far_hbm, wg_hbm, wu_hbm, wd_hbm,
    hidden_ref, gh_ref, branch_ref, ffn_ref, ffn_far_ref, do_ref, gain_part_ref, *refs,
):
    stacks, refs = (refs[:3], refs[3:])
    (
        wg, wu, wd, wo, inner, gg, gu, x_ref, att_in, d_out, d_in, e_out, e_in,
        acc_f, acc_g, rows_buf, load_sem, y_sem, out_sem,
    ) = refs
    spot = Spot(cycle_size // 4)
    wa = spot.wa
    pair, model = tokens_ref.shape
    half = pair // 2
    units = wd.shape[1]
    chunk = half // 4
    block = pair // 4
    loads = [
        pltpu.make_async_copy(src, dst, load_sem.at[i])
        for i, (src, dst) in enumerate(
            (
                (wo_hbm, wo.at[0, 64:]),
                (wo_far_hbm, wo.at[1, 64:]),
                (wg_hbm, wg),
                (wu_hbm, wu),
                (wd_hbm, wd),
            )
        )
    ]
    for load in loads:
        load.start()
    barrier = pltpu.get_barrier_semaphore()
    pl.semaphore_signal(
        barrier, inc=1, device_id=spot.y_mate(), device_id_type=pl.DeviceIdType.MESH
    )
    wo[:, :64, :] = jnp.zeros((2, 64, model), bf16)
    pl.semaphore_wait(barrier, 1)
    ours = wa * half
    theirs = (1 - wa) * half

    def rows_at(start, size):
        return pl.ds(pl.multiple_of(start, size), size)

    def a_start(i):
        return (theirs + i * block) if i < 2 else (ours + (i - 2) * block)

    def a_copy(i, base):
        at = rows_at(base + (i % 2) * block, block)
        return send(att_ref.at[at], att_in.at[at], y_sem.at[0, i], y_sem.at[1, i], spot.y_mate())

    order = (0, 1, 2, 3)
    for i in order:
        a_copy(i, ours if i < 2 else theirs).start()
    loads[0].wait()
    loads[1].wait()

    def normal(i, base, keep):
        a_copy(i, base).wait_recv()
        at = rows_at(base + (i % 2) * block, block)
        branch = nn(att_ref[at, :], wo[0]) + nn(att_in[at, :], wo[1])
        hidden = tokens_ref[at, :].astype(f32) + branch
        if keep:
            hidden_ref[(i % 2) * block : (i % 2 + 1) * block, :] = hidden
        inv = lax.rsqrt(jnp.mean(hidden * hidden, axis=-1, keepdims=True) + eps)
        x_ref[at, :] = (hidden * inv * gain_ref[...]).astype(bf16)

    normal(0, theirs, False)
    normal(1, theirs, False)
    for load in loads[2:]:
        load.wait()
    wide = 256

    def feed(base):
        rows = rows_at(base, half)
        acc_f[...] = jnp.zeros_like(acc_f)
        acc_g[...] = jnp.zeros_like(acc_g)

        def tile(u, unused):
            cols = rows_at(u * wide, wide)
            gate = nn(x_ref[rows, :], wg[:, cols])
            upward = nn(x_ref[rows, :], wu[:, cols])
            grad_inner = nn(cot_ref[rows, :], wd[:, cols])
            square = gate * gate
            bend = jnp.tanh(root * gate * (1.0 + cubic * square))
            side = 0.5 * (1.0 + bend)
            gelu = gate * side
            slope = side + 0.5 * gate * (1.0 - bend * bend) * (
                root * (1.0 + 3.0 * cubic * square)
            )
            inner_low = (gelu * upward).astype(bf16)
            gate_low = (grad_inner * upward * slope).astype(bf16)
            up_low = (grad_inner * gelu).astype(bf16)
            inner[rows, cols] = inner_low
            gg[rows, cols] = gate_low
            gu[rows, cols] = up_low
            acc_g[...] += nt(gate_low, wg[:, cols]) + nt(up_low, wu[:, cols])
            acc_f[...] += nt(inner_low, wd[:, cols])
            return unused

        lax.fori_loop(0, units // wide, tile, 0)

    def d_copy(i):
        return send(
            d_out.at[i], d_in.at[i], y_sem.at[0, 4 + i], y_sem.at[1, 4 + i], spot.y_mate()
        )

    def send_grad(i, unused):
        d_out[i] = acc_g[rows_at(i * chunk, chunk), :].astype(bf16)
        d_copy(i).start()
        return unused

    def half_pass(k, unused):
        base = theirs + k * (ours - theirs)
        feed(base)

        @pl.when(k == 0)
        def _():
            lax.fori_loop(0, 4, send_grad, 0)
            normal(2, ours, True)
            normal(3, ours, True)
            ffn_far_ref[...] = acc_f[...].astype(bf16)

        @pl.when(k == 1)
        def _():
            ffn_ref[...] = acc_f[...].astype(bf16)

        return unused

    lax.fori_loop(0, 2, half_pass, 0)
    count = units // wide

    def out_copy(m, u):
        return pltpu.make_async_copy(
            rows_buf.at[m, u % 2],
            stacks[m].at[rows_at(u * wide, wide)],
            out_sem.at[m, u % 2],
        )

    for m in range(3):
        left = (inner, gg, gu)[m]
        right = (cot_ref, x_ref, x_ref)[m]

        def weight_rows(u, unused, m=m, left=left, right=right):
            @pl.when(u >= 2)
            def _():
                out_copy(m, u - 2).wait()

            turned = jnp.transpose(left[:, rows_at(u * wide, wide)])
            rows_buf[m, u % 2] = nn(turned, right[...]).astype(bf16)
            out_copy(m, u).start()
            return unused

        lax.fori_loop(0, count, weight_rows, 0)

    def e_copy(i):
        return send(
            e_out.at[i], e_in.at[i], y_sem.at[0, 8 + i], y_sem.at[1, 8 + i], spot.y_mate()
        )

    def normal_back(i, total):
        d_copy(i).wait()
        at = rows_at(i * chunk, chunk)
        grad = acc_g[at, :] + d_in[i].astype(f32)
        hidden = hidden_ref[at, :]
        inv = lax.rsqrt(jnp.mean(hidden * hidden, axis=-1, keepdims=True) + eps)
        scaled = gain_ref[...] * grad
        mean = jnp.mean(hidden * scaled, axis=-1, keepdims=True)
        grad_hidden = (
            cot_ref[rows_at(ours + i * chunk, chunk), :].astype(f32)
            + inv * scaled
            - hidden * (inv * inv * inv * mean)
        )
        gh_ref[at, :] = grad_hidden
        low = grad_hidden.astype(bf16)
        branch_ref[at, :] = low
        e_out[i] = nt(low, wo[1]).astype(bf16)
        e_copy(i).start()
        do_ref[rows_at(ours + i * chunk, chunk), :] = nt(low, wo[0]).astype(bf16)
        return total + jnp.sum(grad * hidden * inv, axis=0, keepdims=True)

    gain_part_ref[...] = lax.fori_loop(0, 4, normal_back, jnp.zeros((1, model), f32))

    def row_terms(at, grad):
        lane = lanes_of(chunk)
        terms = grad.astype(f32) * mixed_ref[at, :]
        out = grad
        for h in range(plan.heads):
            row_term = jnp.sum(
                jnp.where(lane // 64 == h + 1, terms, 0.0), axis=1, keepdims=True
            )
            for i, part in enumerate(split3(-row_term)):
                out = jnp.where(lane == 3 * h + i, part, out)
        do_ref[at, :] = out

    def own_terms(i, unused):
        at = rows_at(ours + i * chunk, chunk)
        row_terms(at, do_ref[at, :])
        return unused

    lax.fori_loop(0, 4, own_terms, 0)

    def far_terms(i, unused):
        e_copy(i).wait()
        row_terms(rows_at(theirs + i * chunk, chunk), e_in[i])
        return unused

    lax.fori_loop(0, 4, far_terms, 0)
    for m in range(3):
        for u in range(max(0, count - 2), count):
            out_copy(m, u).wait()
    for i in order:
        a_copy(i, ours if i < 2 else theirs).wait_send()


def middle(
    plan, cycle_size, attended, mixed, tokens, cot, gain, w_out, w_out_far, w_gate, w_up, w_down
):
    pair, model = tokens.shape
    half = pair // 2
    units = w_down.shape[0]
    chunk = half // 4
    hbm = pl.BlockSpec(memory_space=pl.ANY)
    dma = pltpu.SemaphoreType.DMA
    return pl.pallas_call(
        functools.partial(middle_kernel, plan, cycle_size),
        out_shape=[
            jax.ShapeDtypeStruct((half, model), f32),
            jax.ShapeDtypeStruct((half, model), f32),
            jax.ShapeDtypeStruct((half, model), bf16),
            jax.ShapeDtypeStruct((half, model), bf16),
            jax.ShapeDtypeStruct((half, model), bf16),
            jax.ShapeDtypeStruct((pair, WIDE), bf16),
            jax.ShapeDtypeStruct((1, model), f32),
        ]
        + [jax.ShapeDtypeStruct((units, model), bf16)] * 3,
        in_specs=[vmem] * 5 + [hbm] * 5,
        out_specs=[vmem] * 7 + [hbm] * 3,
        scratch_shapes=[
            pltpu.VMEM((model, units), bf16),
            pltpu.VMEM((model, units), bf16),
            pltpu.VMEM((model, units), bf16),
            pltpu.VMEM((2, WIDE, model), bf16),
            pltpu.VMEM((pair, units), bf16),
            pltpu.VMEM((pair, units), bf16),
            pltpu.VMEM((pair, units), bf16),
            pltpu.VMEM((pair, model), bf16),
            pltpu.VMEM((pair, WIDE), bf16),
            pltpu.VMEM((4, chunk, model), bf16),
            pltpu.VMEM((4, chunk, model), bf16),
            pltpu.VMEM((4, chunk, WIDE), bf16),
            pltpu.VMEM((4, chunk, WIDE), bf16),
            pltpu.VMEM((half, model), f32),
            pltpu.VMEM((half, model), f32),
            pltpu.VMEM((3, 2, WIDE, model), bf16),
            dma((5,)),
            dma((2, 12)),
            dma((3, 2)),
        ],
        compiler_params=pltpu.CompilerParams(
            vmem_limit_bytes=60 * 2**20, collective_id=3, has_side_effects=True
        ),
        name="feed_forward",
    )(attended, mixed, tokens, cot, gain, w_out, w_out_far, w_gate, w_up, w_down.T)


class Scatter:
    def __init__(self, spot, units, parts, outs, buffers, sems):
        self.spot = spot
        self.units = units
        self.parts = parts
        self.outs = outs
        self.mine, self.core_in, self.x_in, self.up_in, self.down_in = buffers
        self.load_sem, self.core_sem, self.x_sem, self.up_sem, self.down_sem = sems

    def rows_of(self, u):
        return pl.ds(self.units[u][1], self.units[u][2])

    def load(self, u):
        m = self.units[u][0]
        return pltpu.make_async_copy(
            self.parts[m].at[:, :, self.spot.core, self.rows_of(u)],
            self.mine.at[m, :, :, self.rows_of(u)],
            self.load_sem.at[u],
        )

    def core_copy(self, u):
        m = self.units[u][0]
        return send(
            self.parts[m].at[:, :, 1 - self.spot.core, self.rows_of(u)],
            self.core_in.at[m, :, :, self.rows_of(u)],
            self.core_sem.at[0, u],
            self.core_sem.at[1, u],
            self.spot.core_mate(),
        )

    def x_copy(self, u):
        m = self.units[u][0]
        x = self.spot.x
        src = self.mine.at[m, :, 1 - x, self.rows_of(u)]
        dst = self.x_in.at[m, :, self.rows_of(u)]
        return send(src, dst, self.x_sem.at[0, u], self.x_sem.at[1, u], self.spot.x_mate())

    def begin(self, u):
        self.load(u).start()
        self.core_copy(u).start()

    def core_stage(self, u):
        m = self.units[u][0]
        x = self.spot.x
        self.load(u).wait()
        self.core_copy(u).wait()

        def add(slot):
            def body(line, unused):
                at = (m, line, slot, self.rows_of(u))
                self.mine[at] = added(self.mine[at], self.core_in[at])
                return unused

            lax.fori_loop(0, self.spot.lines, body, 0)

        add(1 - x)
        self.x_copy(u).start()
        add(x)

    def x_stage(self, u):
        m = self.units[u][0]
        x = self.spot.x
        self.x_copy(u).wait()

        def body(line, unused):
            at = (m, line, x, self.rows_of(u))
            self.mine[at] = added(self.mine[at], self.x_in[m, line, self.rows_of(u)])
            return unused

        lax.fori_loop(0, self.spot.lines, body, 0)
        self.ends(u)

    def copy(self, u, step, d):
        m = self.units[u][0]
        sem = self.up_sem if step > 0 else self.down_sem
        ring = self.up_in if step > 0 else self.down_in
        return send(
            self.mine.at[m, d, self.spot.x, self.rows_of(u)],
            ring.at[m, d, self.rows_of(u)],
            sem.at[0, u, d],
            sem.at[1, u, d],
            self.spot.z_mate(step),
        )

    def receive(self, u, step, d):
        m = self.units[u][0]
        self.copy(u, step, d).wait_recv()
        ring = self.up_in if step > 0 else self.down_in
        at = (m, d, self.spot.x, self.rows_of(u))
        self.mine[at] = added(self.mine[at], ring[m, d, self.rows_of(u)])

    def start(self, u, step, d):
        self.copy(u, step, d).start()

    def ends(self, u):
        z, lines = (self.spot.z, self.spot.lines)

        @pl.when(z == 0)
        def _():
            def up(k, unused):
                self.start(u, 1, lines - 1 - k)
                return unused

            lax.fori_loop(0, lines - 1, up, 0)

        @pl.when(z == lines - 1)
        def _():
            def down(k, unused):
                self.start(u, -1, k)
                return unused

            lax.fori_loop(0, lines - 1, down, 0)

    def relay(self, u, lag):
        z, lines = (self.spot.z, self.spot.lines)
        top = lines - 2 if lag == 2 else lag

        @pl.when((z >= lag) & (z <= top))
        def _():
            def up(k, unused):
                self.receive(u, 1, lines - 1 - k)
                self.start(u, 1, lines - 1 - k)
                return unused

            lax.fori_loop(0, lines - 1 - z, up, 0)

        @pl.when((lines - 1 - z >= lag) & (lines - 1 - z <= top))
        def _():
            def down(k, unused):
                self.receive(u, -1, k)
                self.start(u, -1, k)
                return unused

            lax.fori_loop(0, z, down, 0)

    def settle(self, u):
        z, lines = (self.spot.z, self.spot.lines)

        @pl.when(z > 0)
        def _():
            self.receive(u, 1, z)

        @pl.when(z + 1 < lines)
        def _():
            self.receive(u, -1, z)

        self.store(u)

    def store(self, u):
        m = self.units[u][0]
        self.outs[m][self.rows_of(u), :] = self.mine[
            m, self.spot.z, self.spot.x, self.rows_of(u)
        ].astype(f32)

    def drain(self, u):
        z, lines = (self.spot.z, self.spot.lines)

        def body(k, unused):
            @pl.when(z < lines - 1 - k)
            def _():
                self.copy(u, 1, lines - 1 - k).wait_send()

            @pl.when(z > k)
            def _():
                self.copy(u, -1, k).wait_send()

            return unused

        lax.fori_loop(0, lines - 1, body, 0)


def scatter_units(rows):
    if rows % 16 or rows < 112:
        return [(m, 0, rows) for m in range(3)]
    tail = rows - 64
    return [
        (0, 0, 64), (1, 0, 64), (2, 0, 64), (0, 64, tail), (1, 64, tail), (2, 64, tail - 16),
        (2, rows - 16, 16),
    ]


def backward_kernel(
    plan, lines, span, reach, doc_most, rows, pair, table_ref, qb_ref, do_ref,
    own_kv, own_aug, near_hbm, aug_hbm, masks_hbm, g_hbm, qall_hbm, branch_hbm, ffn_hbm, p0, p1, p2,
    dq_ref, tab_ref, dk_ref, dv_ref, mask_ref, o0, o1, o2, far_hbm, ffn_in_hbm, all_do,
    mine, core_in, x_in, up_in, down_in,
    km, vm, mask_row, g_buf, aug_buf, qh_ref, doh_ref, acc, near_ref, near_acc, far_acc,
    load_sem, core_sem, rx_sem, up_sem, down_sem, own_sem, zero_sem, z_sem, x_sem, c_sem, g_sem,
    q_sem,
):
    spot = Spot(lines)
    z, x, core = (spot.z, spot.x, spot.core)
    units = scatter_units(o0.shape[0])
    scatter = Scatter(
        spot,
        units,
        (p0, p1, p2),
        (o0, o1, o2),
        (mine, core_in, x_in, up_in, down_in),
        (load_sem, core_sem, rx_sem, up_sem, down_sem),
    )
    order = range(len(units))
    greet(spot, True)
    far_copy = send(branch_hbm, far_hbm, own_sem.at[2], own_sem.at[3], spot.y_mate())
    far_copy.start()
    ffn_copy = send(ffn_hbm, ffn_in_hbm, own_sem.at[4], own_sem.at[5], spot.y_mate())
    ffn_copy.start()

    def outside(d):
        return (d < z - span) | (d > z + span)

    def pass_copy(step, d):
        i = 0 if step > 0 else 1
        part = all_do.at[d, :, core]
        return send(part, part, z_sem.at[i, d], z_sem.at[2 + i, d], spot.z_mate(step))

    across = send(do_ref, all_do.at[z, x, core], x_sem.at[0], x_sem.at[1], spot.x_mate())

    def beside(d):
        part = all_do.at[d, :, core]
        return send(part, part, c_sem.at[0, d], c_sem.at[1, d], spot.core_mate())

    own_copy = pltpu.make_async_copy(do_ref, all_do.at[z, x, core], own_sem.at[0])

    def zero_copies(d):
        return [
            pltpu.make_async_copy(vm.at[pl.ds(0, pair)], all_do.at[d, a, b], zero_sem.at[d, a, b])
            for a in range(2)
            for b in range(2)
        ]

    def zero_start(d, unused):
        @pl.when(outside(d))
        def _():
            for copy in zero_copies(d):
                copy.start()

        return unused

    def turn():
        across.wait()
        own_copy.wait()

        @pl.when(z + 1 < lines)
        def _():
            pass_copy(1, z).start()

        @pl.when(z > 0)
        def _():
            pass_copy(-1, z).start()

        beside(z).start()

    def level(k):
        @pl.when(z - k >= 0)
        def _():
            d = jnp.maximum(z - k, 0)
            pass_copy(1, d).wait_recv()
            if k < span:

                @pl.when(z + 1 < lines)
                def _():
                    pass_copy(1, d).start()

            beside(d).start()

        @pl.when(z + k < lines)
        def _():
            d = jnp.minimum(z + k, lines - 1)
            pass_copy(-1, d).wait_recv()
            if k < span:

                @pl.when(z > 0)
                def _():
                    pass_copy(-1, d).start()

            beside(d).start()

    def gathered(d, unused):
        @pl.when(~outside(d))
        def _():
            beside(d).wait()

        @pl.when(outside(d))
        def _():
            for copy in zero_copies(d):
                copy.wait()

        @pl.when((z + 1 < lines) & (d <= z) & (d > z - span))
        def _():
            pass_copy(1, d).wait_send()

        @pl.when((z > 0) & (d >= z) & (d < z + span))
        def _():
            pass_copy(-1, d).wait_send()

        return unused

    own_copy.start()
    across.start()
    for u in order:
        scatter.begin(u)
    vm[:PAD, :] = jnp.zeros((PAD, WIDE), bf16)
    lax.fori_loop(0, lines, zero_start, 0)

    base = spot.index * pair
    total = 4 * lines * pair
    origin = jnp.clip(base - reach * pair, 0, total - rows)
    local = base - origin
    blocks = rows // pair

    def mask_copy(n):
        to = pl.ds(pl.multiple_of(PAD + n * pair, 128), pair)
        return pltpu.make_async_copy(masks_hbm.at[n], mask_row.at[:, to], q_sem.at[1 + n])

    def mask_start(n, unused):
        mask_copy(n).start()
        return unused

    lax.fori_loop(0, blocks, mask_start, 0)
    mask_row[:, :PAD] = jnp.zeros((8, PAD), f32)
    mask_row[:, PAD + rows :] = jnp.zeros((8, PAD), f32)
    km[:PAD, :] = jnp.broadcast_to(
        jnp.where(pad_lanes(plan), neg_big, 0.0).astype(bf16), (PAD, WIDE)
    )
    km[PAD + rows :, :] = km[:PAD, :]
    vm[PAD + rows :, :] = jnp.zeros((PAD, WIDE), bf16)
    low_block = lanes_of(pair, 128) < 64
    ones_block = (lanes_of(pair, 128) < 3 * plan.heads).astype(bf16)

    def g_copy(n):
        at = pl.ds(pl.multiple_of(n * pair, pair), pair)
        return pltpu.make_async_copy(g_hbm.at[at], g_buf.at[n % 2], g_sem.at[0, n % 2])

    def aug_copy(n):
        at = pl.ds(pl.multiple_of(n * pair, pair), pair)
        return pltpu.make_async_copy(aug_hbm.at[at], aug_buf.at[n % 2], g_sem.at[1, n % 2])

    def near_copy(flip):
        return pltpu.make_async_copy(near_hbm.at[flip], near_ref, own_sem.at[1])

    g_copy(0).start()
    aug_copy(0).start()
    near_copy(0).start()

    def build(n, unused):
        g_copy(n).wait()
        aug_copy(n).wait()

        @pl.when(n + 1 < blocks)
        def _():
            g_copy(n + 1).start()
            aug_copy(n + 1).start()

        mask_copy(n).wait()
        to = pl.ds(pl.multiple_of(PAD + n * pair, 128), pair)
        middle = g_buf[n % 2, :, 128:256]
        km[to, 0:128] = g_buf[n % 2, :, 0:128]
        km[to, 128:256] = jnp.where(low_block, middle, aug_buf[n % 2])
        vm[to, 0:128] = jnp.where(low_block, ones_block, middle)
        vm[to, 128:256] = g_buf[n % 2, :, 256:384]
        return unused

    early = min(6, blocks)
    lax.fori_loop(0, early, build, 0)
    scatter.core_stage(0)
    lax.fori_loop(early, blocks, build, 0)
    near_copy(0).wait()
    near_acc[...] = jnp.zeros_like(near_acc)
    far_acc[...] = jnp.zeros_like(far_acc)
    lane = lanes_of(TQ)
    low = lanes_of(TQ, 128) < 64
    ones = (lanes_of(TQ, 128) < 3 * plan.heads).astype(bf16)

    def chunks(t):
        start = local + t * TQ
        least = jnp.maximum(start - doc_most + 1, 0)
        most = jnp.minimum(start + TQ + doc_most - 1, rows)
        n_left = jnp.maximum(start - EDGE - least + TK - 1, 0) // TK
        n_right = jnp.maximum(most - (start + TK - EDGE) + TK - 1, 0) // TK
        return start, n_left, n_right

    def rows_of_tile(t):
        return pl.ds(pl.multiple_of(t * TQ, TQ), TQ)

    def near_of(start):
        return pl.ds(pl.multiple_of(start + PAD - EDGE, 128), TK)

    def query_grads(h, s, part):
        return jnp.exp(s) * nt(doh_ref[h], vm[part, :])

    def dq_near(t, start):
        out = rows_of_tile(t)
        near = near_of(start)
        q = qb_ref[out, :]
        do = do_ref[out, :]
        for h in range(plan.heads):
            qh_ref[h] = jnp.where(plan.key_lanes(lane, h), q, jnp.zeros_like(q))
            doh_ref[h] = jnp.where(plan.value_lanes(lane, h), do, jnp.zeros_like(do))
            ds = query_grads(
                h, nt(qh_ref[h], km[near, :]) + near_ref[h] + mask_row[0:1, near], near
            )
            near_acc[h] += ds
            acc[h] = nn(ds.astype(bf16), km[near, :])

    def far_pair(start, n, n_left, count, left, right):
        pair_of = []
        for i in range(2):
            part, bucket = far_span(start, 2 * n + i, n_left, left, right)
            at = jnp.where(2 * n + i < count, part.start, 0)
            pair_of.append((pl.ds(pl.multiple_of(at, 128), TK), bucket))
        return pair_of

    def dq_far(start, n, n_left, count):
        parts = far_pair(start, n, n_left, count, far_left_bucket, far_right_bucket)
        for h in range(plan.heads):
            grads = []
            for i, (part, bucket) in enumerate(parts):
                slot = (2 * n + i >= n_left).astype(jnp.int32)
                offset = mask_row[0:1, part] + table_ref[bucket, h]
                ds = query_grads(h, nt(qh_ref[h], km[part, :]) + offset, part)
                grads.append(nn(ds.astype(bf16), km[part, :]))
                far_acc[slot, h] += (
                    ds[:, 0:128] + ds[:, 128:256] + ds[:, 256:384] + ds[:, 384:512]
                )
            acc[h] += grads[0] + grads[1]

    def dq_end(t):
        result = jnp.zeros((TQ, WIDE), f32)
        for h in range(plan.heads):
            result = jnp.where(lane // 64 == h, acc[h], result)
        dq_ref[rows_of_tile(t), :] = result.astype(bf16)

    def table_end():
        row = lax.broadcasted_iota(jnp.int32, (EDGE, 3 * EDGE), 0)
        col = lax.broadcasted_iota(jnp.int32, (EDGE, 3 * EDGE), 1)
        bucket = bucket_of(col - EDGE - row)
        for h in range(plan.heads):
            band = near_acc[h, :EDGE, : 3 * EDGE] + near_acc[h, EDGE:, EDGE:]

            def one(b, unused, band=band, h=h):
                part = jnp.sum(jnp.where(bucket == b, band, 0.0), axis=0, keepdims=True)
                tab_ref[h, pl.ds(b, 1), :] = part[:, :128] + part[:, 128:256] + part[:, 256:]
                return unused

            lax.fori_loop(0, 32, one, 0)
            for b, slot, extra in (
                (far_left_bucket, 0, near_acc[h, EDGE:, :EDGE]),
                (far_right_bucket, 1, near_acc[h, :EDGE, 3 * EDGE :]),
            ):
                tab_ref[h, b : b + 1, :] += jnp.sum(
                    far_acc[slot, h], axis=0, keepdims=True
                ) + jnp.sum(extra, axis=0, keepdims=True)

    def swap_operands():
        near_copy(1).start()
        lax.fori_loop(0, lines, gathered, 0)
        q_copy = pltpu.make_async_copy(qall_hbm, km.at[pl.ds(PAD, rows)], q_sem.at[0])
        q_copy.start()

        def block_copy(n):
            b = origin // pair + n
            return pltpu.make_async_copy(
                all_do.at[b // 4, (b // 2) % 2, b % 2],
                vm.at[pl.ds(pl.multiple_of(PAD + n * pair, 128), pair)],
                q_sem.at[1 + n],
            )

        def block_start(n, unused):
            block_copy(n).start()
            return unused

        lax.fori_loop(0, blocks, block_start, 0)
        first = lanes_of(1)
        stat = (first >= plan.stat_lane) & (first < plan.stat_lane + 3 * plan.heads)
        km[:PAD, :] = jnp.broadcast_to(jnp.where(stat, neg_big, 0.0).astype(bf16), (PAD, WIDE))
        km[PAD + rows :, :] = km[:PAD, :]

        def block_wait(n, unused):
            block_copy(n).wait()
            return unused

        lax.fori_loop(0, blocks, block_wait, 0)
        q_copy.wait()
        near_copy(1).wait()

    def key_grads(h, s, part):
        p = jnp.exp(s)
        ds = p * nt(doh_ref[h], vm[part, :])
        return nn(p.astype(bf16), vm[part, :]), nn(ds.astype(bf16), km[part, :])

    def dkv_near(t, start):
        out = rows_of_tile(t)
        near = near_of(start)
        middle = own_kv[out, 128:256]
        k = jnp.concatenate([own_kv[out, 0:128], jnp.where(low, middle, own_aug[out, :])], axis=1)
        v = jnp.concatenate([jnp.where(low, ones, middle), own_kv[out, 256:384]], axis=1)
        for h in range(plan.heads):
            qh_ref[h] = jnp.where(plan.key_lanes(lane, h), k, jnp.zeros_like(k))
            doh_ref[h] = jnp.where(plan.value_lanes(lane, h), v, jnp.zeros_like(v))
            near_acc[h, :, :WIDE], acc[h] = key_grads(
                h, nt(qh_ref[h], km[near, :]) + near_ref[h], near
            )

    def dkv_far(start, n, n_left, count):
        parts = far_pair(start, n, n_left, count, far_right_bucket, far_left_bucket)
        for h in range(plan.heads):
            (v_one, k_one), (v_two, k_two) = [
                key_grads(h, nt(qh_ref[h], km[part, :]) + table_ref[bucket, h], part)
                for part, bucket in parts
            ]
            near_acc[h, :, :WIDE] += v_one + v_two
            acc[h] += k_one + k_two

    def dkv_end(t):
        out = rows_of_tile(t)
        dk = jnp.zeros((TQ, WIDE), f32)
        dv = jnp.zeros((TQ, WIDE), f32)
        mask_grad = jnp.zeros((TQ, 1), f32)
        for h in range(plan.heads):
            dk = jnp.where(lane // 64 == h, acc[h], dk)
            dv = jnp.where(lane // 64 == h + 1, near_acc[h, :, :WIDE], dv)
            mask_grad = mask_grad + acc[h][:, plan.mask_lane : plan.mask_lane + 1]
        mask_ref[t] = jnp.transpose(jnp.broadcast_to(mask_grad, (TQ, 128)))[:8, :]
        dk_ref[out, :] = dk.astype(bf16)
        dv_ref[out, :] = dv.astype(bf16)

    tiles = pair // TQ
    steps = 1 + -(-(2 * (-(-doc_most // TK)) + 1) // 2)
    half_slots = tiles * steps
    last_step = steps - 1

    def attention(w):
        backward = w >= half_slots
        t = (w % half_slots) // steps
        n = w % steps
        start, n_left, n_right = chunks(t)
        count = n_left + n_right
        live = (n > 0) & (2 * (n - 1) < count)

        @pl.when(~backward)
        def _():
            @pl.when(n == 0)
            def _():
                dq_near(t, start)

            @pl.when(live)
            def _():
                dq_far(start, n - 1, n_left, count)

            @pl.when(n == last_step)
            def _():
                dq_end(t)

        @pl.when(backward & (w < 2 * half_slots))
        def _():
            @pl.when(w == half_slots)
            def _():
                table_end()
                swap_operands()

            @pl.when(n == 0)
            def _():
                dkv_near(t, start)

            @pl.when(live)
            def _():
                dkv_far(start, n - 1, n_left, count)

            @pl.when(n == last_step)
            def _():
                dkv_end(t)

    work = 2 * half_slots
    events = []

    def due(time, run, *args):
        events.append((max(0, int((time - start_us) / slot_us)), functools.partial(run, *args)))

    start_us, slot_us = (6.0, 2.0)
    due(6.0, turn)
    for k in range(1, span + 1):
        due((22.0, 36.0)[min(k, 2) - 1], level, k)
    times = (
        (7.0, 26.0, 51.0, 61.0, 68.0),
        (10.5, 43.0, 64.0, 74.0, 81.0),
        (14.0, 60.0, 77.0, 87.0, 94.0),
        (17.0, 73.0, 87.0, 95.0, 101.0),
        (20.0, 86.0, 97.5, 106.0, 111.0),
        (22.0, 95.0, 104.0, 110.0, 114.0),
        (23.0, 99.0, 107.0, 111.0, 114.5),
    )
    for u in order:
        core_at, x_at, one_at, two_at, end_at = times[u]
        if u > 0:
            due(core_at, scatter.core_stage, u)
        due(x_at, scatter.x_stage, u)
        due(one_at, scatter.relay, u, 1)
        due(two_at, scatter.relay, u, 2)
        due(end_at, scatter.settle, u)
    events.sort(key=lambda event: event[0])
    end = max(work, events[-1][0] + 1)

    def slot(w, unused):
        for at, run in events:

            @pl.when(w == at)
            def _(run=run):
                run()

        attention(w)
        return unused

    lax.fori_loop(0, end, slot, 0)
    for u in order:
        scatter.drain(u)
    far_copy.wait()
    ffn_copy.wait()


def backward(
    plan, cycle_size, reach, doc_most, rows, table, aug, masks, q_back, do_wide, own_kv, own_aug,
    near_bias, kv_all, q_all, branch, ffn_far, parts,
):
    lines = cycle_size // 4
    span = min(lines - 1, (reach + 3) // 4)
    pair = q_back.shape[0]
    units_here, model = parts[0].shape
    size = units_here // cycle_size
    units = scatter_units(size)
    shaped = [part.reshape(lines, 2, 2, size, model) for part in parts]
    n = len(units)
    heads = plan.heads
    padded = rows + 2 * PAD
    hbm = pl.BlockSpec(memory_space=pl.ANY)
    dma = pltpu.SemaphoreType.DMA
    return pl.pallas_call(
        functools.partial(backward_kernel, plan, lines, span, reach, doc_most, rows, pair),
        out_shape=[
            jax.ShapeDtypeStruct((pair, WIDE), bf16),
            jax.ShapeDtypeStruct((heads, 32, 128), f32),
            jax.ShapeDtypeStruct((pair, WIDE), bf16),
            jax.ShapeDtypeStruct((pair, WIDE), bf16),
            jax.ShapeDtypeStruct((pair // TQ, 8, TQ), f32),
        ]
        + [jax.ShapeDtypeStruct((size, model), f32)] * 3
        + [
            jax.ShapeDtypeStruct(branch.shape, bf16),
            jax.ShapeDtypeStruct(branch.shape, bf16),
            jax.ShapeDtypeStruct((lines, 2, 2, pair, WIDE), bf16),
        ],
        in_specs=[smem] + [vmem] * 4 + [hbm] * 10,
        out_specs=[vmem] * 8 + [hbm] * 3,
        scratch_shapes=[
            pltpu.VMEM((3, lines, 2, size, model), bf16),
            pltpu.VMEM((3, lines, 2, size, model), bf16),
            pltpu.VMEM((3, lines, size, model), bf16),
            pltpu.VMEM((3, lines, size, model), bf16),
            pltpu.VMEM((3, lines, size, model), bf16),
            pltpu.VMEM((padded, WIDE), bf16),
            pltpu.VMEM((padded, WIDE), bf16),
            pltpu.VMEM((8, padded), f32),
            pltpu.VMEM((2, pair, 2 * plan.cols), bf16),
            pltpu.VMEM((2, pair, 128), bf16),
            pltpu.VMEM((heads, TQ, WIDE), bf16),
            pltpu.VMEM((heads, TQ, WIDE), bf16),
            pltpu.VMEM((heads, TQ, WIDE), f32),
            pltpu.VMEM((heads, TQ, TK), f32),
            pltpu.VMEM((heads, TQ, TK), f32),
            pltpu.VMEM((2, heads, TQ, 128), f32),
            dma((n,)),
            dma((2, n)),
            dma((2, n)),
            dma((2, n, lines)),
            dma((2, n, lines)),
            dma((6,)),
            dma((lines, 2, 2)),
            dma((4, lines)),
            dma((2,)),
            dma((2, lines)),
            dma((2, 2)),
            dma((1 + rows // pair,)),
        ],
        compiler_params=pltpu.CompilerParams(
            vmem_limit_bytes=62 * 2**20, collective_id=1, has_side_effects=True
        ),
        name="backward",
    )(
        table, q_back, do_wide, own_kv, own_aug, near_bias, aug, masks, kv_all, q_all,
        branch, ffn_far, *shaped
    )


def shards(
    tokens,
    doc_lengths,
    key_mask,
    gain_attn,
    w_query,
    w_key,
    w_value,
    w_out,
    bias_table,
    gain_ffn,
    w_gate,
    w_up,
    w_down,
    cotangent,
):
    own_rows, model = tokens.shape
    group = lax.axis_size("wa")
    cycle_size = lax.axis_size("ctx")
    pair = own_rows * group
    heads = bias_table.shape[1]
    docs = doc_lengths.shape[0]
    plan = Plan(heads, w_query.shape[1] // heads, docs)
    total_rows = pair * cycle_size
    doc_most = min(MAXLEN, total_rows // 2)
    reach = min(cycle_size - 1, (doc_most - 1) // pair + 1)
    base = lax.axis_index("ctx") * pair
    rows = min(total_rows, (2 * reach + 1) * pair)
    origin = jnp.clip(base - reach * pair, 0, total_rows - rows).astype(jnp.int32)
    ends = jnp.cumsum(doc_lengths).astype(jnp.int32)
    starts = ends - doc_lengths

    def doc_at(positions):
        return jnp.sum((positions[:, None] >= starts[None, :]).astype(jnp.int32), axis=1) - 1

    tiles = pair // TQ
    tile_start = base + TQ * jnp.arange(tiles, dtype=jnp.int32)
    first_doc = jnp.arange(docs, dtype=jnp.int32)[None, :] == doc_at(tile_start)[:, None]
    last_doc = jnp.arange(docs, dtype=jnp.int32)[None, :] == doc_at(tile_start + TQ - 1)[:, None]
    low_end = jnp.sum(jnp.where(first_doc, starts[None, :], 0), axis=1)
    high_end = jnp.sum(jnp.where(last_doc, ends[None, :], 0), axis=1)
    n_left = jnp.maximum(0, (tile_start - EDGE - low_end + TK - 1) // TK)
    n_right = jnp.maximum(0, (high_end - (tile_start - EDGE + TK) + TK - 1) // TK)
    bounds = jnp.concatenate(
        [(base - origin)[None], jnp.stack([n_left, n_right], axis=1).reshape(-1)]
    ).astype(jnp.int32)

    def window(gathered):
        if rows == total_rows:
            return gathered
        return lax.dynamic_slice_in_dim(gathered, origin, rows, 0)

    gather = functools.partial(lax.all_gather, axis_name="ctx", axis=0, tiled=True)
    (
        pair_normed, pair_tokens, q_wide, own_kv, k_aug, own_aug, near_bias, masks, far_out, kv_all,
    ) = first(
        plan,
        cycle_size,
        reach,
        rows,
        starts,
        bias_table,
        tokens,
        gain_attn[None],
        jnp.broadcast_to(key_mask.astype(f32)[None], (8, pair)),
        w_query,
        w_key,
        w_value,
        w_out,
    )
    masks = masks.reshape(cycle_size, 8, pair)
    cot_late, near_bias = lax.optimization_barrier((cotangent, near_bias))
    pair_cot = lax.all_gather(cot_late, "wa", axis=0, tiled=True)
    if rows < total_rows:
        masks = lax.dynamic_slice_in_dim(masks, origin // pair, rows // pair, 0)
    kv_all = window(kv_all.reshape(total_rows, 2 * plan.cols))
    padded = rows + 2 * PAD
    attended, mixed, q_back = pl.pallas_call(
        functools.partial(fwd_kernel, plan, rows, pair),
        out_shape=(
            jax.ShapeDtypeStruct((pair, WIDE), bf16),
            jax.ShapeDtypeStruct((pair, WIDE), f32),
            jax.ShapeDtypeStruct((pair, WIDE), bf16),
        ),
        in_specs=[smem, smem] + [vmem] * 5,
        out_specs=(vmem, vmem, vmem),
        scratch_shapes=[
            pltpu.VMEM((padded, WIDE), bf16),
            pltpu.VMEM((padded, WIDE), bf16),
            pltpu.VMEM((8, padded), f32),
            pltpu.VMEM((heads, TQ, WIDE), f32),
            pltpu.VMEM((heads, TQ, 128), f32),
            pltpu.VMEM((heads, TQ, WIDE), bf16),
        ],
        compiler_params=params(),
        name="attention_forward",
    )(bounds, bias_table, kv_all, k_aug, masks, q_wide, near_bias)
    q_all = window(gather(q_back))
    hidden, grad_hidden, branch, ffn_own, ffn_far, do_wide, gain_ffn_part, *stacks = middle(
        plan,
        cycle_size,
        attended,
        mixed,
        pair_tokens,
        pair_cot,
        gain_ffn[None],
        w_out,
        far_out,
        w_gate,
        w_up,
        w_down,
    )
    (
        grad_queries, table_part, grad_keys, grad_values, mask_part,
        grad_w_down, grad_w_gate, grad_w_up, far_branch, ffn_in, unused_gathered,
    ) = backward(
        plan,
        cycle_size,
        reach,
        doc_most,
        rows,
        bias_table,
        k_aug,
        masks,
        q_back,
        do_wide,
        own_kv,
        own_aug,
        near_bias,
        kv_all,
        q_all,
        branch,
        ffn_far,
        stacks,
    )
    grad_w_gate, grad_w_up = (grad_w_gate.T, grad_w_up.T)
    cols = plan.cols
    table_row = jnp.sum(table_part, axis=2).reshape(1, -1)
    table_row = jnp.pad(table_row, ((0, 0), (0, model - table_row.shape[1])))
    small = jnp.concatenate(
        [jnp.zeros((1, model), f32), gain_ffn_part, table_row, jnp.zeros((5, model), f32)],
        axis=0,
    )
    layer_out = (hidden + ffn_own.astype(f32) + ffn_in.astype(f32)).astype(bf16)
    grad_tokens, grad_mask, weights, totals = finish(
        plan,
        cycle_size,
        grad_queries,
        grad_keys,
        grad_values,
        mask_part.reshape(group, 8, own_rows),
        w_query.T,
        w_key.T,
        w_value.T,
        pair_normed,
        attended,
        branch,
        far_branch,
        tokens,
        gain_attn[None],
        grad_hidden,
        small,
    )
    weights = weights.reshape(4, cols, model).astype(f32)
    return (
        layer_out,
        grad_tokens,
        grad_mask[0],
        totals[0],
        weights[0].T,
        weights[1].T,
        weights[2].T,
        weights[3],
        totals[2, : heads * 32].reshape(heads, 32).T,
        totals[1],
        grad_w_gate,
        grad_w_up,
        grad_w_down,
    )


def solution(mesh):
    placed = (
        P(("ctx", "wa"), None),
        P(),
        P("ctx"),
        P(),
        P(None, "wa"),
        P(None, "wa"),
        P(None, "wa"),
        P("wa", None),
        P(None, "wa"),
        P(),
        P(None, "wa"),
        P(None, "wa"),
        P("wa", None),
        P(("ctx", "wa"), None),
    )
    return jax.shard_map(
        shards,
        mesh=mesh,
        in_specs=placed,
        out_specs=(
            P(("ctx", "wa"), None),
            P(("ctx", "wa"), None),
            P(("ctx", "wa")),
            P(),
            P(None, "wa"),
            P(None, "wa"),
            P(None, "wa"),
            P("wa", None),
            P(None, "wa"),
            P(),
            P(None, ("wa", "ctx")),
            P(None, ("wa", "ctx")),
            P(("wa", "ctx"), None),
        ),
        check_vma=False,
    )
```

```python
import functools

import jax
import jax.numpy as jnp
from jax import lax
from jax.experimental import pallas as pl
from jax.experimental.pallas import tpu as pltpu
from jax.sharding import PartitionSpec as P

MAXLEN = 8192

bucket_edges = (12, 16, 23, 32, 46, 64, 91)
neg_big = -1e30
eps = 1e-06
far_left_bucket = 15
far_right_bucket = 31
WIDE = 256
TQ = 256
TK = 512
EDGE = 128
PAD = TK + EDGE
f32 = jnp.float32
bf16 = jnp.bfloat16


def bucket_of(relative):
    distance = jnp.abs(relative)
    bucket = jnp.minimum(distance, 8) + 16 * (relative > 0).astype(jnp.int32)
    for edge in bucket_edges:
        bucket = bucket + (distance >= edge).astype(jnp.int32)
    return bucket


def norm_forward(inputs, gain):
    inv_root = lax.rsqrt(jnp.mean(inputs * inputs, axis=-1, keepdims=True) + eps)
    return (inputs * inv_root * gain, inv_root)


def norm_backward(inputs, inv_root, gain, grad_normed):
    scaled = gain * grad_normed
    cubed = inv_root * inv_root * inv_root
    grad_inputs = inv_root * scaled - inputs * cubed * jnp.mean(
        inputs * scaled, axis=-1, keepdims=True
    )
    grad_gain = jnp.sum(grad_normed * inputs * inv_root, axis=0)
    return (grad_inputs, grad_gain)


def gated(gate, upward):
    return jax.nn.gelu(gate, approximate=True) * upward


def nt(a, b):
    return lax.dot_general(a, b, (((1,), (1,)), ((), ())), preferred_element_type=f32)


def nn(a, b):
    return lax.dot_general(a, b, (((1,), (0,)), ((), ())), preferred_element_type=f32)


def split3(x):
    hi = x.astype(bf16)
    rest = x - hi.astype(f32)
    mid = rest.astype(bf16)
    return (hi, mid, (rest - mid.astype(f32)).astype(bf16))


class Plan:
    def __init__(self, heads, width, docs):
        self.heads = heads
        self.width = width
        self.bits = max(1, (docs - 1).bit_length())
        self.cols = heads * width
        self.mask_lane = self.cols
        self.doc_lane = self.cols + 1
        self.stat_lane = self.doc_lane + 2 * self.bits
        assert self.stat_lane + 3 * heads <= WIDE and self.cols + 64 == WIDE and width == 64

    def key_lanes(self, lane, h):
        own = (lane >= h * self.width) & (lane < (h + 1) * self.width)
        aug = (lane >= self.mask_lane) & (lane < self.stat_lane)
        stat = (lane >= self.stat_lane + 3 * h) & (lane < self.stat_lane + 3 * h + 3)
        return own | aug | stat

    def value_lanes(self, lane, h):
        own = (lane >= 64 + h * self.width) & (lane < 64 + (h + 1) * self.width)
        return own | ((lane >= 3 * h) & (lane < 3 * h + 3))


def lanes_of(rows, width=WIDE):
    return lax.broadcasted_iota(jnp.int32, (rows, width), 1)


def near_lanes(heads, table_ref, near_ref):
    row = lax.broadcasted_iota(jnp.int32, (EDGE, 3 * EDGE), 0)
    col = lax.broadcasted_iota(jnp.int32, (EDGE, 3 * EDGE), 1)
    relative = col - EDGE - row
    for flip in range(2):
        bucket = bucket_of(-relative if flip else relative)
        left, right = (far_left_bucket, far_right_bucket)
        if flip:
            left, right = (right, left)
        for h in range(heads):
            base = jnp.full((EDGE, 3 * EDGE), table_ref[h, 0], f32)
            for b in range(1, 32):
                base = jnp.where(bucket == b, table_ref[h, b], base)
            far_l = jnp.full((EDGE, EDGE), table_ref[h, left], f32)
            far_r = jnp.full((EDGE, EDGE), table_ref[h, right], f32)
            near_ref[flip, h, :EDGE, : 3 * EDGE] = base
            near_ref[flip, h, :EDGE, 3 * EDGE :] = far_r
            near_ref[flip, h, EDGE:, EDGE:] = base
            near_ref[flip, h, EDGE:, :EDGE] = far_l


def far_span(start, n, n_left, left_bucket, right_bucket):
    on_left = n < n_left
    at = start + PAD - EDGE + TK * jnp.where(on_left, -1 - n, 1 + n - n_left)
    bucket = jnp.where(on_left, left_bucket, right_bucket)
    return pl.ds(pl.multiple_of(at, 128), TK), bucket


def pad_lanes(plan):
    lane = lanes_of(1)
    return (lane >= plan.doc_lane) & (lane < plan.stat_lane)


def far_pair(start, n, n_left, count, left, right):
    pair_of = []
    for i in range(2):
        part, bucket = far_span(start, 2 * n + i, n_left, left, right)
        at = jnp.where(2 * n + i < count, part.start, 0)
        pair_of.append((pl.ds(pl.multiple_of(at, 128), TK), bucket))
    return pair_of


def fwd_kernel(
    plan, lines, reach, rows, pair, lengths, table_ref, q_ref, near_hbm, g_hbm, aug_hbm, masks_hbm,
    low_ref, wide_ref, qb_ref,
    km, vm, mask_row, g_buf, aug_buf, near_ref, acc, row_max, qh_ref, g_sem, near_sem,
):
    base = lax.axis_index("ctx") * pair
    origin = jnp.clip(base - reach * pair, 0, 4 * lines * pair - rows)
    blocks = rows // pair
    tiles = pair // TQ
    near_copy = pltpu.make_async_copy(near_hbm.at[0], near_ref, near_sem.at[0])
    near_copy.start()

    def document(position):
        def look(e, carry):
            begin, low, high = carry
            end = begin + lengths[e]
            inside = (begin <= position) & (position < end)
            return (end, jnp.where(inside, begin, low), jnp.where(inside, end, high))

        zero = jnp.int32(0)
        return lax.fori_loop(0, lengths.shape[0], look, (zero, zero, zero))[1:]

    def extent(t):
        first = base + t * TQ
        low = document(first)[0]
        high = document(first + TQ - 1)[1]
        n_left = jnp.maximum(0, first - EDGE - low + TK - 1) // TK
        n_right = jnp.maximum(0, high - (first - EDGE + TK) + TK - 1) // TK
        return low, high, n_left, n_right

    low_end = extent(0)[0] - origin
    high_end = extent(tiles - 1)[1] - origin
    from_block = jnp.maximum(0, low_end - TK) // pair
    to_block = jnp.minimum(blocks, (high_end + TK + pair - 1) // pair)

    def loads(n):
        at = pl.ds(pl.multiple_of(n * pair, pair), pair)
        to = pl.ds(pl.multiple_of(PAD + n * pair, 128), pair)
        slot = n % 2
        return (
            pltpu.make_async_copy(g_hbm.at[at], g_buf.at[slot], g_sem.at[0, slot]),
            pltpu.make_async_copy(aug_hbm.at[at], aug_buf.at[slot], g_sem.at[1, slot]),
            pltpu.make_async_copy(masks_hbm.at[n], mask_row.at[:, to], g_sem.at[2, slot]),
        )

    for copy in loads(from_block):
        copy.start()
    mask_row[:, :PAD] = jnp.zeros((8, PAD), f32)
    mask_row[:, PAD + rows :] = jnp.zeros((8, PAD), f32)
    km[:PAD, :] = jnp.broadcast_to(
        jnp.where(pad_lanes(plan), neg_big, 0.0).astype(bf16), (PAD, WIDE)
    )
    km[PAD + rows :, :] = km[:PAD, :]
    vm[:PAD, :] = jnp.zeros((PAD, WIDE), bf16)
    vm[PAD + rows :, :] = jnp.zeros((PAD, WIDE), bf16)
    low_lanes = lanes_of(pair, 128) < 64
    ones = (lanes_of(pair, 128) < 3 * plan.heads).astype(bf16)

    def build(n, unused):
        for copy in loads(n):
            copy.wait()

        @pl.when(n + 1 < to_block)
        def _():
            for copy in loads(n + 1):
                copy.start()

        to = pl.ds(pl.multiple_of(PAD + n * pair, 128), pair)
        middle = g_buf[n % 2, :, 128:256]
        km[to, 0:128] = g_buf[n % 2, :, 0:128]
        km[to, 128:256] = jnp.where(low_lanes, middle, aug_buf[n % 2])
        vm[to, 0:128] = jnp.where(low_lanes, ones, middle)
        vm[to, 128:256] = g_buf[n % 2, :, 256:384]
        return unused

    lax.fori_loop(from_block, to_block, build, 0)
    near_copy.wait()
    lane = lanes_of(TQ)

    def tile(t, unused):
        start = base - origin + t * TQ
        low_doc, high_doc, n_left, n_right = extent(t)
        count = n_left + n_right
        out = pl.ds(pl.multiple_of(t * TQ, TQ), TQ)
        q = q_ref[out, :]
        near = pl.ds(pl.multiple_of(start + PAD - EDGE, 128), TK)
        for h in range(plan.heads):
            qh = jnp.where(plan.key_lanes(lane, h), q, jnp.zeros_like(q))
            qh_ref[h] = qh
            s = nt(qh, km[near, :]) + near_ref[h] + mask_row[0:1, near]
            top = jnp.max(s, axis=1, keepdims=True)
            p = jnp.exp(s - top).astype(bf16)
            acc[h] = nn(p, vm[near, :])
            row_max[h] = jnp.broadcast_to(top, (TQ, 128))

        def far(n, unused):
            parts = far_pair(start, n, n_left, count, far_left_bucket, far_right_bucket)
            for h in range(plan.heads):
                scores = [
                    (nt(qh_ref[h], km[part, :]) + mask_row[0:1, part], table_ref[h, bucket])
                    for part, bucket in parts
                ]
                old = row_max[h][:, :1]
                top = old
                for s, offset in scores:
                    top = jnp.maximum(top, jnp.max(s, axis=1, keepdims=True) + offset)
                more = [
                    nn(jnp.exp(s - (top - offset)).astype(bf16), vm[part, :])
                    for (s, offset), (part, bucket) in zip(scores, parts)
                ]
                acc[h] = acc[h] * jnp.exp(old - top) + (more[0] + more[1])
                row_max[h] = jnp.broadcast_to(top, (TQ, 128))
            return unused

        lax.fori_loop(0, (count + 1) // 2, far, 0)
        wide = jnp.zeros((TQ, WIDE), f32)
        qb = jnp.where(lane < plan.stat_lane, q, jnp.zeros_like(q))
        for h in range(plan.heads):
            total = acc[h][:, 3 * h : 3 * h + 1]
            log_total = row_max[h][:, :1] + jnp.log(total)
            wide = jnp.where(lane // 64 == h + 1, acc[h] / total, wide)
            for i, part in enumerate(split3(-log_total)):
                qb = jnp.where(lane == plan.stat_lane + 3 * h + i, part, qb)
        wide_ref[out, :] = wide
        low_ref[out, :] = wide.astype(bf16)
        qb_ref[out, :] = qb
        return unused

    lax.fori_loop(0, tiles, tile, 0)


def attend(plan, cycle_size, reach, rows, lengths, table, q_wide, near_bias, kv_all, aug, masks):
    pair = q_wide.shape[0]
    heads = plan.heads
    padded = rows + 2 * PAD
    hbm = pl.BlockSpec(memory_space=pl.ANY)
    return pl.pallas_call(
        functools.partial(fwd_kernel, plan, cycle_size // 4, reach, rows, pair),
        out_shape=(
            jax.ShapeDtypeStruct((pair, WIDE), bf16),
            jax.ShapeDtypeStruct((pair, WIDE), f32),
            jax.ShapeDtypeStruct((pair, WIDE), bf16),
        ),
        in_specs=[smem, smem, vmem] + [hbm] * 4,
        out_specs=(vmem, vmem, vmem),
        scratch_shapes=[
            pltpu.VMEM((padded, WIDE), bf16),
            pltpu.VMEM((padded, WIDE), bf16),
            pltpu.VMEM((8, padded), f32),
            pltpu.VMEM((2, pair, 2 * plan.cols), bf16),
            pltpu.VMEM((2, pair, 128), bf16),
            pltpu.VMEM((heads, TQ, TK), f32),
            pltpu.VMEM((heads, TQ, WIDE), f32),
            pltpu.VMEM((heads, TQ, 128), f32),
            pltpu.VMEM((heads, TQ, WIDE), bf16),
            pltpu.SemaphoreType.DMA((3, 2)),
            pltpu.SemaphoreType.DMA((1,)),
        ],
        compiler_params=params(),
        name="attention_forward",
    )(lengths, table, q_wide, near_bias, kv_all, aug, masks)


vmem = pl.BlockSpec(memory_space=pltpu.VMEM)
smem = pl.BlockSpec(memory_space=pltpu.SMEM)


def params():
    return pltpu.CompilerParams(vmem_limit_bytes=56 * 2**20)


class Spot:
    def __init__(self, lines):
        index = lax.axis_index("ctx")
        self.wa = lax.axis_index("wa")
        self.index = index
        self.lines = lines
        self.z = index // 4
        self.x = (index // 2) % 2
        self.core = index % 2

    def core_mate(self):
        return (self.index + 1 - 2 * self.core, self.wa)

    def x_mate(self):
        return (self.index + 2 - 4 * self.x, self.wa)

    def z_mate(self, step):
        return (jnp.clip(self.index + 4 * step, 0, 4 * self.lines - 1), self.wa)

    def y_mate(self):
        return (self.index, 1 - self.wa)


def send(src, dst, send_sem, recv_sem, device):
    return pltpu.make_async_remote_copy(
        src_ref=src,
        dst_ref=dst,
        send_sem=send_sem,
        recv_sem=recv_sem,
        device_id=device,
        device_id_type=pl.DeviceIdType.MESH,
    )


def greet(spot, with_y):
    barrier = pltpu.get_barrier_semaphore()
    mates = [spot.core_mate(), spot.x_mate()] + ([spot.y_mate()] if with_y else [])
    for mate in mates:
        pl.semaphore_signal(barrier, inc=1, device_id=mate, device_id_type=pl.DeviceIdType.MESH)

    @pl.when(spot.z + 1 < spot.lines)
    def _():
        pl.semaphore_signal(
            barrier, inc=1, device_id=spot.z_mate(1), device_id_type=pl.DeviceIdType.MESH
        )

    @pl.when(spot.z > 0)
    def _():
        pl.semaphore_signal(
            barrier, inc=1, device_id=spot.z_mate(-1), device_id_type=pl.DeviceIdType.MESH
        )

    above = (spot.z + 1 < spot.lines).astype(jnp.int32)
    below = (spot.z > 0).astype(jnp.int32)
    pl.semaphore_wait(barrier, len(mates) + above + below)


def added(a, b):
    return a + b


def first_kernel(
    plan, lines, span, reach, rows, lengths, table_ref, tokens_ref, gain_ref, key_mask_ref,
    wq_hbm, wk_hbm, wv_hbm, wo_hbm,
    x_ref, tok_ref, q_ref, own_ref, aug_ref, own_aug_ref, near_ref, masks_ref, wo_far_hbm, all_hbm,
    weights, zeros, mask_ref, load_sem, y_sem, own_sem, zero_sem, z_sem, x_sem, c_sem,
):
    spot = Spot(lines)
    z, x, core, wa = (spot.z, spot.x, spot.core, spot.wa)
    half, model = tokens_ref.shape
    cols = plan.cols
    chunk = half // 4
    loads = [
        pltpu.make_async_copy(src, weights.at[pl.ds(i * cols, cols)], load_sem.at[i])
        for i, src in enumerate((wk_hbm, wv_hbm, wq_hbm))
    ]
    for load in loads:
        load.start()
    mask_ref[...] = jnp.broadcast_to(key_mask_ref[...].astype(f32)[None, :], mask_ref.shape)
    greet(spot, True)
    zeros[...] = jnp.zeros_like(zeros)

    def outside(d):
        return (d < z - span) | (d > z + span)

    def zero_copies(d):
        return [
            pltpu.make_async_copy(zeros, all_hbm.at[d, a, b], zero_sem.at[d, a, b])
            for a in range(2)
            for b in range(2)
        ]

    def zero_start(d, unused):
        @pl.when(outside(d))
        def _():
            masks_ref[d] = jnp.zeros((2, 2) + mask_ref.shape, f32)
            for copy in zero_copies(d):
                copy.start()

        return unused

    def rows_at(start, size):
        return pl.ds(pl.multiple_of(start, size), size)

    ours = wa * half
    theirs = (1 - wa) * half

    def y_copy(i, base):
        return send(
            tokens_ref.at[rows_at(i * chunk, chunk)],
            tok_ref.at[rows_at(base + i * chunk, chunk)],
            y_sem.at[0, i],
            y_sem.at[1, i],
            spot.y_mate(),
        )

    def y_start(i, unused):
        y_copy(i, ours).start()
        return unused

    lax.fori_loop(0, 4, y_start, 0)
    far_copy = send(wo_hbm, wo_far_hbm, y_sem.at[0, 4], y_sem.at[1, 4], spot.y_mate())

    def scaled(rows_in):
        rows_in = rows_in.astype(f32)
        inv = lax.rsqrt(jnp.mean(rows_in * rows_in, axis=-1, keepdims=True) + eps)
        return (rows_in * inv * gain_ref[...][None, :]).astype(bf16)

    def normal(i, unused):
        at = rows_at(ours + i * chunk, chunk)
        rows_in = tokens_ref[rows_at(i * chunk, chunk), :]
        tok_ref[at, :] = rows_in
        x_ref[at, :] = scaled(rows_in)
        return unused

    lax.fori_loop(0, 4, normal, 0)
    for load in loads:
        load.wait()

    def project(base):
        rows = rows_at(base, half)
        qkv = nt(x_ref[rows, :], weights[...]).astype(bf16)
        own_ref[rows, :] = qkv[:, : 2 * cols]
        q_ref[rows, :cols] = qkv[:, 2 * cols :]

    pieces = [
        (ours, half, True),
        (theirs, half // 2, True),
        (theirs + half // 2, half // 2, False),
        None,
    ]
    mask_piece = 3

    def line_first(p):
        return p == mask_piece or pieces[p][2]

    def piece_rows(p):
        return rows_at(pieces[p][0], pieces[p][1])

    def source(p, d, a):
        if p == mask_piece:
            return masks_ref.at[d, a, core]
        return all_hbm.at[d, a, core, piece_rows(p)]

    def own_source(p):
        return mask_ref if p == mask_piece else own_ref.at[piece_rows(p)]

    def pass_copy(p, step, d, own):
        i = 0 if step > 0 else 1
        if line_first(p):
            dst = source(p, d, x)
            src = own_source(p) if own else dst
        else:
            dst = all_hbm.at[d, :, core, piece_rows(p)]
            src = dst
        return send(src, dst, z_sem.at[p, i, d], z_sem.at[p, 2 + i, d], spot.z_mate(step))

    def across(p, d, own):
        dst = source(p, d, x)
        src = own_source(p) if own else dst
        return send(src, dst, x_sem.at[p, 0, d], x_sem.at[p, 1, d], spot.x_mate())

    def beside(p, d):
        if p == mask_piece:
            part = masks_ref.at[d, :, core]
        else:
            part = all_hbm.at[d, :, core, piece_rows(p)]
        return send(part, part, c_sem.at[p, 0, d], c_sem.at[p, 1, d], spot.core_mate())

    def own_copy(p):
        return pltpu.make_async_copy(
            own_source(p), source(p, z, x), own_sem.at[p]
        )

    def both_ways(p, own):
        @pl.when(z + 1 < lines)
        def _():
            pass_copy(p, 1, z, own).start()

        @pl.when(z > 0)
        def _():
            pass_copy(p, -1, z, own).start()

    def begin(p):
        own_copy(p).start()
        across(p, z, True).start()
        if line_first(p):
            both_ways(p, True)

    def level(p, k):
        @pl.when(z - k >= 0)
        def _():
            d = jnp.maximum(z - k, 0)
            pass_copy(p, 1, d, False).wait_recv()
            if k < span:

                @pl.when(z + 1 < lines)
                def _():
                    pass_copy(p, 1, d, False).start()

            if line_first(p):
                across(p, d, False).start()
            else:
                beside(p, d).start()

        @pl.when(z + k < lines)
        def _():
            d = jnp.minimum(z + k, lines - 1)
            pass_copy(p, -1, d, False).wait_recv()
            if k < span:

                @pl.when(z > 0)
                def _():
                    pass_copy(p, -1, d, False).start()

            if line_first(p):
                across(p, d, False).start()
            else:
                beside(p, d).start()

    def turn(p):
        across(p, z, True).wait()
        own_copy(p).wait()
        both_ways(p, False)
        beside(p, z).start()

    def settle(p, k):
        for sign in (1, -1) if k else (1,):
            d = z - sign * k

            @pl.when((d >= 0) & (d < lines))
            def _(d=d):
                d = jnp.clip(d, 0, lines - 1)
                across(p, d, k == 0).wait()
                if k == 0:
                    own_copy(p).wait()
                beside(p, d).start()

    def doc_of(start, size):
        position = start + lax.broadcasted_iota(jnp.int32, (size, 128), 0)

        def count(e, carry):
            begin, total = carry
            begin = begin + lengths[e]
            return (begin, total + (position >= begin).astype(jnp.int32))

        zero = (jnp.int32(0), jnp.zeros((size, 128), jnp.int32))
        return lax.fori_loop(0, lengths.shape[0] - 1, count, zero)[1]

    def code_lanes(start, size):
        lane = lanes_of(size, 128) + 128
        code = jnp.maximum(lane - plan.doc_lane, 0)
        bit = jnp.bitwise_and(jnp.right_shift(doc_of(start, size), code // 2), 1)
        coded = (lane >= plan.doc_lane) & (lane < plan.stat_lane)
        ones = (lane >= plan.stat_lane) & (lane < plan.stat_lane + 3 * plan.heads)
        return lane, coded, bit != code % 2, ones

    pair = 2 * half
    base = spot.index * pair
    origin = jnp.clip(base - reach * pair, 0, 4 * lines * pair - rows)

    def key_lanes(n, unused):
        at = rows_at(n * half, half)
        lane, coded, differs, ones = code_lanes(origin + n * half, half)
        aug_ref[at, :] = jnp.where(
            coded & differs, neg_big, jnp.where(ones, 1.0, 0.0)
        ).astype(bf16)
        return unused

    def own_lanes(n, unused):
        at = rows_at(n * half, half)
        lane, coded, differs, ones = code_lanes(base + n * half, half)
        column = jnp.transpose(
            jnp.broadcast_to(mask_ref[0:1, at], (128, half))
        )
        own_aug_ref[at, :] = jnp.where(
            lane == plan.mask_lane,
            column,
            jnp.where(coded & differs, neg_big, jnp.where(ones, 1.0, 0.0)),
        ).astype(bf16)
        tail = jnp.where(
            (lane == plan.mask_lane) | (coded & ~differs), 1.0, 0.0
        ).astype(bf16)
        q_ref[at, 128:] = tail
        return unused

    begin(mask_piece)
    lax.fori_loop(0, 2, own_lanes, 0)
    project(ours)
    begin(0)
    lax.fori_loop(0, lines, zero_start, 0)
    near_lanes(plan.heads, table_ref, near_ref)
    lax.fori_loop(0, rows // half, key_lanes, 0)

    def y_wait(i, unused):
        y_copy(i, theirs).wait_recv()
        at = rows_at(theirs + i * chunk, chunk)
        x_ref[at, :] = scaled(tok_ref[at, :])
        return unused

    lax.fori_loop(0, 2, y_wait, 0)
    level(0, 1)
    level(mask_piece, 1)
    lax.fori_loop(2, 4, y_wait, 0)
    far_copy.start()
    project(theirs)
    begin(2)
    begin(1)
    if span > 1:
        level(0, 2)
        level(mask_piece, 2)
    settle(0, 0)
    settle(mask_piece, 0)
    turn(2)
    level(1, 1)
    settle(0, 1)
    settle(mask_piece, 1)
    level(2, 1)
    if span > 1:
        level(1, 2)
        settle(0, 2)
        settle(mask_piece, 2)
    settle(1, 0)
    settle(1, 1)
    if span > 1:
        level(2, 2)
        settle(1, 2)
    for k in range(3, span + 1):
        for p in range(4):
            level(p, k)
        for p in (0, 1, mask_piece):
            settle(p, k)

    def finish_line(d, unused):
        @pl.when(~outside(d))
        def _():
            for p in range(4):
                beside(p, d).wait()

        @pl.when(outside(d))
        def _():
            for copy in zero_copies(d):
                copy.wait()

        for p in range(4):

            @pl.when((z + 1 < lines) & (d <= z) & (d > z - span))
            def _(p=p):
                pass_copy(p, 1, d, False).wait_send()

            @pl.when((z > 0) & (d >= z) & (d < z + span))
            def _(p=p):
                pass_copy(p, -1, d, False).wait_send()

        return unused

    lax.fori_loop(0, lines, finish_line, 0)

    def y_drain(i, unused):
        y_copy(i, ours).wait_send()
        return unused

    lax.fori_loop(0, 4, y_drain, 0)
    far_copy.wait()


def first(
    plan, cycle_size, reach, rows, lengths, table, tokens, gain, mask, w_query, w_key, w_value, w_out
):
    lines = cycle_size // 4
    span = min(lines - 1, (reach + 3) // 4)
    half, model = tokens.shape
    pair = 2 * half
    hbm = pl.BlockSpec(memory_space=pl.ANY)
    dma = pltpu.SemaphoreType.DMA
    return pl.pallas_call(
        functools.partial(first_kernel, plan, lines, span, reach, rows),
        out_shape=[
            jax.ShapeDtypeStruct((pair, model), bf16),
            jax.ShapeDtypeStruct((pair, model), bf16),
            jax.ShapeDtypeStruct((pair, WIDE), bf16),
            jax.ShapeDtypeStruct((pair, 2 * plan.cols), bf16),
            jax.ShapeDtypeStruct((rows, 128), bf16),
            jax.ShapeDtypeStruct((pair, 128), bf16),
            jax.ShapeDtypeStruct((2, plan.heads, TQ, TK), f32),
            jax.ShapeDtypeStruct((lines, 2, 2, 8, pair), f32),
            jax.ShapeDtypeStruct(w_out.shape, bf16),
            jax.ShapeDtypeStruct((lines, 2, 2, pair, 2 * plan.cols), bf16),
        ],
        in_specs=[smem] * 2 + [vmem] * 3 + [hbm] * 4,
        out_specs=[vmem] * 8 + [hbm] * 2,
        scratch_shapes=[
            pltpu.VMEM((3 * plan.cols, model), bf16),
            pltpu.VMEM((pair, 2 * plan.cols), bf16),
            pltpu.VMEM((8, pair), f32),
            dma((3,)),
            dma((2, 5)),
            dma((4,)),
            dma((lines, 2, 2)),
            dma((4, 4, lines)),
            dma((4, 2, lines)),
            dma((4, 2, lines)),
        ],
        compiler_params=pltpu.CompilerParams(
            vmem_limit_bytes=56 * 2**20, collective_id=4, has_side_effects=True
        ),
        name="project_gather",
    )(lengths, table, tokens, gain, mask, w_query.T, w_key.T, w_value.T, w_out)


def tn(a, b):
    return lax.dot_general(a, b, (((0,), (0,)), ((), ())), preferred_element_type=f32)


def line_relay(spot, start, receive):
    def level(k, unused):
        @pl.when(spot.z - k >= 0)
        def _():
            if_first(k, lambda: receive(1, spot.z - k))

            @pl.when(spot.z + 1 < spot.lines)
            def _():
                start(1, spot.z - k)

        @pl.when(spot.z + k < spot.lines)
        def _():
            if_first(k, lambda: receive(-1, spot.z + k))

            @pl.when(spot.z > 0)
            def _():
                start(-1, spot.z + k)

        return unused

    def if_first(k, run):
        @pl.when(k > 0)
        def _():
            run()

    return level


def finish_kernel(
    plan, lines, dq_hbm, dk_hbm, dv_hbm, att_hbm, normed_hbm, branch_hbm, far_hbm,
    wq_hbm, wk_hbm, wv_hbm, mask_ref, tokens_ref, gain_ref, gh_ref, table_ref, gain_part_ref,
    gt_ref, gm_ref, weights_ref, gain_one_ref, gain_two_ref, table_out_ref,
    w3_ref, load_sem, lefts, rights, product, mine, core_in, x_in, up_in, down_in, all_w, y_out, y_in, own_part, mask_in,
    small_own, small_y, small_core, small_x, small_all,
    y_sem, core_sem, x_sem, up_sem, down_sem, gz_sem, gx_sem, gc_sem, sz_sem,
):
    spot = Spot(lines)
    z, x, core, wa = (spot.z, spot.x, spot.core, spot.wa)
    cols = plan.cols
    half = tokens_ref.shape[0]
    our_rows = pl.ds(pl.multiple_of(wa * half, half), half)
    their_rows = pl.ds(pl.multiple_of((1 - wa) * half, half), half)
    targets = (
        (dq_hbm, lefts.at[0]),
        (normed_hbm, rights.at[0]),
        (att_hbm, lefts.at[3]),
        (branch_hbm, rights.at[1, our_rows]),
        (far_hbm, rights.at[1, their_rows]),
        (dk_hbm, lefts.at[1]),
        (dv_hbm, lefts.at[2]),
        (wq_hbm, w3_ref.at[pl.ds(0, cols)]),
        (wk_hbm, w3_ref.at[pl.ds(WIDE, cols)]),
        (wv_hbm, w3_ref.at[pl.ds(3 * WIDE - cols, cols)]),
    )
    loads = [
        pltpu.make_async_copy(src, dst, load_sem.at[i]) for i, (src, dst) in enumerate(targets)
    ]
    for load in loads:
        load.start()
    gap = jnp.zeros((WIDE - cols, tokens_ref.shape[1]), bf16)
    w3_ref[cols:WIDE] = gap
    w3_ref[WIDE + cols : 2 * WIDE] = gap
    w3_ref[2 * WIDE : 3 * WIDE - cols] = gap
    greet(spot, True)
    quarter = half // 2
    model = tokens_ref.shape[1]
    rows = mine.shape[3]

    def grad_rows(at):
        at = pl.ds(pl.multiple_of(at, quarter), quarter)
        return (
            nn(lefts[0, at, :], w3_ref[0:256])
            + nn(lefts[1, at, :], w3_ref[256:512])
            + nn(lefts[2, at, :], w3_ref[512:768])
        )

    def y_copy(i):
        return send(y_out.at[i], y_in.at[i], y_sem.at[0, i], y_sem.at[1, i], spot.y_mate())

    def theirs(i, unused):
        y_out[i] = grad_rows((1 - wa) * half + i * quarter).astype(bf16)
        y_copy(i).start()
        return unused

    for i in (0, 5, 6, 7, 8, 9):
        loads[i].wait()
    lax.fori_loop(0, 2, theirs, 0)
    mask_copy = send(
        mask_ref.at[1 - wa], mask_in, y_sem.at[0, 2], y_sem.at[1, 2], spot.y_mate()
    )
    mask_copy.start()
    for i in (1, 2, 3, 4):
        loads[i].wait()
    per = plan.cols // rows

    def core_copy(m):
        part = pl.ds(m * per // 4, per // 4)
        return send(
            mine.at[part, :, 1 - core],
            core_in.at[part],
            core_sem.at[0, m],
            core_sem.at[1, m],
            spot.core_mate(),
        )

    def fill(i, unused):
        m = (3 * i) % 4
        product[...] = tn(lefts[m], rights[m // 3]).astype(bf16)

        def place(offset):
            for j in range(per):
                mine[m * per // 4 + j // 4, (j // 2) % 2, j % 2] = product[
                    offset + j * rows : offset + (j + 1) * rows, :
                ]

        @pl.when(m < 2)
        def _():
            place(0)

        @pl.when(m >= 2)
        def _():
            place(WIDE - plan.cols)

        core_copy(m).start()
        return unused

    lax.fori_loop(0, 4, fill, 0)
    def x_copy(d):
        return send(
            mine.at[d, 1 - x, core], x_in.at[d], x_sem.at[0, d], x_sem.at[1, d], spot.x_mate()
        )

    def core_add(d, unused):
        mine[d, 1 - x, core] = added(mine[d, 1 - x, core], core_in[d, 1 - x])
        x_copy(d).start()
        return unused

    def ours(i, unused):
        own_part[pl.ds(pl.multiple_of(i * quarter, quarter), quarter), :] = grad_rows(
            wa * half + i * quarter
        )
        return unused

    def core_stage(i, unused):
        m = (3 * i) % 4
        core_copy(m).wait()
        lax.fori_loop(m * per // 4, (m + 1) * per // 4, core_add, 0)
        return unused

    lax.fori_loop(0, 4, core_stage, 0)

    def core_add_own(d, unused):
        mine[d, x, core] = added(mine[d, x, core], core_in[d, x])
        return unused

    lax.fori_loop(0, lines, core_add_own, 0)
    lax.fori_loop(0, 2, ours, 0)

    def flow(step, d):
        ring, sem = (up_in, up_sem) if step > 0 else (down_in, down_sem)
        return send(
            mine.at[d, x, core], ring.at[d], sem.at[0, d], sem.at[1, d], spot.z_mate(step)
        )

    def merge(step, d):
        flow(step, d).wait_recv()
        ring = up_in if step > 0 else down_in
        mine[d, x, core] = added(mine[d, x, core], ring[d])

    def x_add(i, unused):
        d = (i * (lines - 1)) % lines
        x_copy(d).wait()
        mine[d, x, core] = added(mine[d, x, core], x_in[d])

        @pl.when((z == 0) & (d > 0))
        def _():
            flow(1, d).start()

        @pl.when((z == lines - 1) & (d < lines - 1))
        def _():
            flow(-1, d).start()

        return unused

    lax.fori_loop(0, lines, x_add, 0)
    gain_sum = jnp.zeros((1, model), f32)
    step = 32
    for i in range(2):
        y_copy(i).wait()

        def normal(j, total, i=i):
            at = pl.ds(pl.multiple_of(i * quarter + j * step, step), step)
            there = pl.ds(pl.multiple_of(j * step, step), step)
            grad = own_part[at, :] + y_in[i, there, :].astype(f32)
            rows_in = tokens_ref[at, :].astype(f32)
            inv = lax.rsqrt(jnp.mean(rows_in * rows_in, axis=-1, keepdims=True) + eps)
            scaled = gain_ref[...][None, :] * grad
            mean = jnp.mean(rows_in * scaled, axis=-1, keepdims=True)
            gt_ref[at, :] = gh_ref[at, :] + inv * scaled - rows_in * (inv * inv * inv * mean)
            return total + jnp.sum(grad * rows_in * inv, axis=0, keepdims=True)

        gain_sum = lax.fori_loop(0, quarter // step, normal, gain_sum)
    small_own[...] = jnp.zeros_like(small_own)
    small_own[0:1, :] = gain_sum
    small_own[1:2, :] = gain_part_ref[...]
    for h in range(plan.heads):
        small_own[2:3, 32 * h : 32 * h + 32] = jnp.sum(
            jnp.transpose(table_ref[h]), axis=0, keepdims=True
        )
    small_copy = send(
        small_own, small_y, y_sem.at[0, 4], y_sem.at[1, 4], spot.y_mate()
    )
    small_copy.start()
    mask_copy.wait()
    gm_ref[...] = jnp.sum(mask_ref[wa, 0:1] + mask_in[0:1], axis=0)
    def relay(k, unused):
        high = lines - 1 - k

        @pl.when((z < high) & (z > 0))
        def _():
            merge(1, high)
            flow(1, high).start()

        @pl.when((z > k) & (z + 1 < lines))
        def _():
            merge(-1, k)
            flow(-1, k).start()

        return unused

    lax.fori_loop(0, 1, relay, 0)
    small_copy.wait()
    row = lax.broadcasted_iota(jnp.int32, small_own.shape, 0)
    small_x[0] = small_own[...] + jnp.where(row < 2, small_y[...], 0.0)
    small_core_copy = send(
        small_x.at[0], small_core, core_sem.at[0, 4], core_sem.at[1, 4], spot.core_mate()
    )
    small_core_copy.start()
    lax.fori_loop(1, lines - 1, relay, 0)
    small_core_copy.wait()
    small_x[1] = small_x[0] + small_core[...]
    small_x_copy = send(
        small_x.at[1], small_x.at[2], x_sem.at[0, lines], x_sem.at[1, lines], spot.x_mate()
    )
    small_x_copy.start()

    @pl.when(z > 0)
    def _():
        merge(1, z)

    @pl.when(z + 1 < lines)
    def _():
        merge(-1, z)

    all_w[z, x, core] = mine[z, x, core]

    def pass_w(step, d):
        i = 0 if step > 0 else 1
        return send(
            all_w.at[d, x, core], all_w.at[d, x, core], gz_sem.at[i, d], gz_sem.at[2 + i, d],
            spot.z_mate(step),
        )

    def pass_s(step, d):
        i = 0 if step > 0 else 1
        return send(
            small_all.at[d], small_all.at[d], sz_sem.at[i, d], sz_sem.at[2 + i, d],
            spot.z_mate(step),
        )

    def across(d):
        return send(
            all_w.at[d, x, core], all_w.at[d, x, core], gx_sem.at[0, d], gx_sem.at[1, d],
            spot.x_mate(),
        )

    def beside(d):
        return send(
            all_w.at[d, :, core], all_w.at[d, :, core], gc_sem.at[0, d], gc_sem.at[1, d],
            spot.core_mate(),
        )

    small_x_copy.wait()
    small_all[z] = small_x[1] + small_x[2]

    def receive(step, d):
        pass_w(step, d).wait_recv()
        across(d).start()

    across(z).start()
    def pass_both(step, d):
        pass_s(step, d).start()
        pass_w(step, d).start()

    def receive_both(step, d):
        pass_s(step, d).wait_recv()
        receive(step, d)

    lax.fori_loop(0, lines, line_relay(spot, pass_both, receive_both), 0)

    def add_small(d, total):
        return total + small_all[d]

    totals = lax.fori_loop(1, lines, add_small, small_all[0])
    gain_one_ref[...] = jnp.sum(totals[0:1], axis=0)
    gain_two_ref[...] = jnp.sum(totals[1:2], axis=0)
    for h in range(plan.heads):
        table_out_ref[h : h + 1, :] = totals[2:3, 32 * h : 32 * h + 32]
    def spread(d, unused):
        across(d).wait()
        beside(d).start()
        return unused

    lax.fori_loop(0, lines, spread, 0)

    def copy_out(d, unused):
        beside(d).wait()
        weights_ref[d] = all_w[d]
        return unused

    lax.fori_loop(0, lines, copy_out, 0)

    def drain(d, unused):
        @pl.when((z < d))
        def _():
            flow(1, d).wait_send()

        @pl.when((z > d))
        def _():
            flow(-1, d).wait_send()

        @pl.when((d <= z) & (z + 1 < lines))
        def _():
            pass_w(1, d).wait_send()
            pass_s(1, d).wait_send()

        @pl.when((d >= z) & (z > 0))
        def _():
            pass_w(-1, d).wait_send()
            pass_s(-1, d).wait_send()

        return unused

    lax.fori_loop(0, lines, drain, 0)


def finish(plan, cycle_size, *operands):
    lines = cycle_size // 4
    half, model = operands[11].shape
    rows = 4 * plan.cols // cycle_size
    dma = pltpu.SemaphoreType.DMA
    return pl.pallas_call(
        functools.partial(finish_kernel, plan, lines),
        out_shape=[
            jax.ShapeDtypeStruct((half, model), f32),
            jax.ShapeDtypeStruct((half,), f32),
            jax.ShapeDtypeStruct((lines, 2, 2, rows, model), bf16),
            jax.ShapeDtypeStruct((model,), f32),
            jax.ShapeDtypeStruct((model,), f32),
            jax.ShapeDtypeStruct((plan.heads, 32), f32),
        ],
        in_specs=[pl.BlockSpec(memory_space=pl.ANY)] * 10 + [vmem] * 6,
        out_specs=[vmem] * 6,
        scratch_shapes=[
            pltpu.VMEM((3 * WIDE, model), bf16),
            dma((10,)),
            pltpu.VMEM((4, 2 * half, WIDE), bf16),
            pltpu.VMEM((2, 2 * half, model), bf16),
            pltpu.VMEM((WIDE, model), bf16),
            pltpu.VMEM((lines, 2, 2, rows, model), bf16),
            pltpu.VMEM((lines, 2, rows, model), bf16),
            pltpu.VMEM((lines, rows, model), bf16),
            pltpu.VMEM((lines, rows, model), bf16),
            pltpu.VMEM((lines, rows, model), bf16),
            pltpu.VMEM((lines, 2, 2, rows, model), bf16),
            pltpu.VMEM((2, half // 2, model), bf16),
            pltpu.VMEM((2, half // 2, model), bf16),
            pltpu.VMEM((half, model), f32),
            pltpu.VMEM((8, half), f32),
            pltpu.VMEM((8, model), f32),
            pltpu.VMEM((8, model), f32),
            pltpu.VMEM((8, model), f32),
            pltpu.VMEM((3, 8, model), f32),
            pltpu.VMEM((lines, 8, model), f32),
            dma((2, 5)),
            dma((2, 5)),
            dma((2, lines + 1)),
            dma((2, lines)),
            dma((2, lines)),
            dma((4, lines)),
            dma((2, lines)),
            dma((2, lines)),
            dma((4, lines)),
        ],
        compiler_params=pltpu.CompilerParams(
            vmem_limit_bytes=58 * 2**20, collective_id=2, has_side_effects=True
        ),
        name="finish",
    )(*operands)


root = 0.7978845608028654
cubic = 0.044715


def middle_kernel(
    plan, cycle_size, att_ref, mixed_ref, tokens_ref, cot_ref, gain_ref,
    wo_hbm, wo_far_hbm, wg_hbm, wu_hbm, wd_hbm,
    hidden_ref, gh_ref, branch_ref, ffn_ref, ffn_far_ref, do_ref, gain_part_ref, *refs,
):
    stacks, refs = (refs[:3], refs[3:])
    (
        wg, wu, wd, wo, inner, gg, gu, x_ref, att_in, d_out, d_in, e_out, e_in,
        acc_f, acc_g, rows_buf, load_sem, y_sem, out_sem,
    ) = refs
    spot = Spot(cycle_size // 4)
    wa = spot.wa
    pair, model = tokens_ref.shape
    half = pair // 2
    units = wd.shape[1]
    chunk = half // 4
    block = pair // 4
    loads = [
        pltpu.make_async_copy(src, dst, load_sem.at[i])
        for i, (src, dst) in enumerate(
            (
                (wo_hbm, wo.at[0, 64:]),
                (wo_far_hbm, wo.at[1, 64:]),
                (wg_hbm, wg),
                (wu_hbm, wu),
                (wd_hbm, wd),
            )
        )
    ]
    for load in loads:
        load.start()
    barrier = pltpu.get_barrier_semaphore()
    pl.semaphore_signal(
        barrier, inc=1, device_id=spot.y_mate(), device_id_type=pl.DeviceIdType.MESH
    )
    wo[:, :64, :] = jnp.zeros((2, 64, model), bf16)
    pl.semaphore_wait(barrier, 1)
    ours = wa * half
    theirs = (1 - wa) * half

    def rows_at(start, size):
        return pl.ds(pl.multiple_of(start, size), size)

    def a_start(i):
        return (theirs + i * block) if i < 2 else (ours + (i - 2) * block)

    def a_copy(i, base):
        at = rows_at(base + (i % 2) * block, block)
        return send(att_ref.at[at], att_in.at[at], y_sem.at[0, i], y_sem.at[1, i], spot.y_mate())

    order = (0, 1, 2, 3)
    for i in order:
        a_copy(i, ours if i < 2 else theirs).start()
    loads[0].wait()
    loads[1].wait()

    def normal(i, base, keep):
        a_copy(i, base).wait_recv()
        at = rows_at(base + (i % 2) * block, block)
        branch = nn(att_ref[at, :], wo[0]) + nn(att_in[at, :], wo[1])
        hidden = tokens_ref[at, :].astype(f32) + branch
        if keep:
            hidden_ref[(i % 2) * block : (i % 2 + 1) * block, :] = hidden
        inv = lax.rsqrt(jnp.mean(hidden * hidden, axis=-1, keepdims=True) + eps)
        x_ref[at, :] = (hidden * inv * gain_ref[...][None, :]).astype(bf16)

    normal(0, theirs, False)
    normal(1, theirs, False)
    for load in loads[2:]:
        load.wait()
    wide = 256

    def feed(base):
        rows = rows_at(base, half)
        acc_f[...] = jnp.zeros_like(acc_f)
        acc_g[...] = jnp.zeros_like(acc_g)

        def tile(u, unused):
            cols = rows_at(u * wide, wide)
            gate = nn(x_ref[rows, :], wg[:, cols])
            upward = nn(x_ref[rows, :], wu[:, cols])
            grad_inner = nn(cot_ref[rows, :], wd[:, cols])
            square = gate * gate
            bend = jnp.tanh(root * gate * (1.0 + cubic * square))
            side = 0.5 * (1.0 + bend)
            gelu = gate * side
            slope = side + 0.5 * gate * (1.0 - bend * bend) * (
                root * (1.0 + 3.0 * cubic * square)
            )
            inner_low = (gelu * upward).astype(bf16)
            gate_low = (grad_inner * upward * slope).astype(bf16)
            up_low = (grad_inner * gelu).astype(bf16)
            inner[rows, cols] = inner_low
            gg[rows, cols] = gate_low
            gu[rows, cols] = up_low
            acc_g[...] += nt(gate_low, wg[:, cols]) + nt(up_low, wu[:, cols])
            acc_f[...] += nt(inner_low, wd[:, cols])
            return unused

        lax.fori_loop(0, units // wide, tile, 0)

    def d_copy(i):
        return send(
            d_out.at[i], d_in.at[i], y_sem.at[0, 4 + i], y_sem.at[1, 4 + i], spot.y_mate()
        )

    def send_grad(i, unused):
        d_out[i] = acc_g[rows_at(i * chunk, chunk), :].astype(bf16)
        d_copy(i).start()
        return unused

    def half_pass(k, unused):
        base = theirs + k * (ours - theirs)
        feed(base)

        @pl.when(k == 0)
        def _():
            lax.fori_loop(0, 4, send_grad, 0)
            normal(2, ours, True)
            normal(3, ours, True)
            ffn_far_ref[...] = acc_f[...].astype(bf16)

        @pl.when(k == 1)
        def _():
            ffn_ref[...] = acc_f[...].astype(bf16)

        return unused

    lax.fori_loop(0, 2, half_pass, 0)
    count = units // wide

    def out_copy(m, u):
        return pltpu.make_async_copy(
            rows_buf.at[m, u % 2],
            stacks[m].at[rows_at(u * wide, wide)],
            out_sem.at[m, u % 2],
        )

    for m in range(3):
        left = (inner, gg, gu)[m]
        right = (cot_ref, x_ref, x_ref)[m]

        def weight_rows(u, unused, m=m, left=left, right=right):
            @pl.when(u >= 2)
            def _():
                out_copy(m, u - 2).wait()

            turned = jnp.transpose(left[:, rows_at(u * wide, wide)])
            rows_buf[m, u % 2] = nn(turned, right[...]).astype(bf16)
            out_copy(m, u).start()
            return unused

        lax.fori_loop(0, count, weight_rows, 0)

    def e_copy(i):
        return send(
            e_out.at[i], e_in.at[i], y_sem.at[0, 8 + i], y_sem.at[1, 8 + i], spot.y_mate()
        )

    def normal_back(i, total):
        d_copy(i).wait()
        at = rows_at(i * chunk, chunk)
        grad = acc_g[at, :] + d_in[i].astype(f32)
        hidden = hidden_ref[at, :]
        inv = lax.rsqrt(jnp.mean(hidden * hidden, axis=-1, keepdims=True) + eps)
        scaled = gain_ref[...][None, :] * grad
        mean = jnp.mean(hidden * scaled, axis=-1, keepdims=True)
        grad_hidden = (
            cot_ref[rows_at(ours + i * chunk, chunk), :].astype(f32)
            + inv * scaled
            - hidden * (inv * inv * inv * mean)
        )
        gh_ref[at, :] = grad_hidden
        low = grad_hidden.astype(bf16)
        branch_ref[at, :] = low
        e_out[i] = nt(low, wo[1]).astype(bf16)
        e_copy(i).start()
        do_ref[rows_at(ours + i * chunk, chunk), :] = nt(low, wo[0]).astype(bf16)
        return total + jnp.sum(grad * hidden * inv, axis=0, keepdims=True)

    gain_part_ref[...] = lax.fori_loop(0, 4, normal_back, jnp.zeros((1, model), f32))

    def row_terms(at, grad):
        lane = lanes_of(chunk)
        terms = grad.astype(f32) * mixed_ref[at, :]
        out = grad
        for h in range(plan.heads):
            row_term = jnp.sum(
                jnp.where(lane // 64 == h + 1, terms, 0.0), axis=1, keepdims=True
            )
            for i, part in enumerate(split3(-row_term)):
                out = jnp.where(lane == 3 * h + i, part, out)
        do_ref[at, :] = out

    def own_terms(i, unused):
        at = rows_at(ours + i * chunk, chunk)
        row_terms(at, do_ref[at, :])
        return unused

    lax.fori_loop(0, 4, own_terms, 0)

    def far_terms(i, unused):
        e_copy(i).wait()
        row_terms(rows_at(theirs + i * chunk, chunk), e_in[i])
        return unused

    lax.fori_loop(0, 4, far_terms, 0)
    for m in range(3):
        for u in range(max(0, count - 2), count):
            out_copy(m, u).wait()
    for i in order:
        a_copy(i, ours if i < 2 else theirs).wait_send()


def middle(
    plan, cycle_size, attended, mixed, tokens, cot, gain, w_out, w_out_far, w_gate, w_up, w_down
):
    pair, model = tokens.shape
    half = pair // 2
    units = w_down.shape[0]
    chunk = half // 4
    hbm = pl.BlockSpec(memory_space=pl.ANY)
    dma = pltpu.SemaphoreType.DMA
    return pl.pallas_call(
        functools.partial(middle_kernel, plan, cycle_size),
        out_shape=[
            jax.ShapeDtypeStruct((half, model), f32),
            jax.ShapeDtypeStruct((half, model), f32),
            jax.ShapeDtypeStruct((half, model), bf16),
            jax.ShapeDtypeStruct((half, model), bf16),
            jax.ShapeDtypeStruct((half, model), bf16),
            jax.ShapeDtypeStruct((pair, WIDE), bf16),
            jax.ShapeDtypeStruct((1, model), f32),
        ]
        + [jax.ShapeDtypeStruct((units, model), bf16)] * 3,
        in_specs=[vmem] * 5 + [hbm] * 5,
        out_specs=[vmem] * 7 + [hbm] * 3,
        scratch_shapes=[
            pltpu.VMEM((model, units), bf16),
            pltpu.VMEM((model, units), bf16),
            pltpu.VMEM((model, units), bf16),
            pltpu.VMEM((2, WIDE, model), bf16),
            pltpu.VMEM((pair, units), bf16),
            pltpu.VMEM((pair, units), bf16),
            pltpu.VMEM((pair, units), bf16),
            pltpu.VMEM((pair, model), bf16),
            pltpu.VMEM((pair, WIDE), bf16),
            pltpu.VMEM((4, chunk, model), bf16),
            pltpu.VMEM((4, chunk, model), bf16),
            pltpu.VMEM((4, chunk, WIDE), bf16),
            pltpu.VMEM((4, chunk, WIDE), bf16),
            pltpu.VMEM((half, model), f32),
            pltpu.VMEM((half, model), f32),
            pltpu.VMEM((3, 2, WIDE, model), bf16),
            dma((5,)),
            dma((2, 12)),
            dma((3, 2)),
        ],
        compiler_params=pltpu.CompilerParams(
            vmem_limit_bytes=60 * 2**20, collective_id=3, has_side_effects=True
        ),
        name="feed_forward",
    )(attended, mixed, tokens, cot, gain, w_out, w_out_far, w_gate, w_up, w_down.T)


class Scatter:
    def __init__(self, spot, units, parts, outs, buffers, sems):
        self.spot = spot
        self.units = units
        self.parts = parts
        self.outs = outs
        self.mine, self.core_in, self.x_in, self.up_in, self.down_in = buffers
        self.load_sem, self.core_sem, self.x_sem, self.up_sem, self.down_sem = sems

    def rows_of(self, u):
        return pl.ds(self.units[u][1], self.units[u][2])

    def load(self, u):
        m = self.units[u][0]
        return pltpu.make_async_copy(
            self.parts[m].at[:, :, self.spot.core, self.rows_of(u)],
            self.mine.at[m, :, :, self.rows_of(u)],
            self.load_sem.at[u],
        )

    def core_copy(self, u):
        m = self.units[u][0]
        return send(
            self.parts[m].at[:, :, 1 - self.spot.core, self.rows_of(u)],
            self.core_in.at[m, :, :, self.rows_of(u)],
            self.core_sem.at[0, u],
            self.core_sem.at[1, u],
            self.spot.core_mate(),
        )

    def x_copy(self, u):
        m = self.units[u][0]
        x = self.spot.x
        src = self.mine.at[m, :, 1 - x, self.rows_of(u)]
        dst = self.x_in.at[m, :, self.rows_of(u)]
        return send(src, dst, self.x_sem.at[0, u], self.x_sem.at[1, u], self.spot.x_mate())

    def begin(self, u):
        self.load(u).start()
        self.core_copy(u).start()

    def core_stage(self, u):
        m = self.units[u][0]
        x = self.spot.x
        self.load(u).wait()
        self.core_copy(u).wait()

        def add(slot):
            def body(line, unused):
                at = (m, line, slot, self.rows_of(u))
                self.mine[at] = added(self.mine[at], self.core_in[at])
                return unused

            lax.fori_loop(0, self.spot.lines, body, 0)

        add(1 - x)
        self.x_copy(u).start()
        add(x)

    def x_stage(self, u):
        m = self.units[u][0]
        x = self.spot.x
        self.x_copy(u).wait()

        def body(line, unused):
            at = (m, line, x, self.rows_of(u))
            self.mine[at] = added(self.mine[at], self.x_in[m, line, self.rows_of(u)])
            return unused

        lax.fori_loop(0, self.spot.lines, body, 0)
        self.ends(u)

    def copy(self, u, step, d):
        m = self.units[u][0]
        sem = self.up_sem if step > 0 else self.down_sem
        ring = self.up_in if step > 0 else self.down_in
        return send(
            self.mine.at[m, d, self.spot.x, self.rows_of(u)],
            ring.at[m, d, self.rows_of(u)],
            sem.at[0, u, d],
            sem.at[1, u, d],
            self.spot.z_mate(step),
        )

    def receive(self, u, step, d):
        m = self.units[u][0]
        self.copy(u, step, d).wait_recv()
        ring = self.up_in if step > 0 else self.down_in
        at = (m, d, self.spot.x, self.rows_of(u))
        self.mine[at] = added(self.mine[at], ring[m, d, self.rows_of(u)])

    def start(self, u, step, d):
        self.copy(u, step, d).start()

    def ends(self, u):
        z, lines = (self.spot.z, self.spot.lines)

        @pl.when(z == 0)
        def _():
            def up(k, unused):
                self.start(u, 1, lines - 1 - k)
                return unused

            lax.fori_loop(0, lines - 1, up, 0)

        @pl.when(z == lines - 1)
        def _():
            def down(k, unused):
                self.start(u, -1, k)
                return unused

            lax.fori_loop(0, lines - 1, down, 0)

    def relay(self, u, lag):
        z, lines = (self.spot.z, self.spot.lines)
        top = lines - 2 if lag == 2 else lag

        @pl.when((z >= lag) & (z <= top))
        def _():
            def up(k, unused):
                self.receive(u, 1, lines - 1 - k)
                self.start(u, 1, lines - 1 - k)
                return unused

            lax.fori_loop(0, lines - 1 - z, up, 0)

        @pl.when((lines - 1 - z >= lag) & (lines - 1 - z <= top))
        def _():
            def down(k, unused):
                self.receive(u, -1, k)
                self.start(u, -1, k)
                return unused

            lax.fori_loop(0, z, down, 0)

    def settle(self, u):
        z, lines = (self.spot.z, self.spot.lines)

        @pl.when(z > 0)
        def _():
            self.receive(u, 1, z)

        @pl.when(z + 1 < lines)
        def _():
            self.receive(u, -1, z)

        self.store(u)

    def store(self, u):
        m = self.units[u][0]
        self.outs[m][self.rows_of(u), :] = self.mine[
            m, self.spot.z, self.spot.x, self.rows_of(u)
        ].astype(f32)

    def drain(self, u):
        z, lines = (self.spot.z, self.spot.lines)

        def body(k, unused):
            @pl.when(z < lines - 1 - k)
            def _():
                self.copy(u, 1, lines - 1 - k).wait_send()

            @pl.when(z > k)
            def _():
                self.copy(u, -1, k).wait_send()

            return unused

        lax.fori_loop(0, lines - 1, body, 0)


def scatter_units(rows):
    if rows % 16 or rows < 112:
        return [(m, 0, rows) for m in range(3)]
    tail = rows - 64
    return [
        (0, 0, 64), (1, 0, 64), (2, 0, 64), (0, 64, tail), (1, 64, tail), (2, 64, tail - 16),
        (2, rows - 16, 16),
    ]


def backward_kernel(
    plan, lines, span, reach, doc_most, rows, pair, table_ref, qb_ref, do_ref,
    own_kv, own_aug, near_hbm, aug_hbm, masks_hbm, g_hbm, qall_hbm, branch_hbm, ffn_hbm, p0, p1, p2,
    dq_ref, tab_ref, dk_ref, dv_ref, mask_ref, o0, o1, o2, far_hbm, ffn_in_hbm, all_do,
    mine, core_in, x_in, up_in, down_in,
    km, vm, mask_row, g_buf, aug_buf, qh_ref, doh_ref, acc, near_ref, near_acc, far_acc,
    load_sem, core_sem, rx_sem, up_sem, down_sem, own_sem, zero_sem, z_sem, x_sem, c_sem, g_sem,
    q_sem,
):
    spot = Spot(lines)
    z, x, core = (spot.z, spot.x, spot.core)
    units = scatter_units(o0.shape[0])
    scatter = Scatter(
        spot,
        units,
        (p0, p1, p2),
        (o0, o1, o2),
        (mine, core_in, x_in, up_in, down_in),
        (load_sem, core_sem, rx_sem, up_sem, down_sem),
    )
    order = range(len(units))
    greet(spot, True)
    far_copy = send(branch_hbm, far_hbm, own_sem.at[2], own_sem.at[3], spot.y_mate())
    far_copy.start()
    ffn_copy = send(ffn_hbm, ffn_in_hbm, own_sem.at[4], own_sem.at[5], spot.y_mate())
    ffn_copy.start()

    def outside(d):
        return (d < z - span) | (d > z + span)

    def pass_copy(step, d):
        i = 0 if step > 0 else 1
        part = all_do.at[d, :, core]
        return send(part, part, z_sem.at[i, d], z_sem.at[2 + i, d], spot.z_mate(step))

    across = send(do_ref, all_do.at[z, x, core], x_sem.at[0], x_sem.at[1], spot.x_mate())

    def beside(d):
        part = all_do.at[d, :, core]
        return send(part, part, c_sem.at[0, d], c_sem.at[1, d], spot.core_mate())

    own_copy = pltpu.make_async_copy(do_ref, all_do.at[z, x, core], own_sem.at[0])

    def zero_copies(d):
        return [
            pltpu.make_async_copy(vm.at[pl.ds(0, pair)], all_do.at[d, a, b], zero_sem.at[d, a, b])
            for a in range(2)
            for b in range(2)
        ]

    def zero_start(d, unused):
        @pl.when(outside(d))
        def _():
            for copy in zero_copies(d):
                copy.start()

        return unused

    def turn():
        across.wait()
        own_copy.wait()

        @pl.when(z + 1 < lines)
        def _():
            pass_copy(1, z).start()

        @pl.when(z > 0)
        def _():
            pass_copy(-1, z).start()

        beside(z).start()

    def level(k):
        @pl.when(z - k >= 0)
        def _():
            d = jnp.maximum(z - k, 0)
            pass_copy(1, d).wait_recv()
            if k < span:

                @pl.when(z + 1 < lines)
                def _():
                    pass_copy(1, d).start()

            beside(d).start()

        @pl.when(z + k < lines)
        def _():
            d = jnp.minimum(z + k, lines - 1)
            pass_copy(-1, d).wait_recv()
            if k < span:

                @pl.when(z > 0)
                def _():
                    pass_copy(-1, d).start()

            beside(d).start()

    def gathered(d, unused):
        @pl.when(~outside(d))
        def _():
            beside(d).wait()

        @pl.when(outside(d))
        def _():
            for copy in zero_copies(d):
                copy.wait()

        @pl.when((z + 1 < lines) & (d <= z) & (d > z - span))
        def _():
            pass_copy(1, d).wait_send()

        @pl.when((z > 0) & (d >= z) & (d < z + span))
        def _():
            pass_copy(-1, d).wait_send()

        return unused

    own_copy.start()
    across.start()
    for u in order:
        scatter.begin(u)
    vm[:PAD, :] = jnp.zeros((PAD, WIDE), bf16)
    lax.fori_loop(0, lines, zero_start, 0)

    base = spot.index * pair
    total = 4 * lines * pair
    origin = jnp.clip(base - reach * pair, 0, total - rows)
    local = base - origin
    blocks = rows // pair

    def mask_copy(n):
        to = pl.ds(pl.multiple_of(PAD + n * pair, 128), pair)
        return pltpu.make_async_copy(masks_hbm.at[n], mask_row.at[:, to], q_sem.at[1 + n])

    def mask_start(n, unused):
        mask_copy(n).start()
        return unused

    lax.fori_loop(0, blocks, mask_start, 0)
    mask_row[:, :PAD] = jnp.zeros((8, PAD), f32)
    mask_row[:, PAD + rows :] = jnp.zeros((8, PAD), f32)
    km[:PAD, :] = jnp.broadcast_to(
        jnp.where(pad_lanes(plan), neg_big, 0.0).astype(bf16), (PAD, WIDE)
    )
    km[PAD + rows :, :] = km[:PAD, :]
    vm[PAD + rows :, :] = jnp.zeros((PAD, WIDE), bf16)
    low_block = lanes_of(pair, 128) < 64
    ones_block = (lanes_of(pair, 128) < 3 * plan.heads).astype(bf16)

    def g_copy(n):
        at = pl.ds(pl.multiple_of(n * pair, pair), pair)
        return pltpu.make_async_copy(g_hbm.at[at], g_buf.at[n % 2], g_sem.at[0, n % 2])

    def aug_copy(n):
        at = pl.ds(pl.multiple_of(n * pair, pair), pair)
        return pltpu.make_async_copy(aug_hbm.at[at], aug_buf.at[n % 2], g_sem.at[1, n % 2])

    def near_copy(flip):
        return pltpu.make_async_copy(near_hbm.at[flip], near_ref, own_sem.at[1])

    g_copy(0).start()
    aug_copy(0).start()
    near_copy(0).start()

    def build(n, unused):
        g_copy(n).wait()
        aug_copy(n).wait()

        @pl.when(n + 1 < blocks)
        def _():
            g_copy(n + 1).start()
            aug_copy(n + 1).start()

        mask_copy(n).wait()
        to = pl.ds(pl.multiple_of(PAD + n * pair, 128), pair)
        middle = g_buf[n % 2, :, 128:256]
        km[to, 0:128] = g_buf[n % 2, :, 0:128]
        km[to, 128:256] = jnp.where(low_block, middle, aug_buf[n % 2])
        vm[to, 0:128] = jnp.where(low_block, ones_block, middle)
        vm[to, 128:256] = g_buf[n % 2, :, 256:384]
        return unused

    early = min(6, blocks)
    lax.fori_loop(0, early, build, 0)
    scatter.core_stage(0)
    lax.fori_loop(early, blocks, build, 0)
    near_copy(0).wait()
    near_acc[...] = jnp.zeros_like(near_acc)
    far_acc[...] = jnp.zeros_like(far_acc)
    lane = lanes_of(TQ)
    low = lanes_of(TQ, 128) < 64
    ones = (lanes_of(TQ, 128) < 3 * plan.heads).astype(bf16)

    def chunks(t):
        start = local + t * TQ
        least = jnp.maximum(start - doc_most + 1, 0)
        most = jnp.minimum(start + TQ + doc_most - 1, rows)
        n_left = jnp.maximum(start - EDGE - least + TK - 1, 0) // TK
        n_right = jnp.maximum(most - (start + TK - EDGE) + TK - 1, 0) // TK
        return start, n_left, n_right

    def rows_of_tile(t):
        return pl.ds(pl.multiple_of(t * TQ, TQ), TQ)

    def near_of(start):
        return pl.ds(pl.multiple_of(start + PAD - EDGE, 128), TK)

    def query_grads(h, s, part):
        return jnp.exp(s) * nt(doh_ref[h], vm[part, :])

    def dq_near(t, start):
        out = rows_of_tile(t)
        near = near_of(start)
        q = qb_ref[out, :]
        do = do_ref[out, :]
        for h in range(plan.heads):
            qh_ref[h] = jnp.where(plan.key_lanes(lane, h), q, jnp.zeros_like(q))
            doh_ref[h] = jnp.where(plan.value_lanes(lane, h), do, jnp.zeros_like(do))
            ds = query_grads(
                h, nt(qh_ref[h], km[near, :]) + near_ref[h] + mask_row[0:1, near], near
            )
            near_acc[h] += ds
            acc[h] = nn(ds.astype(bf16), km[near, :])

    def dq_far(start, n, n_left, count):
        parts = far_pair(start, n, n_left, count, far_left_bucket, far_right_bucket)
        for h in range(plan.heads):
            grads = []
            for i, (part, bucket) in enumerate(parts):
                slot = (2 * n + i >= n_left).astype(jnp.int32)
                offset = mask_row[0:1, part] + table_ref[h, bucket]
                ds = query_grads(h, nt(qh_ref[h], km[part, :]) + offset, part)
                grads.append(nn(ds.astype(bf16), km[part, :]))
                far_acc[slot, h] += (
                    ds[:, 0:128] + ds[:, 128:256] + ds[:, 256:384] + ds[:, 384:512]
                )
            acc[h] += grads[0] + grads[1]

    def dq_end(t):
        result = jnp.zeros((TQ, WIDE), f32)
        for h in range(plan.heads):
            result = jnp.where(lane // 64 == h, acc[h], result)
        dq_ref[rows_of_tile(t), :] = result.astype(bf16)

    def table_end():
        row = lax.broadcasted_iota(jnp.int32, (EDGE, 3 * EDGE), 0)
        col = lax.broadcasted_iota(jnp.int32, (EDGE, 3 * EDGE), 1)
        bucket = bucket_of(col - EDGE - row)
        for h in range(plan.heads):
            band = near_acc[h, :EDGE, : 3 * EDGE] + near_acc[h, EDGE:, EDGE:]

            def one(b, unused, band=band, h=h):
                part = jnp.sum(jnp.where(bucket == b, band, 0.0), axis=0, keepdims=True)
                tab_ref[h, pl.ds(b, 1), :] = part[:, :128] + part[:, 128:256] + part[:, 256:]
                return unused

            lax.fori_loop(0, 32, one, 0)
            for b, slot, extra in (
                (far_left_bucket, 0, near_acc[h, EDGE:, :EDGE]),
                (far_right_bucket, 1, near_acc[h, :EDGE, 3 * EDGE :]),
            ):
                tab_ref[h, b : b + 1, :] += jnp.sum(
                    far_acc[slot, h], axis=0, keepdims=True
                ) + jnp.sum(extra, axis=0, keepdims=True)

    def swap_operands():
        near_copy(1).start()
        lax.fori_loop(0, lines, gathered, 0)
        q_copy = pltpu.make_async_copy(qall_hbm, km.at[pl.ds(PAD, rows)], q_sem.at[0])
        q_copy.start()

        def block_copy(n):
            b = origin // pair + n
            return pltpu.make_async_copy(
                all_do.at[b // 4, (b // 2) % 2, b % 2],
                vm.at[pl.ds(pl.multiple_of(PAD + n * pair, 128), pair)],
                q_sem.at[1 + n],
            )

        def block_start(n, unused):
            block_copy(n).start()
            return unused

        lax.fori_loop(0, blocks, block_start, 0)
        first = lanes_of(1)
        stat = (first >= plan.stat_lane) & (first < plan.stat_lane + 3 * plan.heads)
        km[:PAD, :] = jnp.broadcast_to(jnp.where(stat, neg_big, 0.0).astype(bf16), (PAD, WIDE))
        km[PAD + rows :, :] = km[:PAD, :]

        def block_wait(n, unused):
            block_copy(n).wait()
            return unused

        lax.fori_loop(0, blocks, block_wait, 0)
        q_copy.wait()
        near_copy(1).wait()

    def key_grads(h, s, part):
        p = jnp.exp(s)
        ds = p * nt(doh_ref[h], vm[part, :])
        return nn(p.astype(bf16), vm[part, :]), nn(ds.astype(bf16), km[part, :])

    def dkv_near(t, start):
        out = rows_of_tile(t)
        near = near_of(start)
        middle = own_kv[out, 128:256]
        k = jnp.concatenate([own_kv[out, 0:128], jnp.where(low, middle, own_aug[out, :])], axis=1)
        v = jnp.concatenate([jnp.where(low, ones, middle), own_kv[out, 256:384]], axis=1)
        for h in range(plan.heads):
            qh_ref[h] = jnp.where(plan.key_lanes(lane, h), k, jnp.zeros_like(k))
            doh_ref[h] = jnp.where(plan.value_lanes(lane, h), v, jnp.zeros_like(v))
            near_acc[h, :, :WIDE], acc[h] = key_grads(
                h, nt(qh_ref[h], km[near, :]) + near_ref[h], near
            )

    def dkv_far(start, n, n_left, count):
        parts = far_pair(start, n, n_left, count, far_right_bucket, far_left_bucket)
        for h in range(plan.heads):
            (v_one, k_one), (v_two, k_two) = [
                key_grads(h, nt(qh_ref[h], km[part, :]) + table_ref[h, bucket], part)
                for part, bucket in parts
            ]
            near_acc[h, :, :WIDE] += v_one + v_two
            acc[h] += k_one + k_two

    def dkv_end(t):
        out = rows_of_tile(t)
        dk = jnp.zeros((TQ, WIDE), f32)
        dv = jnp.zeros((TQ, WIDE), f32)
        mask_grad = jnp.zeros((TQ, 1), f32)
        for h in range(plan.heads):
            dk = jnp.where(lane // 64 == h, acc[h], dk)
            dv = jnp.where(lane // 64 == h + 1, near_acc[h, :, :WIDE], dv)
            mask_grad = mask_grad + acc[h][:, plan.mask_lane : plan.mask_lane + 1]
        mask_ref[t] = jnp.transpose(jnp.broadcast_to(mask_grad, (TQ, 128)))[:8, :]
        dk_ref[out, :] = dk.astype(bf16)
        dv_ref[out, :] = dv.astype(bf16)

    tiles = pair // TQ
    steps = 1 + -(-(2 * (-(-doc_most // TK)) + 1) // 2)
    half_slots = tiles * steps
    last_step = steps - 1

    def attention(w):
        backward = w >= half_slots
        t = (w % half_slots) // steps
        n = w % steps
        start, n_left, n_right = chunks(t)
        count = n_left + n_right
        live = (n > 0) & (2 * (n - 1) < count)

        @pl.when(~backward)
        def _():
            @pl.when(n == 0)
            def _():
                dq_near(t, start)

            @pl.when(live)
            def _():
                dq_far(start, n - 1, n_left, count)

            @pl.when(n == last_step)
            def _():
                dq_end(t)

        @pl.when(backward & (w < 2 * half_slots))
        def _():
            @pl.when(w == half_slots)
            def _():
                table_end()
                swap_operands()

            @pl.when(n == 0)
            def _():
                dkv_near(t, start)

            @pl.when(live)
            def _():
                dkv_far(start, n - 1, n_left, count)

            @pl.when(n == last_step)
            def _():
                dkv_end(t)

    work = 2 * half_slots
    events = []

    def due(time, run, *args):
        events.append((max(0, int((time - start_us) / slot_us)), functools.partial(run, *args)))

    start_us, slot_us = (6.0, 2.0)
    due(6.0, turn)
    for k in range(1, span + 1):
        due((22.0, 36.0)[min(k, 2) - 1], level, k)
    times = (
        (7.0, 26.0, 51.0, 61.0, 68.0),
        (10.5, 43.0, 64.0, 74.0, 81.0),
        (14.0, 60.0, 77.0, 87.0, 94.0),
        (17.0, 73.0, 87.0, 95.0, 101.0),
        (20.0, 86.0, 97.5, 106.0, 111.0),
        (22.0, 95.0, 104.0, 110.0, 114.0),
        (23.0, 99.0, 107.0, 111.0, 114.5),
    )
    for u in order:
        core_at, x_at, one_at, two_at, end_at = times[u]
        if u > 0:
            due(core_at, scatter.core_stage, u)
        due(x_at, scatter.x_stage, u)
        due(one_at, scatter.relay, u, 1)
        due(two_at, scatter.relay, u, 2)
        due(end_at, scatter.settle, u)
    events.sort(key=lambda event: event[0])
    end = max(work, events[-1][0] + 1)

    def slot(w, unused):
        for at, run in events:

            @pl.when(w == at)
            def _(run=run):
                run()

        attention(w)
        return unused

    lax.fori_loop(0, end, slot, 0)
    for u in order:
        scatter.drain(u)
    far_copy.wait()
    ffn_copy.wait()


def backward(
    plan, cycle_size, reach, doc_most, rows, table, aug, masks, q_back, do_wide, own_kv, own_aug,
    near_bias, kv_all, q_all, branch, ffn_far, parts,
):
    lines = cycle_size // 4
    span = min(lines - 1, (reach + 3) // 4)
    pair = q_back.shape[0]
    units_here, model = parts[0].shape
    size = units_here // cycle_size
    units = scatter_units(size)
    shaped = [part.reshape(lines, 2, 2, size, model) for part in parts]
    n = len(units)
    heads = plan.heads
    padded = rows + 2 * PAD
    hbm = pl.BlockSpec(memory_space=pl.ANY)
    dma = pltpu.SemaphoreType.DMA
    return pl.pallas_call(
        functools.partial(backward_kernel, plan, lines, span, reach, doc_most, rows, pair),
        out_shape=[
            jax.ShapeDtypeStruct((pair, WIDE), bf16),
            jax.ShapeDtypeStruct((heads, 32, 128), f32),
            jax.ShapeDtypeStruct((pair, WIDE), bf16),
            jax.ShapeDtypeStruct((pair, WIDE), bf16),
            jax.ShapeDtypeStruct((pair // TQ, 8, TQ), f32),
        ]
        + [jax.ShapeDtypeStruct((size, model), f32)] * 3
        + [
            jax.ShapeDtypeStruct(branch.shape, bf16),
            jax.ShapeDtypeStruct(branch.shape, bf16),
            jax.ShapeDtypeStruct((lines, 2, 2, pair, WIDE), bf16),
        ],
        in_specs=[smem] + [vmem] * 4 + [hbm] * 10,
        out_specs=[vmem] * 8 + [hbm] * 3,
        scratch_shapes=[
            pltpu.VMEM((3, lines, 2, size, model), bf16),
            pltpu.VMEM((3, lines, 2, size, model), bf16),
            pltpu.VMEM((3, lines, size, model), bf16),
            pltpu.VMEM((3, lines, size, model), bf16),
            pltpu.VMEM((3, lines, size, model), bf16),
            pltpu.VMEM((padded, WIDE), bf16),
            pltpu.VMEM((padded, WIDE), bf16),
            pltpu.VMEM((8, padded), f32),
            pltpu.VMEM((2, pair, 2 * plan.cols), bf16),
            pltpu.VMEM((2, pair, 128), bf16),
            pltpu.VMEM((heads, TQ, WIDE), bf16),
            pltpu.VMEM((heads, TQ, WIDE), bf16),
            pltpu.VMEM((heads, TQ, WIDE), f32),
            pltpu.VMEM((heads, TQ, TK), f32),
            pltpu.VMEM((heads, TQ, TK), f32),
            pltpu.VMEM((2, heads, TQ, 128), f32),
            dma((n,)),
            dma((2, n)),
            dma((2, n)),
            dma((2, n, lines)),
            dma((2, n, lines)),
            dma((6,)),
            dma((lines, 2, 2)),
            dma((4, lines)),
            dma((2,)),
            dma((2, lines)),
            dma((2, 2)),
            dma((1 + rows // pair,)),
        ],
        compiler_params=pltpu.CompilerParams(
            vmem_limit_bytes=62 * 2**20, collective_id=1, has_side_effects=True
        ),
        name="backward",
    )(
        table, q_back, do_wide, own_kv, own_aug, near_bias, aug, masks, kv_all, q_all,
        branch, ffn_far, *shaped
    )


def shards(
    tokens,
    doc_lengths,
    key_mask,
    gain_attn,
    w_query,
    w_key,
    w_value,
    w_out,
    bias_table,
    gain_ffn,
    w_gate,
    w_up,
    w_down,
    cotangent,
):
    own_rows, model = tokens.shape
    group = lax.axis_size("wa")
    cycle_size = lax.axis_size("ctx")
    pair = own_rows * group
    heads = bias_table.shape[1]
    docs = doc_lengths.shape[0]
    plan = Plan(heads, w_query.shape[1] // heads, docs)
    total_rows = pair * cycle_size
    doc_most = min(MAXLEN, total_rows // 2)
    reach = min(cycle_size - 1, (doc_most - 1) // pair + 1)
    base = lax.axis_index("ctx") * pair
    rows = min(total_rows, (2 * reach + 1) * pair)
    origin = jnp.clip(base - reach * pair, 0, total_rows - rows).astype(jnp.int32)
    table = bias_table.T

    def window(gathered):
        if rows == total_rows:
            return gathered
        return lax.dynamic_slice_in_dim(gathered, origin, rows, 0)

    gather = functools.partial(lax.all_gather, axis_name="ctx", axis=0, tiled=True)
    (
        pair_normed, pair_tokens, q_wide, own_kv, k_aug, own_aug, near_bias, masks, far_out, kv_all,
    ) = first(
        plan,
        cycle_size,
        reach,
        rows,
        doc_lengths,
        table,
        tokens,
        gain_attn,
        key_mask,
        w_query,
        w_key,
        w_value,
        w_out,
    )
    masks = masks.reshape(cycle_size, 8, pair)
    cot_late, near_bias = lax.optimization_barrier((cotangent, near_bias))
    pair_cot = lax.all_gather(cot_late, "wa", axis=0, tiled=True)
    if rows < total_rows:
        masks = lax.dynamic_slice_in_dim(masks, origin // pair, rows // pair, 0)
    kv_all = window(kv_all.reshape(total_rows, 2 * plan.cols))
    attended, mixed, q_back = attend(
        plan, cycle_size, reach, rows, doc_lengths, table, q_wide, near_bias, kv_all, k_aug, masks
    )
    q_all = window(gather(q_back))
    hidden, grad_hidden, branch, ffn_own, ffn_far, do_wide, gain_ffn_part, *stacks = middle(
        plan,
        cycle_size,
        attended,
        mixed,
        pair_tokens,
        pair_cot,
        gain_ffn,
        w_out,
        far_out,
        w_gate,
        w_up,
        w_down,
    )
    (
        grad_queries, table_part, grad_keys, grad_values, mask_part,
        grad_w_down, grad_w_gate, grad_w_up, far_branch, ffn_in, unused_gathered,
    ) = backward(
        plan,
        cycle_size,
        reach,
        doc_most,
        rows,
        table,
        k_aug,
        masks,
        q_back,
        do_wide,
        own_kv,
        own_aug,
        near_bias,
        kv_all,
        q_all,
        branch,
        ffn_far,
        stacks,
    )
    grad_w_gate, grad_w_up = (grad_w_gate.T, grad_w_up.T)
    layer_out = (hidden + ffn_own.astype(f32) + ffn_in.astype(f32)).astype(bf16)
    grad_tokens, grad_mask, weights, grad_gain_attn, grad_gain_ffn, grad_table = finish(
        plan,
        cycle_size,
        grad_queries,
        grad_keys,
        grad_values,
        attended,
        pair_normed,
        branch,
        far_branch,
        w_query.T,
        w_key.T,
        w_value.T,
        mask_part.reshape(group, 8, own_rows),
        tokens,
        gain_attn,
        grad_hidden,
        table_part,
        gain_ffn_part,
    )
    weights = weights.reshape(4, plan.cols, model).astype(f32)
    return (
        layer_out,
        grad_tokens,
        grad_mask,
        grad_gain_attn,
        weights[0].T,
        weights[1].T,
        weights[2].T,
        weights[3],
        grad_table.T,
        grad_gain_ffn,
        grad_w_gate,
        grad_w_up,
        grad_w_down,
    )


def solution(mesh):
    placed = (
        P(("ctx", "wa"), None),
        P(),
        P("ctx"),
        P(),
        P(None, "wa"),
        P(None, "wa"),
        P(None, "wa"),
        P("wa", None),
        P(None, "wa"),
        P(),
        P(None, "wa"),
        P(None, "wa"),
        P("wa", None),
        P(("ctx", "wa"), None),
    )
    return jax.shard_map(
        shards,
        mesh=mesh,
        in_specs=placed,
        out_specs=(
            P(("ctx", "wa"), None),
            P(("ctx", "wa"), None),
            P(("ctx", "wa")),
            P(),
            P(None, "wa"),
            P(None, "wa"),
            P(None, "wa"),
            P("wa", None),
            P(None, "wa"),
            P(),
            P(None, ("wa", "ctx")),
            P(None, ("wa", "ctx")),
            P(("wa", "ctx"), None),
        ),
        check_vma=False,
    )
```

```python
import functools

import jax
import jax.numpy as jnp
from jax import lax
from jax.experimental import pallas as pl
from jax.experimental.pallas import tpu as pltpu
from jax.sharding import PartitionSpec as P

MAXLEN = 8192

bucket_edges = (12, 16, 23, 32, 46, 64, 91)
neg_big = -1e30
eps = 1e-06
far_left_bucket = 15
far_right_bucket = 31
slack = 20.0
WIDE = 256
TQ = 256
TK = 512
EDGE = 128
PAD = TK + EDGE
f32 = jnp.float32
bf16 = jnp.bfloat16


def bucket_of(relative):
    distance = jnp.abs(relative)
    bucket = jnp.minimum(distance, 8) + 16 * (relative > 0).astype(jnp.int32)
    for edge in bucket_edges:
        bucket = bucket + (distance >= edge).astype(jnp.int32)
    return bucket


def norm_forward(inputs, gain):
    inv_root = lax.rsqrt(jnp.mean(inputs * inputs, axis=-1, keepdims=True) + eps)
    return (inputs * inv_root * gain, inv_root)


def norm_backward(inputs, inv_root, gain, grad_normed):
    scaled = gain * grad_normed
    cubed = inv_root * inv_root * inv_root
    grad_inputs = inv_root * scaled - inputs * cubed * jnp.mean(
        inputs * scaled, axis=-1, keepdims=True
    )
    grad_gain = jnp.sum(grad_normed * inputs * inv_root, axis=0)
    return (grad_inputs, grad_gain)


def gated(gate, upward):
    return jax.nn.gelu(gate, approximate=True) * upward


def nt(a, b):
    return lax.dot_general(a, b, (((1,), (1,)), ((), ())), preferred_element_type=f32)


def nn(a, b):
    return lax.dot_general(a, b, (((1,), (0,)), ((), ())), preferred_element_type=f32)


def split3(x):
    hi = x.astype(bf16)
    rest = x - hi.astype(f32)
    mid = rest.astype(bf16)
    return (hi, mid, (rest - mid.astype(f32)).astype(bf16))


class Plan:
    def __init__(self, heads, width, docs):
        self.heads = heads
        self.width = width
        self.bits = max(1, (docs - 1).bit_length())
        self.cols = heads * width
        self.mask_lane = self.cols
        self.doc_lane = self.cols + 1
        self.stat_lane = self.doc_lane + 2 * self.bits
        assert self.stat_lane + 3 * heads <= WIDE and self.cols + 64 == WIDE and width == 64

    def key_lanes(self, lane, h):
        own = (lane >= h * self.width) & (lane < (h + 1) * self.width)
        aug = (lane >= self.mask_lane) & (lane < self.stat_lane)
        stat = (lane >= self.stat_lane + 3 * h) & (lane < self.stat_lane + 3 * h + 3)
        return own | aug | stat

    def value_lanes(self, lane, h):
        own = (lane >= 64 + h * self.width) & (lane < 64 + (h + 1) * self.width)
        return own | ((lane >= 3 * h) & (lane < 3 * h + 3))


def lanes_of(rows, width=WIDE):
    return lax.broadcasted_iota(jnp.int32, (rows, width), 1)


def near_lanes(heads, table_ref, near_ref):
    row = lax.broadcasted_iota(jnp.int32, (EDGE, 3 * EDGE), 0)
    col = lax.broadcasted_iota(jnp.int32, (EDGE, 3 * EDGE), 1)
    relative = col - EDGE - row
    for flip in range(2):
        bucket = bucket_of(-relative if flip else relative)
        left, right = (far_left_bucket, far_right_bucket)
        if flip:
            left, right = (right, left)
        for h in range(heads):
            base = jnp.full((EDGE, 3 * EDGE), table_ref[h, 0], f32)
            for b in range(1, 32):
                base = jnp.where(bucket == b, table_ref[h, b], base)
            far_l = jnp.full((EDGE, EDGE), table_ref[h, left], f32)
            far_r = jnp.full((EDGE, EDGE), table_ref[h, right], f32)
            near_ref[flip, h, :EDGE, : 3 * EDGE] = base
            near_ref[flip, h, :EDGE, 3 * EDGE :] = far_r
            near_ref[flip, h, EDGE:, EDGE:] = base
            near_ref[flip, h, EDGE:, :EDGE] = far_l


def far_span(start, n, n_left, left_bucket, right_bucket):
    on_left = n < n_left
    at = start + PAD - EDGE + TK * jnp.where(on_left, -1 - n, 1 + n - n_left)
    bucket = jnp.where(on_left, left_bucket, right_bucket)
    return pl.ds(pl.multiple_of(at, 128), TK), bucket


def pad_lanes(plan):
    lane = lanes_of(1)
    return (lane >= plan.doc_lane) & (lane < plan.stat_lane)


def far_pair(start, n, n_left, count, left, right):
    pair_of = []
    for i in range(2):
        part, bucket = far_span(start, 2 * n + i, n_left, left, right)
        at = jnp.where(2 * n + i < count, part.start, 0)
        pair_of.append((pl.ds(pl.multiple_of(at, 128), TK), bucket))
    return pair_of


def fwd_kernel(
    plan, lines, reach, rows, pair, lengths, table_ref, q_ref, near_hbm, g_hbm, aug_hbm, masks_hbm,
    low_ref, wide_ref, qb_ref,
    km, vm, mask_row, g_buf, aug_buf, near_ref, acc, extra, row_max, qh_ref, g_sem, near_sem,
):
    base = lax.axis_index("ctx") * pair
    origin = jnp.clip(base - reach * pair, 0, 4 * lines * pair - rows)
    blocks = rows // pair
    tiles = pair // TQ
    near_copy = pltpu.make_async_copy(near_hbm.at[0], near_ref, near_sem.at[0])
    near_copy.start()

    def document(position):
        def look(e, carry):
            begin, low, high = carry
            end = begin + lengths[e]
            inside = (begin <= position) & (position < end)
            return (end, jnp.where(inside, begin, low), jnp.where(inside, end, high))

        zero = jnp.int32(0)
        return lax.fori_loop(0, lengths.shape[0], look, (zero, zero, zero))[1:]

    def extent(t):
        first = base + t * TQ
        low = document(first)[0]
        high = document(first + TQ - 1)[1]
        n_left = jnp.maximum(0, first - EDGE - low + TK - 1) // TK
        n_right = jnp.maximum(0, high - (first - EDGE + TK) + TK - 1) // TK
        return low, high, n_left, n_right

    low_end = extent(0)[0] - origin
    high_end = extent(tiles - 1)[1] - origin
    from_block = jnp.maximum(0, low_end - TK) // pair
    to_block = jnp.minimum(blocks, (high_end + TK + pair - 1) // pair)

    def loads(n):
        at = pl.ds(pl.multiple_of(n * pair, pair), pair)
        to = pl.ds(pl.multiple_of(PAD + n * pair, 128), pair)
        slot = n % 2
        return (
            pltpu.make_async_copy(g_hbm.at[at], g_buf.at[slot], g_sem.at[0, slot]),
            pltpu.make_async_copy(aug_hbm.at[at], aug_buf.at[slot], g_sem.at[1, slot]),
            pltpu.make_async_copy(masks_hbm.at[n], mask_row.at[:, to], g_sem.at[2, slot]),
        )

    for copy in loads(from_block):
        copy.start()
    mask_row[:, :PAD] = jnp.zeros((8, PAD), f32)
    mask_row[:, PAD + rows :] = jnp.zeros((8, PAD), f32)
    km[:PAD, :] = jnp.broadcast_to(
        jnp.where(pad_lanes(plan), neg_big, 0.0).astype(bf16), (PAD, WIDE)
    )
    km[PAD + rows :, :] = km[:PAD, :]
    vm[:PAD, :] = jnp.zeros((PAD, WIDE), bf16)
    vm[PAD + rows :, :] = jnp.zeros((PAD, WIDE), bf16)
    low_lanes = lanes_of(pair, 128) < 64
    ones = (lanes_of(pair, 128) < 3 * plan.heads).astype(bf16)

    def build(n, unused):
        for copy in loads(n):
            copy.wait()

        @pl.when(n + 1 < to_block)
        def _():
            for copy in loads(n + 1):
                copy.start()

        to = pl.ds(pl.multiple_of(PAD + n * pair, 128), pair)
        middle = g_buf[n % 2, :, 128:256]
        km[to, 0:128] = g_buf[n % 2, :, 0:128]
        km[to, 128:256] = jnp.where(low_lanes, middle, aug_buf[n % 2])
        vm[to, 0:128] = jnp.where(low_lanes, ones, middle)
        vm[to, 128:256] = g_buf[n % 2, :, 256:384]
        return unused

    lax.fori_loop(from_block, to_block, build, 0)
    near_copy.wait()
    lane = lanes_of(TQ)

    def tile(t, unused):
        start = base - origin + t * TQ
        low_doc, high_doc, n_left, n_right = extent(t)
        count = n_left + n_right
        out = pl.ds(pl.multiple_of(t * TQ, TQ), TQ)
        q = q_ref[out, :]
        near = pl.ds(pl.multiple_of(start + PAD - EDGE, 128), TK)
        for h in range(plan.heads):
            qh = jnp.where(plan.key_lanes(lane, h), q, jnp.zeros_like(q))
            qh_ref[h] = qh
            s = nt(qh, km[near, :]) + near_ref[h] + mask_row[0:1, near]
            top = jnp.max(s, axis=1, keepdims=True)
            p = jnp.exp(s - top).astype(bf16)
            acc[h] = nn(p, vm[near, :])
            row_max[h] = jnp.broadcast_to(top, (TQ, 128))

        def far(n, unused):
            parts = far_pair(start, n, n_left, count, far_left_bucket, far_right_bucket)

            def scores_of(h):
                return [
                    (nt(qh_ref[h], km[part, :]) + (mask_row[0:1, part] + table_ref[h, bucket]), part)
                    for part, bucket in parts
                ]

            worst = jnp.full((TQ, 128), -slack, f32)
            for h in range(plan.heads):
                top = row_max[h]
                more = jnp.zeros((TQ, WIDE), f32)
                for s, part in scores_of(h):
                    tiles_of = []
                    for c in range(0, TK, 128):
                        over = s[:, c : c + 128] - top
                        worst = jnp.maximum(worst, over)
                        tiles_of.append(jnp.exp(over).astype(bf16))
                    more = more + nn(jnp.concatenate(tiles_of, axis=1), vm[part, :])
                extra[h] = more
            passed = jnp.max(worst) > slack

            @pl.when(jnp.logical_not(passed))
            def _():
                for h in range(plan.heads):
                    acc[h] += extra[h]

            @pl.when(passed)
            def _():
                for h in range(plan.heads):
                    scores = scores_of(h)
                    old = row_max[h][:, :1]
                    top = old
                    for s, part in scores:
                        top = jnp.maximum(top, jnp.max(s, axis=1, keepdims=True))
                    more = [nn(jnp.exp(s - top).astype(bf16), vm[part, :]) for s, part in scores]
                    acc[h] = acc[h] * jnp.exp(old - top) + (more[0] + more[1])
                    row_max[h] = jnp.broadcast_to(top, (TQ, 128))

            return unused

        lax.fori_loop(0, (count + 1) // 2, far, 0)
        wide = jnp.zeros((TQ, WIDE), f32)
        qb = jnp.where(lane < plan.stat_lane, q, jnp.zeros_like(q))
        for h in range(plan.heads):
            total = acc[h][:, 3 * h : 3 * h + 1]
            log_total = row_max[h][:, :1] + jnp.log(total)
            wide = jnp.where(lane // 64 == h + 1, acc[h] / total, wide)
            for i, part in enumerate(split3(-log_total)):
                qb = jnp.where(lane == plan.stat_lane + 3 * h + i, part, qb)
        wide_ref[out, :] = wide
        low_ref[out, :] = wide.astype(bf16)
        qb_ref[out, :] = qb
        return unused

    lax.fori_loop(0, tiles, tile, 0)


def attend(plan, cycle_size, reach, rows, lengths, table, q_wide, near_bias, kv_all, aug, masks):
    pair = q_wide.shape[0]
    heads = plan.heads
    padded = rows + 2 * PAD
    hbm = pl.BlockSpec(memory_space=pl.ANY)
    return pl.pallas_call(
        functools.partial(fwd_kernel, plan, cycle_size // 4, reach, rows, pair),
        out_shape=(
            jax.ShapeDtypeStruct((pair, WIDE), bf16),
            jax.ShapeDtypeStruct((pair, WIDE), f32),
            jax.ShapeDtypeStruct((pair, WIDE), bf16),
        ),
        in_specs=[smem, smem, vmem] + [hbm] * 4,
        out_specs=(vmem, vmem, vmem),
        scratch_shapes=[
            pltpu.VMEM((padded, WIDE), bf16),
            pltpu.VMEM((padded, WIDE), bf16),
            pltpu.VMEM((8, padded), f32),
            pltpu.VMEM((2, pair, 2 * plan.cols), bf16),
            pltpu.VMEM((2, pair, 128), bf16),
            pltpu.VMEM((heads, TQ, TK), f32),
            pltpu.VMEM((heads, TQ, WIDE), f32),
            pltpu.VMEM((heads, TQ, WIDE), f32),
            pltpu.VMEM((heads, TQ, 128), f32),
            pltpu.VMEM((heads, TQ, WIDE), bf16),
            pltpu.SemaphoreType.DMA((3, 2)),
            pltpu.SemaphoreType.DMA((1,)),
        ],
        compiler_params=params(),
        name="attention_forward",
    )(lengths, table, q_wide, near_bias, kv_all, aug, masks)


vmem = pl.BlockSpec(memory_space=pltpu.VMEM)
smem = pl.BlockSpec(memory_space=pltpu.SMEM)


def params():
    return pltpu.CompilerParams(vmem_limit_bytes=56 * 2**20)


class Spot:
    def __init__(self, lines):
        index = lax.axis_index("ctx")
        self.wa = lax.axis_index("wa")
        self.index = index
        self.lines = lines
        self.z = index // 4
        self.x = (index // 2) % 2
        self.core = index % 2

    def core_mate(self):
        return (self.index + 1 - 2 * self.core, self.wa)

    def x_mate(self):
        return (self.index + 2 - 4 * self.x, self.wa)

    def z_mate(self, step):
        return (jnp.clip(self.index + 4 * step, 0, 4 * self.lines - 1), self.wa)

    def y_mate(self):
        return (self.index, 1 - self.wa)


def send(src, dst, send_sem, recv_sem, device):
    return pltpu.make_async_remote_copy(
        src_ref=src,
        dst_ref=dst,
        send_sem=send_sem,
        recv_sem=recv_sem,
        device_id=device,
        device_id_type=pl.DeviceIdType.MESH,
    )


def greet(spot, with_y):
    barrier = pltpu.get_barrier_semaphore()
    mates = [spot.core_mate(), spot.x_mate()] + ([spot.y_mate()] if with_y else [])
    for mate in mates:
        pl.semaphore_signal(barrier, inc=1, device_id=mate, device_id_type=pl.DeviceIdType.MESH)

    @pl.when(spot.z + 1 < spot.lines)
    def _():
        pl.semaphore_signal(
            barrier, inc=1, device_id=spot.z_mate(1), device_id_type=pl.DeviceIdType.MESH
        )

    @pl.when(spot.z > 0)
    def _():
        pl.semaphore_signal(
            barrier, inc=1, device_id=spot.z_mate(-1), device_id_type=pl.DeviceIdType.MESH
        )

    above = (spot.z + 1 < spot.lines).astype(jnp.int32)
    below = (spot.z > 0).astype(jnp.int32)
    pl.semaphore_wait(barrier, len(mates) + above + below)


def added(a, b):
    return a + b


def first_kernel(
    plan, lines, span, reach, rows, lengths, table_ref, tokens_ref, gain_ref, key_mask_ref,
    wq_hbm, wk_hbm, wv_hbm, wo_hbm,
    x_ref, tok_ref, q_ref, own_ref, aug_ref, own_aug_ref, near_ref, masks_ref, wo_far_hbm, all_hbm,
    weights, zeros, mask_ref, load_sem, y_sem, own_sem, zero_sem, z_sem, x_sem, c_sem,
):
    spot = Spot(lines)
    z, x, core, wa = (spot.z, spot.x, spot.core, spot.wa)
    half, model = tokens_ref.shape
    cols = plan.cols
    chunk = half // 4
    loads = [
        pltpu.make_async_copy(src, weights.at[pl.ds(i * cols, cols)], load_sem.at[i])
        for i, src in enumerate((wk_hbm, wv_hbm, wq_hbm))
    ]
    for load in loads:
        load.start()
    mask_ref[...] = jnp.broadcast_to(key_mask_ref[...].astype(f32)[None, :], mask_ref.shape)
    greet(spot, True)
    zeros[...] = jnp.zeros_like(zeros)

    def outside(d):
        return (d < z - span) | (d > z + span)

    def zero_copies(d):
        return [
            pltpu.make_async_copy(zeros, all_hbm.at[d, a, b], zero_sem.at[d, a, b])
            for a in range(2)
            for b in range(2)
        ]

    def zero_start(d, unused):
        @pl.when(outside(d))
        def _():
            masks_ref[d] = jnp.zeros((2, 2) + mask_ref.shape, f32)
            for copy in zero_copies(d):
                copy.start()

        return unused

    def rows_at(start, size):
        return pl.ds(pl.multiple_of(start, size), size)

    ours = wa * half
    theirs = (1 - wa) * half

    def y_copy(i, base):
        return send(
            tokens_ref.at[rows_at(i * chunk, chunk)],
            tok_ref.at[rows_at(base + i * chunk, chunk)],
            y_sem.at[0, i],
            y_sem.at[1, i],
            spot.y_mate(),
        )

    def y_start(i, unused):
        y_copy(i, ours).start()
        return unused

    lax.fori_loop(0, 4, y_start, 0)
    far_copy = send(wo_hbm, wo_far_hbm, y_sem.at[0, 4], y_sem.at[1, 4], spot.y_mate())

    def scaled(rows_in):
        rows_in = rows_in.astype(f32)
        inv = lax.rsqrt(jnp.mean(rows_in * rows_in, axis=-1, keepdims=True) + eps)
        return (rows_in * inv * gain_ref[...][None, :]).astype(bf16)

    def normal(i, unused):
        at = rows_at(ours + i * chunk, chunk)
        rows_in = tokens_ref[rows_at(i * chunk, chunk), :]
        tok_ref[at, :] = rows_in
        x_ref[at, :] = scaled(rows_in)
        return unused

    lax.fori_loop(0, 4, normal, 0)
    for load in loads:
        load.wait()

    def project(base, size):
        rows = rows_at(base, size)
        qkv = nt(x_ref[rows, :], weights[...]).astype(bf16)
        own_ref[rows, :] = qkv[:, : 2 * cols]
        q_ref[rows, :cols] = qkv[:, 2 * cols :]

    pieces = [
        (ours, half, True),
        (theirs + half // 2, half // 2, True),
        (theirs, half // 2, False),
        None,
    ]
    mask_piece = 3

    def line_first(p):
        return p == mask_piece or pieces[p][2]

    def piece_rows(p):
        return rows_at(pieces[p][0], pieces[p][1])

    def source(p, d, a):
        if p == mask_piece:
            return masks_ref.at[d, a, core]
        return all_hbm.at[d, a, core, piece_rows(p)]

    def own_source(p):
        return mask_ref if p == mask_piece else own_ref.at[piece_rows(p)]

    def pass_copy(p, step, d, own):
        i = 0 if step > 0 else 1
        if line_first(p):
            dst = source(p, d, x)
            src = own_source(p) if own else dst
        else:
            dst = all_hbm.at[d, :, core, piece_rows(p)]
            src = dst
        return send(src, dst, z_sem.at[p, i, d], z_sem.at[p, 2 + i, d], spot.z_mate(step))

    def across(p, d, own):
        dst = source(p, d, x)
        src = own_source(p) if own else dst
        return send(src, dst, x_sem.at[p, 0, d], x_sem.at[p, 1, d], spot.x_mate())

    def beside(p, d):
        if p == mask_piece:
            part = masks_ref.at[d, :, core]
        else:
            part = all_hbm.at[d, :, core, piece_rows(p)]
        return send(part, part, c_sem.at[p, 0, d], c_sem.at[p, 1, d], spot.core_mate())

    def own_copy(p):
        return pltpu.make_async_copy(
            own_source(p), source(p, z, x), own_sem.at[p]
        )

    def both_ways(p, own):
        @pl.when(z + 1 < lines)
        def _():
            pass_copy(p, 1, z, own).start()

        @pl.when(z > 0)
        def _():
            pass_copy(p, -1, z, own).start()

    def begin(p):
        own_copy(p).start()
        across(p, z, True).start()
        if line_first(p):
            both_ways(p, True)

    def level(p, k):
        @pl.when(z - k >= 0)
        def _():
            d = jnp.maximum(z - k, 0)
            pass_copy(p, 1, d, False).wait_recv()
            if k < span:

                @pl.when(z + 1 < lines)
                def _():
                    pass_copy(p, 1, d, False).start()

            if line_first(p):
                across(p, d, False).start()
            else:
                beside(p, d).start()

        @pl.when(z + k < lines)
        def _():
            d = jnp.minimum(z + k, lines - 1)
            pass_copy(p, -1, d, False).wait_recv()
            if k < span:

                @pl.when(z > 0)
                def _():
                    pass_copy(p, -1, d, False).start()

            if line_first(p):
                across(p, d, False).start()
            else:
                beside(p, d).start()

    def turn(p):
        across(p, z, True).wait()
        own_copy(p).wait()
        both_ways(p, False)
        beside(p, z).start()

    def settle(p, k):
        for sign in (1, -1) if k else (1,):
            d = z - sign * k

            @pl.when((d >= 0) & (d < lines))
            def _(d=d):
                d = jnp.clip(d, 0, lines - 1)
                across(p, d, k == 0).wait()
                if k == 0:
                    own_copy(p).wait()
                beside(p, d).start()

    def doc_of(start, size):
        position = start + lax.broadcasted_iota(jnp.int32, (size, 128), 0)

        def count(e, carry):
            begin, total = carry
            begin = begin + lengths[e]
            return (begin, total + (position >= begin).astype(jnp.int32))

        zero = (jnp.int32(0), jnp.zeros((size, 128), jnp.int32))
        return lax.fori_loop(0, lengths.shape[0] - 1, count, zero)[1]

    def code_lanes(start, size):
        lane = lanes_of(size, 128) + 128
        code = jnp.maximum(lane - plan.doc_lane, 0)
        bit = jnp.bitwise_and(jnp.right_shift(doc_of(start, size), code // 2), 1)
        coded = (lane >= plan.doc_lane) & (lane < plan.stat_lane)
        ones = (lane >= plan.stat_lane) & (lane < plan.stat_lane + 3 * plan.heads)
        return lane, coded, bit != code % 2, ones

    pair = 2 * half
    base = spot.index * pair
    origin = jnp.clip(base - reach * pair, 0, 4 * lines * pair - rows)

    def key_lanes(n, unused):
        at = rows_at(n * half, half)
        lane, coded, differs, ones = code_lanes(origin + n * half, half)
        aug_ref[at, :] = jnp.where(
            coded & differs, neg_big, jnp.where(ones, 1.0, 0.0)
        ).astype(bf16)
        return unused

    def own_lanes(n, unused):
        at = rows_at(n * half, half)
        lane, coded, differs, ones = code_lanes(base + n * half, half)
        column = jnp.transpose(
            jnp.broadcast_to(mask_ref[0:1, at], (128, half))
        )
        own_aug_ref[at, :] = jnp.where(
            lane == plan.mask_lane,
            column,
            jnp.where(coded & differs, neg_big, jnp.where(ones, 1.0, 0.0)),
        ).astype(bf16)
        tail = jnp.where(
            (lane == plan.mask_lane) | (coded & ~differs), 1.0, 0.0
        ).astype(bf16)
        q_ref[at, 128:] = tail
        return unused

    begin(mask_piece)
    lax.fori_loop(0, 2, own_lanes, 0)
    project(ours, half)
    begin(0)
    lax.fori_loop(0, lines, zero_start, 0)
    near_lanes(plan.heads, table_ref, near_ref)
    lax.fori_loop(0, rows // half, key_lanes, 0)

    def y_wait(i, unused):
        y_copy(i, theirs).wait_recv()
        at = rows_at(theirs + i * chunk, chunk)
        x_ref[at, :] = scaled(tok_ref[at, :])
        return unused

    lax.fori_loop(0, 2, y_wait, 0)
    project(theirs, half // 2)
    begin(2)
    level(0, 1)
    level(mask_piece, 1)
    lax.fori_loop(2, 4, y_wait, 0)
    far_copy.start()
    project(theirs + half // 2, half // 2)
    begin(1)
    if span > 1:
        level(0, 2)
        level(mask_piece, 2)
    settle(0, 0)
    settle(mask_piece, 0)
    turn(2)
    level(1, 1)
    settle(0, 1)
    settle(mask_piece, 1)
    level(2, 1)
    if span > 1:
        level(1, 2)
        settle(0, 2)
        settle(mask_piece, 2)
    settle(1, 0)
    settle(1, 1)
    if span > 1:
        level(2, 2)
        settle(1, 2)
    for k in range(3, span + 1):
        for p in range(4):
            level(p, k)
        for p in (0, 1, mask_piece):
            settle(p, k)

    def finish_line(d, unused):
        @pl.when(~outside(d))
        def _():
            for p in range(4):
                beside(p, d).wait()

        @pl.when(outside(d))
        def _():
            for copy in zero_copies(d):
                copy.wait()

        for p in range(4):

            @pl.when((z + 1 < lines) & (d <= z) & (d > z - span))
            def _(p=p):
                pass_copy(p, 1, d, False).wait_send()

            @pl.when((z > 0) & (d >= z) & (d < z + span))
            def _(p=p):
                pass_copy(p, -1, d, False).wait_send()

        return unused

    lax.fori_loop(0, lines, finish_line, 0)

    def y_drain(i, unused):
        y_copy(i, ours).wait_send()
        return unused

    lax.fori_loop(0, 4, y_drain, 0)
    far_copy.wait()


def first(
    plan, cycle_size, reach, rows, lengths, table, tokens, gain, mask, w_query, w_key, w_value, w_out
):
    lines = cycle_size // 4
    span = min(lines - 1, (reach + 3) // 4)
    half, model = tokens.shape
    pair = 2 * half
    hbm = pl.BlockSpec(memory_space=pl.ANY)
    dma = pltpu.SemaphoreType.DMA
    return pl.pallas_call(
        functools.partial(first_kernel, plan, lines, span, reach, rows),
        out_shape=[
            jax.ShapeDtypeStruct((pair, model), bf16),
            jax.ShapeDtypeStruct((pair, model), bf16),
            jax.ShapeDtypeStruct((pair, WIDE), bf16),
            jax.ShapeDtypeStruct((pair, 2 * plan.cols), bf16),
            jax.ShapeDtypeStruct((rows, 128), bf16),
            jax.ShapeDtypeStruct((pair, 128), bf16),
            jax.ShapeDtypeStruct((2, plan.heads, TQ, TK), f32),
            jax.ShapeDtypeStruct((lines, 2, 2, 8, pair), f32),
            jax.ShapeDtypeStruct(w_out.shape, bf16),
            jax.ShapeDtypeStruct((lines, 2, 2, pair, 2 * plan.cols), bf16),
        ],
        in_specs=[smem] * 2 + [vmem] * 3 + [hbm] * 4,
        out_specs=[vmem] * 8 + [hbm] * 2,
        scratch_shapes=[
            pltpu.VMEM((3 * plan.cols, model), bf16),
            pltpu.VMEM((pair, 2 * plan.cols), bf16),
            pltpu.VMEM((8, pair), f32),
            dma((3,)),
            dma((2, 5)),
            dma((4,)),
            dma((lines, 2, 2)),
            dma((4, 4, lines)),
            dma((4, 2, lines)),
            dma((4, 2, lines)),
        ],
        compiler_params=pltpu.CompilerParams(
            vmem_limit_bytes=56 * 2**20, collective_id=4, has_side_effects=True
        ),
        name="project_gather",
    )(lengths, table, tokens, gain, mask, w_query.T, w_key.T, w_value.T, w_out)


def tn(a, b):
    return lax.dot_general(a, b, (((0,), (0,)), ((), ())), preferred_element_type=f32)


def line_relay(spot, start, receive):
    def level(k, unused):
        @pl.when(spot.z - k >= 0)
        def _():
            if_first(k, lambda: receive(1, spot.z - k))

            @pl.when(spot.z + 1 < spot.lines)
            def _():
                start(1, spot.z - k)

        @pl.when(spot.z + k < spot.lines)
        def _():
            if_first(k, lambda: receive(-1, spot.z + k))

            @pl.when(spot.z > 0)
            def _():
                start(-1, spot.z + k)

        return unused

    def if_first(k, run):
        @pl.when(k > 0)
        def _():
            run()

    return level


def finish_kernel(
    plan, lines, dq_hbm, dk_hbm, dv_hbm, att_hbm, normed_hbm, branch_hbm, far_hbm,
    wq_hbm, wk_hbm, wv_hbm, mask_ref, tokens_ref, gain_ref, gh_ref, table_ref, gain_part_ref,
    gt_ref, gm_ref, weights_ref, gain_one_ref, gain_two_ref, table_out_ref,
    w3_ref, load_sem, lefts, rights, product, mine, core_in, x_in, up_in, down_in, all_w, y_out, y_in, own_part, mask_in,
    small_own, small_y, small_core, small_x, small_all,
    y_sem, core_sem, x_sem, up_sem, down_sem, gz_sem, gx_sem, gc_sem, sz_sem,
):
    spot = Spot(lines)
    z, x, core, wa = (spot.z, spot.x, spot.core, spot.wa)
    cols = plan.cols
    half = tokens_ref.shape[0]
    our_rows = pl.ds(pl.multiple_of(wa * half, half), half)
    their_rows = pl.ds(pl.multiple_of((1 - wa) * half, half), half)
    targets = (
        (dq_hbm, lefts.at[0]),
        (normed_hbm, rights.at[0]),
        (att_hbm, lefts.at[3]),
        (branch_hbm, rights.at[1, our_rows]),
        (far_hbm, rights.at[1, their_rows]),
        (dk_hbm, lefts.at[1]),
        (dv_hbm, lefts.at[2]),
        (wq_hbm, w3_ref.at[pl.ds(0, cols)]),
        (wk_hbm, w3_ref.at[pl.ds(WIDE, cols)]),
        (wv_hbm, w3_ref.at[pl.ds(3 * WIDE - cols, cols)]),
    )
    loads = [
        pltpu.make_async_copy(src, dst, load_sem.at[i]) for i, (src, dst) in enumerate(targets)
    ]
    for load in loads:
        load.start()
    gap = jnp.zeros((WIDE - cols, tokens_ref.shape[1]), bf16)
    w3_ref[cols:WIDE] = gap
    w3_ref[WIDE + cols : 2 * WIDE] = gap
    w3_ref[2 * WIDE : 3 * WIDE - cols] = gap
    greet(spot, True)
    quarter = half // 2
    model = tokens_ref.shape[1]
    rows = mine.shape[3]

    def grad_rows(at):
        at = pl.ds(pl.multiple_of(at, quarter), quarter)
        return (
            nn(lefts[0, at, :], w3_ref[0:256])
            + nn(lefts[1, at, :], w3_ref[256:512])
            + nn(lefts[2, at, :], w3_ref[512:768])
        )

    def y_copy(i):
        return send(y_out.at[i], y_in.at[i], y_sem.at[0, i], y_sem.at[1, i], spot.y_mate())

    def theirs(i, unused):
        y_out[i] = grad_rows((1 - wa) * half + i * quarter).astype(bf16)
        y_copy(i).start()
        return unused

    for i in (0, 5, 6, 7, 8, 9):
        loads[i].wait()
    lax.fori_loop(0, 2, theirs, 0)
    mask_copy = send(
        mask_ref.at[1 - wa], mask_in, y_sem.at[0, 2], y_sem.at[1, 2], spot.y_mate()
    )
    mask_copy.start()
    for i in (1, 2, 3, 4):
        loads[i].wait()
    per = plan.cols // rows

    def core_copy(m):
        part = pl.ds(m * per // 4, per // 4)
        return send(
            mine.at[part, :, 1 - core],
            core_in.at[part],
            core_sem.at[0, m],
            core_sem.at[1, m],
            spot.core_mate(),
        )

    def fill(i, unused):
        m = (3 * i) % 4
        product[...] = tn(lefts[m], rights[m // 3]).astype(bf16)

        def place(offset):
            for j in range(per):
                mine[m * per // 4 + j // 4, (j // 2) % 2, j % 2] = product[
                    offset + j * rows : offset + (j + 1) * rows, :
                ]

        @pl.when(m < 2)
        def _():
            place(0)

        @pl.when(m >= 2)
        def _():
            place(WIDE - plan.cols)

        core_copy(m).start()
        return unused

    lax.fori_loop(0, 4, fill, 0)
    def x_copy(d):
        return send(
            mine.at[d, 1 - x, core], x_in.at[d], x_sem.at[0, d], x_sem.at[1, d], spot.x_mate()
        )

    def core_add(d, unused):
        mine[d, 1 - x, core] = added(mine[d, 1 - x, core], core_in[d, 1 - x])
        x_copy(d).start()
        return unused

    def ours(i, unused):
        own_part[pl.ds(pl.multiple_of(i * quarter, quarter), quarter), :] = grad_rows(
            wa * half + i * quarter
        )
        return unused

    def core_stage(i, unused):
        m = (3 * i) % 4
        core_copy(m).wait()
        lax.fori_loop(m * per // 4, (m + 1) * per // 4, core_add, 0)
        return unused

    lax.fori_loop(0, 4, core_stage, 0)

    def core_add_own(d, unused):
        mine[d, x, core] = added(mine[d, x, core], core_in[d, x])
        return unused

    lax.fori_loop(0, lines, core_add_own, 0)
    lax.fori_loop(0, 2, ours, 0)

    def flow(step, d):
        ring, sem = (up_in, up_sem) if step > 0 else (down_in, down_sem)
        return send(
            mine.at[d, x, core], ring.at[d], sem.at[0, d], sem.at[1, d], spot.z_mate(step)
        )

    def merge(step, d):
        flow(step, d).wait_recv()
        ring = up_in if step > 0 else down_in
        mine[d, x, core] = added(mine[d, x, core], ring[d])

    def x_add(i, unused):
        d = (i * (lines - 1)) % lines
        x_copy(d).wait()
        mine[d, x, core] = added(mine[d, x, core], x_in[d])

        @pl.when((z == 0) & (d > 0))
        def _():
            flow(1, d).start()

        @pl.when((z == lines - 1) & (d < lines - 1))
        def _():
            flow(-1, d).start()

        return unused

    lax.fori_loop(0, lines, x_add, 0)
    gain_sum = jnp.zeros((1, model), f32)
    step = 32
    for i in range(2):
        y_copy(i).wait()

        def normal(j, total, i=i):
            at = pl.ds(pl.multiple_of(i * quarter + j * step, step), step)
            there = pl.ds(pl.multiple_of(j * step, step), step)
            grad = own_part[at, :] + y_in[i, there, :].astype(f32)
            rows_in = tokens_ref[at, :].astype(f32)
            inv = lax.rsqrt(jnp.mean(rows_in * rows_in, axis=-1, keepdims=True) + eps)
            scaled = gain_ref[...][None, :] * grad
            mean = jnp.mean(rows_in * scaled, axis=-1, keepdims=True)
            gt_ref[at, :] = gh_ref[at, :] + inv * scaled - rows_in * (inv * inv * inv * mean)
            return total + jnp.sum(grad * rows_in * inv, axis=0, keepdims=True)

        gain_sum = lax.fori_loop(0, quarter // step, normal, gain_sum)
    small_own[...] = jnp.zeros_like(small_own)
    small_own[0:1, :] = gain_sum
    small_own[1:2, :] = gain_part_ref[...]
    for h in range(plan.heads):
        small_own[2:3, 32 * h : 32 * h + 32] = jnp.sum(
            jnp.transpose(table_ref[h]), axis=0, keepdims=True
        )
    small_copy = send(
        small_own, small_y, y_sem.at[0, 4], y_sem.at[1, 4], spot.y_mate()
    )
    small_copy.start()
    mask_copy.wait()
    gm_ref[...] = jnp.sum(mask_ref[wa, 0:1] + mask_in[0:1], axis=0)
    def relay(k, unused):
        high = lines - 1 - k

        @pl.when((z < high) & (z > 0))
        def _():
            merge(1, high)
            flow(1, high).start()

        @pl.when((z > k) & (z + 1 < lines))
        def _():
            merge(-1, k)
            flow(-1, k).start()

        return unused

    lax.fori_loop(0, 1, relay, 0)
    small_copy.wait()
    row = lax.broadcasted_iota(jnp.int32, small_own.shape, 0)
    small_x[0] = small_own[...] + jnp.where(row < 2, small_y[...], 0.0)
    small_core_copy = send(
        small_x.at[0], small_core, core_sem.at[0, 4], core_sem.at[1, 4], spot.core_mate()
    )
    small_core_copy.start()
    lax.fori_loop(1, lines - 1, relay, 0)
    small_core_copy.wait()
    small_x[1] = small_x[0] + small_core[...]
    small_x_copy = send(
        small_x.at[1], small_x.at[2], x_sem.at[0, lines], x_sem.at[1, lines], spot.x_mate()
    )
    small_x_copy.start()

    @pl.when(z > 0)
    def _():
        merge(1, z)

    @pl.when(z + 1 < lines)
    def _():
        merge(-1, z)

    all_w[z, x, core] = mine[z, x, core]

    def pass_w(step, d):
        i = 0 if step > 0 else 1
        return send(
            all_w.at[d, x, core], all_w.at[d, x, core], gz_sem.at[i, d], gz_sem.at[2 + i, d],
            spot.z_mate(step),
        )

    def pass_s(step, d):
        i = 0 if step > 0 else 1
        return send(
            small_all.at[d], small_all.at[d], sz_sem.at[i, d], sz_sem.at[2 + i, d],
            spot.z_mate(step),
        )

    def across(d):
        return send(
            all_w.at[d, x, core], all_w.at[d, x, core], gx_sem.at[0, d], gx_sem.at[1, d],
            spot.x_mate(),
        )

    def beside(d):
        return send(
            all_w.at[d, :, core], all_w.at[d, :, core], gc_sem.at[0, d], gc_sem.at[1, d],
            spot.core_mate(),
        )

    small_x_copy.wait()
    small_all[z] = small_x[1] + small_x[2]

    def receive(step, d):
        pass_w(step, d).wait_recv()
        across(d).start()

    across(z).start()
    def pass_both(step, d):
        pass_s(step, d).start()
        pass_w(step, d).start()

    def receive_both(step, d):
        pass_s(step, d).wait_recv()
        receive(step, d)

    lax.fori_loop(0, lines, line_relay(spot, pass_both, receive_both), 0)

    def add_small(d, total):
        return total + small_all[d]

    totals = lax.fori_loop(1, lines, add_small, small_all[0])
    gain_one_ref[...] = jnp.sum(totals[0:1], axis=0)
    gain_two_ref[...] = jnp.sum(totals[1:2], axis=0)
    for h in range(plan.heads):
        table_out_ref[h : h + 1, :] = totals[2:3, 32 * h : 32 * h + 32]
    def spread(d, unused):
        across(d).wait()
        beside(d).start()
        return unused

    lax.fori_loop(0, lines, spread, 0)

    def copy_out(d, unused):
        beside(d).wait()
        weights_ref[d] = all_w[d]
        return unused

    lax.fori_loop(0, lines, copy_out, 0)

    def drain(d, unused):
        @pl.when((z < d))
        def _():
            flow(1, d).wait_send()

        @pl.when((z > d))
        def _():
            flow(-1, d).wait_send()

        @pl.when((d <= z) & (z + 1 < lines))
        def _():
            pass_w(1, d).wait_send()
            pass_s(1, d).wait_send()

        @pl.when((d >= z) & (z > 0))
        def _():
            pass_w(-1, d).wait_send()
            pass_s(-1, d).wait_send()

        return unused

    lax.fori_loop(0, lines, drain, 0)


def finish(plan, cycle_size, *operands):
    lines = cycle_size // 4
    half, model = operands[11].shape
    rows = 4 * plan.cols // cycle_size
    dma = pltpu.SemaphoreType.DMA
    return pl.pallas_call(
        functools.partial(finish_kernel, plan, lines),
        out_shape=[
            jax.ShapeDtypeStruct((half, model), f32),
            jax.ShapeDtypeStruct((half,), f32),
            jax.ShapeDtypeStruct((lines, 2, 2, rows, model), bf16),
            jax.ShapeDtypeStruct((model,), f32),
            jax.ShapeDtypeStruct((model,), f32),
            jax.ShapeDtypeStruct((plan.heads, 32), f32),
        ],
        in_specs=[pl.BlockSpec(memory_space=pl.ANY)] * 10 + [vmem] * 6,
        out_specs=[vmem] * 6,
        scratch_shapes=[
            pltpu.VMEM((3 * WIDE, model), bf16),
            dma((10,)),
            pltpu.VMEM((4, 2 * half, WIDE), bf16),
            pltpu.VMEM((2, 2 * half, model), bf16),
            pltpu.VMEM((WIDE, model), bf16),
            pltpu.VMEM((lines, 2, 2, rows, model), bf16),
            pltpu.VMEM((lines, 2, rows, model), bf16),
            pltpu.VMEM((lines, rows, model), bf16),
            pltpu.VMEM((lines, rows, model), bf16),
            pltpu.VMEM((lines, rows, model), bf16),
            pltpu.VMEM((lines, 2, 2, rows, model), bf16),
            pltpu.VMEM((2, half // 2, model), bf16),
            pltpu.VMEM((2, half // 2, model), bf16),
            pltpu.VMEM((half, model), f32),
            pltpu.VMEM((8, half), f32),
            pltpu.VMEM((8, model), f32),
            pltpu.VMEM((8, model), f32),
            pltpu.VMEM((8, model), f32),
            pltpu.VMEM((3, 8, model), f32),
            pltpu.VMEM((lines, 8, model), f32),
            dma((2, 5)),
            dma((2, 5)),
            dma((2, lines + 1)),
            dma((2, lines)),
            dma((2, lines)),
            dma((4, lines)),
            dma((2, lines)),
            dma((2, lines)),
            dma((4, lines)),
        ],
        compiler_params=pltpu.CompilerParams(
            vmem_limit_bytes=58 * 2**20, collective_id=2, has_side_effects=True
        ),
        name="finish",
    )(*operands)


root = 0.7978845608028654
cubic = 0.044715


def middle_kernel(
    plan, cycle_size, att_ref, mixed_ref, tokens_ref, cot_ref, gain_ref,
    wo_hbm, wo_far_hbm, wg_hbm, wu_hbm, wd_hbm,
    hidden_ref, gh_ref, branch_ref, ffn_ref, ffn_far_ref, do_ref, gain_part_ref, *refs,
):
    stacks, refs = (refs[:3], refs[3:])
    (
        wg, wu, wd, wo, inner, gg, gu, x_ref, att_in, d_out, d_in, e_out, e_in,
        acc_g, rows_buf, load_sem, y_sem, out_sem,
    ) = refs
    spot = Spot(cycle_size // 4)
    wa = spot.wa
    pair, model = tokens_ref.shape
    half = pair // 2
    units = wd.shape[1]
    chunk = half // 4
    block = pair // 4
    loads = [
        pltpu.make_async_copy(src, dst, load_sem.at[i])
        for i, (src, dst) in enumerate(
            (
                (wo_hbm, wo.at[0, 64:]),
                (wo_far_hbm, wo.at[1, 64:]),
                (wg_hbm, wg),
                (wu_hbm, wu),
                (wd_hbm, wd),
            )
        )
    ]
    for load in loads:
        load.start()
    barrier = pltpu.get_barrier_semaphore()
    pl.semaphore_signal(
        barrier, inc=1, device_id=spot.y_mate(), device_id_type=pl.DeviceIdType.MESH
    )
    wo[:, :64, :] = jnp.zeros((2, 64, model), bf16)
    pl.semaphore_wait(barrier, 1)
    ours = wa * half
    theirs = (1 - wa) * half

    def rows_at(start, size):
        return pl.ds(pl.multiple_of(start, size), size)

    def a_start(i):
        return (theirs + i * block) if i < 2 else (ours + (i - 2) * block)

    def a_copy(i, base):
        at = rows_at(base + (i % 2) * block, block)
        return send(att_ref.at[at], att_in.at[at], y_sem.at[0, i], y_sem.at[1, i], spot.y_mate())

    order = (0, 1, 2, 3)
    for i in order:
        a_copy(i, ours if i < 2 else theirs).start()
    loads[0].wait()
    loads[1].wait()

    def normal(i, base, keep):
        a_copy(i, base).wait_recv()
        at = rows_at(base + (i % 2) * block, block)
        branch = nn(att_ref[at, :], wo[0]) + nn(att_in[at, :], wo[1])
        hidden = tokens_ref[at, :].astype(f32) + branch
        if keep:
            hidden_ref[(i % 2) * block : (i % 2 + 1) * block, :] = hidden
        inv = lax.rsqrt(jnp.mean(hidden * hidden, axis=-1, keepdims=True) + eps)
        x_ref[at, :] = (hidden * inv * gain_ref[...][None, :]).astype(bf16)

    normal(0, theirs, False)
    normal(1, theirs, False)
    for load in loads[2:]:
        load.wait()
    wide = 256

    def feed(base):
        rows = rows_at(base, half)
        def tile(u, unused):
            cols = rows_at(u * wide, wide)
            gate = nn(x_ref[rows, :], wg[:, cols])
            upward = nn(x_ref[rows, :], wu[:, cols])
            grad_inner = nn(cot_ref[rows, :], wd[:, cols])
            square = gate * gate
            bend = jnp.tanh(root * gate * (1.0 + cubic * square))
            side = 0.5 * (1.0 + bend)
            gelu = gate * side
            slope = side + 0.5 * gate * (1.0 - bend * bend) * (
                root * (1.0 + 3.0 * cubic * square)
            )
            inner_low = (gelu * upward).astype(bf16)
            gate_low = (grad_inner * upward * slope).astype(bf16)
            up_low = (grad_inner * gelu).astype(bf16)
            inner[rows, cols] = inner_low
            gg[rows, cols] = gate_low
            gu[rows, cols] = up_low
            return unused

        lax.fori_loop(0, units // wide, tile, 0)

    def columns(body):
        def chunk_of(c, unused):
            body(rows_at(c * wide, wide))
            return unused

        lax.fori_loop(0, model // wide, chunk_of, 0)
        if model % wide:
            body(pl.ds(model // wide * wide, model % wide))

    def back_to_rows(base):
        rows = rows_at(base, half)

        def body(cols):
            acc_g[:, cols] = nt(gg[rows, :], wg[cols, :]) + nt(gu[rows, :], wu[cols, :])

        columns(body)

    def forward_to_rows(base, out):
        rows = rows_at(base, half)

        def body(cols):
            out[:, cols] = nt(inner[rows, :], wd[cols, :]).astype(bf16)

        columns(body)

    def d_copy(i):
        return send(
            d_out.at[i], d_in.at[i], y_sem.at[0, 4 + i], y_sem.at[1, 4 + i], spot.y_mate()
        )

    def send_grad(i, unused):
        d_out[i] = acc_g[rows_at(i * chunk, chunk), :].astype(bf16)
        d_copy(i).start()
        return unused

    def half_pass(k, unused):
        base = theirs + k * (ours - theirs)
        feed(base)
        back_to_rows(base)

        @pl.when(k == 0)
        def _():
            lax.fori_loop(0, 4, send_grad, 0)
            normal(2, ours, True)
            normal(3, ours, True)

        return unused

    lax.fori_loop(0, 2, half_pass, 0)
    forward_to_rows(theirs, ffn_far_ref)
    forward_to_rows(ours, ffn_ref)
    count = units // wide

    def out_copy(m, u):
        return pltpu.make_async_copy(
            rows_buf.at[m, u % 2],
            stacks[m].at[rows_at(u * wide, wide)],
            out_sem.at[m, u % 2],
        )

    for m in range(3):
        left = (inner, gg, gu)[m]
        right = (cot_ref, x_ref, x_ref)[m]

        def weight_rows(u, unused, m=m, left=left, right=right):
            @pl.when(u >= 2)
            def _():
                out_copy(m, u - 2).wait()

            turned = jnp.transpose(left[:, rows_at(u * wide, wide)])
            rows_buf[m, u % 2] = nn(turned, right[...]).astype(bf16)
            out_copy(m, u).start()
            return unused

        lax.fori_loop(0, count, weight_rows, 0)

    def e_copy(i):
        return send(
            e_out.at[i], e_in.at[i], y_sem.at[0, 8 + i], y_sem.at[1, 8 + i], spot.y_mate()
        )

    def normal_back(i, total):
        d_copy(i).wait()
        at = rows_at(i * chunk, chunk)
        grad = acc_g[at, :] + d_in[i].astype(f32)
        hidden = hidden_ref[at, :]
        inv = lax.rsqrt(jnp.mean(hidden * hidden, axis=-1, keepdims=True) + eps)
        scaled = gain_ref[...][None, :] * grad
        mean = jnp.mean(hidden * scaled, axis=-1, keepdims=True)
        grad_hidden = (
            cot_ref[rows_at(ours + i * chunk, chunk), :].astype(f32)
            + inv * scaled
            - hidden * (inv * inv * inv * mean)
        )
        gh_ref[at, :] = grad_hidden
        low = grad_hidden.astype(bf16)
        branch_ref[at, :] = low
        e_out[i] = nt(low, wo[1]).astype(bf16)
        e_copy(i).start()
        do_ref[rows_at(ours + i * chunk, chunk), :] = nt(low, wo[0]).astype(bf16)
        return total + jnp.sum(grad * hidden * inv, axis=0, keepdims=True)

    gain_part_ref[...] = lax.fori_loop(0, 4, normal_back, jnp.zeros((1, model), f32))

    def row_terms(at, grad):
        lane = lanes_of(chunk)
        terms = grad.astype(f32) * mixed_ref[at, :]
        out = grad
        for h in range(plan.heads):
            row_term = jnp.sum(
                jnp.where(lane // 64 == h + 1, terms, 0.0), axis=1, keepdims=True
            )
            for i, part in enumerate(split3(-row_term)):
                out = jnp.where(lane == 3 * h + i, part, out)
        do_ref[at, :] = out

    def own_terms(i, unused):
        at = rows_at(ours + i * chunk, chunk)
        row_terms(at, do_ref[at, :])
        return unused

    lax.fori_loop(0, 4, own_terms, 0)

    def far_terms(i, unused):
        e_copy(i).wait()
        row_terms(rows_at(theirs + i * chunk, chunk), e_in[i])
        return unused

    lax.fori_loop(0, 4, far_terms, 0)
    for m in range(3):
        for u in range(max(0, count - 2), count):
            out_copy(m, u).wait()
    for i in order:
        a_copy(i, ours if i < 2 else theirs).wait_send()


def middle(
    plan, cycle_size, attended, mixed, tokens, cot, gain, w_out, w_out_far, w_gate, w_up, w_down
):
    pair, model = tokens.shape
    half = pair // 2
    units = w_down.shape[0]
    chunk = half // 4
    hbm = pl.BlockSpec(memory_space=pl.ANY)
    dma = pltpu.SemaphoreType.DMA
    return pl.pallas_call(
        functools.partial(middle_kernel, plan, cycle_size),
        out_shape=[
            jax.ShapeDtypeStruct((half, model), f32),
            jax.ShapeDtypeStruct((half, model), f32),
            jax.ShapeDtypeStruct((half, model), bf16),
            jax.ShapeDtypeStruct((half, model), bf16),
            jax.ShapeDtypeStruct((half, model), bf16),
            jax.ShapeDtypeStruct((pair, WIDE), bf16),
            jax.ShapeDtypeStruct((1, model), f32),
        ]
        + [jax.ShapeDtypeStruct((units, model), bf16)] * 3,
        in_specs=[vmem] * 5 + [hbm] * 5,
        out_specs=[vmem] * 7 + [hbm] * 3,
        scratch_shapes=[
            pltpu.VMEM((model, units), bf16),
            pltpu.VMEM((model, units), bf16),
            pltpu.VMEM((model, units), bf16),
            pltpu.VMEM((2, WIDE, model), bf16),
            pltpu.VMEM((pair, units), bf16),
            pltpu.VMEM((pair, units), bf16),
            pltpu.VMEM((pair, units), bf16),
            pltpu.VMEM((pair, model), bf16),
            pltpu.VMEM((pair, WIDE), bf16),
            pltpu.VMEM((4, chunk, model), bf16),
            pltpu.VMEM((4, chunk, model), bf16),
            pltpu.VMEM((4, chunk, WIDE), bf16),
            pltpu.VMEM((4, chunk, WIDE), bf16),
            pltpu.VMEM((half, model), f32),
            pltpu.VMEM((3, 2, WIDE, model), bf16),
            dma((5,)),
            dma((2, 12)),
            dma((3, 2)),
        ],
        compiler_params=pltpu.CompilerParams(
            vmem_limit_bytes=60 * 2**20, collective_id=3, has_side_effects=True
        ),
        name="feed_forward",
    )(attended, mixed, tokens, cot, gain, w_out, w_out_far, w_gate, w_up, w_down.T)


class Scatter:
    def __init__(self, spot, units, parts, outs, buffers, sems):
        self.spot = spot
        self.units = units
        self.parts = parts
        self.outs = outs
        self.mine, self.core_in, self.x_in, self.up_in, self.down_in = buffers
        self.load_sem, self.core_sem, self.x_sem, self.up_sem, self.down_sem = sems

    def rows_of(self, u):
        return pl.ds(self.units[u][1], self.units[u][2])

    def load(self, u):
        m = self.units[u][0]
        return pltpu.make_async_copy(
            self.parts[m].at[:, :, self.spot.core, self.rows_of(u)],
            self.mine.at[m, :, :, self.rows_of(u)],
            self.load_sem.at[u],
        )

    def core_copy(self, u):
        m = self.units[u][0]
        return send(
            self.parts[m].at[:, :, 1 - self.spot.core, self.rows_of(u)],
            self.core_in.at[m, :, :, self.rows_of(u)],
            self.core_sem.at[0, u],
            self.core_sem.at[1, u],
            self.spot.core_mate(),
        )

    def x_copy(self, u):
        m = self.units[u][0]
        x = self.spot.x
        src = self.mine.at[m, :, 1 - x, self.rows_of(u)]
        dst = self.x_in.at[m, :, self.rows_of(u)]
        return send(src, dst, self.x_sem.at[0, u], self.x_sem.at[1, u], self.spot.x_mate())

    def begin(self, u):
        self.load(u).start()
        self.core_copy(u).start()

    def core_stage(self, u):
        m = self.units[u][0]
        x = self.spot.x
        self.load(u).wait()
        self.core_copy(u).wait()

        def add(slot):
            def body(line, unused):
                at = (m, line, slot, self.rows_of(u))
                self.mine[at] = added(self.mine[at], self.core_in[at])
                return unused

            lax.fori_loop(0, self.spot.lines, body, 0)

        add(1 - x)
        self.x_copy(u).start()
        add(x)

    def x_stage(self, u):
        m = self.units[u][0]
        x = self.spot.x
        self.x_copy(u).wait()

        def body(line, unused):
            at = (m, line, x, self.rows_of(u))
            self.mine[at] = added(self.mine[at], self.x_in[m, line, self.rows_of(u)])
            return unused

        lax.fori_loop(0, self.spot.lines, body, 0)
        self.ends(u)

    def copy(self, u, step, d):
        m = self.units[u][0]
        sem = self.up_sem if step > 0 else self.down_sem
        ring = self.up_in if step > 0 else self.down_in
        return send(
            self.mine.at[m, d, self.spot.x, self.rows_of(u)],
            ring.at[m, d, self.rows_of(u)],
            sem.at[0, u, d],
            sem.at[1, u, d],
            self.spot.z_mate(step),
        )

    def receive(self, u, step, d):
        m = self.units[u][0]
        self.copy(u, step, d).wait_recv()
        ring = self.up_in if step > 0 else self.down_in
        at = (m, d, self.spot.x, self.rows_of(u))
        self.mine[at] = added(self.mine[at], ring[m, d, self.rows_of(u)])

    def start(self, u, step, d):
        self.copy(u, step, d).start()

    def ends(self, u):
        z, lines = (self.spot.z, self.spot.lines)

        @pl.when(z == 0)
        def _():
            def up(k, unused):
                self.start(u, 1, lines - 1 - k)
                return unused

            lax.fori_loop(0, lines - 1, up, 0)

        @pl.when(z == lines - 1)
        def _():
            def down(k, unused):
                self.start(u, -1, k)
                return unused

            lax.fori_loop(0, lines - 1, down, 0)

    def relay(self, u, lag):
        z, lines = (self.spot.z, self.spot.lines)
        top = lines - 2 if lag == 2 else lag

        @pl.when((z >= lag) & (z <= top))
        def _():
            def up(k, unused):
                self.receive(u, 1, lines - 1 - k)
                self.start(u, 1, lines - 1 - k)
                return unused

            lax.fori_loop(0, lines - 1 - z, up, 0)

        @pl.when((lines - 1 - z >= lag) & (lines - 1 - z <= top))
        def _():
            def down(k, unused):
                self.receive(u, -1, k)
                self.start(u, -1, k)
                return unused

            lax.fori_loop(0, z, down, 0)

    def settle(self, u):
        z, lines = (self.spot.z, self.spot.lines)

        @pl.when(z > 0)
        def _():
            self.receive(u, 1, z)

        @pl.when(z + 1 < lines)
        def _():
            self.receive(u, -1, z)

        self.store(u)

    def store(self, u):
        m = self.units[u][0]
        self.outs[m][self.rows_of(u), :] = self.mine[
            m, self.spot.z, self.spot.x, self.rows_of(u)
        ].astype(f32)

    def drain(self, u):
        z, lines = (self.spot.z, self.spot.lines)

        def body(k, unused):
            @pl.when(z < lines - 1 - k)
            def _():
                self.copy(u, 1, lines - 1 - k).wait_send()

            @pl.when(z > k)
            def _():
                self.copy(u, -1, k).wait_send()

            return unused

        lax.fori_loop(0, lines - 1, body, 0)


def scatter_units(rows):
    if rows % 16 or rows < 112:
        return [(m, 0, rows) for m in range(3)]
    tail = rows - 64
    return [
        (0, 0, 64), (1, 0, 64), (2, 0, 64), (0, 64, tail), (1, 64, tail), (2, 64, tail - 16),
        (2, rows - 16, 16),
    ]


def backward_kernel(
    plan, lines, span, reach, doc_most, rows, pair, table_ref, qb_ref, do_ref,
    own_kv, own_aug, near_hbm, aug_hbm, masks_hbm, g_hbm, qall_hbm, branch_hbm, ffn_hbm, p0, p1, p2,
    dq_ref, tab_ref, dk_ref, dv_ref, mask_ref, o0, o1, o2, far_hbm, ffn_in_hbm, all_do,
    mine, core_in, x_in, up_in, down_in,
    km, vm, mask_row, g_buf, aug_buf, qh_ref, doh_ref, acc, near_ref, near_acc, far_acc,
    load_sem, core_sem, rx_sem, up_sem, down_sem, own_sem, zero_sem, z_sem, x_sem, c_sem, g_sem,
    q_sem,
):
    spot = Spot(lines)
    z, x, core = (spot.z, spot.x, spot.core)
    units = scatter_units(o0.shape[0])
    scatter = Scatter(
        spot,
        units,
        (p0, p1, p2),
        (o0, o1, o2),
        (mine, core_in, x_in, up_in, down_in),
        (load_sem, core_sem, rx_sem, up_sem, down_sem),
    )
    order = range(len(units))
    greet(spot, True)
    far_copy = send(branch_hbm, far_hbm, own_sem.at[2], own_sem.at[3], spot.y_mate())
    far_copy.start()
    ffn_copy = send(ffn_hbm, ffn_in_hbm, own_sem.at[4], own_sem.at[5], spot.y_mate())
    ffn_copy.start()

    def outside(d):
        return (d < z - span) | (d > z + span)

    def pass_copy(step, d):
        i = 0 if step > 0 else 1
        part = all_do.at[d, :, core]
        return send(part, part, z_sem.at[i, d], z_sem.at[2 + i, d], spot.z_mate(step))

    across = send(do_ref, all_do.at[z, x, core], x_sem.at[0], x_sem.at[1], spot.x_mate())

    def beside(d):
        part = all_do.at[d, :, core]
        return send(part, part, c_sem.at[0, d], c_sem.at[1, d], spot.core_mate())

    own_copy = pltpu.make_async_copy(do_ref, all_do.at[z, x, core], own_sem.at[0])

    def zero_copies(d):
        return [
            pltpu.make_async_copy(vm.at[pl.ds(0, pair)], all_do.at[d, a, b], zero_sem.at[d, a, b])
            for a in range(2)
            for b in range(2)
        ]

    def zero_start(d, unused):
        @pl.when(outside(d))
        def _():
            for copy in zero_copies(d):
                copy.start()

        return unused

    def turn():
        across.wait()
        own_copy.wait()

        @pl.when(z + 1 < lines)
        def _():
            pass_copy(1, z).start()

        @pl.when(z > 0)
        def _():
            pass_copy(-1, z).start()

        beside(z).start()

    def level(k):
        @pl.when(z - k >= 0)
        def _():
            d = jnp.maximum(z - k, 0)
            pass_copy(1, d).wait_recv()
            if k < span:

                @pl.when(z + 1 < lines)
                def _():
                    pass_copy(1, d).start()

            beside(d).start()

        @pl.when(z + k < lines)
        def _():
            d = jnp.minimum(z + k, lines - 1)
            pass_copy(-1, d).wait_recv()
            if k < span:

                @pl.when(z > 0)
                def _():
                    pass_copy(-1, d).start()

            beside(d).start()

    def gathered(d, unused):
        @pl.when(~outside(d))
        def _():
            beside(d).wait()

        @pl.when(outside(d))
        def _():
            for copy in zero_copies(d):
                copy.wait()

        @pl.when((z + 1 < lines) & (d <= z) & (d > z - span))
        def _():
            pass_copy(1, d).wait_send()

        @pl.when((z > 0) & (d >= z) & (d < z + span))
        def _():
            pass_copy(-1, d).wait_send()

        return unused

    own_copy.start()
    across.start()
    for u in order:
        scatter.begin(u)
    vm[:PAD, :] = jnp.zeros((PAD, WIDE), bf16)
    lax.fori_loop(0, lines, zero_start, 0)

    base = spot.index * pair
    total = 4 * lines * pair
    origin = jnp.clip(base - reach * pair, 0, total - rows)
    local = base - origin
    blocks = rows // pair

    def mask_copy(n):
        to = pl.ds(pl.multiple_of(PAD + n * pair, 128), pair)
        return pltpu.make_async_copy(masks_hbm.at[n], mask_row.at[:, to], q_sem.at[1 + n])

    def mask_start(n, unused):
        mask_copy(n).start()
        return unused

    lax.fori_loop(0, blocks, mask_start, 0)
    mask_row[:, :PAD] = jnp.zeros((8, PAD), f32)
    mask_row[:, PAD + rows :] = jnp.zeros((8, PAD), f32)
    km[:PAD, :] = jnp.broadcast_to(
        jnp.where(pad_lanes(plan), neg_big, 0.0).astype(bf16), (PAD, WIDE)
    )
    km[PAD + rows :, :] = km[:PAD, :]
    vm[PAD + rows :, :] = jnp.zeros((PAD, WIDE), bf16)
    low_block = lanes_of(pair, 128) < 64
    ones_block = (lanes_of(pair, 128) < 3 * plan.heads).astype(bf16)

    def g_copy(n):
        at = pl.ds(pl.multiple_of(n * pair, pair), pair)
        return pltpu.make_async_copy(g_hbm.at[at], g_buf.at[n % 2], g_sem.at[0, n % 2])

    def aug_copy(n):
        at = pl.ds(pl.multiple_of(n * pair, pair), pair)
        return pltpu.make_async_copy(aug_hbm.at[at], aug_buf.at[n % 2], g_sem.at[1, n % 2])

    def near_copy(flip):
        return pltpu.make_async_copy(near_hbm.at[flip], near_ref, own_sem.at[1])

    g_copy(0).start()
    aug_copy(0).start()
    near_copy(0).start()

    def build(n, unused):
        g_copy(n).wait()
        aug_copy(n).wait()

        @pl.when(n + 1 < blocks)
        def _():
            g_copy(n + 1).start()
            aug_copy(n + 1).start()

        mask_copy(n).wait()
        to = pl.ds(pl.multiple_of(PAD + n * pair, 128), pair)
        middle = g_buf[n % 2, :, 128:256]
        km[to, 0:128] = g_buf[n % 2, :, 0:128]
        km[to, 128:256] = jnp.where(low_block, middle, aug_buf[n % 2])
        vm[to, 0:128] = jnp.where(low_block, ones_block, middle)
        vm[to, 128:256] = g_buf[n % 2, :, 256:384]
        return unused

    early = min(6, blocks)
    lax.fori_loop(0, early, build, 0)
    scatter.core_stage(0)
    lax.fori_loop(early, blocks, build, 0)
    near_copy(0).wait()
    near_acc[...] = jnp.zeros_like(near_acc)
    far_acc[...] = jnp.zeros_like(far_acc)
    lane = lanes_of(TQ)
    low = lanes_of(TQ, 128) < 64
    ones = (lanes_of(TQ, 128) < 3 * plan.heads).astype(bf16)

    def chunks(t):
        start = local + t * TQ
        least = jnp.maximum(start - doc_most + 1, 0)
        most = jnp.minimum(start + TQ + doc_most - 1, rows)
        n_left = jnp.maximum(start - EDGE - least + TK - 1, 0) // TK
        n_right = jnp.maximum(most - (start + TK - EDGE) + TK - 1, 0) // TK
        return start, n_left, n_right

    def rows_of_tile(t):
        return pl.ds(pl.multiple_of(t * TQ, TQ), TQ)

    def near_of(start):
        return pl.ds(pl.multiple_of(start + PAD - EDGE, 128), TK)

    def query_grads(h, s, part):
        return jnp.exp(s) * nt(doh_ref[h], vm[part, :])

    def dq_near(t, start):
        out = rows_of_tile(t)
        near = near_of(start)
        q = qb_ref[out, :]
        do = do_ref[out, :]
        for h in range(plan.heads):
            qh_ref[h] = jnp.where(plan.key_lanes(lane, h), q, jnp.zeros_like(q))
            doh_ref[h] = jnp.where(plan.value_lanes(lane, h), do, jnp.zeros_like(do))
            ds = query_grads(
                h, nt(qh_ref[h], km[near, :]) + near_ref[h] + mask_row[0:1, near], near
            )
            near_acc[h] += ds
            acc[h] = nn(ds.astype(bf16), km[near, :])

    def dq_far(start, n, n_left, count):
        parts = far_pair(start, n, n_left, count, far_left_bucket, far_right_bucket)
        for h in range(plan.heads):
            grads = []
            for i, (part, bucket) in enumerate(parts):
                slot = (2 * n + i >= n_left).astype(jnp.int32)
                offset = mask_row[0:1, part] + table_ref[h, bucket]
                ds = query_grads(h, nt(qh_ref[h], km[part, :]) + offset, part)
                grads.append(nn(ds.astype(bf16), km[part, :]))
                far_acc[slot, h] += (
                    ds[:, 0:128] + ds[:, 128:256] + ds[:, 256:384] + ds[:, 384:512]
                )
            acc[h] += grads[0] + grads[1]

    def dq_end(t):
        result = jnp.zeros((TQ, WIDE), f32)
        for h in range(plan.heads):
            result = jnp.where(lane // 64 == h, acc[h], result)
        dq_ref[rows_of_tile(t), :] = result.astype(bf16)

    def table_end():
        row = lax.broadcasted_iota(jnp.int32, (EDGE, 3 * EDGE), 0)
        col = lax.broadcasted_iota(jnp.int32, (EDGE, 3 * EDGE), 1)
        bucket = bucket_of(col - EDGE - row)
        for h in range(plan.heads):
            band = near_acc[h, :EDGE, : 3 * EDGE] + near_acc[h, EDGE:, EDGE:]

            def one(b, unused, band=band, h=h):
                part = jnp.sum(jnp.where(bucket == b, band, 0.0), axis=0, keepdims=True)
                tab_ref[h, pl.ds(b, 1), :] = part[:, :128] + part[:, 128:256] + part[:, 256:]
                return unused

            lax.fori_loop(0, 32, one, 0)
            for b, slot, extra in (
                (far_left_bucket, 0, near_acc[h, EDGE:, :EDGE]),
                (far_right_bucket, 1, near_acc[h, :EDGE, 3 * EDGE :]),
            ):
                tab_ref[h, b : b + 1, :] += jnp.sum(
                    far_acc[slot, h], axis=0, keepdims=True
                ) + jnp.sum(extra, axis=0, keepdims=True)

    def swap_operands():
        near_copy(1).start()
        lax.fori_loop(0, lines, gathered, 0)
        q_copy = pltpu.make_async_copy(qall_hbm, km.at[pl.ds(PAD, rows)], q_sem.at[0])
        q_copy.start()

        def block_copy(n):
            b = origin // pair + n
            return pltpu.make_async_copy(
                all_do.at[b // 4, (b // 2) % 2, b % 2],
                vm.at[pl.ds(pl.multiple_of(PAD + n * pair, 128), pair)],
                q_sem.at[1 + n],
            )

        def block_start(n, unused):
            block_copy(n).start()
            return unused

        lax.fori_loop(0, blocks, block_start, 0)
        first = lanes_of(1)
        stat = (first >= plan.stat_lane) & (first < plan.stat_lane + 3 * plan.heads)
        km[:PAD, :] = jnp.broadcast_to(jnp.where(stat, neg_big, 0.0).astype(bf16), (PAD, WIDE))
        km[PAD + rows :, :] = km[:PAD, :]

        def block_wait(n, unused):
            block_copy(n).wait()
            return unused

        lax.fori_loop(0, blocks, block_wait, 0)
        q_copy.wait()
        near_copy(1).wait()

    def key_grads(h, s, part):
        p = jnp.exp(s)
        ds = p * nt(doh_ref[h], vm[part, :])
        return nn(p.astype(bf16), vm[part, :]), nn(ds.astype(bf16), km[part, :])

    def dkv_near(t, start):
        out = rows_of_tile(t)
        near = near_of(start)
        middle = own_kv[out, 128:256]
        k = jnp.concatenate([own_kv[out, 0:128], jnp.where(low, middle, own_aug[out, :])], axis=1)
        v = jnp.concatenate([jnp.where(low, ones, middle), own_kv[out, 256:384]], axis=1)
        for h in range(plan.heads):
            qh_ref[h] = jnp.where(plan.key_lanes(lane, h), k, jnp.zeros_like(k))
            doh_ref[h] = jnp.where(plan.value_lanes(lane, h), v, jnp.zeros_like(v))
            near_acc[h, :, :WIDE], acc[h] = key_grads(
                h, nt(qh_ref[h], km[near, :]) + near_ref[h], near
            )

    def dkv_far(start, n, n_left, count):
        parts = far_pair(start, n, n_left, count, far_right_bucket, far_left_bucket)
        for h in range(plan.heads):
            (v_one, k_one), (v_two, k_two) = [
                key_grads(h, nt(qh_ref[h], km[part, :]) + table_ref[h, bucket], part)
                for part, bucket in parts
            ]
            near_acc[h, :, :WIDE] += v_one + v_two
            acc[h] += k_one + k_two

    def dkv_end(t):
        out = rows_of_tile(t)
        dk = jnp.zeros((TQ, WIDE), f32)
        dv = jnp.zeros((TQ, WIDE), f32)
        mask_grad = jnp.zeros((TQ, 1), f32)
        for h in range(plan.heads):
            dk = jnp.where(lane // 64 == h, acc[h], dk)
            dv = jnp.where(lane // 64 == h + 1, near_acc[h, :, :WIDE], dv)
            mask_grad = mask_grad + acc[h][:, plan.mask_lane : plan.mask_lane + 1]
        mask_ref[t] = jnp.transpose(jnp.broadcast_to(mask_grad, (TQ, 128)))[:8, :]
        dk_ref[out, :] = dk.astype(bf16)
        dv_ref[out, :] = dv.astype(bf16)

    tiles = pair // TQ
    steps = 1 + -(-(2 * (-(-doc_most // TK)) + 1) // 2)
    half_slots = tiles * steps
    last_step = steps - 1

    def attention(w):
        backward = w >= half_slots
        t = (w % half_slots) // steps
        n = w % steps
        start, n_left, n_right = chunks(t)
        count = n_left + n_right
        live = (n > 0) & (2 * (n - 1) < count)

        @pl.when(~backward)
        def _():
            @pl.when(n == 0)
            def _():
                dq_near(t, start)

            @pl.when(live)
            def _():
                dq_far(start, n - 1, n_left, count)

            @pl.when(n == last_step)
            def _():
                dq_end(t)

        @pl.when(backward & (w < 2 * half_slots))
        def _():
            @pl.when(w == half_slots)
            def _():
                table_end()
                swap_operands()

            @pl.when(n == 0)
            def _():
                dkv_near(t, start)

            @pl.when(live)
            def _():
                dkv_far(start, n - 1, n_left, count)

            @pl.when(n == last_step)
            def _():
                dkv_end(t)

    work = 2 * half_slots
    events = []

    def due(time, run, *args):
        events.append((max(0, int((time - start_us) / slot_us)), functools.partial(run, *args)))

    start_us, slot_us = (6.0, 2.5)
    due(6.0, turn)
    for k in range(1, span + 1):
        due((22.0, 36.0)[min(k, 2) - 1], level, k)
    times = (
        (7.0, 26.0, 51.0, 61.0, 68.0),
        (10.5, 43.0, 64.0, 74.0, 81.0),
        (14.0, 60.0, 77.0, 87.0, 94.0),
        (17.0, 73.0, 87.0, 95.0, 101.0),
        (20.0, 86.0, 97.5, 106.0, 111.0),
        (22.0, 95.0, 104.0, 110.0, 114.0),
        (23.0, 99.0, 107.0, 111.0, 114.5),
    )
    for u in order:
        core_at, x_at, one_at, two_at, end_at = times[u]
        if u > 0:
            due(core_at, scatter.core_stage, u)
        due(x_at, scatter.x_stage, u)
        due(one_at, scatter.relay, u, 1)
        due(two_at, scatter.relay, u, 2)
        due(end_at, scatter.settle, u)
    events.sort(key=lambda event: event[0])
    end = max(work, events[-1][0] + 1)

    def slot(w, unused):
        for at, run in events:

            @pl.when(w == at)
            def _(run=run):
                run()

        attention(w)
        return unused

    lax.fori_loop(0, end, slot, 0)
    for u in order:
        scatter.drain(u)
    far_copy.wait()
    ffn_copy.wait()


def backward(
    plan, cycle_size, reach, doc_most, rows, table, aug, masks, q_back, do_wide, own_kv, own_aug,
    near_bias, kv_all, q_all, branch, ffn_far, parts,
):
    lines = cycle_size // 4
    span = min(lines - 1, (reach + 3) // 4)
    pair = q_back.shape[0]
    units_here, model = parts[0].shape
    size = units_here // cycle_size
    units = scatter_units(size)
    shaped = [part.reshape(lines, 2, 2, size, model) for part in parts]
    n = len(units)
    heads = plan.heads
    padded = rows + 2 * PAD
    hbm = pl.BlockSpec(memory_space=pl.ANY)
    dma = pltpu.SemaphoreType.DMA
    return pl.pallas_call(
        functools.partial(backward_kernel, plan, lines, span, reach, doc_most, rows, pair),
        out_shape=[
            jax.ShapeDtypeStruct((pair, WIDE), bf16),
            jax.ShapeDtypeStruct((heads, 32, 128), f32),
            jax.ShapeDtypeStruct((pair, WIDE), bf16),
            jax.ShapeDtypeStruct((pair, WIDE), bf16),
            jax.ShapeDtypeStruct((pair // TQ, 8, TQ), f32),
        ]
        + [jax.ShapeDtypeStruct((size, model), f32)] * 3
        + [
            jax.ShapeDtypeStruct(branch.shape, bf16),
            jax.ShapeDtypeStruct(branch.shape, bf16),
            jax.ShapeDtypeStruct((lines, 2, 2, pair, WIDE), bf16),
        ],
        in_specs=[smem] + [vmem] * 4 + [hbm] * 10,
        out_specs=[vmem] * 8 + [hbm] * 3,
        scratch_shapes=[
            pltpu.VMEM((3, lines, 2, size, model), bf16),
            pltpu.VMEM((3, lines, 2, size, model), bf16),
            pltpu.VMEM((3, lines, size, model), bf16),
            pltpu.VMEM((3, lines, size, model), bf16),
            pltpu.VMEM((3, lines, size, model), bf16),
            pltpu.VMEM((padded, WIDE), bf16),
            pltpu.VMEM((padded, WIDE), bf16),
            pltpu.VMEM((8, padded), f32),
            pltpu.VMEM((2, pair, 2 * plan.cols), bf16),
            pltpu.VMEM((2, pair, 128), bf16),
            pltpu.VMEM((heads, TQ, WIDE), bf16),
            pltpu.VMEM((heads, TQ, WIDE), bf16),
            pltpu.VMEM((heads, TQ, WIDE), f32),
            pltpu.VMEM((heads, TQ, TK), f32),
            pltpu.VMEM((heads, TQ, TK), f32),
            pltpu.VMEM((2, heads, TQ, 128), f32),
            dma((n,)),
            dma((2, n)),
            dma((2, n)),
            dma((2, n, lines)),
            dma((2, n, lines)),
            dma((6,)),
            dma((lines, 2, 2)),
            dma((4, lines)),
            dma((2,)),
            dma((2, lines)),
            dma((2, 2)),
            dma((1 + rows // pair,)),
        ],
        compiler_params=pltpu.CompilerParams(
            vmem_limit_bytes=62 * 2**20, collective_id=1, has_side_effects=True
        ),
        name="backward",
    )(
        table, q_back, do_wide, own_kv, own_aug, near_bias, aug, masks, kv_all, q_all,
        branch, ffn_far, *shaped
    )


def shards(
    tokens,
    doc_lengths,
    key_mask,
    gain_attn,
    w_query,
    w_key,
    w_value,
    w_out,
    bias_table,
    gain_ffn,
    w_gate,
    w_up,
    w_down,
    cotangent,
):
    own_rows, model = tokens.shape
    group = lax.axis_size("wa")
    cycle_size = lax.axis_size("ctx")
    pair = own_rows * group
    heads = bias_table.shape[1]
    docs = doc_lengths.shape[0]
    plan = Plan(heads, w_query.shape[1] // heads, docs)
    total_rows = pair * cycle_size
    doc_most = min(MAXLEN, total_rows // 2)
    reach = min(cycle_size - 1, (doc_most - 1) // pair + 1)
    base = lax.axis_index("ctx") * pair
    rows = min(total_rows, (2 * reach + 1) * pair)
    origin = jnp.clip(base - reach * pair, 0, total_rows - rows).astype(jnp.int32)
    table = bias_table.T

    def window(gathered):
        if rows == total_rows:
            return gathered
        return lax.dynamic_slice_in_dim(gathered, origin, rows, 0)

    gather = functools.partial(lax.all_gather, axis_name="ctx", axis=0, tiled=True)
    (
        pair_normed, pair_tokens, q_wide, own_kv, k_aug, own_aug, near_bias, masks, far_out, kv_all,
    ) = first(
        plan,
        cycle_size,
        reach,
        rows,
        doc_lengths,
        table,
        tokens,
        gain_attn,
        key_mask,
        w_query,
        w_key,
        w_value,
        w_out,
    )
    masks = masks.reshape(cycle_size, 8, pair)
    cot_late, near_bias = lax.optimization_barrier((cotangent, near_bias))
    pair_cot = lax.all_gather(cot_late, "wa", axis=0, tiled=True)
    if rows < total_rows:
        masks = lax.dynamic_slice_in_dim(masks, origin // pair, rows // pair, 0)
    kv_all = window(kv_all.reshape(total_rows, 2 * plan.cols))
    attended, mixed, q_back = attend(
        plan, cycle_size, reach, rows, doc_lengths, table, q_wide, near_bias, kv_all, k_aug, masks
    )
    q_all = window(gather(q_back))
    hidden, grad_hidden, branch, ffn_own, ffn_far, do_wide, gain_ffn_part, *stacks = middle(
        plan,
        cycle_size,
        attended,
        mixed,
        pair_tokens,
        pair_cot,
        gain_ffn,
        w_out,
        far_out,
        w_gate,
        w_up,
        w_down,
    )
    (
        grad_queries, table_part, grad_keys, grad_values, mask_part,
        grad_w_down, grad_w_gate, grad_w_up, far_branch, ffn_in, unused_gathered,
    ) = backward(
        plan,
        cycle_size,
        reach,
        doc_most,
        rows,
        table,
        k_aug,
        masks,
        q_back,
        do_wide,
        own_kv,
        own_aug,
        near_bias,
        kv_all,
        q_all,
        branch,
        ffn_far,
        stacks,
    )
    grad_w_gate, grad_w_up = (grad_w_gate.T, grad_w_up.T)
    layer_out = (hidden + ffn_own.astype(f32) + ffn_in.astype(f32)).astype(bf16)
    grad_tokens, grad_mask, weights, grad_gain_attn, grad_gain_ffn, grad_table = finish(
        plan,
        cycle_size,
        grad_queries,
        grad_keys,
        grad_values,
        attended,
        pair_normed,
        branch,
        far_branch,
        w_query.T,
        w_key.T,
        w_value.T,
        mask_part.reshape(group, 8, own_rows),
        tokens,
        gain_attn,
        grad_hidden,
        table_part,
        gain_ffn_part,
    )
    weights = weights.reshape(4, plan.cols, model).astype(f32)
    return (
        layer_out,
        grad_tokens,
        grad_mask,
        grad_gain_attn,
        weights[0].T,
        weights[1].T,
        weights[2].T,
        weights[3],
        grad_table.T,
        grad_gain_ffn,
        grad_w_gate,
        grad_w_up,
        grad_w_down,
    )


def solution(mesh):
    placed = (
        P(("ctx", "wa"), None),
        P(),
        P("ctx"),
        P(),
        P(None, "wa"),
        P(None, "wa"),
        P(None, "wa"),
        P("wa", None),
        P(None, "wa"),
        P(),
        P(None, "wa"),
        P(None, "wa"),
        P("wa", None),
        P(("ctx", "wa"), None),
    )
    return jax.shard_map(
        shards,
        mesh=mesh,
        in_specs=placed,
        out_specs=(
            P(("ctx", "wa"), None),
            P(("ctx", "wa"), None),
            P(("ctx", "wa")),
            P(),
            P(None, "wa"),
            P(None, "wa"),
            P(None, "wa"),
            P("wa", None),
            P(None, "wa"),
            P(),
            P(None, ("wa", "ctx")),
            P(None, ("wa", "ctx")),
            P(("wa", "ctx"), None),
        ),
        check_vma=False,
    )
```

```python
import functools

import jax
import jax.numpy as jnp
from jax import lax
from jax.experimental import pallas as pl
from jax.experimental.pallas import tpu as pltpu
from jax.sharding import PartitionSpec as P

MAXLEN = 8192

bucket_edges = (12, 16, 23, 32, 46, 64, 91)
neg_big = -1e30
eps = 1e-06
far_left_bucket = 15
far_right_bucket = 31
slack = 20.0
WIDE = 256
TQ = 256
TK = 512
EDGE = 128
PAD = TK + EDGE
f32 = jnp.float32
bf16 = jnp.bfloat16


def bucket_of(relative):
    distance = jnp.abs(relative)
    bucket = jnp.minimum(distance, 8) + 16 * (relative > 0).astype(jnp.int32)
    for edge in bucket_edges:
        bucket = bucket + (distance >= edge).astype(jnp.int32)
    return bucket


def norm_forward(inputs, gain):
    inv_root = lax.rsqrt(jnp.mean(inputs * inputs, axis=-1, keepdims=True) + eps)
    return (inputs * inv_root * gain, inv_root)


def norm_backward(inputs, inv_root, gain, grad_normed):
    scaled = gain * grad_normed
    cubed = inv_root * inv_root * inv_root
    grad_inputs = inv_root * scaled - inputs * cubed * jnp.mean(
        inputs * scaled, axis=-1, keepdims=True
    )
    grad_gain = jnp.sum(grad_normed * inputs * inv_root, axis=0)
    return (grad_inputs, grad_gain)


def gated(gate, upward):
    return jax.nn.gelu(gate, approximate=True) * upward


def nt(a, b):
    return lax.dot_general(a, b, (((1,), (1,)), ((), ())), preferred_element_type=f32)


def nn(a, b):
    return lax.dot_general(a, b, (((1,), (0,)), ((), ())), preferred_element_type=f32)


def split3(x):
    hi = x.astype(bf16)
    rest = x - hi.astype(f32)
    mid = rest.astype(bf16)
    return (hi, mid, (rest - mid.astype(f32)).astype(bf16))


class Plan:
    def __init__(self, heads, width, docs):
        self.heads = heads
        self.width = width
        self.bits = max(1, (docs - 1).bit_length())
        self.cols = heads * width
        self.mask_lane = self.cols
        self.doc_lane = self.cols + 1
        self.stat_lane = self.doc_lane + 2 * self.bits
        assert self.stat_lane + 3 * heads <= WIDE and self.cols + 64 == WIDE and width == 64

    def key_lanes(self, lane, h):
        own = (lane >= h * self.width) & (lane < (h + 1) * self.width)
        aug = (lane >= self.mask_lane) & (lane < self.stat_lane)
        stat = (lane >= self.stat_lane + 3 * h) & (lane < self.stat_lane + 3 * h + 3)
        return own | aug | stat

    def value_lanes(self, lane, h):
        own = (lane >= 64 + h * self.width) & (lane < 64 + (h + 1) * self.width)
        return own | ((lane >= 3 * h) & (lane < 3 * h + 3))


def lanes_of(rows, width=WIDE):
    return lax.broadcasted_iota(jnp.int32, (rows, width), 1)


def near_lanes(heads, table_ref, near_ref):
    row = lax.broadcasted_iota(jnp.int32, (EDGE, 3 * EDGE), 0)
    col = lax.broadcasted_iota(jnp.int32, (EDGE, 3 * EDGE), 1)
    relative = col - EDGE - row
    for flip in range(2):
        bucket = bucket_of(-relative if flip else relative)
        left, right = (far_left_bucket, far_right_bucket)
        if flip:
            left, right = (right, left)
        for h in range(heads):
            base = jnp.full((EDGE, 3 * EDGE), table_ref[h, 0], f32)
            for b in range(1, 32):
                base = jnp.where(bucket == b, table_ref[h, b], base)
            far_l = jnp.full((EDGE, EDGE), table_ref[h, left], f32)
            far_r = jnp.full((EDGE, EDGE), table_ref[h, right], f32)
            near_ref[flip, h, :EDGE, : 3 * EDGE] = base
            near_ref[flip, h, :EDGE, 3 * EDGE :] = far_r
            near_ref[flip, h, EDGE:, EDGE:] = base
            near_ref[flip, h, EDGE:, :EDGE] = far_l


def far_span(start, n, n_left, left_bucket, right_bucket):
    on_left = n < n_left
    at = start + PAD - EDGE + TK * jnp.where(on_left, -1 - n, 1 + n - n_left)
    bucket = jnp.where(on_left, left_bucket, right_bucket)
    return pl.ds(pl.multiple_of(at, 128), TK), bucket


def pad_lanes(plan):
    lane = lanes_of(1)
    return (lane >= plan.doc_lane) & (lane < plan.stat_lane)


def far_pair(start, n, n_left, count, left, right):
    pair_of = []
    for i in range(2):
        part, bucket = far_span(start, 2 * n + i, n_left, left, right)
        at = jnp.where(2 * n + i < count, part.start, 0)
        pair_of.append((pl.ds(pl.multiple_of(at, 128), TK), bucket))
    return pair_of


def fwd_kernel(
    plan, lines, reach, rows, pair, lengths, table_ref, q_ref, near_hbm, g_hbm, aug_hbm, masks_hbm,
    low_ref, wide_ref, qb_ref,
    km, vm, mask_row, g_buf, aug_buf, near_ref, acc, extra, row_max, qh_ref, g_sem, near_sem,
):
    base = lax.axis_index("ctx") * pair
    origin = jnp.clip(base - reach * pair, 0, 4 * lines * pair - rows)
    blocks = rows // pair
    tiles = pair // TQ
    near_copy = pltpu.make_async_copy(near_hbm.at[0], near_ref, near_sem.at[0])
    near_copy.start()

    def document(position):
        def look(e, carry):
            begin, low, high = carry
            end = begin + lengths[e]
            inside = (begin <= position) & (position < end)
            return (end, jnp.where(inside, begin, low), jnp.where(inside, end, high))

        zero = jnp.int32(0)
        return lax.fori_loop(0, lengths.shape[0], look, (zero, zero, zero))[1:]

    def extent(t):
        first = base + t * TQ
        low = document(first)[0]
        high = document(first + TQ - 1)[1]
        n_left = jnp.maximum(0, first - EDGE - low + TK - 1) // TK
        n_right = jnp.maximum(0, high - (first - EDGE + TK) + TK - 1) // TK
        return low, high, n_left, n_right

    low_end = extent(0)[0] - origin
    high_end = extent(tiles - 1)[1] - origin
    from_block = jnp.maximum(0, low_end - TK) // pair
    to_block = jnp.minimum(blocks, (high_end + TK + pair - 1) // pair)

    def loads(n):
        at = pl.ds(pl.multiple_of(n * pair, pair), pair)
        to = pl.ds(pl.multiple_of(PAD + n * pair, 128), pair)
        slot = n % 2
        return (
            pltpu.make_async_copy(g_hbm.at[at], g_buf.at[slot], g_sem.at[0, slot]),
            pltpu.make_async_copy(aug_hbm.at[at], aug_buf.at[slot], g_sem.at[1, slot]),
            pltpu.make_async_copy(masks_hbm.at[n], mask_row.at[:, to], g_sem.at[2, slot]),
        )

    for copy in loads(from_block):
        copy.start()
    mask_row[:, :PAD] = jnp.zeros((8, PAD), f32)
    mask_row[:, PAD + rows :] = jnp.zeros((8, PAD), f32)
    km[:PAD, :] = jnp.broadcast_to(
        jnp.where(pad_lanes(plan), neg_big, 0.0).astype(bf16), (PAD, WIDE)
    )
    km[PAD + rows :, :] = km[:PAD, :]
    vm[:PAD, :] = jnp.zeros((PAD, WIDE), bf16)
    vm[PAD + rows :, :] = jnp.zeros((PAD, WIDE), bf16)
    low_lanes = lanes_of(pair, 128) < 64
    ones = (lanes_of(pair, 128) < 3 * plan.heads).astype(bf16)

    def build(n, unused):
        for copy in loads(n):
            copy.wait()

        @pl.when(n + 1 < to_block)
        def _():
            for copy in loads(n + 1):
                copy.start()

        to = pl.ds(pl.multiple_of(PAD + n * pair, 128), pair)
        middle = g_buf[n % 2, :, 128:256]
        km[to, 0:128] = g_buf[n % 2, :, 0:128]
        km[to, 128:256] = jnp.where(low_lanes, middle, aug_buf[n % 2])
        vm[to, 0:128] = jnp.where(low_lanes, ones, middle)
        vm[to, 128:256] = g_buf[n % 2, :, 256:384]
        return unused

    lax.fori_loop(from_block, to_block, build, 0)
    near_copy.wait()
    lane = lanes_of(TQ)

    def tile(t, unused):
        start = base - origin + t * TQ
        low_doc, high_doc, n_left, n_right = extent(t)
        count = n_left + n_right
        out = pl.ds(pl.multiple_of(t * TQ, TQ), TQ)
        q = q_ref[out, :]
        near = pl.ds(pl.multiple_of(start + PAD - EDGE, 128), TK)
        for h in range(plan.heads):
            qh = jnp.where(plan.key_lanes(lane, h), q, jnp.zeros_like(q))
            qh_ref[h] = qh
            s = nt(qh, km[near, :]) + near_ref[h] + mask_row[0:1, near]
            top = jnp.max(s, axis=1, keepdims=True)
            p = jnp.exp(s - top).astype(bf16)
            acc[h] = nn(p, vm[near, :])
            row_max[h] = jnp.broadcast_to(top, (TQ, 128))

        def far(n, unused):
            parts = far_pair(start, n, n_left, count, far_left_bucket, far_right_bucket)

            def scores_of(h):
                return [
                    (nt(qh_ref[h], km[part, :]) + (mask_row[0:1, part] + table_ref[h, bucket]), part)
                    for part, bucket in parts
                ]

            worst = jnp.full((TQ, 128), -slack, f32)
            for h in range(plan.heads):
                top = row_max[h]
                more = jnp.zeros((TQ, WIDE), f32)
                for s, part in scores_of(h):
                    tiles_of = []
                    for c in range(0, TK, 128):
                        over = s[:, c : c + 128] - top
                        worst = jnp.maximum(worst, over)
                        tiles_of.append(jnp.exp(over).astype(bf16))
                    more = more + nn(jnp.concatenate(tiles_of, axis=1), vm[part, :])
                extra[h] = more
            passed = jnp.max(worst) > slack

            @pl.when(jnp.logical_not(passed))
            def _():
                for h in range(plan.heads):
                    acc[h] += extra[h]

            @pl.when(passed)
            def _():
                for h in range(plan.heads):
                    scores = scores_of(h)
                    old = row_max[h][:, :1]
                    top = old
                    for s, part in scores:
                        top = jnp.maximum(top, jnp.max(s, axis=1, keepdims=True))
                    more = [nn(jnp.exp(s - top).astype(bf16), vm[part, :]) for s, part in scores]
                    acc[h] = acc[h] * jnp.exp(old - top) + (more[0] + more[1])
                    row_max[h] = jnp.broadcast_to(top, (TQ, 128))

            return unused

        lax.fori_loop(0, (count + 1) // 2, far, 0)
        wide = jnp.zeros((TQ, WIDE), f32)
        qb = jnp.where(lane < plan.stat_lane, q, jnp.zeros_like(q))
        for h in range(plan.heads):
            total = acc[h][:, 3 * h : 3 * h + 1]
            log_total = row_max[h][:, :1] + jnp.log(total)
            wide = jnp.where(lane // 64 == h + 1, acc[h] / total, wide)
            for i, part in enumerate(split3(-log_total)):
                qb = jnp.where(lane == plan.stat_lane + 3 * h + i, part, qb)
        wide_ref[out, :] = wide
        low_ref[out, :] = wide.astype(bf16)
        qb_ref[out, :] = qb
        return unused

    lax.fori_loop(0, tiles, tile, 0)


def attend(plan, cycle_size, reach, rows, lengths, table, q_wide, near_bias, kv_all, aug, masks):
    pair = q_wide.shape[0]
    heads = plan.heads
    padded = rows + 2 * PAD
    hbm = pl.BlockSpec(memory_space=pl.ANY)
    return pl.pallas_call(
        functools.partial(fwd_kernel, plan, cycle_size // 4, reach, rows, pair),
        out_shape=(
            jax.ShapeDtypeStruct((pair, WIDE), bf16),
            jax.ShapeDtypeStruct((pair, WIDE), f32),
            jax.ShapeDtypeStruct((pair, WIDE), bf16),
        ),
        in_specs=[smem, smem, vmem] + [hbm] * 4,
        out_specs=(vmem, vmem, vmem),
        scratch_shapes=[
            pltpu.VMEM((padded, WIDE), bf16),
            pltpu.VMEM((padded, WIDE), bf16),
            pltpu.VMEM((8, padded), f32),
            pltpu.VMEM((2, pair, 2 * plan.cols), bf16),
            pltpu.VMEM((2, pair, 128), bf16),
            pltpu.VMEM((heads, TQ, TK), f32),
            pltpu.VMEM((heads, TQ, WIDE), f32),
            pltpu.VMEM((heads, TQ, WIDE), f32),
            pltpu.VMEM((heads, TQ, 128), f32),
            pltpu.VMEM((heads, TQ, WIDE), bf16),
            pltpu.SemaphoreType.DMA((3, 2)),
            pltpu.SemaphoreType.DMA((1,)),
        ],
        compiler_params=params(),
        name="attention_forward",
    )(lengths, table, q_wide, near_bias, kv_all, aug, masks)


vmem = pl.BlockSpec(memory_space=pltpu.VMEM)
smem = pl.BlockSpec(memory_space=pltpu.SMEM)


def params():
    return pltpu.CompilerParams(vmem_limit_bytes=56 * 2**20)


class Spot:
    def __init__(self, lines):
        index = lax.axis_index("ctx")
        self.wa = lax.axis_index("wa")
        self.index = index
        self.lines = lines
        self.z = index // 4
        self.x = (index // 2) % 2
        self.core = index % 2

    def core_mate(self):
        return (self.index + 1 - 2 * self.core, self.wa)

    def x_mate(self):
        return (self.index + 2 - 4 * self.x, self.wa)

    def z_mate(self, step):
        return (jnp.clip(self.index + 4 * step, 0, 4 * self.lines - 1), self.wa)

    def y_mate(self):
        return (self.index, 1 - self.wa)


def send(src, dst, send_sem, recv_sem, device):
    return pltpu.make_async_remote_copy(
        src_ref=src,
        dst_ref=dst,
        send_sem=send_sem,
        recv_sem=recv_sem,
        device_id=device,
        device_id_type=pl.DeviceIdType.MESH,
    )


def greet(spot, with_y):
    barrier = pltpu.get_barrier_semaphore()
    mates = [spot.core_mate(), spot.x_mate()] + ([spot.y_mate()] if with_y else [])
    for mate in mates:
        pl.semaphore_signal(barrier, inc=1, device_id=mate, device_id_type=pl.DeviceIdType.MESH)

    @pl.when(spot.z + 1 < spot.lines)
    def _():
        pl.semaphore_signal(
            barrier, inc=1, device_id=spot.z_mate(1), device_id_type=pl.DeviceIdType.MESH
        )

    @pl.when(spot.z > 0)
    def _():
        pl.semaphore_signal(
            barrier, inc=1, device_id=spot.z_mate(-1), device_id_type=pl.DeviceIdType.MESH
        )

    above = (spot.z + 1 < spot.lines).astype(jnp.int32)
    below = (spot.z > 0).astype(jnp.int32)
    pl.semaphore_wait(barrier, len(mates) + above + below)


def added(a, b):
    return a + b


def first_kernel(
    plan, lines, span, reach, rows, lengths, table_ref, tokens_ref, gain_ref, key_mask_ref,
    wq_hbm, wk_hbm, wv_hbm, cot_hbm,
    x_ref, tok_ref, q_ref, own_ref, aug_ref, own_aug_ref, near_ref, masks_ref, cot_pair_hbm, all_hbm,
    weights, zeros, mask_ref, load_sem, y_sem, own_sem, zero_sem, z_sem, x_sem, c_sem,
):
    spot = Spot(lines)
    z, x, core, wa = (spot.z, spot.x, spot.core, spot.wa)
    half, model = tokens_ref.shape
    cols = plan.cols
    chunk = half // 4
    loads = [
        pltpu.make_async_copy(src, weights.at[pl.ds(i * cols, cols)], load_sem.at[i])
        for i, src in enumerate((wk_hbm, wv_hbm, wq_hbm))
    ]
    for load in loads:
        load.start()
    mask_ref[...] = jnp.broadcast_to(key_mask_ref[...].astype(f32)[None, :], mask_ref.shape)
    greet(spot, True)
    zeros[...] = jnp.zeros_like(zeros)

    def outside(d):
        return (d < z - span) | (d > z + span)

    def zero_copies(d):
        return [
            pltpu.make_async_copy(zeros, all_hbm.at[d, a, b], zero_sem.at[d, a, b])
            for a in range(2)
            for b in range(2)
        ]

    def zero_start(d, unused):
        @pl.when(outside(d))
        def _():
            masks_ref[d] = jnp.zeros((2, 2) + mask_ref.shape, f32)
            for copy in zero_copies(d):
                copy.start()

        return unused

    def rows_at(start, size):
        return pl.ds(pl.multiple_of(start, size), size)

    ours = wa * half
    theirs = (1 - wa) * half

    def y_copy(i, base):
        return send(
            tokens_ref.at[rows_at(i * chunk, chunk)],
            tok_ref.at[rows_at(base + i * chunk, chunk)],
            y_sem.at[0, i],
            y_sem.at[1, i],
            spot.y_mate(),
        )

    def y_start(i, unused):
        y_copy(i, ours).start()
        return unused

    lax.fori_loop(0, 4, y_start, 0)
    far_copy = send(
        cot_hbm,
        cot_pair_hbm.at[rows_at(ours, half)],
        y_sem.at[0, 4],
        y_sem.at[1, 4],
        spot.y_mate(),
    )
    near_copy = pltpu.make_async_copy(
        cot_hbm, cot_pair_hbm.at[rows_at(ours, half)], load_sem.at[3]
    )
    near_copy.start()

    def scaled(rows_in):
        rows_in = rows_in.astype(f32)
        inv = lax.rsqrt(jnp.mean(rows_in * rows_in, axis=-1, keepdims=True) + eps)
        return (rows_in * inv * gain_ref[...][None, :]).astype(bf16)

    def normal(i, unused):
        at = rows_at(ours + i * chunk, chunk)
        rows_in = tokens_ref[rows_at(i * chunk, chunk), :]
        tok_ref[at, :] = rows_in
        x_ref[at, :] = scaled(rows_in)
        return unused

    lax.fori_loop(0, 4, normal, 0)
    for load in loads:
        load.wait()

    def project(base, size):
        rows = rows_at(base, size)
        qkv = nt(x_ref[rows, :], weights[...]).astype(bf16)
        own_ref[rows, :] = qkv[:, : 2 * cols]
        q_ref[rows, :cols] = qkv[:, 2 * cols :]

    pieces = [
        (ours, half, True),
        (theirs + half // 2, half // 2, True),
        (theirs, half // 2, False),
        None,
    ]
    mask_piece = 3

    def line_first(p):
        return p == mask_piece or pieces[p][2]

    def piece_rows(p):
        return rows_at(pieces[p][0], pieces[p][1])

    def source(p, d, a):
        if p == mask_piece:
            return masks_ref.at[d, a, core]
        return all_hbm.at[d, a, core, piece_rows(p)]

    def own_source(p):
        return mask_ref if p == mask_piece else own_ref.at[piece_rows(p)]

    def pass_copy(p, step, d, own):
        i = 0 if step > 0 else 1
        if line_first(p):
            dst = source(p, d, x)
            src = own_source(p) if own else dst
        else:
            dst = all_hbm.at[d, :, core, piece_rows(p)]
            src = dst
        return send(src, dst, z_sem.at[p, i, d], z_sem.at[p, 2 + i, d], spot.z_mate(step))

    def across(p, d, own):
        dst = source(p, d, x)
        src = own_source(p) if own else dst
        return send(src, dst, x_sem.at[p, 0, d], x_sem.at[p, 1, d], spot.x_mate())

    def beside(p, d):
        if p == mask_piece:
            part = masks_ref.at[d, :, core]
        else:
            part = all_hbm.at[d, :, core, piece_rows(p)]
        return send(part, part, c_sem.at[p, 0, d], c_sem.at[p, 1, d], spot.core_mate())

    def own_copy(p):
        return pltpu.make_async_copy(
            own_source(p), source(p, z, x), own_sem.at[p]
        )

    def both_ways(p, own):
        @pl.when(z + 1 < lines)
        def _():
            pass_copy(p, 1, z, own).start()

        @pl.when(z > 0)
        def _():
            pass_copy(p, -1, z, own).start()

    def begin(p):
        own_copy(p).start()
        across(p, z, True).start()
        if line_first(p):
            both_ways(p, True)

    def level(p, k):
        @pl.when(z - k >= 0)
        def _():
            d = jnp.maximum(z - k, 0)
            pass_copy(p, 1, d, False).wait_recv()
            if k < span:

                @pl.when(z + 1 < lines)
                def _():
                    pass_copy(p, 1, d, False).start()

            if line_first(p):
                across(p, d, False).start()
            else:
                beside(p, d).start()

        @pl.when(z + k < lines)
        def _():
            d = jnp.minimum(z + k, lines - 1)
            pass_copy(p, -1, d, False).wait_recv()
            if k < span:

                @pl.when(z > 0)
                def _():
                    pass_copy(p, -1, d, False).start()

            if line_first(p):
                across(p, d, False).start()
            else:
                beside(p, d).start()

    def turn(p):
        across(p, z, True).wait()
        own_copy(p).wait()
        both_ways(p, False)
        beside(p, z).start()

    def settle(p, k):
        for sign in (1, -1) if k else (1,):
            d = z - sign * k

            @pl.when((d >= 0) & (d < lines))
            def _(d=d):
                d = jnp.clip(d, 0, lines - 1)
                across(p, d, k == 0).wait()
                if k == 0:
                    own_copy(p).wait()
                beside(p, d).start()

    def doc_of(start, size):
        position = start + lax.broadcasted_iota(jnp.int32, (size, 128), 0)

        def count(e, carry):
            begin, total = carry
            begin = begin + lengths[e]
            return (begin, total + (position >= begin).astype(jnp.int32))

        zero = (jnp.int32(0), jnp.zeros((size, 128), jnp.int32))
        return lax.fori_loop(0, lengths.shape[0] - 1, count, zero)[1]

    def code_lanes(start, size):
        lane = lanes_of(size, 128) + 128
        code = jnp.maximum(lane - plan.doc_lane, 0)
        bit = jnp.bitwise_and(jnp.right_shift(doc_of(start, size), code // 2), 1)
        coded = (lane >= plan.doc_lane) & (lane < plan.stat_lane)
        ones = (lane >= plan.stat_lane) & (lane < plan.stat_lane + 3 * plan.heads)
        return lane, coded, bit != code % 2, ones

    pair = 2 * half
    base = spot.index * pair
    origin = jnp.clip(base - reach * pair, 0, 4 * lines * pair - rows)

    def key_lanes(n, unused):
        at = rows_at(n * half, half)
        lane, coded, differs, ones = code_lanes(origin + n * half, half)
        aug_ref[at, :] = jnp.where(
            coded & differs, neg_big, jnp.where(ones, 1.0, 0.0)
        ).astype(bf16)
        return unused

    def own_lanes(n, unused):
        at = rows_at(n * half, half)
        lane, coded, differs, ones = code_lanes(base + n * half, half)
        column = jnp.transpose(
            jnp.broadcast_to(mask_ref[0:1, at], (128, half))
        )
        own_aug_ref[at, :] = jnp.where(
            lane == plan.mask_lane,
            column,
            jnp.where(coded & differs, neg_big, jnp.where(ones, 1.0, 0.0)),
        ).astype(bf16)
        tail = jnp.where(
            (lane == plan.mask_lane) | (coded & ~differs), 1.0, 0.0
        ).astype(bf16)
        q_ref[at, 128:] = tail
        return unused

    begin(mask_piece)
    lax.fori_loop(0, 2, own_lanes, 0)
    project(ours, half)
    begin(0)
    lax.fori_loop(0, lines, zero_start, 0)
    near_lanes(plan.heads, table_ref, near_ref)
    lax.fori_loop(0, rows // half, key_lanes, 0)

    def y_wait(i, unused):
        y_copy(i, theirs).wait_recv()
        at = rows_at(theirs + i * chunk, chunk)
        x_ref[at, :] = scaled(tok_ref[at, :])
        return unused

    lax.fori_loop(0, 2, y_wait, 0)
    project(theirs, half // 2)
    begin(2)
    level(0, 1)
    level(mask_piece, 1)
    lax.fori_loop(2, 4, y_wait, 0)
    far_copy.start()
    project(theirs + half // 2, half // 2)
    begin(1)
    if span > 1:
        level(0, 2)
        level(mask_piece, 2)
    settle(0, 0)
    settle(mask_piece, 0)
    turn(2)
    level(1, 1)
    settle(0, 1)
    settle(mask_piece, 1)
    level(2, 1)
    if span > 1:
        level(1, 2)
        settle(0, 2)
        settle(mask_piece, 2)
    settle(1, 0)
    settle(1, 1)
    if span > 1:
        level(2, 2)
        settle(1, 2)
    for k in range(3, span + 1):
        for p in range(4):
            level(p, k)
        for p in (0, 1, mask_piece):
            settle(p, k)

    def finish_line(d, unused):
        @pl.when(~outside(d))
        def _():
            for p in range(4):
                beside(p, d).wait()

        @pl.when(outside(d))
        def _():
            for copy in zero_copies(d):
                copy.wait()

        for p in range(4):

            @pl.when((z + 1 < lines) & (d <= z) & (d > z - span))
            def _(p=p):
                pass_copy(p, 1, d, False).wait_send()

            @pl.when((z > 0) & (d >= z) & (d < z + span))
            def _(p=p):
                pass_copy(p, -1, d, False).wait_send()

        return unused

    lax.fori_loop(0, lines, finish_line, 0)

    def y_drain(i, unused):
        y_copy(i, ours).wait_send()
        return unused

    lax.fori_loop(0, 4, y_drain, 0)
    far_copy.wait()
    near_copy.wait()


def first(
    plan, cycle_size, reach, rows, lengths, table, tokens, gain, mask, w_query, w_key, w_value, cot
):
    lines = cycle_size // 4
    span = min(lines - 1, (reach + 3) // 4)
    half, model = tokens.shape
    pair = 2 * half
    hbm = pl.BlockSpec(memory_space=pl.ANY)
    dma = pltpu.SemaphoreType.DMA
    return pl.pallas_call(
        functools.partial(first_kernel, plan, lines, span, reach, rows),
        out_shape=[
            jax.ShapeDtypeStruct((pair, model), bf16),
            jax.ShapeDtypeStruct((pair, model), bf16),
            jax.ShapeDtypeStruct((pair, WIDE), bf16),
            jax.ShapeDtypeStruct((pair, 2 * plan.cols), bf16),
            jax.ShapeDtypeStruct((rows, 128), bf16),
            jax.ShapeDtypeStruct((pair, 128), bf16),
            jax.ShapeDtypeStruct((2, plan.heads, TQ, TK), f32),
            jax.ShapeDtypeStruct((lines, 2, 2, 8, pair), f32),
            jax.ShapeDtypeStruct((pair, model), bf16),
            jax.ShapeDtypeStruct((lines, 2, 2, pair, 2 * plan.cols), bf16),
        ],
        in_specs=[smem] * 2 + [vmem] * 3 + [hbm] * 4,
        out_specs=[vmem] * 8 + [hbm] * 2,
        scratch_shapes=[
            pltpu.VMEM((3 * plan.cols, model), bf16),
            pltpu.VMEM((pair, 2 * plan.cols), bf16),
            pltpu.VMEM((8, pair), f32),
            dma((4,)),
            dma((2, 5)),
            dma((4,)),
            dma((lines, 2, 2)),
            dma((4, 4, lines)),
            dma((4, 2, lines)),
            dma((4, 2, lines)),
        ],
        compiler_params=pltpu.CompilerParams(
            vmem_limit_bytes=56 * 2**20, collective_id=4, has_side_effects=True
        ),
        name="project_gather",
    )(lengths, table, tokens, gain, mask, w_query.T, w_key.T, w_value.T, cot)


def tn(a, b):
    return lax.dot_general(a, b, (((0,), (0,)), ((), ())), preferred_element_type=f32)


def line_relay(spot, start, receive):
    def level(k, unused):
        @pl.when(spot.z - k >= 0)
        def _():
            if_first(k, lambda: receive(1, spot.z - k))

            @pl.when(spot.z + 1 < spot.lines)
            def _():
                start(1, spot.z - k)

        @pl.when(spot.z + k < spot.lines)
        def _():
            if_first(k, lambda: receive(-1, spot.z + k))

            @pl.when(spot.z > 0)
            def _():
                start(-1, spot.z + k)

        return unused

    def if_first(k, run):
        @pl.when(k > 0)
        def _():
            run()

    return level


def finish_kernel(
    plan, lines, dq_hbm, dk_hbm, dv_hbm, att_hbm, normed_hbm, branch_hbm, far_hbm,
    wq_hbm, wk_hbm, wv_hbm, hidden_hbm, own_hbm, in_hbm,
    mask_ref, tokens_ref, gain_ref, gh_ref, table_ref, gain_part_ref,
    out_ref, turned_ref, gm_ref, weights_ref, gain_one_ref, gain_two_ref, table_out_ref,
    gt_ref, hidden_ref, ffn_own, ffn_in, w3_ref, load_sem, lefts, rights, product, mine, core_in, x_in, up_in, down_in, all_w, y_out, y_in, own_part, mask_in,
    small_own, small_y, small_core, small_x, small_all,
    y_sem, core_sem, x_sem, up_sem, down_sem, gz_sem, gx_sem, gc_sem, sz_sem,
):
    spot = Spot(lines)
    z, x, core, wa = (spot.z, spot.x, spot.core, spot.wa)
    cols = plan.cols
    half = tokens_ref.shape[0]
    our_rows = pl.ds(pl.multiple_of(wa * half, half), half)
    their_rows = pl.ds(pl.multiple_of((1 - wa) * half, half), half)
    targets = (
        (dq_hbm, lefts.at[0]),
        (normed_hbm, rights.at[0]),
        (att_hbm, lefts.at[3]),
        (branch_hbm, rights.at[1, our_rows]),
        (far_hbm, rights.at[1, their_rows]),
        (dk_hbm, lefts.at[1]),
        (dv_hbm, lefts.at[2]),
        (wq_hbm, w3_ref.at[pl.ds(0, cols)]),
        (wk_hbm, w3_ref.at[pl.ds(WIDE, cols)]),
        (wv_hbm, w3_ref.at[pl.ds(3 * WIDE - cols, cols)]),
        (hidden_hbm, hidden_ref),
        (own_hbm, ffn_own),
        (in_hbm, ffn_in),
    )
    loads = [
        pltpu.make_async_copy(src, dst, load_sem.at[i]) for i, (src, dst) in enumerate(targets)
    ]
    for load in loads:
        load.start()
    gap = jnp.zeros((WIDE - cols, tokens_ref.shape[1]), bf16)
    w3_ref[cols:WIDE] = gap
    w3_ref[WIDE + cols : 2 * WIDE] = gap
    w3_ref[2 * WIDE : 3 * WIDE - cols] = gap
    greet(spot, True)
    quarter = half // 2
    model = tokens_ref.shape[1]
    rows = mine.shape[3]

    def grad_rows(at):
        at = pl.ds(pl.multiple_of(at, quarter), quarter)
        return (
            nn(lefts[0, at, :], w3_ref[0:256])
            + nn(lefts[1, at, :], w3_ref[256:512])
            + nn(lefts[2, at, :], w3_ref[512:768])
        )

    def y_copy(i):
        return send(y_out.at[i], y_in.at[i], y_sem.at[0, i], y_sem.at[1, i], spot.y_mate())

    def theirs(i, unused):
        y_out[i] = grad_rows((1 - wa) * half + i * quarter).astype(bf16)
        y_copy(i).start()
        return unused

    for i in (0, 5, 6, 7, 8, 9):
        loads[i].wait()
    lax.fori_loop(0, 2, theirs, 0)
    mask_copy = send(
        mask_ref.at[1 - wa], mask_in, y_sem.at[0, 2], y_sem.at[1, 2], spot.y_mate()
    )
    mask_copy.start()
    for i in (1, 2, 3, 4):
        loads[i].wait()
    per = plan.cols // rows

    def core_copy(m):
        part = pl.ds(m * per // 4, per // 4)
        return send(
            mine.at[part, :, 1 - core],
            core_in.at[part],
            core_sem.at[0, m],
            core_sem.at[1, m],
            spot.core_mate(),
        )

    def fill(i, unused):
        m = (3 * i) % 4
        product[...] = tn(lefts[m], rights[m // 3]).astype(bf16)

        def place(offset):
            for j in range(per):
                mine[m * per // 4 + j // 4, (j // 2) % 2, j % 2] = product[
                    offset + j * rows : offset + (j + 1) * rows, :
                ]

        @pl.when(m < 2)
        def _():
            place(0)

        @pl.when(m >= 2)
        def _():
            place(WIDE - plan.cols)

        core_copy(m).start()
        return unused

    lax.fori_loop(0, 4, fill, 0)
    def x_copy(d):
        return send(
            mine.at[d, 1 - x, core], x_in.at[d], x_sem.at[0, d], x_sem.at[1, d], spot.x_mate()
        )

    def core_add(d, unused):
        mine[d, 1 - x, core] = added(mine[d, 1 - x, core], core_in[d, 1 - x])
        x_copy(d).start()
        return unused

    def ours(i, unused):
        own_part[pl.ds(pl.multiple_of(i * quarter, quarter), quarter), :] = grad_rows(
            wa * half + i * quarter
        )
        return unused

    def core_stage(i, unused):
        m = (3 * i) % 4
        core_copy(m).wait()
        lax.fori_loop(m * per // 4, (m + 1) * per // 4, core_add, 0)
        return unused

    lax.fori_loop(0, 4, core_stage, 0)

    def core_add_own(d, unused):
        mine[d, x, core] = added(mine[d, x, core], core_in[d, x])
        return unused

    lax.fori_loop(0, lines, core_add_own, 0)
    lax.fori_loop(0, 2, ours, 0)

    def flow(step, d):
        ring, sem = (up_in, up_sem) if step > 0 else (down_in, down_sem)
        return send(
            mine.at[d, x, core], ring.at[d], sem.at[0, d], sem.at[1, d], spot.z_mate(step)
        )

    def merge(step, d):
        flow(step, d).wait_recv()
        ring = up_in if step > 0 else down_in
        mine[d, x, core] = added(mine[d, x, core], ring[d])

    def x_add(i, unused):
        d = (i * (lines - 1)) % lines
        x_copy(d).wait()
        mine[d, x, core] = added(mine[d, x, core], x_in[d])

        @pl.when((z == 0) & (d > 0))
        def _():
            flow(1, d).start()

        @pl.when((z == lines - 1) & (d < lines - 1))
        def _():
            flow(-1, d).start()

        return unused

    lax.fori_loop(0, lines, x_add, 0)
    gain_sum = jnp.zeros((1, model), f32)
    step = 32
    for i in range(2):
        y_copy(i).wait()

        def normal(j, total, i=i):
            at = pl.ds(pl.multiple_of(i * quarter + j * step, step), step)
            there = pl.ds(pl.multiple_of(j * step, step), step)
            grad = own_part[at, :] + y_in[i, there, :].astype(f32)
            rows_in = tokens_ref[at, :].astype(f32)
            inv = lax.rsqrt(jnp.mean(rows_in * rows_in, axis=-1, keepdims=True) + eps)
            scaled = gain_ref[...][None, :] * grad
            mean = jnp.mean(rows_in * scaled, axis=-1, keepdims=True)
            gt_ref[at, :] = gh_ref[at, :] + inv * scaled - rows_in * (inv * inv * inv * mean)
            return total + jnp.sum(grad * rows_in * inv, axis=0, keepdims=True)

        gain_sum = lax.fori_loop(0, quarter // step, normal, gain_sum)
    small_own[...] = jnp.zeros_like(small_own)
    small_own[0:1, :] = gain_sum
    small_own[1:2, :] = gain_part_ref[...]
    for h in range(plan.heads):
        small_own[2:3, 32 * h : 32 * h + 32] = jnp.sum(
            jnp.transpose(table_ref[h]), axis=0, keepdims=True
        )
    small_copy = send(
        small_own, small_y, y_sem.at[0, 4], y_sem.at[1, 4], spot.y_mate()
    )
    small_copy.start()
    mask_copy.wait()
    gm_ref[...] = jnp.sum(mask_ref[wa, 0:1] + mask_in[0:1], axis=0)
    def relay(k, unused):
        high = lines - 1 - k

        @pl.when((z < high) & (z > 0))
        def _():
            merge(1, high)
            flow(1, high).start()

        @pl.when((z > k) & (z + 1 < lines))
        def _():
            merge(-1, k)
            flow(-1, k).start()

        return unused

    lax.fori_loop(0, 1, relay, 0)
    small_copy.wait()
    row = lax.broadcasted_iota(jnp.int32, small_own.shape, 0)
    small_x[0] = small_own[...] + jnp.where(row < 2, small_y[...], 0.0)
    small_core_copy = send(
        small_x.at[0], small_core, core_sem.at[0, 4], core_sem.at[1, 4], spot.core_mate()
    )
    small_core_copy.start()
    lax.fori_loop(1, lines - 1, relay, 0)
    small_core_copy.wait()
    small_x[1] = small_x[0] + small_core[...]
    small_x_copy = send(
        small_x.at[1], small_x.at[2], x_sem.at[0, lines], x_sem.at[1, lines], spot.x_mate()
    )
    small_x_copy.start()

    @pl.when(z > 0)
    def _():
        merge(1, z)

    @pl.when(z + 1 < lines)
    def _():
        merge(-1, z)

    all_w[z, x, core] = mine[z, x, core]

    def pass_w(step, d):
        i = 0 if step > 0 else 1
        return send(
            all_w.at[d, x, core], all_w.at[d, x, core], gz_sem.at[i, d], gz_sem.at[2 + i, d],
            spot.z_mate(step),
        )

    def pass_s(step, d):
        i = 0 if step > 0 else 1
        return send(
            small_all.at[d], small_all.at[d], sz_sem.at[i, d], sz_sem.at[2 + i, d],
            spot.z_mate(step),
        )

    def across(d):
        return send(
            all_w.at[d, x, core], all_w.at[d, x, core], gx_sem.at[0, d], gx_sem.at[1, d],
            spot.x_mate(),
        )

    def beside(d):
        return send(
            all_w.at[d, :, core], all_w.at[d, :, core], gc_sem.at[0, d], gc_sem.at[1, d],
            spot.core_mate(),
        )

    small_x_copy.wait()
    small_all[z] = small_x[1] + small_x[2]

    def receive(step, d):
        pass_w(step, d).wait_recv()
        across(d).start()

    across(z).start()
    def pass_both(step, d):
        pass_s(step, d).start()
        pass_w(step, d).start()

    def receive_both(step, d):
        pass_s(step, d).wait_recv()
        receive(step, d)

    lax.fori_loop(0, lines, line_relay(spot, pass_both, receive_both), 0)

    def add_small(d, total):
        return total + small_all[d]

    totals = lax.fori_loop(1, lines, add_small, small_all[0])
    gain_one_ref[...] = jnp.sum(totals[0:1], axis=0)
    gain_two_ref[...] = jnp.sum(totals[1:2], axis=0)
    for h in range(plan.heads):
        table_out_ref[h : h + 1, :] = totals[2:3, 32 * h : 32 * h + 32]
    for i in (10, 11, 12):
        loads[i].wait()
    for c in range(0, model, 128):
        end = min(model, c + 128)
        turned_ref[c:end, :] = jnp.transpose(gt_ref[:, c:end])
        total = hidden_ref[:, c:end] + ffn_own[:, c:end].astype(f32) + ffn_in[:, c:end].astype(f32)
        out_ref[c:end, :] = jnp.transpose(total).astype(bf16)

    def spread(d, unused):
        across(d).wait()
        beside(d).start()
        return unused

    lax.fori_loop(0, lines, spread, 0)

    def copy_out(d, unused):
        beside(d).wait()
        weights_ref[d] = all_w[d]
        return unused

    lax.fori_loop(0, lines, copy_out, 0)

    def drain(d, unused):
        @pl.when((z < d))
        def _():
            flow(1, d).wait_send()

        @pl.when((z > d))
        def _():
            flow(-1, d).wait_send()

        @pl.when((d <= z) & (z + 1 < lines))
        def _():
            pass_w(1, d).wait_send()
            pass_s(1, d).wait_send()

        @pl.when((d >= z) & (z > 0))
        def _():
            pass_w(-1, d).wait_send()
            pass_s(-1, d).wait_send()

        return unused

    lax.fori_loop(0, lines, drain, 0)


def finish(plan, cycle_size, *operands):
    lines = cycle_size // 4
    half, model = operands[14].shape
    rows = 4 * plan.cols // cycle_size
    dma = pltpu.SemaphoreType.DMA
    return pl.pallas_call(
        functools.partial(finish_kernel, plan, lines),
        out_shape=[
            jax.ShapeDtypeStruct((model, half), bf16),
            jax.ShapeDtypeStruct((model, half), f32),
            jax.ShapeDtypeStruct((half,), f32),
            jax.ShapeDtypeStruct((lines, 2, 2, rows, model), bf16),
            jax.ShapeDtypeStruct((model,), f32),
            jax.ShapeDtypeStruct((model,), f32),
            jax.ShapeDtypeStruct((plan.heads, 32), f32),
        ],
        in_specs=[pl.BlockSpec(memory_space=pl.ANY)] * 13 + [vmem] * 6,
        out_specs=[vmem] * 7,
        scratch_shapes=[
            pltpu.VMEM((half, model), f32),
            pltpu.VMEM((half, model), f32),
            pltpu.VMEM((half, model), bf16),
            pltpu.VMEM((half, model), bf16),
            pltpu.VMEM((3 * WIDE, model), bf16),
            dma((13,)),
            pltpu.VMEM((4, 2 * half, WIDE), bf16),
            pltpu.VMEM((2, 2 * half, model), bf16),
            pltpu.VMEM((WIDE, model), bf16),
            pltpu.VMEM((lines, 2, 2, rows, model), bf16),
            pltpu.VMEM((lines, 2, rows, model), bf16),
            pltpu.VMEM((lines, rows, model), bf16),
            pltpu.VMEM((lines, rows, model), bf16),
            pltpu.VMEM((lines, rows, model), bf16),
            pltpu.VMEM((lines, 2, 2, rows, model), bf16),
            pltpu.VMEM((2, half // 2, model), bf16),
            pltpu.VMEM((2, half // 2, model), bf16),
            pltpu.VMEM((half, model), f32),
            pltpu.VMEM((8, half), f32),
            pltpu.VMEM((8, model), f32),
            pltpu.VMEM((8, model), f32),
            pltpu.VMEM((8, model), f32),
            pltpu.VMEM((3, 8, model), f32),
            pltpu.VMEM((lines, 8, model), f32),
            dma((2, 5)),
            dma((2, 5)),
            dma((2, lines + 1)),
            dma((2, lines)),
            dma((2, lines)),
            dma((4, lines)),
            dma((2, lines)),
            dma((2, lines)),
            dma((4, lines)),
        ],
        compiler_params=pltpu.CompilerParams(
            vmem_limit_bytes=58 * 2**20, collective_id=2, has_side_effects=True
        ),
        name="finish",
    )(*operands)


root = 0.7978845608028654
cubic = 0.044715


def middle_kernel(
    plan, cycle_size, att_ref, mixed_ref, tokens_ref, cot_ref, gain_ref,
    wo_hbm, wo_pair_hbm, wg_hbm, wu_hbm, wd_hbm,
    hidden_ref, gh_ref, branch_ref, ffn_ref, ffn_far_ref, do_ref, gain_part_ref, *refs,
):
    stacks, refs = (refs[:3], refs[3:])
    (
        wg, wu, wd, wo, inner, gg, gu, x_ref, att_in, d_out, d_in, e_out, e_in,
        acc_g, rows_buf, load_sem, y_sem, out_sem,
    ) = refs
    spot = Spot(cycle_size // 4)
    wa = spot.wa
    pair, model = tokens_ref.shape
    half = pair // 2
    units = wd.shape[1]
    chunk = half // 4
    block = pair // 4
    loads = [
        pltpu.make_async_copy(src, dst, load_sem.at[i])
        for i, (src, dst) in enumerate(
            (
                (wo_hbm, wo.at[0, 64:]),
                (wo_pair_hbm.at[1 - wa], wo.at[1, 64:]),
                (wg_hbm, wg),
                (wu_hbm, wu),
                (wd_hbm, wd),
            )
        )
    ]
    for load in loads:
        load.start()
    barrier = pltpu.get_barrier_semaphore()
    pl.semaphore_signal(
        barrier, inc=1, device_id=spot.y_mate(), device_id_type=pl.DeviceIdType.MESH
    )
    wo[:, :64, :] = jnp.zeros((2, 64, model), bf16)
    pl.semaphore_wait(barrier, 1)
    ours = wa * half
    theirs = (1 - wa) * half

    def rows_at(start, size):
        return pl.ds(pl.multiple_of(start, size), size)

    def a_start(i):
        return (theirs + i * block) if i < 2 else (ours + (i - 2) * block)

    def a_copy(i, base):
        at = rows_at(base + (i % 2) * block, block)
        return send(att_ref.at[at], att_in.at[at], y_sem.at[0, i], y_sem.at[1, i], spot.y_mate())

    order = (0, 1, 2, 3)
    for i in order:
        a_copy(i, ours if i < 2 else theirs).start()
    loads[0].wait()
    loads[1].wait()

    def normal(i, base, keep):
        a_copy(i, base).wait_recv()
        at = rows_at(base + (i % 2) * block, block)
        branch = nn(att_ref[at, :], wo[0]) + nn(att_in[at, :], wo[1])
        hidden = tokens_ref[at, :].astype(f32) + branch
        if keep:
            hidden_ref[(i % 2) * block : (i % 2 + 1) * block, :] = hidden
        inv = lax.rsqrt(jnp.mean(hidden * hidden, axis=-1, keepdims=True) + eps)
        x_ref[at, :] = (hidden * inv * gain_ref[...][None, :]).astype(bf16)

    normal(0, theirs, False)
    normal(1, theirs, False)
    for load in loads[2:]:
        load.wait()
    wide = 256

    def feed(base):
        rows = rows_at(base, half)
        def tile(u, unused):
            cols = rows_at(u * wide, wide)
            gate = nn(x_ref[rows, :], wg[:, cols])
            upward = nn(x_ref[rows, :], wu[:, cols])
            grad_inner = nn(cot_ref[rows, :], wd[:, cols])
            square = gate * gate
            bend = jnp.tanh(root * gate * (1.0 + cubic * square))
            side = 0.5 * (1.0 + bend)
            gelu = gate * side
            slope = side + 0.5 * gate * (1.0 - bend * bend) * (
                root * (1.0 + 3.0 * cubic * square)
            )
            inner_low = (gelu * upward).astype(bf16)
            gate_low = (grad_inner * upward * slope).astype(bf16)
            up_low = (grad_inner * gelu).astype(bf16)
            inner[rows, cols] = inner_low
            gg[rows, cols] = gate_low
            gu[rows, cols] = up_low
            return unused

        lax.fori_loop(0, units // wide, tile, 0)

    def columns(body):
        def chunk_of(c, unused):
            body(rows_at(c * wide, wide))
            return unused

        lax.fori_loop(0, model // wide, chunk_of, 0)
        if model % wide:
            body(pl.ds(model // wide * wide, model % wide))

    def back_to_rows(base):
        rows = rows_at(base, half)

        def body(cols):
            acc_g[:, cols] = nt(gg[rows, :], wg[cols, :]) + nt(gu[rows, :], wu[cols, :])

        columns(body)

    def forward_to_rows(base, out):
        rows = rows_at(base, half)

        def body(cols):
            out[:, cols] = nt(inner[rows, :], wd[cols, :]).astype(bf16)

        columns(body)

    def d_copy(i):
        return send(
            d_out.at[i], d_in.at[i], y_sem.at[0, 4 + i], y_sem.at[1, 4 + i], spot.y_mate()
        )

    def send_grad(i, unused):
        d_out[i] = acc_g[rows_at(i * chunk, chunk), :].astype(bf16)
        d_copy(i).start()
        return unused

    def half_pass(k, unused):
        base = theirs + k * (ours - theirs)
        feed(base)
        back_to_rows(base)

        @pl.when(k == 0)
        def _():
            lax.fori_loop(0, 4, send_grad, 0)
            normal(2, ours, True)
            normal(3, ours, True)

        return unused

    lax.fori_loop(0, 2, half_pass, 0)
    forward_to_rows(theirs, ffn_far_ref)
    forward_to_rows(ours, ffn_ref)
    count = units // wide

    def out_copy(m, u):
        return pltpu.make_async_copy(
            rows_buf.at[m, u % 2],
            stacks[m].at[rows_at(u * wide, wide)],
            out_sem.at[m, u % 2],
        )

    for m in range(3):
        left = (inner, gg, gu)[m]
        right = (cot_ref, x_ref, x_ref)[m]

        def weight_rows(u, unused, m=m, left=left, right=right):
            @pl.when(u >= 2)
            def _():
                out_copy(m, u - 2).wait()

            turned = jnp.transpose(left[:, rows_at(u * wide, wide)])
            rows_buf[m, u % 2] = nn(turned, right[...]).astype(bf16)
            out_copy(m, u).start()
            return unused

        lax.fori_loop(0, count, weight_rows, 0)

    def e_copy(i):
        return send(
            e_out.at[i], e_in.at[i], y_sem.at[0, 8 + i], y_sem.at[1, 8 + i], spot.y_mate()
        )

    def normal_back(i, total):
        d_copy(i).wait()
        at = rows_at(i * chunk, chunk)
        grad = acc_g[at, :] + d_in[i].astype(f32)
        hidden = hidden_ref[at, :]
        inv = lax.rsqrt(jnp.mean(hidden * hidden, axis=-1, keepdims=True) + eps)
        scaled = gain_ref[...][None, :] * grad
        mean = jnp.mean(hidden * scaled, axis=-1, keepdims=True)
        grad_hidden = (
            cot_ref[rows_at(ours + i * chunk, chunk), :].astype(f32)
            + inv * scaled
            - hidden * (inv * inv * inv * mean)
        )
        gh_ref[at, :] = grad_hidden
        low = grad_hidden.astype(bf16)
        branch_ref[at, :] = low
        e_out[i] = nt(low, wo[1]).astype(bf16)
        e_copy(i).start()
        do_ref[rows_at(ours + i * chunk, chunk), :] = nt(low, wo[0]).astype(bf16)
        return total + jnp.sum(grad * hidden * inv, axis=0, keepdims=True)

    gain_part_ref[...] = lax.fori_loop(0, 4, normal_back, jnp.zeros((1, model), f32))

    def row_terms(at, grad):
        lane = lanes_of(chunk)
        terms = grad.astype(f32) * mixed_ref[at, :]
        out = grad
        for h in range(plan.heads):
            row_term = jnp.sum(
                jnp.where(lane // 64 == h + 1, terms, 0.0), axis=1, keepdims=True
            )
            for i, part in enumerate(split3(-row_term)):
                out = jnp.where(lane == 3 * h + i, part, out)
        do_ref[at, :] = out

    def own_terms(i, unused):
        at = rows_at(ours + i * chunk, chunk)
        row_terms(at, do_ref[at, :])
        return unused

    lax.fori_loop(0, 4, own_terms, 0)

    def far_terms(i, unused):
        e_copy(i).wait()
        row_terms(rows_at(theirs + i * chunk, chunk), e_in[i])
        return unused

    lax.fori_loop(0, 4, far_terms, 0)
    for m in range(3):
        for u in range(max(0, count - 2), count):
            out_copy(m, u).wait()
    for i in order:
        a_copy(i, ours if i < 2 else theirs).wait_send()


def middle(
    plan, cycle_size, attended, mixed, tokens, cot, gain, w_out, w_out_pair, w_gate, w_up, w_down
):
    pair, model = tokens.shape
    half = pair // 2
    units = w_down.shape[0]
    chunk = half // 4
    hbm = pl.BlockSpec(memory_space=pl.ANY)
    dma = pltpu.SemaphoreType.DMA
    return pl.pallas_call(
        functools.partial(middle_kernel, plan, cycle_size),
        out_shape=[
            jax.ShapeDtypeStruct((half, model), f32),
            jax.ShapeDtypeStruct((half, model), f32),
            jax.ShapeDtypeStruct((half, model), bf16),
            jax.ShapeDtypeStruct((half, model), bf16),
            jax.ShapeDtypeStruct((half, model), bf16),
            jax.ShapeDtypeStruct((pair, WIDE), bf16),
            jax.ShapeDtypeStruct((1, model), f32),
        ]
        + [jax.ShapeDtypeStruct((units, model), bf16)] * 3,
        in_specs=[vmem] * 5 + [hbm] * 5,
        out_specs=[vmem] * 7 + [hbm] * 3,
        scratch_shapes=[
            pltpu.VMEM((model, units), bf16),
            pltpu.VMEM((model, units), bf16),
            pltpu.VMEM((model, units), bf16),
            pltpu.VMEM((2, WIDE, model), bf16),
            pltpu.VMEM((pair, units), bf16),
            pltpu.VMEM((pair, units), bf16),
            pltpu.VMEM((pair, units), bf16),
            pltpu.VMEM((pair, model), bf16),
            pltpu.VMEM((pair, WIDE), bf16),
            pltpu.VMEM((4, chunk, model), bf16),
            pltpu.VMEM((4, chunk, model), bf16),
            pltpu.VMEM((4, chunk, WIDE), bf16),
            pltpu.VMEM((4, chunk, WIDE), bf16),
            pltpu.VMEM((half, model), f32),
            pltpu.VMEM((3, 2, WIDE, model), bf16),
            dma((5,)),
            dma((2, 12)),
            dma((3, 2)),
        ],
        compiler_params=pltpu.CompilerParams(
            vmem_limit_bytes=60 * 2**20, collective_id=3, has_side_effects=True
        ),
        name="feed_forward",
    )(attended, mixed, tokens, cot, gain, w_out, w_out_pair, w_gate, w_up, w_down.T)


class Scatter:
    def __init__(self, spot, units, parts, outs, buffers, sems):
        self.spot = spot
        self.units = units
        self.parts = parts
        self.outs = outs
        self.mine, self.core_in, self.x_in, self.up_in, self.down_in = buffers
        self.load_sem, self.core_sem, self.x_sem, self.up_sem, self.down_sem = sems

    def rows_of(self, u):
        return pl.ds(self.units[u][1], self.units[u][2])

    def load(self, u):
        m = self.units[u][0]
        return pltpu.make_async_copy(
            self.parts[m].at[:, :, self.spot.core, self.rows_of(u)],
            self.mine.at[m, :, :, self.rows_of(u)],
            self.load_sem.at[u],
        )

    def core_copy(self, u):
        m = self.units[u][0]
        return send(
            self.parts[m].at[:, :, 1 - self.spot.core, self.rows_of(u)],
            self.core_in.at[m, :, :, self.rows_of(u)],
            self.core_sem.at[0, u],
            self.core_sem.at[1, u],
            self.spot.core_mate(),
        )

    def x_copy(self, u):
        m = self.units[u][0]
        x = self.spot.x
        src = self.mine.at[m, :, 1 - x, self.rows_of(u)]
        dst = self.x_in.at[m, :, self.rows_of(u)]
        return send(src, dst, self.x_sem.at[0, u], self.x_sem.at[1, u], self.spot.x_mate())

    def begin(self, u):
        self.load(u).start()
        self.core_copy(u).start()

    def core_stage(self, u):
        m = self.units[u][0]
        x = self.spot.x
        self.load(u).wait()
        self.core_copy(u).wait()

        def add(slot):
            def body(line, unused):
                at = (m, line, slot, self.rows_of(u))
                self.mine[at] = added(self.mine[at], self.core_in[at])
                return unused

            lax.fori_loop(0, self.spot.lines, body, 0)

        add(1 - x)
        self.x_copy(u).start()
        add(x)

    def x_stage(self, u):
        m = self.units[u][0]
        x = self.spot.x
        self.x_copy(u).wait()

        def body(line, unused):
            at = (m, line, x, self.rows_of(u))
            self.mine[at] = added(self.mine[at], self.x_in[m, line, self.rows_of(u)])
            return unused

        lax.fori_loop(0, self.spot.lines, body, 0)
        self.ends(u)

    def copy(self, u, step, d):
        m = self.units[u][0]
        sem = self.up_sem if step > 0 else self.down_sem
        ring = self.up_in if step > 0 else self.down_in
        return send(
            self.mine.at[m, d, self.spot.x, self.rows_of(u)],
            ring.at[m, d, self.rows_of(u)],
            sem.at[0, u, d],
            sem.at[1, u, d],
            self.spot.z_mate(step),
        )

    def receive(self, u, step, d):
        m = self.units[u][0]
        self.copy(u, step, d).wait_recv()
        ring = self.up_in if step > 0 else self.down_in
        at = (m, d, self.spot.x, self.rows_of(u))
        self.mine[at] = added(self.mine[at], ring[m, d, self.rows_of(u)])

    def start(self, u, step, d):
        self.copy(u, step, d).start()

    def ends(self, u):
        z, lines = (self.spot.z, self.spot.lines)

        @pl.when(z == 0)
        def _():
            def up(k, unused):
                self.start(u, 1, lines - 1 - k)
                return unused

            lax.fori_loop(0, lines - 1, up, 0)

        @pl.when(z == lines - 1)
        def _():
            def down(k, unused):
                self.start(u, -1, k)
                return unused

            lax.fori_loop(0, lines - 1, down, 0)

    def relay(self, u, lag):
        z, lines = (self.spot.z, self.spot.lines)
        top = lines - 2 if lag == 2 else lag

        @pl.when((z >= lag) & (z <= top))
        def _():
            def up(k, unused):
                self.receive(u, 1, lines - 1 - k)
                self.start(u, 1, lines - 1 - k)
                return unused

            lax.fori_loop(0, lines - 1 - z, up, 0)

        @pl.when((lines - 1 - z >= lag) & (lines - 1 - z <= top))
        def _():
            def down(k, unused):
                self.receive(u, -1, k)
                self.start(u, -1, k)
                return unused

            lax.fori_loop(0, z, down, 0)

    def settle(self, u):
        z, lines = (self.spot.z, self.spot.lines)

        @pl.when(z > 0)
        def _():
            self.receive(u, 1, z)

        @pl.when(z + 1 < lines)
        def _():
            self.receive(u, -1, z)

        self.store(u)

    def store(self, u):
        m = self.units[u][0]
        self.outs[m][self.rows_of(u), :] = self.mine[
            m, self.spot.z, self.spot.x, self.rows_of(u)
        ]

    def drain(self, u):
        z, lines = (self.spot.z, self.spot.lines)

        def body(k, unused):
            @pl.when(z < lines - 1 - k)
            def _():
                self.copy(u, 1, lines - 1 - k).wait_send()

            @pl.when(z > k)
            def _():
                self.copy(u, -1, k).wait_send()

            return unused

        lax.fori_loop(0, lines - 1, body, 0)


def scatter_units(rows):
    if rows % 16 or rows < 112:
        return [(m, 0, rows) for m in range(3)]
    tail = rows - 64
    return [
        (0, 0, 64), (1, 0, 64), (2, 0, 64), (0, 64, tail), (1, 64, tail), (2, 64, tail - 16),
        (2, rows - 16, 16),
    ]


def backward_kernel(
    plan, lines, span, reach, doc_most, rows, pair, table_ref, qb_ref, do_ref,
    own_kv, own_aug, near_hbm, aug_hbm, masks_hbm, g_hbm, qall_hbm, branch_hbm, ffn_hbm, p0, p1, p2,
    dq_ref, tab_ref, dk_ref, dv_ref, mask_ref, o0, o1, o2, far_hbm, ffn_in_hbm, all_do,
    mine, core_in, x_in, up_in, down_in,
    km, vm, mask_row, g_buf, aug_buf, qh_ref, doh_ref, acc, near_ref, near_acc, far_acc,
    load_sem, core_sem, rx_sem, up_sem, down_sem, own_sem, zero_sem, z_sem, x_sem, c_sem, g_sem,
    q_sem,
):
    spot = Spot(lines)
    z, x, core = (spot.z, spot.x, spot.core)
    units = scatter_units(o0.shape[0])
    scatter = Scatter(
        spot,
        units,
        (p0, p1, p2),
        (o0, o1, o2),
        (mine, core_in, x_in, up_in, down_in),
        (load_sem, core_sem, rx_sem, up_sem, down_sem),
    )
    order = range(len(units))
    greet(spot, True)
    far_copy = send(branch_hbm, far_hbm, own_sem.at[2], own_sem.at[3], spot.y_mate())
    far_copy.start()
    ffn_copy = send(ffn_hbm, ffn_in_hbm, own_sem.at[4], own_sem.at[5], spot.y_mate())
    ffn_copy.start()

    def outside(d):
        return (d < z - span) | (d > z + span)

    def pass_copy(step, d):
        i = 0 if step > 0 else 1
        part = all_do.at[d, :, core]
        return send(part, part, z_sem.at[i, d], z_sem.at[2 + i, d], spot.z_mate(step))

    across = send(do_ref, all_do.at[z, x, core], x_sem.at[0], x_sem.at[1], spot.x_mate())

    def beside(d):
        part = all_do.at[d, :, core]
        return send(part, part, c_sem.at[0, d], c_sem.at[1, d], spot.core_mate())

    own_copy = pltpu.make_async_copy(do_ref, all_do.at[z, x, core], own_sem.at[0])

    def zero_copies(d):
        return [
            pltpu.make_async_copy(vm.at[pl.ds(0, pair)], all_do.at[d, a, b], zero_sem.at[d, a, b])
            for a in range(2)
            for b in range(2)
        ]

    def zero_start(d, unused):
        @pl.when(outside(d))
        def _():
            for copy in zero_copies(d):
                copy.start()

        return unused

    def turn():
        across.wait()
        own_copy.wait()

        @pl.when(z + 1 < lines)
        def _():
            pass_copy(1, z).start()

        @pl.when(z > 0)
        def _():
            pass_copy(-1, z).start()

        beside(z).start()

    def level(k):
        @pl.when(z - k >= 0)
        def _():
            d = jnp.maximum(z - k, 0)
            pass_copy(1, d).wait_recv()
            if k < span:

                @pl.when(z + 1 < lines)
                def _():
                    pass_copy(1, d).start()

            beside(d).start()

        @pl.when(z + k < lines)
        def _():
            d = jnp.minimum(z + k, lines - 1)
            pass_copy(-1, d).wait_recv()
            if k < span:

                @pl.when(z > 0)
                def _():
                    pass_copy(-1, d).start()

            beside(d).start()

    def gathered(d, unused):
        @pl.when(~outside(d))
        def _():
            beside(d).wait()

        @pl.when(outside(d))
        def _():
            for copy in zero_copies(d):
                copy.wait()

        @pl.when((z + 1 < lines) & (d <= z) & (d > z - span))
        def _():
            pass_copy(1, d).wait_send()

        @pl.when((z > 0) & (d >= z) & (d < z + span))
        def _():
            pass_copy(-1, d).wait_send()

        return unused

    own_copy.start()
    across.start()
    for u in order:
        scatter.begin(u)
    vm[:PAD, :] = jnp.zeros((PAD, WIDE), bf16)
    lax.fori_loop(0, lines, zero_start, 0)

    base = spot.index * pair
    total = 4 * lines * pair
    origin = jnp.clip(base - reach * pair, 0, total - rows)
    local = base - origin
    blocks = rows // pair

    def mask_copy(n):
        to = pl.ds(pl.multiple_of(PAD + n * pair, 128), pair)
        return pltpu.make_async_copy(masks_hbm.at[n], mask_row.at[:, to], q_sem.at[1 + n])

    def mask_start(n, unused):
        mask_copy(n).start()
        return unused

    lax.fori_loop(0, blocks, mask_start, 0)
    mask_row[:, :PAD] = jnp.zeros((8, PAD), f32)
    mask_row[:, PAD + rows :] = jnp.zeros((8, PAD), f32)
    km[:PAD, :] = jnp.broadcast_to(
        jnp.where(pad_lanes(plan), neg_big, 0.0).astype(bf16), (PAD, WIDE)
    )
    km[PAD + rows :, :] = km[:PAD, :]
    vm[PAD + rows :, :] = jnp.zeros((PAD, WIDE), bf16)
    low_block = lanes_of(pair, 128) < 64
    ones_block = (lanes_of(pair, 128) < 3 * plan.heads).astype(bf16)

    def g_copy(n):
        at = pl.ds(pl.multiple_of(n * pair, pair), pair)
        return pltpu.make_async_copy(g_hbm.at[at], g_buf.at[n % 2], g_sem.at[0, n % 2])

    def aug_copy(n):
        at = pl.ds(pl.multiple_of(n * pair, pair), pair)
        return pltpu.make_async_copy(aug_hbm.at[at], aug_buf.at[n % 2], g_sem.at[1, n % 2])

    def near_copy(flip):
        return pltpu.make_async_copy(near_hbm.at[flip], near_ref, own_sem.at[1])

    g_copy(0).start()
    aug_copy(0).start()
    near_copy(0).start()

    def build(n, unused):
        g_copy(n).wait()
        aug_copy(n).wait()

        @pl.when(n + 1 < blocks)
        def _():
            g_copy(n + 1).start()
            aug_copy(n + 1).start()

        mask_copy(n).wait()
        to = pl.ds(pl.multiple_of(PAD + n * pair, 128), pair)
        middle = g_buf[n % 2, :, 128:256]
        km[to, 0:128] = g_buf[n % 2, :, 0:128]
        km[to, 128:256] = jnp.where(low_block, middle, aug_buf[n % 2])
        vm[to, 0:128] = jnp.where(low_block, ones_block, middle)
        vm[to, 128:256] = g_buf[n % 2, :, 256:384]
        return unused

    early = min(6, blocks)
    lax.fori_loop(0, early, build, 0)
    scatter.core_stage(0)
    lax.fori_loop(early, blocks, build, 0)
    near_copy(0).wait()
    near_acc[...] = jnp.zeros_like(near_acc)
    far_acc[...] = jnp.zeros_like(far_acc)
    lane = lanes_of(TQ)
    low = lanes_of(TQ, 128) < 64
    ones = (lanes_of(TQ, 128) < 3 * plan.heads).astype(bf16)

    def chunks(t):
        start = local + t * TQ
        least = jnp.maximum(start - doc_most + 1, 0)
        most = jnp.minimum(start + TQ + doc_most - 1, rows)
        n_left = jnp.maximum(start - EDGE - least + TK - 1, 0) // TK
        n_right = jnp.maximum(most - (start + TK - EDGE) + TK - 1, 0) // TK
        return start, n_left, n_right

    def rows_of_tile(t):
        return pl.ds(pl.multiple_of(t * TQ, TQ), TQ)

    def near_of(start):
        return pl.ds(pl.multiple_of(start + PAD - EDGE, 128), TK)

    def query_grads(h, s, part):
        return jnp.exp(s) * nt(doh_ref[h], vm[part, :])

    def dq_near(t, start):
        out = rows_of_tile(t)
        near = near_of(start)
        q = qb_ref[out, :]
        do = do_ref[out, :]
        for h in range(plan.heads):
            qh_ref[h] = jnp.where(plan.key_lanes(lane, h), q, jnp.zeros_like(q))
            doh_ref[h] = jnp.where(plan.value_lanes(lane, h), do, jnp.zeros_like(do))
            ds = query_grads(
                h, nt(qh_ref[h], km[near, :]) + near_ref[h] + mask_row[0:1, near], near
            )
            near_acc[h] += ds
            acc[h] = nn(ds.astype(bf16), km[near, :])

    def dq_far(start, n, n_left, count):
        parts = far_pair(start, n, n_left, count, far_left_bucket, far_right_bucket)
        for h in range(plan.heads):
            grads = []
            for i, (part, bucket) in enumerate(parts):
                slot = (2 * n + i >= n_left).astype(jnp.int32)
                offset = mask_row[0:1, part] + table_ref[h, bucket]
                ds = query_grads(h, nt(qh_ref[h], km[part, :]) + offset, part)
                grads.append(nn(ds.astype(bf16), km[part, :]))
                far_acc[slot, h] += (
                    ds[:, 0:128] + ds[:, 128:256] + ds[:, 256:384] + ds[:, 384:512]
                )
            acc[h] += grads[0] + grads[1]

    def dq_end(t):
        result = jnp.zeros((TQ, WIDE), f32)
        for h in range(plan.heads):
            result = jnp.where(lane // 64 == h, acc[h], result)
        dq_ref[rows_of_tile(t), :] = result.astype(bf16)

    def table_end():
        row = lax.broadcasted_iota(jnp.int32, (EDGE, 3 * EDGE), 0)
        col = lax.broadcasted_iota(jnp.int32, (EDGE, 3 * EDGE), 1)
        bucket = bucket_of(col - EDGE - row)
        for h in range(plan.heads):
            band = near_acc[h, :EDGE, : 3 * EDGE] + near_acc[h, EDGE:, EDGE:]

            def one(b, unused, band=band, h=h):
                part = jnp.sum(jnp.where(bucket == b, band, 0.0), axis=0, keepdims=True)
                tab_ref[h, pl.ds(b, 1), :] = part[:, :128] + part[:, 128:256] + part[:, 256:]
                return unused

            lax.fori_loop(0, 32, one, 0)
            for b, slot, extra in (
                (far_left_bucket, 0, near_acc[h, EDGE:, :EDGE]),
                (far_right_bucket, 1, near_acc[h, :EDGE, 3 * EDGE :]),
            ):
                tab_ref[h, b : b + 1, :] += jnp.sum(
                    far_acc[slot, h], axis=0, keepdims=True
                ) + jnp.sum(extra, axis=0, keepdims=True)

    def swap_operands():
        near_copy(1).start()
        lax.fori_loop(0, lines, gathered, 0)
        q_copy = pltpu.make_async_copy(qall_hbm, km.at[pl.ds(PAD, rows)], q_sem.at[0])
        q_copy.start()

        def block_copy(n):
            b = origin // pair + n
            return pltpu.make_async_copy(
                all_do.at[b // 4, (b // 2) % 2, b % 2],
                vm.at[pl.ds(pl.multiple_of(PAD + n * pair, 128), pair)],
                q_sem.at[1 + n],
            )

        def block_start(n, unused):
            block_copy(n).start()
            return unused

        lax.fori_loop(0, blocks, block_start, 0)
        first = lanes_of(1)
        stat = (first >= plan.stat_lane) & (first < plan.stat_lane + 3 * plan.heads)
        km[:PAD, :] = jnp.broadcast_to(jnp.where(stat, neg_big, 0.0).astype(bf16), (PAD, WIDE))
        km[PAD + rows :, :] = km[:PAD, :]

        def block_wait(n, unused):
            block_copy(n).wait()
            return unused

        lax.fori_loop(0, blocks, block_wait, 0)
        q_copy.wait()
        near_copy(1).wait()

    def key_grads(h, s, part):
        p = jnp.exp(s)
        ds = p * nt(doh_ref[h], vm[part, :])
        return nn(p.astype(bf16), vm[part, :]), nn(ds.astype(bf16), km[part, :])

    def dkv_near(t, start):
        out = rows_of_tile(t)
        near = near_of(start)
        middle = own_kv[out, 128:256]
        k = jnp.concatenate([own_kv[out, 0:128], jnp.where(low, middle, own_aug[out, :])], axis=1)
        v = jnp.concatenate([jnp.where(low, ones, middle), own_kv[out, 256:384]], axis=1)
        for h in range(plan.heads):
            qh_ref[h] = jnp.where(plan.key_lanes(lane, h), k, jnp.zeros_like(k))
            doh_ref[h] = jnp.where(plan.value_lanes(lane, h), v, jnp.zeros_like(v))
            near_acc[h, :, :WIDE], acc[h] = key_grads(
                h, nt(qh_ref[h], km[near, :]) + near_ref[h], near
            )

    def dkv_far(start, n, n_left, count):
        parts = far_pair(start, n, n_left, count, far_right_bucket, far_left_bucket)
        for h in range(plan.heads):
            (v_one, k_one), (v_two, k_two) = [
                key_grads(h, nt(qh_ref[h], km[part, :]) + table_ref[h, bucket], part)
                for part, bucket in parts
            ]
            near_acc[h, :, :WIDE] += v_one + v_two
            acc[h] += k_one + k_two

    def dkv_end(t):
        out = rows_of_tile(t)
        dk = jnp.zeros((TQ, WIDE), f32)
        dv = jnp.zeros((TQ, WIDE), f32)
        mask_grad = jnp.zeros((TQ, 1), f32)
        for h in range(plan.heads):
            dk = jnp.where(lane // 64 == h, acc[h], dk)
            dv = jnp.where(lane // 64 == h + 1, near_acc[h, :, :WIDE], dv)
            mask_grad = mask_grad + acc[h][:, plan.mask_lane : plan.mask_lane + 1]
        mask_ref[t] = jnp.transpose(jnp.broadcast_to(mask_grad, (TQ, 128)))[:8, :]
        dk_ref[out, :] = dk.astype(bf16)
        dv_ref[out, :] = dv.astype(bf16)

    tiles = pair // TQ
    steps = 1 + -(-(2 * (-(-doc_most // TK)) + 1) // 2)
    half_slots = tiles * steps
    last_step = steps - 1

    def attention(w):
        backward = w >= half_slots
        t = (w % half_slots) // steps
        n = w % steps
        start, n_left, n_right = chunks(t)
        count = n_left + n_right
        live = (n > 0) & (2 * (n - 1) < count)

        @pl.when(~backward)
        def _():
            @pl.when(n == 0)
            def _():
                dq_near(t, start)

            @pl.when(live)
            def _():
                dq_far(start, n - 1, n_left, count)

            @pl.when(n == last_step)
            def _():
                dq_end(t)

        @pl.when(backward & (w < 2 * half_slots))
        def _():
            @pl.when(w == half_slots)
            def _():
                table_end()
                swap_operands()

            @pl.when(n == 0)
            def _():
                dkv_near(t, start)

            @pl.when(live)
            def _():
                dkv_far(start, n - 1, n_left, count)

            @pl.when(n == last_step)
            def _():
                dkv_end(t)

    work = 2 * half_slots
    events = []

    def due(time, run, *args):
        events.append((max(0, int((time - start_us) / slot_us)), functools.partial(run, *args)))

    start_us, slot_us = (6.0, 2.5)
    due(6.0, turn)
    for k in range(1, span + 1):
        due((22.0, 36.0)[min(k, 2) - 1], level, k)
    times = (
        (7.0, 26.0, 51.0, 61.0, 68.0),
        (10.5, 43.0, 64.0, 74.0, 81.0),
        (14.0, 60.0, 77.0, 87.0, 94.0),
        (17.0, 73.0, 87.0, 95.0, 101.0),
        (20.0, 86.0, 97.5, 106.0, 111.0),
        (22.0, 95.0, 104.0, 110.0, 114.0),
        (23.0, 99.0, 107.0, 111.0, 114.5),
    )
    for u in order:
        core_at, x_at, one_at, two_at, end_at = times[u]
        if u > 0:
            due(core_at, scatter.core_stage, u)
        due(x_at, scatter.x_stage, u)
        due(one_at, scatter.relay, u, 1)
        due(two_at, scatter.relay, u, 2)
        due(end_at, scatter.settle, u)
    events.sort(key=lambda event: event[0])
    end = max(work, events[-1][0] + 1)

    def slot(w, unused):
        for at, run in events:

            @pl.when(w == at)
            def _(run=run):
                run()

        attention(w)
        return unused

    lax.fori_loop(0, end, slot, 0)
    for u in order:
        scatter.drain(u)
    far_copy.wait()
    ffn_copy.wait()


def backward(
    plan, cycle_size, reach, doc_most, rows, table, aug, masks, q_back, do_wide, own_kv, own_aug,
    near_bias, kv_all, q_all, branch, ffn_far, parts,
):
    lines = cycle_size // 4
    span = min(lines - 1, (reach + 3) // 4)
    pair = q_back.shape[0]
    units_here, model = parts[0].shape
    size = units_here // cycle_size
    units = scatter_units(size)
    shaped = [part.reshape(lines, 2, 2, size, model) for part in parts]
    n = len(units)
    heads = plan.heads
    padded = rows + 2 * PAD
    hbm = pl.BlockSpec(memory_space=pl.ANY)
    dma = pltpu.SemaphoreType.DMA
    return pl.pallas_call(
        functools.partial(backward_kernel, plan, lines, span, reach, doc_most, rows, pair),
        out_shape=[
            jax.ShapeDtypeStruct((pair, WIDE), bf16),
            jax.ShapeDtypeStruct((heads, 32, 128), f32),
            jax.ShapeDtypeStruct((pair, WIDE), bf16),
            jax.ShapeDtypeStruct((pair, WIDE), bf16),
            jax.ShapeDtypeStruct((pair // TQ, 8, TQ), f32),
        ]
        + [jax.ShapeDtypeStruct((size, model), bf16)] * 3
        + [
            jax.ShapeDtypeStruct(branch.shape, bf16),
            jax.ShapeDtypeStruct(branch.shape, bf16),
            jax.ShapeDtypeStruct((lines, 2, 2, pair, WIDE), bf16),
        ],
        in_specs=[smem] + [vmem] * 4 + [hbm] * 10,
        out_specs=[vmem] * 8 + [hbm] * 3,
        scratch_shapes=[
            pltpu.VMEM((3, lines, 2, size, model), bf16),
            pltpu.VMEM((3, lines, 2, size, model), bf16),
            pltpu.VMEM((3, lines, size, model), bf16),
            pltpu.VMEM((3, lines, size, model), bf16),
            pltpu.VMEM((3, lines, size, model), bf16),
            pltpu.VMEM((padded, WIDE), bf16),
            pltpu.VMEM((padded, WIDE), bf16),
            pltpu.VMEM((8, padded), f32),
            pltpu.VMEM((2, pair, 2 * plan.cols), bf16),
            pltpu.VMEM((2, pair, 128), bf16),
            pltpu.VMEM((heads, TQ, WIDE), bf16),
            pltpu.VMEM((heads, TQ, WIDE), bf16),
            pltpu.VMEM((heads, TQ, WIDE), f32),
            pltpu.VMEM((heads, TQ, TK), f32),
            pltpu.VMEM((heads, TQ, TK), f32),
            pltpu.VMEM((2, heads, TQ, 128), f32),
            dma((n,)),
            dma((2, n)),
            dma((2, n)),
            dma((2, n, lines)),
            dma((2, n, lines)),
            dma((6,)),
            dma((lines, 2, 2)),
            dma((4, lines)),
            dma((2,)),
            dma((2, lines)),
            dma((2, 2)),
            dma((1 + rows // pair,)),
        ],
        compiler_params=pltpu.CompilerParams(
            vmem_limit_bytes=62 * 2**20, collective_id=1, has_side_effects=True
        ),
        name="backward",
    )(
        table, q_back, do_wide, own_kv, own_aug, near_bias, aug, masks, kv_all, q_all,
        branch, ffn_far, *shaped
    )


def shards(
    tokens,
    doc_lengths,
    key_mask,
    gain_attn,
    w_query,
    w_key,
    w_value,
    w_out,
    bias_table,
    gain_ffn,
    w_gate,
    w_up,
    w_down,
    cotangent,
):
    own_rows, model = tokens.shape
    group = lax.axis_size("wa")
    cycle_size = lax.axis_size("ctx")
    pair = own_rows * group
    heads = bias_table.shape[1]
    docs = doc_lengths.shape[0]
    plan = Plan(heads, w_query.shape[1] // heads, docs)
    total_rows = pair * cycle_size
    doc_most = min(MAXLEN, total_rows // 2)
    reach = min(cycle_size - 1, (doc_most - 1) // pair + 1)
    base = lax.axis_index("ctx") * pair
    rows = min(total_rows, (2 * reach + 1) * pair)
    origin = jnp.clip(base - reach * pair, 0, total_rows - rows).astype(jnp.int32)
    table = bias_table.T

    def window(gathered):
        if rows == total_rows:
            return gathered
        return lax.dynamic_slice_in_dim(gathered, origin, rows, 0)

    gather = functools.partial(lax.all_gather, axis_name="ctx", axis=0, tiled=True)
    (
        pair_normed, pair_tokens, q_wide, own_kv, k_aug, own_aug, near_bias, masks, pair_cot, kv_all,
    ) = first(
        plan,
        cycle_size,
        reach,
        rows,
        doc_lengths,
        table,
        tokens,
        gain_attn,
        key_mask,
        w_query,
        w_key,
        w_value,
        cotangent,
    )
    masks = masks.reshape(cycle_size, 8, pair)
    w_late, near_bias = lax.optimization_barrier((w_out, near_bias))
    pair_w_out = lax.all_gather(w_late, "wa", axis=0)
    if rows < total_rows:
        masks = lax.dynamic_slice_in_dim(masks, origin // pair, rows // pair, 0)
    kv_all = window(kv_all.reshape(total_rows, 2 * plan.cols))
    attended, mixed, q_back = attend(
        plan, cycle_size, reach, rows, doc_lengths, table, q_wide, near_bias, kv_all, k_aug, masks
    )
    q_all = window(gather(q_back))
    hidden, grad_hidden, branch, ffn_own, ffn_far, do_wide, gain_ffn_part, *stacks = middle(
        plan,
        cycle_size,
        attended,
        mixed,
        pair_tokens,
        pair_cot,
        gain_ffn,
        w_out,
        pair_w_out,
        w_gate,
        w_up,
        w_down,
    )
    (
        grad_queries, table_part, grad_keys, grad_values, mask_part,
        grad_w_down, grad_w_gate, grad_w_up, far_branch, ffn_in, unused_gathered,
    ) = backward(
        plan,
        cycle_size,
        reach,
        doc_most,
        rows,
        table,
        k_aug,
        masks,
        q_back,
        do_wide,
        own_kv,
        own_aug,
        near_bias,
        kv_all,
        q_all,
        branch,
        ffn_far,
        stacks,
    )
    grad_w_down, grad_w_gate, grad_w_up = (
        grad_w_down.astype(f32), grad_w_gate.astype(f32).T, grad_w_up.astype(f32).T
    )
    layer_out, grad_tokens, grad_mask, weights, grad_gain_attn, grad_gain_ffn, grad_table = finish(
        plan,
        cycle_size,
        grad_queries,
        grad_keys,
        grad_values,
        attended,
        pair_normed,
        branch,
        far_branch,
        w_query.T,
        w_key.T,
        w_value.T,
        hidden,
        ffn_own,
        ffn_in,
        mask_part.reshape(group, 8, own_rows),
        tokens,
        gain_attn,
        grad_hidden,
        table_part,
        gain_ffn_part,
    )
    weights = weights.reshape(4, plan.cols, model).astype(f32)
    return (
        layer_out.T,
        grad_tokens.T,
        grad_mask,
        grad_gain_attn,
        weights[0].T,
        weights[1].T,
        weights[2].T,
        weights[3],
        grad_table.T,
        grad_gain_ffn,
        grad_w_gate,
        grad_w_up,
        grad_w_down,
    )


def solution(mesh):
    placed = (
        P(("ctx", "wa"), None),
        P(),
        P("ctx"),
        P(),
        P(None, "wa"),
        P(None, "wa"),
        P(None, "wa"),
        P("wa", None),
        P(None, "wa"),
        P(),
        P(None, "wa"),
        P(None, "wa"),
        P("wa", None),
        P(("ctx", "wa"), None),
    )
    return jax.shard_map(
        shards,
        mesh=mesh,
        in_specs=placed,
        out_specs=(
            P(("ctx", "wa"), None),
            P(("ctx", "wa"), None),
            P(("ctx", "wa")),
            P(),
            P(None, "wa"),
            P(None, "wa"),
            P(None, "wa"),
            P("wa", None),
            P(None, "wa"),
            P(),
            P(None, ("wa", "ctx")),
            P(None, ("wa", "ctx")),
            P(("wa", "ctx"), None),
        ),
        check_vma=False,
    )
```

```python
import functools

import jax
import jax.numpy as jnp
from jax import lax
from jax.experimental import pallas as pl
from jax.experimental.pallas import tpu as pltpu
from jax.sharding import PartitionSpec as P

MAXLEN = 8192

bucket_edges = (12, 16, 23, 32, 46, 64, 91)
neg_big = -1e30
eps = 1e-06
far_left_bucket = 15
far_right_bucket = 31
slack = 20.0
WIDE = 256
TQ = 256
TK = 512
EDGE = 128
PAD = TK + EDGE
f32 = jnp.float32
bf16 = jnp.bfloat16


def bucket_of(relative):
    distance = jnp.abs(relative)
    bucket = jnp.minimum(distance, 8) + 16 * (relative > 0).astype(jnp.int32)
    for edge in bucket_edges:
        bucket = bucket + (distance >= edge).astype(jnp.int32)
    return bucket


def norm_forward(inputs, gain):
    inv_root = lax.rsqrt(jnp.mean(inputs * inputs, axis=-1, keepdims=True) + eps)
    return (inputs * inv_root * gain, inv_root)


def norm_backward(inputs, inv_root, gain, grad_normed):
    scaled = gain * grad_normed
    cubed = inv_root * inv_root * inv_root
    grad_inputs = inv_root * scaled - inputs * cubed * jnp.mean(
        inputs * scaled, axis=-1, keepdims=True
    )
    grad_gain = jnp.sum(grad_normed * inputs * inv_root, axis=0)
    return (grad_inputs, grad_gain)


def gated(gate, upward):
    return jax.nn.gelu(gate, approximate=True) * upward


def nt(a, b):
    return lax.dot_general(a, b, (((1,), (1,)), ((), ())), preferred_element_type=f32)


def nn(a, b):
    return lax.dot_general(a, b, (((1,), (0,)), ((), ())), preferred_element_type=f32)


def split3(x):
    hi = x.astype(bf16)
    rest = x - hi.astype(f32)
    mid = rest.astype(bf16)
    return (hi, mid, (rest - mid.astype(f32)).astype(bf16))


class Plan:
    def __init__(self, heads, width, docs):
        self.heads = heads
        self.width = width
        self.bits = max(1, (docs - 1).bit_length())
        self.cols = heads * width
        self.mask_lane = self.cols
        self.doc_lane = self.cols + 1
        self.stat_lane = self.doc_lane + 2 * self.bits
        assert self.stat_lane + 3 * heads <= WIDE and self.cols + 64 == WIDE and width == 64

    def key_lanes(self, lane, h):
        own = (lane >= h * self.width) & (lane < (h + 1) * self.width)
        aug = (lane >= self.mask_lane) & (lane < self.stat_lane)
        stat = (lane >= self.stat_lane + 3 * h) & (lane < self.stat_lane + 3 * h + 3)
        return own | aug | stat

    def value_lanes(self, lane, h):
        own = (lane >= 64 + h * self.width) & (lane < 64 + (h + 1) * self.width)
        return own | ((lane >= 3 * h) & (lane < 3 * h + 3))


def lanes_of(rows, width=WIDE):
    return lax.broadcasted_iota(jnp.int32, (rows, width), 1)


def near_lanes(heads, table_ref, near_ref):
    row = lax.broadcasted_iota(jnp.int32, (EDGE, 3 * EDGE), 0)
    col = lax.broadcasted_iota(jnp.int32, (EDGE, 3 * EDGE), 1)
    relative = col - EDGE - row
    for flip in range(2):
        bucket = bucket_of(-relative if flip else relative)
        left, right = (far_left_bucket, far_right_bucket)
        if flip:
            left, right = (right, left)
        for h in range(heads):
            base = jnp.full((EDGE, 3 * EDGE), table_ref[h, 0], f32)
            for b in range(1, 32):
                base = jnp.where(bucket == b, table_ref[h, b], base)
            far_l = jnp.full((EDGE, EDGE), table_ref[h, left], f32)
            far_r = jnp.full((EDGE, EDGE), table_ref[h, right], f32)
            near_ref[flip, h, :EDGE, : 3 * EDGE] = base
            near_ref[flip, h, :EDGE, 3 * EDGE :] = far_r
            near_ref[flip, h, EDGE:, EDGE:] = base
            near_ref[flip, h, EDGE:, :EDGE] = far_l


def far_span(start, n, n_left, left_bucket, right_bucket):
    on_left = n < n_left
    at = start + PAD - EDGE + TK * jnp.where(on_left, -1 - n, 1 + n - n_left)
    bucket = jnp.where(on_left, left_bucket, right_bucket)
    return pl.ds(pl.multiple_of(at, 128), TK), bucket


def pad_lanes(plan):
    lane = lanes_of(1)
    return (lane >= plan.doc_lane) & (lane < plan.stat_lane)


def far_pair(start, n, n_left, count, left, right):
    pair_of = []
    for i in range(2):
        part, bucket = far_span(start, 2 * n + i, n_left, left, right)
        at = jnp.where(2 * n + i < count, part.start, 0)
        pair_of.append((pl.ds(pl.multiple_of(at, 128), TK), bucket))
    return pair_of


def fwd_kernel(
    plan, lines, reach, rows, pair, lengths, table_ref, q_ref, near_hbm, g_hbm, aug_hbm, masks_hbm,
    low_ref, wide_ref, qb_ref,
    km, vm, mask_row, g_buf, aug_buf, near_ref, acc, extra, row_max, qh_ref, g_sem, near_sem,
):
    base = lax.axis_index("ctx") * pair
    origin = jnp.clip(base - reach * pair, 0, 4 * lines * pair - rows)
    blocks = rows // pair
    tiles = pair // TQ
    near_copy = pltpu.make_async_copy(near_hbm.at[0], near_ref, near_sem.at[0])
    near_copy.start()

    def document(position):
        def look(e, carry):
            begin, low, high = carry
            end = begin + lengths[e]
            inside = (begin <= position) & (position < end)
            return (end, jnp.where(inside, begin, low), jnp.where(inside, end, high))

        zero = jnp.int32(0)
        return lax.fori_loop(0, lengths.shape[0], look, (zero, zero, zero))[1:]

    def extent(t):
        first = base + t * TQ
        low = document(first)[0]
        high = document(first + TQ - 1)[1]
        n_left = jnp.maximum(0, first - EDGE - low + TK - 1) // TK
        n_right = jnp.maximum(0, high - (first - EDGE + TK) + TK - 1) // TK
        return low, high, n_left, n_right

    low_end = extent(0)[0] - origin
    high_end = extent(tiles - 1)[1] - origin
    from_block = jnp.maximum(0, low_end - TK) // pair
    to_block = jnp.minimum(blocks, (high_end + TK + pair - 1) // pair)

    def loads(n):
        at = pl.ds(pl.multiple_of(n * pair, pair), pair)
        to = pl.ds(pl.multiple_of(PAD + n * pair, 128), pair)
        slot = n % 2
        return (
            pltpu.make_async_copy(g_hbm.at[at], g_buf.at[slot], g_sem.at[0, slot]),
            pltpu.make_async_copy(aug_hbm.at[at], aug_buf.at[slot], g_sem.at[1, slot]),
            pltpu.make_async_copy(masks_hbm.at[n], mask_row.at[:, to], g_sem.at[2, slot]),
        )

    for copy in loads(from_block):
        copy.start()
    mask_row[:, :PAD] = jnp.zeros((8, PAD), f32)
    mask_row[:, PAD + rows :] = jnp.zeros((8, PAD), f32)
    km[:PAD, :] = jnp.broadcast_to(
        jnp.where(pad_lanes(plan), neg_big, 0.0).astype(bf16), (PAD, WIDE)
    )
    km[PAD + rows :, :] = km[:PAD, :]
    vm[:PAD, :] = jnp.zeros((PAD, WIDE), bf16)
    vm[PAD + rows :, :] = jnp.zeros((PAD, WIDE), bf16)
    low_lanes = lanes_of(pair, 128) < 64
    ones = (lanes_of(pair, 128) < 3 * plan.heads).astype(bf16)

    def build(n, unused):
        for copy in loads(n):
            copy.wait()

        @pl.when(n + 1 < to_block)
        def _():
            for copy in loads(n + 1):
                copy.start()

        to = pl.ds(pl.multiple_of(PAD + n * pair, 128), pair)
        middle = g_buf[n % 2, :, 128:256]
        km[to, 0:128] = g_buf[n % 2, :, 0:128]
        km[to, 128:256] = jnp.where(low_lanes, middle, aug_buf[n % 2])
        vm[to, 0:128] = jnp.where(low_lanes, ones, middle)
        vm[to, 128:256] = g_buf[n % 2, :, 256:384]
        return unused

    lax.fori_loop(from_block, to_block, build, 0)
    near_copy.wait()
    lane = lanes_of(TQ)

    def tile(t, unused):
        start = base - origin + t * TQ
        low_doc, high_doc, n_left, n_right = extent(t)
        count = n_left + n_right
        out = pl.ds(pl.multiple_of(t * TQ, TQ), TQ)
        q = q_ref[out, :]
        near = pl.ds(pl.multiple_of(start + PAD - EDGE, 128), TK)
        for h in range(plan.heads):
            qh = jnp.where(plan.key_lanes(lane, h), q, jnp.zeros_like(q))
            qh_ref[h] = qh
            s = nt(qh, km[near, :]) + near_ref[h] + mask_row[0:1, near]
            top = jnp.max(s, axis=1, keepdims=True)
            p = jnp.exp(s - top).astype(bf16)
            acc[h] = nn(p, vm[near, :])
            row_max[h] = jnp.broadcast_to(top, (TQ, 128))

        def far(n, unused):
            parts = far_pair(start, n, n_left, count, far_left_bucket, far_right_bucket)

            def scores_of(h):
                return [
                    (nt(qh_ref[h], km[part, :]) + (mask_row[0:1, part] + table_ref[h, bucket]), part)
                    for part, bucket in parts
                ]

            worst = jnp.full((TQ, 128), -slack, f32)
            for h in range(plan.heads):
                top = row_max[h]
                more = jnp.zeros((TQ, WIDE), f32)
                for s, part in scores_of(h):
                    tiles_of = []
                    for c in range(0, TK, 128):
                        over = s[:, c : c + 128] - top
                        worst = jnp.maximum(worst, over)
                        tiles_of.append(jnp.exp(over).astype(bf16))
                    more = more + nn(jnp.concatenate(tiles_of, axis=1), vm[part, :])
                extra[h] = more
            passed = jnp.max(worst) > slack

            @pl.when(jnp.logical_not(passed))
            def _():
                for h in range(plan.heads):
                    acc[h] += extra[h]

            @pl.when(passed)
            def _():
                for h in range(plan.heads):
                    scores = scores_of(h)
                    old = row_max[h][:, :1]
                    top = old
                    for s, part in scores:
                        top = jnp.maximum(top, jnp.max(s, axis=1, keepdims=True))
                    more = [nn(jnp.exp(s - top).astype(bf16), vm[part, :]) for s, part in scores]
                    acc[h] = acc[h] * jnp.exp(old - top) + (more[0] + more[1])
                    row_max[h] = jnp.broadcast_to(top, (TQ, 128))

            return unused

        lax.fori_loop(0, (count + 1) // 2, far, 0)
        wide = jnp.zeros((TQ, WIDE), f32)
        qb = jnp.where(lane < plan.stat_lane, q, jnp.zeros_like(q))
        for h in range(plan.heads):
            total = acc[h][:, 3 * h : 3 * h + 1]
            log_total = row_max[h][:, :1] + jnp.log(total)
            wide = jnp.where(lane // 64 == h + 1, acc[h] / total, wide)
            for i, part in enumerate(split3(-log_total)):
                qb = jnp.where(lane == plan.stat_lane + 3 * h + i, part, qb)
        wide_ref[out, :] = wide
        low_ref[out, :] = wide.astype(bf16)
        qb_ref[out, :] = qb
        return unused

    lax.fori_loop(0, tiles, tile, 0)


def attend(plan, cycle_size, reach, rows, lengths, table, q_wide, near_bias, kv_all, aug, masks):
    pair = q_wide.shape[0]
    heads = plan.heads
    padded = rows + 2 * PAD
    hbm = pl.BlockSpec(memory_space=pl.ANY)
    return pl.pallas_call(
        functools.partial(fwd_kernel, plan, cycle_size // 4, reach, rows, pair),
        out_shape=(
            jax.ShapeDtypeStruct((pair, WIDE), bf16),
            jax.ShapeDtypeStruct((pair, WIDE), f32),
            jax.ShapeDtypeStruct((pair, WIDE), bf16),
        ),
        in_specs=[smem, smem, vmem] + [hbm] * 4,
        out_specs=(vmem, vmem, vmem),
        scratch_shapes=[
            pltpu.VMEM((padded, WIDE), bf16),
            pltpu.VMEM((padded, WIDE), bf16),
            pltpu.VMEM((8, padded), f32),
            pltpu.VMEM((2, pair, 2 * plan.cols), bf16),
            pltpu.VMEM((2, pair, 128), bf16),
            pltpu.VMEM((heads, TQ, TK), f32),
            pltpu.VMEM((heads, TQ, WIDE), f32),
            pltpu.VMEM((heads, TQ, WIDE), f32),
            pltpu.VMEM((heads, TQ, 128), f32),
            pltpu.VMEM((heads, TQ, WIDE), bf16),
            pltpu.SemaphoreType.DMA((3, 2)),
            pltpu.SemaphoreType.DMA((1,)),
        ],
        compiler_params=params(),
        name="attention_forward",
    )(lengths, table, q_wide, near_bias, kv_all, aug, masks)


vmem = pl.BlockSpec(memory_space=pltpu.VMEM)
smem = pl.BlockSpec(memory_space=pltpu.SMEM)


def params():
    return pltpu.CompilerParams(vmem_limit_bytes=56 * 2**20)


class Spot:
    def __init__(self, lines):
        index = lax.axis_index("ctx")
        self.wa = lax.axis_index("wa")
        self.index = index
        self.lines = lines
        self.z = index // 4
        self.x = (index // 2) % 2
        self.core = index % 2

    def core_mate(self):
        return (self.index + 1 - 2 * self.core, self.wa)

    def x_mate(self):
        return (self.index + 2 - 4 * self.x, self.wa)

    def z_mate(self, step):
        return (jnp.clip(self.index + 4 * step, 0, 4 * self.lines - 1), self.wa)

    def y_mate(self):
        return (self.index, 1 - self.wa)


def send(src, dst, send_sem, recv_sem, device):
    return pltpu.make_async_remote_copy(
        src_ref=src,
        dst_ref=dst,
        send_sem=send_sem,
        recv_sem=recv_sem,
        device_id=device,
        device_id_type=pl.DeviceIdType.MESH,
    )


def greet(spot, with_y):
    barrier = pltpu.get_barrier_semaphore()
    mates = [spot.core_mate(), spot.x_mate()] + ([spot.y_mate()] if with_y else [])
    for mate in mates:
        pl.semaphore_signal(barrier, inc=1, device_id=mate, device_id_type=pl.DeviceIdType.MESH)

    @pl.when(spot.z + 1 < spot.lines)
    def _():
        pl.semaphore_signal(
            barrier, inc=1, device_id=spot.z_mate(1), device_id_type=pl.DeviceIdType.MESH
        )

    @pl.when(spot.z > 0)
    def _():
        pl.semaphore_signal(
            barrier, inc=1, device_id=spot.z_mate(-1), device_id_type=pl.DeviceIdType.MESH
        )

    above = (spot.z + 1 < spot.lines).astype(jnp.int32)
    below = (spot.z > 0).astype(jnp.int32)
    pl.semaphore_wait(barrier, len(mates) + above + below)


def added(a, b):
    return a + b


def first_kernel(
    plan, lines, span, reach, rows, lengths, table_ref, tokens_ref, gain_ref, key_mask_ref,
    wq_hbm, wk_hbm, wv_hbm, cot_hbm,
    x_ref, tok_ref, q_ref, own_ref, aug_ref, own_aug_ref, near_ref, masks_ref, cot_pair_hbm, all_hbm,
    weights, zeros, mask_ref, load_sem, y_sem, own_sem, zero_sem, z_sem, x_sem, c_sem,
):
    spot = Spot(lines)
    z, x, core, wa = (spot.z, spot.x, spot.core, spot.wa)
    half, model = tokens_ref.shape
    cols = plan.cols
    chunk = half // 4
    loads = [
        pltpu.make_async_copy(src, weights.at[pl.ds(i * cols, cols)], load_sem.at[i])
        for i, src in enumerate((wk_hbm, wv_hbm, wq_hbm))
    ]
    for load in loads:
        load.start()
    mask_ref[...] = jnp.broadcast_to(key_mask_ref[...].astype(f32)[None, :], mask_ref.shape)
    greet(spot, True)
    zeros[...] = jnp.zeros_like(zeros)

    def outside(d):
        return (d < z - span) | (d > z + span)

    def zero_copies(d):
        return [
            pltpu.make_async_copy(zeros, all_hbm.at[d, a, b], zero_sem.at[d, a, b])
            for a in range(2)
            for b in range(2)
        ]

    def zero_start(d, unused):
        @pl.when(outside(d))
        def _():
            masks_ref[d] = jnp.zeros((2, 2) + mask_ref.shape, f32)
            for copy in zero_copies(d):
                copy.start()

        return unused

    def rows_at(start, size):
        return pl.ds(pl.multiple_of(start, size), size)

    ours = wa * half
    theirs = (1 - wa) * half

    def y_copy(i, base):
        return send(
            tokens_ref.at[rows_at(i * chunk, chunk)],
            tok_ref.at[rows_at(base + i * chunk, chunk)],
            y_sem.at[0, i],
            y_sem.at[1, i],
            spot.y_mate(),
        )

    def y_start(i, unused):
        y_copy(i, ours).start()
        return unused

    lax.fori_loop(0, 4, y_start, 0)
    far_copy = send(
        cot_hbm,
        cot_pair_hbm.at[rows_at(ours, half)],
        y_sem.at[0, 4],
        y_sem.at[1, 4],
        spot.y_mate(),
    )
    near_copy = pltpu.make_async_copy(
        cot_hbm, cot_pair_hbm.at[rows_at(ours, half)], load_sem.at[3]
    )
    near_copy.start()

    def scaled(rows_in):
        rows_in = rows_in.astype(f32)
        inv = lax.rsqrt(jnp.mean(rows_in * rows_in, axis=-1, keepdims=True) + eps)
        return (rows_in * inv * gain_ref[...][None, :]).astype(bf16)

    def normal(i, unused):
        at = rows_at(ours + i * chunk, chunk)
        rows_in = tokens_ref[rows_at(i * chunk, chunk), :]
        tok_ref[at, :] = rows_in
        x_ref[at, :] = scaled(rows_in)
        return unused

    lax.fori_loop(0, 4, normal, 0)
    for load in loads:
        load.wait()

    def project(base, size):
        rows = rows_at(base, size)
        qkv = nt(x_ref[rows, :], weights[...]).astype(bf16)
        own_ref[rows, :] = qkv[:, : 2 * cols]
        q_ref[rows, :cols] = qkv[:, 2 * cols :]

    pieces = [
        (ours, half, True),
        (theirs + half // 2, half // 2, True),
        (theirs, half // 2, False),
        None,
    ]
    mask_piece = 3

    def line_first(p):
        return p == mask_piece or pieces[p][2]

    def piece_rows(p):
        return rows_at(pieces[p][0], pieces[p][1])

    def source(p, d, a):
        if p == mask_piece:
            return masks_ref.at[d, a, core]
        return all_hbm.at[d, a, core, piece_rows(p)]

    def own_source(p):
        return mask_ref if p == mask_piece else own_ref.at[piece_rows(p)]

    def pass_copy(p, step, d, own):
        i = 0 if step > 0 else 1
        if line_first(p):
            dst = source(p, d, x)
            src = own_source(p) if own else dst
        else:
            dst = all_hbm.at[d, :, core, piece_rows(p)]
            src = dst
        return send(src, dst, z_sem.at[p, i, d], z_sem.at[p, 2 + i, d], spot.z_mate(step))

    def across(p, d, own):
        dst = source(p, d, x)
        src = own_source(p) if own else dst
        return send(src, dst, x_sem.at[p, 0, d], x_sem.at[p, 1, d], spot.x_mate())

    def beside(p, d):
        if p == mask_piece:
            part = masks_ref.at[d, :, core]
        else:
            part = all_hbm.at[d, :, core, piece_rows(p)]
        return send(part, part, c_sem.at[p, 0, d], c_sem.at[p, 1, d], spot.core_mate())

    def own_copy(p):
        return pltpu.make_async_copy(
            own_source(p), source(p, z, x), own_sem.at[p]
        )

    def both_ways(p, own):
        @pl.when(z + 1 < lines)
        def _():
            pass_copy(p, 1, z, own).start()

        @pl.when(z > 0)
        def _():
            pass_copy(p, -1, z, own).start()

    def begin(p):
        own_copy(p).start()
        across(p, z, True).start()
        if line_first(p):
            both_ways(p, True)

    def level(p, k):
        @pl.when(z - k >= 0)
        def _():
            d = jnp.maximum(z - k, 0)
            pass_copy(p, 1, d, False).wait_recv()
            if k < span:

                @pl.when(z + 1 < lines)
                def _():
                    pass_copy(p, 1, d, False).start()

            if line_first(p):
                across(p, d, False).start()
            else:
                beside(p, d).start()

        @pl.when(z + k < lines)
        def _():
            d = jnp.minimum(z + k, lines - 1)
            pass_copy(p, -1, d, False).wait_recv()
            if k < span:

                @pl.when(z > 0)
                def _():
                    pass_copy(p, -1, d, False).start()

            if line_first(p):
                across(p, d, False).start()
            else:
                beside(p, d).start()

    def turn(p):
        across(p, z, True).wait()
        own_copy(p).wait()
        both_ways(p, False)
        beside(p, z).start()

    def settle(p, k):
        for sign in (1, -1) if k else (1,):
            d = z - sign * k

            @pl.when((d >= 0) & (d < lines))
            def _(d=d):
                d = jnp.clip(d, 0, lines - 1)
                across(p, d, k == 0).wait()
                if k == 0:
                    own_copy(p).wait()
                beside(p, d).start()

    def doc_of(start, size):
        position = start + lax.broadcasted_iota(jnp.int32, (size, 128), 0)

        def count(e, carry):
            begin, total = carry
            begin = begin + lengths[e]
            return (begin, total + (position >= begin).astype(jnp.int32))

        zero = (jnp.int32(0), jnp.zeros((size, 128), jnp.int32))
        return lax.fori_loop(0, lengths.shape[0] - 1, count, zero)[1]

    def code_lanes(start, size):
        lane = lanes_of(size, 128) + 128
        code = jnp.maximum(lane - plan.doc_lane, 0)
        bit = jnp.bitwise_and(jnp.right_shift(doc_of(start, size), code // 2), 1)
        coded = (lane >= plan.doc_lane) & (lane < plan.stat_lane)
        ones = (lane >= plan.stat_lane) & (lane < plan.stat_lane + 3 * plan.heads)
        return lane, coded, bit != code % 2, ones

    pair = 2 * half
    base = spot.index * pair
    origin = jnp.clip(base - reach * pair, 0, 4 * lines * pair - rows)

    def key_lanes(n, unused):
        at = rows_at(n * half, half)
        lane, coded, differs, ones = code_lanes(origin + n * half, half)
        aug_ref[at, :] = jnp.where(
            coded & differs, neg_big, jnp.where(ones, 1.0, 0.0)
        ).astype(bf16)
        return unused

    def own_lanes(n, unused):
        at = rows_at(n * half, half)
        lane, coded, differs, ones = code_lanes(base + n * half, half)
        column = jnp.transpose(
            jnp.broadcast_to(mask_ref[0:1, at], (128, half))
        )
        own_aug_ref[at, :] = jnp.where(
            lane == plan.mask_lane,
            column,
            jnp.where(coded & differs, neg_big, jnp.where(ones, 1.0, 0.0)),
        ).astype(bf16)
        tail = jnp.where(
            (lane == plan.mask_lane) | (coded & ~differs), 1.0, 0.0
        ).astype(bf16)
        q_ref[at, 128:] = tail
        return unused

    begin(mask_piece)
    lax.fori_loop(0, 2, own_lanes, 0)
    project(ours, half)
    begin(0)
    lax.fori_loop(0, lines, zero_start, 0)
    near_lanes(plan.heads, table_ref, near_ref)
    lax.fori_loop(0, rows // half, key_lanes, 0)

    def y_wait(i, unused):
        y_copy(i, theirs).wait_recv()
        at = rows_at(theirs + i * chunk, chunk)
        x_ref[at, :] = scaled(tok_ref[at, :])
        return unused

    lax.fori_loop(0, 2, y_wait, 0)
    project(theirs, half // 2)
    begin(2)
    level(0, 1)
    level(mask_piece, 1)
    lax.fori_loop(2, 4, y_wait, 0)
    far_copy.start()
    project(theirs + half // 2, half // 2)
    begin(1)
    if span > 1:
        level(0, 2)
        level(mask_piece, 2)
    settle(0, 0)
    settle(mask_piece, 0)
    turn(2)
    level(1, 1)
    settle(0, 1)
    settle(mask_piece, 1)
    level(2, 1)
    if span > 1:
        level(1, 2)
        settle(0, 2)
        settle(mask_piece, 2)
    settle(1, 0)
    settle(1, 1)
    if span > 1:
        level(2, 2)
        settle(1, 2)
    for k in range(3, span + 1):
        for p in range(4):
            level(p, k)
        for p in (0, 1, mask_piece):
            settle(p, k)

    def finish_line(d, unused):
        @pl.when(~outside(d))
        def _():
            for p in range(4):
                beside(p, d).wait()

        @pl.when(outside(d))
        def _():
            for copy in zero_copies(d):
                copy.wait()

        for p in range(4):

            @pl.when((z + 1 < lines) & (d <= z) & (d > z - span))
            def _(p=p):
                pass_copy(p, 1, d, False).wait_send()

            @pl.when((z > 0) & (d >= z) & (d < z + span))
            def _(p=p):
                pass_copy(p, -1, d, False).wait_send()

        return unused

    lax.fori_loop(0, lines, finish_line, 0)

    def y_drain(i, unused):
        y_copy(i, ours).wait_send()
        return unused

    lax.fori_loop(0, 4, y_drain, 0)
    far_copy.wait()
    near_copy.wait()


def first(
    plan, cycle_size, reach, rows, lengths, table, tokens, gain, mask, w_query, w_key, w_value, cot
):
    lines = cycle_size // 4
    span = min(lines - 1, (reach + 3) // 4)
    half, model = tokens.shape
    pair = 2 * half
    hbm = pl.BlockSpec(memory_space=pl.ANY)
    dma = pltpu.SemaphoreType.DMA
    return pl.pallas_call(
        functools.partial(first_kernel, plan, lines, span, reach, rows),
        out_shape=[
            jax.ShapeDtypeStruct((pair, model), bf16),
            jax.ShapeDtypeStruct((pair, model), bf16),
            jax.ShapeDtypeStruct((pair, WIDE), bf16),
            jax.ShapeDtypeStruct((pair, 2 * plan.cols), bf16),
            jax.ShapeDtypeStruct((rows, 128), bf16),
            jax.ShapeDtypeStruct((pair, 128), bf16),
            jax.ShapeDtypeStruct((2, plan.heads, TQ, TK), f32),
            jax.ShapeDtypeStruct((lines, 2, 2, 8, pair), f32),
            jax.ShapeDtypeStruct((pair, model), bf16),
            jax.ShapeDtypeStruct((lines, 2, 2, pair, 2 * plan.cols), bf16),
        ],
        in_specs=[smem] * 2 + [vmem] * 3 + [hbm] * 4,
        out_specs=[vmem] * 8 + [hbm] * 2,
        scratch_shapes=[
            pltpu.VMEM((3 * plan.cols, model), bf16),
            pltpu.VMEM((pair, 2 * plan.cols), bf16),
            pltpu.VMEM((8, pair), f32),
            dma((4,)),
            dma((2, 5)),
            dma((4,)),
            dma((lines, 2, 2)),
            dma((4, 4, lines)),
            dma((4, 2, lines)),
            dma((4, 2, lines)),
        ],
        compiler_params=pltpu.CompilerParams(
            vmem_limit_bytes=56 * 2**20, collective_id=4, has_side_effects=True
        ),
        name="project_gather",
    )(lengths, table, tokens, gain, mask, w_query.T, w_key.T, w_value.T, cot)


def tn(a, b):
    return lax.dot_general(a, b, (((0,), (0,)), ((), ())), preferred_element_type=f32)


def line_relay(spot, start, receive):
    def level(k, unused):
        @pl.when(spot.z - k >= 0)
        def _():
            if_first(k, lambda: receive(1, spot.z - k))

            @pl.when(spot.z + 1 < spot.lines)
            def _():
                start(1, spot.z - k)

        @pl.when(spot.z + k < spot.lines)
        def _():
            if_first(k, lambda: receive(-1, spot.z + k))

            @pl.when(spot.z > 0)
            def _():
                start(-1, spot.z + k)

        return unused

    def if_first(k, run):
        @pl.when(k > 0)
        def _():
            run()

    return level


def finish_kernel(
    plan, lines, dq_hbm, dk_hbm, dv_hbm, att_hbm, normed_hbm, branch_hbm, far_hbm,
    wq_hbm, wk_hbm, wv_hbm, hidden_hbm, own_hbm, in_hbm,
    mask_ref, tokens_ref, gain_ref, gh_ref, table_ref, gain_part_ref,
    out_ref, turned_ref, gm_ref, weights_ref, gain_one_ref, gain_two_ref, table_out_ref,
    gt_ref, hidden_ref, ffn_own, ffn_in, w3_ref, load_sem, lefts, rights, product, mine, core_in, x_in, up_in, down_in, all_w, y_out, y_in, own_part, mask_in,
    small_own, small_y, small_core, small_x, small_all,
    y_sem, core_sem, x_sem, up_sem, down_sem, gz_sem, gx_sem, gc_sem, sz_sem,
):
    spot = Spot(lines)
    z, x, core, wa = (spot.z, spot.x, spot.core, spot.wa)
    cols = plan.cols
    half = tokens_ref.shape[0]
    our_rows = pl.ds(pl.multiple_of(wa * half, half), half)
    their_rows = pl.ds(pl.multiple_of((1 - wa) * half, half), half)
    targets = (
        (dq_hbm, lefts.at[0]),
        (normed_hbm, rights.at[0]),
        (att_hbm, lefts.at[3]),
        (branch_hbm, rights.at[1, our_rows]),
        (far_hbm, rights.at[1, their_rows]),
        (dk_hbm, lefts.at[1]),
        (dv_hbm, lefts.at[2]),
        (wq_hbm, w3_ref.at[pl.ds(0, cols)]),
        (wk_hbm, w3_ref.at[pl.ds(WIDE, cols)]),
        (wv_hbm, w3_ref.at[pl.ds(3 * WIDE - cols, cols)]),
        (hidden_hbm, hidden_ref),
        (own_hbm, ffn_own),
        (in_hbm, ffn_in),
    )
    loads = [
        pltpu.make_async_copy(src, dst, load_sem.at[i]) for i, (src, dst) in enumerate(targets)
    ]
    for load in loads:
        load.start()
    gap = jnp.zeros((WIDE - cols, tokens_ref.shape[1]), bf16)
    w3_ref[cols:WIDE] = gap
    w3_ref[WIDE + cols : 2 * WIDE] = gap
    w3_ref[2 * WIDE : 3 * WIDE - cols] = gap
    greet(spot, True)
    quarter = half // 2
    model = tokens_ref.shape[1]
    rows = mine.shape[3]

    def grad_rows(at):
        at = pl.ds(pl.multiple_of(at, quarter), quarter)
        return (
            nn(lefts[0, at, :], w3_ref[0:256])
            + nn(lefts[1, at, :], w3_ref[256:512])
            + nn(lefts[2, at, :], w3_ref[512:768])
        )

    def y_copy(i):
        return send(y_out.at[i], y_in.at[i], y_sem.at[0, i], y_sem.at[1, i], spot.y_mate())

    def theirs(i, unused):
        y_out[i] = grad_rows((1 - wa) * half + i * quarter).astype(bf16)
        y_copy(i).start()
        return unused

    for i in (0, 5, 6, 7, 8, 9):
        loads[i].wait()
    lax.fori_loop(0, 2, theirs, 0)
    mask_copy = send(
        mask_ref.at[1 - wa], mask_in, y_sem.at[0, 2], y_sem.at[1, 2], spot.y_mate()
    )
    mask_copy.start()
    for i in (1, 2, 3, 4):
        loads[i].wait()
    per = plan.cols // rows

    def core_copy(m):
        part = pl.ds(m * per // 4, per // 4)
        return send(
            mine.at[part, :, 1 - core],
            core_in.at[part],
            core_sem.at[0, m],
            core_sem.at[1, m],
            spot.core_mate(),
        )

    def fill(i, unused):
        m = (3 * i) % 4
        product[...] = tn(lefts[m], rights[m // 3]).astype(bf16)

        def place(offset):
            for j in range(per):
                mine[m * per // 4 + j // 4, (j // 2) % 2, j % 2] = product[
                    offset + j * rows : offset + (j + 1) * rows, :
                ]

        @pl.when(m < 2)
        def _():
            place(0)

        @pl.when(m >= 2)
        def _():
            place(WIDE - plan.cols)

        core_copy(m).start()
        return unused

    lax.fori_loop(0, 4, fill, 0)
    def x_copy(d):
        return send(
            mine.at[d, 1 - x, core], x_in.at[d], x_sem.at[0, d], x_sem.at[1, d], spot.x_mate()
        )

    def core_add(d, unused):
        mine[d, 1 - x, core] = added(mine[d, 1 - x, core], core_in[d, 1 - x])
        x_copy(d).start()
        return unused

    def ours(i, unused):
        own_part[pl.ds(pl.multiple_of(i * quarter, quarter), quarter), :] = grad_rows(
            wa * half + i * quarter
        )
        return unused

    def core_stage(i, unused):
        m = (3 * i) % 4
        core_copy(m).wait()
        lax.fori_loop(m * per // 4, (m + 1) * per // 4, core_add, 0)
        return unused

    lax.fori_loop(0, 4, core_stage, 0)

    def core_add_own(d, unused):
        mine[d, x, core] = added(mine[d, x, core], core_in[d, x])
        return unused

    lax.fori_loop(0, lines, core_add_own, 0)
    lax.fori_loop(0, 2, ours, 0)

    def flow(step, d):
        ring, sem = (up_in, up_sem) if step > 0 else (down_in, down_sem)
        return send(
            mine.at[d, x, core], ring.at[d], sem.at[0, d], sem.at[1, d], spot.z_mate(step)
        )

    def merge(step, d):
        flow(step, d).wait_recv()
        ring = up_in if step > 0 else down_in
        mine[d, x, core] = added(mine[d, x, core], ring[d])

    def x_add(i, unused):
        d = (i * (lines - 1)) % lines
        x_copy(d).wait()
        mine[d, x, core] = added(mine[d, x, core], x_in[d])

        @pl.when((z == 0) & (d > 0))
        def _():
            flow(1, d).start()

        @pl.when((z == lines - 1) & (d < lines - 1))
        def _():
            flow(-1, d).start()

        return unused

    lax.fori_loop(0, lines, x_add, 0)
    gain_sum = jnp.zeros((1, model), f32)
    step = 32
    for i in range(2):
        y_copy(i).wait()

        def normal(j, total, i=i):
            at = pl.ds(pl.multiple_of(i * quarter + j * step, step), step)
            there = pl.ds(pl.multiple_of(j * step, step), step)
            grad = own_part[at, :] + y_in[i, there, :].astype(f32)
            rows_in = tokens_ref[at, :].astype(f32)
            inv = lax.rsqrt(jnp.mean(rows_in * rows_in, axis=-1, keepdims=True) + eps)
            scaled = gain_ref[...][None, :] * grad
            mean = jnp.mean(rows_in * scaled, axis=-1, keepdims=True)
            gt_ref[at, :] = gh_ref[at, :] + inv * scaled - rows_in * (inv * inv * inv * mean)
            return total + jnp.sum(grad * rows_in * inv, axis=0, keepdims=True)

        gain_sum = lax.fori_loop(0, quarter // step, normal, gain_sum)
    small_own[...] = jnp.zeros_like(small_own)
    small_own[0:1, :] = gain_sum
    small_own[1:2, :] = gain_part_ref[...]
    for h in range(plan.heads):
        small_own[2:3, 32 * h : 32 * h + 32] = jnp.sum(
            jnp.transpose(table_ref[h]), axis=0, keepdims=True
        )
    small_copy = send(
        small_own, small_y, y_sem.at[0, 4], y_sem.at[1, 4], spot.y_mate()
    )
    small_copy.start()
    mask_copy.wait()
    gm_ref[...] = jnp.sum(mask_ref[wa, 0:1] + mask_in[0:1], axis=0)
    def relay(k, unused):
        high = lines - 1 - k

        @pl.when((z < high) & (z > 0))
        def _():
            merge(1, high)
            flow(1, high).start()

        @pl.when((z > k) & (z + 1 < lines))
        def _():
            merge(-1, k)
            flow(-1, k).start()

        return unused

    lax.fori_loop(0, 1, relay, 0)
    small_copy.wait()
    row = lax.broadcasted_iota(jnp.int32, small_own.shape, 0)
    small_x[0] = small_own[...] + jnp.where(row < 2, small_y[...], 0.0)
    small_core_copy = send(
        small_x.at[0], small_core, core_sem.at[0, 4], core_sem.at[1, 4], spot.core_mate()
    )
    small_core_copy.start()
    lax.fori_loop(1, lines - 1, relay, 0)
    small_core_copy.wait()
    small_x[1] = small_x[0] + small_core[...]
    small_x_copy = send(
        small_x.at[1], small_x.at[2], x_sem.at[0, lines], x_sem.at[1, lines], spot.x_mate()
    )
    small_x_copy.start()

    @pl.when(z > 0)
    def _():
        merge(1, z)

    @pl.when(z + 1 < lines)
    def _():
        merge(-1, z)

    all_w[z, x, core] = mine[z, x, core]

    def pass_w(step, d):
        i = 0 if step > 0 else 1
        return send(
            all_w.at[d, x, core], all_w.at[d, x, core], gz_sem.at[i, d], gz_sem.at[2 + i, d],
            spot.z_mate(step),
        )

    def pass_s(step, d):
        i = 0 if step > 0 else 1
        return send(
            small_all.at[d], small_all.at[d], sz_sem.at[i, d], sz_sem.at[2 + i, d],
            spot.z_mate(step),
        )

    def across(d):
        return send(
            all_w.at[d, x, core], all_w.at[d, x, core], gx_sem.at[0, d], gx_sem.at[1, d],
            spot.x_mate(),
        )

    def beside(d):
        return send(
            all_w.at[d, :, core], all_w.at[d, :, core], gc_sem.at[0, d], gc_sem.at[1, d],
            spot.core_mate(),
        )

    small_x_copy.wait()
    small_all[z] = small_x[1] + small_x[2]

    def receive(step, d):
        pass_w(step, d).wait_recv()
        across(d).start()

    across(z).start()
    def pass_both(step, d):
        pass_s(step, d).start()
        pass_w(step, d).start()

    def receive_both(step, d):
        pass_s(step, d).wait_recv()
        receive(step, d)

    lax.fori_loop(0, lines, line_relay(spot, pass_both, receive_both), 0)

    def add_small(d, total):
        return total + small_all[d]

    totals = lax.fori_loop(1, lines, add_small, small_all[0])
    gain_one_ref[...] = jnp.sum(totals[0:1], axis=0)
    gain_two_ref[...] = jnp.sum(totals[1:2], axis=0)
    for h in range(plan.heads):
        table_out_ref[h : h + 1, :] = totals[2:3, 32 * h : 32 * h + 32]
    for i in (10, 11, 12):
        loads[i].wait()
    for c in range(0, model, 128):
        end = min(model, c + 128)
        turned_ref[c:end, :] = jnp.transpose(gt_ref[:, c:end])
        total = hidden_ref[:, c:end] + ffn_own[:, c:end].astype(f32) + ffn_in[:, c:end].astype(f32)
        out_ref[c:end, :] = jnp.transpose(total).astype(bf16)

    def spread(d, unused):
        across(d).wait()
        beside(d).start()
        return unused

    lax.fori_loop(0, lines, spread, 0)

    def copy_out(d, unused):
        beside(d).wait()
        weights_ref[d] = all_w[d]
        return unused

    lax.fori_loop(0, lines, copy_out, 0)

    def drain(d, unused):
        @pl.when((z < d))
        def _():
            flow(1, d).wait_send()

        @pl.when((z > d))
        def _():
            flow(-1, d).wait_send()

        @pl.when((d <= z) & (z + 1 < lines))
        def _():
            pass_w(1, d).wait_send()
            pass_s(1, d).wait_send()

        @pl.when((d >= z) & (z > 0))
        def _():
            pass_w(-1, d).wait_send()
            pass_s(-1, d).wait_send()

        return unused

    lax.fori_loop(0, lines, drain, 0)


def finish(plan, cycle_size, *operands):
    lines = cycle_size // 4
    half, model = operands[14].shape
    rows = 4 * plan.cols // cycle_size
    dma = pltpu.SemaphoreType.DMA
    return pl.pallas_call(
        functools.partial(finish_kernel, plan, lines),
        out_shape=[
            jax.ShapeDtypeStruct((model, half), bf16),
            jax.ShapeDtypeStruct((model, half), f32),
            jax.ShapeDtypeStruct((half,), f32),
            jax.ShapeDtypeStruct((lines, 2, 2, rows, model), bf16),
            jax.ShapeDtypeStruct((model,), f32),
            jax.ShapeDtypeStruct((model,), f32),
            jax.ShapeDtypeStruct((plan.heads, 32), f32),
        ],
        in_specs=[pl.BlockSpec(memory_space=pl.ANY)] * 13 + [vmem] * 6,
        out_specs=[vmem] * 7,
        scratch_shapes=[
            pltpu.VMEM((half, model), f32),
            pltpu.VMEM((half, model), f32),
            pltpu.VMEM((half, model), bf16),
            pltpu.VMEM((half, model), bf16),
            pltpu.VMEM((3 * WIDE, model), bf16),
            dma((13,)),
            pltpu.VMEM((4, 2 * half, WIDE), bf16),
            pltpu.VMEM((2, 2 * half, model), bf16),
            pltpu.VMEM((WIDE, model), bf16),
            pltpu.VMEM((lines, 2, 2, rows, model), bf16),
            pltpu.VMEM((lines, 2, rows, model), bf16),
            pltpu.VMEM((lines, rows, model), bf16),
            pltpu.VMEM((lines, rows, model), bf16),
            pltpu.VMEM((lines, rows, model), bf16),
            pltpu.VMEM((lines, 2, 2, rows, model), bf16),
            pltpu.VMEM((2, half // 2, model), bf16),
            pltpu.VMEM((2, half // 2, model), bf16),
            pltpu.VMEM((half, model), f32),
            pltpu.VMEM((8, half), f32),
            pltpu.VMEM((8, model), f32),
            pltpu.VMEM((8, model), f32),
            pltpu.VMEM((8, model), f32),
            pltpu.VMEM((3, 8, model), f32),
            pltpu.VMEM((lines, 8, model), f32),
            dma((2, 5)),
            dma((2, 5)),
            dma((2, lines + 1)),
            dma((2, lines)),
            dma((2, lines)),
            dma((4, lines)),
            dma((2, lines)),
            dma((2, lines)),
            dma((4, lines)),
        ],
        compiler_params=pltpu.CompilerParams(
            vmem_limit_bytes=58 * 2**20, collective_id=2, has_side_effects=True
        ),
        name="finish",
    )(*operands)


root = 0.7978845608028654
cubic = 0.044715


def middle_kernel(
    plan, cycle_size, att_ref, mixed_ref, tokens_ref, cot_ref, gain_ref,
    wo_hbm, wo_pair_hbm, wg_hbm, wu_hbm, wd_hbm,
    hidden_ref, gh_ref, branch_ref, ffn_ref, ffn_far_ref, do_ref, gain_part_ref, *refs,
):
    stacks, refs = (refs[:3], refs[3:])
    (
        wg, wu, wd, wo, inner, gg, gu, x_ref, att_in, d_out, d_in, e_out, e_in,
        acc_g, rows_buf, load_sem, y_sem, out_sem,
    ) = refs
    spot = Spot(cycle_size // 4)
    wa = spot.wa
    pair, model = tokens_ref.shape
    half = pair // 2
    units = wd.shape[1]
    chunk = half // 4
    block = pair // 4
    loads = [
        pltpu.make_async_copy(src, dst, load_sem.at[i])
        for i, (src, dst) in enumerate(
            (
                (wo_hbm, wo.at[0, 64:]),
                (wo_pair_hbm.at[1 - wa], wo.at[1, 64:]),
                (wg_hbm, wg),
                (wu_hbm, wu),
                (wd_hbm, wd),
            )
        )
    ]
    for load in loads:
        load.start()
    barrier = pltpu.get_barrier_semaphore()
    pl.semaphore_signal(
        barrier, inc=1, device_id=spot.y_mate(), device_id_type=pl.DeviceIdType.MESH
    )
    wo[:, :64, :] = jnp.zeros((2, 64, model), bf16)
    pl.semaphore_wait(barrier, 1)
    ours = wa * half
    theirs = (1 - wa) * half

    def rows_at(start, size):
        return pl.ds(pl.multiple_of(start, size), size)

    def a_start(i):
        return (theirs + i * block) if i < 2 else (ours + (i - 2) * block)

    def a_copy(i, base):
        at = rows_at(base + (i % 2) * block, block)
        return send(att_ref.at[at], att_in.at[at], y_sem.at[0, i], y_sem.at[1, i], spot.y_mate())

    order = (0, 1, 2, 3)
    for i in order:
        a_copy(i, ours if i < 2 else theirs).start()
    loads[0].wait()
    loads[1].wait()

    def normal(i, base, keep):
        a_copy(i, base).wait_recv()
        at = rows_at(base + (i % 2) * block, block)
        branch = nn(att_ref[at, :], wo[0]) + nn(att_in[at, :], wo[1])
        hidden = tokens_ref[at, :].astype(f32) + branch
        if keep:
            hidden_ref[(i % 2) * block : (i % 2 + 1) * block, :] = hidden
        inv = lax.rsqrt(jnp.mean(hidden * hidden, axis=-1, keepdims=True) + eps)
        x_ref[at, :] = (hidden * inv * gain_ref[...][None, :]).astype(bf16)

    normal(0, theirs, False)
    normal(1, theirs, False)
    for load in loads[2:]:
        load.wait()
    wide = 256

    def feed(base):
        rows = rows_at(base, half)
        def tile(u, unused):
            cols = rows_at(u * wide, wide)
            gate = nn(x_ref[rows, :], wg[:, cols])
            upward = nn(x_ref[rows, :], wu[:, cols])
            grad_inner = nn(cot_ref[rows, :], wd[:, cols])
            square = gate * gate
            bend = jnp.tanh(root * gate * (1.0 + cubic * square))
            side = 0.5 * (1.0 + bend)
            gelu = gate * side
            slope = side + 0.5 * gate * (1.0 - bend * bend) * (
                root * (1.0 + 3.0 * cubic * square)
            )
            inner_low = (gelu * upward).astype(bf16)
            gate_low = (grad_inner * upward * slope).astype(bf16)
            up_low = (grad_inner * gelu).astype(bf16)
            inner[rows, cols] = inner_low
            gg[rows, cols] = gate_low
            gu[rows, cols] = up_low
            return unused

        lax.fori_loop(0, units // wide, tile, 0)

    def columns(body):
        def chunk_of(c, unused):
            body(rows_at(c * wide, wide))
            return unused

        lax.fori_loop(0, model // wide, chunk_of, 0)
        if model % wide:
            body(pl.ds(model // wide * wide, model % wide))

    def back_to_rows(base):
        rows = rows_at(base, half)

        def body(cols):
            acc_g[:, cols] = nt(gg[rows, :], wg[cols, :]) + nt(gu[rows, :], wu[cols, :])

        columns(body)

    def forward_to_rows(base, out):
        rows = rows_at(base, half)

        def body(cols):
            out[:, cols] = nt(inner[rows, :], wd[cols, :]).astype(bf16)

        columns(body)

    def d_copy(i):
        return send(
            d_out.at[i], d_in.at[i], y_sem.at[0, 4 + i], y_sem.at[1, 4 + i], spot.y_mate()
        )

    def send_grad(i, unused):
        d_out[i] = acc_g[rows_at(i * chunk, chunk), :].astype(bf16)
        d_copy(i).start()
        return unused

    def half_pass(k, unused):
        base = theirs + k * (ours - theirs)
        feed(base)
        back_to_rows(base)

        @pl.when(k == 0)
        def _():
            lax.fori_loop(0, 4, send_grad, 0)
            normal(2, ours, True)
            normal(3, ours, True)

        return unused

    lax.fori_loop(0, 2, half_pass, 0)
    forward_to_rows(theirs, ffn_far_ref)
    forward_to_rows(ours, ffn_ref)
    count = units // wide

    def out_copy(m, u):
        return pltpu.make_async_copy(
            rows_buf.at[m, u % 2],
            stacks[m].at[rows_at(u * wide, wide)],
            out_sem.at[m, u % 2],
        )

    for m in range(3):
        left = (inner, gg, gu)[m]
        right = (cot_ref, x_ref, x_ref)[m]

        def weight_rows(u, unused, m=m, left=left, right=right):
            @pl.when(u >= 2)
            def _():
                out_copy(m, u - 2).wait()

            turned = jnp.transpose(left[:, rows_at(u * wide, wide)])
            rows_buf[m, u % 2] = nn(turned, right[...]).astype(bf16)
            out_copy(m, u).start()
            return unused

        lax.fori_loop(0, count, weight_rows, 0)

    def e_copy(i):
        return send(
            e_out.at[i], e_in.at[i], y_sem.at[0, 8 + i], y_sem.at[1, 8 + i], spot.y_mate()
        )

    def normal_back(i, total):
        d_copy(i).wait()
        at = rows_at(i * chunk, chunk)
        grad = acc_g[at, :] + d_in[i].astype(f32)
        hidden = hidden_ref[at, :]
        inv = lax.rsqrt(jnp.mean(hidden * hidden, axis=-1, keepdims=True) + eps)
        scaled = gain_ref[...][None, :] * grad
        mean = jnp.mean(hidden * scaled, axis=-1, keepdims=True)
        grad_hidden = (
            cot_ref[rows_at(ours + i * chunk, chunk), :].astype(f32)
            + inv * scaled
            - hidden * (inv * inv * inv * mean)
        )
        gh_ref[at, :] = grad_hidden
        low = grad_hidden.astype(bf16)
        branch_ref[at, :] = low
        e_out[i] = nt(low, wo[1]).astype(bf16)
        e_copy(i).start()
        do_ref[rows_at(ours + i * chunk, chunk), :] = nt(low, wo[0]).astype(bf16)
        return total + jnp.sum(grad * hidden * inv, axis=0, keepdims=True)

    gain_part_ref[...] = lax.fori_loop(0, 4, normal_back, jnp.zeros((1, model), f32))

    def row_terms(at, grad):
        lane = lanes_of(chunk)
        terms = grad.astype(f32) * mixed_ref[at, :]
        out = grad
        for h in range(plan.heads):
            row_term = jnp.sum(
                jnp.where(lane // 64 == h + 1, terms, 0.0), axis=1, keepdims=True
            )
            for i, part in enumerate(split3(-row_term)):
                out = jnp.where(lane == 3 * h + i, part, out)
        do_ref[at, :] = out

    def own_terms(i, unused):
        at = rows_at(ours + i * chunk, chunk)
        row_terms(at, do_ref[at, :])
        return unused

    lax.fori_loop(0, 4, own_terms, 0)

    def far_terms(i, unused):
        e_copy(i).wait()
        row_terms(rows_at(theirs + i * chunk, chunk), e_in[i])
        return unused

    lax.fori_loop(0, 4, far_terms, 0)
    for m in range(3):
        for u in range(max(0, count - 2), count):
            out_copy(m, u).wait()
    for i in order:
        a_copy(i, ours if i < 2 else theirs).wait_send()


def middle(
    plan, cycle_size, attended, mixed, tokens, cot, gain, w_out, w_out_pair, w_gate, w_up, w_down
):
    pair, model = tokens.shape
    half = pair // 2
    units = w_down.shape[0]
    chunk = half // 4
    hbm = pl.BlockSpec(memory_space=pl.ANY)
    dma = pltpu.SemaphoreType.DMA
    return pl.pallas_call(
        functools.partial(middle_kernel, plan, cycle_size),
        out_shape=[
            jax.ShapeDtypeStruct((half, model), f32),
            jax.ShapeDtypeStruct((half, model), f32),
            jax.ShapeDtypeStruct((half, model), bf16),
            jax.ShapeDtypeStruct((half, model), bf16),
            jax.ShapeDtypeStruct((half, model), bf16),
            jax.ShapeDtypeStruct((pair, WIDE), bf16),
            jax.ShapeDtypeStruct((1, model), f32),
        ]
        + [jax.ShapeDtypeStruct((units, model), bf16)] * 3,
        in_specs=[vmem] * 5 + [hbm] * 5,
        out_specs=[vmem] * 7 + [hbm] * 3,
        scratch_shapes=[
            pltpu.VMEM((model, units), bf16),
            pltpu.VMEM((model, units), bf16),
            pltpu.VMEM((model, units), bf16),
            pltpu.VMEM((2, WIDE, model), bf16),
            pltpu.VMEM((pair, units), bf16),
            pltpu.VMEM((pair, units), bf16),
            pltpu.VMEM((pair, units), bf16),
            pltpu.VMEM((pair, model), bf16),
            pltpu.VMEM((pair, WIDE), bf16),
            pltpu.VMEM((4, chunk, model), bf16),
            pltpu.VMEM((4, chunk, model), bf16),
            pltpu.VMEM((4, chunk, WIDE), bf16),
            pltpu.VMEM((4, chunk, WIDE), bf16),
            pltpu.VMEM((half, model), f32),
            pltpu.VMEM((3, 2, WIDE, model), bf16),
            dma((5,)),
            dma((2, 12)),
            dma((3, 2)),
        ],
        compiler_params=pltpu.CompilerParams(
            vmem_limit_bytes=60 * 2**20, collective_id=3, has_side_effects=True
        ),
        name="feed_forward",
    )(attended, mixed, tokens, cot, gain, w_out, w_out_pair, w_gate, w_up, w_down.T)


class Scatter:
    def __init__(self, spot, units, parts, outs, buffers, sems):
        self.spot = spot
        self.units = units
        self.parts = parts
        self.outs = outs
        self.mine, self.core_in, self.x_in, self.up_in, self.down_in = buffers
        self.load_sem, self.core_sem, self.x_sem, self.up_sem, self.down_sem = sems

    def rows_of(self, u):
        return pl.ds(self.units[u][1], self.units[u][2])

    def load(self, u):
        m = self.units[u][0]
        return pltpu.make_async_copy(
            self.parts[m].at[:, :, self.spot.core, self.rows_of(u)],
            self.mine.at[m, :, :, self.rows_of(u)],
            self.load_sem.at[u],
        )

    def core_copy(self, u):
        m = self.units[u][0]
        return send(
            self.parts[m].at[:, :, 1 - self.spot.core, self.rows_of(u)],
            self.core_in.at[m, :, :, self.rows_of(u)],
            self.core_sem.at[0, u],
            self.core_sem.at[1, u],
            self.spot.core_mate(),
        )

    def x_copy(self, u):
        m = self.units[u][0]
        x = self.spot.x
        src = self.mine.at[m, :, 1 - x, self.rows_of(u)]
        dst = self.x_in.at[m, :, self.rows_of(u)]
        return send(src, dst, self.x_sem.at[0, u], self.x_sem.at[1, u], self.spot.x_mate())

    def begin(self, u):
        self.load(u).start()
        self.core_copy(u).start()

    def core_stage(self, u):
        m = self.units[u][0]
        x = self.spot.x
        self.load(u).wait()
        self.core_copy(u).wait()

        def add(slot):
            def body(line, unused):
                at = (m, line, slot, self.rows_of(u))
                self.mine[at] = added(self.mine[at], self.core_in[at])
                return unused

            lax.fori_loop(0, self.spot.lines, body, 0)

        add(1 - x)
        self.x_copy(u).start()
        add(x)

    def x_stage(self, u):
        m = self.units[u][0]
        x = self.spot.x
        self.x_copy(u).wait()

        def body(line, unused):
            at = (m, line, x, self.rows_of(u))
            self.mine[at] = added(self.mine[at], self.x_in[m, line, self.rows_of(u)])
            return unused

        lax.fori_loop(0, self.spot.lines, body, 0)
        self.ends(u)

    def copy(self, u, step, d):
        m = self.units[u][0]
        sem = self.up_sem if step > 0 else self.down_sem
        ring = self.up_in if step > 0 else self.down_in
        return send(
            self.mine.at[m, d, self.spot.x, self.rows_of(u)],
            ring.at[m, d, self.rows_of(u)],
            sem.at[0, u, d],
            sem.at[1, u, d],
            self.spot.z_mate(step),
        )

    def receive(self, u, step, d):
        m = self.units[u][0]
        self.copy(u, step, d).wait_recv()
        ring = self.up_in if step > 0 else self.down_in
        at = (m, d, self.spot.x, self.rows_of(u))
        self.mine[at] = added(self.mine[at], ring[m, d, self.rows_of(u)])

    def start(self, u, step, d):
        self.copy(u, step, d).start()

    def ends(self, u):
        z, lines = (self.spot.z, self.spot.lines)

        @pl.when(z == 0)
        def _():
            def up(k, unused):
                self.start(u, 1, lines - 1 - k)
                return unused

            lax.fori_loop(0, lines - 1, up, 0)

        @pl.when(z == lines - 1)
        def _():
            def down(k, unused):
                self.start(u, -1, k)
                return unused

            lax.fori_loop(0, lines - 1, down, 0)

    def relay(self, u, lag):
        z, lines = (self.spot.z, self.spot.lines)
        top = lines - 2 if lag == 2 else lag

        @pl.when((z >= lag) & (z <= top))
        def _():
            def up(k, unused):
                self.receive(u, 1, lines - 1 - k)
                self.start(u, 1, lines - 1 - k)
                return unused

            lax.fori_loop(0, lines - 1 - z, up, 0)

        @pl.when((lines - 1 - z >= lag) & (lines - 1 - z <= top))
        def _():
            def down(k, unused):
                self.receive(u, -1, k)
                self.start(u, -1, k)
                return unused

            lax.fori_loop(0, z, down, 0)

    def settle(self, u):
        z, lines = (self.spot.z, self.spot.lines)

        @pl.when(z > 0)
        def _():
            self.receive(u, 1, z)

        @pl.when(z + 1 < lines)
        def _():
            self.receive(u, -1, z)

        self.store(u)

    def store(self, u):
        m = self.units[u][0]
        self.outs[m][self.rows_of(u), :] = self.mine[
            m, self.spot.z, self.spot.x, self.rows_of(u)
        ]

    def drain(self, u):
        z, lines = (self.spot.z, self.spot.lines)

        def body(k, unused):
            @pl.when(z < lines - 1 - k)
            def _():
                self.copy(u, 1, lines - 1 - k).wait_send()

            @pl.when(z > k)
            def _():
                self.copy(u, -1, k).wait_send()

            return unused

        lax.fori_loop(0, lines - 1, body, 0)


def scatter_units(rows):
    if rows % 16 or rows < 112:
        return [(m, 0, rows) for m in range(3)]
    tail = rows - 64
    return [
        (0, 0, 64), (1, 0, 64), (2, 0, 64), (0, 64, tail), (1, 64, tail), (2, 64, tail - 16),
        (2, rows - 16, 16),
    ]


def backward_kernel(
    plan, lines, span, reach, doc_most, rows, pair, table_ref, qb_ref, do_ref,
    own_kv, own_aug, near_hbm, aug_hbm, masks_hbm, g_hbm, qall_hbm, branch_hbm, ffn_hbm, p0, p1, p2,
    dq_ref, tab_ref, dk_ref, dv_ref, mask_ref, o0, o1, o2, far_hbm, ffn_in_hbm, all_do,
    mine, core_in, x_in, up_in, down_in,
    km, vm, mask_row, g_buf, aug_buf, qh_ref, doh_ref, acc, near_ref, near_acc, far_acc,
    load_sem, core_sem, rx_sem, up_sem, down_sem, own_sem, zero_sem, z_sem, x_sem, c_sem, g_sem,
    q_sem,
):
    spot = Spot(lines)
    z, x, core = (spot.z, spot.x, spot.core)
    units = scatter_units(o0.shape[0])
    scatter = Scatter(
        spot,
        units,
        (p0, p1, p2),
        (o0, o1, o2),
        (mine, core_in, x_in, up_in, down_in),
        (load_sem, core_sem, rx_sem, up_sem, down_sem),
    )
    order = range(len(units))
    greet(spot, True)
    far_copy = send(branch_hbm, far_hbm, own_sem.at[2], own_sem.at[3], spot.y_mate())
    far_copy.start()
    ffn_copy = send(ffn_hbm, ffn_in_hbm, own_sem.at[4], own_sem.at[5], spot.y_mate())
    ffn_copy.start()

    def outside(d):
        return (d < z - span) | (d > z + span)

    def pass_copy(step, d):
        i = 0 if step > 0 else 1
        part = all_do.at[d, :, core]
        return send(part, part, z_sem.at[i, d], z_sem.at[2 + i, d], spot.z_mate(step))

    across = send(do_ref, all_do.at[z, x, core], x_sem.at[0], x_sem.at[1], spot.x_mate())

    def beside(d):
        part = all_do.at[d, :, core]
        return send(part, part, c_sem.at[0, d], c_sem.at[1, d], spot.core_mate())

    own_copy = pltpu.make_async_copy(do_ref, all_do.at[z, x, core], own_sem.at[0])

    def zero_copies(d):
        return [
            pltpu.make_async_copy(vm.at[pl.ds(0, pair)], all_do.at[d, a, b], zero_sem.at[d, a, b])
            for a in range(2)
            for b in range(2)
        ]

    def zero_start(d, unused):
        @pl.when(outside(d))
        def _():
            for copy in zero_copies(d):
                copy.start()

        return unused

    def turn():
        across.wait()
        own_copy.wait()

        @pl.when(z + 1 < lines)
        def _():
            pass_copy(1, z).start()

        @pl.when(z > 0)
        def _():
            pass_copy(-1, z).start()

        beside(z).start()

    def level(k):
        @pl.when(z - k >= 0)
        def _():
            d = jnp.maximum(z - k, 0)
            pass_copy(1, d).wait_recv()
            if k < span:

                @pl.when(z + 1 < lines)
                def _():
                    pass_copy(1, d).start()

            beside(d).start()

        @pl.when(z + k < lines)
        def _():
            d = jnp.minimum(z + k, lines - 1)
            pass_copy(-1, d).wait_recv()
            if k < span:

                @pl.when(z > 0)
                def _():
                    pass_copy(-1, d).start()

            beside(d).start()

    def gathered(d, unused):
        @pl.when(~outside(d))
        def _():
            beside(d).wait()

        @pl.when(outside(d))
        def _():
            for copy in zero_copies(d):
                copy.wait()

        @pl.when((z + 1 < lines) & (d <= z) & (d > z - span))
        def _():
            pass_copy(1, d).wait_send()

        @pl.when((z > 0) & (d >= z) & (d < z + span))
        def _():
            pass_copy(-1, d).wait_send()

        return unused

    own_copy.start()
    across.start()
    for u in order:
        scatter.begin(u)
    vm[:PAD, :] = jnp.zeros((PAD, WIDE), bf16)
    lax.fori_loop(0, lines, zero_start, 0)

    base = spot.index * pair
    total = 4 * lines * pair
    origin = jnp.clip(base - reach * pair, 0, total - rows)
    local = base - origin
    blocks = rows // pair

    def mask_copy(n):
        to = pl.ds(pl.multiple_of(PAD + n * pair, 128), pair)
        return pltpu.make_async_copy(masks_hbm.at[n], mask_row.at[:, to], q_sem.at[1 + n])

    def mask_start(n, unused):
        mask_copy(n).start()
        return unused

    lax.fori_loop(0, blocks, mask_start, 0)
    mask_row[:, :PAD] = jnp.zeros((8, PAD), f32)
    mask_row[:, PAD + rows :] = jnp.zeros((8, PAD), f32)
    km[:PAD, :] = jnp.broadcast_to(
        jnp.where(pad_lanes(plan), neg_big, 0.0).astype(bf16), (PAD, WIDE)
    )
    km[PAD + rows :, :] = km[:PAD, :]
    vm[PAD + rows :, :] = jnp.zeros((PAD, WIDE), bf16)
    low_block = lanes_of(pair, 128) < 64
    ones_block = (lanes_of(pair, 128) < 3 * plan.heads).astype(bf16)

    def g_copy(n):
        at = pl.ds(pl.multiple_of(n * pair, pair), pair)
        return pltpu.make_async_copy(g_hbm.at[at], g_buf.at[n % 2], g_sem.at[0, n % 2])

    def aug_copy(n):
        at = pl.ds(pl.multiple_of(n * pair, pair), pair)
        return pltpu.make_async_copy(aug_hbm.at[at], aug_buf.at[n % 2], g_sem.at[1, n % 2])

    def near_copy(flip):
        return pltpu.make_async_copy(near_hbm.at[flip], near_ref, own_sem.at[1])

    g_copy(0).start()
    aug_copy(0).start()
    near_copy(0).start()

    def build(n, unused):
        g_copy(n).wait()
        aug_copy(n).wait()

        @pl.when(n + 1 < blocks)
        def _():
            g_copy(n + 1).start()
            aug_copy(n + 1).start()

        mask_copy(n).wait()
        to = pl.ds(pl.multiple_of(PAD + n * pair, 128), pair)
        middle = g_buf[n % 2, :, 128:256]
        km[to, 0:128] = g_buf[n % 2, :, 0:128]
        km[to, 128:256] = jnp.where(low_block, middle, aug_buf[n % 2])
        vm[to, 0:128] = jnp.where(low_block, ones_block, middle)
        vm[to, 128:256] = g_buf[n % 2, :, 256:384]
        return unused

    early = min(6, blocks)
    lax.fori_loop(0, early, build, 0)
    scatter.core_stage(0)
    lax.fori_loop(early, blocks, build, 0)
    near_copy(0).wait()
    near_acc[...] = jnp.zeros_like(near_acc)
    far_acc[...] = jnp.zeros_like(far_acc)
    lane = lanes_of(TQ)
    low = lanes_of(TQ, 128) < 64
    ones = (lanes_of(TQ, 128) < 3 * plan.heads).astype(bf16)

    def chunks(t):
        start = local + t * TQ
        least = jnp.maximum(start - doc_most + 1, 0)
        most = jnp.minimum(start + TQ + doc_most - 1, rows)
        n_left = jnp.maximum(start - EDGE - least + TK - 1, 0) // TK
        n_right = jnp.maximum(most - (start + TK - EDGE) + TK - 1, 0) // TK
        return start, n_left, n_right

    def rows_of_tile(t):
        return pl.ds(pl.multiple_of(t * TQ, TQ), TQ)

    def near_of(start):
        return pl.ds(pl.multiple_of(start + PAD - EDGE, 128), TK)

    def query_grads(h, s, part):
        return jnp.exp(s) * nt(doh_ref[h], vm[part, :])

    def dq_near(t, start):
        out = rows_of_tile(t)
        near = near_of(start)
        q = qb_ref[out, :]
        do = do_ref[out, :]
        for h in range(plan.heads):
            qh_ref[h] = jnp.where(plan.key_lanes(lane, h), q, jnp.zeros_like(q))
            doh_ref[h] = jnp.where(plan.value_lanes(lane, h), do, jnp.zeros_like(do))
            ds = query_grads(
                h, nt(qh_ref[h], km[near, :]) + near_ref[h] + mask_row[0:1, near], near
            )
            near_acc[h] += ds
            acc[h] = nn(ds.astype(bf16), km[near, :])

    def dq_far(start, n, n_left, count):
        parts = far_pair(start, n, n_left, count, far_left_bucket, far_right_bucket)
        for h in range(plan.heads):
            grads = []
            for i, (part, bucket) in enumerate(parts):
                slot = (2 * n + i >= n_left).astype(jnp.int32)
                offset = mask_row[0:1, part] + table_ref[h, bucket]
                ds = query_grads(h, nt(qh_ref[h], km[part, :]) + offset, part)
                grads.append(nn(ds.astype(bf16), km[part, :]))
                far_acc[slot, h] += (
                    ds[:, 0:128] + ds[:, 128:256] + ds[:, 256:384] + ds[:, 384:512]
                )
            acc[h] += grads[0] + grads[1]

    def dq_end(t):
        result = jnp.zeros((TQ, WIDE), f32)
        for h in range(plan.heads):
            result = jnp.where(lane // 64 == h, acc[h], result)
        dq_ref[rows_of_tile(t), :] = result.astype(bf16)

    def table_end():
        row = lax.broadcasted_iota(jnp.int32, (EDGE, 3 * EDGE), 0)
        col = lax.broadcasted_iota(jnp.int32, (EDGE, 3 * EDGE), 1)
        bucket = bucket_of(col - EDGE - row)
        for h in range(plan.heads):
            band = near_acc[h, :EDGE, : 3 * EDGE] + near_acc[h, EDGE:, EDGE:]

            def one(b, unused, band=band, h=h):
                part = jnp.sum(jnp.where(bucket == b, band, 0.0), axis=0, keepdims=True)
                tab_ref[h, pl.ds(b, 1), :] = part[:, :128] + part[:, 128:256] + part[:, 256:]
                return unused

            lax.fori_loop(0, 32, one, 0)
            for b, slot, extra in (
                (far_left_bucket, 0, near_acc[h, EDGE:, :EDGE]),
                (far_right_bucket, 1, near_acc[h, :EDGE, 3 * EDGE :]),
            ):
                tab_ref[h, b : b + 1, :] += jnp.sum(
                    far_acc[slot, h], axis=0, keepdims=True
                ) + jnp.sum(extra, axis=0, keepdims=True)

    def swap_operands():
        near_copy(1).start()
        lax.fori_loop(0, lines, gathered, 0)
        q_copy = pltpu.make_async_copy(qall_hbm, km.at[pl.ds(PAD, rows)], q_sem.at[0])
        q_copy.start()

        def block_copy(n):
            b = origin // pair + n
            return pltpu.make_async_copy(
                all_do.at[b // 4, (b // 2) % 2, b % 2],
                vm.at[pl.ds(pl.multiple_of(PAD + n * pair, 128), pair)],
                q_sem.at[1 + n],
            )

        def block_start(n, unused):
            block_copy(n).start()
            return unused

        lax.fori_loop(0, blocks, block_start, 0)
        first = lanes_of(1)
        stat = (first >= plan.stat_lane) & (first < plan.stat_lane + 3 * plan.heads)
        km[:PAD, :] = jnp.broadcast_to(jnp.where(stat, neg_big, 0.0).astype(bf16), (PAD, WIDE))
        km[PAD + rows :, :] = km[:PAD, :]

        def block_wait(n, unused):
            block_copy(n).wait()
            return unused

        lax.fori_loop(0, blocks, block_wait, 0)
        q_copy.wait()
        near_copy(1).wait()

    def key_grads(h, s, part):
        p = jnp.exp(s)
        ds = p * nt(doh_ref[h], vm[part, :])
        return nn(p.astype(bf16), vm[part, :]), nn(ds.astype(bf16), km[part, :])

    def dkv_near(t, start):
        out = rows_of_tile(t)
        near = near_of(start)
        middle = own_kv[out, 128:256]
        k = jnp.concatenate([own_kv[out, 0:128], jnp.where(low, middle, own_aug[out, :])], axis=1)
        v = jnp.concatenate([jnp.where(low, ones, middle), own_kv[out, 256:384]], axis=1)
        for h in range(plan.heads):
            qh_ref[h] = jnp.where(plan.key_lanes(lane, h), k, jnp.zeros_like(k))
            doh_ref[h] = jnp.where(plan.value_lanes(lane, h), v, jnp.zeros_like(v))
            near_acc[h, :, :WIDE], acc[h] = key_grads(
                h, nt(qh_ref[h], km[near, :]) + near_ref[h], near
            )

    def dkv_far(start, n, n_left, count):
        parts = far_pair(start, n, n_left, count, far_right_bucket, far_left_bucket)
        for h in range(plan.heads):
            (v_one, k_one), (v_two, k_two) = [
                key_grads(h, nt(qh_ref[h], km[part, :]) + table_ref[h, bucket], part)
                for part, bucket in parts
            ]
            near_acc[h, :, :WIDE] += v_one + v_two
            acc[h] += k_one + k_two

    def dkv_end(t):
        out = rows_of_tile(t)
        dk = jnp.zeros((TQ, WIDE), f32)
        dv = jnp.zeros((TQ, WIDE), f32)
        mask_grad = jnp.zeros((TQ, 1), f32)
        for h in range(plan.heads):
            dk = jnp.where(lane // 64 == h, acc[h], dk)
            dv = jnp.where(lane // 64 == h + 1, near_acc[h, :, :WIDE], dv)
            mask_grad = mask_grad + acc[h][:, plan.mask_lane : plan.mask_lane + 1]
        mask_ref[t] = jnp.transpose(jnp.broadcast_to(mask_grad, (TQ, 128)))[:8, :]
        dk_ref[out, :] = dk.astype(bf16)
        dv_ref[out, :] = dv.astype(bf16)

    tiles = pair // TQ
    steps = 1 + -(-(2 * (-(-doc_most // TK)) + 1) // 2)
    half_slots = tiles * steps
    last_step = steps - 1

    def attention(w):
        backward = w >= half_slots
        t = (w % half_slots) // steps
        n = w % steps
        start, n_left, n_right = chunks(t)
        count = n_left + n_right
        live = (n > 0) & (2 * (n - 1) < count)

        @pl.when(~backward)
        def _():
            @pl.when(n == 0)
            def _():
                dq_near(t, start)

            @pl.when(live)
            def _():
                dq_far(start, n - 1, n_left, count)

            @pl.when(n == last_step)
            def _():
                dq_end(t)

        @pl.when(backward & (w < 2 * half_slots))
        def _():
            @pl.when(w == half_slots)
            def _():
                table_end()
                swap_operands()

            @pl.when(n == 0)
            def _():
                dkv_near(t, start)

            @pl.when(live)
            def _():
                dkv_far(start, n - 1, n_left, count)

            @pl.when(n == last_step)
            def _():
                dkv_end(t)

    work = 2 * half_slots
    events = []

    def due(time, run, *args):
        events.append((max(0, int((time - start_us) / slot_us)), functools.partial(run, *args)))

    start_us, slot_us = (6.0, 2.5)
    due(6.0, turn)
    for k in range(1, span + 1):
        due((22.0, 36.0)[min(k, 2) - 1], level, k)
    times = (
        (7.0, 26.0, 51.0, 61.0, 68.0),
        (10.5, 43.0, 64.0, 74.0, 81.0),
        (14.0, 60.0, 77.0, 87.0, 94.0),
        (17.0, 73.0, 87.0, 95.0, 101.0),
        (20.0, 86.0, 97.5, 106.0, 111.0),
        (22.0, 95.0, 104.0, 110.0, 114.0),
        (23.0, 99.0, 107.0, 111.0, 114.5),
    )
    for u in order:
        core_at, x_at, one_at, two_at, end_at = times[u]
        if u > 0:
            due(core_at, scatter.core_stage, u)
        due(x_at, scatter.x_stage, u)
        due(one_at - 3.0, scatter.relay, u, 1)
        due(two_at - 3.0, scatter.relay, u, 2)
        due(end_at, scatter.settle, u)
    events.sort(key=lambda event: event[0])
    end = max(work, events[-1][0] + 1)

    def slot(w, unused):
        for at, run in events:

            @pl.when(w == at)
            def _(run=run):
                run()

        attention(w)
        return unused

    lax.fori_loop(0, end, slot, 0)
    for u in order:
        scatter.drain(u)
    far_copy.wait()
    ffn_copy.wait()


def backward(
    plan, cycle_size, reach, doc_most, rows, table, aug, masks, q_back, do_wide, own_kv, own_aug,
    near_bias, kv_all, q_all, branch, ffn_far, parts,
):
    lines = cycle_size // 4
    span = min(lines - 1, (reach + 3) // 4)
    pair = q_back.shape[0]
    units_here, model = parts[0].shape
    size = units_here // cycle_size
    units = scatter_units(size)
    shaped = [part.reshape(lines, 2, 2, size, model) for part in parts]
    n = len(units)
    heads = plan.heads
    padded = rows + 2 * PAD
    hbm = pl.BlockSpec(memory_space=pl.ANY)
    dma = pltpu.SemaphoreType.DMA
    return pl.pallas_call(
        functools.partial(backward_kernel, plan, lines, span, reach, doc_most, rows, pair),
        out_shape=[
            jax.ShapeDtypeStruct((pair, WIDE), bf16),
            jax.ShapeDtypeStruct((heads, 32, 128), f32),
            jax.ShapeDtypeStruct((pair, WIDE), bf16),
            jax.ShapeDtypeStruct((pair, WIDE), bf16),
            jax.ShapeDtypeStruct((pair // TQ, 8, TQ), f32),
        ]
        + [jax.ShapeDtypeStruct((size, model), bf16)] * 3
        + [
            jax.ShapeDtypeStruct(branch.shape, bf16),
            jax.ShapeDtypeStruct(branch.shape, bf16),
            jax.ShapeDtypeStruct((lines, 2, 2, pair, WIDE), bf16),
        ],
        in_specs=[smem] + [vmem] * 4 + [hbm] * 10,
        out_specs=[vmem] * 8 + [hbm] * 3,
        scratch_shapes=[
            pltpu.VMEM((3, lines, 2, size, model), bf16),
            pltpu.VMEM((3, lines, 2, size, model), bf16),
            pltpu.VMEM((3, lines, size, model), bf16),
            pltpu.VMEM((3, lines, size, model), bf16),
            pltpu.VMEM((3, lines, size, model), bf16),
            pltpu.VMEM((padded, WIDE), bf16),
            pltpu.VMEM((padded, WIDE), bf16),
            pltpu.VMEM((8, padded), f32),
            pltpu.VMEM((2, pair, 2 * plan.cols), bf16),
            pltpu.VMEM((2, pair, 128), bf16),
            pltpu.VMEM((heads, TQ, WIDE), bf16),
            pltpu.VMEM((heads, TQ, WIDE), bf16),
            pltpu.VMEM((heads, TQ, WIDE), f32),
            pltpu.VMEM((heads, TQ, TK), f32),
            pltpu.VMEM((heads, TQ, TK), f32),
            pltpu.VMEM((2, heads, TQ, 128), f32),
            dma((n,)),
            dma((2, n)),
            dma((2, n)),
            dma((2, n, lines)),
            dma((2, n, lines)),
            dma((6,)),
            dma((lines, 2, 2)),
            dma((4, lines)),
            dma((2,)),
            dma((2, lines)),
            dma((2, 2)),
            dma((1 + rows // pair,)),
        ],
        compiler_params=pltpu.CompilerParams(
            vmem_limit_bytes=62 * 2**20, collective_id=1, has_side_effects=True
        ),
        name="backward",
    )(
        table, q_back, do_wide, own_kv, own_aug, near_bias, aug, masks, kv_all, q_all,
        branch, ffn_far, *shaped
    )


def shards(
    tokens,
    doc_lengths,
    key_mask,
    gain_attn,
    w_query,
    w_key,
    w_value,
    w_out,
    bias_table,
    gain_ffn,
    w_gate,
    w_up,
    w_down,
    cotangent,
):
    own_rows, model = tokens.shape
    group = lax.axis_size("wa")
    cycle_size = lax.axis_size("ctx")
    pair = own_rows * group
    heads = bias_table.shape[1]
    docs = doc_lengths.shape[0]
    plan = Plan(heads, w_query.shape[1] // heads, docs)
    total_rows = pair * cycle_size
    doc_most = min(MAXLEN, total_rows // 2)
    reach = min(cycle_size - 1, (doc_most - 1) // pair + 1)
    base = lax.axis_index("ctx") * pair
    rows = min(total_rows, (2 * reach + 1) * pair)
    origin = jnp.clip(base - reach * pair, 0, total_rows - rows).astype(jnp.int32)
    table = bias_table.T

    def window(gathered):
        if rows == total_rows:
            return gathered
        return lax.dynamic_slice_in_dim(gathered, origin, rows, 0)

    gather = functools.partial(lax.all_gather, axis_name="ctx", axis=0, tiled=True)
    (
        pair_normed, pair_tokens, q_wide, own_kv, k_aug, own_aug, near_bias, masks, pair_cot, kv_all,
    ) = first(
        plan,
        cycle_size,
        reach,
        rows,
        doc_lengths,
        table,
        tokens,
        gain_attn,
        key_mask,
        w_query,
        w_key,
        w_value,
        cotangent,
    )
    masks = masks.reshape(cycle_size, 8, pair)
    w_late, near_bias = lax.optimization_barrier((w_out, near_bias))
    pair_w_out = lax.all_gather(w_late, "wa", axis=0)
    if rows < total_rows:
        masks = lax.dynamic_slice_in_dim(masks, origin // pair, rows // pair, 0)
    kv_all = window(kv_all.reshape(total_rows, 2 * plan.cols))
    attended, mixed, q_back = attend(
        plan, cycle_size, reach, rows, doc_lengths, table, q_wide, near_bias, kv_all, k_aug, masks
    )
    q_all = window(gather(q_back))
    hidden, grad_hidden, branch, ffn_own, ffn_far, do_wide, gain_ffn_part, *stacks = middle(
        plan,
        cycle_size,
        attended,
        mixed,
        pair_tokens,
        pair_cot,
        gain_ffn,
        w_out,
        pair_w_out,
        w_gate,
        w_up,
        w_down,
    )
    (
        grad_queries, table_part, grad_keys, grad_values, mask_part,
        grad_w_down, grad_w_gate, grad_w_up, far_branch, ffn_in, unused_gathered,
    ) = backward(
        plan,
        cycle_size,
        reach,
        doc_most,
        rows,
        table,
        k_aug,
        masks,
        q_back,
        do_wide,
        own_kv,
        own_aug,
        near_bias,
        kv_all,
        q_all,
        branch,
        ffn_far,
        stacks,
    )
    grad_w_down, grad_w_gate, grad_w_up = (
        grad_w_down.astype(f32), grad_w_gate.astype(f32).T, grad_w_up.astype(f32).T
    )
    layer_out, grad_tokens, grad_mask, weights, grad_gain_attn, grad_gain_ffn, grad_table = finish(
        plan,
        cycle_size,
        grad_queries,
        grad_keys,
        grad_values,
        attended,
        pair_normed,
        branch,
        far_branch,
        w_query.T,
        w_key.T,
        w_value.T,
        hidden,
        ffn_own,
        ffn_in,
        mask_part.reshape(group, 8, own_rows),
        tokens,
        gain_attn,
        grad_hidden,
        table_part,
        gain_ffn_part,
    )
    weights = weights.reshape(4, plan.cols, model).astype(f32)
    return (
        layer_out.T,
        grad_tokens.T,
        grad_mask,
        grad_gain_attn,
        weights[0].T,
        weights[1].T,
        weights[2].T,
        weights[3],
        grad_table.T,
        grad_gain_ffn,
        grad_w_gate,
        grad_w_up,
        grad_w_down,
    )


def solution(mesh):
    placed = (
        P(("ctx", "wa"), None),
        P(),
        P("ctx"),
        P(),
        P(None, "wa"),
        P(None, "wa"),
        P(None, "wa"),
        P("wa", None),
        P(None, "wa"),
        P(),
        P(None, "wa"),
        P(None, "wa"),
        P("wa", None),
        P(("ctx", "wa"), None),
    )
    return jax.shard_map(
        shards,
        mesh=mesh,
        in_specs=placed,
        out_specs=(
            P(("ctx", "wa"), None),
            P(("ctx", "wa"), None),
            P(("ctx", "wa")),
            P(),
            P(None, "wa"),
            P(None, "wa"),
            P(None, "wa"),
            P("wa", None),
            P(None, "wa"),
            P(),
            P(None, ("wa", "ctx")),
            P(None, ("wa", "ctx")),
            P(("wa", "ctx"), None),
        ),
        check_vma=False,
    )
```
